32 devices in a mesh: items: 2 (over x), rows: 16 (over z, y, core).
Axes of the slice: x: 2, y: 2, z: 4, core: 2. Of those that a mesh axis runs over, the one named last changes fastest.
Arguments:
- image: bfloat16 [2, 8192, 512], P('items', 'rows'), may hold values from -6 to 6
- embedding: bfloat16 [2, 16, 2048], P('items'), may hold values from -6 to 6
- caption: bfloat16 [2, 16, 128, 2048], P('items', 'rows'), may hold values from -6 to 6
- item_of_band: int32 [2, 16], P('items'), may hold values from 0 to 2, as said below
- out_grad: bfloat16 [2, 8192, 512], P('items', 'rows'), may hold values from -6 to 6
- norm_gains: float32 [3, 512], replicated, may hold values from 0.5 to 1.5
- norm_biases: float32 [3, 512], replicated, may hold values from -1.75 to 1.75
- conv_first: bfloat16 [4608, 512], replicated, may hold values from -0.09375 to 0.09375
- conv_second: bfloat16 [4608, 512], replicated, may hold values from -0.09375 to 0.09375
- conv_biases: float32 [2, 512], replicated, may hold values from -1.75 to 1.75
- embed_weight: bfloat16 [2048, 1024], replicated, may hold values from -0.125 to 0.125
- embed_bias: float32 [1024], replicated, may hold values from -1.75 to 1.75
- qkv_weight: bfloat16 [512, 1536], replicated, may hold values from -0.25 to 0.25
- qv_bias: float32 [1024], replicated, may hold values from -1.75 to 1.75
- text_weight: bfloat16 [2048, 1024], replicated, may hold values from -0.125 to 0.125
- text_bias: float32 [1024], replicated, may hold values from -1.75 to 1.75
- proj_weight: bfloat16 [512, 512], replicated, may hold values from -0.5 to 0.5
- proj_bias: float32 [512], replicated, may hold values from -1.75 to 1.75
Outputs:
- result: bfloat16 [2, 8192, 512], P('items', 'rows')
- image_grad: float32 [2, 8192, 512], P('items', 'rows')
- embedding_grad: float32 [2, 16, 2048], P('items')
- caption_grad: float32 [2, 16, 128, 2048], P('items', 'rows')
- norm_gains_grad: float32 [3, 512], replicated
- norm_biases_grad: float32 [3, 512], replicated
- conv_first_grad: float32 [4608, 512], P('rows')
- conv_second_grad: float32 [4608, 512], P('rows')
- conv_biases_grad: float32 [2, 512], replicated
- embed_weight_grad: float32 [2048, 1024], P('rows')
- embed_bias_grad: float32 [1024], replicated
- qkv_weight_grad: float32 [512, 1536], P('rows')
- qv_bias_grad: float32 [1024], replicated
- text_weight_grad: float32 [2048, 1024], P('rows')
- text_bias_grad: float32 [1024], replicated
- proj_weight_grad: float32 [512, 512], P('rows')
- proj_bias_grad: float32 [512], replicated
The draws below stay inside these ranges and needn't reach their ends.
Inputs may be any that keep to these rules, and one draw needn't show every extreme that they name: `item_of_band`: in each group the numbers start at 0 and rise by one at each new item; each item covers consecutive bands, between max(1, 4) and 8 of them, except that a group's last item may be shorter; every group's first item covers exactly 8 bands.
All inputs are finite; a program needn't handle non-finite values.
Results may differ from the reference program's by a relative error of at most 0.018.
Values may be sent and summed in bfloat16 or wider, within the bound.
A program may use at most 192 MiB of HBM per device.

```python
import jax
import jax.numpy as jnp
from jax import lax

C = 512
HEADS = 8
HEAD = 64
EMB = 2048
TEXT = 128
NORM_GROUPS = 32
W = 64
MAX_ROWS = 64
BAND = 8
PIX = 512
BUCKETS = 2
SLOTS = 16
GROUP_PIX = 8192
N_ROWS = 16


def draw_item_of_band(key, part):
    span_top = MAX_ROWS // BAND
    span_low = max(1, span_top // 2)
    drawn_spans = jax.random.randint(key, (BUCKETS, SLOTS), span_low, span_top + 1)
    column = jnp.arange(SLOTS)
    bucket_row = jnp.arange(BUCKETS)
    shortest = jnp.where(bucket_row[:, None] == 0, span_low, drawn_spans)
    lengths = jnp.where(column[None, :] == 0, span_top, shortest)
    finish = jnp.cumsum(lengths, axis=1)
    begins = finish - lengths
    counted = (begins[:, None, :] <= column[None, :, None]).astype(jnp.int32)
    return (jnp.sum(counted, axis=2) - 1).astype(jnp.int32)


def block_scale(key, extent, cuts, low, high):
    def one(axis_at, blocks):
        steps = jax.random.uniform(jax.random.fold_in(jax.random.fold_in(key, 6), axis_at), (blocks,), jnp.float32, low / len(cuts), high / len(cuts))
        return jnp.repeat(jnp.exp(steps), extent[axis_at] // blocks).reshape((-1,) + (1,) * (len(extent) - axis_at - 1))

    loudness = one(*cuts[0])
    for cut in cuts[1:]:
        loudness = loudness * one(*cut)
    return loudness


def scatter_about(own_key, extent, scale, bound, shards=(), dtype=jnp.bfloat16):
    drawn = jax.random.normal(own_key, extent, jnp.float32) * scale
    if len(shards) > 0:
        drawn = block_scale(own_key, extent, shards, -0.22, 0.18) * drawn
    return jnp.clip(drawn, min=-bound, max=bound).astype(dtype)


def setup_inputs(seed: int = 0) -> dict:
    arg_keys = jax.random.split(jax.random.key(seed), 19)
    return {
        "image": scatter_about(arg_keys[0], (BUCKETS, GROUP_PIX, C), 1.0, 6.0, ((0, 2), (1, 16))),
        "embedding": scatter_about(arg_keys[1], (BUCKETS, SLOTS, EMB), 1.0, 6.0, ((0, 2),)),
        "caption": scatter_about(arg_keys[2], (BUCKETS, SLOTS, TEXT, EMB), 1.0, 6.0, ((0, 2), (1, 16))),
        "item_of_band": draw_item_of_band(jax.random.fold_in(arg_keys[18], 71), 0),
        "out_grad": scatter_about(arg_keys[4], (BUCKETS, GROUP_PIX, C), 1.0, 6.0, ((0, 2), (1, 16))),
        "norm_gains": jnp.clip(1.0 + 0.1 * jax.random.normal(arg_keys[5], (3, C), jnp.float32), 0.5, 1.5),
        "norm_biases": scatter_about(arg_keys[6], (3, C), 0.3, 1.75, (), jnp.float32),
        "conv_first": scatter_about(arg_keys[7], (9 * C, C), (9 * C) ** -0.5, 0.09375),
        "conv_second": scatter_about(arg_keys[8], (9 * C, C), (9 * C) ** -0.5, 0.09375),
        "conv_biases": scatter_about(arg_keys[9], (2, C), 0.3, 1.75, (), jnp.float32),
        "embed_weight": scatter_about(arg_keys[10], (EMB, 2 * C), EMB ** -0.5, 0.125),
        "embed_bias": scatter_about(arg_keys[11], (2 * C,), 0.3, 1.75, (), jnp.float32),
        "qkv_weight": scatter_about(arg_keys[12], (C, 3 * C), C ** -0.5, 0.25),
        "qv_bias": scatter_about(arg_keys[13], (2 * C,), 0.3, 1.75, (), jnp.float32),
        "text_weight": scatter_about(arg_keys[14], (EMB, 2 * C), EMB ** -0.5, 0.125),
        "text_bias": scatter_about(arg_keys[15], (2 * C,), 0.3, 1.75, (), jnp.float32),
        "proj_weight": scatter_about(arg_keys[16], (C, C), (2 * C * C // (MAX_ROWS * W)) ** -0.5, 0.5),
        "proj_bias": scatter_about(arg_keys[17], (C,), 0.3, 1.75, (), jnp.float32),
    }


epsilon = 1e-05

@jax.custom_vjp
def low(v):
    return lax.optimization_barrier(v.astype(jnp.bfloat16)).astype(jnp.float32)

@jax.custom_vjp
def low_back(v):
    return v

def low_keep(v):
    return (low(v), None)

def low_pass(kept, grad):
    return (grad,)

def back_keep(v):
    return (v, None)

def back_low(kept, grad):
    return (low(grad),)
low.defvjp(low_keep, low_pass)
low_back.defvjp(back_keep, back_low)

def exact_dot(left, right):
    return jnp.dot(left, right, precision=lax.Precision.HIGHEST)

def group_stats(pixels_in, onehot, counts):
    grouped = pixels_in.reshape(pixels_in.shape[0], NORM_GROUPS, -1)
    first_sum = lax.optimization_barrier(jnp.sum(grouped, axis=2))
    second_sum = lax.optimization_barrier(jnp.sum(grouped * grouped, axis=2))
    item_first = exact_dot(onehot.T, first_sum)
    item_second = exact_dot(onehot.T, second_sum)
    group_means = item_first / counts[:, None]
    spread = item_second / counts[:, None] - group_means * group_means
    scales = lax.rsqrt(spread + epsilon)
    return (exact_dot(onehot, group_means), exact_dot(onehot, scales))

def conv_taps(image_rows, above_ok, below_ok):
    zero_row = jnp.zeros_like(image_rows[:1])
    above = jnp.concatenate([zero_row, image_rows[:-1]], axis=0) * above_ok[:, None, None]
    below = jnp.concatenate([image_rows[1:], zero_row], axis=0) * below_ok[:, None, None]
    zero_column = jnp.zeros_like(image_rows[:, :1])
    columns = []
    for row_view in (above, image_rows, below):
        left_view = jnp.concatenate([zero_column, row_view[:, :-1]], axis=1)
        right_view = jnp.concatenate([row_view[:, 1:], zero_column], axis=1)
        columns = columns + [left_view, row_view, right_view]
    return jnp.concatenate(columns, axis=2).reshape(-1, 9 * C)

def attend(queries, keys_in, values_in, query_ids, key_ids):
    block_rows = min(512, queries.shape[0])
    key_heads = keys_in.reshape(-1, HEADS, HEAD)
    value_heads = values_in.reshape(-1, HEADS, HEAD)

    def one_block(block_data):
        query_block, id_block = block_data
        query_heads = query_block.reshape(-1, HEADS, HEAD)
        scores = jnp.einsum('qhd,khd->hqk', query_heads, key_heads, precision=lax.Precision.HIGHEST) * HEAD ** (-0.5)
        scores = low_back(scores)
        allowed = id_block[:, None] == key_ids[None, :]
        scores = jnp.where(allowed[None], scores, -jnp.inf)
        row_top = lax.optimization_barrier(jnp.max(scores, axis=2, keepdims=True))
        log_total = row_top + jnp.log(lax.optimization_barrier(jnp.sum(jnp.exp(scores - row_top), axis=2, keepdims=True)))
        weights = low(jnp.exp(scores - log_total))
        return jnp.einsum('hqk,khd->qhd', weights, value_heads, precision=lax.Precision.HIGHEST).reshape(-1, C)
    outputs = lax.map(jax.checkpoint(one_block), (queries.reshape(-1, block_rows, C), query_ids.reshape(-1, block_rows)))
    return outputs.reshape(-1, C)

def group_forward(params, group_data):
    gain_rows, bias_rows, first_conv, second_conv, conv_shift, embed_matrix, embed_shift, qkv_matrix, qv_shift, text_matrix, text_shift, proj_matrix, proj_shift = params
    pixels_in, embeds, captions, band_items = group_data
    pixel_ids = jnp.repeat(band_items, PIX)
    row_ids = jnp.repeat(band_items, BAND)
    onehot = (pixel_ids[:, None] == jnp.arange(SLOTS)[None, :]).astype(jnp.float32)
    counts = jnp.maximum(lax.optimization_barrier(jnp.sum(onehot, axis=0)) * (C // NORM_GROUPS), 1.0)
    same_rows = (row_ids[1:] == row_ids[:-1]).astype(jnp.float32)
    above_ok = jnp.concatenate([jnp.zeros((1,), jnp.float32), same_rows])
    below_ok = jnp.concatenate([same_rows, jnp.zeros((1,), jnp.float32)])

    def group_norm(source, which_norm):
        group_means, scales = group_stats(source, onehot, counts)
        grouped = source.reshape(GROUP_PIX, NORM_GROUPS, -1)
        unit_value = ((grouped - group_means[:, :, None]) * scales[:, :, None]).reshape(GROUP_PIX, C)
        return unit_value * gain_rows[which_norm] + bias_rows[which_norm]

    def convolve(activation, matrix, which_bias):
        taps = conv_taps(activation.reshape(N_ROWS * BAND, W, C), above_ok, below_ok)
        return exact_dot(taps, matrix) + conv_shift[which_bias]
    act_one = low(jax.nn.silu(group_norm(pixels_in, 0)))
    hidden_one = low_back(convolve(act_one, first_conv, 0))
    embed_silu = low(jax.nn.silu(embeds))
    modulation = low_back(exact_dot(embed_silu, embed_matrix) + embed_shift)
    pixel_mod = exact_dot(onehot, modulation)
    shifted = group_norm(hidden_one, 1) * (1.0 + pixel_mod[:, :C]) + pixel_mod[:, C:]
    act_two = low(jax.nn.silu(shifted))
    middle = pixels_in + low_back(convolve(act_two, second_conv, 1))
    act_three = low(group_norm(middle, 2))
    projected = exact_dot(act_three, qkv_matrix)
    queries = low(low_back(projected[:, :C] + qv_shift[:C]))
    keys_own = low(low_back(projected[:, C:2 * C]))
    values_own = low(low_back(projected[:, 2 * C:] + qv_shift[C:]))
    text_kv = low(low_back(exact_dot(captions.reshape(-1, EMB), text_matrix) + text_shift))
    leads = jnp.concatenate([jnp.ones((1,), bool), band_items[1:] != band_items[:-1]])
    text_ids = jnp.repeat(jnp.where(leads, band_items, -1), TEXT)
    all_keys = jnp.concatenate([keys_own, text_kv[:, :C]], axis=0)
    all_values = jnp.concatenate([values_own, text_kv[:, C:]], axis=0)
    key_ids = jnp.concatenate([pixel_ids, text_ids])
    attended = low(low_back(attend(queries, all_keys, all_values, pixel_ids, key_ids)))
    return middle + exact_dot(attended, proj_matrix) + proj_shift

def reference(image, embedding, caption, item_of_band, out_grad, norm_gains, norm_biases, conv_first, conv_second, conv_biases, embed_weight, embed_bias, qkv_weight, qv_bias, text_weight, text_bias, proj_weight, proj_bias):
    floats = (image.astype(jnp.float32), embedding.astype(jnp.float32), caption.astype(jnp.float32), norm_gains, norm_biases, conv_first.astype(jnp.float32), conv_second.astype(jnp.float32), conv_biases, embed_weight.astype(jnp.float32), embed_bias, qkv_weight.astype(jnp.float32), qv_bias, text_weight.astype(jnp.float32), text_bias, proj_weight.astype(jnp.float32), proj_bias)

    def forward(*inputs):
        params = inputs[3:]

        def one_group(group_data):
            return group_forward(params, group_data)
        return lax.map(one_group, (inputs[0], inputs[1], inputs[2], item_of_band))
    result, pullback = jax.vjp(forward, *floats)
    grads = pullback(out_grad.astype(jnp.float32))
    return (result.astype(jnp.bfloat16), grads[0], grads[1], grads[2], grads[3], grads[4], grads[5], grads[6], grads[7], grads[8], grads[9], grads[10], grads[11], grads[12], grads[13], grads[14], grads[15])
```

```python
import functools

import jax
import jax.numpy as jnp
from jax import lax
from jax.experimental import pallas as pl
from jax.experimental.pallas import tpu as pltpu
from jax.sharding import PartitionSpec as P

C = 512
HEADS = 8
HEAD = 64
EMB = 2048
TEXT = 128
NORM_GROUPS = 32
W = 64
SPAN = 8


epsilon = 1e-05


def from_behind(array, axis, by):
    length = lax.axis_size(axis)
    pairs = [(i, i + by) for i in range(length) if 0 <= i + by < length]
    return lax.ppermute(array, axis, pairs)


def as_sent(array):
    return jax.tree.map(lambda a: a.astype(jnp.bfloat16) if a.dtype == jnp.float32 else a, array)


def keep_state(state):
    return state


def silu_slope(source):
    sigma = jax.nn.sigmoid(source)
    return sigma * (1.0 + source * (1.0 - sigma))


def dot_first(left_side, right_side):
    return lax.dot_general(
        left_side, right_side, (((0,), (0,)), ((), ())), preferred_element_type=jnp.float32
    )


def dot_last(left_side, right_side):
    return lax.dot_general(
        left_side, right_side, (((1,), (1,)), ((), ())), preferred_element_type=jnp.float32
    )


def head_split(source):
    return source.reshape(source.shape[0], HEADS, HEAD)


def piece_scores(query_heads, key_piece, allowed):
    key_heads = head_split(key_piece[:, :C])
    scores = jnp.einsum(
        "qhd,khd->hqk", query_heads, key_heads, preferred_element_type=jnp.float32
    ) * HEAD ** (-0.5)
    return jnp.where(allowed[None, None, :], scores, -jnp.inf)


def piece_grads(query_heads, grad_heads, log_total, row_dots, key_piece, allowed):
    scores = piece_scores(query_heads, key_piece, allowed)
    weights = jnp.exp(scores - log_total[:, :, None])
    value_heads = head_split(key_piece[:, C:])
    weight_grad = jnp.einsum(
        "qhd,khd->hqk", grad_heads, value_heads, preferred_element_type=jnp.float32
    )
    score_grad = (weights * (weight_grad - row_dots[:, :, None])).astype(jnp.bfloat16)
    outcome = []
    key_heads = head_split(key_piece[:, :C])
    query_grad = jnp.einsum(
        "hqk,khd->qhd", score_grad, key_heads, preferred_element_type=jnp.float32
    ) * HEAD ** (-0.5)
    outcome.append(query_grad.reshape(query_grad.shape[0], C))
    key_grad = jnp.einsum(
        "hqk,qhd->khd", score_grad, query_heads, preferred_element_type=jnp.float32
    ) * HEAD ** (-0.5)
    value_grad = jnp.einsum(
        "hqk,qhd->khd", weights.astype(jnp.bfloat16), grad_heads, preferred_element_type=jnp.float32
    )
    outcome.append(jnp.concatenate([key_grad.reshape(-1, C), value_grad.reshape(-1, C)], axis=1))
    return tuple(outcome)


def source_masks(band_items, source, my_item, pixels):
    slots = band_items.shape[0]
    inside = (source >= 0) & (source < slots)
    clipped = jnp.clip(source, 0, slots - 1)
    source_item = band_items[clipped]
    before_item = band_items[jnp.maximum(clipped - 1, 0)]
    same_item = inside & (source_item == my_item)
    leading = same_item & ((clipped == 0) | (before_item != source_item))
    allowed = jnp.concatenate(
        [jnp.broadcast_to(same_item, (pixels,)), jnp.broadcast_to(leading, (TEXT,))]
    )
    return (allowed, same_item)


REACH = SPAN - 1
LOG2E = 1.4426950408889634
PIX = 512


def dot(left, right):
    return jnp.dot(left, right, preferred_element_type=jnp.float32)


def reach_of(here, slots):
    first = here < SPAN
    low = jnp.maximum(jnp.where(first, 0, SPAN), here - REACH)
    high = jnp.minimum(jnp.where(first, SPAN - 1, slots - 1), here + REACH)
    return low, high


def exchange_kernel(slots, with_edges, *refs):
    if with_edges:
        tile, top, bottom, window, above, below, send_sem, recv_sem, edge_send, edge_recv = refs
    else:
        tile, window, send_sem, recv_sem = refs
    here = lax.axis_index("rows")
    low, high = reach_of(here, slots)
    offsets = [o for o in range(-REACH, REACH + 1) if o != 0]

    def reached(offset):
        return (here + offset >= low) & (here + offset <= high)

    barrier = pltpu.get_barrier_semaphore()
    for o in offsets:

        @pl.when(reached(o))
        def _(o=o):
            pl.semaphore_signal(barrier, 1, device_id={"rows": here + o})

    pl.semaphore_wait(barrier, high - low)

    def edge_copy(o):
        source, target, k = (top, below, 0) if o < 0 else (bottom, above, 1)
        return pltpu.make_async_remote_copy(
            source, target, edge_send.at[k], edge_recv.at[k], device_id={"rows": here + o}
        )

    def tile_copy(o):
        return pltpu.make_async_remote_copy(
            tile,
            window.at[REACH - o],
            send_sem.at[REACH - o],
            recv_sem.at[REACH - o],
            device_id={"rows": here + o},
        )

    if with_edges:
        for o in (-1, 1):

            @pl.when(reached(o))
            def _(o=o):
                edge_copy(o).start()

    for o in offsets:

        @pl.when(reached(o))
        def _(o=o):
            tile_copy(o).start()

        @pl.when(jnp.logical_not(reached(-o)))
        def _(o=o):
            window[REACH - o] = jnp.zeros_like(tile)

    window[REACH] = tile[...]
    if with_edges:

        @pl.when(jnp.logical_not(reached(-1)))
        def _():
            above[...] = jnp.zeros_like(above)

        @pl.when(jnp.logical_not(reached(1)))
        def _():
            below[...] = jnp.zeros_like(below)

    for o in offsets:

        @pl.when(reached(o))
        def _(o=o):
            tile_copy(o).wait_send()

        @pl.when(reached(-o))
        def _(o=o):
            tile_copy(o).wait_recv()

    if with_edges:
        for o in (-1, 1):

            @pl.when(reached(o))
            def _(o=o):
                edge_copy(o).wait_send()

            @pl.when(reached(-o))
            def _(o=o):
                edge_copy(o).wait_recv()


def exchange(ident, slots, tile, edges=None):
    vmem = pl.BlockSpec(memory_space=pltpu.VMEM)
    shapes = [jax.ShapeDtypeStruct((2 * REACH + 1,) + tile.shape, tile.dtype)]
    scratch = [pltpu.SemaphoreType.DMA((2 * REACH + 1,))] * 2
    operands = [tile]
    if edges is not None:
        shapes += [jax.ShapeDtypeStruct(e.shape, e.dtype) for e in edges]
        scratch += [pltpu.SemaphoreType.DMA((2,))] * 2
        operands += list(edges)
    return pl.pallas_call(
        functools.partial(exchange_kernel, slots, edges is not None),
        out_shape=tuple(shapes),
        in_specs=[vmem] * len(operands),
        out_specs=(vmem,) * len(shapes),
        scratch_shapes=scratch,
        compiler_params=pltpu.CompilerParams(collective_id=ident, has_side_effects=True),
        name=f"exchange_{ident}",
    )(*operands)


def swap_kernel(count, *refs):
    sources, targets = refs[:count], refs[count : 2 * count]
    send_sem, recv_sem, own_sem = refs[2 * count :]
    here = lax.axis_index("rows")
    base = (here // SPAN) * SPAN
    lane = here - base
    barrier = pltpu.get_barrier_semaphore()
    for o in range(1, SPAN):
        pl.semaphore_signal(barrier, 1, device_id={"rows": base + lax.rem(lane + o, SPAN)})
    pl.semaphore_wait(barrier, SPAN - 1)
    copies = []
    for o in range(1, SPAN):
        other = lax.rem(lane + o, SPAN)
        for k in range(count):
            copies.append(
                pltpu.make_async_remote_copy(
                    sources[k].at[other],
                    targets[k].at[lane],
                    send_sem.at[k, o],
                    recv_sem.at[k, o],
                    device_id={"rows": base + other},
                )
            )
    for copy in copies:
        copy.start()
    own = []
    for k in range(count):
        own.append(pltpu.make_async_copy(sources[k].at[lane], targets[k].at[lane], own_sem.at[k]))
        own[-1].start()
    for copy in own:
        copy.wait()
    for copy in copies:
        copy.wait()


def swap(ident, *arrays):
    anywhere = pl.BlockSpec(memory_space=pl.ANY)
    count = len(arrays)
    return pl.pallas_call(
        functools.partial(swap_kernel, count),
        out_shape=tuple(jax.ShapeDtypeStruct(a.shape, a.dtype) for a in arrays),
        in_specs=[anywhere] * count,
        out_specs=(anywhere,) * count,
        scratch_shapes=[
            pltpu.SemaphoreType.DMA((count, SPAN)),
            pltpu.SemaphoreType.DMA((count, SPAN)),
            pltpu.SemaphoreType.DMA((count,)),
        ],
        compiler_params=pltpu.CompilerParams(collective_id=ident, has_side_effects=True),
        name=f"swap_{ident}",
    )(*arrays)


def head_kernel(
    starts, ends, y_ref, t_ref, z_ref, zt_ref, xt, vx, tt, tvx, s_ref, p_ref, dk, dv, dkt, dvt
):
    low = jnp.bfloat16
    full = jnp.float32
    bands, pixels = y_ref.shape[0], y_ref.shape[1]
    text = t_ref.shape[1]
    scale = HEAD ** (-0.5)

    def widened(values, rows):
        lanes = lax.broadcasted_iota(jnp.int32, (rows, 2 * HEAD), 1)
        units = jnp.where(lanes < HEAD + 2, 1.0, 0.0).astype(low)
        return jnp.where(lanes < HEAD, values, units)

    def prepare(b, carry):
        block = y_ref[b]
        xt[b] = block.T
        vx[b] = widened(block[:, 2 * HEAD :], pixels)
        words = t_ref[b]
        tt[b] = words.T
        tvx[b] = widened(pltpu.roll(words.astype(full), HEAD, 1).astype(low), text)
        dk[b] = jnp.zeros((pixels, 2 * HEAD), full)
        dv[b] = jnp.zeros((pixels, 2 * HEAD), full)
        dkt[b] = jnp.zeros((text, 2 * HEAD), full)
        dvt[b] = jnp.zeros((text, 2 * HEAD), full)
        return carry

    lax.fori_loop(0, bands, prepare, 0)

    def one_row(columns):
        rows = lax.broadcasted_iota(jnp.int32, (16, columns), 0)
        return jnp.where(rows == 0, 1.0, 0.0).astype(low)

    ones_pixels = one_row(pixels)
    ones_text = one_row(text)
    zeros = jnp.zeros((HEAD, pixels), low)

    def query_band(i, carry):
        start, end = starts[i], ends[i]
        query_t = (xt[i, 0:HEAD, :].astype(full) * scale).astype(low)
        query_rhs = jnp.concatenate([zeros, query_t], 0)
        query_text = jnp.concatenate([query_t, zeros], 0)

        def score(j, top):
            scores = dot(y_ref[j, :, 0 : 2 * HEAD], query_rhs)
            s_ref[j] = scores
            return jnp.maximum(top, jnp.max(scores.reshape(pixels // 8, 8, pixels), axis=0))

        top = lax.fori_loop(start, end, score, jnp.full((8, pixels), -jnp.inf, full))
        scores = dot(t_ref[start], query_text)
        top = jnp.maximum(top, jnp.max(scores.reshape(text // 8, 8, pixels), axis=0))
        top = jnp.max(top, axis=0, keepdims=True)
        weights_text = jnp.exp2((scores - top) * LOG2E).astype(low)
        total = dot(jnp.concatenate([tt[start, HEAD:, :], ones_text], 0), weights_text)

        def gather(j, total):
            weights = jnp.exp2((s_ref[j] - top) * LOG2E).astype(low)
            p_ref[j] = weights
            values = jnp.concatenate([xt[j, 2 * HEAD : 3 * HEAD, :], ones_pixels], 0)
            return total + dot(values, weights)

        total = lax.fori_loop(start, end, gather, total)
        inverse = 1.0 / total[HEAD : HEAD + 1, :]
        attended = total[0:HEAD, :] * inverse
        grad = xt[i, 3 * HEAD :, :].astype(full)
        minus_dots = -jnp.sum(grad * attended, axis=0, keepdims=True) * inverse
        grad_scaled = (grad * inverse).astype(low)
        coarse = minus_dots.astype(low)
        fine = minus_dots - coarse.astype(full)
        rows = lax.broadcasted_iota(jnp.int32, (HEAD, pixels), 0)
        extra = jnp.where(rows == 0, coarse.astype(full), jnp.where(rows == 1, fine, 0.0))
        grad_rhs = jnp.concatenate([grad_scaled, extra.astype(low)], 0)
        grad_rows = jnp.concatenate([grad_scaled, zeros], 0).T
        query_rows = jnp.concatenate([query_t, zeros], 0).T

        def back(j, query_grad):
            weights = p_ref[j]
            steps = (weights.astype(full) * dot(vx[j], grad_rhs)).astype(low)
            dv[j] += dot(weights, grad_rows)
            dk[j] += dot(steps, query_rows)
            return query_grad + dot(xt[j, HEAD : 2 * HEAD, :], steps)

        steps = (weights_text.astype(full) * dot(tvx[start], grad_rhs)).astype(low)
        dvt[start] += dot(weights_text, grad_rows)
        dkt[start] += dot(steps, query_rows)
        query_grad = dot(tt[start, 0:HEAD, :], steps)
        query_grad = lax.fori_loop(start, end, back, query_grad)
        z_ref[i, :, 0 : 2 * HEAD] = jnp.concatenate(
            [attended.astype(low), (query_grad * scale).astype(low)], 0
        ).T
        return carry

    lax.fori_loop(0, bands, query_band, 0)

    def finish(b, carry):
        lanes = lax.broadcasted_iota(jnp.int32, (pixels, 2 * HEAD), 1)
        z_ref[b, :, 2 * HEAD :] = jnp.where(
            lanes < HEAD, dk[b], pltpu.roll(dv[b], HEAD, 1)
        ).astype(low)
        lanes = lax.broadcasted_iota(jnp.int32, (text, 2 * HEAD), 1)
        zt_ref[b] = jnp.where(lanes < HEAD, dkt[b], pltpu.roll(dvt[b], HEAD, 1)).astype(low)
        return carry

    lax.fori_loop(0, bands, finish, 0)


def one_head(starts, ends, pieces, words):
    bands, pixels, _ = pieces.shape
    text = words.shape[1]
    low, full = jnp.bfloat16, jnp.float32
    smem = pl.BlockSpec(memory_space=pltpu.SMEM)
    vmem = pl.BlockSpec(memory_space=pltpu.VMEM)
    return pl.pallas_call(
        head_kernel,
        out_shape=(
            jax.ShapeDtypeStruct(pieces.shape, low),
            jax.ShapeDtypeStruct(words.shape, low),
        ),
        in_specs=[smem, smem, vmem, vmem],
        out_specs=(vmem, vmem),
        scratch_shapes=[
            pltpu.VMEM((bands, 4 * HEAD, pixels), low),
            pltpu.VMEM((bands, pixels, 2 * HEAD), low),
            pltpu.VMEM((bands, 2 * HEAD, text), low),
            pltpu.VMEM((bands, text, 2 * HEAD), low),
            pltpu.VMEM((bands, pixels, pixels), full),
            pltpu.VMEM((bands, pixels, pixels), low),
            pltpu.VMEM((bands, pixels, 2 * HEAD), full),
            pltpu.VMEM((bands, pixels, 2 * HEAD), full),
            pltpu.VMEM((bands, text, 2 * HEAD), full),
            pltpu.VMEM((bands, text, 2 * HEAD), full),
        ],
        compiler_params=pltpu.CompilerParams(vmem_limit_bytes=56 << 20),
        name="one_head",
    )(starts, ends, pieces, words)


def by_head(*flat):
    split = [f.reshape(f.shape[0], HEADS, HEAD).transpose(1, 0, 2) for f in flat]
    return jnp.concatenate(split, axis=2)


def from_heads(joined, k):
    part = joined[:, :, k * HEAD : (k + 1) * HEAD]
    return part.transpose(1, 0, 2).reshape(part.shape[1], C)


def attention_by_head(band_items, position, queries, keys_values, text_kv, attended_grad):
    base = (position // SPAN) * SPAN
    items = lax.dynamic_slice_in_dim(band_items, base, SPAN)
    same = items[:, None] == items[None, :]
    column = jnp.arange(SPAN)
    starts = jnp.min(jnp.where(same, column[None, :], SPAN), axis=1).astype(jnp.int32)
    ends = jnp.max(jnp.where(same, column[None, :] + 1, 0), axis=1).astype(jnp.int32)
    pieces, words = swap(
        6,
        by_head(queries, keys_values[:, :C], keys_values[:, C:], attended_grad),
        by_head(text_kv[:, :C], text_kv[:, C:]),
    )
    outcome, outcome_text = one_head(starts, ends, pieces, words)
    outcome, outcome_text = swap(7, outcome, outcome_text)
    attended, query_grad, key_grad, value_grad = [from_heads(outcome, k) for k in range(4)]
    text_low = jnp.concatenate([from_heads(outcome_text, k) for k in range(2)], axis=1)
    return attended, query_grad, jnp.concatenate([key_grad, value_grad], axis=1), text_low


def attention_by_band(band_items, position, queries, keys_values, text_kv, attended_grad):
    my_item = band_items[position]
    pixels = queries.shape[0]
    own_allowed, own_same = source_masks(band_items, position, my_item, pixels)
    packed = jnp.concatenate([keys_values, text_kv], axis=0)
    pieces = [(0, packed, own_allowed, own_same)]
    for distance in range(1, SPAN):
        for offset in (distance, -distance):
            arrived = from_behind(packed, "rows", offset)
            allowed, same_item = source_masks(band_items, position - offset, my_item, pixels)
            pieces.append((offset, arrived, allowed, same_item))
    query_heads = head_split(queries)
    row_top = jnp.full((HEADS, pixels), -jnp.inf, jnp.float32)
    weight_sum = jnp.zeros((HEADS, pixels), jnp.float32)
    for offset, key_piece, allowed, same_item in pieces:

        def gather_scores(state, key_piece=key_piece, allowed=allowed):
            top_old, sum_old = state
            scores = piece_scores(query_heads, key_piece, allowed)
            top_new = jnp.maximum(top_old, jnp.max(scores, axis=2))
            sum_new = sum_old * jnp.exp(top_old - top_new) + jnp.sum(
                jnp.exp(scores - top_new[:, :, None]), axis=2
            )
            return (top_new, sum_new)

        row_top, weight_sum = lax.cond(same_item, gather_scores, keep_state, (row_top, weight_sum))
    log_total = row_top + jnp.log(weight_sum)
    attended = jnp.zeros((pixels, HEADS, HEAD), jnp.float32)
    for offset, key_piece, allowed, same_item in pieces:

        def add_values(totals, key_piece=key_piece, allowed=allowed):
            scores = piece_scores(query_heads, key_piece, allowed)
            weights = jnp.exp(scores - log_total[:, :, None]).astype(jnp.bfloat16)
            return totals + jnp.einsum(
                "hqk,khd->qhd",
                weights,
                head_split(key_piece[:, C:]),
                preferred_element_type=jnp.float32,
            )

        attended = lax.cond(same_item, add_values, keep_state, attended)
    attended_flat = attended.reshape(pixels, C)
    row_dots = jnp.sum(
        (attended_grad.astype(jnp.float32) * attended_flat).reshape(pixels, HEADS, HEAD), axis=2
    ).T
    grad_heads = head_split(attended_grad)
    query_grad = jnp.zeros((pixels, C), jnp.float32)
    packed_grad = jnp.zeros((pixels + TEXT, 2 * C), jnp.float32)
    zero_piece = jnp.zeros((pixels + TEXT, 2 * C), jnp.float32)
    for offset, key_piece, allowed, same_item in pieces:

        def grad_both(totals, key_piece=key_piece, allowed=allowed):
            outcome = piece_grads(query_heads, grad_heads, log_total, row_dots, key_piece, allowed)
            return (totals + outcome[0], outcome[1])

        def grad_none(totals):
            return (totals, zero_piece)

        query_grad, piece_grad = lax.cond(same_item, grad_both, grad_none, query_grad)
        if offset == 0:
            packed_grad = packed_grad + piece_grad
        else:
            packed_grad = packed_grad + from_behind(
                as_sent(piece_grad), "rows", -offset
            ).astype(jnp.float32)
    packed_low = packed_grad.astype(jnp.bfloat16)
    return (
        attended_flat.astype(jnp.bfloat16),
        query_grad.astype(jnp.bfloat16),
        packed_low[:pixels],
        packed_low[pixels:],
    )


def taps_of(rows, reverse):
    padded = rows.reshape(-1, W, rows.shape[1])
    row_list = [padded[:-2], padded[1:-1], padded[2:]]
    if reverse:
        row_list = row_list[::-1]
    zero_column = jnp.zeros_like(row_list[0][:, :1])
    views = []
    for row_view in row_list:
        left_view = jnp.concatenate([zero_column, row_view[:, :-1]], axis=1)
        right_view = jnp.concatenate([row_view[:, 1:], zero_column], axis=1)
        view_list = [left_view, row_view, right_view]
        if reverse:
            view_list = view_list[::-1]
        views = views + view_list
    return [view.reshape(-1, rows.shape[1]) for view in views]


def blocks_of(rows):
    return rows.reshape(rows.shape[0], NORM_GROUPS, -1)


def spread(values):
    return jnp.repeat(values, C // NORM_GROUPS)


def shards(
    image,
    embedding,
    caption,
    item_of_band,
    out_grad,
    norm_gains,
    norm_biases,
    conv_first,
    conv_second,
    conv_biases,
    embed_weight,
    embed_bias,
    qkv_weight,
    qv_bias,
    text_weight,
    text_bias,
    proj_weight,
    proj_bias,
):
    low = jnp.bfloat16
    full = jnp.float32
    pixels = image.shape[1]
    band_items = item_of_band[0]
    slots = band_items.shape[0]
    position = lax.axis_index("rows")
    my_item = band_items[position]
    slot_hot = (jnp.arange(slots) == my_item).astype(full)
    item_count = jnp.sum((band_items == my_item).astype(full)) * pixels * (C // NORM_GROUPS)
    reach = position + jnp.arange(-REACH, REACH + 1)
    near = (reach >= 0) & (reach < slots)
    near = near & (band_items[jnp.clip(reach, 0, slots - 1)] == my_item)
    keep = jnp.concatenate(
        [
            jnp.full((W, 1), near[REACH - 1]),
            jnp.full((pixels, 1), True),
            jnp.full((W, 1), near[REACH + 1]),
        ]
    )
    own_lead = jnp.logical_not(near[REACH - 1])

    def totals(ident, first, second, edges=None):
        sums = jnp.stack([jnp.sum(blocks_of(first), axis=(0, 2)), jnp.sum(blocks_of(second), axis=(0, 2))])
        tile = jnp.pad(sums, ((0, 6), (0, 128 - NORM_GROUPS)))
        if edges is not None:
            outcome = exchange(ident, slots, tile, (edges[:W], edges[-W:]))
        else:
            outcome = exchange(ident, slots, tile)
        summed = jnp.sum(jnp.where(near[:, None, None], outcome[0], 0.0), axis=0)
        summed = summed[:2, :NORM_GROUPS] / item_count
        return summed, outcome[1:]

    def stats(summed):
        scales = lax.rsqrt(summed[1] - summed[0] * summed[0] + epsilon)
        return spread(summed[0]), spread(scales)

    inputs = image[0].astype(full)
    summed, (above, below) = totals(0, inputs, inputs * inputs, image[0])
    means_one, scales_one = stats(summed)
    padded = jnp.concatenate([above, image[0], below]).astype(full)
    unit_padded = (padded - means_one) * scales_one
    normed_padded = unit_padded * norm_gains[0] + norm_biases[0]
    act_padded = jnp.where(keep, jax.nn.silu(normed_padded), 0.0).astype(low)
    unit_one = unit_padded[W:-W]
    normed_one = normed_padded[W:-W]
    taps_one = jnp.concatenate(taps_of(act_padded, False), axis=1)
    hidden_one = dot(taps_one, conv_first) + conv_biases[0]
    embed_silu = jax.nn.silu(embedding[0].astype(full)).astype(low)
    my_silu = dot(slot_hot.astype(low)[None], embed_silu).astype(low)
    modulation = dot(my_silu, embed_weight)[0] + embed_bias
    scale_part = modulation[:C]
    shift_part = modulation[C:]
    summed, (above, below) = totals(1, hidden_one, hidden_one * hidden_one, hidden_one)
    means_two, scales_two = stats(summed)
    padded = jnp.concatenate([above, hidden_one, below])
    unit_padded = (padded - means_two) * scales_two
    normed_padded = unit_padded * norm_gains[1] + norm_biases[1]
    shifted_padded = normed_padded * (1.0 + scale_part) + shift_part
    act_padded = jnp.where(keep, jax.nn.silu(shifted_padded), 0.0).astype(low)
    unit_two = unit_padded[W:-W]
    normed_two = normed_padded[W:-W]
    shifted = shifted_padded[W:-W]
    taps_two = jnp.concatenate(taps_of(act_padded, False), axis=1)
    middle = inputs + dot(taps_two, conv_second) + conv_biases[1]
    summed, _ = totals(2, middle, middle * middle)
    means_three, scales_three = stats(summed)
    unit_three = (middle - means_three) * scales_three
    act_three = (unit_three * norm_gains[2] + norm_biases[2]).astype(low)
    projected = dot(act_three, qkv_weight)
    queries = (projected[:, :C] + qv_bias[:C]).astype(low)
    keys_values = jnp.concatenate(
        [projected[:, C : 2 * C], projected[:, 2 * C :] + qv_bias[C:]], axis=1
    ).astype(low)
    captions = caption[0, 0]
    text_kv = lax.cond(
        own_lead,
        lambda: (dot(captions, text_weight) + text_bias).astype(low),
        lambda: jnp.zeros((TEXT, 2 * C), low),
    )
    upstream = out_grad[0]
    upstream_float = upstream.astype(full)
    attended_grad = dot_last(upstream, proj_weight).astype(low)
    attend = attention_by_head if slots == 2 * SPAN and HEADS == SPAN else attention_by_band
    attended_low, query_low, key_value_low, text_low = attend(
        band_items, position, queries, keys_values, text_kv, attended_grad
    )
    result = middle + dot(attended_low, proj_weight) + proj_bias
    proj_weight_grad = dot_first(attended_low, upstream)
    proj_bias_grad = jnp.sum(upstream_float, axis=0)
    qkv_grad = jnp.concatenate([query_low, key_value_low], axis=1)
    qkv_weight_grad = dot_first(act_three, qkv_grad)
    qv_bias_grad = jnp.sum(
        jnp.concatenate([query_low, key_value_low[:, C:]], axis=1).astype(full), axis=0
    )
    text_weight_grad = dot_first(captions, text_low)
    text_bias_grad = jnp.sum(text_low.astype(full), axis=0)
    caption_grad = dot_last(text_low, text_weight)[None, None]
    three_grad = dot_last(qkv_grad, qkv_weight)
    gain_three = jnp.sum(three_grad * unit_three, axis=0)
    bias_three = jnp.sum(three_grad, axis=0)

    def conv_back(padded, weight):
        views = jnp.stack(taps_of(padded, True))
        return jnp.einsum(
            "tpd,tcd->pc", views, weight.reshape(9, C, C), preferred_element_type=full
        )

    def norm_back(ident, grad_unit, unit_value, scales, base, with_edges=True):
        scaled = base + grad_unit * scales
        edges = jnp.concatenate([scaled, unit_value], axis=1) if with_edges else None
        summed, around = totals(ident, grad_unit, grad_unit * unit_value, edges)
        mean_grad, mean_cross = spread(summed[0]) * scales, spread(summed[1]) * scales
        if not with_edges:
            return scaled - mean_grad - unit_value * mean_cross
        both = jnp.concatenate([around[0], edges, around[1]])
        return both[:, :C] - mean_grad - both[:, C:] * mean_cross

    middle_padded = norm_back(3, three_grad * norm_gains[2], unit_three, scales_three, upstream_float)
    middle_grad = middle_padded[W:-W]
    low_padded = jnp.where(keep, middle_padded, 0.0).astype(low)
    hidden_two_low = low_padded[W:-W]
    conv_bias_two = jnp.sum(hidden_two_low.astype(full), axis=0)
    conv_second_grad = dot_first(taps_two, hidden_two_low)
    act_two_grad = conv_back(low_padded, conv_second)
    shifted_grad = act_two_grad * silu_slope(shifted)
    modulation_grad = jnp.concatenate(
        [jnp.sum(shifted_grad * normed_two, axis=0), jnp.sum(shifted_grad, axis=0)]
    )
    normed_two_grad = shifted_grad * (1.0 + scale_part)
    gain_two = jnp.sum(normed_two_grad * unit_two, axis=0)
    bias_two = jnp.sum(normed_two_grad, axis=0)
    hidden_padded = norm_back(4, normed_two_grad * norm_gains[1], unit_two, scales_two, 0.0)
    low_padded = jnp.where(keep, hidden_padded, 0.0).astype(low)
    hidden_one_low = low_padded[W:-W]
    conv_bias_one = jnp.sum(hidden_one_low.astype(full), axis=0)
    conv_first_grad = dot_first(taps_one, hidden_one_low)
    act_one_grad = conv_back(low_padded, conv_first)
    normed_one_grad = act_one_grad * silu_slope(normed_one)
    gain_one = jnp.sum(normed_one_grad * unit_one, axis=0)
    bias_one = jnp.sum(normed_one_grad, axis=0)
    image_grad = norm_back(
        5, normed_one_grad * norm_gains[0], unit_one, scales_one, middle_grad, False
    )
    group = lax.axis_index("items")
    groups = lax.axis_size("items")
    group_hot = (jnp.arange(groups) == group).astype(full)
    tables = group_hot[:, None, None] * slot_hot[None, :, None] * modulation_grad
    vectors = jnp.concatenate(
        [
            gain_one,
            gain_two,
            gain_three,
            bias_one,
            bias_two,
            bias_three,
            conv_bias_one,
            conv_bias_two,
            qv_bias_grad,
            text_bias_grad,
            proj_bias_grad,
        ]
    )
    small = jnp.concatenate([tables.reshape(-1, C), vectors.reshape(-1, C)]).astype(low)
    small = lax.psum(small, ("rows", "items"))
    tables_sum = small[: groups * slots * 2].reshape(groups, slots, 2 * C)
    vectors_sum = small[groups * slots * 2 :].astype(full)
    modulation_low = jnp.take(tables_sum, group, axis=0)
    embed_bias_grad = jnp.sum(tables_sum.astype(full), axis=(0, 1))
    row_share = EMB // lax.axis_size("rows")
    embed_weight_part = dot_first(
        lax.dynamic_slice_in_dim(embed_silu, position * row_share, row_share, 1), modulation_low
    )
    embedding_grad = dot_last(modulation_low, embed_weight) * silu_slope(embedding[0].astype(full))
    matrices = [
        lax.psum_scatter(m.astype(low), "rows", scatter_dimension=0, tiled=True)
        for m in (conv_first_grad, conv_second_grad, qkv_weight_grad, text_weight_grad, proj_weight_grad)
    ]
    matrices = [
        lax.psum(m, "items").astype(full) for m in matrices + [embed_weight_part.astype(low)]
    ]
    return (
        result.astype(low)[None],
        image_grad[None],
        embedding_grad[None],
        caption_grad,
        vectors_sum[0:3],
        vectors_sum[3:6],
        matrices[0],
        matrices[1],
        vectors_sum[6:8],
        matrices[5],
        embed_bias_grad,
        matrices[2],
        vectors_sum[8:10].reshape(-1),
        matrices[3],
        vectors_sum[10:12].reshape(-1),
        matrices[4],
        vectors_sum[12],
    )


def solution(mesh):
    in_specs = (
        P("items", "rows", None),
        P("items", None, None),
        P("items", "rows", None, None),
        P("items", None),
        P("items", "rows", None),
        P(),
        P(),
        P(),
        P(),
        P(),
        P(),
        P(),
        P(),
        P(),
        P(),
        P(),
        P(),
        P(),
    )
    out_specs = (
        P("items", "rows", None),
        P("items", "rows", None),
        P("items", None, None),
        P("items", "rows", None, None),
        P(),
        P(),
        P("rows", None),
        P("rows", None),
        P(),
        P("rows", None),
        P(),
        P("rows", None),
        P(),
        P("rows", None),
        P(),
        P("rows", None),
        P(),
    )
    return jax.shard_map(shards, mesh=mesh, in_specs=in_specs, out_specs=out_specs, check_vma=False)
```

```python
import functools

import jax
import jax.numpy as jnp
from jax import lax
from jax.experimental import pallas as pl
from jax.experimental.pallas import tpu as pltpu
from jax.sharding import PartitionSpec as P

C = 512
HEADS = 8
HEAD = 64
EMB = 2048
TEXT = 128
NORM_GROUPS = 32
W = 64
SPAN = 8


epsilon = 1e-05


def from_behind(array, axis, by):
    length = lax.axis_size(axis)
    pairs = [(i, i + by) for i in range(length) if 0 <= i + by < length]
    return lax.ppermute(array, axis, pairs)


def as_sent(array):
    return jax.tree.map(lambda a: a.astype(jnp.bfloat16) if a.dtype == jnp.float32 else a, array)


def keep_state(state):
    return state


def silu_slope(source):
    sigma = jax.nn.sigmoid(source)
    return sigma * (1.0 + source * (1.0 - sigma))


def dot_first(left_side, right_side):
    return lax.dot_general(
        left_side, right_side, (((0,), (0,)), ((), ())), preferred_element_type=jnp.float32
    )


def dot_last(left_side, right_side):
    return lax.dot_general(
        left_side, right_side, (((1,), (1,)), ((), ())), preferred_element_type=jnp.float32
    )


def head_split(source):
    return source.reshape(source.shape[0], HEADS, HEAD)


def piece_scores(query_heads, key_piece, allowed):
    key_heads = head_split(key_piece[:, :C])
    scores = jnp.einsum(
        "qhd,khd->hqk", query_heads, key_heads, preferred_element_type=jnp.float32
    ) * HEAD ** (-0.5)
    return jnp.where(allowed[None, None, :], scores, -jnp.inf)


def piece_grads(query_heads, grad_heads, log_total, row_dots, key_piece, allowed):
    scores = piece_scores(query_heads, key_piece, allowed)
    weights = jnp.exp(scores - log_total[:, :, None])
    value_heads = head_split(key_piece[:, C:])
    weight_grad = jnp.einsum(
        "qhd,khd->hqk", grad_heads, value_heads, preferred_element_type=jnp.float32
    )
    score_grad = (weights * (weight_grad - row_dots[:, :, None])).astype(jnp.bfloat16)
    outcome = []
    key_heads = head_split(key_piece[:, :C])
    query_grad = jnp.einsum(
        "hqk,khd->qhd", score_grad, key_heads, preferred_element_type=jnp.float32
    ) * HEAD ** (-0.5)
    outcome.append(query_grad.reshape(query_grad.shape[0], C))
    key_grad = jnp.einsum(
        "hqk,qhd->khd", score_grad, query_heads, preferred_element_type=jnp.float32
    ) * HEAD ** (-0.5)
    value_grad = jnp.einsum(
        "hqk,qhd->khd", weights.astype(jnp.bfloat16), grad_heads, preferred_element_type=jnp.float32
    )
    outcome.append(jnp.concatenate([key_grad.reshape(-1, C), value_grad.reshape(-1, C)], axis=1))
    return tuple(outcome)


def source_masks(band_items, source, my_item, pixels):
    slots = band_items.shape[0]
    inside = (source >= 0) & (source < slots)
    clipped = jnp.clip(source, 0, slots - 1)
    source_item = band_items[clipped]
    before_item = band_items[jnp.maximum(clipped - 1, 0)]
    same_item = inside & (source_item == my_item)
    leading = same_item & ((clipped == 0) | (before_item != source_item))
    allowed = jnp.concatenate(
        [jnp.broadcast_to(same_item, (pixels,)), jnp.broadcast_to(leading, (TEXT,))]
    )
    return (allowed, same_item)


REACH = SPAN - 1
LOG2E = 1.4426950408889634
PIX = 512


def dot(left, right):
    return jnp.dot(left, right, preferred_element_type=jnp.float32)


def reach_of(here, slots):
    first = here < SPAN
    low = jnp.maximum(jnp.where(first, 0, SPAN), here - REACH)
    high = jnp.minimum(jnp.where(first, SPAN - 1, slots - 1), here + REACH)
    return low, high


def exchange_kernel(slots, with_edges, *refs):
    if with_edges:
        tile, top, bottom, window, above, below, send_sem, recv_sem, edge_send, edge_recv = refs
    else:
        tile, window, send_sem, recv_sem = refs
    here = lax.axis_index("rows")
    low, high = reach_of(here, slots)
    offsets = [o for o in range(-REACH, REACH + 1) if o != 0]

    def reached(offset):
        return (here + offset >= low) & (here + offset <= high)

    barrier = pltpu.get_barrier_semaphore()
    for o in offsets:

        @pl.when(reached(o))
        def _(o=o):
            pl.semaphore_signal(barrier, 1, device_id={"rows": here + o})

    pl.semaphore_wait(barrier, high - low)

    def edge_copy(o):
        source, target, k = (top, below, 0) if o < 0 else (bottom, above, 1)
        return pltpu.make_async_remote_copy(
            source, target, edge_send.at[k], edge_recv.at[k], device_id={"rows": here + o}
        )

    def tile_copy(o):
        return pltpu.make_async_remote_copy(
            tile,
            window.at[REACH - o],
            send_sem.at[REACH - o],
            recv_sem.at[REACH - o],
            device_id={"rows": here + o},
        )

    if with_edges:
        for o in (-1, 1):

            @pl.when(reached(o))
            def _(o=o):
                edge_copy(o).start()

    for o in offsets:

        @pl.when(reached(o))
        def _(o=o):
            tile_copy(o).start()

        @pl.when(jnp.logical_not(reached(-o)))
        def _(o=o):
            window[REACH - o] = jnp.zeros_like(tile)

    window[REACH] = tile[...]
    if with_edges:

        @pl.when(jnp.logical_not(reached(-1)))
        def _():
            above[...] = jnp.zeros_like(above)

        @pl.when(jnp.logical_not(reached(1)))
        def _():
            below[...] = jnp.zeros_like(below)

    for o in offsets:

        @pl.when(reached(o))
        def _(o=o):
            tile_copy(o).wait_send()

        @pl.when(reached(-o))
        def _(o=o):
            tile_copy(o).wait_recv()

    if with_edges:
        for o in (-1, 1):

            @pl.when(reached(o))
            def _(o=o):
                edge_copy(o).wait_send()

            @pl.when(reached(-o))
            def _(o=o):
                edge_copy(o).wait_recv()


def exchange(ident, slots, tile, edges=None):
    vmem = pl.BlockSpec(memory_space=pltpu.VMEM)
    shapes = [jax.ShapeDtypeStruct((2 * REACH + 1,) + tile.shape, tile.dtype)]
    scratch = [pltpu.SemaphoreType.DMA((2 * REACH + 1,))] * 2
    operands = [tile]
    if edges is not None:
        shapes += [jax.ShapeDtypeStruct(e.shape, e.dtype) for e in edges]
        scratch += [pltpu.SemaphoreType.DMA((2,))] * 2
        operands += list(edges)
    return pl.pallas_call(
        functools.partial(exchange_kernel, slots, edges is not None),
        out_shape=tuple(shapes),
        in_specs=[vmem] * len(operands),
        out_specs=(vmem,) * len(shapes),
        scratch_shapes=scratch,
        compiler_params=pltpu.CompilerParams(collective_id=ident, has_side_effects=True),
        name=f"exchange_{ident}",
    )(*operands)


def swap_kernel(count, *refs):
    sources, targets = refs[:count], refs[count : 2 * count]
    send_sem, recv_sem, own_sem = refs[2 * count :]
    here = lax.axis_index("rows")
    base = (here // SPAN) * SPAN
    lane = here - base
    barrier = pltpu.get_barrier_semaphore()
    for o in range(1, SPAN):
        pl.semaphore_signal(barrier, 1, device_id={"rows": base + lax.rem(lane + o, SPAN)})
    pl.semaphore_wait(barrier, SPAN - 1)
    copies = []
    for o in range(1, SPAN):
        other = lax.rem(lane + o, SPAN)
        for k in range(count):
            copies.append(
                pltpu.make_async_remote_copy(
                    sources[k].at[other],
                    targets[k].at[lane],
                    send_sem.at[k, o],
                    recv_sem.at[k, o],
                    device_id={"rows": base + other},
                )
            )
    for copy in copies:
        copy.start()
    own = []
    for k in range(count):
        own.append(pltpu.make_async_copy(sources[k].at[lane], targets[k].at[lane], own_sem.at[k]))
        own[-1].start()
    for copy in own:
        copy.wait()
    for copy in copies:
        copy.wait()


def swap(ident, *arrays):
    anywhere = pl.BlockSpec(memory_space=pl.ANY)
    count = len(arrays)
    return pl.pallas_call(
        functools.partial(swap_kernel, count),
        out_shape=tuple(jax.ShapeDtypeStruct(a.shape, a.dtype) for a in arrays),
        in_specs=[anywhere] * count,
        out_specs=(anywhere,) * count,
        scratch_shapes=[
            pltpu.SemaphoreType.DMA((count, SPAN)),
            pltpu.SemaphoreType.DMA((count, SPAN)),
            pltpu.SemaphoreType.DMA((count,)),
        ],
        compiler_params=pltpu.CompilerParams(collective_id=ident, has_side_effects=True),
        name=f"swap_{ident}",
    )(*arrays)


def head_kernel(
    starts, ends, y_ref, t_ref, z_ref, zt_ref, xt, vx, tt, tvx, s_ref, p_ref, dk, dv, dkt, dvt
):
    low = jnp.bfloat16
    full = jnp.float32
    bands, pixels = y_ref.shape[0], y_ref.shape[1]
    text = t_ref.shape[1]
    scale = HEAD ** (-0.5)

    def widened(values, rows):
        lanes = lax.broadcasted_iota(jnp.int32, (rows, 2 * HEAD), 1)
        units = jnp.where(lanes < HEAD + 2, 1.0, 0.0).astype(low)
        return jnp.where(lanes < HEAD, values, units)

    def prepare(b, carry):
        block = y_ref[b]
        xt[b] = block.T
        vx[b] = widened(block[:, 2 * HEAD :], pixels)
        words = t_ref[b]
        tt[b] = words.T
        tvx[b] = widened(pltpu.roll(words.astype(full), HEAD, 1).astype(low), text)
        dk[b] = jnp.zeros((pixels, 2 * HEAD), full)
        dv[b] = jnp.zeros((pixels, 2 * HEAD), full)
        dkt[b] = jnp.zeros((text, 2 * HEAD), full)
        dvt[b] = jnp.zeros((text, 2 * HEAD), full)
        return carry

    lax.fori_loop(0, bands, prepare, 0)

    def one_row(columns):
        rows = lax.broadcasted_iota(jnp.int32, (16, columns), 0)
        return jnp.where(rows == 0, 1.0, 0.0).astype(low)

    ones_pixels = one_row(pixels)
    ones_text = one_row(text)
    zeros = jnp.zeros((HEAD, pixels), low)

    def query_band(i, carry):
        start, end = starts[i], ends[i]
        query_t = (xt[i, 0:HEAD, :].astype(full) * scale).astype(low)
        query_rhs = jnp.concatenate([zeros, query_t], 0)
        query_text = jnp.concatenate([query_t, zeros], 0)

        def score(j, top):
            scores = dot(y_ref[j, :, 0 : 2 * HEAD], query_rhs)
            s_ref[j] = scores
            return jnp.maximum(top, jnp.max(scores.reshape(pixels // 8, 8, pixels), axis=0))

        top = lax.fori_loop(start, end, score, jnp.full((8, pixels), -jnp.inf, full))
        scores = dot(t_ref[start], query_text)
        top = jnp.maximum(top, jnp.max(scores.reshape(text // 8, 8, pixels), axis=0))
        top = jnp.max(top, axis=0, keepdims=True)
        weights_text = jnp.exp2((scores - top) * LOG2E).astype(low)
        total = dot(jnp.concatenate([tt[start, HEAD:, :], ones_text], 0), weights_text)

        def gather(j, total):
            weights = jnp.exp2((s_ref[j] - top) * LOG2E).astype(low)
            p_ref[j] = weights
            values = jnp.concatenate([xt[j, 2 * HEAD : 3 * HEAD, :], ones_pixels], 0)
            return total + dot(values, weights)

        total = lax.fori_loop(start, end, gather, total)
        inverse = 1.0 / total[HEAD : HEAD + 1, :]
        attended = total[0:HEAD, :] * inverse
        grad = xt[i, 3 * HEAD :, :].astype(full)
        minus_dots = -jnp.sum(grad * attended, axis=0, keepdims=True) * inverse
        grad_scaled = (grad * inverse).astype(low)
        coarse = minus_dots.astype(low)
        fine = minus_dots - coarse.astype(full)
        rows = lax.broadcasted_iota(jnp.int32, (HEAD, pixels), 0)
        extra = jnp.where(rows == 0, coarse.astype(full), jnp.where(rows == 1, fine, 0.0))
        grad_rhs = jnp.concatenate([grad_scaled, extra.astype(low)], 0)
        grad_rows = jnp.concatenate([grad_scaled, zeros], 0).T
        query_rows = jnp.concatenate([query_t, zeros], 0).T

        def back(j, query_grad):
            weights = p_ref[j]
            steps = (weights.astype(full) * dot(vx[j], grad_rhs)).astype(low)
            dv[j] += dot(weights, grad_rows)
            dk[j] += dot(steps, query_rows)
            return query_grad + dot(xt[j, HEAD : 2 * HEAD, :], steps)

        steps = (weights_text.astype(full) * dot(tvx[start], grad_rhs)).astype(low)
        dvt[start] += dot(weights_text, grad_rows)
        dkt[start] += dot(steps, query_rows)
        query_grad = dot(tt[start, 0:HEAD, :], steps)
        query_grad = lax.fori_loop(start, end, back, query_grad)
        z_ref[i, :, 0 : 2 * HEAD] = jnp.concatenate(
            [attended.astype(low), (query_grad * scale).astype(low)], 0
        ).T
        return carry

    lax.fori_loop(0, bands, query_band, 0)

    def finish(b, carry):
        lanes = lax.broadcasted_iota(jnp.int32, (pixels, 2 * HEAD), 1)
        z_ref[b, :, 2 * HEAD :] = jnp.where(
            lanes < HEAD, dk[b], pltpu.roll(dv[b], HEAD, 1)
        ).astype(low)
        lanes = lax.broadcasted_iota(jnp.int32, (text, 2 * HEAD), 1)
        zt_ref[b] = jnp.where(lanes < HEAD, dkt[b], pltpu.roll(dvt[b], HEAD, 1)).astype(low)
        return carry

    lax.fori_loop(0, bands, finish, 0)


def one_head(starts, ends, pieces, words):
    bands, pixels, _ = pieces.shape
    text = words.shape[1]
    low, full = jnp.bfloat16, jnp.float32
    smem = pl.BlockSpec(memory_space=pltpu.SMEM)
    vmem = pl.BlockSpec(memory_space=pltpu.VMEM)
    return pl.pallas_call(
        head_kernel,
        out_shape=(
            jax.ShapeDtypeStruct(pieces.shape, low),
            jax.ShapeDtypeStruct(words.shape, low),
        ),
        in_specs=[smem, smem, vmem, vmem],
        out_specs=(vmem, vmem),
        scratch_shapes=[
            pltpu.VMEM((bands, 4 * HEAD, pixels), low),
            pltpu.VMEM((bands, pixels, 2 * HEAD), low),
            pltpu.VMEM((bands, 2 * HEAD, text), low),
            pltpu.VMEM((bands, text, 2 * HEAD), low),
            pltpu.VMEM((bands, pixels, pixels), full),
            pltpu.VMEM((bands, pixels, pixels), low),
            pltpu.VMEM((bands, pixels, 2 * HEAD), full),
            pltpu.VMEM((bands, pixels, 2 * HEAD), full),
            pltpu.VMEM((bands, text, 2 * HEAD), full),
            pltpu.VMEM((bands, text, 2 * HEAD), full),
        ],
        compiler_params=pltpu.CompilerParams(vmem_limit_bytes=56 << 20),
        name="one_head",
    )(starts, ends, pieces, words)


def by_head(*flat):
    split = [f.reshape(f.shape[0], HEADS, HEAD).transpose(1, 0, 2) for f in flat]
    return jnp.concatenate(split, axis=2)


def from_heads(joined, k):
    part = joined[:, :, k * HEAD : (k + 1) * HEAD]
    return part.transpose(1, 0, 2).reshape(part.shape[1], C)


def attention_by_head(band_items, position, queries, keys_values, text_kv, attended_grad):
    base = (position // SPAN) * SPAN
    items = lax.dynamic_slice_in_dim(band_items, base, SPAN)
    same = items[:, None] == items[None, :]
    column = jnp.arange(SPAN)
    starts = jnp.min(jnp.where(same, column[None, :], SPAN), axis=1).astype(jnp.int32)
    ends = jnp.max(jnp.where(same, column[None, :] + 1, 0), axis=1).astype(jnp.int32)
    pieces, words = swap(
        6,
        by_head(queries, keys_values[:, :C], keys_values[:, C:], attended_grad),
        by_head(text_kv[:, :C], text_kv[:, C:]),
    )
    outcome, outcome_text = one_head(starts, ends, pieces, words)
    outcome, outcome_text = swap(7, outcome, outcome_text)
    attended, query_grad, key_grad, value_grad = [from_heads(outcome, k) for k in range(4)]
    text_low = jnp.concatenate([from_heads(outcome_text, k) for k in range(2)], axis=1)
    return attended, query_grad, jnp.concatenate([key_grad, value_grad], axis=1), text_low


def attention_by_band(band_items, position, queries, keys_values, text_kv, attended_grad):
    my_item = band_items[position]
    pixels = queries.shape[0]
    own_allowed, own_same = source_masks(band_items, position, my_item, pixels)
    packed = jnp.concatenate([keys_values, text_kv], axis=0)
    pieces = [(0, packed, own_allowed, own_same)]
    for distance in range(1, SPAN):
        for offset in (distance, -distance):
            arrived = from_behind(packed, "rows", offset)
            allowed, same_item = source_masks(band_items, position - offset, my_item, pixels)
            pieces.append((offset, arrived, allowed, same_item))
    query_heads = head_split(queries)
    row_top = jnp.full((HEADS, pixels), -jnp.inf, jnp.float32)
    weight_sum = jnp.zeros((HEADS, pixels), jnp.float32)
    for offset, key_piece, allowed, same_item in pieces:

        def gather_scores(state, key_piece=key_piece, allowed=allowed):
            top_old, sum_old = state
            scores = piece_scores(query_heads, key_piece, allowed)
            top_new = jnp.maximum(top_old, jnp.max(scores, axis=2))
            sum_new = sum_old * jnp.exp(top_old - top_new) + jnp.sum(
                jnp.exp(scores - top_new[:, :, None]), axis=2
            )
            return (top_new, sum_new)

        row_top, weight_sum = lax.cond(same_item, gather_scores, keep_state, (row_top, weight_sum))
    log_total = row_top + jnp.log(weight_sum)
    attended = jnp.zeros((pixels, HEADS, HEAD), jnp.float32)
    for offset, key_piece, allowed, same_item in pieces:

        def add_values(totals, key_piece=key_piece, allowed=allowed):
            scores = piece_scores(query_heads, key_piece, allowed)
            weights = jnp.exp(scores - log_total[:, :, None]).astype(jnp.bfloat16)
            return totals + jnp.einsum(
                "hqk,khd->qhd",
                weights,
                head_split(key_piece[:, C:]),
                preferred_element_type=jnp.float32,
            )

        attended = lax.cond(same_item, add_values, keep_state, attended)
    attended_flat = attended.reshape(pixels, C)
    row_dots = jnp.sum(
        (attended_grad.astype(jnp.float32) * attended_flat).reshape(pixels, HEADS, HEAD), axis=2
    ).T
    grad_heads = head_split(attended_grad)
    query_grad = jnp.zeros((pixels, C), jnp.float32)
    packed_grad = jnp.zeros((pixels + TEXT, 2 * C), jnp.float32)
    zero_piece = jnp.zeros((pixels + TEXT, 2 * C), jnp.float32)
    for offset, key_piece, allowed, same_item in pieces:

        def grad_both(totals, key_piece=key_piece, allowed=allowed):
            outcome = piece_grads(query_heads, grad_heads, log_total, row_dots, key_piece, allowed)
            return (totals + outcome[0], outcome[1])

        def grad_none(totals):
            return (totals, zero_piece)

        query_grad, piece_grad = lax.cond(same_item, grad_both, grad_none, query_grad)
        if offset == 0:
            packed_grad = packed_grad + piece_grad
        else:
            packed_grad = packed_grad + from_behind(
                as_sent(piece_grad), "rows", -offset
            ).astype(jnp.float32)
    packed_low = packed_grad.astype(jnp.bfloat16)
    return (
        attended_flat.astype(jnp.bfloat16),
        query_grad.astype(jnp.bfloat16),
        packed_low[:pixels],
        packed_low[pixels:],
    )


def taps_of(rows, reverse):
    padded = rows.reshape(-1, W, rows.shape[1])
    row_list = [padded[:-2], padded[1:-1], padded[2:]]
    if reverse:
        row_list = row_list[::-1]
    zero_column = jnp.zeros_like(row_list[0][:, :1])
    views = []
    for row_view in row_list:
        left_view = jnp.concatenate([zero_column, row_view[:, :-1]], axis=1)
        right_view = jnp.concatenate([row_view[:, 1:], zero_column], axis=1)
        view_list = [left_view, row_view, right_view]
        if reverse:
            view_list = view_list[::-1]
        views = views + view_list
    return [view.reshape(-1, rows.shape[1]) for view in views]


ROW_DIMS = ("far", "near", "side", "core")


def fold_kernel(orders, shapes, *refs):
    count = len(orders)
    grads, refs = refs[:count], refs[count:]
    small, shard, refs = refs[0], refs[1], refs[2:]
    outs, refs = refs[:count], refs[count:]
    small_out, shard_out, refs = refs[0], refs[1], refs[2:]
    mine, refs = refs[:count], refs[count:]
    steps = len(ROW_DIMS) + 1
    arrived = [refs[k * steps : (k + 1) * steps] for k in range(count)]
    refs = refs[count * steps :]
    both, refs = refs[:count], refs[count:]
    small_parts, refs = refs[:steps], refs[steps:]
    send_sem, recv_sem, own_sem = refs
    row = lax.axis_index("rows")
    group = lax.axis_index("items")
    place = {d: (row // 2 ** (len(ROW_DIMS) - 1 - i)) % 2 for i, d in enumerate(ROW_DIMS)}
    place["group"] = group
    partner = {
        d: {"rows": row + (1 - 2 * place[d]) * 2 ** (len(ROW_DIMS) - 1 - i)}
        for i, d in enumerate(ROW_DIMS)
    }
    partner["group"] = {"items": 1 - group}
    barrier = pltpu.get_barrier_semaphore()
    for d in place:
        pl.semaphore_signal(barrier, 1, device_id=partner[d])
    pl.semaphore_wait(barrier, len(place))

    def remote(source, target, k, step, d):
        return pltpu.make_async_remote_copy(
            source, target, send_sem.at[k, step], recv_sem.at[k, step], device_id=partner[d]
        )

    def at(ref, axis, index):
        return ref.at[(slice(None),) * axis + (index,)]

    started = []
    left = []
    waiting = []
    own = []
    for k, order in enumerate(orders):
        dims = list(ROW_DIMS) + ["group"]
        axis = dims.index(order[0])
        waiting.append(
            remote(at(grads[k], axis, 1 - place[order[0]]), arrived[k][0], k, 0, order[0])
        )
        waiting[k].start()
        own.append(
            pltpu.make_async_copy(at(grads[k], axis, place[order[0]]), mine[k], own_sem.at[k])
        )
        own[k].start()
        dims.pop(axis)
        left.append(dims)
    shard_copy = remote(shard, shard_out, count + 1, 0, "group")
    shard_copy.start()
    small_dims = ("core", "side", "group", "near", "far")
    small_copy = remote(small, small_parts[0], count, 0, small_dims[0])
    small_copy.start()
    small_out[...] = small[...]
    for k in range(count):
        own[k].wait()
    current = list(mine)
    for step in range(steps):
        for k, order in enumerate(orders):
            waiting[k].wait()
            landed = arrived[k][step]
            if step == 0:
                here = current[k]
            else:
                here = current[k]
            lead = landed.shape[:-2]
            pieces = 1
            for n in lead:
                pieces *= n

            def add(i, carry, landed=landed, here=here, lead=lead):
                index = []
                for n in reversed(lead):
                    index.insert(0, i % n)
                    i = i // n
                index = tuple(index)
                total = landed[index].astype(jnp.float32) + here[index].astype(jnp.float32)
                landed[index] = total.astype(landed.dtype)
                return carry

            lax.fori_loop(0, pieces, add, 0)
            if step + 1 < steps:
                d = order[step + 1]
                axis = left[k].index(d)
                waiting[k] = remote(
                    at(landed, axis, 1 - place[d]), arrived[k][step + 1], k, step + 1, d
                )
                waiting[k].start()
                current[k] = at(landed, axis, place[d])
                left[k].pop(axis)
            else:
                both[k][group] = landed[...]
                waiting[k] = remote(landed, both[k].at[group], k, steps, "group")
                waiting[k].start()
        small_copy.wait()
        small_out[...] = small_out[...] + small_parts[step][...]
        if step + 1 < steps:
            started.append(None)
            small_copy = remote(
                small_out, small_parts[step + 1], count, step + 1, small_dims[step + 1]
            )
            small_copy.start()
    for k in range(count):
        waiting[k].wait()
        outs[k][...] = both[k][...].astype(jnp.float32)
    shard_copy.wait()


def fold(ident, orders, grads, small, shard):
    low, full = jnp.bfloat16, jnp.float32
    steps = len(ROW_DIMS) + 1
    vmem = pl.BlockSpec(memory_space=pltpu.VMEM)
    anywhere = pl.BlockSpec(memory_space=pl.ANY)
    shapes = []
    cut = []
    for g in grads:
        rows = g.shape[0] // 2**steps
        cut.append(g.reshape((2,) * steps + (rows, g.shape[1])))
        shapes.append((rows, g.shape[1]))
    count = len(grads)
    halves = [
        [pltpu.VMEM((2,) * (steps - 1 - i) + shape, low) for i in range(steps)] for shape in shapes
    ]
    outcome = pl.pallas_call(
        functools.partial(fold_kernel, orders, shapes),
        out_shape=tuple(jax.ShapeDtypeStruct((2,) + s, full) for s in shapes)
        + (
            jax.ShapeDtypeStruct(small.shape, small.dtype),
            jax.ShapeDtypeStruct(shard.shape, shard.dtype),
        ),
        in_specs=[anywhere] * count + [vmem, vmem],
        out_specs=(vmem,) * (count + 2),
        scratch_shapes=[h[0] for h in halves]
        + [buffer for h in halves for buffer in h]
        + [pltpu.VMEM((2,) + s, low) for s in shapes]
        + [pltpu.VMEM(small.shape, small.dtype)] * steps
        + [
            pltpu.SemaphoreType.DMA((count + 2, steps + 1)),
            pltpu.SemaphoreType.DMA((count + 2, steps + 1)),
            pltpu.SemaphoreType.DMA((count,)),
        ],
        compiler_params=pltpu.CompilerParams(
            collective_id=ident, has_side_effects=True, vmem_limit_bytes=56 << 20
        ),
        name=f"fold_{ident}",
    )(*cut, small, shard)
    summed = [o.reshape(-1, o.shape[-1]) for o in outcome[:count]]
    return summed, outcome[count], outcome[count + 1]


def blocks_of(rows):
    return rows.reshape(rows.shape[0], NORM_GROUPS, -1)


def spread(values):
    return jnp.repeat(values, C // NORM_GROUPS)


def shards(
    image,
    embedding,
    caption,
    item_of_band,
    out_grad,
    norm_gains,
    norm_biases,
    conv_first,
    conv_second,
    conv_biases,
    embed_weight,
    embed_bias,
    qkv_weight,
    qv_bias,
    text_weight,
    text_bias,
    proj_weight,
    proj_bias,
):
    low = jnp.bfloat16
    full = jnp.float32
    pixels = image.shape[1]
    band_items = item_of_band[0]
    slots = band_items.shape[0]
    position = lax.axis_index("rows")
    my_item = band_items[position]
    slot_hot = (jnp.arange(slots) == my_item).astype(full)
    item_count = jnp.sum((band_items == my_item).astype(full)) * pixels * (C // NORM_GROUPS)
    reach = position + jnp.arange(-REACH, REACH + 1)
    near = (reach >= 0) & (reach < slots)
    near = near & (band_items[jnp.clip(reach, 0, slots - 1)] == my_item)
    keep = jnp.concatenate(
        [
            jnp.full((W, 1), near[REACH - 1]),
            jnp.full((pixels, 1), True),
            jnp.full((W, 1), near[REACH + 1]),
        ]
    )
    own_lead = jnp.logical_not(near[REACH - 1])

    def totals(ident, first, second, edges=None):
        sums = jnp.stack([jnp.sum(blocks_of(first), axis=(0, 2)), jnp.sum(blocks_of(second), axis=(0, 2))])
        tile = jnp.pad(sums, ((0, 6), (0, 128 - NORM_GROUPS)))
        if edges is not None:
            outcome = exchange(ident, slots, tile, (edges[:W], edges[-W:]))
        else:
            outcome = exchange(ident, slots, tile)
        summed = jnp.sum(jnp.where(near[:, None, None], outcome[0], 0.0), axis=0)
        summed = summed[:2, :NORM_GROUPS] / item_count
        return summed, outcome[1:]

    def stats(summed):
        scales = lax.rsqrt(summed[1] - summed[0] * summed[0] + epsilon)
        return spread(summed[0]), spread(scales)

    inputs = image[0].astype(full)
    summed, (above, below) = totals(0, inputs, inputs * inputs, image[0])
    means_one, scales_one = stats(summed)
    padded = jnp.concatenate([above, image[0], below]).astype(full)
    unit_padded = (padded - means_one) * scales_one
    normed_padded = unit_padded * norm_gains[0] + norm_biases[0]
    act_padded = jnp.where(keep, jax.nn.silu(normed_padded), 0.0).astype(low)
    unit_one = unit_padded[W:-W]
    normed_one = normed_padded[W:-W]
    taps_one = jnp.concatenate(taps_of(act_padded, False), axis=1)
    hidden_one = dot(taps_one, conv_first) + conv_biases[0]
    embed_silu = jax.nn.silu(embedding[0].astype(full)).astype(low)
    my_silu = dot(slot_hot.astype(low)[None], embed_silu).astype(low)
    modulation = dot(my_silu, embed_weight)[0] + embed_bias
    scale_part = modulation[:C]
    shift_part = modulation[C:]
    summed, (above, below) = totals(1, hidden_one, hidden_one * hidden_one, hidden_one)
    means_two, scales_two = stats(summed)
    padded = jnp.concatenate([above, hidden_one, below])
    unit_padded = (padded - means_two) * scales_two
    normed_padded = unit_padded * norm_gains[1] + norm_biases[1]
    shifted_padded = normed_padded * (1.0 + scale_part) + shift_part
    act_padded = jnp.where(keep, jax.nn.silu(shifted_padded), 0.0).astype(low)
    unit_two = unit_padded[W:-W]
    normed_two = normed_padded[W:-W]
    shifted = shifted_padded[W:-W]
    taps_two = jnp.concatenate(taps_of(act_padded, False), axis=1)
    middle = inputs + dot(taps_two, conv_second) + conv_biases[1]
    summed, _ = totals(2, middle, middle * middle)
    means_three, scales_three = stats(summed)
    unit_three = (middle - means_three) * scales_three
    act_three = (unit_three * norm_gains[2] + norm_biases[2]).astype(low)
    projected = dot(act_three, qkv_weight)
    queries = (projected[:, :C] + qv_bias[:C]).astype(low)
    keys_values = jnp.concatenate(
        [projected[:, C : 2 * C], projected[:, 2 * C :] + qv_bias[C:]], axis=1
    ).astype(low)
    captions = caption[0, 0]
    text_kv = lax.cond(
        own_lead,
        lambda: (dot(captions, text_weight) + text_bias).astype(low),
        lambda: jnp.zeros((TEXT, 2 * C), low),
    )
    upstream = out_grad[0]
    upstream_float = upstream.astype(full)
    attended_grad = dot_last(upstream, proj_weight).astype(low)
    attend = attention_by_head if slots == 2 * SPAN and HEADS == SPAN else attention_by_band
    attended_low, query_low, key_value_low, text_low = attend(
        band_items, position, queries, keys_values, text_kv, attended_grad
    )
    result = middle + dot(attended_low, proj_weight) + proj_bias
    proj_weight_grad = dot_first(attended_low, upstream)
    proj_bias_grad = jnp.sum(upstream_float, axis=0)
    qkv_grad = jnp.concatenate([query_low, key_value_low], axis=1)
    qkv_weight_grad = dot_first(act_three, qkv_grad)
    qv_bias_grad = jnp.sum(
        jnp.concatenate([query_low, key_value_low[:, C:]], axis=1).astype(full), axis=0
    )
    text_weight_grad = dot_first(captions, text_low)
    text_bias_grad = jnp.sum(text_low.astype(full), axis=0)
    caption_grad = dot_last(text_low, text_weight)[None, None]
    three_grad = dot_last(qkv_grad, qkv_weight)
    gain_three = jnp.sum(three_grad * unit_three, axis=0)
    bias_three = jnp.sum(three_grad, axis=0)

    def conv_back(padded, weight):
        views = jnp.stack(taps_of(padded, True))
        return jnp.einsum(
            "tpd,tcd->pc", views, weight.reshape(9, C, C), preferred_element_type=full
        )

    def norm_back(ident, grad_unit, unit_value, scales, base, with_edges=True):
        scaled = base + grad_unit * scales
        edges = jnp.concatenate([scaled, unit_value], axis=1) if with_edges else None
        summed, around = totals(ident, grad_unit, grad_unit * unit_value, edges)
        mean_grad, mean_cross = spread(summed[0]) * scales, spread(summed[1]) * scales
        if not with_edges:
            return scaled - mean_grad - unit_value * mean_cross
        both = jnp.concatenate([around[0], edges, around[1]])
        return both[:, :C] - mean_grad - both[:, C:] * mean_cross

    middle_padded = norm_back(3, three_grad * norm_gains[2], unit_three, scales_three, upstream_float)
    middle_grad = middle_padded[W:-W]
    low_padded = jnp.where(keep, middle_padded, 0.0).astype(low)
    hidden_two_low = low_padded[W:-W]
    conv_bias_two = jnp.sum(hidden_two_low.astype(full), axis=0)
    conv_second_grad = dot_first(taps_two, hidden_two_low)
    act_two_grad = conv_back(low_padded, conv_second)
    shifted_grad = act_two_grad * silu_slope(shifted)
    modulation_grad = jnp.concatenate(
        [jnp.sum(shifted_grad * normed_two, axis=0), jnp.sum(shifted_grad, axis=0)]
    )
    normed_two_grad = shifted_grad * (1.0 + scale_part)
    gain_two = jnp.sum(normed_two_grad * unit_two, axis=0)
    bias_two = jnp.sum(normed_two_grad, axis=0)
    hidden_padded = norm_back(4, normed_two_grad * norm_gains[1], unit_two, scales_two, 0.0)
    low_padded = jnp.where(keep, hidden_padded, 0.0).astype(low)
    hidden_one_low = low_padded[W:-W]
    conv_bias_one = jnp.sum(hidden_one_low.astype(full), axis=0)
    conv_first_grad = dot_first(taps_one, hidden_one_low)
    act_one_grad = conv_back(low_padded, conv_first)
    normed_one_grad = act_one_grad * silu_slope(normed_one)
    gain_one = jnp.sum(normed_one_grad * unit_one, axis=0)
    bias_one = jnp.sum(normed_one_grad, axis=0)
    image_grad = norm_back(
        5, normed_one_grad * norm_gains[0], unit_one, scales_one, middle_grad, False
    )
    group = lax.axis_index("items")
    groups = lax.axis_size("items")
    group_hot = (jnp.arange(groups) == group).astype(full)
    tables = group_hot[:, None, None] * slot_hot[None, :, None] * modulation_grad
    vectors = jnp.concatenate(
        [
            gain_one,
            gain_two,
            gain_three,
            bias_one,
            bias_two,
            bias_three,
            conv_bias_one,
            conv_bias_two,
            qv_bias_grad,
            text_bias_grad,
            proj_bias_grad,
        ]
    )
    small = jnp.concatenate([tables.reshape(-1, C), vectors.reshape(-1, C)])
    row_share = EMB // lax.axis_size("rows")
    silu_share = lax.dynamic_slice_in_dim(embed_silu, position * row_share, row_share, 1)
    grads = (conv_first_grad, conv_second_grad, qkv_weight_grad, text_weight_grad, proj_weight_grad)
    grads = [g.astype(low) for g in grads]
    if groups == 2 and lax.axis_size("rows") == 2 ** len(ROW_DIMS):
        orders = (
            ("core", "side", "group", "near", "far"),
            ("core", "group", "side", "near", "far"),
            ("core", "side", "group", "near", "far"),
            ("core", "near", "side", "group", "far"),
            ("core", "group", "side", "near", "far"),
        )
        small = jnp.pad(small, ((0, -small.shape[0] % 8), (0, 0)))
        matrices, small, other_share = fold(8, orders, grads, small, silu_share)
        tables_sum = small[: groups * slots * 2].reshape(groups, slots, 2 * C).astype(low)
        both_shares = jnp.stack([silu_share, other_share])
        both_tables = jnp.stack(
            [jnp.take(tables_sum, group, axis=0), jnp.take(tables_sum, 1 - group, axis=0)]
        )
        embed_weight_grad = lax.dot_general(
            both_shares, both_tables, (((0, 1), (0, 1)), ((), ())), preferred_element_type=full
        )
    else:
        small = lax.psum(small.astype(low), ("rows", "items")).astype(full)
        tables_sum = small[: groups * slots * 2].reshape(groups, slots, 2 * C).astype(low)
        part = dot_first(silu_share, jnp.take(tables_sum, group, axis=0)).astype(low)
        matrices = [
            lax.psum_scatter(g, "rows", scatter_dimension=0, tiled=True) for g in grads
        ]
        *matrices, embed_weight_grad = [
            lax.psum(m, "items").astype(full) for m in matrices + [part]
        ]
    vectors_sum = small[groups * slots * 2 :]
    modulation_low = jnp.take(tables_sum, group, axis=0)
    embed_bias_grad = jnp.sum(tables_sum.astype(full), axis=(0, 1))
    embedding_grad = dot_last(modulation_low, embed_weight) * silu_slope(embedding[0].astype(full))
    return (
        result.astype(low)[None],
        image_grad[None],
        embedding_grad[None],
        caption_grad,
        vectors_sum[0:3],
        vectors_sum[3:6],
        matrices[0],
        matrices[1],
        vectors_sum[6:8],
        embed_weight_grad,
        embed_bias_grad,
        matrices[2],
        vectors_sum[8:10].reshape(-1),
        matrices[3],
        vectors_sum[10:12].reshape(-1),
        matrices[4],
        vectors_sum[12],
    )


def solution(mesh):
    in_specs = (
        P("items", "rows", None),
        P("items", None, None),
        P("items", "rows", None, None),
        P("items", None),
        P("items", "rows", None),
        P(),
        P(),
        P(),
        P(),
        P(),
        P(),
        P(),
        P(),
        P(),
        P(),
        P(),
        P(),
        P(),
    )
    out_specs = (
        P("items", "rows", None),
        P("items", "rows", None),
        P("items", None, None),
        P("items", "rows", None, None),
        P(),
        P(),
        P("rows", None),
        P("rows", None),
        P(),
        P("rows", None),
        P(),
        P("rows", None),
        P(),
        P("rows", None),
        P(),
        P("rows", None),
        P(),
    )
    return jax.shard_map(shards, mesh=mesh, in_specs=in_specs, out_specs=out_specs, check_vma=False)
```

```python
import functools

import jax
import jax.numpy as jnp
from jax import lax
from jax.experimental import pallas as pl
from jax.experimental.pallas import tpu as pltpu
from jax.sharding import PartitionSpec as P

C = 512
HEADS = 8
HEAD = 64
EMB = 2048
TEXT = 128
NORM_GROUPS = 32
W = 64
SPAN = 8


epsilon = 1e-05


def from_behind(array, axis, by):
    length = lax.axis_size(axis)
    pairs = [(i, i + by) for i in range(length) if 0 <= i + by < length]
    return lax.ppermute(array, axis, pairs)


def as_sent(array):
    return jax.tree.map(lambda a: a.astype(jnp.bfloat16) if a.dtype == jnp.float32 else a, array)


def keep_state(state):
    return state


def silu_slope(source):
    sigma = jax.nn.sigmoid(source)
    return sigma * (1.0 + source * (1.0 - sigma))


def dot_first(left_side, right_side):
    return lax.dot_general(
        left_side, right_side, (((0,), (0,)), ((), ())), preferred_element_type=jnp.float32
    )


def dot_last(left_side, right_side):
    return lax.dot_general(
        left_side, right_side, (((1,), (1,)), ((), ())), preferred_element_type=jnp.float32
    )


def head_split(source):
    return source.reshape(source.shape[0], HEADS, HEAD)


def piece_scores(query_heads, key_piece, allowed):
    key_heads = head_split(key_piece[:, :C])
    scores = jnp.einsum(
        "qhd,khd->hqk", query_heads, key_heads, preferred_element_type=jnp.float32
    ) * HEAD ** (-0.5)
    return jnp.where(allowed[None, None, :], scores, -jnp.inf)


def piece_grads(query_heads, grad_heads, log_total, row_dots, key_piece, allowed):
    scores = piece_scores(query_heads, key_piece, allowed)
    weights = jnp.exp(scores - log_total[:, :, None])
    value_heads = head_split(key_piece[:, C:])
    weight_grad = jnp.einsum(
        "qhd,khd->hqk", grad_heads, value_heads, preferred_element_type=jnp.float32
    )
    score_grad = (weights * (weight_grad - row_dots[:, :, None])).astype(jnp.bfloat16)
    outcome = []
    key_heads = head_split(key_piece[:, :C])
    query_grad = jnp.einsum(
        "hqk,khd->qhd", score_grad, key_heads, preferred_element_type=jnp.float32
    ) * HEAD ** (-0.5)
    outcome.append(query_grad.reshape(query_grad.shape[0], C))
    key_grad = jnp.einsum(
        "hqk,qhd->khd", score_grad, query_heads, preferred_element_type=jnp.float32
    ) * HEAD ** (-0.5)
    value_grad = jnp.einsum(
        "hqk,qhd->khd", weights.astype(jnp.bfloat16), grad_heads, preferred_element_type=jnp.float32
    )
    outcome.append(jnp.concatenate([key_grad.reshape(-1, C), value_grad.reshape(-1, C)], axis=1))
    return tuple(outcome)


def source_masks(band_items, source, my_item, pixels):
    slots = band_items.shape[0]
    inside = (source >= 0) & (source < slots)
    clipped = jnp.clip(source, 0, slots - 1)
    source_item = band_items[clipped]
    before_item = band_items[jnp.maximum(clipped - 1, 0)]
    same_item = inside & (source_item == my_item)
    leading = same_item & ((clipped == 0) | (before_item != source_item))
    allowed = jnp.concatenate(
        [jnp.broadcast_to(same_item, (pixels,)), jnp.broadcast_to(leading, (TEXT,))]
    )
    return (allowed, same_item)


REACH = SPAN - 1
LOG2E = 1.4426950408889634
PIX = 512


def dot(left, right):
    return jnp.dot(left, right, preferred_element_type=jnp.float32)


def reach_of(here, slots):
    first = here < SPAN
    low = jnp.maximum(jnp.where(first, 0, SPAN), here - REACH)
    high = jnp.minimum(jnp.where(first, SPAN - 1, slots - 1), here + REACH)
    return low, high


def exchange_kernel(slots, with_edges, *refs):
    if with_edges:
        tile, top, bottom, window, above, below, send_sem, recv_sem, edge_send, edge_recv = refs
    else:
        tile, window, send_sem, recv_sem = refs
    here = lax.axis_index("rows")
    low, high = reach_of(here, slots)
    offsets = [o for o in range(-REACH, REACH + 1) if o != 0]

    def reached(offset):
        return (here + offset >= low) & (here + offset <= high)

    barrier = pltpu.get_barrier_semaphore()
    for o in offsets:

        @pl.when(reached(o))
        def _(o=o):
            pl.semaphore_signal(barrier, 1, device_id={"rows": here + o})

    pl.semaphore_wait(barrier, high - low)

    def edge_copy(o):
        source, target, k = (top, below, 0) if o < 0 else (bottom, above, 1)
        return pltpu.make_async_remote_copy(
            source, target, edge_send.at[k], edge_recv.at[k], device_id={"rows": here + o}
        )

    def tile_copy(o):
        return pltpu.make_async_remote_copy(
            tile,
            window.at[REACH - o],
            send_sem.at[REACH - o],
            recv_sem.at[REACH - o],
            device_id={"rows": here + o},
        )

    if with_edges:
        for o in (-1, 1):

            @pl.when(reached(o))
            def _(o=o):
                edge_copy(o).start()

    for o in offsets:

        @pl.when(reached(o))
        def _(o=o):
            tile_copy(o).start()

        @pl.when(jnp.logical_not(reached(-o)))
        def _(o=o):
            window[REACH - o] = jnp.zeros_like(tile)

    window[REACH] = tile[...]
    if with_edges:

        @pl.when(jnp.logical_not(reached(-1)))
        def _():
            above[...] = jnp.zeros_like(above)

        @pl.when(jnp.logical_not(reached(1)))
        def _():
            below[...] = jnp.zeros_like(below)

    for o in offsets:

        @pl.when(reached(o))
        def _(o=o):
            tile_copy(o).wait_send()

        @pl.when(reached(-o))
        def _(o=o):
            tile_copy(o).wait_recv()

    if with_edges:
        for o in (-1, 1):

            @pl.when(reached(o))
            def _(o=o):
                edge_copy(o).wait_send()

            @pl.when(reached(-o))
            def _(o=o):
                edge_copy(o).wait_recv()


def exchange(ident, slots, tile, edges=None):
    vmem = pl.BlockSpec(memory_space=pltpu.VMEM)
    shapes = [jax.ShapeDtypeStruct((2 * REACH + 1,) + tile.shape, tile.dtype)]
    scratch = [pltpu.SemaphoreType.DMA((2 * REACH + 1,))] * 2
    operands = [tile]
    if edges is not None:
        shapes += [jax.ShapeDtypeStruct(e.shape, e.dtype) for e in edges]
        scratch += [pltpu.SemaphoreType.DMA((2,))] * 2
        operands += list(edges)
    return pl.pallas_call(
        functools.partial(exchange_kernel, slots, edges is not None),
        out_shape=tuple(shapes),
        in_specs=[vmem] * len(operands),
        out_specs=(vmem,) * len(shapes),
        scratch_shapes=scratch,
        compiler_params=pltpu.CompilerParams(collective_id=ident, has_side_effects=True),
        name=f"exchange_{ident}",
    )(*operands)


def swap_kernel(count, *refs):
    sources, targets = refs[:count], refs[count : 2 * count]
    send_sem, recv_sem, own_sem = refs[2 * count :]
    here = lax.axis_index("rows")
    base = (here // SPAN) * SPAN
    lane = here - base
    barrier = pltpu.get_barrier_semaphore()
    for o in range(1, SPAN):
        pl.semaphore_signal(barrier, 1, device_id={"rows": base + lax.rem(lane + o, SPAN)})
    pl.semaphore_wait(barrier, SPAN - 1)
    copies = []
    for o in range(1, SPAN):
        other = lax.rem(lane + o, SPAN)
        for k in range(count):
            copies.append(
                pltpu.make_async_remote_copy(
                    sources[k].at[other],
                    targets[k].at[lane],
                    send_sem.at[k, o],
                    recv_sem.at[k, o],
                    device_id={"rows": base + other},
                )
            )
    for copy in copies:
        copy.start()
    own = []
    for k in range(count):
        own.append(pltpu.make_async_copy(sources[k].at[lane], targets[k].at[lane], own_sem.at[k]))
        own[-1].start()
    for copy in own:
        copy.wait()
    for copy in copies:
        copy.wait()


def swap(ident, *arrays):
    anywhere = pl.BlockSpec(memory_space=pl.ANY)
    count = len(arrays)
    return pl.pallas_call(
        functools.partial(swap_kernel, count),
        out_shape=tuple(jax.ShapeDtypeStruct(a.shape, a.dtype) for a in arrays),
        in_specs=[anywhere] * count,
        out_specs=(anywhere,) * count,
        scratch_shapes=[
            pltpu.SemaphoreType.DMA((count, SPAN)),
            pltpu.SemaphoreType.DMA((count, SPAN)),
            pltpu.SemaphoreType.DMA((count,)),
        ],
        compiler_params=pltpu.CompilerParams(collective_id=ident, has_side_effects=True),
        name=f"swap_{ident}",
    )(*arrays)


def head_kernel(
    starts, ends, y_ref, t_ref, z_ref, zt_ref, xt, vx, tt, tvx, s_ref, p_ref, dk, dv, dkt, dvt
):
    low = jnp.bfloat16
    full = jnp.float32
    bands, pixels = y_ref.shape[0], y_ref.shape[1]
    text = t_ref.shape[1]
    scale = HEAD ** (-0.5)

    def widened(values, rows):
        lanes = lax.broadcasted_iota(jnp.int32, (rows, 2 * HEAD), 1)
        units = jnp.where(lanes < HEAD + 2, 1.0, 0.0).astype(low)
        return jnp.where(lanes < HEAD, values, units)

    def prepare(b, carry):
        block = y_ref[b]
        xt[b] = block.T
        vx[b] = widened(block[:, 2 * HEAD :], pixels)
        words = t_ref[b]
        tt[b] = words.T
        tvx[b] = widened(pltpu.roll(words.astype(full), HEAD, 1).astype(low), text)
        dk[b] = jnp.zeros((pixels, 2 * HEAD), full)
        dv[b] = jnp.zeros((pixels, 2 * HEAD), full)
        dkt[b] = jnp.zeros((text, 2 * HEAD), full)
        dvt[b] = jnp.zeros((text, 2 * HEAD), full)
        return carry

    lax.fori_loop(0, bands, prepare, 0)

    def one_row(columns):
        rows = lax.broadcasted_iota(jnp.int32, (16, columns), 0)
        return jnp.where(rows == 0, 1.0, 0.0).astype(low)

    ones_pixels = one_row(pixels)
    ones_text = one_row(text)
    zeros = jnp.zeros((HEAD, pixels), low)

    def query_band(i, carry):
        start, end = starts[i], ends[i]
        query_t = (xt[i, 0:HEAD, :].astype(full) * scale).astype(low)
        query_rhs = jnp.concatenate([zeros, query_t], 0)
        query_text = jnp.concatenate([query_t, zeros], 0)

        def score(j, top):
            scores = dot(y_ref[j, :, 0 : 2 * HEAD], query_rhs)
            s_ref[j] = scores
            return jnp.maximum(top, jnp.max(scores.reshape(pixels // 8, 8, pixels), axis=0))

        top = lax.fori_loop(start, end, score, jnp.full((8, pixels), -jnp.inf, full))
        scores = dot(t_ref[start], query_text)
        top = jnp.maximum(top, jnp.max(scores.reshape(text // 8, 8, pixels), axis=0))
        top = jnp.max(top, axis=0, keepdims=True)
        weights_text = jnp.exp2((scores - top) * LOG2E).astype(low)
        total = dot(jnp.concatenate([tt[start, HEAD:, :], ones_text], 0), weights_text)

        def gather(j, total):
            weights = jnp.exp2((s_ref[j] - top) * LOG2E).astype(low)
            p_ref[j] = weights
            values = jnp.concatenate([xt[j, 2 * HEAD : 3 * HEAD, :], ones_pixels], 0)
            return total + dot(values, weights)

        total = lax.fori_loop(start, end, gather, total)
        inverse = 1.0 / total[HEAD : HEAD + 1, :]
        attended = total[0:HEAD, :] * inverse
        grad = xt[i, 3 * HEAD :, :].astype(full)
        minus_dots = -jnp.sum(grad * attended, axis=0, keepdims=True) * inverse
        grad_scaled = (grad * inverse).astype(low)
        coarse = minus_dots.astype(low)
        fine = minus_dots - coarse.astype(full)
        rows = lax.broadcasted_iota(jnp.int32, (HEAD, pixels), 0)
        extra = jnp.where(rows == 0, coarse.astype(full), jnp.where(rows == 1, fine, 0.0))
        grad_rhs = jnp.concatenate([grad_scaled, extra.astype(low)], 0)
        grad_rows = jnp.concatenate([grad_scaled, zeros], 0).T
        query_rows = jnp.concatenate([query_t, zeros], 0).T

        def back(j, query_grad):
            weights = p_ref[j]
            steps = (weights.astype(full) * dot(vx[j], grad_rhs)).astype(low)
            dv[j] += dot(weights, grad_rows)
            dk[j] += dot(steps, query_rows)
            return query_grad + dot(xt[j, HEAD : 2 * HEAD, :], steps)

        steps = (weights_text.astype(full) * dot(tvx[start], grad_rhs)).astype(low)
        dvt[start] += dot(weights_text, grad_rows)
        dkt[start] += dot(steps, query_rows)
        query_grad = dot(tt[start, 0:HEAD, :], steps)
        query_grad = lax.fori_loop(start, end, back, query_grad)
        z_ref[i, :, 0 : 2 * HEAD] = jnp.concatenate(
            [attended.astype(low), (query_grad * scale).astype(low)], 0
        ).T
        return carry

    lax.fori_loop(0, bands, query_band, 0)

    def finish(b, carry):
        lanes = lax.broadcasted_iota(jnp.int32, (pixels, 2 * HEAD), 1)
        z_ref[b, :, 2 * HEAD :] = jnp.where(
            lanes < HEAD, dk[b], pltpu.roll(dv[b], HEAD, 1)
        ).astype(low)
        lanes = lax.broadcasted_iota(jnp.int32, (text, 2 * HEAD), 1)
        zt_ref[b] = jnp.where(lanes < HEAD, dkt[b], pltpu.roll(dvt[b], HEAD, 1)).astype(low)
        return carry

    lax.fori_loop(0, bands, finish, 0)


def one_head(starts, ends, pieces, words):
    bands, pixels, _ = pieces.shape
    text = words.shape[1]
    low, full = jnp.bfloat16, jnp.float32
    smem = pl.BlockSpec(memory_space=pltpu.SMEM)
    vmem = pl.BlockSpec(memory_space=pltpu.VMEM)
    return pl.pallas_call(
        head_kernel,
        out_shape=(
            jax.ShapeDtypeStruct(pieces.shape, low),
            jax.ShapeDtypeStruct(words.shape, low),
        ),
        in_specs=[smem, smem, vmem, vmem],
        out_specs=(vmem, vmem),
        scratch_shapes=[
            pltpu.VMEM((bands, 4 * HEAD, pixels), low),
            pltpu.VMEM((bands, pixels, 2 * HEAD), low),
            pltpu.VMEM((bands, 2 * HEAD, text), low),
            pltpu.VMEM((bands, text, 2 * HEAD), low),
            pltpu.VMEM((bands, pixels, pixels), full),
            pltpu.VMEM((bands, pixels, pixels), low),
            pltpu.VMEM((bands, pixels, 2 * HEAD), full),
            pltpu.VMEM((bands, pixels, 2 * HEAD), full),
            pltpu.VMEM((bands, text, 2 * HEAD), full),
            pltpu.VMEM((bands, text, 2 * HEAD), full),
        ],
        compiler_params=pltpu.CompilerParams(vmem_limit_bytes=56 << 20),
        name="one_head",
    )(starts, ends, pieces, words)


def by_head(*flat):
    split = [f.reshape(f.shape[0], HEADS, HEAD).transpose(1, 0, 2) for f in flat]
    return jnp.concatenate(split, axis=2)


def attention_by_head(band_items, position, queries, keys_values, text_kv, attended_grad):
    base = (position // SPAN) * SPAN
    items = lax.dynamic_slice_in_dim(band_items, base, SPAN)
    same = items[:, None] == items[None, :]
    column = jnp.arange(SPAN)
    starts = jnp.min(jnp.where(same, column[None, :], SPAN), axis=1).astype(jnp.int32)
    ends = jnp.max(jnp.where(same, column[None, :] + 1, 0), axis=1).astype(jnp.int32)
    pieces, words = swap(
        6,
        by_head(queries, keys_values[:, :C], keys_values[:, C:], attended_grad),
        by_head(text_kv[:, :C], text_kv[:, C:]),
    )
    return one_head(starts, ends, pieces, words)


def attention_by_band(band_items, position, queries, keys_values, text_kv, attended_grad):
    my_item = band_items[position]
    pixels = queries.shape[0]
    own_allowed, own_same = source_masks(band_items, position, my_item, pixels)
    packed = jnp.concatenate([keys_values, text_kv], axis=0)
    pieces = [(0, packed, own_allowed, own_same)]
    for distance in range(1, SPAN):
        for offset in (distance, -distance):
            arrived = from_behind(packed, "rows", offset)
            allowed, same_item = source_masks(band_items, position - offset, my_item, pixels)
            pieces.append((offset, arrived, allowed, same_item))
    query_heads = head_split(queries)
    row_top = jnp.full((HEADS, pixels), -jnp.inf, jnp.float32)
    weight_sum = jnp.zeros((HEADS, pixels), jnp.float32)
    for offset, key_piece, allowed, same_item in pieces:

        def gather_scores(state, key_piece=key_piece, allowed=allowed):
            top_old, sum_old = state
            scores = piece_scores(query_heads, key_piece, allowed)
            top_new = jnp.maximum(top_old, jnp.max(scores, axis=2))
            sum_new = sum_old * jnp.exp(top_old - top_new) + jnp.sum(
                jnp.exp(scores - top_new[:, :, None]), axis=2
            )
            return (top_new, sum_new)

        row_top, weight_sum = lax.cond(same_item, gather_scores, keep_state, (row_top, weight_sum))
    log_total = row_top + jnp.log(weight_sum)
    attended = jnp.zeros((pixels, HEADS, HEAD), jnp.float32)
    for offset, key_piece, allowed, same_item in pieces:

        def add_values(totals, key_piece=key_piece, allowed=allowed):
            scores = piece_scores(query_heads, key_piece, allowed)
            weights = jnp.exp(scores - log_total[:, :, None]).astype(jnp.bfloat16)
            return totals + jnp.einsum(
                "hqk,khd->qhd",
                weights,
                head_split(key_piece[:, C:]),
                preferred_element_type=jnp.float32,
            )

        attended = lax.cond(same_item, add_values, keep_state, attended)
    attended_flat = attended.reshape(pixels, C)
    row_dots = jnp.sum(
        (attended_grad.astype(jnp.float32) * attended_flat).reshape(pixels, HEADS, HEAD), axis=2
    ).T
    grad_heads = head_split(attended_grad)
    query_grad = jnp.zeros((pixels, C), jnp.float32)
    packed_grad = jnp.zeros((pixels + TEXT, 2 * C), jnp.float32)
    zero_piece = jnp.zeros((pixels + TEXT, 2 * C), jnp.float32)
    for offset, key_piece, allowed, same_item in pieces:

        def grad_both(totals, key_piece=key_piece, allowed=allowed):
            outcome = piece_grads(query_heads, grad_heads, log_total, row_dots, key_piece, allowed)
            return (totals + outcome[0], outcome[1])

        def grad_none(totals):
            return (totals, zero_piece)

        query_grad, piece_grad = lax.cond(same_item, grad_both, grad_none, query_grad)
        if offset == 0:
            packed_grad = packed_grad + piece_grad
        else:
            packed_grad = packed_grad + from_behind(
                as_sent(piece_grad), "rows", -offset
            ).astype(jnp.float32)
    packed_low = packed_grad.astype(jnp.bfloat16)
    return (
        attended_flat.astype(jnp.bfloat16),
        query_grad.astype(jnp.bfloat16),
        packed_low[:pixels],
        packed_low[pixels:],
    )


def taps_of(rows, reverse):
    padded = rows.reshape(-1, W, rows.shape[1])
    row_list = [padded[:-2], padded[1:-1], padded[2:]]
    if reverse:
        row_list = row_list[::-1]
    zero_column = jnp.zeros_like(row_list[0][:, :1])
    views = []
    for row_view in row_list:
        left_view = jnp.concatenate([zero_column, row_view[:, :-1]], axis=1)
        right_view = jnp.concatenate([row_view[:, 1:], zero_column], axis=1)
        view_list = [left_view, row_view, right_view]
        if reverse:
            view_list = view_list[::-1]
        views = views + view_list
    return [view.reshape(-1, rows.shape[1]) for view in views]


VECTORS = (
    "mean_one",
    "scale_one",
    "gain_one",
    "bias_one",
    "mean_two",
    "scale_two",
    "gain_two",
    "bias_two",
    "mean_three",
    "scale_three",
    "gain_three",
    "bias_three",
    "stretch",
    "shift",
    "proj_bias",
    "keep_above",
    "keep_below",
    "per_item",
)
VECTOR_ROWS = 24
CROSS = ("far", "near", "side")
SIDE_FIRST = ("side", "group", "near", "far")
GROUP_FIRST = ("group", "near", "side", "far")
NEAR_FIRST = ("near", "side", "group", "far")
STREAMS = {
    "first0": (48, C // 2, SIDE_FIRST),
    "first1": (48, C // 2, GROUP_FIRST),
    "first2": (48, C // 2, NEAR_FIRST),
    "second0": (48, C // 2, SIDE_FIRST),
    "second1": (48, C // 2, GROUP_FIRST),
    "second2": (48, C // 2, NEAR_FIRST),
    "text0": (32, C, SIDE_FIRST),
    "text1": (32, C, NEAR_FIRST),
    "qkv": (16, 3 * C // 2, GROUP_FIRST),
    "proj": (16, C // 2, GROUP_FIRST),
}
LANDINGS = 4
IMAGE_ROWS = 8


def back_kernel(names, *refs):
    low, full = jnp.bfloat16, jnp.float32
    r = dict(zip(names, refs))
    row = lax.axis_index("rows")
    group = lax.axis_index("items")
    lane = row % SPAN
    base = row - lane
    place = {"far": row // 8, "near": (row // 4) % 2, "side": (row // 2) % 2, "core": row % 2}
    place["group"] = group
    width = {"far": 8, "near": 4, "side": 2, "core": 1}
    partner = {d: {"rows": row + (1 - 2 * place[d]) * n} for d, n in width.items()}
    partner["group"] = {"items": 1 - group}
    core = place["core"]
    peers = [{"rows": base + (lane + o) % SPAN} for o in range(1, SPAN)]

    barrier = pltpu.get_barrier_semaphore()
    for target in peers + [partner["far"], partner["group"]]:
        pl.semaphore_signal(barrier, 1, device_id=target)
    pl.semaphore_wait(barrier, SPAN + 1)

    def remote(source, target, send, recv, device):
        return pltpu.make_async_remote_copy(source, target, send, recv, device_id=device)

    swaps = []
    for o in range(1, SPAN):
        other = (lane + o) % SPAN
        for k, (source, target) in enumerate((("pieces", "heads"), ("words", "head_words"))):
            swaps.append(
                remote(
                    r[source].at[other],
                    r[target].at[lane],
                    r["swap_send"].at[k, o],
                    r["swap_recv"].at[k, o],
                    peers[o - 1],
                )
            )
    for copy in swaps:
        copy.start()

    loads = {}

    def load(k, name, source, target):
        loads[name] = pltpu.make_async_copy(source, target, r["load_sem"].at[k])
        loads[name].start()

    load(0, "own", r["pieces"].at[lane], r["heads"].at[lane])
    load(1, "own_words", r["words"].at[lane], r["head_words"].at[lane])
    load(2, "middle", r["middle"], r["mid"].at[1 : IMAGE_ROWS + 1])
    load(3, "qkv_weight", r["qkv_weight"], r["qkv_w"])
    load(4, "proj_weight", r["proj_weight"], r["proj_w"])
    load(5, "upstream", r["upstream"], r["up"])
    load(6, "act_three", r["act_three"], r["act3"])
    load(7, "caption", r["caption"], r["cap"])
    load(8, "conv_second", r["conv_second"], r["conv_w"])
    load(9, "hidden", r["hidden"], r["hid"])
    load(10, "act_two", r["act_two"], r["act2"])
    load(11, "act_one", r["act_one"], r["act1"])
    load(12, "image", r["image"], r["img"])
    load(13, "text_weight", r["text_weight"], r["text_w"])

    sibling = {}

    def to_sibling(k, name, source, target):
        sibling[name] = remote(
            source, target, r["sib_send"].at[k], r["sib_recv"].at[k], partner["core"]
        )
        sibling[name].start()

    half = pl.ds(pl.multiple_of((1 - core) * (C // 2), C // 2), C // 2)
    to_sibling(0, "upstream", r["upstream"].at[:, half], r["sib_up"])
    to_sibling(1, "act3", r["act_three"], r["sib_act3"])
    to_sibling(2, "cap", r["caption"], r["sib_cap"])
    to_sibling(3, "act2", r["act_two"], r["sib_act2"])
    to_sibling(4, "act1", r["act_one"], r["sib_act1"])

    above, below = {"rows": row - 1}, {"rows": row + 1}
    has_above, has_below = lane > 0, lane < SPAN - 1

    def edges(k, source, target):
        up = remote(
            source[0], target.at[IMAGE_ROWS + 1], r["edge_send"].at[k, 0], r["edge_recv"].at[k, 0], above
        )
        down = remote(source[1], target.at[0], r["edge_send"].at[k, 1], r["edge_recv"].at[k, 1], below)
        return up, down

    def send_edges(pair):
        pl.when(has_above)(pair[0].start)
        pl.when(has_below)(pair[1].start)

    def wait_edges(pair):
        @pl.when(has_above)
        def _():
            pair[0].wait_send()
            pair[1].wait_recv()

        @pl.when(has_below)
        def _():
            pair[1].wait_send()
            pair[0].wait_recv()

    mid_edges = edges(0, (r["middle"].at[0], r["middle"].at[IMAGE_ROWS - 1]), r["mid"])
    send_edges(mid_edges)

    def zero_edges(target):
        @pl.when(jnp.logical_not(has_above))
        def _():
            target[0] = jnp.zeros((W, C), full)

        @pl.when(jnp.logical_not(has_below))
        def _():
            target[IMAGE_ROWS + 1] = jnp.zeros((W, C), full)

    for name in ("mid", "part_two", "part_one"):
        zero_edges(r[name])

    vec = {name: r["vectors"][i : i + 1, :] for i, name in enumerate(VECTORS)}

    def send_tile(k, source, target, o_sem):
        copies = []
        for o in range(1, SPAN):
            copies.append(
                remote(
                    source,
                    target.at[lane],
                    r["tile_send"].at[k, o],
                    r["tile_recv"].at[k, o],
                    peers[o - 1],
                )
            )
        for copy in copies:
            copy.start()
        target[lane] = source[...]
        return copies

    rows_of_blocks = lax.broadcasted_iota(jnp.int32, (C, C), 0) // (C // NORM_GROUPS)
    columns_of_blocks = lax.broadcasted_iota(jnp.int32, (C, C), 1) // (C // NORM_GROUPS)
    r["blocks"][...] = jnp.where(rows_of_blocks == columns_of_blocks, 1.0, 0.0).astype(low)

    def item_means(window):
        total = jnp.zeros((8, C), full)
        for b in range(SPAN):
            mask = r["vectors"][VECTOR_ROWS + b : VECTOR_ROWS + b + 1, :]
            total = total + jnp.where(mask > 0.0, window[b], 0.0)
        total = total * vec["per_item"]
        coarse = total.astype(low)
        rest = total - coarse.astype(full)
        finer = rest.astype(low)
        finest = (rest - finer.astype(full)).astype(low)
        blocks = r["blocks"][...]
        return dot(coarse, blocks) + dot(finer, blocks) + dot(finest, blocks)

    def sums_tile(first, second):
        rows = lax.broadcasted_iota(jnp.int32, (8, C), 0)
        return jnp.where(rows == 0, first, jnp.where(rows == 1, second, 0.0))

    class Stream:
        def __init__(self, k, name):
            self.k, self.name = k, name
            self.order = STREAMS[name][2]
            self.dims = list(CROSS) + ["core", "group"]
            self.step = 0
            self.copy = None

        def at(self, ref, d, index):
            return ref.at[(slice(None),) * self.dims.index(d) + (index,)]

        def start(self):
            self.launch(r["grad_" + self.name])

        def launch(self, ref):
            k, step = self.k, self.step
            if step < LANDINGS:
                d = self.order[step]
                self.copy = remote(
                    self.at(ref, d, 1 - place[d]),
                    r[f"landing_{self.name}_{step}"],
                    r["fold_send"].at[k, step],
                    r["fold_recv"].at[k, step],
                    partner[d],
                )
                self.mine = self.at(ref, d, place[d])
                self.dims.remove(d)
            elif step == LANDINGS:
                fin = r["joined_" + self.name]
                self.copy = remote(
                    ref.at[1 - core],
                    fin.at[core],
                    r["fold_send"].at[k, step],
                    r["fold_recv"].at[k, step],
                    partner["core"],
                )
                self.mine = ref.at[core]
            else:
                self.copy = remote(
                    r["joined_" + self.name],
                    r["whole_" + self.name],
                    r["fold_send"].at[k, step],
                    r["fold_recv"].at[k, step],
                    partner["group"],
                )
            self.copy.start()

        def advance(self):
            self.copy.wait()
            if self.step < LANDINGS:
                landed, mine = r[f"landing_{self.name}_{self.step}"], self.mine
                lead = landed.shape[:-2]
                pieces = 1
                for n in lead:
                    pieces *= n

                def add(i, carry):
                    index = []
                    for n in reversed(lead):
                        index.insert(0, i % n)
                        i = i // n
                    index = tuple(index)
                    total = landed[index].astype(full) + mine[index].astype(full)
                    landed[index] = total.astype(low)
                    return carry

                lax.fori_loop(0, pieces, add, 0)
                self.step += 1
                self.launch(landed)
            elif self.step == LANDINGS:
                r["joined_" + self.name][core] = self.mine[...]
                self.step += 1
                self.launch(None)
            else:
                self.step += 1

    streams = {name: Stream(k, name) for k, name in enumerate(STREAMS)}

    loads["own"].wait()
    loads["own_words"].wait()
    for copy in swaps:
        copy.wait()
    for h in range(0, HEADS, 2):
        for k in range(4):
            pair = [r["heads"][h + i, :, k * HEAD : (k + 1) * HEAD] for i in range(2)]
            r["joined"][:, k * C + h * HEAD : k * C + (h + 2) * HEAD] = jnp.concatenate(pair, axis=1)
        for k in range(2):
            pair = [r["head_words"][h + i, :, k * HEAD : (k + 1) * HEAD] for i in range(2)]
            r["joined_words"][:, k * C + h * HEAD : k * C + (h + 2) * HEAD] = jnp.concatenate(
                pair, axis=1
            )
    to_sibling(5, "attended", r["joined"].at[:, 0:C], r["sib_attended"])
    three_half = C + (1 - core) * (3 * C // 2)
    to_sibling(
        6,
        "qkv",
        r["joined"].at[:, pl.ds(pl.multiple_of(three_half, C // 2), 3 * C // 2)],
        r["sib_qkv"],
    )
    to_sibling(
        7,
        "words",
        r["joined_words"].at[:, pl.ds(pl.multiple_of((1 - core) * C, C), C)],
        r["sib_words"],
    )
    for name in ("middle", "qkv_weight", "proj_weight", "upstream"):
        loads[name].wait()
    wait_edges(mid_edges)

    def pixel_block(ref, i, count=4):
        return ref[1 + i * count : 1 + (i + 1) * count].reshape(count * W, C)

    def unit(values, which):
        return (values - vec["mean_" + which]) * vec["scale_" + which]

    def column_sum(values):
        return jnp.sum(values, axis=0, keepdims=True)

    plain = jnp.zeros((1, C), full)
    crossed = jnp.zeros((1, C), full)
    up_sum = jnp.zeros((1, C), full)
    for i in range(2):
        block = slice(i * 4 * W, (i + 1) * 4 * W)
        middle = pixel_block(r["mid"], i)
        upstream = r["up"][block, :].astype(full)
        result = middle + dot(r["joined"][block, 0:C], r["proj_w"][...]) + vec["proj_bias"]
        r["result"][block, :] = result.astype(low)
        grad = dot_last(r["joined"][block, C:], r["qkv_w"][...])
        plain = plain + column_sum(grad)
        crossed = crossed + column_sum(grad * unit(middle, "three"))
        up_sum = up_sum + column_sum(upstream)
        part = upstream + grad * (vec["gain_three"] * vec["scale_three"])
        r["part_two"][1 + i * 4 : 5 + i * 4] = part.reshape(4, W, C)
    gains = {"three": crossed}
    biases = {"three": plain}
    r["tile"][0] = sums_tile(plain * vec["gain_three"], crossed * vec["gain_three"])
    three_edges = edges(1, (r["part_two"].at[1], r["part_two"].at[IMAGE_ROWS]), r["part_two"])
    send_edges(three_edges)
    tiles = send_tile(0, r["tile"].at[0], r["window"].at[0], 0)

    def mine_of(ref, start, size):
        return ref[:, pl.ds(pl.multiple_of(start, size if size % 256 else 256), size)]

    for name in ("upstream", "act3", "cap", "attended", "qkv", "words"):
        sibling[name].wait()
    for name in ("act_three", "caption"):
        loads[name].wait()
    grad = dot_first(r["joined"][:, 0:C], mine_of(r["up"], core * (C // 2), C // 2))
    grad = grad + dot_first(r["sib_attended"][...], r["sib_up"][...])
    r["grad_proj"][...] = grad.astype(low).reshape(r["grad_proj"].shape)
    streams["proj"].start()
    for n in range(3):
        own = mine_of(r["joined"], C + core * (3 * C // 2) + n * (C // 2), C // 2)
        columns = slice(n * (C // 2), (n + 1) * (C // 2))
        grad = dot_first(r["act3"][...], own)
        grad = grad + dot_first(r["sib_act3"][...], r["sib_qkv"][:, columns])
        r["grad_qkv"][:, :, :, :, :, :, columns] = grad.astype(low).reshape(2, 2, 2, 2, 2, 16, C // 2)
    streams["qkv"].start()

    def text_rows(s, carry):
        columns = pl.ds(pl.multiple_of(s * 128, 128), 128)
        own = mine_of(r["joined_words"], core * C, C)
        grad = dot_first(r["cap"][:, columns], own)
        grad = grad + dot_first(r["sib_cap"][:, columns], r["sib_words"][...])
        grad = grad.astype(low)
        index = (s // 8, (s // 4) % 2, (s // 2) % 2, s % 2)
        r["grad_text0"][index] = grad[0:64].reshape(2, 32, C)
        r["grad_text1"][index] = grad[64:128].reshape(2, 32, C)
        return carry

    lax.fori_loop(0, 2 ** len(CROSS) * 2, text_rows, 0)
    streams["text0"].start()
    streams["text1"].start()
    query_sum = column_sum(r["joined"][:, C : 2 * C].astype(full))
    value_sum = column_sum(r["joined"][:, 3 * C :].astype(full))
    word_sum = [column_sum(r["joined_words"][:, k * C : (k + 1) * C].astype(full)) for k in range(2)]

    def spread_rows(i, values):
        rows = lax.broadcasted_iota(jnp.int32, (W, C), 0)
        right = jnp.where(rows == 0, 0.0, pltpu.roll(values, 1, 0))
        left = jnp.where(rows == W - 1, 0.0, pltpu.roll(values, W - 1, 0))
        r["shifts"][0, i] = left.astype(low)
        r["shifts"][1, i] = values.astype(low)
        r["shifts"][2, i] = right.astype(low)

    def kept(i, values):
        keep = jnp.where(i == 0, vec["keep_above"], jnp.where(i == IMAGE_ROWS + 1, vec["keep_below"], 1.0))
        return jnp.where(keep > 0.0, values, 0.0)

    def conv_back():
        total = jnp.zeros((IMAGE_ROWS * W, C), full)
        for t in range(9):
            dy, dx = t // 3, t % 3
            view = r["shifts"][dx, 2 - dy : 2 - dy + IMAGE_ROWS].reshape(IMAGE_ROWS * W, C)
            total = total + dot_last(view, r["conv_w"][t * C : (t + 1) * C, :])
        return total

    def conv_grads(kind, own, other, landing):
        for t in range(9):
            dy, dx = t // 3, t % 3
            shifted = r["shifts"][
                dx, 1 : IMAGE_ROWS + 1, :, pl.ds(pl.multiple_of(core * (C // 2), C // 2), C // 2)
            ].reshape(IMAGE_ROWS * W, C // 2)
            grad = dot_first(r[own][dy * W : dy * W + IMAGE_ROWS * W, :], shifted)
            grad = grad + dot_first(
                r[other][dy * W : dy * W + IMAGE_ROWS * W, :],
                r[landing][dx].reshape(IMAGE_ROWS * W, C // 2),
            )
            grad = grad.astype(low)
            begin = t * C
            while begin < (t + 1) * C:
                shard, within = divmod(begin, 288)
                stream, offset = divmod(within, 96)
                part, offset = divmod(offset, 48)
                size = min(48 - offset, (t + 1) * C - begin)
                target = r[f"grad_{kind}{stream}"]
                target[
                    shard // 8, (shard // 4) % 2, (shard // 2) % 2, shard % 2, part, offset : offset + size
                ] = grad[begin - t * C : begin - t * C + size]
                begin += size
        for j in range(3):
            streams[f"{kind}{j}"].start()

    for copy in tiles:
        copy.wait()
    wait_edges(three_edges)
    means = item_means(r["window"].at[0])
    offset_three, slope_three = means[0:1] * vec["scale_three"], means[1:2] * vec["scale_three"]

    def middle_row(i, bias):
        values = r["part_two"][i] - offset_three - unit(r["mid"][i], "three") * slope_three
        r["part_two"][i] = values
        values = kept(i, values)
        spread_rows(i, values)
        inside = jnp.where((i > 0) & (i <= IMAGE_ROWS), 1.0, 0.0)
        return bias + inside * column_sum(values.astype(low).astype(full))

    conv_bias_two = lax.fori_loop(0, IMAGE_ROWS + 2, middle_row, jnp.zeros((1, C), full))
    shift_half = r["shifts"].at[:, 1 : IMAGE_ROWS + 1, :, half]
    to_sibling(8, "shifts_two", shift_half, r["sib_shifts_two"])
    loads["conv_second"].wait()
    loads["hidden"].wait()
    r["product"][...] = conv_back().reshape(IMAGE_ROWS, W, C)
    load(8, "conv_first", r["conv_first"], r["conv_w"])
    stretched = vec["stretch"] * vec["gain_two"] * vec["scale_two"]

    def second_row(i, sums):
        unit_two = unit(r["hid"][i + 1], "two")
        normed = unit_two * vec["gain_two"] + vec["bias_two"]
        grad = r["product"][i] * silu_slope_of(normed * vec["stretch"] + vec["shift"])
        r["part_one"][i + 1] = grad * stretched
        return sums[0] + column_sum(grad), sums[1] + column_sum(grad * unit_two)

    nothing = (jnp.zeros((1, C), full), jnp.zeros((1, C), full))
    plain, crossed = lax.fori_loop(0, IMAGE_ROWS, second_row, nothing)
    scale_grad = crossed * vec["gain_two"] + plain * vec["bias_two"]
    shift_grad = plain
    gains["two"], biases["two"] = crossed * vec["stretch"], plain * vec["stretch"]
    r["tile"][1] = sums_tile(biases["two"] * vec["gain_two"], gains["two"] * vec["gain_two"])
    two_edges = edges(2, (r["part_one"].at[1], r["part_one"].at[IMAGE_ROWS]), r["part_one"])
    send_edges(two_edges)
    tiles = send_tile(1, r["tile"].at[1], r["window"].at[1], 0)
    loads["act_two"].wait()
    sibling["act2"].wait()
    sibling["shifts_two"].wait()
    conv_grads("second", "act2", "sib_act2", "sib_shifts_two")
    for copy in tiles:
        copy.wait()
    wait_edges(two_edges)
    means = item_means(r["window"].at[1])
    offset_two, slope_two = means[0:1] * vec["scale_two"], means[1:2] * vec["scale_two"]

    def hidden_row(i, bias):
        values = r["part_one"][i] - offset_two - unit(r["hid"][i], "two") * slope_two
        values = kept(i, values)
        spread_rows(i, values)
        inside = jnp.where((i > 0) & (i <= IMAGE_ROWS), 1.0, 0.0)
        return bias + inside * column_sum(values.astype(low).astype(full))

    conv_bias_one = lax.fori_loop(0, IMAGE_ROWS + 2, hidden_row, jnp.zeros((1, C), full))
    to_sibling(9, "shifts_one", shift_half, r["sib_shifts_one"])
    for name in ("proj", "qkv", "text0", "text1"):
        streams[name].advance()
    loads["conv_first"].wait()
    loads["image"].wait()
    r["product"][...] = conv_back().reshape(IMAGE_ROWS, W, C)

    def first_row(i, sums):
        unit_one = unit(r["img"][i].astype(full), "one")
        normed = unit_one * vec["gain_one"] + vec["bias_one"]
        grad = r["product"][i] * silu_slope_of(normed)
        r["product"][i] = grad
        return sums[0] + column_sum(grad), sums[1] + column_sum(grad * unit_one)

    plain, crossed = lax.fori_loop(0, IMAGE_ROWS, first_row, nothing)
    gains["one"], biases["one"] = crossed, plain
    r["tile"][2] = sums_tile(plain * vec["gain_one"], crossed * vec["gain_one"])
    tiles = send_tile(2, r["tile"].at[2], r["window"].at[2], 0)
    rows = [
        gains["one"],
        gains["two"],
        gains["three"],
        biases["one"],
        biases["two"],
        biases["three"],
        conv_bias_one,
        conv_bias_two,
        query_sum,
        value_sum,
        word_sum[0],
        word_sum[1],
        up_sum,
        jnp.zeros((1, C), full),
        scale_grad,
        shift_grad,
    ]
    for i, values in enumerate(rows):
        r["own_rows"][i : i + 1, :] = values
    row_copies = send_tile(3, r["own_rows"], r["band_rows"], 0)
    loads["act_one"].wait()
    sibling["act1"].wait()
    sibling["shifts_one"].wait()
    conv_grads("first", "act1", "sib_act1", "sib_shifts_one")
    for copy in tiles:
        copy.wait()
    means = item_means(r["window"].at[2])
    offset_one, slope_one = means[0:1] * vec["scale_one"], means[1:2] * vec["scale_one"]
    ratio = vec["gain_one"] * vec["scale_one"]

    def image_row(i, carry):
        unit_one = unit(r["img"][i].astype(full), "one")
        values = r["part_two"][i + 1] + r["product"][i] * ratio - offset_one - unit_one * slope_one
        r["image_grad"][i] = values
        return carry

    lax.fori_loop(0, IMAGE_ROWS, image_row, 0)

    for copy in row_copies:
        copy.wait()
    total = jnp.zeros((16, C), full)
    for b in range(SPAN):
        total = total + r["band_rows"][b]
    r["half_rows"][0:16, :] = total
    for b in range(SPAN):
        r["half_rows"][16 + 2 * b : 18 + 2 * b, :] = r["band_rows"][b, 14:16, :]
    far_copy = remote(
        r["half_rows"], r["far_rows"], r["small_send"].at[0], r["small_recv"].at[0], partner["far"]
    )
    far_copy.start()
    for name in ("second0", "second1", "second2", "proj", "qkv", "text0", "text1"):
        streams[name].advance()
    loads["text_weight"].wait()

    def caption_columns(n, carry):
        columns = pl.ds(pl.multiple_of(n * C, C), C)
        r["caption_grad"][:, columns] = dot_last(r["joined_words"][...], r["text_w"][columns, :])
        return carry

    lax.fori_loop(0, EMB // C, caption_columns, 0)
    far_copy.wait()
    first_half = jnp.where(place["far"] == 0, r["half_rows"][16:32, :], r["far_rows"][16:32, :])
    other_half = jnp.where(place["far"] == 0, r["far_rows"][16:32, :], r["half_rows"][16:32, :])
    r["group_rows"][0:16, :] = r["half_rows"][0:16, :] + r["far_rows"][0:16, :]
    r["group_rows"][16:32, :] = first_half
    r["group_rows"][32:48, :] = other_half
    slots = r["slot_of_band"].shape[0]
    for k in range(2):
        table = jnp.zeros((slots, C), full)
        for b in range(2 * SPAN):
            values = r["group_rows"][16 + 2 * b + k : 17 + 2 * b + k, :]
            table = table + jnp.where(r["slot_of_band"][:, b * 128 : b * 128 + 1] > 0.0, values, 0.0)
        r["own_table"][slots * k : slots * (k + 1), :] = table
    r["own_table"][2 * slots :, :] = r["group_rows"][0:16, :]
    group_copy = remote(
        r["own_table"],
        r["other_table"],
        r["small_send"].at[1],
        r["small_recv"].at[1],
        partner["group"],
    )
    group_copy.start()
    share_copy = remote(
        r["silu_share"],
        r["other_share"],
        r["small_send"].at[2],
        r["small_recv"].at[2],
        partner["group"],
    )
    share_copy.start()

    for _ in range(LANDINGS + 2):
        for stream in streams.values():
            if stream.step < LANDINGS + 2:
                stream.advance()
    group_copy.wait()
    share_copy.wait()

    def write(name, target, first_row, rows, first_column):
        columns = STREAMS[name][1]
        for side, source in ((group, "joined_"), (1 - group, "whole_")):
            for k in range(2):
                target[
                    pl.ds(pl.multiple_of(first_row + side * rows, rows), rows),
                    first_column + k * columns : first_column + (k + 1) * columns,
                ] = r[source + name][k].astype(full)

    for j in range(3):
        write(f"first{j}", r["conv_first_grad"], j * 96, 48, 0)
        write(f"second{j}", r["conv_second_grad"], j * 96, 48, 0)
    for j in range(2):
        write(f"text{j}", r["text_grad"], j * 64, 32, 0)
    write("qkv", r["qkv_grad"], 0, 16, 0)
    write("proj", r["proj_grad"], 0, 16, 0)


def silu_slope_of(source):
    sigma = 1.0 / (1.0 + jnp.exp(-source))
    return sigma * (1.0 + source * (1.0 - sigma))


def back(ident, vectors, slot_of_band, silu_share, anywhere):
    low, full = jnp.bfloat16, jnp.float32
    pixels = IMAGE_ROWS * W
    vmem = pl.BlockSpec(memory_space=pltpu.VMEM)
    slots = slot_of_band.shape[0]
    outs = {
        "result": ((pixels, C), low),
        "image_grad": ((IMAGE_ROWS, W, C), full),
        "caption_grad": ((TEXT, EMB), full),
        "conv_first_grad": ((288, C), full),
        "conv_second_grad": ((288, C), full),
        "qkv_grad": ((32, 3 * C), full),
        "text_grad": ((128, 2 * C), full),
        "proj_grad": ((32, C), full),
        "own_table": ((2 * slots + 16, C), full),
        "other_table": ((2 * slots + 16, C), full),
        "other_share": (silu_share.shape, low),
    }
    padded = (IMAGE_ROWS + 2, W, C)
    scratch = {
        "heads": ((HEADS, pixels, 4 * HEAD), low),
        "head_words": ((HEADS, TEXT, 2 * HEAD), low),
        "joined": ((pixels, 4 * C), low),
        "joined_words": ((TEXT, 2 * C), low),
        "mid": (padded, full),
        "part_two": (padded, full),
        "part_one": (padded, full),
        "hid": (padded, full),
        "product": ((IMAGE_ROWS, W, C), full),
        "img": ((IMAGE_ROWS, W, C), low),
        "up": ((pixels, C), low),
        "act1": ((pixels + 2 * W, C), low),
        "act2": ((pixels + 2 * W, C), low),
        "act3": ((pixels, C), low),
        "cap": ((TEXT, EMB), low),
        "conv_w": ((9 * C, C), low),
        "qkv_w": ((C, 3 * C), low),
        "proj_w": ((C, C), low),
        "text_w": ((EMB, 2 * C), low),
        "sib_up": ((pixels, C // 2), low),
        "sib_act1": ((pixels + 2 * W, C), low),
        "sib_act2": ((pixels + 2 * W, C), low),
        "sib_act3": ((pixels, C), low),
        "sib_cap": ((TEXT, EMB), low),
        "sib_attended": ((pixels, C), low),
        "sib_qkv": ((pixels, 3 * C // 2), low),
        "sib_words": ((TEXT, C), low),
        "sib_shifts_one": ((3, IMAGE_ROWS, W, C // 2), low),
        "sib_shifts_two": ((3, IMAGE_ROWS, W, C // 2), low),
        "shifts": ((3,) + padded, low),
        "blocks": ((C, C), low),
        "tile": ((3, 8, C), full),
        "window": ((3, SPAN, 8, C), full),
        "own_rows": ((16, C), full),
        "band_rows": ((SPAN, 16, C), full),
        "half_rows": ((32, C), full),
        "far_rows": ((32, C), full),
        "group_rows": ((48, C), full),
    }
    for name, (rows, columns, order) in STREAMS.items():
        scratch["grad_" + name] = ((2,) * 5 + (rows, columns), low)
        for step in range(LANDINGS):
            scratch[f"landing_{name}_{step}"] = ((2,) * (4 - step) + (rows, columns), low)
        scratch["joined_" + name] = ((2, rows, columns), low)
        scratch["whole_" + name] = ((2, rows, columns), low)
    semaphores = {
        "swap_send": (2, SPAN),
        "swap_recv": (2, SPAN),
        "load_sem": (14,),
        "sib_send": (10,),
        "sib_recv": (10,),
        "edge_send": (3, 2),
        "edge_recv": (3, 2),
        "tile_send": (4, SPAN),
        "tile_recv": (4, SPAN),
        "fold_send": (len(STREAMS), LANDINGS + 2),
        "fold_recv": (len(STREAMS), LANDINGS + 2),
        "small_send": (3,),
        "small_recv": (3,),
    }
    names = (
        ["vectors", "slot_of_band", "silu_share"]
        + list(anywhere)
        + list(outs)
        + list(scratch)
        + list(semaphores)
    )
    outcome = pl.pallas_call(
        functools.partial(back_kernel, names),
        out_shape=tuple(jax.ShapeDtypeStruct(*o) for o in outs.values()),
        in_specs=[vmem] * 3 + [pl.BlockSpec(memory_space=pl.ANY)] * len(anywhere),
        out_specs=(vmem,) * len(outs),
        scratch_shapes=[pltpu.VMEM(*s) for s in scratch.values()]
        + [pltpu.SemaphoreType.DMA(s) for s in semaphores.values()],
        compiler_params=pltpu.CompilerParams(
            collective_id=ident, has_side_effects=True, vmem_limit_bytes=60 << 20
        ),
        name="back",
    )(vectors, slot_of_band, silu_share, *anywhere.values())
    return dict(zip(outs, outcome))


def blocks_of(rows):
    return rows.reshape(rows.shape[0], NORM_GROUPS, -1)


def spread(values):
    return jnp.repeat(values, C // NORM_GROUPS)


def shards(
    image,
    embedding,
    caption,
    item_of_band,
    out_grad,
    norm_gains,
    norm_biases,
    conv_first,
    conv_second,
    conv_biases,
    embed_weight,
    embed_bias,
    qkv_weight,
    qv_bias,
    text_weight,
    text_bias,
    proj_weight,
    proj_bias,
):
    low = jnp.bfloat16
    full = jnp.float32
    pixels = image.shape[1]
    band_items = item_of_band[0]
    slots = band_items.shape[0]
    position = lax.axis_index("rows")
    my_item = band_items[position]
    slot_hot = (jnp.arange(slots) == my_item).astype(full)
    item_count = jnp.sum((band_items == my_item).astype(full)) * pixels * (C // NORM_GROUPS)
    reach = position + jnp.arange(-REACH, REACH + 1)
    near = (reach >= 0) & (reach < slots)
    near = near & (band_items[jnp.clip(reach, 0, slots - 1)] == my_item)
    keep = jnp.concatenate(
        [
            jnp.full((W, 1), near[REACH - 1]),
            jnp.full((pixels, 1), True),
            jnp.full((W, 1), near[REACH + 1]),
        ]
    )
    own_lead = jnp.logical_not(near[REACH - 1])

    def totals(ident, first, second, edges=None):
        sums = jnp.stack([jnp.sum(blocks_of(first), axis=(0, 2)), jnp.sum(blocks_of(second), axis=(0, 2))])
        tile = jnp.pad(sums, ((0, 6), (0, 128 - NORM_GROUPS)))
        if edges is not None:
            outcome = exchange(ident, slots, tile, (edges[:W], edges[-W:]))
        else:
            outcome = exchange(ident, slots, tile)
        summed = jnp.sum(jnp.where(near[:, None, None], outcome[0], 0.0), axis=0)
        summed = summed[:2, :NORM_GROUPS] / item_count
        return summed, outcome[1:]

    def stats(summed):
        scales = lax.rsqrt(summed[1] - summed[0] * summed[0] + epsilon)
        return spread(summed[0]), spread(scales)

    inputs = image[0].astype(full)
    summed, (above, below) = totals(0, inputs, inputs * inputs, image[0])
    means_one, scales_one = stats(summed)
    padded = jnp.concatenate([above, image[0], below]).astype(full)
    unit_padded = (padded - means_one) * scales_one
    normed_padded = unit_padded * norm_gains[0] + norm_biases[0]
    act_one_padded = jnp.where(keep, jax.nn.silu(normed_padded), 0.0).astype(low)
    unit_one = unit_padded[W:-W]
    normed_one = normed_padded[W:-W]
    taps_one = jnp.concatenate(taps_of(act_one_padded, False), axis=1)
    hidden_one = dot(taps_one, conv_first) + conv_biases[0]
    embed_silu = jax.nn.silu(embedding[0].astype(full)).astype(low)
    my_silu = dot(slot_hot.astype(low)[None], embed_silu).astype(low)
    modulation = dot(my_silu, embed_weight)[0] + embed_bias
    scale_part = modulation[:C]
    shift_part = modulation[C:]
    summed, (above, below) = totals(1, hidden_one, hidden_one * hidden_one, hidden_one)
    means_two, scales_two = stats(summed)
    hidden_padded = jnp.concatenate([above, hidden_one, below])
    unit_padded = (hidden_padded - means_two) * scales_two
    normed_padded = unit_padded * norm_gains[1] + norm_biases[1]
    shifted_padded = normed_padded * (1.0 + scale_part) + shift_part
    act_two_padded = jnp.where(keep, jax.nn.silu(shifted_padded), 0.0).astype(low)
    unit_two = unit_padded[W:-W]
    normed_two = normed_padded[W:-W]
    shifted = shifted_padded[W:-W]
    taps_two = jnp.concatenate(taps_of(act_two_padded, False), axis=1)
    middle = inputs + dot(taps_two, conv_second) + conv_biases[1]
    summed, _ = totals(2, middle, middle * middle)
    means_three, scales_three = stats(summed)
    unit_three = (middle - means_three) * scales_three
    act_three = (unit_three * norm_gains[2] + norm_biases[2]).astype(low)
    projected = dot(act_three, qkv_weight)
    queries = (projected[:, :C] + qv_bias[:C]).astype(low)
    keys_values = jnp.concatenate(
        [projected[:, C : 2 * C], projected[:, 2 * C :] + qv_bias[C:]], axis=1
    ).astype(low)
    captions = caption[0, 0]
    text_kv = lax.cond(
        own_lead,
        lambda: (dot(captions, text_weight) + text_bias).astype(low),
        lambda: jnp.zeros((TEXT, 2 * C), low),
    )
    upstream = out_grad[0]
    upstream_float = upstream.astype(full)
    attended_grad = dot_last(upstream, proj_weight).astype(low)
    group = lax.axis_index("items")
    groups = lax.axis_size("items")
    if slots == 2 * SPAN and groups == 2 and HEADS == SPAN:
        outcome, outcome_text = attention_by_head(
            band_items, position, queries, keys_values, text_kv, attended_grad
        )
        constants = {
            "mean_one": means_one,
            "scale_one": scales_one,
            "gain_one": norm_gains[0],
            "bias_one": norm_biases[0],
            "mean_two": means_two,
            "scale_two": scales_two,
            "gain_two": norm_gains[1],
            "bias_two": norm_biases[1],
            "mean_three": means_three,
            "scale_three": scales_three,
            "gain_three": norm_gains[2],
            "bias_three": norm_biases[2],
            "stretch": 1.0 + scale_part,
            "shift": shift_part,
            "proj_bias": proj_bias,
            "keep_above": jnp.full((C,), near[REACH - 1]),
            "keep_below": jnp.full((C,), near[REACH + 1]),
            "per_item": jnp.full((C,), 1.0 / item_count),
        }
        halves = band_items.reshape(2, SPAN)[position // SPAN]
        vectors = jnp.concatenate(
            [jnp.stack([constants[name].astype(full) for name in VECTORS])]
            + [jnp.zeros((VECTOR_ROWS - len(VECTORS), C), full)]
            + [jnp.broadcast_to((halves == my_item).astype(full)[:, None], (SPAN, C))]
        )
        slot_of_band = (jnp.arange(slots)[:, None] == band_items[None, :]).astype(full)
        row_share = EMB // lax.axis_size("rows")
        silu_share = lax.dynamic_slice_in_dim(embed_silu, position * row_share, row_share, 1)
        by_row = (-1, W, C)
        out = back(
            8,
            vectors,
            jnp.repeat(slot_of_band, 128, axis=1),
            silu_share,
            {
                "pieces": outcome,
                "words": outcome_text,
                "middle": middle.reshape(by_row),
                "qkv_weight": qkv_weight,
                "proj_weight": proj_weight,
                "upstream": upstream,
                "act_three": act_three,
                "caption": captions,
                "conv_second": conv_second,
                "conv_first": conv_first,
                "hidden": hidden_padded.reshape(by_row),
                "act_two": act_two_padded,
                "act_one": act_one_padded,
                "image": image.reshape(by_row),
                "text_weight": text_weight,
            },
        )
        own_table = out["own_table"][: 2 * slots].reshape(2, slots, C).astype(low)
        other_table = out["other_table"][: 2 * slots].reshape(2, slots, C).astype(low)
        tables = jnp.stack([own_table, other_table])
        shares = jnp.stack([silu_share, out["other_share"]])
        embed_weight_grad = jnp.concatenate(
            [
                lax.dot_general(
                    shares, tables[:, k], (((0, 1), (0, 1)), ((), ())), preferred_element_type=full
                )
                for k in range(2)
            ],
            axis=1,
        )
        embed_bias_grad = jnp.sum(tables.astype(full), axis=(0, 2)).reshape(-1)
        embedding_grad = (
            dot_last(own_table[0], embed_weight[:, :C]) + dot_last(own_table[1], embed_weight[:, C:])
        ) * silu_slope(embedding[0].astype(full))
        sums = out["own_table"][2 * slots :] + out["other_table"][2 * slots :]
        return (
            out["result"][None],
            out["image_grad"].reshape(1, pixels, C),
            embedding_grad[None],
            out["caption_grad"][None, None],
            sums[0:3],
            sums[3:6],
            out["conv_first_grad"],
            out["conv_second_grad"],
            sums[6:8],
            embed_weight_grad,
            embed_bias_grad,
            out["qkv_grad"],
            sums[8:10].reshape(-1),
            out["text_grad"],
            sums[10:12].reshape(-1),
            out["proj_grad"],
            sums[12],
        )
    attended_low, query_low, key_value_low, text_low = attention_by_band(
        band_items, position, queries, keys_values, text_kv, attended_grad
    )
    result = middle + dot(attended_low, proj_weight) + proj_bias
    proj_weight_grad = dot_first(attended_low, upstream)
    proj_bias_grad = jnp.sum(upstream_float, axis=0)
    qkv_grad = jnp.concatenate([query_low, key_value_low], axis=1)
    qkv_weight_grad = dot_first(act_three, qkv_grad)
    qv_bias_grad = jnp.sum(
        jnp.concatenate([query_low, key_value_low[:, C:]], axis=1).astype(full), axis=0
    )
    text_weight_grad = dot_first(captions, text_low)
    text_bias_grad = jnp.sum(text_low.astype(full), axis=0)
    caption_grad = dot_last(text_low, text_weight)[None, None]
    three_grad = dot_last(qkv_grad, qkv_weight)
    gain_three = jnp.sum(three_grad * unit_three, axis=0)
    bias_three = jnp.sum(three_grad, axis=0)

    def conv_back(padded, weight):
        views = jnp.stack(taps_of(padded, True))
        return jnp.einsum(
            "tpd,tcd->pc", views, weight.reshape(9, C, C), preferred_element_type=full
        )

    def norm_back(ident, grad_unit, unit_value, scales, base, with_edges=True):
        scaled = base + grad_unit * scales
        edges = jnp.concatenate([scaled, unit_value], axis=1) if with_edges else None
        summed, around = totals(ident, grad_unit, grad_unit * unit_value, edges)
        mean_grad, mean_cross = spread(summed[0]) * scales, spread(summed[1]) * scales
        if not with_edges:
            return scaled - mean_grad - unit_value * mean_cross
        both = jnp.concatenate([around[0], edges, around[1]])
        return both[:, :C] - mean_grad - both[:, C:] * mean_cross

    middle_padded = norm_back(3, three_grad * norm_gains[2], unit_three, scales_three, upstream_float)
    middle_grad = middle_padded[W:-W]
    low_padded = jnp.where(keep, middle_padded, 0.0).astype(low)
    hidden_two_low = low_padded[W:-W]
    conv_bias_two = jnp.sum(hidden_two_low.astype(full), axis=0)
    conv_second_grad = dot_first(taps_two, hidden_two_low)
    act_two_grad = conv_back(low_padded, conv_second)
    shifted_grad = act_two_grad * silu_slope(shifted)
    modulation_grad = jnp.concatenate(
        [jnp.sum(shifted_grad * normed_two, axis=0), jnp.sum(shifted_grad, axis=0)]
    )
    normed_two_grad = shifted_grad * (1.0 + scale_part)
    gain_two = jnp.sum(normed_two_grad * unit_two, axis=0)
    bias_two = jnp.sum(normed_two_grad, axis=0)
    hidden_back = norm_back(4, normed_two_grad * norm_gains[1], unit_two, scales_two, 0.0)
    low_padded = jnp.where(keep, hidden_back, 0.0).astype(low)
    hidden_one_low = low_padded[W:-W]
    conv_bias_one = jnp.sum(hidden_one_low.astype(full), axis=0)
    conv_first_grad = dot_first(taps_one, hidden_one_low)
    act_one_grad = conv_back(low_padded, conv_first)
    normed_one_grad = act_one_grad * silu_slope(normed_one)
    gain_one = jnp.sum(normed_one_grad * unit_one, axis=0)
    bias_one = jnp.sum(normed_one_grad, axis=0)
    image_grad = norm_back(
        5, normed_one_grad * norm_gains[0], unit_one, scales_one, middle_grad, False
    )
    group_hot = (jnp.arange(groups) == group).astype(full)
    tables = group_hot[:, None, None] * slot_hot[None, :, None] * modulation_grad
    vectors = jnp.concatenate(
        [
            gain_one,
            gain_two,
            gain_three,
            bias_one,
            bias_two,
            bias_three,
            conv_bias_one,
            conv_bias_two,
            qv_bias_grad,
            text_bias_grad,
            proj_bias_grad,
        ]
    )
    small = jnp.concatenate([tables.reshape(-1, C), vectors.reshape(-1, C)])
    row_share = EMB // lax.axis_size("rows")
    silu_share = lax.dynamic_slice_in_dim(embed_silu, position * row_share, row_share, 1)
    grads = (conv_first_grad, conv_second_grad, qkv_weight_grad, text_weight_grad, proj_weight_grad)
    grads = [g.astype(low) for g in grads]
    small = lax.psum(small.astype(low), ("rows", "items")).astype(full)
    tables_sum = small[: groups * slots * 2].reshape(groups, slots, 2 * C).astype(low)
    part = dot_first(silu_share, jnp.take(tables_sum, group, axis=0)).astype(low)
    matrices = [lax.psum_scatter(g, "rows", scatter_dimension=0, tiled=True) for g in grads]
    *matrices, embed_weight_grad = [
        lax.psum(m, "items").astype(full) for m in matrices + [part]
    ]
    vectors_sum = small[groups * slots * 2 :]
    modulation_low = jnp.take(tables_sum, group, axis=0)
    embed_bias_grad = jnp.sum(tables_sum.astype(full), axis=(0, 1))
    embedding_grad = dot_last(modulation_low, embed_weight) * silu_slope(embedding[0].astype(full))
    return (
        result.astype(low)[None],
        image_grad[None],
        embedding_grad[None],
        caption_grad,
        vectors_sum[0:3],
        vectors_sum[3:6],
        matrices[0],
        matrices[1],
        vectors_sum[6:8],
        embed_weight_grad,
        embed_bias_grad,
        matrices[2],
        vectors_sum[8:10].reshape(-1),
        matrices[3],
        vectors_sum[10:12].reshape(-1),
        matrices[4],
        vectors_sum[12],
    )


def solution(mesh):
    in_specs = (
        P("items", "rows", None),
        P("items", None, None),
        P("items", "rows", None, None),
        P("items", None),
        P("items", "rows", None),
        P(),
        P(),
        P(),
        P(),
        P(),
        P(),
        P(),
        P(),
        P(),
        P(),
        P(),
        P(),
        P(),
    )
    out_specs = (
        P("items", "rows", None),
        P("items", "rows", None),
        P("items", None, None),
        P("items", "rows", None, None),
        P(),
        P(),
        P("rows", None),
        P("rows", None),
        P(),
        P("rows", None),
        P(),
        P("rows", None),
        P(),
        P("rows", None),
        P(),
        P("rows", None),
        P(),
    )
    return jax.shard_map(shards, mesh=mesh, in_specs=in_specs, out_specs=out_specs, check_vma=False)
```

```python
import functools
import types
import typing

import jax
import jax.numpy as jnp
from jax import lax
from jax.experimental import pallas as pl
from jax.experimental.pallas import tpu as pltpu
from jax.sharding import PartitionSpec as P

C = 512
HEADS = 8
HEAD = 64
EMB = 2048
TEXT = 128
NORM_GROUPS = 32
W = 64
SPAN = 8
ROWS, ITEMS = "rows", "items"


epsilon = 1e-05


def from_behind(array, axis, by):
    length = lax.axis_size(axis)
    pairs = [(i, i + by) for i in range(length) if 0 <= i + by < length]
    return lax.ppermute(array, axis, pairs)


def as_sent(array):
    return jax.tree.map(lambda a: a.astype(jnp.bfloat16) if a.dtype == jnp.float32 else a, array)


def keep_state(state):
    return state


def silu_slope(source):
    sigma = jax.nn.sigmoid(source)
    return sigma * (1.0 + source * (1.0 - sigma))


def dot_first(left_side, right_side):
    return lax.dot_general(
        left_side, right_side, (((0,), (0,)), ((), ())), preferred_element_type=jnp.float32
    )


def dot_last(left_side, right_side):
    return lax.dot_general(
        left_side, right_side, (((1,), (1,)), ((), ())), preferred_element_type=jnp.float32
    )


def head_split(source):
    return source.reshape(source.shape[0], HEADS, HEAD)


def piece_scores(query_heads, key_piece, allowed):
    key_heads = head_split(key_piece[:, :C])
    scores = jnp.einsum(
        "qhd,khd->hqk", query_heads, key_heads, preferred_element_type=jnp.float32
    ) * HEAD ** (-0.5)
    return jnp.where(allowed[None, None, :], scores, -jnp.inf)


def piece_grads(query_heads, grad_heads, log_total, row_dots, key_piece, allowed):
    scores = piece_scores(query_heads, key_piece, allowed)
    weights = jnp.exp(scores - log_total[:, :, None])
    value_heads = head_split(key_piece[:, C:])
    weight_grad = jnp.einsum(
        "qhd,khd->hqk", grad_heads, value_heads, preferred_element_type=jnp.float32
    )
    score_grad = (weights * (weight_grad - row_dots[:, :, None])).astype(jnp.bfloat16)
    outcome = []
    key_heads = head_split(key_piece[:, :C])
    query_grad = jnp.einsum(
        "hqk,khd->qhd", score_grad, key_heads, preferred_element_type=jnp.float32
    ) * HEAD ** (-0.5)
    outcome.append(query_grad.reshape(query_grad.shape[0], C))
    key_grad = jnp.einsum(
        "hqk,qhd->khd", score_grad, query_heads, preferred_element_type=jnp.float32
    ) * HEAD ** (-0.5)
    value_grad = jnp.einsum(
        "hqk,qhd->khd", weights.astype(jnp.bfloat16), grad_heads, preferred_element_type=jnp.float32
    )
    outcome.append(jnp.concatenate([key_grad.reshape(-1, C), value_grad.reshape(-1, C)], axis=1))
    return tuple(outcome)


def source_masks(band_items, source, my_item, pixels):
    slots = band_items.shape[0]
    inside = (source >= 0) & (source < slots)
    clipped = jnp.clip(source, 0, slots - 1)
    source_item = band_items[clipped]
    before_item = band_items[jnp.maximum(clipped - 1, 0)]
    same_item = inside & (source_item == my_item)
    leading = same_item & ((clipped == 0) | (before_item != source_item))
    allowed = jnp.concatenate(
        [jnp.broadcast_to(same_item, (pixels,)), jnp.broadcast_to(leading, (TEXT,))]
    )
    return (allowed, same_item)


REACH = SPAN - 1
LOG2E = 1.4426950408889634
PIX = 512


def dot(left, right):
    return jnp.dot(left, right, preferred_element_type=jnp.float32)


def reach_of(here, slots):
    first = here < SPAN
    low = jnp.maximum(jnp.where(first, 0, SPAN), here - REACH)
    high = jnp.minimum(jnp.where(first, SPAN - 1, slots - 1), here + REACH)
    return low, high


def exchange_kernel(slots, with_edges, *refs):
    if with_edges:
        tile, top, bottom, window, above, below, send_sem, recv_sem, edge_send, edge_recv = refs
    else:
        tile, window, send_sem, recv_sem = refs
    here = lax.axis_index(ROWS)
    low, high = reach_of(here, slots)
    offsets = [o for o in range(-REACH, REACH + 1) if o != 0]

    def reached(offset):
        return (here + offset >= low) & (here + offset <= high)

    barrier = pltpu.get_barrier_semaphore()
    for o in offsets:

        @pl.when(reached(o))
        def _(o=o):
            pl.semaphore_signal(barrier, 1, device_id={ROWS: here + o})

    pl.semaphore_wait(barrier, high - low)

    def edge_copy(o):
        source, target, k = (top, below, 0) if o < 0 else (bottom, above, 1)
        return pltpu.make_async_remote_copy(
            source, target, edge_send.at[k], edge_recv.at[k], device_id={ROWS: here + o}
        )

    def tile_copy(o):
        return pltpu.make_async_remote_copy(
            tile,
            window.at[REACH - o],
            send_sem.at[REACH - o],
            recv_sem.at[REACH - o],
            device_id={ROWS: here + o},
        )

    if with_edges:
        for o in (-1, 1):

            @pl.when(reached(o))
            def _(o=o):
                edge_copy(o).start()

    for o in offsets:

        @pl.when(reached(o))
        def _(o=o):
            tile_copy(o).start()

        @pl.when(jnp.logical_not(reached(-o)))
        def _(o=o):
            window[REACH - o] = jnp.zeros_like(tile)

    window[REACH] = tile[...]
    if with_edges:

        @pl.when(jnp.logical_not(reached(-1)))
        def _():
            above[...] = jnp.zeros_like(above)

        @pl.when(jnp.logical_not(reached(1)))
        def _():
            below[...] = jnp.zeros_like(below)

    for o in offsets:

        @pl.when(reached(o))
        def _(o=o):
            tile_copy(o).wait_send()

        @pl.when(reached(-o))
        def _(o=o):
            tile_copy(o).wait_recv()

    if with_edges:
        for o in (-1, 1):

            @pl.when(reached(o))
            def _(o=o):
                edge_copy(o).wait_send()

            @pl.when(reached(-o))
            def _(o=o):
                edge_copy(o).wait_recv()


def exchange(ident, slots, tile, edges=None):
    vmem = pl.BlockSpec(memory_space=pltpu.VMEM)
    shapes = [jax.ShapeDtypeStruct((2 * REACH + 1,) + tile.shape, tile.dtype)]
    scratch = [pltpu.SemaphoreType.DMA((2 * REACH + 1,))] * 2
    operands = [tile]
    if edges is not None:
        shapes += [jax.ShapeDtypeStruct(e.shape, e.dtype) for e in edges]
        scratch += [pltpu.SemaphoreType.DMA((2,))] * 2
        operands += list(edges)
    return pl.pallas_call(
        functools.partial(exchange_kernel, slots, edges is not None),
        out_shape=tuple(shapes),
        in_specs=[vmem] * len(operands),
        out_specs=(vmem,) * len(shapes),
        scratch_shapes=scratch,
        compiler_params=pltpu.CompilerParams(collective_id=ident, has_side_effects=True),
        name=f"exchange_{ident}",
    )(*operands)


def swap_kernel(count, *refs):
    sources, targets = refs[:count], refs[count : 2 * count]
    send_sem, recv_sem, own_sem = refs[2 * count :]
    here = lax.axis_index(ROWS)
    base = (here // SPAN) * SPAN
    lane = here - base
    barrier = pltpu.get_barrier_semaphore()
    for o in range(1, SPAN):
        pl.semaphore_signal(barrier, 1, device_id={ROWS: base + lax.rem(lane + o, SPAN)})
    pl.semaphore_wait(barrier, SPAN - 1)
    copies = []
    for o in range(1, SPAN):
        other = lax.rem(lane + o, SPAN)
        for k in range(count):
            copies.append(
                pltpu.make_async_remote_copy(
                    sources[k].at[other],
                    targets[k].at[lane],
                    send_sem.at[k, o],
                    recv_sem.at[k, o],
                    device_id={ROWS: base + other},
                )
            )
    for copy in copies:
        copy.start()
    own = []
    for k in range(count):
        own.append(pltpu.make_async_copy(sources[k].at[lane], targets[k].at[lane], own_sem.at[k]))
        own[-1].start()
    for copy in own:
        copy.wait()
    for copy in copies:
        copy.wait()


def swap(ident, *arrays):
    anywhere = pl.BlockSpec(memory_space=pl.ANY)
    count = len(arrays)
    return pl.pallas_call(
        functools.partial(swap_kernel, count),
        out_shape=tuple(jax.ShapeDtypeStruct(a.shape, a.dtype) for a in arrays),
        in_specs=[anywhere] * count,
        out_specs=(anywhere,) * count,
        scratch_shapes=[
            pltpu.SemaphoreType.DMA((count, SPAN)),
            pltpu.SemaphoreType.DMA((count, SPAN)),
            pltpu.SemaphoreType.DMA((count,)),
        ],
        compiler_params=pltpu.CompilerParams(collective_id=ident, has_side_effects=True),
        name=f"swap_{ident}",
    )(*arrays)


def head_kernel(
    starts, ends, y_ref, t_ref, z_ref, zt_ref, xt, vx, tt, tvx, s_ref, p_ref, dk, dv, dkt, dvt
):
    low = jnp.bfloat16
    full = jnp.float32
    bands, pixels = y_ref.shape[0], y_ref.shape[1]
    text = t_ref.shape[1]
    scale = HEAD ** (-0.5)

    def widened(values, rows):
        lanes = lax.broadcasted_iota(jnp.int32, (rows, 2 * HEAD), 1)
        units = jnp.where(lanes < HEAD + 2, 1.0, 0.0).astype(low)
        return jnp.where(lanes < HEAD, values, units)

    def prepare(b, carry):
        block = y_ref[b]
        xt[b] = block.T
        vx[b] = widened(block[:, 2 * HEAD :], pixels)
        words = t_ref[b]
        tt[b] = words.T
        tvx[b] = widened(pltpu.roll(words.astype(full), HEAD, 1).astype(low), text)
        dk[b] = jnp.zeros((pixels, 2 * HEAD), full)
        dv[b] = jnp.zeros((pixels, 2 * HEAD), full)
        dkt[b] = jnp.zeros((text, 2 * HEAD), full)
        dvt[b] = jnp.zeros((text, 2 * HEAD), full)
        return carry

    lax.fori_loop(0, bands, prepare, 0)

    def one_row(columns):
        rows = lax.broadcasted_iota(jnp.int32, (16, columns), 0)
        return jnp.where(rows == 0, 1.0, 0.0).astype(low)

    ones_pixels = one_row(pixels)
    ones_text = one_row(text)
    zeros = jnp.zeros((HEAD, pixels), low)

    def query_band(i, carry):
        start, end = starts[i], ends[i]
        query_t = (xt[i, 0:HEAD, :].astype(full) * scale).astype(low)
        query_rhs = jnp.concatenate([zeros, query_t], 0)
        query_text = jnp.concatenate([query_t, zeros], 0)

        def score(j, top):
            scores = dot(y_ref[j, :, 0 : 2 * HEAD], query_rhs)
            s_ref[j] = scores
            return jnp.maximum(top, jnp.max(scores.reshape(pixels // 8, 8, pixels), axis=0))

        top = lax.fori_loop(start, end, score, jnp.full((8, pixels), -jnp.inf, full))
        scores = dot(t_ref[start], query_text)
        top = jnp.maximum(top, jnp.max(scores.reshape(text // 8, 8, pixels), axis=0))
        top = jnp.max(top, axis=0, keepdims=True)
        weights_text = jnp.exp2((scores - top) * LOG2E).astype(low)
        total = dot(jnp.concatenate([tt[start, HEAD:, :], ones_text], 0), weights_text)

        def gather(j, total):
            weights = jnp.exp2((s_ref[j] - top) * LOG2E).astype(low)
            p_ref[j] = weights
            values = jnp.concatenate([xt[j, 2 * HEAD : 3 * HEAD, :], ones_pixels], 0)
            return total + dot(values, weights)

        total = lax.fori_loop(start, end, gather, total)
        inverse = 1.0 / total[HEAD : HEAD + 1, :]
        attended = total[0:HEAD, :] * inverse
        grad = xt[i, 3 * HEAD :, :].astype(full)
        minus_dots = -jnp.sum(grad * attended, axis=0, keepdims=True) * inverse
        grad_scaled = (grad * inverse).astype(low)
        coarse = minus_dots.astype(low)
        fine = minus_dots - coarse.astype(full)
        rows = lax.broadcasted_iota(jnp.int32, (HEAD, pixels), 0)
        extra = jnp.where(rows == 0, coarse.astype(full), jnp.where(rows == 1, fine, 0.0))
        grad_rhs = jnp.concatenate([grad_scaled, extra.astype(low)], 0)
        grad_rows = jnp.concatenate([grad_scaled, zeros], 0).T
        query_rows = jnp.concatenate([query_t, zeros], 0).T

        def back(j, query_grad):
            weights = p_ref[j]
            steps = (weights.astype(full) * dot(vx[j], grad_rhs)).astype(low)
            dv[j] += dot(weights, grad_rows)
            dk[j] += dot(steps, query_rows)
            return query_grad + dot(xt[j, HEAD : 2 * HEAD, :], steps)

        steps = (weights_text.astype(full) * dot(tvx[start], grad_rhs)).astype(low)
        dvt[start] += dot(weights_text, grad_rows)
        dkt[start] += dot(steps, query_rows)
        query_grad = dot(tt[start, 0:HEAD, :], steps)
        query_grad = lax.fori_loop(start, end, back, query_grad)
        z_ref[i, :, 0 : 2 * HEAD] = jnp.concatenate(
            [attended.astype(low), (query_grad * scale).astype(low)], 0
        ).T
        return carry

    lax.fori_loop(0, bands, query_band, 0)

    def finish(b, carry):
        lanes = lax.broadcasted_iota(jnp.int32, (pixels, 2 * HEAD), 1)
        z_ref[b, :, 2 * HEAD :] = jnp.where(
            lanes < HEAD, dk[b], pltpu.roll(dv[b], HEAD, 1)
        ).astype(low)
        lanes = lax.broadcasted_iota(jnp.int32, (text, 2 * HEAD), 1)
        zt_ref[b] = jnp.where(lanes < HEAD, dkt[b], pltpu.roll(dvt[b], HEAD, 1)).astype(low)
        return carry

    lax.fori_loop(0, bands, finish, 0)


def one_head(starts, ends, pieces, words):
    bands, pixels, _ = pieces.shape
    text = words.shape[1]
    low, full = jnp.bfloat16, jnp.float32
    smem = pl.BlockSpec(memory_space=pltpu.SMEM)
    vmem = pl.BlockSpec(memory_space=pltpu.VMEM)
    return pl.pallas_call(
        head_kernel,
        out_shape=(
            jax.ShapeDtypeStruct(pieces.shape, low),
            jax.ShapeDtypeStruct(words.shape, low),
        ),
        in_specs=[smem, smem, vmem, vmem],
        out_specs=(vmem, vmem),
        scratch_shapes=[
            pltpu.VMEM((bands, 4 * HEAD, pixels), low),
            pltpu.VMEM((bands, pixels, 2 * HEAD), low),
            pltpu.VMEM((bands, 2 * HEAD, text), low),
            pltpu.VMEM((bands, text, 2 * HEAD), low),
            pltpu.VMEM((bands, pixels, pixels), full),
            pltpu.VMEM((bands, pixels, pixels), low),
            pltpu.VMEM((bands, pixels, 2 * HEAD), full),
            pltpu.VMEM((bands, pixels, 2 * HEAD), full),
            pltpu.VMEM((bands, text, 2 * HEAD), full),
            pltpu.VMEM((bands, text, 2 * HEAD), full),
        ],
        compiler_params=pltpu.CompilerParams(vmem_limit_bytes=56 << 20),
        name="one_head",
    )(starts, ends, pieces, words)


def by_head(*flat):
    split = [f.reshape(f.shape[0], HEADS, HEAD).transpose(1, 0, 2) for f in flat]
    return jnp.concatenate(split, axis=2)


def attention_by_head(band_items, position, queries, keys_values, text_kv, attended_grad):
    base = (position // SPAN) * SPAN
    items = lax.dynamic_slice_in_dim(band_items, base, SPAN)
    same = items[:, None] == items[None, :]
    column = jnp.arange(SPAN)
    starts = jnp.min(jnp.where(same, column[None, :], SPAN), axis=1).astype(jnp.int32)
    ends = jnp.max(jnp.where(same, column[None, :] + 1, 0), axis=1).astype(jnp.int32)
    pieces, words = swap(
        6,
        by_head(queries, keys_values[:, :C], keys_values[:, C:], attended_grad),
        by_head(text_kv[:, :C], text_kv[:, C:]),
    )
    return one_head(starts, ends, pieces, words)


def attention_by_band(band_items, position, queries, keys_values, text_kv, attended_grad):
    my_item = band_items[position]
    pixels = queries.shape[0]
    own_allowed, own_same = source_masks(band_items, position, my_item, pixels)
    packed = jnp.concatenate([keys_values, text_kv], axis=0)
    pieces = [(0, packed, own_allowed, own_same)]
    for distance in range(1, SPAN):
        for offset in (distance, -distance):
            arrived = from_behind(packed, ROWS, offset)
            allowed, same_item = source_masks(band_items, position - offset, my_item, pixels)
            pieces.append((offset, arrived, allowed, same_item))
    query_heads = head_split(queries)
    row_top = jnp.full((HEADS, pixels), -jnp.inf, jnp.float32)
    weight_sum = jnp.zeros((HEADS, pixels), jnp.float32)
    for offset, key_piece, allowed, same_item in pieces:

        def gather_scores(state, key_piece=key_piece, allowed=allowed):
            top_old, sum_old = state
            scores = piece_scores(query_heads, key_piece, allowed)
            top_new = jnp.maximum(top_old, jnp.max(scores, axis=2))
            sum_new = sum_old * jnp.exp(top_old - top_new) + jnp.sum(
                jnp.exp(scores - top_new[:, :, None]), axis=2
            )
            return (top_new, sum_new)

        row_top, weight_sum = lax.cond(same_item, gather_scores, keep_state, (row_top, weight_sum))
    log_total = row_top + jnp.log(weight_sum)
    attended = jnp.zeros((pixels, HEADS, HEAD), jnp.float32)
    for offset, key_piece, allowed, same_item in pieces:

        def add_values(totals, key_piece=key_piece, allowed=allowed):
            scores = piece_scores(query_heads, key_piece, allowed)
            weights = jnp.exp(scores - log_total[:, :, None]).astype(jnp.bfloat16)
            return totals + jnp.einsum(
                "hqk,khd->qhd",
                weights,
                head_split(key_piece[:, C:]),
                preferred_element_type=jnp.float32,
            )

        attended = lax.cond(same_item, add_values, keep_state, attended)
    attended_flat = attended.reshape(pixels, C)
    row_dots = jnp.sum(
        (attended_grad.astype(jnp.float32) * attended_flat).reshape(pixels, HEADS, HEAD), axis=2
    ).T
    grad_heads = head_split(attended_grad)
    query_grad = jnp.zeros((pixels, C), jnp.float32)
    packed_grad = jnp.zeros((pixels + TEXT, 2 * C), jnp.float32)
    zero_piece = jnp.zeros((pixels + TEXT, 2 * C), jnp.float32)
    for offset, key_piece, allowed, same_item in pieces:

        def grad_both(totals, key_piece=key_piece, allowed=allowed):
            outcome = piece_grads(query_heads, grad_heads, log_total, row_dots, key_piece, allowed)
            return (totals + outcome[0], outcome[1])

        def grad_none(totals):
            return (totals, zero_piece)

        query_grad, piece_grad = lax.cond(same_item, grad_both, grad_none, query_grad)
        if offset == 0:
            packed_grad = packed_grad + piece_grad
        else:
            packed_grad = packed_grad + from_behind(
                as_sent(piece_grad), ROWS, -offset
            ).astype(jnp.float32)
    packed_low = packed_grad.astype(jnp.bfloat16)
    return (
        attended_flat.astype(jnp.bfloat16),
        query_grad.astype(jnp.bfloat16),
        packed_low[:pixels],
        packed_low[pixels:],
    )


def taps_of(rows, reverse):
    padded = rows.reshape(-1, W, rows.shape[1])
    row_list = [padded[:-2], padded[1:-1], padded[2:]]
    if reverse:
        row_list = row_list[::-1]
    zero_column = jnp.zeros_like(row_list[0][:, :1])
    views = []
    for row_view in row_list:
        left_view = jnp.concatenate([zero_column, row_view[:, :-1]], axis=1)
        right_view = jnp.concatenate([row_view[:, 1:], zero_column], axis=1)
        view_list = [left_view, row_view, right_view]
        if reverse:
            view_list = view_list[::-1]
        views = views + view_list
    return [view.reshape(-1, rows.shape[1]) for view in views]


class Vectors(typing.NamedTuple):
    mean_one: jax.Array
    scale_one: jax.Array
    gain_one: jax.Array
    bias_one: jax.Array
    mean_two: jax.Array
    scale_two: jax.Array
    gain_two: jax.Array
    bias_two: jax.Array
    mean_three: jax.Array
    scale_three: jax.Array
    gain_three: jax.Array
    bias_three: jax.Array
    stretch: jax.Array
    shift: jax.Array
    proj_bias: jax.Array
    keep_above: jax.Array
    keep_below: jax.Array
    per_item: jax.Array


def grouped(names, refs):
    found, position = types.SimpleNamespace(), 0
    for name, count in names:
        if count is None:
            setattr(found, name, refs[position])
            position += 1
        else:
            setattr(found, name, refs[position : position + count])
            position += count
    return found


def call_named(kernel, ident, inputs, anywhere, outs, scratch, semaphores):
    names = [(name, None) for name in [*inputs, *anywhere, *outs]]
    buffers = []
    for name, entry in scratch.items():
        many = isinstance(entry, list)
        names.append((name, len(entry) if many else None))
        buffers += [pltpu.VMEM(*e) for e in (entry if many else [entry])]
    names += [(name, None) for name in semaphores]
    vmem = pl.BlockSpec(memory_space=pltpu.VMEM)
    outcome = pl.pallas_call(
        functools.partial(kernel, names),
        out_shape=tuple(jax.ShapeDtypeStruct(*o) for o in outs.values()),
        in_specs=[vmem] * len(inputs) + [pl.BlockSpec(memory_space=pl.ANY)] * len(anywhere),
        out_specs=(vmem,) * len(outs),
        scratch_shapes=buffers + [pltpu.SemaphoreType.DMA(s) for s in semaphores.values()],
        compiler_params=pltpu.CompilerParams(
            collective_id=ident, has_side_effects=True, vmem_limit_bytes=60 << 20
        ),
        name=kernel.__name__,
    )(*inputs.values(), *anywhere.values())
    return types.SimpleNamespace(**dict(zip(outs, outcome)))


VECTOR_ROWS = 24
FAR, NEAR, SIDE, CORE, GROUP = range(5)
CROSS = (FAR, NEAR, SIDE)
SIDE_FIRST = (SIDE, GROUP, NEAR, FAR)
GROUP_FIRST = (GROUP, NEAR, SIDE, FAR)
NEAR_FIRST = (NEAR, SIDE, GROUP, FAR)
STREAMS = (
    (48, C // 2, SIDE_FIRST),
    (48, C // 2, GROUP_FIRST),
    (48, C // 2, NEAR_FIRST),
    (48, C // 2, SIDE_FIRST),
    (48, C // 2, GROUP_FIRST),
    (48, C // 2, NEAR_FIRST),
    (32, C, SIDE_FIRST),
    (32, C, NEAR_FIRST),
    (16, 3 * C // 2, GROUP_FIRST),
    (16, C // 2, GROUP_FIRST),
)
FIRST_CONV, SECOND_CONV, WORDS, QKV, PROJ = 0, 3, 6, 8, 9
LANDINGS = 4
IMAGE_ROWS = 8


def back_kernel(names, *refs):
    low, full = jnp.bfloat16, jnp.float32
    r = grouped(names, refs)
    row = lax.axis_index(ROWS)
    group = lax.axis_index(ITEMS)
    lane = row % SPAN
    base = row - lane
    place = [row // 8, (row // 4) % 2, (row // 2) % 2, row % 2, group]
    partner = [{ROWS: row + (1 - 2 * place[d]) * (8 >> d)} for d in range(CORE + 1)]
    partner.append({ITEMS: 1 - group})
    core = place[CORE]
    peers = [{ROWS: base + (lane + o) % SPAN} for o in range(1, SPAN)]

    barrier = pltpu.get_barrier_semaphore()
    for target in peers + [partner[FAR], partner[GROUP]]:
        pl.semaphore_signal(barrier, 1, device_id=target)
    pl.semaphore_wait(barrier, SPAN + 1)

    def remote(source, target, send, recv, device):
        return pltpu.make_async_remote_copy(source, target, send, recv, device_id=device)

    swaps = []
    for o in range(1, SPAN):
        other = (lane + o) % SPAN
        for k, (source, target) in enumerate(((r.pieces, r.heads), (r.words, r.head_words))):
            swaps.append(
                remote(
                    source.at[other],
                    target.at[lane],
                    r.swap_send.at[k, o],
                    r.swap_recv.at[k, o],
                    peers[o - 1],
                )
            )
    for copy in swaps:
        copy.start()

    loads = types.SimpleNamespace()

    def load(k, source, target):
        copy = pltpu.make_async_copy(source, target, r.load_sem.at[k])
        copy.start()
        return copy

    loads.own = load(0, r.pieces.at[lane], r.heads.at[lane])
    loads.own_words = load(1, r.words.at[lane], r.head_words.at[lane])
    loads.middle = load(2, r.middle, r.mid.at[1 : IMAGE_ROWS + 1])
    loads.qkv_weight = load(3, r.qkv_weight, r.qkv_w)
    loads.proj_weight = load(4, r.proj_weight, r.proj_w)
    loads.upstream = load(5, r.upstream, r.up)
    loads.act_three = load(6, r.act_three, r.act3)
    loads.caption = load(7, r.caption, r.cap)
    loads.conv_second = load(8, r.conv_second, r.conv_w)
    loads.hidden = load(9, r.hidden, r.hid)
    loads.act_two = load(10, r.act_two, r.act2)
    loads.act_one = load(11, r.act_one, r.act1)
    loads.image = load(12, r.image, r.img)
    loads.text_weight = load(13, r.text_weight, r.text_w)

    sibling = types.SimpleNamespace()

    def to_sibling(k, source, target):
        copy = remote(source, target, r.sib_send.at[k], r.sib_recv.at[k], partner[CORE])
        copy.start()
        return copy

    half = pl.ds(pl.multiple_of((1 - core) * (C // 2), C // 2), C // 2)
    sibling.upstream = to_sibling(0, r.upstream.at[:, half], r.sib_up)
    sibling.act3 = to_sibling(1, r.act_three, r.sib_act3)
    sibling.cap = to_sibling(2, r.caption, r.sib_cap)
    sibling.act2 = to_sibling(3, r.act_two, r.sib_act2)
    sibling.act1 = to_sibling(4, r.act_one, r.sib_act1)

    above, below = {ROWS: row - 1}, {ROWS: row + 1}
    has_above, has_below = lane > 0, lane < SPAN - 1

    def edges(k, source, target):
        up = remote(
            source[0], target.at[IMAGE_ROWS + 1], r.edge_send.at[k, 0], r.edge_recv.at[k, 0], above
        )
        down = remote(source[1], target.at[0], r.edge_send.at[k, 1], r.edge_recv.at[k, 1], below)
        return up, down

    def send_edges(pair):
        pl.when(has_above)(pair[0].start)
        pl.when(has_below)(pair[1].start)

    def wait_edges(pair):
        @pl.when(has_above)
        def _():
            pair[0].wait_send()
            pair[1].wait_recv()

        @pl.when(has_below)
        def _():
            pair[1].wait_send()
            pair[0].wait_recv()

    mid_edges = edges(0, (r.middle.at[0], r.middle.at[IMAGE_ROWS - 1]), r.mid)
    send_edges(mid_edges)

    def zero_edges(target):
        @pl.when(jnp.logical_not(has_above))
        def _():
            target[0] = jnp.zeros((W, C), full)

        @pl.when(jnp.logical_not(has_below))
        def _():
            target[IMAGE_ROWS + 1] = jnp.zeros((W, C), full)

    for target in (r.mid, r.part_two, r.part_one):
        zero_edges(target)

    vec = Vectors(*[r.vectors[i : i + 1, :] for i in range(len(Vectors._fields))])
    norm_one = (vec.mean_one, vec.scale_one)
    norm_two = (vec.mean_two, vec.scale_two)
    norm_three = (vec.mean_three, vec.scale_three)

    def send_tile(k, source, target, o_sem):
        copies = []
        for o in range(1, SPAN):
            copies.append(
                remote(
                    source,
                    target.at[lane],
                    r.tile_send.at[k, o],
                    r.tile_recv.at[k, o],
                    peers[o - 1],
                )
            )
        for copy in copies:
            copy.start()
        target[lane] = source[...]
        return copies

    rows_of_blocks = lax.broadcasted_iota(jnp.int32, (C, C), 0) // (C // NORM_GROUPS)
    columns_of_blocks = lax.broadcasted_iota(jnp.int32, (C, C), 1) // (C // NORM_GROUPS)
    r.blocks[...] = jnp.where(rows_of_blocks == columns_of_blocks, 1.0, 0.0).astype(low)

    def item_means(window):
        total = jnp.zeros((8, C), full)
        for b in range(SPAN):
            mask = r.vectors[VECTOR_ROWS + b : VECTOR_ROWS + b + 1, :]
            total = total + jnp.where(mask > 0.0, window[b], 0.0)
        total = total * vec.per_item
        coarse = total.astype(low)
        rest = total - coarse.astype(full)
        finer = rest.astype(low)
        finest = (rest - finer.astype(full)).astype(low)
        blocks = r.blocks[...]
        return dot(coarse, blocks) + dot(finer, blocks) + dot(finest, blocks)

    def sums_tile(first, second):
        rows = lax.broadcasted_iota(jnp.int32, (8, C), 0)
        return jnp.where(rows == 0, first, jnp.where(rows == 1, second, 0.0))

    class Stream:
        def __init__(self, k):
            self.k = k
            self.order = STREAMS[k][2]
            self.dims = [FAR, NEAR, SIDE, CORE, GROUP]
            self.step = 0
            self.copy = None

        def at(self, ref, d, index):
            return ref.at[(slice(None),) * self.dims.index(d) + (index,)]

        def start(self):
            self.launch(r.grads[self.k])

        def launch(self, ref):
            k, step = self.k, self.step
            if step < LANDINGS:
                d = self.order[step]
                self.copy = remote(
                    self.at(ref, d, 1 - place[d]),
                    r.landings[k * LANDINGS + step],
                    r.fold_send.at[k, step],
                    r.fold_recv.at[k, step],
                    partner[d],
                )
                self.mine = self.at(ref, d, place[d])
                self.dims.remove(d)
            elif step == LANDINGS:
                fin = r.folded[self.k]
                self.copy = remote(
                    ref.at[1 - core],
                    fin.at[core],
                    r.fold_send.at[k, step],
                    r.fold_recv.at[k, step],
                    partner[CORE],
                )
                self.mine = ref.at[core]
            else:
                self.copy = remote(
                    r.folded[self.k],
                    r.whole[self.k],
                    r.fold_send.at[k, step],
                    r.fold_recv.at[k, step],
                    partner[GROUP],
                )
            self.copy.start()

        def advance(self):
            self.copy.wait()
            if self.step < LANDINGS:
                landed, mine = r.landings[self.k * LANDINGS + self.step], self.mine
                lead = landed.shape[:-2]
                pieces = 1
                for n in lead:
                    pieces *= n

                def add(i, carry):
                    index = []
                    for n in reversed(lead):
                        index.insert(0, i % n)
                        i = i // n
                    index = tuple(index)
                    total = landed[index].astype(full) + mine[index].astype(full)
                    landed[index] = total.astype(low)
                    return carry

                lax.fori_loop(0, pieces, add, 0)
                self.step += 1
                self.launch(landed)
            elif self.step == LANDINGS:
                r.folded[self.k][core] = self.mine[...]
                self.step += 1
                self.launch(None)
            else:
                self.step += 1

    streams = [Stream(k) for k in range(len(STREAMS))]

    loads.own.wait()
    loads.own_words.wait()
    for copy in swaps:
        copy.wait()
    for h in range(0, HEADS, 2):
        for k in range(4):
            pair = [r.heads[h + i, :, k * HEAD : (k + 1) * HEAD] for i in range(2)]
            r.joined[:, k * C + h * HEAD : k * C + (h + 2) * HEAD] = jnp.concatenate(pair, axis=1)
        for k in range(2):
            pair = [r.head_words[h + i, :, k * HEAD : (k + 1) * HEAD] for i in range(2)]
            r.joined_words[:, k * C + h * HEAD : k * C + (h + 2) * HEAD] = jnp.concatenate(
                pair, axis=1
            )
    sibling.attended = to_sibling(5, r.joined.at[:, 0:C], r.sib_attended)
    three_half = C + (1 - core) * (3 * C // 2)
    sibling.qkv = to_sibling(
        6,
        r.joined.at[:, pl.ds(pl.multiple_of(three_half, C // 2), 3 * C // 2)],
        r.sib_qkv,
    )
    sibling.words = to_sibling(
        7,
        r.joined_words.at[:, pl.ds(pl.multiple_of((1 - core) * C, C), C)],
        r.sib_words,
    )
    for copy in (loads.middle, loads.qkv_weight, loads.proj_weight, loads.upstream):
        copy.wait()
    wait_edges(mid_edges)

    def pixel_block(ref, i, count=4):
        return ref[1 + i * count : 1 + (i + 1) * count].reshape(count * W, C)

    def unit(values, norm):
        return (values - norm[0]) * norm[1]

    def column_sum(values):
        return jnp.sum(values, axis=0, keepdims=True)

    plain = jnp.zeros((1, C), full)
    crossed = jnp.zeros((1, C), full)
    up_sum = jnp.zeros((1, C), full)
    for i in range(2):
        block = slice(i * 4 * W, (i + 1) * 4 * W)
        middle = pixel_block(r.mid, i)
        upstream = r.up[block, :].astype(full)
        result = middle + dot(r.joined[block, 0:C], r.proj_w[...]) + vec.proj_bias
        r.result[block, :] = result.astype(low)
        grad = dot_last(r.joined[block, C:], r.qkv_w[...])
        plain = plain + column_sum(grad)
        crossed = crossed + column_sum(grad * unit(middle, norm_three))
        up_sum = up_sum + column_sum(upstream)
        part = upstream + grad * (vec.gain_three * vec.scale_three)
        r.part_two[1 + i * 4 : 5 + i * 4] = part.reshape(4, W, C)
    gain_three, bias_three = crossed, plain
    r.tile[0] = sums_tile(plain * vec.gain_three, crossed * vec.gain_three)
    three_edges = edges(1, (r.part_two.at[1], r.part_two.at[IMAGE_ROWS]), r.part_two)
    send_edges(three_edges)
    tiles = send_tile(0, r.tile.at[0], r.window.at[0], 0)

    def mine_of(ref, start, size):
        return ref[:, pl.ds(pl.multiple_of(start, size if size % 256 else 256), size)]

    for copy in (sibling.upstream, sibling.act3, sibling.cap, sibling.attended, sibling.qkv, sibling.words):
        copy.wait()
    for copy in (loads.act_three, loads.caption):
        copy.wait()
    grad = dot_first(r.joined[:, 0:C], mine_of(r.up, core * (C // 2), C // 2))
    grad = grad + dot_first(r.sib_attended[...], r.sib_up[...])
    r.grads[PROJ][...] = grad.astype(low).reshape(r.grads[PROJ].shape)
    streams[PROJ].start()
    for n in range(3):
        own = mine_of(r.joined, C + core * (3 * C // 2) + n * (C // 2), C // 2)
        columns = slice(n * (C // 2), (n + 1) * (C // 2))
        grad = dot_first(r.act3[...], own)
        grad = grad + dot_first(r.sib_act3[...], r.sib_qkv[:, columns])
        r.grads[QKV][:, :, :, :, :, :, columns] = grad.astype(low).reshape(2, 2, 2, 2, 2, 16, C // 2)
    streams[QKV].start()

    def text_rows(s, carry):
        columns = pl.ds(pl.multiple_of(s * 128, 128), 128)
        own = mine_of(r.joined_words, core * C, C)
        grad = dot_first(r.cap[:, columns], own)
        grad = grad + dot_first(r.sib_cap[:, columns], r.sib_words[...])
        grad = grad.astype(low)
        index = (s // 8, (s // 4) % 2, (s // 2) % 2, s % 2)
        r.grads[WORDS][index] = grad[0:64].reshape(2, 32, C)
        r.grads[WORDS + 1][index] = grad[64:128].reshape(2, 32, C)
        return carry

    lax.fori_loop(0, 2 ** len(CROSS) * 2, text_rows, 0)
    streams[WORDS].start()
    streams[WORDS + 1].start()
    query_sum = column_sum(r.joined[:, C : 2 * C].astype(full))
    value_sum = column_sum(r.joined[:, 3 * C :].astype(full))
    word_sum = [column_sum(r.joined_words[:, k * C : (k + 1) * C].astype(full)) for k in range(2)]

    def spread_rows(i, values):
        rows = lax.broadcasted_iota(jnp.int32, (W, C), 0)
        right = jnp.where(rows == 0, 0.0, pltpu.roll(values, 1, 0))
        left = jnp.where(rows == W - 1, 0.0, pltpu.roll(values, W - 1, 0))
        r.shifts[0, i] = left.astype(low)
        r.shifts[1, i] = values.astype(low)
        r.shifts[2, i] = right.astype(low)

    def kept(i, values):
        keep = jnp.where(i == 0, vec.keep_above, jnp.where(i == IMAGE_ROWS + 1, vec.keep_below, 1.0))
        return jnp.where(keep > 0.0, values, 0.0)

    def conv_back():
        total = jnp.zeros((IMAGE_ROWS * W, C), full)
        for t in range(9):
            dy, dx = t // 3, t % 3
            view = r.shifts[dx, 2 - dy : 2 - dy + IMAGE_ROWS].reshape(IMAGE_ROWS * W, C)
            total = total + dot_last(view, r.conv_w[t * C : (t + 1) * C, :])
        return total

    def conv_grads(kind, own, other, landing):
        for t in range(9):
            dy, dx = t // 3, t % 3
            shifted = r.shifts[
                dx, 1 : IMAGE_ROWS + 1, :, pl.ds(pl.multiple_of(core * (C // 2), C // 2), C // 2)
            ].reshape(IMAGE_ROWS * W, C // 2)
            grad = dot_first(own[dy * W : dy * W + IMAGE_ROWS * W, :], shifted)
            grad = grad + dot_first(
                other[dy * W : dy * W + IMAGE_ROWS * W, :],
                landing[dx].reshape(IMAGE_ROWS * W, C // 2),
            )
            grad = grad.astype(low)
            begin = t * C
            while begin < (t + 1) * C:
                shard, within = divmod(begin, 288)
                stream, offset = divmod(within, 96)
                part, offset = divmod(offset, 48)
                size = min(48 - offset, (t + 1) * C - begin)
                target = r.grads[kind + stream]
                target[
                    shard // 8, (shard // 4) % 2, (shard // 2) % 2, shard % 2, part, offset : offset + size
                ] = grad[begin - t * C : begin - t * C + size]
                begin += size
        for j in range(3):
            streams[kind + j].start()

    for copy in tiles:
        copy.wait()
    wait_edges(three_edges)
    means = item_means(r.window.at[0])
    offset_three, slope_three = means[0:1] * vec.scale_three, means[1:2] * vec.scale_three

    def middle_row(i, bias):
        values = r.part_two[i] - offset_three - unit(r.mid[i], norm_three) * slope_three
        r.part_two[i] = values
        values = kept(i, values)
        spread_rows(i, values)
        inside = jnp.where((i > 0) & (i <= IMAGE_ROWS), 1.0, 0.0)
        return bias + inside * column_sum(values.astype(low).astype(full))

    conv_bias_two = lax.fori_loop(0, IMAGE_ROWS + 2, middle_row, jnp.zeros((1, C), full))
    shift_half = r.shifts.at[:, 1 : IMAGE_ROWS + 1, :, half]
    sibling.shifts_two = to_sibling(8, shift_half, r.sib_shifts_two)
    loads.conv_second.wait()
    loads.hidden.wait()
    r.product[...] = conv_back().reshape(IMAGE_ROWS, W, C)
    loads.conv_first = load(8, r.conv_first, r.conv_w)
    stretched = vec.stretch * vec.gain_two * vec.scale_two

    def second_row(i, sums):
        unit_two = unit(r.hid[i + 1], norm_two)
        normed = unit_two * vec.gain_two + vec.bias_two
        grad = r.product[i] * silu_slope_of(normed * vec.stretch + vec.shift)
        r.part_one[i + 1] = grad * stretched
        return sums[0] + column_sum(grad), sums[1] + column_sum(grad * unit_two)

    nothing = (jnp.zeros((1, C), full), jnp.zeros((1, C), full))
    plain, crossed = lax.fori_loop(0, IMAGE_ROWS, second_row, nothing)
    scale_grad = crossed * vec.gain_two + plain * vec.bias_two
    shift_grad = plain
    gain_two, bias_two = crossed * vec.stretch, plain * vec.stretch
    r.tile[1] = sums_tile(bias_two * vec.gain_two, gain_two * vec.gain_two)
    two_edges = edges(2, (r.part_one.at[1], r.part_one.at[IMAGE_ROWS]), r.part_one)
    send_edges(two_edges)
    tiles = send_tile(1, r.tile.at[1], r.window.at[1], 0)
    loads.act_two.wait()
    sibling.act2.wait()
    sibling.shifts_two.wait()
    conv_grads(SECOND_CONV, r.act2, r.sib_act2, r.sib_shifts_two)
    for copy in tiles:
        copy.wait()
    wait_edges(two_edges)
    means = item_means(r.window.at[1])
    offset_two, slope_two = means[0:1] * vec.scale_two, means[1:2] * vec.scale_two

    def hidden_row(i, bias):
        values = r.part_one[i] - offset_two - unit(r.hid[i], norm_two) * slope_two
        values = kept(i, values)
        spread_rows(i, values)
        inside = jnp.where((i > 0) & (i <= IMAGE_ROWS), 1.0, 0.0)
        return bias + inside * column_sum(values.astype(low).astype(full))

    conv_bias_one = lax.fori_loop(0, IMAGE_ROWS + 2, hidden_row, jnp.zeros((1, C), full))
    sibling.shifts_one = to_sibling(9, shift_half, r.sib_shifts_one)
    for k in (PROJ, QKV, WORDS, WORDS + 1):
        streams[k].advance()
    loads.conv_first.wait()
    loads.image.wait()
    r.product[...] = conv_back().reshape(IMAGE_ROWS, W, C)

    def first_row(i, sums):
        unit_one = unit(r.img[i].astype(full), norm_one)
        normed = unit_one * vec.gain_one + vec.bias_one
        grad = r.product[i] * silu_slope_of(normed)
        r.product[i] = grad
        return sums[0] + column_sum(grad), sums[1] + column_sum(grad * unit_one)

    plain, crossed = lax.fori_loop(0, IMAGE_ROWS, first_row, nothing)
    gain_one, bias_one = crossed, plain
    r.tile[2] = sums_tile(plain * vec.gain_one, crossed * vec.gain_one)
    tiles = send_tile(2, r.tile.at[2], r.window.at[2], 0)
    rows = [
        gain_one,
        gain_two,
        gain_three,
        bias_one,
        bias_two,
        bias_three,
        conv_bias_one,
        conv_bias_two,
        query_sum,
        value_sum,
        word_sum[0],
        word_sum[1],
        up_sum,
        jnp.zeros((1, C), full),
        scale_grad,
        shift_grad,
    ]
    for i, values in enumerate(rows):
        r.own_rows[i : i + 1, :] = values
    row_copies = send_tile(3, r.own_rows, r.band_rows, 0)
    loads.act_one.wait()
    sibling.act1.wait()
    sibling.shifts_one.wait()
    conv_grads(FIRST_CONV, r.act1, r.sib_act1, r.sib_shifts_one)
    for copy in tiles:
        copy.wait()
    means = item_means(r.window.at[2])
    offset_one, slope_one = means[0:1] * vec.scale_one, means[1:2] * vec.scale_one
    ratio = vec.gain_one * vec.scale_one

    def image_row(i, carry):
        unit_one = unit(r.img[i].astype(full), norm_one)
        values = r.part_two[i + 1] + r.product[i] * ratio - offset_one - unit_one * slope_one
        r.image_grad[i] = values
        return carry

    lax.fori_loop(0, IMAGE_ROWS, image_row, 0)

    for copy in row_copies:
        copy.wait()
    total = jnp.zeros((16, C), full)
    for b in range(SPAN):
        total = total + r.band_rows[b]
    r.half_rows[0:16, :] = total
    for b in range(SPAN):
        r.half_rows[16 + 2 * b : 18 + 2 * b, :] = r.band_rows[b, 14:16, :]
    far_copy = remote(
        r.half_rows, r.far_rows, r.small_send.at[0], r.small_recv.at[0], partner[FAR]
    )
    far_copy.start()
    for k in range(SECOND_CONV, len(STREAMS)):
        streams[k].advance()
    loads.text_weight.wait()

    def caption_columns(n, carry):
        columns = pl.ds(pl.multiple_of(n * C, C), C)
        r.caption_grad[:, columns] = dot_last(r.joined_words[...], r.text_w[columns, :])
        return carry

    lax.fori_loop(0, EMB // C, caption_columns, 0)
    far_copy.wait()
    first_half = jnp.where(place[FAR] == 0, r.half_rows[16:32, :], r.far_rows[16:32, :])
    other_half = jnp.where(place[FAR] == 0, r.far_rows[16:32, :], r.half_rows[16:32, :])
    r.group_rows[0:16, :] = r.half_rows[0:16, :] + r.far_rows[0:16, :]
    r.group_rows[16:32, :] = first_half
    r.group_rows[32:48, :] = other_half
    slots = r.slot_of_band.shape[0]
    for k in range(2):
        table = jnp.zeros((slots, C), full)
        for b in range(2 * SPAN):
            values = r.group_rows[16 + 2 * b + k : 17 + 2 * b + k, :]
            table = table + jnp.where(r.slot_of_band[:, b * 128 : b * 128 + 1] > 0.0, values, 0.0)
        r.own_table[slots * k : slots * (k + 1), :] = table
    r.own_table[2 * slots :, :] = r.group_rows[0:16, :]
    group_copy = remote(
        r.own_table,
        r.other_table,
        r.small_send.at[1],
        r.small_recv.at[1],
        partner[GROUP],
    )
    group_copy.start()
    share_copy = remote(
        r.silu_share,
        r.other_share,
        r.small_send.at[2],
        r.small_recv.at[2],
        partner[GROUP],
    )
    share_copy.start()

    for _ in range(LANDINGS + 2):
        for stream in streams:
            if stream.step < LANDINGS + 2:
                stream.advance()
    group_copy.wait()
    share_copy.wait()

    def write(stream, target, first_row):
        rows, columns = STREAMS[stream][:2]
        for side, source in ((group, r.folded[stream]), (1 - group, r.whole[stream])):
            for k in range(2):
                target[
                    pl.ds(pl.multiple_of(first_row + side * rows, rows), rows),
                    k * columns : (k + 1) * columns,
                ] = source[k].astype(full)

    for j in range(3):
        write(FIRST_CONV + j, r.conv_first_grad, j * 96)
        write(SECOND_CONV + j, r.conv_second_grad, j * 96)
    for j in range(2):
        write(WORDS + j, r.text_grad, j * 64)
    write(QKV, r.qkv_grad, 0)
    write(PROJ, r.proj_grad, 0)


def silu_slope_of(source):
    sigma = 1.0 / (1.0 + jnp.exp(-source))
    return sigma * (1.0 + source * (1.0 - sigma))


def back(ident, vectors, slot_of_band, silu_share, anywhere):
    low, full = jnp.bfloat16, jnp.float32
    pixels = IMAGE_ROWS * W
    vmem = pl.BlockSpec(memory_space=pltpu.VMEM)
    slots = slot_of_band.shape[0]
    outs = dict(
        result=((pixels, C), low),
        image_grad=((IMAGE_ROWS, W, C), full),
        caption_grad=((TEXT, EMB), full),
        conv_first_grad=((288, C), full),
        conv_second_grad=((288, C), full),
        qkv_grad=((32, 3 * C), full),
        text_grad=((128, 2 * C), full),
        proj_grad=((32, C), full),
        own_table=((2 * slots + 16, C), full),
        other_table=((2 * slots + 16, C), full),
        other_share=(silu_share.shape, low),
    )
    padded = (IMAGE_ROWS + 2, W, C)
    scratch = dict(
        heads=((HEADS, pixels, 4 * HEAD), low),
        head_words=((HEADS, TEXT, 2 * HEAD), low),
        joined=((pixels, 4 * C), low),
        joined_words=((TEXT, 2 * C), low),
        mid=(padded, full),
        part_two=(padded, full),
        part_one=(padded, full),
        hid=(padded, full),
        product=((IMAGE_ROWS, W, C), full),
        img=((IMAGE_ROWS, W, C), low),
        up=((pixels, C), low),
        act1=((pixels + 2 * W, C), low),
        act2=((pixels + 2 * W, C), low),
        act3=((pixels, C), low),
        cap=((TEXT, EMB), low),
        conv_w=((9 * C, C), low),
        qkv_w=((C, 3 * C), low),
        proj_w=((C, C), low),
        text_w=((EMB, 2 * C), low),
        sib_up=((pixels, C // 2), low),
        sib_act1=((pixels + 2 * W, C), low),
        sib_act2=((pixels + 2 * W, C), low),
        sib_act3=((pixels, C), low),
        sib_cap=((TEXT, EMB), low),
        sib_attended=((pixels, C), low),
        sib_qkv=((pixels, 3 * C // 2), low),
        sib_words=((TEXT, C), low),
        sib_shifts_one=((3, IMAGE_ROWS, W, C // 2), low),
        sib_shifts_two=((3, IMAGE_ROWS, W, C // 2), low),
        shifts=((3,) + padded, low),
        blocks=((C, C), low),
        tile=((3, 8, C), full),
        window=((3, SPAN, 8, C), full),
        own_rows=((16, C), full),
        band_rows=((SPAN, 16, C), full),
        half_rows=((32, C), full),
        far_rows=((32, C), full),
        group_rows=((48, C), full),
    )
    scratch.update(grads=[((2,) * 5 + s[:2], low) for s in STREAMS])
    scratch.update(landings=[((2,) * (4 - i) + s[:2], low) for s in STREAMS for i in range(LANDINGS)])
    scratch.update(folded=[((2,) + s[:2], low) for s in STREAMS])
    scratch.update(whole=[((2,) + s[:2], low) for s in STREAMS])
    semaphores = dict(
        swap_send=(2, SPAN),
        swap_recv=(2, SPAN),
        load_sem=(14,),
        sib_send=(10,),
        sib_recv=(10,),
        edge_send=(3, 2),
        edge_recv=(3, 2),
        tile_send=(4, SPAN),
        tile_recv=(4, SPAN),
        fold_send=(len(STREAMS), LANDINGS + 2),
        fold_recv=(len(STREAMS), LANDINGS + 2),
        small_send=(3,),
        small_recv=(3,),
    )
    inputs = dict(vectors=vectors, slot_of_band=slot_of_band, silu_share=silu_share)
    return call_named(
        back_kernel, ident, inputs, anywhere, outs, scratch, semaphores
    )
def blocks_of(rows):
    return rows.reshape(rows.shape[0], NORM_GROUPS, -1)


def spread(values):
    return jnp.repeat(values, C // NORM_GROUPS)


def shards(
    image,
    embedding,
    caption,
    item_of_band,
    out_grad,
    norm_gains,
    norm_biases,
    conv_first,
    conv_second,
    conv_biases,
    embed_weight,
    embed_bias,
    qkv_weight,
    qv_bias,
    text_weight,
    text_bias,
    proj_weight,
    proj_bias,
):
    low = jnp.bfloat16
    full = jnp.float32
    pixels = image.shape[1]
    band_items = item_of_band[0]
    slots = band_items.shape[0]
    position = lax.axis_index(ROWS)
    my_item = band_items[position]
    slot_hot = (jnp.arange(slots) == my_item).astype(full)
    item_count = jnp.sum((band_items == my_item).astype(full)) * pixels * (C // NORM_GROUPS)
    reach = position + jnp.arange(-REACH, REACH + 1)
    near = (reach >= 0) & (reach < slots)
    near = near & (band_items[jnp.clip(reach, 0, slots - 1)] == my_item)
    keep = jnp.concatenate(
        [
            jnp.full((W, 1), near[REACH - 1]),
            jnp.full((pixels, 1), True),
            jnp.full((W, 1), near[REACH + 1]),
        ]
    )
    own_lead = jnp.logical_not(near[REACH - 1])

    def totals(ident, first, second, edges=None):
        sums = jnp.stack([jnp.sum(blocks_of(first), axis=(0, 2)), jnp.sum(blocks_of(second), axis=(0, 2))])
        tile = jnp.pad(sums, ((0, 6), (0, 128 - NORM_GROUPS)))
        if edges is not None:
            outcome = exchange(ident, slots, tile, (edges[:W], edges[-W:]))
        else:
            outcome = exchange(ident, slots, tile)
        summed = jnp.sum(jnp.where(near[:, None, None], outcome[0], 0.0), axis=0)
        summed = summed[:2, :NORM_GROUPS] / item_count
        return summed, outcome[1:]

    def stats(summed):
        scales = lax.rsqrt(summed[1] - summed[0] * summed[0] + epsilon)
        return spread(summed[0]), spread(scales)

    inputs = image[0].astype(full)
    summed, (above, below) = totals(0, inputs, inputs * inputs, image[0])
    means_one, scales_one = stats(summed)
    padded = jnp.concatenate([above, image[0], below]).astype(full)
    unit_padded = (padded - means_one) * scales_one
    normed_padded = unit_padded * norm_gains[0] + norm_biases[0]
    act_one_padded = jnp.where(keep, jax.nn.silu(normed_padded), 0.0).astype(low)
    unit_one = unit_padded[W:-W]
    normed_one = normed_padded[W:-W]
    taps_one = jnp.concatenate(taps_of(act_one_padded, False), axis=1)
    hidden_one = dot(taps_one, conv_first) + conv_biases[0]
    embed_silu = jax.nn.silu(embedding[0].astype(full)).astype(low)
    my_silu = dot(slot_hot.astype(low)[None], embed_silu).astype(low)
    modulation = dot(my_silu, embed_weight)[0] + embed_bias
    scale_part = modulation[:C]
    shift_part = modulation[C:]
    summed, (above, below) = totals(1, hidden_one, hidden_one * hidden_one, hidden_one)
    means_two, scales_two = stats(summed)
    hidden_padded = jnp.concatenate([above, hidden_one, below])
    unit_padded = (hidden_padded - means_two) * scales_two
    normed_padded = unit_padded * norm_gains[1] + norm_biases[1]
    shifted_padded = normed_padded * (1.0 + scale_part) + shift_part
    act_two_padded = jnp.where(keep, jax.nn.silu(shifted_padded), 0.0).astype(low)
    unit_two = unit_padded[W:-W]
    normed_two = normed_padded[W:-W]
    shifted = shifted_padded[W:-W]
    taps_two = jnp.concatenate(taps_of(act_two_padded, False), axis=1)
    middle = inputs + dot(taps_two, conv_second) + conv_biases[1]
    summed, _ = totals(2, middle, middle * middle)
    means_three, scales_three = stats(summed)
    unit_three = (middle - means_three) * scales_three
    act_three = (unit_three * norm_gains[2] + norm_biases[2]).astype(low)
    projected = dot(act_three, qkv_weight)
    queries = (projected[:, :C] + qv_bias[:C]).astype(low)
    keys_values = jnp.concatenate(
        [projected[:, C : 2 * C], projected[:, 2 * C :] + qv_bias[C:]], axis=1
    ).astype(low)
    captions = caption[0, 0]
    text_kv = lax.cond(
        own_lead,
        lambda: (dot(captions, text_weight) + text_bias).astype(low),
        lambda: jnp.zeros((TEXT, 2 * C), low),
    )
    upstream = out_grad[0]
    upstream_float = upstream.astype(full)
    attended_grad = dot_last(upstream, proj_weight).astype(low)
    group = lax.axis_index(ITEMS)
    groups = lax.axis_size(ITEMS)
    if slots == 2 * SPAN and groups == 2 and HEADS == SPAN:
        outcome, outcome_text = attention_by_head(
            band_items, position, queries, keys_values, text_kv, attended_grad
        )
        constants = Vectors(
            mean_one=means_one,
            scale_one=scales_one,
            gain_one=norm_gains[0],
            bias_one=norm_biases[0],
            mean_two=means_two,
            scale_two=scales_two,
            gain_two=norm_gains[1],
            bias_two=norm_biases[1],
            mean_three=means_three,
            scale_three=scales_three,
            gain_three=norm_gains[2],
            bias_three=norm_biases[2],
            stretch=1.0 + scale_part,
            shift=shift_part,
            proj_bias=proj_bias,
            keep_above=jnp.full((C,), near[REACH - 1]),
            keep_below=jnp.full((C,), near[REACH + 1]),
            per_item=jnp.full((C,), 1.0 / item_count),
        )
        halves = band_items.reshape(2, SPAN)[position // SPAN]
        vectors = jnp.concatenate(
            [jnp.stack([values.astype(full) for values in constants])]
            + [jnp.zeros((VECTOR_ROWS - len(constants), C), full)]
            + [jnp.broadcast_to((halves == my_item).astype(full)[:, None], (SPAN, C))]
        )
        slot_of_band = (jnp.arange(slots)[:, None] == band_items[None, :]).astype(full)
        row_share = EMB // lax.axis_size(ROWS)
        silu_share = lax.dynamic_slice_in_dim(embed_silu, position * row_share, row_share, 1)
        by_row = (-1, W, C)
        out = back(
            8,
            vectors,
            jnp.repeat(slot_of_band, 128, axis=1),
            silu_share,
            dict(
                pieces=outcome,
                words=outcome_text,
                middle=middle.reshape(by_row),
                qkv_weight=qkv_weight,
                proj_weight=proj_weight,
                upstream=upstream,
                act_three=act_three,
                caption=captions,
                conv_second=conv_second,
                conv_first=conv_first,
                hidden=hidden_padded.reshape(by_row),
                act_two=act_two_padded,
                act_one=act_one_padded,
                image=image.reshape(by_row),
                text_weight=text_weight,
            ),
        )
        own_table = out.own_table[: 2 * slots].reshape(2, slots, C).astype(low)
        other_table = out.other_table[: 2 * slots].reshape(2, slots, C).astype(low)
        tables = jnp.stack([own_table, other_table])
        shares = jnp.stack([silu_share, out.other_share])
        embed_weight_grad = jnp.concatenate(
            [
                lax.dot_general(
                    shares, tables[:, k], (((0, 1), (0, 1)), ((), ())), preferred_element_type=full
                )
                for k in range(2)
            ],
            axis=1,
        )
        embed_bias_grad = jnp.sum(tables.astype(full), axis=(0, 2)).reshape(-1)
        embedding_grad = (
            dot_last(own_table[0], embed_weight[:, :C]) + dot_last(own_table[1], embed_weight[:, C:])
        ) * silu_slope(embedding[0].astype(full))
        sums = out.own_table[2 * slots :] + out.other_table[2 * slots :]
        return (
            out.result[None],
            out.image_grad.reshape(1, pixels, C),
            embedding_grad[None],
            out.caption_grad[None, None],
            sums[0:3],
            sums[3:6],
            out.conv_first_grad,
            out.conv_second_grad,
            sums[6:8],
            embed_weight_grad,
            embed_bias_grad,
            out.qkv_grad,
            sums[8:10].reshape(-1),
            out.text_grad,
            sums[10:12].reshape(-1),
            out.proj_grad,
            sums[12],
        )
    attended_low, query_low, key_value_low, text_low = attention_by_band(
        band_items, position, queries, keys_values, text_kv, attended_grad
    )
    result = middle + dot(attended_low, proj_weight) + proj_bias
    proj_weight_grad = dot_first(attended_low, upstream)
    proj_bias_grad = jnp.sum(upstream_float, axis=0)
    qkv_grad = jnp.concatenate([query_low, key_value_low], axis=1)
    qkv_weight_grad = dot_first(act_three, qkv_grad)
    qv_bias_grad = jnp.sum(
        jnp.concatenate([query_low, key_value_low[:, C:]], axis=1).astype(full), axis=0
    )
    text_weight_grad = dot_first(captions, text_low)
    text_bias_grad = jnp.sum(text_low.astype(full), axis=0)
    caption_grad = dot_last(text_low, text_weight)[None, None]
    three_grad = dot_last(qkv_grad, qkv_weight)
    gain_three = jnp.sum(three_grad * unit_three, axis=0)
    bias_three = jnp.sum(three_grad, axis=0)

    def conv_back(padded, weight):
        views = jnp.stack(taps_of(padded, True))
        return jnp.einsum(
            "tpd,tcd->pc", views, weight.reshape(9, C, C), preferred_element_type=full
        )

    def norm_back(ident, grad_unit, unit_value, scales, base, with_edges=True):
        scaled = base + grad_unit * scales
        edges = jnp.concatenate([scaled, unit_value], axis=1) if with_edges else None
        summed, around = totals(ident, grad_unit, grad_unit * unit_value, edges)
        mean_grad, mean_cross = spread(summed[0]) * scales, spread(summed[1]) * scales
        if not with_edges:
            return scaled - mean_grad - unit_value * mean_cross
        both = jnp.concatenate([around[0], edges, around[1]])
        return both[:, :C] - mean_grad - both[:, C:] * mean_cross

    middle_padded = norm_back(3, three_grad * norm_gains[2], unit_three, scales_three, upstream_float)
    middle_grad = middle_padded[W:-W]
    low_padded = jnp.where(keep, middle_padded, 0.0).astype(low)
    hidden_two_low = low_padded[W:-W]
    conv_bias_two = jnp.sum(hidden_two_low.astype(full), axis=0)
    conv_second_grad = dot_first(taps_two, hidden_two_low)
    act_two_grad = conv_back(low_padded, conv_second)
    shifted_grad = act_two_grad * silu_slope(shifted)
    modulation_grad = jnp.concatenate(
        [jnp.sum(shifted_grad * normed_two, axis=0), jnp.sum(shifted_grad, axis=0)]
    )
    normed_two_grad = shifted_grad * (1.0 + scale_part)
    gain_two = jnp.sum(normed_two_grad * unit_two, axis=0)
    bias_two = jnp.sum(normed_two_grad, axis=0)
    hidden_back = norm_back(4, normed_two_grad * norm_gains[1], unit_two, scales_two, 0.0)
    low_padded = jnp.where(keep, hidden_back, 0.0).astype(low)
    hidden_one_low = low_padded[W:-W]
    conv_bias_one = jnp.sum(hidden_one_low.astype(full), axis=0)
    conv_first_grad = dot_first(taps_one, hidden_one_low)
    act_one_grad = conv_back(low_padded, conv_first)
    normed_one_grad = act_one_grad * silu_slope(normed_one)
    gain_one = jnp.sum(normed_one_grad * unit_one, axis=0)
    bias_one = jnp.sum(normed_one_grad, axis=0)
    image_grad = norm_back(
        5, normed_one_grad * norm_gains[0], unit_one, scales_one, middle_grad, False
    )
    group_hot = (jnp.arange(groups) == group).astype(full)
    tables = group_hot[:, None, None] * slot_hot[None, :, None] * modulation_grad
    vectors = jnp.concatenate(
        [
            gain_one,
            gain_two,
            gain_three,
            bias_one,
            bias_two,
            bias_three,
            conv_bias_one,
            conv_bias_two,
            qv_bias_grad,
            text_bias_grad,
            proj_bias_grad,
        ]
    )
    small = jnp.concatenate([tables.reshape(-1, C), vectors.reshape(-1, C)])
    row_share = EMB // lax.axis_size(ROWS)
    silu_share = lax.dynamic_slice_in_dim(embed_silu, position * row_share, row_share, 1)
    grads = (conv_first_grad, conv_second_grad, qkv_weight_grad, text_weight_grad, proj_weight_grad)
    grads = [g.astype(low) for g in grads]
    small = lax.psum(small.astype(low), (ROWS, ITEMS)).astype(full)
    tables_sum = small[: groups * slots * 2].reshape(groups, slots, 2 * C).astype(low)
    part = dot_first(silu_share, jnp.take(tables_sum, group, axis=0)).astype(low)
    matrices = [lax.psum_scatter(g, ROWS, scatter_dimension=0, tiled=True) for g in grads]
    *matrices, embed_weight_grad = [
        lax.psum(m, ITEMS).astype(full) for m in matrices + [part]
    ]
    vectors_sum = small[groups * slots * 2 :]
    modulation_low = jnp.take(tables_sum, group, axis=0)
    embed_bias_grad = jnp.sum(tables_sum.astype(full), axis=(0, 1))
    embedding_grad = dot_last(modulation_low, embed_weight) * silu_slope(embedding[0].astype(full))
    return (
        result.astype(low)[None],
        image_grad[None],
        embedding_grad[None],
        caption_grad,
        vectors_sum[0:3],
        vectors_sum[3:6],
        matrices[0],
        matrices[1],
        vectors_sum[6:8],
        embed_weight_grad,
        embed_bias_grad,
        matrices[2],
        vectors_sum[8:10].reshape(-1),
        matrices[3],
        vectors_sum[10:12].reshape(-1),
        matrices[4],
        vectors_sum[12],
    )


def solution(mesh):
    in_specs = (
        P(ITEMS, ROWS, None),
        P(ITEMS, None, None),
        P(ITEMS, ROWS, None, None),
        P(ITEMS, None),
        P(ITEMS, ROWS, None),
        P(),
        P(),
        P(),
        P(),
        P(),
        P(),
        P(),
        P(),
        P(),
        P(),
        P(),
        P(),
        P(),
    )
    out_specs = (
        P(ITEMS, ROWS, None),
        P(ITEMS, ROWS, None),
        P(ITEMS, None, None),
        P(ITEMS, ROWS, None, None),
        P(),
        P(),
        P(ROWS, None),
        P(ROWS, None),
        P(),
        P(ROWS, None),
        P(),
        P(ROWS, None),
        P(),
        P(ROWS, None),
        P(),
        P(ROWS, None),
        P(),
    )
    return jax.shard_map(shards, mesh=mesh, in_specs=in_specs, out_specs=out_specs, check_vma=False)
```

```python
import functools
import types
import typing

import jax
import jax.numpy as jnp
from jax import lax
from jax.experimental import pallas as pl
from jax.experimental.pallas import tpu as pltpu
from jax.sharding import PartitionSpec as P

C = 512
HEADS = 8
HEAD = 64
EMB = 2048
TEXT = 128
NORM_GROUPS = 32
W = 64
SPAN = 8
ROWS, ITEMS = "rows", "items"


epsilon = 1e-05


def from_behind(array, axis, by):
    length = lax.axis_size(axis)
    pairs = [(i, i + by) for i in range(length) if 0 <= i + by < length]
    return lax.ppermute(array, axis, pairs)


def as_sent(array):
    return jax.tree.map(lambda a: a.astype(jnp.bfloat16) if a.dtype == jnp.float32 else a, array)


def keep_state(state):
    return state


def silu_slope(source):
    sigma = jax.nn.sigmoid(source)
    return sigma * (1.0 + source * (1.0 - sigma))


def dot_first(left_side, right_side):
    return lax.dot_general(
        left_side, right_side, (((0,), (0,)), ((), ())), preferred_element_type=jnp.float32
    )


def dot_last(left_side, right_side):
    return lax.dot_general(
        left_side, right_side, (((1,), (1,)), ((), ())), preferred_element_type=jnp.float32
    )


def head_split(source):
    return source.reshape(source.shape[0], HEADS, HEAD)


def piece_scores(query_heads, key_piece, allowed):
    key_heads = head_split(key_piece[:, :C])
    scores = jnp.einsum(
        "qhd,khd->hqk", query_heads, key_heads, preferred_element_type=jnp.float32
    ) * HEAD ** (-0.5)
    return jnp.where(allowed[None, None, :], scores, -jnp.inf)


def piece_grads(query_heads, grad_heads, log_total, row_dots, key_piece, allowed):
    scores = piece_scores(query_heads, key_piece, allowed)
    weights = jnp.exp(scores - log_total[:, :, None])
    value_heads = head_split(key_piece[:, C:])
    weight_grad = jnp.einsum(
        "qhd,khd->hqk", grad_heads, value_heads, preferred_element_type=jnp.float32
    )
    score_grad = (weights * (weight_grad - row_dots[:, :, None])).astype(jnp.bfloat16)
    outcome = []
    key_heads = head_split(key_piece[:, :C])
    query_grad = jnp.einsum(
        "hqk,khd->qhd", score_grad, key_heads, preferred_element_type=jnp.float32
    ) * HEAD ** (-0.5)
    outcome.append(query_grad.reshape(query_grad.shape[0], C))
    key_grad = jnp.einsum(
        "hqk,qhd->khd", score_grad, query_heads, preferred_element_type=jnp.float32
    ) * HEAD ** (-0.5)
    value_grad = jnp.einsum(
        "hqk,qhd->khd", weights.astype(jnp.bfloat16), grad_heads, preferred_element_type=jnp.float32
    )
    outcome.append(jnp.concatenate([key_grad.reshape(-1, C), value_grad.reshape(-1, C)], axis=1))
    return tuple(outcome)


def source_masks(band_items, source, my_item, pixels):
    slots = band_items.shape[0]
    inside = (source >= 0) & (source < slots)
    clipped = jnp.clip(source, 0, slots - 1)
    source_item = band_items[clipped]
    before_item = band_items[jnp.maximum(clipped - 1, 0)]
    same_item = inside & (source_item == my_item)
    leading = same_item & ((clipped == 0) | (before_item != source_item))
    allowed = jnp.concatenate(
        [jnp.broadcast_to(same_item, (pixels,)), jnp.broadcast_to(leading, (TEXT,))]
    )
    return (allowed, same_item)


REACH = SPAN - 1
LOG2E = 1.4426950408889634
PIX = 512


def dot(left, right):
    return jnp.dot(left, right, preferred_element_type=jnp.float32)


def reach_of(here, slots):
    first = here < SPAN
    low = jnp.maximum(jnp.where(first, 0, SPAN), here - REACH)
    high = jnp.minimum(jnp.where(first, SPAN - 1, slots - 1), here + REACH)
    return low, high


def exchange_kernel(slots, with_edges, *refs):
    if with_edges:
        tile, top, bottom, window, above, below, send_sem, recv_sem, edge_send, edge_recv = refs
    else:
        tile, window, send_sem, recv_sem = refs
    here = lax.axis_index(ROWS)
    low, high = reach_of(here, slots)
    offsets = [o for o in range(-REACH, REACH + 1) if o != 0]

    def reached(offset):
        return (here + offset >= low) & (here + offset <= high)

    barrier = pltpu.get_barrier_semaphore()
    for o in offsets:

        @pl.when(reached(o))
        def _(o=o):
            pl.semaphore_signal(barrier, 1, device_id={ROWS: here + o})

    pl.semaphore_wait(barrier, high - low)

    def edge_copy(o):
        source, target, k = (top, below, 0) if o < 0 else (bottom, above, 1)
        return pltpu.make_async_remote_copy(
            source, target, edge_send.at[k], edge_recv.at[k], device_id={ROWS: here + o}
        )

    def tile_copy(o):
        return pltpu.make_async_remote_copy(
            tile,
            window.at[REACH - o],
            send_sem.at[REACH - o],
            recv_sem.at[REACH - o],
            device_id={ROWS: here + o},
        )

    if with_edges:
        for o in (-1, 1):

            @pl.when(reached(o))
            def _(o=o):
                edge_copy(o).start()

    for o in offsets:

        @pl.when(reached(o))
        def _(o=o):
            tile_copy(o).start()

        @pl.when(jnp.logical_not(reached(-o)))
        def _(o=o):
            window[REACH - o] = jnp.zeros_like(tile)

    window[REACH] = tile[...]
    if with_edges:

        @pl.when(jnp.logical_not(reached(-1)))
        def _():
            above[...] = jnp.zeros_like(above)

        @pl.when(jnp.logical_not(reached(1)))
        def _():
            below[...] = jnp.zeros_like(below)

    for o in offsets:

        @pl.when(reached(o))
        def _(o=o):
            tile_copy(o).wait_send()

        @pl.when(reached(-o))
        def _(o=o):
            tile_copy(o).wait_recv()

    if with_edges:
        for o in (-1, 1):

            @pl.when(reached(o))
            def _(o=o):
                edge_copy(o).wait_send()

            @pl.when(reached(-o))
            def _(o=o):
                edge_copy(o).wait_recv()


def exchange(ident, slots, tile, edges=None):
    vmem = pl.BlockSpec(memory_space=pltpu.VMEM)
    shapes = [jax.ShapeDtypeStruct((2 * REACH + 1,) + tile.shape, tile.dtype)]
    scratch = [pltpu.SemaphoreType.DMA((2 * REACH + 1,))] * 2
    operands = [tile]
    if edges is not None:
        shapes += [jax.ShapeDtypeStruct(e.shape, e.dtype) for e in edges]
        scratch += [pltpu.SemaphoreType.DMA((2,))] * 2
        operands += list(edges)
    return pl.pallas_call(
        functools.partial(exchange_kernel, slots, edges is not None),
        out_shape=tuple(shapes),
        in_specs=[vmem] * len(operands),
        out_specs=(vmem,) * len(shapes),
        scratch_shapes=scratch,
        compiler_params=pltpu.CompilerParams(collective_id=ident, has_side_effects=True),
        name=f"exchange_{ident}",
    )(*operands)


def head_kernel(
    items, y_ref, t_ref, z_ref, zt_ref, xt, vx, tt, tvx, s_ref, p_ref, dk, dv, dkt, dvt
):
    low = jnp.bfloat16
    full = jnp.float32
    bands, pixels = y_ref.shape[0], y_ref.shape[1]
    text = t_ref.shape[1]
    scale = HEAD ** (-0.5)

    def widened(values, rows):
        lanes = lax.broadcasted_iota(jnp.int32, (rows, 2 * HEAD), 1)
        units = jnp.where(lanes < HEAD + 2, 1.0, 0.0).astype(low)
        return jnp.where(lanes < HEAD, values, units)

    def prepare(b, carry):
        block = y_ref[b]
        xt[b] = block.T
        vx[b] = widened(block[:, 2 * HEAD :], pixels)
        words = t_ref[b]
        tt[b] = words.T
        tvx[b] = widened(pltpu.roll(words.astype(full), HEAD, 1).astype(low), text)
        dk[b] = jnp.zeros((pixels, 2 * HEAD), full)
        dv[b] = jnp.zeros((pixels, 2 * HEAD), full)
        dkt[b] = jnp.zeros((text, 2 * HEAD), full)
        dvt[b] = jnp.zeros((text, 2 * HEAD), full)
        return carry

    lax.fori_loop(0, bands, prepare, 0)

    def one_row(columns):
        rows = lax.broadcasted_iota(jnp.int32, (16, columns), 0)
        return jnp.where(rows == 0, 1.0, 0.0).astype(low)

    ones_pixels = one_row(pixels)
    ones_text = one_row(text)
    zeros = jnp.zeros((HEAD, pixels), low)

    base = (lax.axis_index(ROWS) // SPAN) * SPAN

    def query_band(i, carry):
        mine = items[base + i]
        start, end = 0, 0
        for b in range(bands):
            other = items[base + b]
            start = start + jnp.where(other < mine, 1, 0)
            end = end + jnp.where(other <= mine, 1, 0)
        query_t = (xt[i, 0:HEAD, :].astype(full) * scale).astype(low)
        query_rhs = jnp.concatenate([zeros, query_t], 0)
        query_text = jnp.concatenate([query_t, zeros], 0)

        def score(j, top):
            scores = dot(y_ref[j, :, 0 : 2 * HEAD], query_rhs)
            s_ref[j] = scores
            return jnp.maximum(top, jnp.max(scores.reshape(pixels // 8, 8, pixels), axis=0))

        top = lax.fori_loop(start, end, score, jnp.full((8, pixels), -jnp.inf, full))
        scores = dot(t_ref[start], query_text)
        top = jnp.maximum(top, jnp.max(scores.reshape(text // 8, 8, pixels), axis=0))
        top = jnp.max(top, axis=0, keepdims=True)
        weights_text = jnp.exp2((scores - top) * LOG2E).astype(low)
        total = dot(jnp.concatenate([tt[start, HEAD:, :], ones_text], 0), weights_text)

        def gather(j, total):
            weights = jnp.exp2((s_ref[j] - top) * LOG2E).astype(low)
            p_ref[j] = weights
            values = jnp.concatenate([xt[j, 2 * HEAD : 3 * HEAD, :], ones_pixels], 0)
            return total + dot(values, weights)

        total = lax.fori_loop(start, end, gather, total)
        inverse = 1.0 / total[HEAD : HEAD + 1, :]
        attended = total[0:HEAD, :] * inverse
        grad = xt[i, 3 * HEAD :, :].astype(full)
        minus_dots = -jnp.sum(grad * attended, axis=0, keepdims=True) * inverse
        grad_scaled = (grad * inverse).astype(low)
        coarse = minus_dots.astype(low)
        fine = minus_dots - coarse.astype(full)
        rows = lax.broadcasted_iota(jnp.int32, (HEAD, pixels), 0)
        extra = jnp.where(rows == 0, coarse.astype(full), jnp.where(rows == 1, fine, 0.0))
        grad_rhs = jnp.concatenate([grad_scaled, extra.astype(low)], 0)
        grad_rows = jnp.concatenate([grad_scaled, zeros], 0).T
        query_rows = jnp.concatenate([query_t, zeros], 0).T

        def back(j, query_grad):
            weights = p_ref[j]
            steps = (weights.astype(full) * dot(vx[j], grad_rhs)).astype(low)
            dv[j] += dot(weights, grad_rows)
            dk[j] += dot(steps, query_rows)
            return query_grad + dot(xt[j, HEAD : 2 * HEAD, :], steps)

        steps = (weights_text.astype(full) * dot(tvx[start], grad_rhs)).astype(low)
        dvt[start] += dot(weights_text, grad_rows)
        dkt[start] += dot(steps, query_rows)
        query_grad = dot(tt[start, 0:HEAD, :], steps)
        query_grad = lax.fori_loop(start, end, back, query_grad)
        z_ref[i, :, 0 : 2 * HEAD] = jnp.concatenate(
            [attended.astype(low), (query_grad * scale).astype(low)], 0
        ).T
        return carry

    lax.fori_loop(0, bands, query_band, 0)

    def finish(b, carry):
        lanes = lax.broadcasted_iota(jnp.int32, (pixels, 2 * HEAD), 1)
        z_ref[b, :, 2 * HEAD :] = jnp.where(
            lanes < HEAD, dk[b], pltpu.roll(dv[b], HEAD, 1)
        ).astype(low)
        lanes = lax.broadcasted_iota(jnp.int32, (text, 2 * HEAD), 1)
        zt_ref[b] = jnp.where(lanes < HEAD, dkt[b], pltpu.roll(dvt[b], HEAD, 1)).astype(low)
        return carry

    lax.fori_loop(0, bands, finish, 0)


def one_head(items, pieces, words):
    bands, pixels, _ = pieces.shape
    text = words.shape[1]
    low, full = jnp.bfloat16, jnp.float32
    smem = pl.BlockSpec(memory_space=pltpu.SMEM)
    vmem = pl.BlockSpec(memory_space=pltpu.VMEM)
    return pl.pallas_call(
        head_kernel,
        out_shape=(
            jax.ShapeDtypeStruct(pieces.shape, low),
            jax.ShapeDtypeStruct(words.shape, low),
        ),
        in_specs=[smem, vmem, vmem],
        out_specs=(vmem, vmem),
        scratch_shapes=[
            pltpu.VMEM((bands, 4 * HEAD, pixels), low),
            pltpu.VMEM((bands, pixels, 2 * HEAD), low),
            pltpu.VMEM((bands, 2 * HEAD, text), low),
            pltpu.VMEM((bands, text, 2 * HEAD), low),
            pltpu.VMEM((bands, pixels, pixels), full),
            pltpu.VMEM((bands, pixels, pixels), low),
            pltpu.VMEM((bands, pixels, 2 * HEAD), full),
            pltpu.VMEM((bands, pixels, 2 * HEAD), full),
            pltpu.VMEM((bands, text, 2 * HEAD), full),
            pltpu.VMEM((bands, text, 2 * HEAD), full),
        ],
        compiler_params=pltpu.CompilerParams(vmem_limit_bytes=56 << 20),
        name="one_head",
    )(items, pieces, words)


def attention_by_band(band_items, position, queries, keys_values, text_kv, attended_grad):
    my_item = band_items[position]
    pixels = queries.shape[0]
    own_allowed, own_same = source_masks(band_items, position, my_item, pixels)
    packed = jnp.concatenate([keys_values, text_kv], axis=0)
    pieces = [(0, packed, own_allowed, own_same)]
    for distance in range(1, SPAN):
        for offset in (distance, -distance):
            arrived = from_behind(packed, ROWS, offset)
            allowed, same_item = source_masks(band_items, position - offset, my_item, pixels)
            pieces.append((offset, arrived, allowed, same_item))
    query_heads = head_split(queries)
    row_top = jnp.full((HEADS, pixels), -jnp.inf, jnp.float32)
    weight_sum = jnp.zeros((HEADS, pixels), jnp.float32)
    for offset, key_piece, allowed, same_item in pieces:

        def gather_scores(state, key_piece=key_piece, allowed=allowed):
            top_old, sum_old = state
            scores = piece_scores(query_heads, key_piece, allowed)
            top_new = jnp.maximum(top_old, jnp.max(scores, axis=2))
            sum_new = sum_old * jnp.exp(top_old - top_new) + jnp.sum(
                jnp.exp(scores - top_new[:, :, None]), axis=2
            )
            return (top_new, sum_new)

        row_top, weight_sum = lax.cond(same_item, gather_scores, keep_state, (row_top, weight_sum))
    log_total = row_top + jnp.log(weight_sum)
    attended = jnp.zeros((pixels, HEADS, HEAD), jnp.float32)
    for offset, key_piece, allowed, same_item in pieces:

        def add_values(totals, key_piece=key_piece, allowed=allowed):
            scores = piece_scores(query_heads, key_piece, allowed)
            weights = jnp.exp(scores - log_total[:, :, None]).astype(jnp.bfloat16)
            return totals + jnp.einsum(
                "hqk,khd->qhd",
                weights,
                head_split(key_piece[:, C:]),
                preferred_element_type=jnp.float32,
            )

        attended = lax.cond(same_item, add_values, keep_state, attended)
    attended_flat = attended.reshape(pixels, C)
    row_dots = jnp.sum(
        (attended_grad.astype(jnp.float32) * attended_flat).reshape(pixels, HEADS, HEAD), axis=2
    ).T
    grad_heads = head_split(attended_grad)
    query_grad = jnp.zeros((pixels, C), jnp.float32)
    packed_grad = jnp.zeros((pixels + TEXT, 2 * C), jnp.float32)
    zero_piece = jnp.zeros((pixels + TEXT, 2 * C), jnp.float32)
    for offset, key_piece, allowed, same_item in pieces:

        def grad_both(totals, key_piece=key_piece, allowed=allowed):
            outcome = piece_grads(query_heads, grad_heads, log_total, row_dots, key_piece, allowed)
            return (totals + outcome[0], outcome[1])

        def grad_none(totals):
            return (totals, zero_piece)

        query_grad, piece_grad = lax.cond(same_item, grad_both, grad_none, query_grad)
        if offset == 0:
            packed_grad = packed_grad + piece_grad
        else:
            packed_grad = packed_grad + from_behind(
                as_sent(piece_grad), ROWS, -offset
            ).astype(jnp.float32)
    packed_low = packed_grad.astype(jnp.bfloat16)
    return (
        attended_flat.astype(jnp.bfloat16),
        query_grad.astype(jnp.bfloat16),
        packed_low[:pixels],
        packed_low[pixels:],
    )


def taps_of(rows, reverse):
    padded = rows.reshape(-1, W, rows.shape[1])
    row_list = [padded[:-2], padded[1:-1], padded[2:]]
    if reverse:
        row_list = row_list[::-1]
    zero_column = jnp.zeros_like(row_list[0][:, :1])
    views = []
    for row_view in row_list:
        left_view = jnp.concatenate([zero_column, row_view[:, :-1]], axis=1)
        right_view = jnp.concatenate([row_view[:, 1:], zero_column], axis=1)
        view_list = [left_view, row_view, right_view]
        if reverse:
            view_list = view_list[::-1]
        views = views + view_list
    return [view.reshape(-1, rows.shape[1]) for view in views]


class Vectors(typing.NamedTuple):
    mean_one: jax.Array
    scale_one: jax.Array
    gain_one: jax.Array
    bias_one: jax.Array
    mean_two: jax.Array
    scale_two: jax.Array
    gain_two: jax.Array
    bias_two: jax.Array
    mean_three: jax.Array
    scale_three: jax.Array
    gain_three: jax.Array
    bias_three: jax.Array
    stretch: jax.Array
    shift: jax.Array
    proj_bias: jax.Array
    keep_above: jax.Array
    keep_below: jax.Array
    per_item: jax.Array


def grouped(names, refs):
    found, position = types.SimpleNamespace(), 0
    for name, count in names:
        if count is None:
            setattr(found, name, refs[position])
            position += 1
        else:
            setattr(found, name, refs[position : position + count])
            position += count
    return found


def call_named(kernel, ident, scalars, inputs, anywhere, outs, scratch, semaphores):
    names = [(name, None) for name in [*scalars, *inputs, *anywhere, *outs]]
    buffers = []
    for name, entry in scratch.items():
        many = isinstance(entry, list)
        names.append((name, len(entry) if many else None))
        buffers += [pltpu.VMEM(*e) for e in (entry if many else [entry])]
    names += [(name, None) for name in semaphores]
    vmem = pl.BlockSpec(memory_space=pltpu.VMEM)
    outcome = pl.pallas_call(
        functools.partial(kernel, names),
        out_shape=tuple(jax.ShapeDtypeStruct(*o) for o in outs.values()),
        in_specs=[pl.BlockSpec(memory_space=pltpu.SMEM)] * len(scalars)
        + [vmem] * len(inputs)
        + [pl.BlockSpec(memory_space=pl.ANY)] * len(anywhere),
        out_specs=(vmem,) * len(outs),
        scratch_shapes=buffers + [pltpu.SemaphoreType.DMA(s) for s in semaphores.values()],
        compiler_params=pltpu.CompilerParams(
            collective_id=ident, has_side_effects=True, vmem_limit_bytes=60 << 20
        ),
        name=kernel.__name__,
    )(*[v for group in (scalars, inputs, anywhere) for v in dict(group).values()])
    return types.SimpleNamespace(**dict(zip(outs, outcome)))


VECTOR_ROWS = 24
FAR, NEAR, SIDE, CORE, GROUP = range(5)
CROSS = (FAR, NEAR, SIDE)
SIDE_FIRST = (SIDE, GROUP, NEAR, FAR)
GROUP_FIRST = (GROUP, NEAR, SIDE, FAR)
NEAR_FIRST = (NEAR, SIDE, GROUP, FAR)
STREAMS = (
    (48, C // 2, SIDE_FIRST),
    (48, C // 2, GROUP_FIRST),
    (48, C // 2, NEAR_FIRST),
    (48, C // 2, SIDE_FIRST),
    (48, C // 2, GROUP_FIRST),
    (48, C // 2, NEAR_FIRST),
    (32, C, SIDE_FIRST),
    (32, C, NEAR_FIRST),
    (16, 3 * C // 2, GROUP_FIRST),
    (16, C // 2, GROUP_FIRST),
)
FIRST_CONV, SECOND_CONV, WORDS, QKV, PROJ = 0, 3, 6, 8, 9
LANDINGS = 4
IMAGE_ROWS = 8


class Band:
    def __init__(self, r):
        self.r = r
        self.row = lax.axis_index(ROWS)
        self.group = lax.axis_index(ITEMS)
        self.lane = self.row % SPAN
        self.base = self.row - self.lane
        row = self.row
        self.place = [row // 8, (row // 4) % 2, (row // 2) % 2, row % 2, self.group]
        self.partner = [
            {ROWS: row + (1 - 2 * self.place[d]) * (8 >> d)} for d in range(CORE + 1)
        ]
        self.partner.append({ITEMS: 1 - self.group})
        self.others = [(self.lane + o) % SPAN for o in range(1, SPAN)]
        self.peers = [{ROWS: self.base + other} for other in self.others]
        self.has_above, self.has_below = self.lane > 0, self.lane < SPAN - 1

    def meet(self, further=()):
        barrier = pltpu.get_barrier_semaphore()
        targets = self.peers + [self.partner[d] for d in further]
        for target in targets:
            pl.semaphore_signal(barrier, 1, device_id=target)
        pl.semaphore_wait(barrier, len(targets))

    def remote(self, source, target, send, recv, device):
        return pltpu.make_async_remote_copy(source, target, send, recv, device_id=device)

    def edges(self, k, top, bottom, target):
        r = self.r
        up = self.remote(
            top,
            target.at[IMAGE_ROWS + 1],
            r.edge_send.at[k, 0],
            r.edge_recv.at[k, 0],
            {ROWS: self.row - 1},
        )
        down = self.remote(
            bottom,
            target.at[0],
            r.edge_send.at[k, 1],
            r.edge_recv.at[k, 1],
            {ROWS: self.row + 1},
        )
        pl.when(self.has_above)(up.start)
        pl.when(self.has_below)(down.start)
        return up, down

    def wait_edges(self, pair):
        up, down = pair

        @pl.when(self.has_above)
        def _():
            up.wait_send()
            down.wait_recv()

        @pl.when(self.has_below)
        def _():
            down.wait_send()
            up.wait_recv()

    def zero_edges(self, target):
        @pl.when(jnp.logical_not(self.has_above))
        def _():
            target[0] = jnp.zeros(target.shape[1:], target.dtype)

        @pl.when(jnp.logical_not(self.has_below))
        def _():
            target[IMAGE_ROWS + 1] = jnp.zeros(target.shape[1:], target.dtype)

    def send_tile(self, k, source, target):
        r = self.r
        copies = []
        for o in range(1, SPAN):
            copies.append(
                self.remote(
                    source,
                    target.at[self.lane],
                    r.tile_send.at[k, o],
                    r.tile_recv.at[k, o],
                    self.peers[o - 1],
                )
            )
        for copy in copies:
            copy.start()
        target[self.lane] = source[...]
        return copies

    def swap(self, k, source, target, order=range(1, SPAN)):
        r = self.r
        copies = []
        for o in order:
            copies.append(
                self.remote(
                    source.at[self.others[o - 1]],
                    target.at[self.lane],
                    r.swap_send.at[k, o],
                    r.swap_recv.at[k, o],
                    self.peers[o - 1],
                )
            )
            copies[-1].start()
        return copies

    def fill_blocks(self):
        rows = lax.broadcasted_iota(jnp.int32, (C, C), 0) // (C // NORM_GROUPS)
        columns = lax.broadcasted_iota(jnp.int32, (C, C), 1) // (C // NORM_GROUPS)
        self.r.blocks[...] = jnp.where(rows == columns, 1.0, 0.0).astype(jnp.bfloat16)

    def item_means(self, window, masks, per_item):
        low, full = jnp.bfloat16, jnp.float32
        total = jnp.zeros((8, C), full)
        for b in range(SPAN):
            total = total + jnp.where(masks[b] > 0.0, window[b], 0.0)
        total = total * per_item
        coarse = total.astype(low)
        rest = total - coarse.astype(full)
        finer = rest.astype(low)
        finest = (rest - finer.astype(full)).astype(low)
        blocks = self.r.blocks[...]
        return dot(coarse, blocks) + dot(finer, blocks) + dot(finest, blocks)


def sums_tile(first, second):
    rows = lax.broadcasted_iota(jnp.int32, (8, C), 0)
    return jnp.where(rows == 0, first, jnp.where(rows == 1, second, 0.0))


def column_sum(values):
    return jnp.sum(values, axis=0, keepdims=True)


def side_shifts(values):
    rows = lax.broadcasted_iota(jnp.int32, (W, C), 0)
    from_left = jnp.where(rows == 0, 0.0, pltpu.roll(values, 1, 0))
    from_right = jnp.where(rows == W - 1, 0.0, pltpu.roll(values, W - 1, 0))
    return from_left, from_right


def kept(i, values, vec):
    keep = jnp.where(i == 0, vec.keep_above, jnp.where(i == IMAGE_ROWS + 1, vec.keep_below, 1.0))
    return jnp.where(keep > 0.0, values, 0.0)


def back_kernel(names, *refs):
    low, full = jnp.bfloat16, jnp.float32
    r = grouped(names, refs)
    band = Band(r)
    lane, group, place, partner = band.lane, band.group, band.place, band.partner
    core = place[CORE]
    remote = band.remote
    band.meet((FAR, GROUP))

    swaps = band.swap(0, r.pieces, r.heads) + band.swap(1, r.words, r.head_words)

    loads = types.SimpleNamespace()

    def load(k, source, target):
        copy = pltpu.make_async_copy(source, target, r.load_sem.at[k])
        copy.start()
        return copy

    loads.own = load(0, r.pieces.at[lane], r.heads.at[lane])
    loads.own_words = load(1, r.words.at[lane], r.head_words.at[lane])
    loads.middle = load(2, r.middle, r.mid)
    loads.qkv_weight = load(3, r.qkv_weight, r.qkv_w)
    loads.proj_weight = load(4, r.proj_weight, r.proj_w)
    loads.upstream = load(5, r.upstream, r.up)
    loads.act_three = load(6, r.act_three, r.act3)
    loads.caption = load(7, r.caption, r.cap)
    loads.conv_second = load(8, r.conv_second, r.conv_w)
    loads.hidden = load(9, r.hidden, r.hid)
    loads.act_two = load(10, r.act_two, r.act2)
    loads.act_one = load(11, r.act_one, r.act1)
    loads.image = load(12, r.image, r.img)
    loads.text_weight = load(13, r.text_weight, r.text_w)

    sibling = types.SimpleNamespace()

    def to_sibling(k, source, target):
        copy = remote(source, target, r.sib_send.at[k], r.sib_recv.at[k], partner[CORE])
        copy.start()
        return copy

    half = pl.ds(pl.multiple_of((1 - core) * (C // 2), C // 2), C // 2)
    sibling.upstream = to_sibling(0, r.upstream.at[:, half], r.sib_up)
    sibling.act3 = to_sibling(1, r.act_three, r.sib_act3)
    sibling.cap = to_sibling(2, r.caption, r.sib_cap)
    sibling.act2 = to_sibling(3, r.act_two, r.sib_act2)
    sibling.act1 = to_sibling(4, r.act_one, r.sib_act1)

    share_copy = remote(
        r.silu_share, r.other_share, r.small_send.at[2], r.small_recv.at[2], partner[GROUP]
    )
    share_copy.start()
    for target in (r.part_two, r.part_one):
        band.zero_edges(target)

    vec = Vectors(*[r.vectors[i : i + 1, :] for i in range(len(Vectors._fields))])
    norm_one = (vec.mean_one, vec.scale_one)
    norm_two = (vec.mean_two, vec.scale_two)
    norm_three = (vec.mean_three, vec.scale_three)

    masks = [r.vectors[VECTOR_ROWS + b : VECTOR_ROWS + b + 1, :] for b in range(SPAN)]
    band.fill_blocks()

    def item_means(window):
        return band.item_means(window, masks, vec.per_item)

    class Stream:
        def __init__(self, k):
            self.k = k
            self.order = STREAMS[k][2]
            self.dims = [FAR, NEAR, SIDE, CORE, GROUP]
            self.step = 0
            self.copy = None

        def at(self, ref, d, index):
            return ref.at[(slice(None),) * self.dims.index(d) + (index,)]

        def start(self):
            self.launch(r.grads[self.k])

        def launch(self, ref):
            k, step = self.k, self.step
            if step < LANDINGS:
                d = self.order[step]
                self.copy = remote(
                    self.at(ref, d, 1 - place[d]),
                    r.landings[k * LANDINGS + step],
                    r.fold_send.at[k, step],
                    r.fold_recv.at[k, step],
                    partner[d],
                )
                self.mine = self.at(ref, d, place[d])
                self.dims.remove(d)
            elif step == LANDINGS:
                fin = r.folded[self.k]
                self.copy = remote(
                    ref.at[1 - core],
                    fin.at[core],
                    r.fold_send.at[k, step],
                    r.fold_recv.at[k, step],
                    partner[CORE],
                )
                self.mine = ref.at[core]
            else:
                self.copy = remote(
                    r.folded[self.k],
                    r.whole[self.k],
                    r.fold_send.at[k, step],
                    r.fold_recv.at[k, step],
                    partner[GROUP],
                )
            self.copy.start()

        def advance(self):
            self.copy.wait()
            if self.step < LANDINGS:
                landed, mine = r.landings[self.k * LANDINGS + self.step], self.mine
                lead = landed.shape[:-2]
                pieces = 1
                for n in lead:
                    pieces *= n

                def add(i, carry):
                    index = []
                    for n in reversed(lead):
                        index.insert(0, i % n)
                        i = i // n
                    index = tuple(index)
                    total = landed[index].astype(full) + mine[index].astype(full)
                    landed[index] = total.astype(low)
                    return carry

                lax.fori_loop(0, pieces, add, 0)
                self.step += 1
                self.launch(landed)
            elif self.step == LANDINGS:
                r.folded[self.k][core] = self.mine[...]
                self.step += 1
                self.launch(None)
            else:
                self.step += 1

    streams = [Stream(k) for k in range(len(STREAMS))]

    loads.own.wait()
    loads.own_words.wait()
    for copy in swaps:
        copy.wait()
    for h in range(0, HEADS, 2):
        for k in range(4):
            pair = [r.heads[h + i, :, k * HEAD : (k + 1) * HEAD] for i in range(2)]
            r.joined[:, k * C + h * HEAD : k * C + (h + 2) * HEAD] = jnp.concatenate(pair, axis=1)
        for k in range(2):
            pair = [r.head_words[h + i, :, k * HEAD : (k + 1) * HEAD] for i in range(2)]
            r.joined_words[:, k * C + h * HEAD : k * C + (h + 2) * HEAD] = jnp.concatenate(
                pair, axis=1
            )
    sibling.attended = to_sibling(5, r.joined.at[:, 0:C], r.sib_attended)
    three_half = C + (1 - core) * (3 * C // 2)
    sibling.qkv = to_sibling(
        6,
        r.joined.at[:, pl.ds(pl.multiple_of(three_half, C // 2), 3 * C // 2)],
        r.sib_qkv,
    )
    sibling.words = to_sibling(
        7,
        r.joined_words.at[:, pl.ds(pl.multiple_of((1 - core) * C, C), C)],
        r.sib_words,
    )
    for copy in (loads.middle, loads.qkv_weight, loads.proj_weight, loads.upstream):
        copy.wait()

    def pixel_block(ref, i, count=4):
        return ref[1 + i * count : 1 + (i + 1) * count].reshape(count * W, C)

    def unit(values, norm):
        return (values - norm[0]) * norm[1]

    plain = jnp.zeros((1, C), full)
    crossed = jnp.zeros((1, C), full)
    up_sum = jnp.zeros((1, C), full)
    for i in range(2):
        block = slice(i * 4 * W, (i + 1) * 4 * W)
        middle = pixel_block(r.mid, i)
        upstream = r.up[block, :].astype(full)
        result = middle + dot(r.joined[block, 0:C], r.proj_w[...]) + vec.proj_bias
        r.result[block, :] = result.astype(low)
        grad = dot_last(r.joined[block, C:], r.qkv_w[...])
        plain = plain + column_sum(grad)
        crossed = crossed + column_sum(grad * unit(middle, norm_three))
        up_sum = up_sum + column_sum(upstream)
        part = upstream + grad * (vec.gain_three * vec.scale_three)
        r.part_two[1 + i * 4 : 5 + i * 4] = part.reshape(4, W, C)
    gain_three, bias_three = crossed, plain
    r.tile[0] = sums_tile(plain * vec.gain_three, crossed * vec.gain_three)
    three_edges = band.edges(0, r.part_two.at[1], r.part_two.at[IMAGE_ROWS], r.part_two)
    tiles = band.send_tile(0, r.tile.at[0], r.window.at[0])

    def mine_of(ref, start, size):
        return ref[:, pl.ds(pl.multiple_of(start, size if size % 256 else 256), size)]

    for copy in (sibling.upstream, sibling.act3, sibling.cap, sibling.attended, sibling.qkv, sibling.words):
        copy.wait()
    for copy in (loads.act_three, loads.caption):
        copy.wait()
    grad = dot_first(r.joined[:, 0:C], mine_of(r.up, core * (C // 2), C // 2))
    grad = grad + dot_first(r.sib_attended[...], r.sib_up[...])
    r.grads[PROJ][...] = grad.astype(low).reshape(r.grads[PROJ].shape)
    streams[PROJ].start()
    for n in range(3):
        own = mine_of(r.joined, C + core * (3 * C // 2) + n * (C // 2), C // 2)
        columns = slice(n * (C // 2), (n + 1) * (C // 2))
        grad = dot_first(r.act3[...], own)
        grad = grad + dot_first(r.sib_act3[...], r.sib_qkv[:, columns])
        r.grads[QKV][:, :, :, :, :, :, columns] = grad.astype(low).reshape(2, 2, 2, 2, 2, 16, C // 2)
    streams[QKV].start()

    def text_rows(s, carry):
        columns = pl.ds(pl.multiple_of(s * 128, 128), 128)
        own = mine_of(r.joined_words, core * C, C)
        grad = dot_first(r.cap[:, columns], own)
        grad = grad + dot_first(r.sib_cap[:, columns], r.sib_words[...])
        grad = grad.astype(low)
        index = (s // 8, (s // 4) % 2, (s // 2) % 2, s % 2)
        r.grads[WORDS][index] = grad[0:64].reshape(2, 32, C)
        r.grads[WORDS + 1][index] = grad[64:128].reshape(2, 32, C)
        return carry

    lax.fori_loop(0, 2 ** len(CROSS) * 2, text_rows, 0)
    streams[WORDS].start()
    streams[WORDS + 1].start()
    query_sum = column_sum(r.joined[:, C : 2 * C].astype(full))
    value_sum = column_sum(r.joined[:, 3 * C :].astype(full))
    word_sum = [column_sum(r.joined_words[:, k * C : (k + 1) * C].astype(full)) for k in range(2)]

    def spread_rows(i, values):
        from_left, from_right = side_shifts(values)
        r.shifts[0, i] = from_right.astype(low)
        r.shifts[1, i] = values.astype(low)
        r.shifts[2, i] = from_left.astype(low)

    def conv_back():
        total = jnp.zeros((IMAGE_ROWS * W, C), full)
        for t in range(9):
            dy, dx = t // 3, t % 3
            view = r.shifts[dx, 2 - dy : 2 - dy + IMAGE_ROWS].reshape(IMAGE_ROWS * W, C)
            total = total + dot_last(view, r.conv_w[t * C : (t + 1) * C, :])
        return total

    def conv_grads(kind, own, other, landing):
        for t in range(9):
            dy, dx = t // 3, t % 3
            shifted = r.shifts[
                dx, 1 : IMAGE_ROWS + 1, :, pl.ds(pl.multiple_of(core * (C // 2), C // 2), C // 2)
            ].reshape(IMAGE_ROWS * W, C // 2)
            grad = dot_first(own[dy * W : dy * W + IMAGE_ROWS * W, :], shifted)
            grad = grad + dot_first(
                other[dy * W : dy * W + IMAGE_ROWS * W, :],
                landing[dx].reshape(IMAGE_ROWS * W, C // 2),
            )
            grad = grad.astype(low)
            begin = t * C
            while begin < (t + 1) * C:
                shard, within = divmod(begin, 288)
                stream, offset = divmod(within, 96)
                part, offset = divmod(offset, 48)
                size = min(48 - offset, (t + 1) * C - begin)
                target = r.grads[kind + stream]
                target[
                    shard // 8, (shard // 4) % 2, (shard // 2) % 2, shard % 2, part, offset : offset + size
                ] = grad[begin - t * C : begin - t * C + size]
                begin += size
        for j in range(3):
            streams[kind + j].start()

    for copy in tiles:
        copy.wait()
    band.wait_edges(three_edges)
    means = item_means(r.window.at[0])
    offset_three, slope_three = means[0:1] * vec.scale_three, means[1:2] * vec.scale_three

    def middle_row(i, bias):
        values = r.part_two[i] - offset_three - unit(r.mid[i], norm_three) * slope_three
        r.part_two[i] = values
        values = kept(i, values, vec)
        spread_rows(i, values)
        inside = jnp.where((i > 0) & (i <= IMAGE_ROWS), 1.0, 0.0)
        return bias + inside * column_sum(values.astype(low).astype(full))

    conv_bias_two = lax.fori_loop(0, IMAGE_ROWS + 2, middle_row, jnp.zeros((1, C), full))
    shift_half = r.shifts.at[:, 1 : IMAGE_ROWS + 1, :, half]
    sibling.shifts_two = to_sibling(8, shift_half, r.sib_shifts_two)
    loads.conv_second.wait()
    loads.hidden.wait()
    r.product[...] = conv_back().reshape(IMAGE_ROWS, W, C)
    loads.conv_first = load(8, r.conv_first, r.conv_w)
    stretched = vec.stretch * vec.gain_two * vec.scale_two

    def second_row(i, sums):
        unit_two = unit(r.hid[i + 1], norm_two)
        normed = unit_two * vec.gain_two + vec.bias_two
        grad = r.product[i] * silu_slope_of(normed * vec.stretch + vec.shift)
        r.part_one[i + 1] = grad * stretched
        return sums[0] + column_sum(grad), sums[1] + column_sum(grad * unit_two)

    nothing = (jnp.zeros((1, C), full), jnp.zeros((1, C), full))
    plain, crossed = lax.fori_loop(0, IMAGE_ROWS, second_row, nothing)
    scale_grad = crossed * vec.gain_two + plain * vec.bias_two
    shift_grad = plain
    gain_two, bias_two = crossed * vec.stretch, plain * vec.stretch
    r.tile[1] = sums_tile(bias_two * vec.gain_two, gain_two * vec.gain_two)
    two_edges = band.edges(1, r.part_one.at[1], r.part_one.at[IMAGE_ROWS], r.part_one)
    tiles = band.send_tile(1, r.tile.at[1], r.window.at[1])
    loads.act_two.wait()
    sibling.act2.wait()
    sibling.shifts_two.wait()
    conv_grads(SECOND_CONV, r.act2, r.sib_act2, r.sib_shifts_two)
    for copy in tiles:
        copy.wait()
    band.wait_edges(two_edges)
    means = item_means(r.window.at[1])
    offset_two, slope_two = means[0:1] * vec.scale_two, means[1:2] * vec.scale_two

    def hidden_row(i, bias):
        values = r.part_one[i] - offset_two - unit(r.hid[i], norm_two) * slope_two
        values = kept(i, values, vec)
        spread_rows(i, values)
        inside = jnp.where((i > 0) & (i <= IMAGE_ROWS), 1.0, 0.0)
        return bias + inside * column_sum(values.astype(low).astype(full))

    conv_bias_one = lax.fori_loop(0, IMAGE_ROWS + 2, hidden_row, jnp.zeros((1, C), full))
    sibling.shifts_one = to_sibling(9, shift_half, r.sib_shifts_one)
    for k in (PROJ, QKV, WORDS, WORDS + 1):
        streams[k].advance()
    loads.conv_first.wait()
    loads.image.wait()
    r.product[...] = conv_back().reshape(IMAGE_ROWS, W, C)

    def first_row(i, sums):
        unit_one = unit(r.img[i].astype(full), norm_one)
        normed = unit_one * vec.gain_one + vec.bias_one
        grad = r.product[i] * silu_slope_of(normed)
        r.product[i] = grad
        return sums[0] + column_sum(grad), sums[1] + column_sum(grad * unit_one)

    plain, crossed = lax.fori_loop(0, IMAGE_ROWS, first_row, nothing)
    gain_one, bias_one = crossed, plain
    r.tile[2] = sums_tile(plain * vec.gain_one, crossed * vec.gain_one)
    tiles = band.send_tile(2, r.tile.at[2], r.window.at[2])
    rows = [
        gain_one,
        gain_two,
        gain_three,
        bias_one,
        bias_two,
        bias_three,
        conv_bias_one,
        conv_bias_two,
        query_sum,
        value_sum,
        word_sum[0],
        word_sum[1],
        up_sum,
        jnp.zeros((1, C), full),
        scale_grad,
        shift_grad,
    ]
    for i, values in enumerate(rows):
        r.own_rows[i : i + 1, :] = values
    row_copies = band.send_tile(3, r.own_rows, r.band_rows)
    loads.act_one.wait()
    sibling.act1.wait()
    sibling.shifts_one.wait()
    conv_grads(FIRST_CONV, r.act1, r.sib_act1, r.sib_shifts_one)
    for copy in tiles:
        copy.wait()
    means = item_means(r.window.at[2])
    offset_one, slope_one = means[0:1] * vec.scale_one, means[1:2] * vec.scale_one
    ratio = vec.gain_one * vec.scale_one

    def image_row(i, carry):
        unit_one = unit(r.img[i].astype(full), norm_one)
        values = r.part_two[i + 1] + r.product[i] * ratio - offset_one - unit_one * slope_one
        r.image_grad[i] = values
        return carry

    lax.fori_loop(0, IMAGE_ROWS, image_row, 0)

    for copy in row_copies:
        copy.wait()
    total = jnp.zeros((16, C), full)
    for b in range(SPAN):
        total = total + r.band_rows[b]
    r.half_rows[0:16, :] = total
    for b in range(SPAN):
        r.half_rows[16 + 2 * b : 18 + 2 * b, :] = r.band_rows[b, 14:16, :]
    far_copy = remote(
        r.half_rows, r.far_rows, r.small_send.at[0], r.small_recv.at[0], partner[FAR]
    )
    far_copy.start()
    for k in range(SECOND_CONV, len(STREAMS)):
        streams[k].advance()
    loads.text_weight.wait()

    def caption_columns(n, carry):
        columns = pl.ds(pl.multiple_of(n * C, C), C)
        r.caption_grad[:, columns] = dot_last(r.joined_words[...], r.text_w[columns, :])
        return carry

    lax.fori_loop(0, EMB // C, caption_columns, 0)
    loads.embed_weight = load(13, r.embed_weight, r.text_w)
    far_copy.wait()
    first_half = jnp.where(place[FAR] == 0, r.half_rows[16:32, :], r.far_rows[16:32, :])
    other_half = jnp.where(place[FAR] == 0, r.far_rows[16:32, :], r.half_rows[16:32, :])
    r.group_rows[0:16, :] = r.half_rows[0:16, :] + r.far_rows[0:16, :]
    r.group_rows[16:32, :] = first_half
    r.group_rows[32:48, :] = other_half
    slots = r.slot_of_band.shape[0]
    for k in range(2):
        table = jnp.zeros((slots, C), full)
        for b in range(2 * SPAN):
            values = r.group_rows[16 + 2 * b + k : 17 + 2 * b + k, :]
            table = table + jnp.where(r.slot_of_band[:, b * 128 : b * 128 + 1] > 0.0, values, 0.0)
        r.own_table[slots * k : slots * (k + 1), :] = table
    r.own_table[2 * slots :, :] = r.group_rows[0:16, :]
    group_copy = remote(
        r.own_table,
        r.other_table,
        r.small_send.at[1],
        r.small_recv.at[1],
        partner[GROUP],
    )
    group_copy.start()
    def advance_all():
        for stream in streams:
            if stream.step < LANDINGS + 2:
                stream.advance()

    advance_all()
    loads.embed_weight.wait()
    table = [r.own_table[slots * k : slots * (k + 1), :].astype(low) for k in range(2)]

    def embedding_columns(n, carry):
        columns = pl.ds(pl.multiple_of(n * C, C), C)
        grad = dot_last(table[0], r.text_w[columns, 0:C]) + dot_last(table[1], r.text_w[columns, C:])
        source = r.embedding[:, columns].astype(full)
        r.embedding_grad[:, columns] = grad * silu_slope_of(source)
        return carry

    lax.fori_loop(0, EMB // C, embedding_columns, 0)
    advance_all()
    group_copy.wait()
    share_copy.wait()
    for k in range(2):
        columns = slice(k * C, (k + 1) * C)
        other = r.other_table[slots * k : slots * (k + 1), :].astype(low)
        r.embed_weight_grad[:, columns] = dot_first(r.silu_share[...], table[k]) + dot_first(
            r.other_share[...], other
        )
        r.embed_bias_grad[:, columns] = column_sum(table[k].astype(full)) + column_sum(
            other.astype(full)
        )
    sums = r.own_table[2 * slots :, :] + r.other_table[2 * slots :, :]
    r.norm_gains_grad[...] = sums[0:3]
    r.norm_biases_grad[...] = sums[3:6]
    r.conv_biases_grad[...] = sums[6:8]
    for target, k in ((r.qv_bias_grad, 8), (r.text_bias_grad, 10)):
        target[:, 0:C] = sums[k : k + 1]
        target[:, C:] = sums[k + 1 : k + 2]
    r.proj_bias_grad[...] = sums[12:13]
    for _ in range(LANDINGS):
        advance_all()

    def write(stream, target, first_row):
        rows, columns = STREAMS[stream][:2]
        for side, source in ((group, r.folded[stream]), (1 - group, r.whole[stream])):
            for k in range(2):
                target[
                    pl.ds(pl.multiple_of(first_row + side * rows, rows), rows),
                    k * columns : (k + 1) * columns,
                ] = source[k].astype(full)

    for j in range(3):
        write(FIRST_CONV + j, r.conv_first_grad, j * 96)
        write(SECOND_CONV + j, r.conv_second_grad, j * 96)
    for j in range(2):
        write(WORDS + j, r.text_grad, j * 64)
    write(QKV, r.qkv_grad, 0)
    write(PROJ, r.proj_grad, 0)


def silu_slope_of(source):
    sigma = 1.0 / (1.0 + jnp.exp(-source))
    return sigma * (1.0 + source * (1.0 - sigma))


def back(ident, vectors, slot_of_band, silu_share, embedding, anywhere):
    low, full = jnp.bfloat16, jnp.float32
    pixels = IMAGE_ROWS * W
    slots = slot_of_band.shape[0]
    outs = dict(
        result=((pixels, C), low),
        image_grad=((IMAGE_ROWS, W, C), full),
        caption_grad=((TEXT, EMB), full),
        conv_first_grad=((288, C), full),
        conv_second_grad=((288, C), full),
        qkv_grad=((32, 3 * C), full),
        text_grad=((128, 2 * C), full),
        proj_grad=((32, C), full),
        embedding_grad=(embedding.shape, full),
        embed_weight_grad=((silu_share.shape[1], 2 * C), full),
        norm_gains_grad=((3, C), full),
        norm_biases_grad=((3, C), full),
        conv_biases_grad=((2, C), full),
        embed_bias_grad=((1, 2 * C), full),
        qv_bias_grad=((1, 2 * C), full),
        text_bias_grad=((1, 2 * C), full),
        proj_bias_grad=((1, C), full),
    )
    padded = (IMAGE_ROWS + 2, W, C)
    scratch = dict(
        heads=((HEADS, pixels, 4 * HEAD), low),
        head_words=((HEADS, TEXT, 2 * HEAD), low),
        joined=((pixels, 4 * C), low),
        joined_words=((TEXT, 2 * C), low),
        mid=(padded, full),
        part_two=(padded, full),
        part_one=(padded, full),
        hid=(padded, full),
        product=((IMAGE_ROWS, W, C), full),
        img=((IMAGE_ROWS, W, C), low),
        up=((pixels, C), low),
        act1=((pixels + 2 * W, C), low),
        act2=((pixels + 2 * W, C), low),
        act3=((pixels, C), low),
        cap=((TEXT, EMB), low),
        conv_w=((9 * C, C), low),
        qkv_w=((C, 3 * C), low),
        proj_w=((C, C), low),
        text_w=((EMB, 2 * C), low),
        sib_up=((pixels, C // 2), low),
        sib_act1=((pixels + 2 * W, C), low),
        sib_act2=((pixels + 2 * W, C), low),
        sib_act3=((pixels, C), low),
        sib_cap=((TEXT, EMB), low),
        sib_attended=((pixels, C), low),
        sib_qkv=((pixels, 3 * C // 2), low),
        sib_words=((TEXT, C), low),
        sib_shifts_one=((3, IMAGE_ROWS, W, C // 2), low),
        sib_shifts_two=((3, IMAGE_ROWS, W, C // 2), low),
        shifts=((3,) + padded, low),
        blocks=((C, C), low),
        tile=((3, 8, C), full),
        window=((3, SPAN, 8, C), full),
        own_rows=((16, C), full),
        band_rows=((SPAN, 16, C), full),
        half_rows=((32, C), full),
        far_rows=((32, C), full),
        group_rows=((48, C), full),
        own_table=((2 * slots + 16, C), full),
        other_table=((2 * slots + 16, C), full),
        other_share=(silu_share.shape, low),
    )
    scratch.update(grads=[((2,) * 5 + s[:2], low) for s in STREAMS])
    scratch.update(landings=[((2,) * (4 - i) + s[:2], low) for s in STREAMS for i in range(LANDINGS)])
    scratch.update(folded=[((2,) + s[:2], low) for s in STREAMS])
    scratch.update(whole=[((2,) + s[:2], low) for s in STREAMS])
    semaphores = dict(
        swap_send=(2, SPAN),
        swap_recv=(2, SPAN),
        load_sem=(14,),
        sib_send=(10,),
        sib_recv=(10,),
        edge_send=(2, 2),
        edge_recv=(2, 2),
        tile_send=(4, SPAN),
        tile_recv=(4, SPAN),
        fold_send=(len(STREAMS), LANDINGS + 2),
        fold_recv=(len(STREAMS), LANDINGS + 2),
        small_send=(3,),
        small_recv=(3,),
    )
    inputs = dict(
        vectors=vectors, slot_of_band=slot_of_band, silu_share=silu_share, embedding=embedding
    )
    return call_named(back_kernel, ident, (), inputs, anywhere, outs, scratch, semaphores)


def front_kernel(names, *refs):
    low, full = jnp.bfloat16, jnp.float32
    r = grouped(names, refs)
    band = Band(r)
    band.meet()
    loads = types.SimpleNamespace()

    def load(k, source, target):
        copy = pltpu.make_async_copy(source, target, r.load_sem.at[k])
        copy.start()
        return copy

    loads.image = load(0, r.image, r.img.at[1 : IMAGE_ROWS + 1])
    image_edges = band.edges(0, r.image.at[0], r.image.at[IMAGE_ROWS - 1], r.img)
    loads.conv_first = load(1, r.conv_first, r.first_w)
    loads.embed_weight = load(2, r.embed_weight, r.embed_w)
    loads.upstream = load(3, r.upstream, r.up)
    loads.proj_weight = load(4, r.proj_weight, r.proj_w)
    loads.conv_second = load(5, r.conv_second, r.second_w)
    loads.caption = load(6, r.caption, r.cap)
    loads.text_weight = load(7, r.text_weight, r.text_w)
    loads.qkv_weight = load(8, r.qkv_weight, r.qkv_w)

    mine = r.items[band.row]
    same = [(r.items[band.base + b] == mine).astype(full) for b in range(SPAN)]
    masks = [jnp.full((1, C), m, full) for m in same]
    bands = masks[0]
    for m in masks[1:]:
        bands = bands + m
    per_item = 1.0 / (bands * (IMAGE_ROWS * W * (C // NORM_GROUPS)))
    before = jnp.where(band.has_above, r.items[jnp.maximum(band.row - 1, 0)], -1)
    after = jnp.where(
        band.has_below, r.items[jnp.minimum(band.row + 1, r.items.shape[0] - 1)], -1
    )
    found = types.SimpleNamespace(
        gain_one=r.norm_gains[0:1, :],
        gain_two=r.norm_gains[1:2, :],
        gain_three=r.norm_gains[2:3, :],
        bias_one=r.norm_biases[0:1, :],
        bias_two=r.norm_biases[1:2, :],
        bias_three=r.norm_biases[2:3, :],
        proj_bias=r.proj_bias[...],
        keep_above=jnp.full((1, C), (before == mine).astype(full)),
        keep_below=jnp.full((1, C), (after == mine).astype(full)),
        per_item=per_item,
    )
    for target in (r.img, r.hidden, r.middle):
        band.zero_edges(target)
    nothing = (jnp.zeros((1, C), full), jnp.zeros((1, C), full))

    def norm_of(k):
        means = band.item_means(r.window.at[k], masks, per_item)
        return means[0:1], lax.rsqrt(means[1:2] - means[0:1] * means[0:1] + epsilon)

    loads.image.wait()

    def image_sums(i, sums):
        values = r.img[i + 1].astype(full)
        return sums[0] + column_sum(values), sums[1] + column_sum(values * values)

    r.tile[0] = sums_tile(*lax.fori_loop(0, IMAGE_ROWS, image_sums, nothing))
    tiles = band.send_tile(0, r.tile.at[0], r.window.at[0])

    band.fill_blocks()
    slot = lax.broadcasted_iota(jnp.int32, r.embedding.shape, 0)
    chosen = jnp.where(slot == mine, r.embedding[...].astype(full), 0.0)
    chosen = jnp.sum(chosen, axis=0, keepdims=True)
    chosen = chosen / (1.0 + jnp.exp(-chosen))
    chosen = jnp.broadcast_to(chosen, (16, EMB)).astype(low)
    loads.embed_weight.wait()
    modulation = dot(chosen, r.embed_w[...])[0:1] + r.embed_bias[...]
    found.stretch = 1.0 + modulation[:, 0:C]
    found.shift = modulation[:, C:]

    def spread_rows(i, values, target):
        values = kept(i, values, found)
        from_left, from_right = side_shifts(values)
        r.shifts[0, i] = from_left.astype(low)
        r.shifts[1, i] = values.astype(low)
        r.shifts[2, i] = from_right.astype(low)
        target[pl.ds(pl.multiple_of(i * W, W), W), :] = values.astype(low)

    def conv(weight):
        total = jnp.zeros((IMAGE_ROWS * W, C), full)
        for t in range(9):
            view = r.shifts[t % 3, t // 3 : t // 3 + IMAGE_ROWS].reshape(IMAGE_ROWS * W, C)
            total = total + dot(view, weight[t * C : (t + 1) * C, :])
        return total

    for copy in tiles:
        copy.wait()
    band.wait_edges(image_edges)
    found.mean_one, found.scale_one = norm_of(0)

    def first_row(i, carry):
        unit = (r.img[i].astype(full) - found.mean_one) * found.scale_one
        normed = unit * found.gain_one + found.bias_one
        spread_rows(i, normed / (1.0 + jnp.exp(-normed)), r.act_one)
        return carry

    lax.fori_loop(0, IMAGE_ROWS + 2, first_row, 0)
    loads.conv_first.wait()
    total = conv(r.first_w) + r.conv_biases[0:1, :]
    r.hidden[1 : IMAGE_ROWS + 1] = total.reshape(IMAGE_ROWS, W, C)
    hidden_edges = band.edges(1, r.hidden.at[1], r.hidden.at[IMAGE_ROWS], r.hidden)
    r.tile[1] = sums_tile(column_sum(total), column_sum(total * total))
    tiles = band.send_tile(1, r.tile.at[1], r.window.at[1])

    loads.caption.wait()
    loads.text_weight.wait()
    words = (dot(r.cap[...], r.text_w[...]) + r.text_bias[...]).astype(low)
    for h in range(HEADS):
        parts = [words[:, k * C + h * HEAD : k * C + (h + 1) * HEAD] for k in range(2)]
        r.words[h] = jnp.concatenate(parts, axis=1)
    swaps = band.swap(0, r.words, r.head_words)
    r.head_words[band.lane] = r.words[band.lane]
    for copy in tiles:
        copy.wait()
    band.wait_edges(hidden_edges)
    found.mean_two, found.scale_two = norm_of(1)

    def second_row(i, carry):
        unit = (r.hidden[i] - found.mean_two) * found.scale_two
        normed = unit * found.gain_two + found.bias_two
        shifted = normed * found.stretch + found.shift
        spread_rows(i, shifted / (1.0 + jnp.exp(-shifted)), r.act_two)
        return carry

    lax.fori_loop(0, IMAGE_ROWS + 2, second_row, 0)
    loads.conv_second.wait()
    total = conv(r.second_w) + r.conv_biases[1:2, :]
    total = total + r.img[1 : IMAGE_ROWS + 1].astype(full).reshape(IMAGE_ROWS * W, C)
    r.middle[1 : IMAGE_ROWS + 1] = total.reshape(IMAGE_ROWS, W, C)
    r.tile[2] = sums_tile(column_sum(total), column_sum(total * total))
    tiles = band.send_tile(2, r.tile.at[2], r.window.at[2])
    middle_edges = band.edges(2, r.middle.at[1], r.middle.at[IMAGE_ROWS], r.middle)

    loads.upstream.wait()
    loads.proj_weight.wait()
    attended_grad = dot_last(r.up[...], r.proj_w[...]).astype(low)
    loads.qkv_weight.wait()
    for h in range(HEADS):
        r.pieces[h, :, 3 * HEAD :] = attended_grad[:, h * HEAD : (h + 1) * HEAD]
    for copy in tiles:
        copy.wait()
    found.mean_three, found.scale_three = norm_of(2)
    for i in range(2):
        middle = r.middle[1 + 4 * i : 5 + 4 * i].reshape(4 * W, C)
        unit = (middle - found.mean_three) * found.scale_three
        block = slice(i * 4 * W, (i + 1) * 4 * W)
        act = (unit * found.gain_three + found.bias_three).astype(low)
        r.act_three[block, :] = act
        projected = dot(act, r.qkv_w[...])
        queries = (projected[:, 0:C] + r.qv_bias[:, 0:C]).astype(low)
        keys = projected[:, C : 2 * C].astype(low)
        values = (projected[:, 2 * C :] + r.qv_bias[:, C:]).astype(low)
        for h in range(HEADS):
            head = slice(h * HEAD, (h + 1) * HEAD)
            r.pieces[h, block, 0 : 2 * HEAD] = jnp.concatenate([queries[:, head], keys[:, head]], axis=1)
            r.pieces[h, block, 2 * HEAD : 3 * HEAD] = values[:, head]
    swaps = swaps + band.swap(1, r.pieces, r.heads)
    r.heads[band.lane] = r.pieces[band.lane]
    fields = [getattr(found, name) for name in Vectors._fields]
    for i, values in enumerate(fields):
        r.vectors[i : i + 1, :] = values
    r.vectors[len(fields) : VECTOR_ROWS, :] = jnp.zeros((VECTOR_ROWS - len(fields), C), full)
    for b in range(SPAN):
        r.vectors[VECTOR_ROWS + b : VECTOR_ROWS + b + 1, :] = masks[b]
    band.wait_edges(middle_edges)
    for copy in swaps:
        copy.wait()


def front(ident, items, inputs, anywhere):
    low, full = jnp.bfloat16, jnp.float32
    pixels = IMAGE_ROWS * W
    padded = (IMAGE_ROWS + 2, W, C)
    outs = dict(
        heads=((HEADS, pixels, 4 * HEAD), low),
        head_words=((HEADS, TEXT, 2 * HEAD), low),
        act_one=((pixels + 2 * W, C), low),
        act_two=((pixels + 2 * W, C), low),
        act_three=((pixels, C), low),
        hidden=(padded, full),
        middle=(padded, full),
        vectors=((VECTOR_ROWS + SPAN, C), full),
    )
    scratch = dict(
        img=(padded, low),
        up=((pixels, C), low),
        cap=((TEXT, EMB), low),
        first_w=((9 * C, C), low),
        second_w=((9 * C, C), low),
        embed_w=((EMB, 2 * C), low),
        text_w=((EMB, 2 * C), low),
        qkv_w=((C, 3 * C), low),
        proj_w=((C, C), low),
        shifts=((3,) + padded, low),
        blocks=((C, C), low),
        tile=((3, 8, C), full),
        window=((3, SPAN, 8, C), full),
        words=((HEADS, TEXT, 2 * HEAD), low),
        pieces=((HEADS, pixels, 4 * HEAD), low),
    )
    semaphores = dict(
        load_sem=(9,),
        edge_send=(3, 2),
        edge_recv=(3, 2),
        tile_send=(3, SPAN),
        tile_recv=(3, SPAN),
        swap_send=(2, SPAN),
        swap_recv=(2, SPAN),
    )
    return call_named(
        front_kernel, ident, dict(items=items), inputs, anywhere, outs, scratch, semaphores
    )


def hand_over_kernel(count, *refs):
    sources, targets, sem = refs[:count], refs[count : 2 * count], refs[2 * count]
    copies = [
        pltpu.make_async_copy(source, target, sem.at[k])
        for k, (source, target) in enumerate(zip(sources, targets))
    ]
    for copy in copies:
        copy.start()
    for copy in copies:
        copy.wait()


def hand_over(arrays):
    anywhere = pl.BlockSpec(memory_space=pl.ANY)
    return pl.pallas_call(
        functools.partial(hand_over_kernel, len(arrays)),
        out_shape=tuple(jax.ShapeDtypeStruct(a.shape, a.dtype) for a in arrays),
        in_specs=[anywhere] * len(arrays),
        out_specs=(anywhere,) * len(arrays),
        scratch_shapes=[pltpu.SemaphoreType.DMA((len(arrays),))],
        name=hand_over.__name__,
    )(*arrays)


def blocks_of(rows):
    return rows.reshape(rows.shape[0], NORM_GROUPS, -1)


def spread(values):
    return jnp.repeat(values, C // NORM_GROUPS)


def in_halves(
    image,
    embedding,
    caption,
    item_of_band,
    out_grad,
    norm_gains,
    norm_biases,
    conv_first,
    conv_second,
    conv_biases,
    embed_weight,
    embed_bias,
    qkv_weight,
    qv_bias,
    text_weight,
    text_bias,
    proj_weight,
    proj_bias,
):
    low = jnp.bfloat16
    pixels = image.shape[1]
    position = lax.axis_index(ROWS)
    items = item_of_band[0]
    slots = items.shape[0]
    by_row = (-1, W, C)
    ahead = front(
        0,
        items,
        dict(
            embedding=embedding[0],
            norm_gains=norm_gains,
            norm_biases=norm_biases,
            conv_biases=conv_biases,
            embed_bias=embed_bias[None],
            qv_bias=qv_bias[None],
            text_bias=text_bias[None],
            proj_bias=proj_bias[None],
        ),
        dict(
            image=image.reshape(by_row),
            conv_first=conv_first,
            embed_weight=embed_weight,
            upstream=out_grad[0],
            proj_weight=proj_weight,
            conv_second=conv_second,
            caption=caption[0, 0],
            text_weight=text_weight,
            qkv_weight=qkv_weight,
        ),
    )
    pieces, words = one_head(items, ahead.heads, ahead.head_words)
    slot_of_band = (jnp.arange(slots)[:, None] == items[None, :]).astype(jnp.float32)
    row_share = EMB // lax.axis_size(ROWS)
    share = lax.dynamic_slice_in_dim(embedding[0], position * row_share, row_share, 1)
    silu_share = jax.nn.silu(share.astype(jnp.float32)).astype(low)
    out = back(
        1,
        ahead.vectors,
        jnp.repeat(slot_of_band, 128, axis=1),
        silu_share,
        embedding[0],
        dict(
            pieces=pieces,
            words=words,
            middle=ahead.middle,
            qkv_weight=qkv_weight,
            proj_weight=proj_weight,
            upstream=out_grad[0],
            act_three=ahead.act_three,
            caption=caption[0, 0],
            conv_second=conv_second,
            conv_first=conv_first,
            hidden=ahead.hidden,
            act_two=ahead.act_two,
            act_one=ahead.act_one,
            image=image.reshape(by_row),
            text_weight=text_weight,
            embed_weight=embed_weight,
        ),
    )
    out = types.SimpleNamespace(**dict(zip(vars(out), hand_over(list(vars(out).values())))))
    return (
        out.result[None],
        out.image_grad.reshape(1, pixels, C),
        out.embedding_grad[None],
        out.caption_grad[None, None],
        out.norm_gains_grad,
        out.norm_biases_grad,
        out.conv_first_grad,
        out.conv_second_grad,
        out.conv_biases_grad,
        out.embed_weight_grad,
        out.embed_bias_grad.reshape(-1),
        out.qkv_grad,
        out.qv_bias_grad.reshape(-1),
        out.text_grad,
        out.text_bias_grad.reshape(-1),
        out.proj_grad,
        out.proj_bias_grad.reshape(-1),
    )


def shards(
    image,
    embedding,
    caption,
    item_of_band,
    out_grad,
    norm_gains,
    norm_biases,
    conv_first,
    conv_second,
    conv_biases,
    embed_weight,
    embed_bias,
    qkv_weight,
    qv_bias,
    text_weight,
    text_bias,
    proj_weight,
    proj_bias,
):
    low = jnp.bfloat16
    full = jnp.float32
    pixels = image.shape[1]
    band_items = item_of_band[0]
    slots = band_items.shape[0]
    if slots == 2 * SPAN and lax.axis_size(ITEMS) == 2 and HEADS == SPAN:
        return in_halves(
            image,
            embedding,
            caption,
            item_of_band,
            out_grad,
            norm_gains,
            norm_biases,
            conv_first,
            conv_second,
            conv_biases,
            embed_weight,
            embed_bias,
            qkv_weight,
            qv_bias,
            text_weight,
            text_bias,
            proj_weight,
            proj_bias,
        )
    position = lax.axis_index(ROWS)
    my_item = band_items[position]
    slot_hot = (jnp.arange(slots) == my_item).astype(full)
    item_count = jnp.sum((band_items == my_item).astype(full)) * pixels * (C // NORM_GROUPS)
    reach = position + jnp.arange(-REACH, REACH + 1)
    near = (reach >= 0) & (reach < slots)
    near = near & (band_items[jnp.clip(reach, 0, slots - 1)] == my_item)
    keep = jnp.concatenate(
        [
            jnp.full((W, 1), near[REACH - 1]),
            jnp.full((pixels, 1), True),
            jnp.full((W, 1), near[REACH + 1]),
        ]
    )
    own_lead = jnp.logical_not(near[REACH - 1])

    def totals(ident, first, second, edges=None):
        sums = jnp.stack([jnp.sum(blocks_of(first), axis=(0, 2)), jnp.sum(blocks_of(second), axis=(0, 2))])
        tile = jnp.pad(sums, ((0, 6), (0, 128 - NORM_GROUPS)))
        if edges is not None:
            outcome = exchange(ident, slots, tile, (edges[:W], edges[-W:]))
        else:
            outcome = exchange(ident, slots, tile)
        summed = jnp.sum(jnp.where(near[:, None, None], outcome[0], 0.0), axis=0)
        summed = summed[:2, :NORM_GROUPS] / item_count
        return summed, outcome[1:]

    def stats(summed):
        scales = lax.rsqrt(summed[1] - summed[0] * summed[0] + epsilon)
        return spread(summed[0]), spread(scales)

    inputs = image[0].astype(full)
    summed, (above, below) = totals(0, inputs, inputs * inputs, image[0])
    means_one, scales_one = stats(summed)
    padded = jnp.concatenate([above, image[0], below]).astype(full)
    unit_padded = (padded - means_one) * scales_one
    normed_padded = unit_padded * norm_gains[0] + norm_biases[0]
    act_one_padded = jnp.where(keep, jax.nn.silu(normed_padded), 0.0).astype(low)
    unit_one = unit_padded[W:-W]
    normed_one = normed_padded[W:-W]
    taps_one = jnp.concatenate(taps_of(act_one_padded, False), axis=1)
    hidden_one = dot(taps_one, conv_first) + conv_biases[0]
    embed_silu = jax.nn.silu(embedding[0].astype(full)).astype(low)
    my_silu = dot(slot_hot.astype(low)[None], embed_silu).astype(low)
    modulation = dot(my_silu, embed_weight)[0] + embed_bias
    scale_part = modulation[:C]
    shift_part = modulation[C:]
    summed, (above, below) = totals(1, hidden_one, hidden_one * hidden_one, hidden_one)
    means_two, scales_two = stats(summed)
    hidden_padded = jnp.concatenate([above, hidden_one, below])
    unit_padded = (hidden_padded - means_two) * scales_two
    normed_padded = unit_padded * norm_gains[1] + norm_biases[1]
    shifted_padded = normed_padded * (1.0 + scale_part) + shift_part
    act_two_padded = jnp.where(keep, jax.nn.silu(shifted_padded), 0.0).astype(low)
    unit_two = unit_padded[W:-W]
    normed_two = normed_padded[W:-W]
    shifted = shifted_padded[W:-W]
    taps_two = jnp.concatenate(taps_of(act_two_padded, False), axis=1)
    middle = inputs + dot(taps_two, conv_second) + conv_biases[1]
    summed, _ = totals(2, middle, middle * middle)
    means_three, scales_three = stats(summed)
    unit_three = (middle - means_three) * scales_three
    act_three = (unit_three * norm_gains[2] + norm_biases[2]).astype(low)
    projected = dot(act_three, qkv_weight)
    queries = (projected[:, :C] + qv_bias[:C]).astype(low)
    keys_values = jnp.concatenate(
        [projected[:, C : 2 * C], projected[:, 2 * C :] + qv_bias[C:]], axis=1
    ).astype(low)
    captions = caption[0, 0]
    text_kv = lax.cond(
        own_lead,
        lambda: (dot(captions, text_weight) + text_bias).astype(low),
        lambda: jnp.zeros((TEXT, 2 * C), low),
    )
    upstream = out_grad[0]
    upstream_float = upstream.astype(full)
    attended_grad = dot_last(upstream, proj_weight).astype(low)
    group = lax.axis_index(ITEMS)
    groups = lax.axis_size(ITEMS)
    attended_low, query_low, key_value_low, text_low = attention_by_band(
        band_items, position, queries, keys_values, text_kv, attended_grad
    )
    result = middle + dot(attended_low, proj_weight) + proj_bias
    proj_weight_grad = dot_first(attended_low, upstream)
    proj_bias_grad = jnp.sum(upstream_float, axis=0)
    qkv_grad = jnp.concatenate([query_low, key_value_low], axis=1)
    qkv_weight_grad = dot_first(act_three, qkv_grad)
    qv_bias_grad = jnp.sum(
        jnp.concatenate([query_low, key_value_low[:, C:]], axis=1).astype(full), axis=0
    )
    text_weight_grad = dot_first(captions, text_low)
    text_bias_grad = jnp.sum(text_low.astype(full), axis=0)
    caption_grad = dot_last(text_low, text_weight)[None, None]
    three_grad = dot_last(qkv_grad, qkv_weight)
    gain_three = jnp.sum(three_grad * unit_three, axis=0)
    bias_three = jnp.sum(three_grad, axis=0)

    def conv_back(padded, weight):
        views = jnp.stack(taps_of(padded, True))
        return jnp.einsum(
            "tpd,tcd->pc", views, weight.reshape(9, C, C), preferred_element_type=full
        )

    def norm_back(ident, grad_unit, unit_value, scales, base, with_edges=True):
        scaled = base + grad_unit * scales
        edges = jnp.concatenate([scaled, unit_value], axis=1) if with_edges else None
        summed, around = totals(ident, grad_unit, grad_unit * unit_value, edges)
        mean_grad, mean_cross = spread(summed[0]) * scales, spread(summed[1]) * scales
        if not with_edges:
            return scaled - mean_grad - unit_value * mean_cross
        both = jnp.concatenate([around[0], edges, around[1]])
        return both[:, :C] - mean_grad - both[:, C:] * mean_cross

    middle_padded = norm_back(3, three_grad * norm_gains[2], unit_three, scales_three, upstream_float)
    middle_grad = middle_padded[W:-W]
    low_padded = jnp.where(keep, middle_padded, 0.0).astype(low)
    hidden_two_low = low_padded[W:-W]
    conv_bias_two = jnp.sum(hidden_two_low.astype(full), axis=0)
    conv_second_grad = dot_first(taps_two, hidden_two_low)
    act_two_grad = conv_back(low_padded, conv_second)
    shifted_grad = act_two_grad * silu_slope(shifted)
    modulation_grad = jnp.concatenate(
        [jnp.sum(shifted_grad * normed_two, axis=0), jnp.sum(shifted_grad, axis=0)]
    )
    normed_two_grad = shifted_grad * (1.0 + scale_part)
    gain_two = jnp.sum(normed_two_grad * unit_two, axis=0)
    bias_two = jnp.sum(normed_two_grad, axis=0)
    hidden_back = norm_back(4, normed_two_grad * norm_gains[1], unit_two, scales_two, 0.0)
    low_padded = jnp.where(keep, hidden_back, 0.0).astype(low)
    hidden_one_low = low_padded[W:-W]
    conv_bias_one = jnp.sum(hidden_one_low.astype(full), axis=0)
    conv_first_grad = dot_first(taps_one, hidden_one_low)
    act_one_grad = conv_back(low_padded, conv_first)
    normed_one_grad = act_one_grad * silu_slope(normed_one)
    gain_one = jnp.sum(normed_one_grad * unit_one, axis=0)
    bias_one = jnp.sum(normed_one_grad, axis=0)
    image_grad = norm_back(
        5, normed_one_grad * norm_gains[0], unit_one, scales_one, middle_grad, False
    )
    group_hot = (jnp.arange(groups) == group).astype(full)
    tables = group_hot[:, None, None] * slot_hot[None, :, None] * modulation_grad
    vectors = jnp.concatenate(
        [
            gain_one,
            gain_two,
            gain_three,
            bias_one,
            bias_two,
            bias_three,
            conv_bias_one,
            conv_bias_two,
            qv_bias_grad,
            text_bias_grad,
            proj_bias_grad,
        ]
    )
    small = jnp.concatenate([tables.reshape(-1, C), vectors.reshape(-1, C)])
    row_share = EMB // lax.axis_size(ROWS)
    silu_share = lax.dynamic_slice_in_dim(embed_silu, position * row_share, row_share, 1)
    grads = (conv_first_grad, conv_second_grad, qkv_weight_grad, text_weight_grad, proj_weight_grad)
    grads = [g.astype(low) for g in grads]
    small = lax.psum(small.astype(low), (ROWS, ITEMS)).astype(full)
    tables_sum = small[: groups * slots * 2].reshape(groups, slots, 2 * C).astype(low)
    part = dot_first(silu_share, jnp.take(tables_sum, group, axis=0)).astype(low)
    matrices = [lax.psum_scatter(g, ROWS, scatter_dimension=0, tiled=True) for g in grads]
    *matrices, embed_weight_grad = [
        lax.psum(m, ITEMS).astype(full) for m in matrices + [part]
    ]
    vectors_sum = small[groups * slots * 2 :]
    modulation_low = jnp.take(tables_sum, group, axis=0)
    embed_bias_grad = jnp.sum(tables_sum.astype(full), axis=(0, 1))
    embedding_grad = dot_last(modulation_low, embed_weight) * silu_slope(embedding[0].astype(full))
    return (
        result.astype(low)[None],
        image_grad[None],
        embedding_grad[None],
        caption_grad,
        vectors_sum[0:3],
        vectors_sum[3:6],
        matrices[0],
        matrices[1],
        vectors_sum[6:8],
        embed_weight_grad,
        embed_bias_grad,
        matrices[2],
        vectors_sum[8:10].reshape(-1),
        matrices[3],
        vectors_sum[10:12].reshape(-1),
        matrices[4],
        vectors_sum[12],
    )


def solution(mesh):
    in_specs = (
        P(ITEMS, ROWS, None),
        P(ITEMS, None, None),
        P(ITEMS, ROWS, None, None),
        P(ITEMS, None),
        P(ITEMS, ROWS, None),
        P(),
        P(),
        P(),
        P(),
        P(),
        P(),
        P(),
        P(),
        P(),
        P(),
        P(),
        P(),
        P(),
    )
    out_specs = (
        P(ITEMS, ROWS, None),
        P(ITEMS, ROWS, None),
        P(ITEMS, None, None),
        P(ITEMS, ROWS, None, None),
        P(),
        P(),
        P(ROWS, None),
        P(ROWS, None),
        P(),
        P(ROWS, None),
        P(),
        P(ROWS, None),
        P(),
        P(ROWS, None),
        P(),
        P(ROWS, None),
        P(),
    )
    return jax.shard_map(shards, mesh=mesh, in_specs=in_specs, out_specs=out_specs, check_vma=False)
```

```python
import functools
import types
import typing

import jax
import jax.numpy as jnp
from jax import lax
from jax.experimental import pallas as pl
from jax.experimental.pallas import tpu as pltpu
from jax.sharding import PartitionSpec as P

C = 512
HEADS = 8
HEAD = 64
EMB = 2048
TEXT = 128
NORM_GROUPS = 32
W = 64
SPAN = 8
ROWS, ITEMS = "rows", "items"


epsilon = 1e-05


def from_behind(array, axis, by):
    length = lax.axis_size(axis)
    pairs = [(i, i + by) for i in range(length) if 0 <= i + by < length]
    return lax.ppermute(array, axis, pairs)


def as_sent(array):
    return jax.tree.map(lambda a: a.astype(jnp.bfloat16) if a.dtype == jnp.float32 else a, array)


def keep_state(state):
    return state


def silu_slope(source):
    sigma = jax.nn.sigmoid(source)
    return sigma * (1.0 + source * (1.0 - sigma))


def dot_first(left_side, right_side):
    return lax.dot_general(
        left_side, right_side, (((0,), (0,)), ((), ())), preferred_element_type=jnp.float32
    )


def dot_last(left_side, right_side):
    return lax.dot_general(
        left_side, right_side, (((1,), (1,)), ((), ())), preferred_element_type=jnp.float32
    )


def head_split(source):
    return source.reshape(source.shape[0], HEADS, HEAD)


def piece_scores(query_heads, key_piece, allowed):
    key_heads = head_split(key_piece[:, :C])
    scores = jnp.einsum(
        "qhd,khd->hqk", query_heads, key_heads, preferred_element_type=jnp.float32
    ) * HEAD ** (-0.5)
    return jnp.where(allowed[None, None, :], scores, -jnp.inf)


def piece_grads(query_heads, grad_heads, log_total, row_dots, key_piece, allowed):
    scores = piece_scores(query_heads, key_piece, allowed)
    weights = jnp.exp(scores - log_total[:, :, None])
    value_heads = head_split(key_piece[:, C:])
    weight_grad = jnp.einsum(
        "qhd,khd->hqk", grad_heads, value_heads, preferred_element_type=jnp.float32
    )
    score_grad = (weights * (weight_grad - row_dots[:, :, None])).astype(jnp.bfloat16)
    outcome = []
    key_heads = head_split(key_piece[:, :C])
    query_grad = jnp.einsum(
        "hqk,khd->qhd", score_grad, key_heads, preferred_element_type=jnp.float32
    ) * HEAD ** (-0.5)
    outcome.append(query_grad.reshape(query_grad.shape[0], C))
    key_grad = jnp.einsum(
        "hqk,qhd->khd", score_grad, query_heads, preferred_element_type=jnp.float32
    ) * HEAD ** (-0.5)
    value_grad = jnp.einsum(
        "hqk,qhd->khd", weights.astype(jnp.bfloat16), grad_heads, preferred_element_type=jnp.float32
    )
    outcome.append(jnp.concatenate([key_grad.reshape(-1, C), value_grad.reshape(-1, C)], axis=1))
    return tuple(outcome)


def source_masks(band_items, source, my_item, pixels):
    slots = band_items.shape[0]
    inside = (source >= 0) & (source < slots)
    clipped = jnp.clip(source, 0, slots - 1)
    source_item = band_items[clipped]
    before_item = band_items[jnp.maximum(clipped - 1, 0)]
    same_item = inside & (source_item == my_item)
    leading = same_item & ((clipped == 0) | (before_item != source_item))
    allowed = jnp.concatenate(
        [jnp.broadcast_to(same_item, (pixels,)), jnp.broadcast_to(leading, (TEXT,))]
    )
    return (allowed, same_item)


REACH = SPAN - 1
LOG2E = 1.4426950408889634
PIX = 512


def dot(left, right):
    return jnp.dot(left, right, preferred_element_type=jnp.float32)


def reach_of(here, slots):
    first = here < SPAN
    low = jnp.maximum(jnp.where(first, 0, SPAN), here - REACH)
    high = jnp.minimum(jnp.where(first, SPAN - 1, slots - 1), here + REACH)
    return low, high


def exchange_kernel(slots, with_edges, *refs):
    if with_edges:
        tile, top, bottom, window, above, below, send_sem, recv_sem, edge_send, edge_recv = refs
    else:
        tile, window, send_sem, recv_sem = refs
    here = lax.axis_index(ROWS)
    low, high = reach_of(here, slots)
    offsets = [o for o in range(-REACH, REACH + 1) if o != 0]

    def reached(offset):
        return (here + offset >= low) & (here + offset <= high)

    barrier = pltpu.get_barrier_semaphore()
    for o in offsets:

        @pl.when(reached(o))
        def _(o=o):
            pl.semaphore_signal(barrier, 1, device_id={ROWS: here + o})

    pl.semaphore_wait(barrier, high - low)

    def edge_copy(o):
        source, target, k = (top, below, 0) if o < 0 else (bottom, above, 1)
        return pltpu.make_async_remote_copy(
            source, target, edge_send.at[k], edge_recv.at[k], device_id={ROWS: here + o}
        )

    def tile_copy(o):
        return pltpu.make_async_remote_copy(
            tile,
            window.at[REACH - o],
            send_sem.at[REACH - o],
            recv_sem.at[REACH - o],
            device_id={ROWS: here + o},
        )

    if with_edges:
        for o in (-1, 1):

            @pl.when(reached(o))
            def _(o=o):
                edge_copy(o).start()

    for o in offsets:

        @pl.when(reached(o))
        def _(o=o):
            tile_copy(o).start()

        @pl.when(jnp.logical_not(reached(-o)))
        def _(o=o):
            window[REACH - o] = jnp.zeros_like(tile)

    window[REACH] = tile[...]
    if with_edges:

        @pl.when(jnp.logical_not(reached(-1)))
        def _():
            above[...] = jnp.zeros_like(above)

        @pl.when(jnp.logical_not(reached(1)))
        def _():
            below[...] = jnp.zeros_like(below)

    for o in offsets:

        @pl.when(reached(o))
        def _(o=o):
            tile_copy(o).wait_send()

        @pl.when(reached(-o))
        def _(o=o):
            tile_copy(o).wait_recv()

    if with_edges:
        for o in (-1, 1):

            @pl.when(reached(o))
            def _(o=o):
                edge_copy(o).wait_send()

            @pl.when(reached(-o))
            def _(o=o):
                edge_copy(o).wait_recv()


def exchange(ident, slots, tile, edges=None):
    vmem = pl.BlockSpec(memory_space=pltpu.VMEM)
    shapes = [jax.ShapeDtypeStruct((2 * REACH + 1,) + tile.shape, tile.dtype)]
    scratch = [pltpu.SemaphoreType.DMA((2 * REACH + 1,))] * 2
    operands = [tile]
    if edges is not None:
        shapes += [jax.ShapeDtypeStruct(e.shape, e.dtype) for e in edges]
        scratch += [pltpu.SemaphoreType.DMA((2,))] * 2
        operands += list(edges)
    return pl.pallas_call(
        functools.partial(exchange_kernel, slots, edges is not None),
        out_shape=tuple(shapes),
        in_specs=[vmem] * len(operands),
        out_specs=(vmem,) * len(shapes),
        scratch_shapes=scratch,
        compiler_params=pltpu.CompilerParams(collective_id=ident, has_side_effects=True),
        name=f"exchange_{ident}",
    )(*operands)


def head_kernel(
    items, y_ref, t_ref, z_ref, zt_ref, xt, vx, tt, tvx, s_ref, p_ref, dk, dv, dkt, dvt
):
    low = jnp.bfloat16
    full = jnp.float32
    bands, pixels = y_ref.shape[0], y_ref.shape[1]
    text = t_ref.shape[1]
    scale = HEAD ** (-0.5)

    def widened(values, rows):
        lanes = lax.broadcasted_iota(jnp.int32, (rows, 2 * HEAD), 1)
        units = jnp.where(lanes < HEAD + 2, 1.0, 0.0).astype(low)
        return jnp.where(lanes < HEAD, values, units)

    def prepare(b, carry):
        block = y_ref[b]
        xt[b] = block.T
        vx[b] = widened(block[:, 2 * HEAD :], pixels)
        words = t_ref[b]
        tt[b] = words.T
        tvx[b] = widened(pltpu.roll(words.astype(full), HEAD, 1).astype(low), text)
        dk[b] = jnp.zeros((pixels, 2 * HEAD), full)
        dv[b] = jnp.zeros((pixels, 2 * HEAD), full)
        dkt[b] = jnp.zeros((text, 2 * HEAD), full)
        dvt[b] = jnp.zeros((text, 2 * HEAD), full)
        return carry

    lax.fori_loop(0, bands, prepare, 0)

    def one_row(columns):
        rows = lax.broadcasted_iota(jnp.int32, (16, columns), 0)
        return jnp.where(rows == 0, 1.0, 0.0).astype(low)

    ones_pixels = one_row(pixels)
    ones_text = one_row(text)
    zeros = jnp.zeros((HEAD, pixels), low)

    base = (lax.axis_index(ROWS) // SPAN) * SPAN

    def query_band(i, carry):
        mine = items[base + i]
        start, end = 0, 0
        for b in range(bands):
            other = items[base + b]
            start = start + jnp.where(other < mine, 1, 0)
            end = end + jnp.where(other <= mine, 1, 0)
        query_t = (xt[i, 0:HEAD, :].astype(full) * scale).astype(low)
        query_rhs = jnp.concatenate([zeros, query_t], 0)
        query_text = jnp.concatenate([query_t, zeros], 0)

        def score(j, top):
            scores = dot(y_ref[j, :, 0 : 2 * HEAD], query_rhs)
            s_ref[j] = scores
            return jnp.maximum(top, jnp.max(scores.reshape(pixels // 8, 8, pixels), axis=0))

        top = lax.fori_loop(start, end, score, jnp.full((8, pixels), -jnp.inf, full))
        scores = dot(t_ref[start], query_text)
        top = jnp.maximum(top, jnp.max(scores.reshape(text // 8, 8, pixels), axis=0))
        top = jnp.max(top, axis=0, keepdims=True)
        weights_text = jnp.exp2((scores - top) * LOG2E).astype(low)
        total = dot(jnp.concatenate([tt[start, HEAD:, :], ones_text], 0), weights_text)

        def gather(j, total):
            weights = jnp.exp2((s_ref[j] - top) * LOG2E).astype(low)
            p_ref[j] = weights
            values = jnp.concatenate([xt[j, 2 * HEAD : 3 * HEAD, :], ones_pixels], 0)
            return total + dot(values, weights)

        total = lax.fori_loop(start, end, gather, total)
        inverse = 1.0 / total[HEAD : HEAD + 1, :]
        attended = total[0:HEAD, :] * inverse
        grad = xt[i, 3 * HEAD :, :].astype(full)
        minus_dots = -jnp.sum(grad * attended, axis=0, keepdims=True) * inverse
        grad_scaled = (grad * inverse).astype(low)
        coarse = minus_dots.astype(low)
        fine = minus_dots - coarse.astype(full)
        rows = lax.broadcasted_iota(jnp.int32, (HEAD, pixels), 0)
        extra = jnp.where(rows == 0, coarse.astype(full), jnp.where(rows == 1, fine, 0.0))
        grad_rhs = jnp.concatenate([grad_scaled, extra.astype(low)], 0)
        grad_rows = jnp.concatenate([grad_scaled, zeros], 0).T
        query_rows = jnp.concatenate([query_t, zeros], 0).T

        def back(j, query_grad):
            weights = p_ref[j]
            steps = (weights.astype(full) * dot(vx[j], grad_rhs)).astype(low)
            dv[j] += dot(weights, grad_rows)
            dk[j] += dot(steps, query_rows)
            return query_grad + dot(xt[j, HEAD : 2 * HEAD, :], steps)

        steps = (weights_text.astype(full) * dot(tvx[start], grad_rhs)).astype(low)
        dvt[start] += dot(weights_text, grad_rows)
        dkt[start] += dot(steps, query_rows)
        query_grad = dot(tt[start, 0:HEAD, :], steps)
        query_grad = lax.fori_loop(start, end, back, query_grad)
        z_ref[i, :, 0 : 2 * HEAD] = jnp.concatenate(
            [attended.astype(low), (query_grad * scale).astype(low)], 0
        ).T
        return carry

    lax.fori_loop(0, bands, query_band, 0)

    def finish(b, carry):
        lanes = lax.broadcasted_iota(jnp.int32, (pixels, 2 * HEAD), 1)
        z_ref[b, :, 2 * HEAD :] = jnp.where(
            lanes < HEAD, dk[b], pltpu.roll(dv[b], HEAD, 1)
        ).astype(low)
        lanes = lax.broadcasted_iota(jnp.int32, (text, 2 * HEAD), 1)
        zt_ref[b] = jnp.where(lanes < HEAD, dkt[b], pltpu.roll(dvt[b], HEAD, 1)).astype(low)
        return carry

    lax.fori_loop(0, bands, finish, 0)


def one_head(items, pieces, words):
    bands, pixels, _ = pieces.shape
    text = words.shape[1]
    low, full = jnp.bfloat16, jnp.float32
    smem = pl.BlockSpec(memory_space=pltpu.SMEM)
    vmem = pl.BlockSpec(memory_space=pltpu.VMEM)
    return pl.pallas_call(
        head_kernel,
        out_shape=(
            jax.ShapeDtypeStruct(pieces.shape, low),
            jax.ShapeDtypeStruct(words.shape, low),
        ),
        in_specs=[smem, vmem, vmem],
        out_specs=(vmem, vmem),
        scratch_shapes=[
            pltpu.VMEM((bands, 4 * HEAD, pixels), low),
            pltpu.VMEM((bands, pixels, 2 * HEAD), low),
            pltpu.VMEM((bands, 2 * HEAD, text), low),
            pltpu.VMEM((bands, text, 2 * HEAD), low),
            pltpu.VMEM((bands, pixels, pixels), full),
            pltpu.VMEM((bands, pixels, pixels), low),
            pltpu.VMEM((bands, pixels, 2 * HEAD), full),
            pltpu.VMEM((bands, pixels, 2 * HEAD), full),
            pltpu.VMEM((bands, text, 2 * HEAD), full),
            pltpu.VMEM((bands, text, 2 * HEAD), full),
        ],
        compiler_params=pltpu.CompilerParams(vmem_limit_bytes=56 << 20),
        name="one_head",
    )(items, pieces, words)


def attention_by_band(band_items, position, queries, keys_values, text_kv, attended_grad):
    my_item = band_items[position]
    pixels = queries.shape[0]
    own_allowed, own_same = source_masks(band_items, position, my_item, pixels)
    packed = jnp.concatenate([keys_values, text_kv], axis=0)
    pieces = [(0, packed, own_allowed, own_same)]
    for distance in range(1, SPAN):
        for offset in (distance, -distance):
            arrived = from_behind(packed, ROWS, offset)
            allowed, same_item = source_masks(band_items, position - offset, my_item, pixels)
            pieces.append((offset, arrived, allowed, same_item))
    query_heads = head_split(queries)
    row_top = jnp.full((HEADS, pixels), -jnp.inf, jnp.float32)
    weight_sum = jnp.zeros((HEADS, pixels), jnp.float32)
    for offset, key_piece, allowed, same_item in pieces:

        def gather_scores(state, key_piece=key_piece, allowed=allowed):
            top_old, sum_old = state
            scores = piece_scores(query_heads, key_piece, allowed)
            top_new = jnp.maximum(top_old, jnp.max(scores, axis=2))
            sum_new = sum_old * jnp.exp(top_old - top_new) + jnp.sum(
                jnp.exp(scores - top_new[:, :, None]), axis=2
            )
            return (top_new, sum_new)

        row_top, weight_sum = lax.cond(same_item, gather_scores, keep_state, (row_top, weight_sum))
    log_total = row_top + jnp.log(weight_sum)
    attended = jnp.zeros((pixels, HEADS, HEAD), jnp.float32)
    for offset, key_piece, allowed, same_item in pieces:

        def add_values(totals, key_piece=key_piece, allowed=allowed):
            scores = piece_scores(query_heads, key_piece, allowed)
            weights = jnp.exp(scores - log_total[:, :, None]).astype(jnp.bfloat16)
            return totals + jnp.einsum(
                "hqk,khd->qhd",
                weights,
                head_split(key_piece[:, C:]),
                preferred_element_type=jnp.float32,
            )

        attended = lax.cond(same_item, add_values, keep_state, attended)
    attended_flat = attended.reshape(pixels, C)
    row_dots = jnp.sum(
        (attended_grad.astype(jnp.float32) * attended_flat).reshape(pixels, HEADS, HEAD), axis=2
    ).T
    grad_heads = head_split(attended_grad)
    query_grad = jnp.zeros((pixels, C), jnp.float32)
    packed_grad = jnp.zeros((pixels + TEXT, 2 * C), jnp.float32)
    zero_piece = jnp.zeros((pixels + TEXT, 2 * C), jnp.float32)
    for offset, key_piece, allowed, same_item in pieces:

        def grad_both(totals, key_piece=key_piece, allowed=allowed):
            outcome = piece_grads(query_heads, grad_heads, log_total, row_dots, key_piece, allowed)
            return (totals + outcome[0], outcome[1])

        def grad_none(totals):
            return (totals, zero_piece)

        query_grad, piece_grad = lax.cond(same_item, grad_both, grad_none, query_grad)
        if offset == 0:
            packed_grad = packed_grad + piece_grad
        else:
            packed_grad = packed_grad + from_behind(
                as_sent(piece_grad), ROWS, -offset
            ).astype(jnp.float32)
    packed_low = packed_grad.astype(jnp.bfloat16)
    return (
        attended_flat.astype(jnp.bfloat16),
        query_grad.astype(jnp.bfloat16),
        packed_low[:pixels],
        packed_low[pixels:],
    )


def taps_of(rows, reverse):
    padded = rows.reshape(-1, W, rows.shape[1])
    row_list = [padded[:-2], padded[1:-1], padded[2:]]
    if reverse:
        row_list = row_list[::-1]
    zero_column = jnp.zeros_like(row_list[0][:, :1])
    views = []
    for row_view in row_list:
        left_view = jnp.concatenate([zero_column, row_view[:, :-1]], axis=1)
        right_view = jnp.concatenate([row_view[:, 1:], zero_column], axis=1)
        view_list = [left_view, row_view, right_view]
        if reverse:
            view_list = view_list[::-1]
        views = views + view_list
    return [view.reshape(-1, rows.shape[1]) for view in views]


class Vectors(typing.NamedTuple):
    mean_one: jax.Array
    scale_one: jax.Array
    gain_one: jax.Array
    bias_one: jax.Array
    mean_two: jax.Array
    scale_two: jax.Array
    gain_two: jax.Array
    bias_two: jax.Array
    mean_three: jax.Array
    scale_three: jax.Array
    gain_three: jax.Array
    bias_three: jax.Array
    stretch: jax.Array
    shift: jax.Array
    proj_bias: jax.Array
    keep_above: jax.Array
    keep_below: jax.Array
    per_item: jax.Array


def grouped(names, refs):
    found, position = types.SimpleNamespace(), 0
    for name, count in names:
        if count is None:
            setattr(found, name, refs[position])
            position += 1
        else:
            setattr(found, name, refs[position : position + count])
            position += count
    return found


def call_named(kernel, ident, scalars, inputs, anywhere, outs, scratch, semaphores):
    names = [(name, None) for name in [*scalars, *inputs, *anywhere, *outs]]
    buffers = []
    for name, entry in scratch.items():
        many = isinstance(entry, list)
        names.append((name, len(entry) if many else None))
        buffers += [pltpu.VMEM(*e) for e in (entry if many else [entry])]
    names += [(name, None) for name in semaphores]
    vmem = pl.BlockSpec(memory_space=pltpu.VMEM)
    outcome = pl.pallas_call(
        functools.partial(kernel, names),
        out_shape=tuple(jax.ShapeDtypeStruct(*o) for o in outs.values()),
        in_specs=[pl.BlockSpec(memory_space=pltpu.SMEM)] * len(scalars)
        + [vmem] * len(inputs)
        + [pl.BlockSpec(memory_space=pl.ANY)] * len(anywhere),
        out_specs=(vmem,) * len(outs),
        scratch_shapes=buffers + [pltpu.SemaphoreType.DMA(s) for s in semaphores.values()],
        compiler_params=pltpu.CompilerParams(
            collective_id=ident, has_side_effects=True, vmem_limit_bytes=60 << 20
        ),
        name=kernel.__name__,
    )(*[v for group in (scalars, inputs, anywhere) for v in dict(group).values()])
    return types.SimpleNamespace(**dict(zip(outs, outcome)))


VECTOR_ROWS = 24
FAR, NEAR, SIDE, CORE, GROUP = range(5)
CROSS = (FAR, NEAR, SIDE)
SIDE_FIRST = (SIDE, GROUP, NEAR, FAR)
GROUP_FIRST = (GROUP, NEAR, SIDE, FAR)
NEAR_FIRST = (NEAR, SIDE, GROUP, FAR)
STREAMS = (
    (48, C // 2, SIDE_FIRST),
    (48, C // 2, GROUP_FIRST),
    (48, C // 2, NEAR_FIRST),
    (48, C // 2, SIDE_FIRST),
    (48, C // 2, GROUP_FIRST),
    (48, C // 2, NEAR_FIRST),
    (32, C, SIDE_FIRST),
    (32, C, NEAR_FIRST),
    (16, 3 * C // 2, GROUP_FIRST),
    (16, C // 2, GROUP_FIRST),
)
FIRST_CONV, SECOND_CONV, WORDS, QKV, PROJ = 0, 3, 6, 8, 9
LANDINGS = 4
IMAGE_ROWS = 8


class Band:
    def __init__(self, r):
        self.r = r
        self.row = lax.axis_index(ROWS)
        self.group = lax.axis_index(ITEMS)
        self.lane = self.row % SPAN
        self.base = self.row - self.lane
        row = self.row
        self.place = [row // 8, (row // 4) % 2, (row // 2) % 2, row % 2, self.group]
        self.partner = [
            {ROWS: row + (1 - 2 * self.place[d]) * (8 >> d)} for d in range(CORE + 1)
        ]
        self.partner.append({ITEMS: 1 - self.group})
        self.others = [(self.lane + o) % SPAN for o in range(1, SPAN)]
        self.peers = [{ROWS: self.base + other} for other in self.others]
        self.has_above, self.has_below = self.lane > 0, self.lane < SPAN - 1

    def meet(self, further=()):
        barrier = pltpu.get_barrier_semaphore()
        targets = self.peers + [self.partner[d] for d in further]
        for target in targets:
            pl.semaphore_signal(barrier, 1, device_id=target)
        pl.semaphore_wait(barrier, len(targets))

    def remote(self, source, target, send, recv, device):
        return pltpu.make_async_remote_copy(source, target, send, recv, device_id=device)

    def edges(self, k, top, bottom, target):
        r = self.r
        up = self.remote(
            top,
            target.at[IMAGE_ROWS + 1],
            r.edge_send.at[k, 0],
            r.edge_recv.at[k, 0],
            {ROWS: self.row - 1},
        )
        down = self.remote(
            bottom,
            target.at[0],
            r.edge_send.at[k, 1],
            r.edge_recv.at[k, 1],
            {ROWS: self.row + 1},
        )
        pl.when(self.has_above)(up.start)
        pl.when(self.has_below)(down.start)
        return up, down

    def wait_edges(self, pair):
        up, down = pair

        @pl.when(self.has_above)
        def _():
            up.wait_send()
            down.wait_recv()

        @pl.when(self.has_below)
        def _():
            down.wait_send()
            up.wait_recv()

    def zero_edges(self, target):
        @pl.when(jnp.logical_not(self.has_above))
        def _():
            target[0] = jnp.zeros(target.shape[1:], target.dtype)

        @pl.when(jnp.logical_not(self.has_below))
        def _():
            target[IMAGE_ROWS + 1] = jnp.zeros(target.shape[1:], target.dtype)

    def send_tile(self, k, source, target):
        r = self.r
        copies = []
        for o in range(1, SPAN):
            copies.append(
                self.remote(
                    source,
                    target.at[self.lane],
                    r.tile_send.at[k, o],
                    r.tile_recv.at[k, o],
                    self.peers[o - 1],
                )
            )
        for copy in copies:
            copy.start()
        target[self.lane] = source[...]
        return copies

    def swap(self, k, source, target, order=range(1, SPAN)):
        r = self.r
        copies = []
        for o in order:
            copies.append(
                self.remote(
                    source.at[self.others[o - 1]],
                    target.at[self.lane],
                    r.swap_send.at[k, o],
                    r.swap_recv.at[k, o],
                    self.peers[o - 1],
                )
            )
            copies[-1].start()
        return copies

    def fill_blocks(self):
        rows = lax.broadcasted_iota(jnp.int32, (C, C), 0) // (C // NORM_GROUPS)
        columns = lax.broadcasted_iota(jnp.int32, (C, C), 1) // (C // NORM_GROUPS)
        self.r.blocks[...] = jnp.where(rows == columns, 1.0, 0.0).astype(jnp.bfloat16)

    def item_means(self, window, masks, per_item):
        low, full = jnp.bfloat16, jnp.float32
        total = jnp.zeros((8, C), full)
        for b in range(SPAN):
            total = total + jnp.where(masks[b] > 0.0, window[b], 0.0)
        total = total * per_item
        coarse = total.astype(low)
        rest = total - coarse.astype(full)
        finer = rest.astype(low)
        finest = (rest - finer.astype(full)).astype(low)
        blocks = self.r.blocks[...]
        return dot(coarse, blocks) + dot(finer, blocks) + dot(finest, blocks)


def sums_tile(first, second):
    rows = lax.broadcasted_iota(jnp.int32, (8, C), 0)
    return jnp.where(rows == 0, first, jnp.where(rows == 1, second, 0.0))


def column_sum(values):
    return jnp.sum(values, axis=0, keepdims=True)


def side_shifts(values):
    rows = lax.broadcasted_iota(jnp.int32, (W, C), 0)
    from_left = jnp.where(rows == 0, 0.0, pltpu.roll(values, 1, 0))
    from_right = jnp.where(rows == W - 1, 0.0, pltpu.roll(values, W - 1, 0))
    return from_left, from_right


def kept(i, values, vec):
    keep = jnp.where(i == 0, vec.keep_above, jnp.where(i == IMAGE_ROWS + 1, vec.keep_below, 1.0))
    return jnp.where(keep > 0.0, values, 0.0)


def back_kernel(names, *refs):
    low, full = jnp.bfloat16, jnp.float32
    r = grouped(names, refs)
    band = Band(r)
    lane, group, place, partner = band.lane, band.group, band.place, band.partner
    core = place[CORE]
    remote = band.remote
    band.meet((FAR, GROUP))

    swaps = band.swap(0, r.pieces, r.heads) + band.swap(1, r.words, r.head_words)

    loads = types.SimpleNamespace()

    def load(k, source, target):
        copy = pltpu.make_async_copy(source, target, r.load_sem.at[k])
        copy.start()
        return copy

    loads.own = load(0, r.pieces.at[lane], r.heads.at[lane])
    loads.own_words = load(1, r.words.at[lane], r.head_words.at[lane])
    loads.middle = load(2, r.middle, r.mid)
    loads.qkv_weight = load(3, r.qkv_weight, r.qkv_w)
    loads.proj_weight = load(4, r.proj_weight, r.proj_w)
    loads.upstream = load(5, r.upstream, r.up)
    loads.act_three = load(6, r.act_three, r.act3)
    loads.caption = load(7, r.caption, r.cap)
    loads.conv_second = load(8, r.conv_second, r.conv_w)
    loads.hidden = load(9, r.hidden, r.hid)
    loads.act_two = load(10, r.act_two, r.act2)
    loads.act_one = load(11, r.act_one, r.act1)
    loads.image = load(12, r.image, r.img)
    loads.text_weight = load(13, r.text_weight, r.text_w)

    sibling = types.SimpleNamespace()

    def to_sibling(k, source, target):
        copy = remote(source, target, r.sib_send.at[k], r.sib_recv.at[k], partner[CORE])
        copy.start()
        return copy

    half = pl.ds(pl.multiple_of((1 - core) * (C // 2), C // 2), C // 2)
    sibling.upstream = to_sibling(0, r.upstream.at[:, half], r.sib_up)
    sibling.act3 = to_sibling(1, r.act_three, r.sib_act3)
    sibling.cap = to_sibling(2, r.caption, r.sib_cap)
    sibling.act2 = to_sibling(3, r.act_two, r.sib_act2)
    sibling.act1 = to_sibling(4, r.act_one, r.sib_act1)

    share_copy = remote(
        r.silu_share, r.other_share, r.small_send.at[2], r.small_recv.at[2], partner[GROUP]
    )
    share_copy.start()
    for target in (r.part_two, r.part_one):
        band.zero_edges(target)

    vec = Vectors(*[r.vectors[i : i + 1, :] for i in range(len(Vectors._fields))])
    norm_one = (vec.mean_one, vec.scale_one)
    norm_two = (vec.mean_two, vec.scale_two)
    norm_three = (vec.mean_three, vec.scale_three)

    masks = [r.vectors[VECTOR_ROWS + b : VECTOR_ROWS + b + 1, :] for b in range(SPAN)]
    band.fill_blocks()

    def item_means(window):
        return band.item_means(window, masks, vec.per_item)

    class Stream:
        def __init__(self, k):
            self.k = k
            self.order = STREAMS[k][2]
            self.dims = [FAR, NEAR, SIDE, CORE, GROUP]
            self.step = 0
            self.copy = None

        def at(self, ref, d, index):
            return ref.at[(slice(None),) * self.dims.index(d) + (index,)]

        def start(self):
            self.launch(r.grads[self.k])

        def launch(self, ref):
            k, step = self.k, self.step
            if step < LANDINGS:
                d = self.order[step]
                self.copy = remote(
                    self.at(ref, d, 1 - place[d]),
                    r.landings[k * LANDINGS + step],
                    r.fold_send.at[k, step],
                    r.fold_recv.at[k, step],
                    partner[d],
                )
                self.mine = self.at(ref, d, place[d])
                self.dims.remove(d)
            elif step == LANDINGS:
                fin = r.folded[self.k]
                self.copy = remote(
                    ref.at[1 - core],
                    fin.at[core],
                    r.fold_send.at[k, step],
                    r.fold_recv.at[k, step],
                    partner[CORE],
                )
                self.mine = ref.at[core]
            else:
                self.copy = remote(
                    r.folded[self.k],
                    r.whole[self.k],
                    r.fold_send.at[k, step],
                    r.fold_recv.at[k, step],
                    partner[GROUP],
                )
            self.copy.start()

        def advance(self):
            self.copy.wait()
            if self.step < LANDINGS:
                landed, mine = r.landings[self.k * LANDINGS + self.step], self.mine
                lead = landed.shape[:-2]
                pieces = 1
                for n in lead:
                    pieces *= n

                def add(i, carry):
                    index = []
                    for n in reversed(lead):
                        index.insert(0, i % n)
                        i = i // n
                    index = tuple(index)
                    total = landed[index].astype(full) + mine[index].astype(full)
                    landed[index] = total.astype(low)
                    return carry

                lax.fori_loop(0, pieces, add, 0)
                self.step += 1
                self.launch(landed)
            elif self.step == LANDINGS:
                r.folded[self.k][core] = self.mine[...]
                self.step += 1
                self.launch(None)
            else:
                self.step += 1

    streams = [Stream(k) for k in range(len(STREAMS))]

    loads.own.wait()
    loads.own_words.wait()
    for copy in swaps:
        copy.wait()
    for h in range(0, HEADS, 2):
        for k in range(4):
            pair = [r.heads[h + i, :, k * HEAD : (k + 1) * HEAD] for i in range(2)]
            r.joined[:, k * C + h * HEAD : k * C + (h + 2) * HEAD] = jnp.concatenate(pair, axis=1)
        for k in range(2):
            pair = [r.head_words[h + i, :, k * HEAD : (k + 1) * HEAD] for i in range(2)]
            r.joined_words[:, k * C + h * HEAD : k * C + (h + 2) * HEAD] = jnp.concatenate(
                pair, axis=1
            )
    sibling.attended = to_sibling(5, r.joined.at[:, 0:C], r.sib_attended)
    three_half = C + (1 - core) * (3 * C // 2)
    sibling.qkv = to_sibling(
        6,
        r.joined.at[:, pl.ds(pl.multiple_of(three_half, C // 2), 3 * C // 2)],
        r.sib_qkv,
    )
    sibling.words = to_sibling(
        7,
        r.joined_words.at[:, pl.ds(pl.multiple_of((1 - core) * C, C), C)],
        r.sib_words,
    )
    for copy in (loads.middle, loads.qkv_weight, loads.proj_weight, loads.upstream):
        copy.wait()

    def pixel_block(ref, i, count=4):
        return ref[1 + i * count : 1 + (i + 1) * count].reshape(count * W, C)

    def unit(values, norm):
        return (values - norm[0]) * norm[1]

    plain = jnp.zeros((1, C), full)
    crossed = jnp.zeros((1, C), full)
    up_sum = jnp.zeros((1, C), full)
    for i in range(2):
        block = slice(i * 4 * W, (i + 1) * 4 * W)
        middle = pixel_block(r.mid, i)
        upstream = r.up[block, :].astype(full)
        result = middle + dot(r.joined[block, 0:C], r.proj_w[...]) + vec.proj_bias
        r.result[block, :] = result.astype(low)
        grad = dot_last(r.joined[block, C:], r.qkv_w[...])
        plain = plain + column_sum(grad)
        crossed = crossed + column_sum(grad * unit(middle, norm_three))
        up_sum = up_sum + column_sum(upstream)
        part = upstream + grad * (vec.gain_three * vec.scale_three)
        r.part_two[1 + i * 4 : 5 + i * 4] = part.reshape(4, W, C)
    gain_three, bias_three = crossed, plain
    r.tile[0] = sums_tile(plain * vec.gain_three, crossed * vec.gain_three)
    three_edges = band.edges(0, r.part_two.at[1], r.part_two.at[IMAGE_ROWS], r.part_two)
    tiles = band.send_tile(0, r.tile.at[0], r.window.at[0])

    def mine_of(ref, start, size):
        return ref[:, pl.ds(pl.multiple_of(start, size if size % 256 else 256), size)]

    for copy in (sibling.upstream, sibling.act3, sibling.cap, sibling.attended, sibling.qkv, sibling.words):
        copy.wait()
    for copy in (loads.act_three, loads.caption):
        copy.wait()
    grad = dot_first(r.joined[:, 0:C], mine_of(r.up, core * (C // 2), C // 2))
    grad = grad + dot_first(r.sib_attended[...], r.sib_up[...])
    r.grads[PROJ][...] = grad.astype(low).reshape(r.grads[PROJ].shape)
    streams[PROJ].start()
    for n in range(3):
        own = mine_of(r.joined, C + core * (3 * C // 2) + n * (C // 2), C // 2)
        columns = slice(n * (C // 2), (n + 1) * (C // 2))
        grad = dot_first(r.act3[...], own)
        grad = grad + dot_first(r.sib_act3[...], r.sib_qkv[:, columns])
        r.grads[QKV][:, :, :, :, :, :, columns] = grad.astype(low).reshape(2, 2, 2, 2, 2, 16, C // 2)
    streams[QKV].start()

    def text_rows(s, carry):
        columns = pl.ds(pl.multiple_of(s * 128, 128), 128)
        own = mine_of(r.joined_words, core * C, C)
        grad = dot_first(r.cap[:, columns], own)
        grad = grad + dot_first(r.sib_cap[:, columns], r.sib_words[...])
        grad = grad.astype(low)
        index = (s // 8, (s // 4) % 2, (s // 2) % 2, s % 2)
        r.grads[WORDS][index] = grad[0:64].reshape(2, 32, C)
        r.grads[WORDS + 1][index] = grad[64:128].reshape(2, 32, C)
        return carry

    lax.fori_loop(0, 2 ** len(CROSS) * 2, text_rows, 0)
    streams[WORDS].start()
    streams[WORDS + 1].start()
    query_sum = column_sum(r.joined[:, C : 2 * C].astype(full))
    value_sum = column_sum(r.joined[:, 3 * C :].astype(full))
    word_sum = [column_sum(r.joined_words[:, k * C : (k + 1) * C].astype(full)) for k in range(2)]

    def spread_rows(i, values):
        from_left, from_right = side_shifts(values)
        r.shifts[0, i] = from_right.astype(low)
        r.shifts[1, i] = values.astype(low)
        r.shifts[2, i] = from_left.astype(low)

    def conv_back():
        total = jnp.zeros((IMAGE_ROWS * W, C), full)
        for t in range(9):
            dy, dx = t // 3, t % 3
            view = r.shifts[dx, 2 - dy : 2 - dy + IMAGE_ROWS].reshape(IMAGE_ROWS * W, C)
            total = total + dot_last(view, r.conv_w[t * C : (t + 1) * C, :])
        return total

    def conv_grads(kind, own, other, landing):
        for t in range(9):
            dy, dx = t // 3, t % 3
            shifted = r.shifts[
                dx, 1 : IMAGE_ROWS + 1, :, pl.ds(pl.multiple_of(core * (C // 2), C // 2), C // 2)
            ].reshape(IMAGE_ROWS * W, C // 2)
            grad = dot_first(own[dy * W : dy * W + IMAGE_ROWS * W, :], shifted)
            grad = grad + dot_first(
                other[dy * W : dy * W + IMAGE_ROWS * W, :],
                landing[dx].reshape(IMAGE_ROWS * W, C // 2),
            )
            grad = grad.astype(low)
            begin = t * C
            while begin < (t + 1) * C:
                shard, within = divmod(begin, 288)
                stream, offset = divmod(within, 96)
                part, offset = divmod(offset, 48)
                size = min(48 - offset, (t + 1) * C - begin)
                target = r.grads[kind + stream]
                target[
                    shard // 8, (shard // 4) % 2, (shard // 2) % 2, shard % 2, part, offset : offset + size
                ] = grad[begin - t * C : begin - t * C + size]
                begin += size
        for j in range(3):
            streams[kind + j].start()

    for copy in tiles:
        copy.wait()
    band.wait_edges(three_edges)
    means = item_means(r.window.at[0])
    offset_three, slope_three = means[0:1] * vec.scale_three, means[1:2] * vec.scale_three

    def middle_row(i, bias):
        values = r.part_two[i] - offset_three - unit(r.mid[i], norm_three) * slope_three
        r.part_two[i] = values
        values = kept(i, values, vec)
        spread_rows(i, values)
        inside = jnp.where((i > 0) & (i <= IMAGE_ROWS), 1.0, 0.0)
        return bias + inside * column_sum(values.astype(low).astype(full))

    conv_bias_two = lax.fori_loop(0, IMAGE_ROWS + 2, middle_row, jnp.zeros((1, C), full))
    shift_half = r.shifts.at[:, 1 : IMAGE_ROWS + 1, :, half]
    sibling.shifts_two = to_sibling(8, shift_half, r.sib_shifts_two)
    loads.conv_second.wait()
    loads.hidden.wait()
    r.product[...] = conv_back().reshape(IMAGE_ROWS, W, C)
    loads.conv_first = load(8, r.conv_first, r.conv_w)
    stretched = vec.stretch * vec.gain_two * vec.scale_two

    def second_row(i, sums):
        unit_two = unit(r.hid[i + 1], norm_two)
        normed = unit_two * vec.gain_two + vec.bias_two
        grad = r.product[i] * silu_slope_of(normed * vec.stretch + vec.shift)
        r.part_one[i + 1] = grad * stretched
        return sums[0] + column_sum(grad), sums[1] + column_sum(grad * unit_two)

    nothing = (jnp.zeros((1, C), full), jnp.zeros((1, C), full))
    plain, crossed = lax.fori_loop(0, IMAGE_ROWS, second_row, nothing)
    scale_grad = crossed * vec.gain_two + plain * vec.bias_two
    shift_grad = plain
    gain_two, bias_two = crossed * vec.stretch, plain * vec.stretch
    r.tile[1] = sums_tile(bias_two * vec.gain_two, gain_two * vec.gain_two)
    two_edges = band.edges(1, r.part_one.at[1], r.part_one.at[IMAGE_ROWS], r.part_one)
    tiles = band.send_tile(1, r.tile.at[1], r.window.at[1])
    loads.act_two.wait()
    sibling.act2.wait()
    sibling.shifts_two.wait()
    conv_grads(SECOND_CONV, r.act2, r.sib_act2, r.sib_shifts_two)
    for copy in tiles:
        copy.wait()
    band.wait_edges(two_edges)
    means = item_means(r.window.at[1])
    offset_two, slope_two = means[0:1] * vec.scale_two, means[1:2] * vec.scale_two

    def hidden_row(i, bias):
        values = r.part_one[i] - offset_two - unit(r.hid[i], norm_two) * slope_two
        values = kept(i, values, vec)
        spread_rows(i, values)
        inside = jnp.where((i > 0) & (i <= IMAGE_ROWS), 1.0, 0.0)
        return bias + inside * column_sum(values.astype(low).astype(full))

    conv_bias_one = lax.fori_loop(0, IMAGE_ROWS + 2, hidden_row, jnp.zeros((1, C), full))
    sibling.shifts_one = to_sibling(9, shift_half, r.sib_shifts_one)
    for k in (PROJ, QKV, WORDS, WORDS + 1):
        streams[k].advance()
    loads.conv_first.wait()
    loads.image.wait()
    r.product[...] = conv_back().reshape(IMAGE_ROWS, W, C)

    def first_row(i, sums):
        unit_one = unit(r.img[i].astype(full), norm_one)
        normed = unit_one * vec.gain_one + vec.bias_one
        grad = r.product[i] * silu_slope_of(normed)
        r.product[i] = grad
        return sums[0] + column_sum(grad), sums[1] + column_sum(grad * unit_one)

    plain, crossed = lax.fori_loop(0, IMAGE_ROWS, first_row, nothing)
    gain_one, bias_one = crossed, plain
    r.tile[2] = sums_tile(plain * vec.gain_one, crossed * vec.gain_one)
    tiles = band.send_tile(2, r.tile.at[2], r.window.at[2])
    rows = [
        gain_one,
        gain_two,
        gain_three,
        bias_one,
        bias_two,
        bias_three,
        conv_bias_one,
        conv_bias_two,
        query_sum,
        value_sum,
        word_sum[0],
        word_sum[1],
        up_sum,
        jnp.zeros((1, C), full),
        scale_grad,
        shift_grad,
    ]
    for i, values in enumerate(rows):
        r.own_rows[i : i + 1, :] = values
    row_copies = band.send_tile(3, r.own_rows, r.band_rows)
    loads.act_one.wait()
    sibling.act1.wait()
    sibling.shifts_one.wait()
    conv_grads(FIRST_CONV, r.act1, r.sib_act1, r.sib_shifts_one)
    for copy in tiles:
        copy.wait()
    means = item_means(r.window.at[2])
    offset_one, slope_one = means[0:1] * vec.scale_one, means[1:2] * vec.scale_one
    ratio = vec.gain_one * vec.scale_one

    def image_row(i, carry):
        unit_one = unit(r.img[i].astype(full), norm_one)
        values = r.part_two[i + 1] + r.product[i] * ratio - offset_one - unit_one * slope_one
        r.image_grad[i] = values
        return carry

    lax.fori_loop(0, IMAGE_ROWS, image_row, 0)

    for copy in row_copies:
        copy.wait()
    total = jnp.zeros((16, C), full)
    for b in range(SPAN):
        total = total + r.band_rows[b]
    r.half_rows[0:16, :] = total
    for b in range(SPAN):
        r.half_rows[16 + 2 * b : 18 + 2 * b, :] = r.band_rows[b, 14:16, :]
    far_copy = remote(
        r.half_rows, r.far_rows, r.small_send.at[0], r.small_recv.at[0], partner[FAR]
    )
    far_copy.start()
    for k in range(SECOND_CONV, len(STREAMS)):
        streams[k].advance()
    loads.text_weight.wait()

    def caption_columns(n, carry):
        columns = pl.ds(pl.multiple_of(n * C, C), C)
        r.caption_grad[:, columns] = dot_last(r.joined_words[...], r.text_w[columns, :])
        return carry

    lax.fori_loop(0, EMB // C, caption_columns, 0)
    loads.embed_weight = load(13, r.embed_weight, r.text_w)
    far_copy.wait()
    first_half = jnp.where(place[FAR] == 0, r.half_rows[16:32, :], r.far_rows[16:32, :])
    other_half = jnp.where(place[FAR] == 0, r.far_rows[16:32, :], r.half_rows[16:32, :])
    r.group_rows[0:16, :] = r.half_rows[0:16, :] + r.far_rows[0:16, :]
    r.group_rows[16:32, :] = first_half
    r.group_rows[32:48, :] = other_half
    slots = r.slot_of_band.shape[0]
    for k in range(2):
        table = jnp.zeros((slots, C), full)
        for b in range(2 * SPAN):
            values = r.group_rows[16 + 2 * b + k : 17 + 2 * b + k, :]
            table = table + jnp.where(r.slot_of_band[:, b * 128 : b * 128 + 1] > 0.0, values, 0.0)
        r.own_table[slots * k : slots * (k + 1), :] = table
    r.own_table[2 * slots :, :] = r.group_rows[0:16, :]
    group_copy = remote(
        r.own_table,
        r.other_table,
        r.small_send.at[1],
        r.small_recv.at[1],
        partner[GROUP],
    )
    group_copy.start()
    def advance_all():
        for stream in streams:
            if stream.step < LANDINGS + 2:
                stream.advance()

    advance_all()
    loads.embed_weight.wait()
    table = [r.own_table[slots * k : slots * (k + 1), :].astype(low) for k in range(2)]

    def embedding_columns(n, carry):
        columns = pl.ds(pl.multiple_of(n * C, C), C)
        grad = dot_last(table[0], r.text_w[columns, 0:C]) + dot_last(table[1], r.text_w[columns, C:])
        source = r.embedding[:, columns].astype(full)
        r.embedding_grad[:, columns] = grad * silu_slope_of(source)
        return carry

    lax.fori_loop(0, EMB // C, embedding_columns, 0)
    advance_all()
    group_copy.wait()
    share_copy.wait()
    for k in range(2):
        columns = slice(k * C, (k + 1) * C)
        other = r.other_table[slots * k : slots * (k + 1), :].astype(low)
        r.embed_weight_grad[:, columns] = dot_first(r.silu_share[...], table[k]) + dot_first(
            r.other_share[...], other
        )
        r.embed_bias_grad[:, columns] = column_sum(table[k].astype(full)) + column_sum(
            other.astype(full)
        )
    sums = r.own_table[2 * slots :, :] + r.other_table[2 * slots :, :]
    r.norm_gains_grad[...] = sums[0:3]
    r.norm_biases_grad[...] = sums[3:6]
    r.conv_biases_grad[...] = sums[6:8]
    for target, k in ((r.qv_bias_grad, 8), (r.text_bias_grad, 10)):
        target[:, 0:C] = sums[k : k + 1]
        target[:, C:] = sums[k + 1 : k + 2]
    r.proj_bias_grad[...] = sums[12:13]
    for _ in range(LANDINGS):
        advance_all()

    def write(stream, target, first_row):
        rows, columns = STREAMS[stream][:2]
        for side, source in ((group, r.folded[stream]), (1 - group, r.whole[stream])):
            for k in range(2):
                target[
                    pl.ds(pl.multiple_of(first_row + side * rows, rows), rows),
                    k * columns : (k + 1) * columns,
                ] = source[k].astype(full)

    for j in range(3):
        write(FIRST_CONV + j, r.conv_first_grad, j * 96)
        write(SECOND_CONV + j, r.conv_second_grad, j * 96)
    for j in range(2):
        write(WORDS + j, r.text_grad, j * 64)
    write(QKV, r.qkv_grad, 0)
    write(PROJ, r.proj_grad, 0)


def silu_slope_of(source):
    sigma = 1.0 / (1.0 + jnp.exp(-source))
    return sigma * (1.0 + source * (1.0 - sigma))


def back(ident, vectors, slot_of_band, silu_share, embedding, anywhere):
    low, full = jnp.bfloat16, jnp.float32
    pixels = IMAGE_ROWS * W
    slots = slot_of_band.shape[0]
    outs = dict(
        result=((pixels, C), low),
        image_grad=((IMAGE_ROWS, W, C), full),
        caption_grad=((TEXT, EMB), full),
        conv_first_grad=((288, C), full),
        conv_second_grad=((288, C), full),
        qkv_grad=((32, 3 * C), full),
        text_grad=((128, 2 * C), full),
        proj_grad=((32, C), full),
        embedding_grad=(embedding.shape, full),
        embed_weight_grad=((silu_share.shape[1], 2 * C), full),
        norm_gains_grad=((3, C), full),
        norm_biases_grad=((3, C), full),
        conv_biases_grad=((2, C), full),
        embed_bias_grad=((1, 2 * C), full),
        qv_bias_grad=((1, 2 * C), full),
        text_bias_grad=((1, 2 * C), full),
        proj_bias_grad=((1, C), full),
    )
    padded = (IMAGE_ROWS + 2, W, C)
    scratch = dict(
        heads=((HEADS, pixels, 4 * HEAD), low),
        head_words=((HEADS, TEXT, 2 * HEAD), low),
        joined=((pixels, 4 * C), low),
        joined_words=((TEXT, 2 * C), low),
        mid=(padded, full),
        part_two=(padded, full),
        part_one=(padded, full),
        hid=(padded, full),
        product=((IMAGE_ROWS, W, C), full),
        img=((IMAGE_ROWS, W, C), low),
        up=((pixels, C), low),
        act1=((pixels + 2 * W, C), low),
        act2=((pixels + 2 * W, C), low),
        act3=((pixels, C), low),
        cap=((TEXT, EMB), low),
        conv_w=((9 * C, C), low),
        qkv_w=((C, 3 * C), low),
        proj_w=((C, C), low),
        text_w=((EMB, 2 * C), low),
        sib_up=((pixels, C // 2), low),
        sib_act1=((pixels + 2 * W, C), low),
        sib_act2=((pixels + 2 * W, C), low),
        sib_act3=((pixels, C), low),
        sib_cap=((TEXT, EMB), low),
        sib_attended=((pixels, C), low),
        sib_qkv=((pixels, 3 * C // 2), low),
        sib_words=((TEXT, C), low),
        sib_shifts_one=((3, IMAGE_ROWS, W, C // 2), low),
        sib_shifts_two=((3, IMAGE_ROWS, W, C // 2), low),
        shifts=((3,) + padded, low),
        blocks=((C, C), low),
        tile=((3, 8, C), full),
        window=((3, SPAN, 8, C), full),
        own_rows=((16, C), full),
        band_rows=((SPAN, 16, C), full),
        half_rows=((32, C), full),
        far_rows=((32, C), full),
        group_rows=((48, C), full),
        own_table=((2 * slots + 16, C), full),
        other_table=((2 * slots + 16, C), full),
        other_share=(silu_share.shape, low),
    )
    scratch.update(grads=[((2,) * 5 + s[:2], low) for s in STREAMS])
    scratch.update(landings=[((2,) * (4 - i) + s[:2], low) for s in STREAMS for i in range(LANDINGS)])
    scratch.update(folded=[((2,) + s[:2], low) for s in STREAMS])
    scratch.update(whole=[((2,) + s[:2], low) for s in STREAMS])
    semaphores = dict(
        swap_send=(2, SPAN),
        swap_recv=(2, SPAN),
        load_sem=(14,),
        sib_send=(10,),
        sib_recv=(10,),
        edge_send=(2, 2),
        edge_recv=(2, 2),
        tile_send=(4, SPAN),
        tile_recv=(4, SPAN),
        fold_send=(len(STREAMS), LANDINGS + 2),
        fold_recv=(len(STREAMS), LANDINGS + 2),
        small_send=(3,),
        small_recv=(3,),
    )
    inputs = dict(
        vectors=vectors, slot_of_band=slot_of_band, silu_share=silu_share, embedding=embedding
    )
    return call_named(back_kernel, ident, (), inputs, anywhere, outs, scratch, semaphores)


def front_kernel(names, *refs):
    low, full = jnp.bfloat16, jnp.float32
    r = grouped(names, refs)
    band = Band(r)
    band.meet()
    loads = types.SimpleNamespace()

    def load(k, source, target):
        copy = pltpu.make_async_copy(source, target, r.load_sem.at[k])
        copy.start()
        return copy

    loads.image = load(0, r.image, r.img.at[1 : IMAGE_ROWS + 1])
    image_edges = band.edges(0, r.image.at[0], r.image.at[IMAGE_ROWS - 1], r.img)
    loads.conv_first = load(1, r.conv_first, r.first_w)
    loads.embed_weight = load(2, r.embed_weight, r.embed_w)
    loads.upstream = load(3, r.upstream, r.up)
    loads.proj_weight = load(4, r.proj_weight, r.proj_w)
    loads.conv_second = load(5, r.conv_second, r.second_w)
    loads.caption = load(6, r.caption, r.cap)
    loads.text_weight = load(7, r.text_weight, r.text_w)
    loads.qkv_weight = load(8, r.qkv_weight, r.qkv_w)

    mine = r.items[band.row]
    same = [(r.items[band.base + b] == mine).astype(full) for b in range(SPAN)]
    masks = [jnp.full((1, C), m, full) for m in same]
    bands = masks[0]
    for m in masks[1:]:
        bands = bands + m
    per_item = 1.0 / (bands * (IMAGE_ROWS * W * (C // NORM_GROUPS)))
    before = jnp.where(band.has_above, r.items[jnp.maximum(band.row - 1, 0)], -1)
    after = jnp.where(
        band.has_below, r.items[jnp.minimum(band.row + 1, r.items.shape[0] - 1)], -1
    )
    found = types.SimpleNamespace(
        gain_one=r.norm_gains[0:1, :],
        gain_two=r.norm_gains[1:2, :],
        gain_three=r.norm_gains[2:3, :],
        bias_one=r.norm_biases[0:1, :],
        bias_two=r.norm_biases[1:2, :],
        bias_three=r.norm_biases[2:3, :],
        proj_bias=r.proj_bias[...],
        keep_above=jnp.full((1, C), (before == mine).astype(full)),
        keep_below=jnp.full((1, C), (after == mine).astype(full)),
        per_item=per_item,
    )
    for target in (r.img, r.hidden, r.middle):
        band.zero_edges(target)
    nothing = (jnp.zeros((1, C), full), jnp.zeros((1, C), full))

    def norm_of(k):
        means = band.item_means(r.window.at[k], masks, per_item)
        return means[0:1], lax.rsqrt(means[1:2] - means[0:1] * means[0:1] + epsilon)

    loads.image.wait()

    def image_sums(i, sums):
        values = r.img[i + 1].astype(full)
        return sums[0] + column_sum(values), sums[1] + column_sum(values * values)

    r.tile[0] = sums_tile(*lax.fori_loop(0, IMAGE_ROWS, image_sums, nothing))
    tiles = band.send_tile(0, r.tile.at[0], r.window.at[0])

    band.fill_blocks()
    slot = lax.broadcasted_iota(jnp.int32, r.embedding.shape, 0)
    chosen = jnp.where(slot == mine, r.embedding[...].astype(full), 0.0)
    chosen = jnp.sum(chosen, axis=0, keepdims=True)
    chosen = chosen / (1.0 + jnp.exp(-chosen))
    chosen = jnp.broadcast_to(chosen, (16, EMB)).astype(low)
    loads.embed_weight.wait()
    modulation = dot(chosen, r.embed_w[...])[0:1] + r.embed_bias[...]
    found.stretch = 1.0 + modulation[:, 0:C]
    found.shift = modulation[:, C:]

    def spread_rows(i, values, target):
        values = kept(i, values, found)
        from_left, from_right = side_shifts(values)
        r.shifts[0, i] = from_left.astype(low)
        r.shifts[1, i] = values.astype(low)
        r.shifts[2, i] = from_right.astype(low)
        target[pl.ds(pl.multiple_of(i * W, W), W), :] = values.astype(low)

    def conv(weight):
        total = jnp.zeros((IMAGE_ROWS * W, C), full)
        for t in range(9):
            view = r.shifts[t % 3, t // 3 : t // 3 + IMAGE_ROWS].reshape(IMAGE_ROWS * W, C)
            total = total + dot(view, weight[t * C : (t + 1) * C, :])
        return total

    for copy in tiles:
        copy.wait()
    band.wait_edges(image_edges)
    found.mean_one, found.scale_one = norm_of(0)

    def first_row(i, carry):
        unit = (r.img[i].astype(full) - found.mean_one) * found.scale_one
        normed = unit * found.gain_one + found.bias_one
        spread_rows(i, normed / (1.0 + jnp.exp(-normed)), r.act_one)
        return carry

    lax.fori_loop(0, IMAGE_ROWS + 2, first_row, 0)
    loads.conv_first.wait()
    total = conv(r.first_w) + r.conv_biases[0:1, :]
    r.hidden[1 : IMAGE_ROWS + 1] = total.reshape(IMAGE_ROWS, W, C)
    hidden_edges = band.edges(1, r.hidden.at[1], r.hidden.at[IMAGE_ROWS], r.hidden)
    r.tile[1] = sums_tile(column_sum(total), column_sum(total * total))
    tiles = band.send_tile(1, r.tile.at[1], r.window.at[1])

    loads.caption.wait()
    loads.text_weight.wait()
    words = (dot(r.cap[...], r.text_w[...]) + r.text_bias[...]).astype(low)
    for h in range(HEADS):
        parts = [words[:, k * C + h * HEAD : k * C + (h + 1) * HEAD] for k in range(2)]
        r.words[h] = jnp.concatenate(parts, axis=1)
    swaps = band.swap(0, r.words, r.head_words)
    r.head_words[band.lane] = r.words[band.lane]
    for copy in tiles:
        copy.wait()
    band.wait_edges(hidden_edges)
    found.mean_two, found.scale_two = norm_of(1)

    def second_row(i, carry):
        unit = (r.hidden[i] - found.mean_two) * found.scale_two
        normed = unit * found.gain_two + found.bias_two
        shifted = normed * found.stretch + found.shift
        spread_rows(i, shifted / (1.0 + jnp.exp(-shifted)), r.act_two)
        return carry

    lax.fori_loop(0, IMAGE_ROWS + 2, second_row, 0)
    loads.conv_second.wait()
    total = conv(r.second_w) + r.conv_biases[1:2, :]
    total = total + r.img[1 : IMAGE_ROWS + 1].astype(full).reshape(IMAGE_ROWS * W, C)
    r.middle[1 : IMAGE_ROWS + 1] = total.reshape(IMAGE_ROWS, W, C)
    r.tile[2] = sums_tile(column_sum(total), column_sum(total * total))
    tiles = band.send_tile(2, r.tile.at[2], r.window.at[2])
    middle_edges = band.edges(2, r.middle.at[1], r.middle.at[IMAGE_ROWS], r.middle)

    loads.upstream.wait()
    loads.proj_weight.wait()
    attended_grad = dot_last(r.up[...], r.proj_w[...]).astype(low)
    loads.qkv_weight.wait()
    for h in range(HEADS):
        r.pieces[h, :, 3 * HEAD :] = attended_grad[:, h * HEAD : (h + 1) * HEAD]
    for copy in tiles:
        copy.wait()
    found.mean_three, found.scale_three = norm_of(2)
    for i in range(2):
        middle = r.middle[1 + 4 * i : 5 + 4 * i].reshape(4 * W, C)
        unit = (middle - found.mean_three) * found.scale_three
        block = slice(i * 4 * W, (i + 1) * 4 * W)
        act = (unit * found.gain_three + found.bias_three).astype(low)
        r.act_three[block, :] = act
        projected = dot(act, r.qkv_w[...])
        queries = (projected[:, 0:C] + r.qv_bias[:, 0:C]).astype(low)
        keys = projected[:, C : 2 * C].astype(low)
        values = (projected[:, 2 * C :] + r.qv_bias[:, C:]).astype(low)
        for h in range(HEADS):
            head = slice(h * HEAD, (h + 1) * HEAD)
            r.pieces[h, block, 0 : 2 * HEAD] = jnp.concatenate([queries[:, head], keys[:, head]], axis=1)
            r.pieces[h, block, 2 * HEAD : 3 * HEAD] = values[:, head]
    swaps = swaps + band.swap(1, r.pieces, r.heads)
    r.heads[band.lane] = r.pieces[band.lane]
    fields = [getattr(found, name) for name in Vectors._fields]
    for i, values in enumerate(fields):
        r.vectors[i : i + 1, :] = values
    r.vectors[len(fields) : VECTOR_ROWS, :] = jnp.zeros((VECTOR_ROWS - len(fields), C), full)
    for b in range(SPAN):
        r.vectors[VECTOR_ROWS + b : VECTOR_ROWS + b + 1, :] = masks[b]
    band.wait_edges(middle_edges)
    for copy in swaps:
        copy.wait()


def front(ident, items, inputs, anywhere):
    low, full = jnp.bfloat16, jnp.float32
    pixels = IMAGE_ROWS * W
    padded = (IMAGE_ROWS + 2, W, C)
    outs = dict(
        heads=((HEADS, pixels, 4 * HEAD), low),
        head_words=((HEADS, TEXT, 2 * HEAD), low),
        act_one=((pixels + 2 * W, C), low),
        act_two=((pixels + 2 * W, C), low),
        act_three=((pixels, C), low),
        hidden=(padded, full),
        middle=(padded, full),
        vectors=((VECTOR_ROWS + SPAN, C), full),
    )
    scratch = dict(
        img=(padded, low),
        up=((pixels, C), low),
        cap=((TEXT, EMB), low),
        first_w=((9 * C, C), low),
        second_w=((9 * C, C), low),
        embed_w=((EMB, 2 * C), low),
        text_w=((EMB, 2 * C), low),
        qkv_w=((C, 3 * C), low),
        proj_w=((C, C), low),
        shifts=((3,) + padded, low),
        blocks=((C, C), low),
        tile=((3, 8, C), full),
        window=((3, SPAN, 8, C), full),
        words=((HEADS, TEXT, 2 * HEAD), low),
        pieces=((HEADS, pixels, 4 * HEAD), low),
    )
    semaphores = dict(
        load_sem=(9,),
        edge_send=(3, 2),
        edge_recv=(3, 2),
        tile_send=(3, SPAN),
        tile_recv=(3, SPAN),
        swap_send=(2, SPAN),
        swap_recv=(2, SPAN),
    )
    return call_named(
        front_kernel, ident, dict(items=items), inputs, anywhere, outs, scratch, semaphores
    )


def hand_over_kernel(count, *refs):
    sources, targets, sem = refs[:count], refs[count : 2 * count], refs[2 * count]
    copies = [
        pltpu.make_async_copy(source, target, sem.at[k])
        for k, (source, target) in enumerate(zip(sources, targets))
    ]
    for copy in copies:
        copy.start()
    for copy in copies:
        copy.wait()


def hand_over(arrays):
    anywhere = pl.BlockSpec(memory_space=pl.ANY)
    return pl.pallas_call(
        functools.partial(hand_over_kernel, len(arrays)),
        out_shape=tuple(jax.ShapeDtypeStruct(a.shape, a.dtype) for a in arrays),
        in_specs=[pl.BlockSpec(memory_space=pltpu.VMEM)] * len(arrays),
        out_specs=(anywhere,) * len(arrays),
        scratch_shapes=[pltpu.SemaphoreType.DMA((len(arrays),))],
        name=hand_over.__name__,
    )(*arrays)


def blocks_of(rows):
    return rows.reshape(rows.shape[0], NORM_GROUPS, -1)


def spread(values):
    return jnp.repeat(values, C // NORM_GROUPS)


def in_halves(
    image,
    embedding,
    caption,
    item_of_band,
    out_grad,
    norm_gains,
    norm_biases,
    conv_first,
    conv_second,
    conv_biases,
    embed_weight,
    embed_bias,
    qkv_weight,
    qv_bias,
    text_weight,
    text_bias,
    proj_weight,
    proj_bias,
):
    low = jnp.bfloat16
    pixels = image.shape[1]
    position = lax.axis_index(ROWS)
    items = item_of_band[0]
    slots = items.shape[0]
    by_row = (-1, W, C)
    ahead = front(
        0,
        items,
        dict(
            embedding=embedding[0],
            norm_gains=norm_gains,
            norm_biases=norm_biases,
            conv_biases=conv_biases,
            embed_bias=embed_bias[None],
            qv_bias=qv_bias[None],
            text_bias=text_bias[None],
            proj_bias=proj_bias[None],
        ),
        dict(
            image=image.reshape(by_row),
            conv_first=conv_first,
            embed_weight=embed_weight,
            upstream=out_grad[0],
            proj_weight=proj_weight,
            conv_second=conv_second,
            caption=caption[0, 0],
            text_weight=text_weight,
            qkv_weight=qkv_weight,
        ),
    )
    pieces, words = one_head(items, ahead.heads, ahead.head_words)
    slot_of_band = (jnp.arange(slots)[:, None] == items[None, :]).astype(jnp.float32)
    row_share = EMB // lax.axis_size(ROWS)
    share = lax.dynamic_slice_in_dim(embedding[0], position * row_share, row_share, 1)
    silu_share = jax.nn.silu(share.astype(jnp.float32)).astype(low)
    out = back(
        1,
        ahead.vectors,
        jnp.repeat(slot_of_band, 128, axis=1),
        silu_share,
        embedding[0],
        dict(
            pieces=pieces,
            words=words,
            middle=ahead.middle,
            qkv_weight=qkv_weight,
            proj_weight=proj_weight,
            upstream=out_grad[0],
            act_three=ahead.act_three,
            caption=caption[0, 0],
            conv_second=conv_second,
            conv_first=conv_first,
            hidden=ahead.hidden,
            act_two=ahead.act_two,
            act_one=ahead.act_one,
            image=image.reshape(by_row),
            text_weight=text_weight,
            embed_weight=embed_weight,
        ),
    )
    out = types.SimpleNamespace(**dict(zip(vars(out), hand_over(list(vars(out).values())))))
    return (
        out.result[None],
        out.image_grad.reshape(1, pixels, C),
        out.embedding_grad[None],
        out.caption_grad[None, None],
        out.norm_gains_grad,
        out.norm_biases_grad,
        out.conv_first_grad,
        out.conv_second_grad,
        out.conv_biases_grad,
        out.embed_weight_grad,
        out.embed_bias_grad.reshape(-1),
        out.qkv_grad,
        out.qv_bias_grad.reshape(-1),
        out.text_grad,
        out.text_bias_grad.reshape(-1),
        out.proj_grad,
        out.proj_bias_grad.reshape(-1),
    )


def shards(
    image,
    embedding,
    caption,
    item_of_band,
    out_grad,
    norm_gains,
    norm_biases,
    conv_first,
    conv_second,
    conv_biases,
    embed_weight,
    embed_bias,
    qkv_weight,
    qv_bias,
    text_weight,
    text_bias,
    proj_weight,
    proj_bias,
):
    low = jnp.bfloat16
    full = jnp.float32
    pixels = image.shape[1]
    band_items = item_of_band[0]
    slots = band_items.shape[0]
    if slots == 2 * SPAN and lax.axis_size(ITEMS) == 2 and HEADS == SPAN:
        return in_halves(
            image,
            embedding,
            caption,
            item_of_band,
            out_grad,
            norm_gains,
            norm_biases,
            conv_first,
            conv_second,
            conv_biases,
            embed_weight,
            embed_bias,
            qkv_weight,
            qv_bias,
            text_weight,
            text_bias,
            proj_weight,
            proj_bias,
        )
    position = lax.axis_index(ROWS)
    my_item = band_items[position]
    slot_hot = (jnp.arange(slots) == my_item).astype(full)
    item_count = jnp.sum((band_items == my_item).astype(full)) * pixels * (C // NORM_GROUPS)
    reach = position + jnp.arange(-REACH, REACH + 1)
    near = (reach >= 0) & (reach < slots)
    near = near & (band_items[jnp.clip(reach, 0, slots - 1)] == my_item)
    keep = jnp.concatenate(
        [
            jnp.full((W, 1), near[REACH - 1]),
            jnp.full((pixels, 1), True),
            jnp.full((W, 1), near[REACH + 1]),
        ]
    )
    own_lead = jnp.logical_not(near[REACH - 1])

    def totals(ident, first, second, edges=None):
        sums = jnp.stack([jnp.sum(blocks_of(first), axis=(0, 2)), jnp.sum(blocks_of(second), axis=(0, 2))])
        tile = jnp.pad(sums, ((0, 6), (0, 128 - NORM_GROUPS)))
        if edges is not None:
            outcome = exchange(ident, slots, tile, (edges[:W], edges[-W:]))
        else:
            outcome = exchange(ident, slots, tile)
        summed = jnp.sum(jnp.where(near[:, None, None], outcome[0], 0.0), axis=0)
        summed = summed[:2, :NORM_GROUPS] / item_count
        return summed, outcome[1:]

    def stats(summed):
        scales = lax.rsqrt(summed[1] - summed[0] * summed[0] + epsilon)
        return spread(summed[0]), spread(scales)

    inputs = image[0].astype(full)
    summed, (above, below) = totals(0, inputs, inputs * inputs, image[0])
    means_one, scales_one = stats(summed)
    padded = jnp.concatenate([above, image[0], below]).astype(full)
    unit_padded = (padded - means_one) * scales_one
    normed_padded = unit_padded * norm_gains[0] + norm_biases[0]
    act_one_padded = jnp.where(keep, jax.nn.silu(normed_padded), 0.0).astype(low)
    unit_one = unit_padded[W:-W]
    normed_one = normed_padded[W:-W]
    taps_one = jnp.concatenate(taps_of(act_one_padded, False), axis=1)
    hidden_one = dot(taps_one, conv_first) + conv_biases[0]
    embed_silu = jax.nn.silu(embedding[0].astype(full)).astype(low)
    my_silu = dot(slot_hot.astype(low)[None], embed_silu).astype(low)
    modulation = dot(my_silu, embed_weight)[0] + embed_bias
    scale_part = modulation[:C]
    shift_part = modulation[C:]
    summed, (above, below) = totals(1, hidden_one, hidden_one * hidden_one, hidden_one)
    means_two, scales_two = stats(summed)
    hidden_padded = jnp.concatenate([above, hidden_one, below])
    unit_padded = (hidden_padded - means_two) * scales_two
    normed_padded = unit_padded * norm_gains[1] + norm_biases[1]
    shifted_padded = normed_padded * (1.0 + scale_part) + shift_part
    act_two_padded = jnp.where(keep, jax.nn.silu(shifted_padded), 0.0).astype(low)
    unit_two = unit_padded[W:-W]
    normed_two = normed_padded[W:-W]
    shifted = shifted_padded[W:-W]
    taps_two = jnp.concatenate(taps_of(act_two_padded, False), axis=1)
    middle = inputs + dot(taps_two, conv_second) + conv_biases[1]
    summed, _ = totals(2, middle, middle * middle)
    means_three, scales_three = stats(summed)
    unit_three = (middle - means_three) * scales_three
    act_three = (unit_three * norm_gains[2] + norm_biases[2]).astype(low)
    projected = dot(act_three, qkv_weight)
    queries = (projected[:, :C] + qv_bias[:C]).astype(low)
    keys_values = jnp.concatenate(
        [projected[:, C : 2 * C], projected[:, 2 * C :] + qv_bias[C:]], axis=1
    ).astype(low)
    captions = caption[0, 0]
    text_kv = lax.cond(
        own_lead,
        lambda: (dot(captions, text_weight) + text_bias).astype(low),
        lambda: jnp.zeros((TEXT, 2 * C), low),
    )
    upstream = out_grad[0]
    upstream_float = upstream.astype(full)
    attended_grad = dot_last(upstream, proj_weight).astype(low)
    group = lax.axis_index(ITEMS)
    groups = lax.axis_size(ITEMS)
    attended_low, query_low, key_value_low, text_low = attention_by_band(
        band_items, position, queries, keys_values, text_kv, attended_grad
    )
    result = middle + dot(attended_low, proj_weight) + proj_bias
    proj_weight_grad = dot_first(attended_low, upstream)
    proj_bias_grad = jnp.sum(upstream_float, axis=0)
    qkv_grad = jnp.concatenate([query_low, key_value_low], axis=1)
    qkv_weight_grad = dot_first(act_three, qkv_grad)
    qv_bias_grad = jnp.sum(
        jnp.concatenate([query_low, key_value_low[:, C:]], axis=1).astype(full), axis=0
    )
    text_weight_grad = dot_first(captions, text_low)
    text_bias_grad = jnp.sum(text_low.astype(full), axis=0)
    caption_grad = dot_last(text_low, text_weight)[None, None]
    three_grad = dot_last(qkv_grad, qkv_weight)
    gain_three = jnp.sum(three_grad * unit_three, axis=0)
    bias_three = jnp.sum(three_grad, axis=0)

    def conv_back(padded, weight):
        views = jnp.stack(taps_of(padded, True))
        return jnp.einsum(
            "tpd,tcd->pc", views, weight.reshape(9, C, C), preferred_element_type=full
        )

    def norm_back(ident, grad_unit, unit_value, scales, base, with_edges=True):
        scaled = base + grad_unit * scales
        edges = jnp.concatenate([scaled, unit_value], axis=1) if with_edges else None
        summed, around = totals(ident, grad_unit, grad_unit * unit_value, edges)
        mean_grad, mean_cross = spread(summed[0]) * scales, spread(summed[1]) * scales
        if not with_edges:
            return scaled - mean_grad - unit_value * mean_cross
        both = jnp.concatenate([around[0], edges, around[1]])
        return both[:, :C] - mean_grad - both[:, C:] * mean_cross

    middle_padded = norm_back(3, three_grad * norm_gains[2], unit_three, scales_three, upstream_float)
    middle_grad = middle_padded[W:-W]
    low_padded = jnp.where(keep, middle_padded, 0.0).astype(low)
    hidden_two_low = low_padded[W:-W]
    conv_bias_two = jnp.sum(hidden_two_low.astype(full), axis=0)
    conv_second_grad = dot_first(taps_two, hidden_two_low)
    act_two_grad = conv_back(low_padded, conv_second)
    shifted_grad = act_two_grad * silu_slope(shifted)
    modulation_grad = jnp.concatenate(
        [jnp.sum(shifted_grad * normed_two, axis=0), jnp.sum(shifted_grad, axis=0)]
    )
    normed_two_grad = shifted_grad * (1.0 + scale_part)
    gain_two = jnp.sum(normed_two_grad * unit_two, axis=0)
    bias_two = jnp.sum(normed_two_grad, axis=0)
    hidden_back = norm_back(4, normed_two_grad * norm_gains[1], unit_two, scales_two, 0.0)
    low_padded = jnp.where(keep, hidden_back, 0.0).astype(low)
    hidden_one_low = low_padded[W:-W]
    conv_bias_one = jnp.sum(hidden_one_low.astype(full), axis=0)
    conv_first_grad = dot_first(taps_one, hidden_one_low)
    act_one_grad = conv_back(low_padded, conv_first)
    normed_one_grad = act_one_grad * silu_slope(normed_one)
    gain_one = jnp.sum(normed_one_grad * unit_one, axis=0)
    bias_one = jnp.sum(normed_one_grad, axis=0)
    image_grad = norm_back(
        5, normed_one_grad * norm_gains[0], unit_one, scales_one, middle_grad, False
    )
    group_hot = (jnp.arange(groups) == group).astype(full)
    tables = group_hot[:, None, None] * slot_hot[None, :, None] * modulation_grad
    vectors = jnp.concatenate(
        [
            gain_one,
            gain_two,
            gain_three,
            bias_one,
            bias_two,
            bias_three,
            conv_bias_one,
            conv_bias_two,
            qv_bias_grad,
            text_bias_grad,
            proj_bias_grad,
        ]
    )
    small = jnp.concatenate([tables.reshape(-1, C), vectors.reshape(-1, C)])
    row_share = EMB // lax.axis_size(ROWS)
    silu_share = lax.dynamic_slice_in_dim(embed_silu, position * row_share, row_share, 1)
    grads = (conv_first_grad, conv_second_grad, qkv_weight_grad, text_weight_grad, proj_weight_grad)
    grads = [g.astype(low) for g in grads]
    small = lax.psum(small.astype(low), (ROWS, ITEMS)).astype(full)
    tables_sum = small[: groups * slots * 2].reshape(groups, slots, 2 * C).astype(low)
    part = dot_first(silu_share, jnp.take(tables_sum, group, axis=0)).astype(low)
    matrices = [lax.psum_scatter(g, ROWS, scatter_dimension=0, tiled=True) for g in grads]
    *matrices, embed_weight_grad = [
        lax.psum(m, ITEMS).astype(full) for m in matrices + [part]
    ]
    vectors_sum = small[groups * slots * 2 :]
    modulation_low = jnp.take(tables_sum, group, axis=0)
    embed_bias_grad = jnp.sum(tables_sum.astype(full), axis=(0, 1))
    embedding_grad = dot_last(modulation_low, embed_weight) * silu_slope(embedding[0].astype(full))
    return (
        result.astype(low)[None],
        image_grad[None],
        embedding_grad[None],
        caption_grad,
        vectors_sum[0:3],
        vectors_sum[3:6],
        matrices[0],
        matrices[1],
        vectors_sum[6:8],
        embed_weight_grad,
        embed_bias_grad,
        matrices[2],
        vectors_sum[8:10].reshape(-1),
        matrices[3],
        vectors_sum[10:12].reshape(-1),
        matrices[4],
        vectors_sum[12],
    )


def solution(mesh):
    in_specs = (
        P(ITEMS, ROWS, None),
        P(ITEMS, None, None),
        P(ITEMS, ROWS, None, None),
        P(ITEMS, None),
        P(ITEMS, ROWS, None),
        P(),
        P(),
        P(),
        P(),
        P(),
        P(),
        P(),
        P(),
        P(),
        P(),
        P(),
        P(),
        P(),
    )
    out_specs = (
        P(ITEMS, ROWS, None),
        P(ITEMS, ROWS, None),
        P(ITEMS, None, None),
        P(ITEMS, ROWS, None, None),
        P(),
        P(),
        P(ROWS, None),
        P(ROWS, None),
        P(),
        P(ROWS, None),
        P(),
        P(ROWS, None),
        P(),
        P(ROWS, None),
        P(),
        P(ROWS, None),
        P(),
    )
    return jax.shard_map(shards, mesh=mesh, in_specs=in_specs, out_specs=out_specs, check_vma=False)
```

```python
import functools
import types
import typing

import jax
import jax.numpy as jnp
from jax import lax
from jax.experimental import pallas as pl
from jax.experimental.pallas import tpu as pltpu
from jax.sharding import PartitionSpec as P

C = 512
HEADS = 8
HEAD = 64
EMB = 2048
TEXT = 128
NORM_GROUPS = 32
W = 64
SPAN = 8
ROWS, ITEMS = "rows", "items"


epsilon = 1e-05


def from_behind(array, axis, by):
    length = lax.axis_size(axis)
    pairs = [(i, i + by) for i in range(length) if 0 <= i + by < length]
    return lax.ppermute(array, axis, pairs)


def as_sent(array):
    return jax.tree.map(lambda a: a.astype(jnp.bfloat16) if a.dtype == jnp.float32 else a, array)


def keep_state(state):
    return state


def silu_slope(source):
    sigma = jax.nn.sigmoid(source)
    return sigma * (1.0 + source * (1.0 - sigma))


def dot_first(left_side, right_side):
    return lax.dot_general(
        left_side, right_side, (((0,), (0,)), ((), ())), preferred_element_type=jnp.float32
    )


def dot_last(left_side, right_side):
    return lax.dot_general(
        left_side, right_side, (((1,), (1,)), ((), ())), preferred_element_type=jnp.float32
    )


def head_split(source):
    return source.reshape(source.shape[0], HEADS, HEAD)


def piece_scores(query_heads, key_piece, allowed):
    key_heads = head_split(key_piece[:, :C])
    scores = jnp.einsum(
        "qhd,khd->hqk", query_heads, key_heads, preferred_element_type=jnp.float32
    ) * HEAD ** (-0.5)
    return jnp.where(allowed[None, None, :], scores, -jnp.inf)


def piece_grads(query_heads, grad_heads, log_total, row_dots, key_piece, allowed):
    scores = piece_scores(query_heads, key_piece, allowed)
    weights = jnp.exp(scores - log_total[:, :, None])
    value_heads = head_split(key_piece[:, C:])
    weight_grad = jnp.einsum(
        "qhd,khd->hqk", grad_heads, value_heads, preferred_element_type=jnp.float32
    )
    score_grad = (weights * (weight_grad - row_dots[:, :, None])).astype(jnp.bfloat16)
    outcome = []
    key_heads = head_split(key_piece[:, :C])
    query_grad = jnp.einsum(
        "hqk,khd->qhd", score_grad, key_heads, preferred_element_type=jnp.float32
    ) * HEAD ** (-0.5)
    outcome.append(query_grad.reshape(query_grad.shape[0], C))
    key_grad = jnp.einsum(
        "hqk,qhd->khd", score_grad, query_heads, preferred_element_type=jnp.float32
    ) * HEAD ** (-0.5)
    value_grad = jnp.einsum(
        "hqk,qhd->khd", weights.astype(jnp.bfloat16), grad_heads, preferred_element_type=jnp.float32
    )
    outcome.append(jnp.concatenate([key_grad.reshape(-1, C), value_grad.reshape(-1, C)], axis=1))
    return tuple(outcome)


def source_masks(band_items, source, my_item, pixels):
    slots = band_items.shape[0]
    inside = (source >= 0) & (source < slots)
    clipped = jnp.clip(source, 0, slots - 1)
    source_item = band_items[clipped]
    before_item = band_items[jnp.maximum(clipped - 1, 0)]
    same_item = inside & (source_item == my_item)
    leading = same_item & ((clipped == 0) | (before_item != source_item))
    allowed = jnp.concatenate(
        [jnp.broadcast_to(same_item, (pixels,)), jnp.broadcast_to(leading, (TEXT,))]
    )
    return (allowed, same_item)


REACH = SPAN - 1
LOG2E = 1.4426950408889634
FAR_ABOVE = 1e30
PIX = 512


def dot(left, right):
    return jnp.dot(left, right, preferred_element_type=jnp.float32)


def reach_of(here, slots):
    first = here < SPAN
    low = jnp.maximum(jnp.where(first, 0, SPAN), here - REACH)
    high = jnp.minimum(jnp.where(first, SPAN - 1, slots - 1), here + REACH)
    return low, high


def exchange_kernel(slots, with_edges, *refs):
    if with_edges:
        tile, top, bottom, window, above, below, send_sem, recv_sem, edge_send, edge_recv = refs
    else:
        tile, window, send_sem, recv_sem = refs
    here = lax.axis_index(ROWS)
    low, high = reach_of(here, slots)
    offsets = [o for o in range(-REACH, REACH + 1) if o != 0]

    def reached(offset):
        return (here + offset >= low) & (here + offset <= high)

    barrier = pltpu.get_barrier_semaphore()
    for o in offsets:

        @pl.when(reached(o))
        def _(o=o):
            pl.semaphore_signal(barrier, 1, device_id={ROWS: here + o})

    pl.semaphore_wait(barrier, high - low)

    def edge_copy(o):
        source, target, k = (top, below, 0) if o < 0 else (bottom, above, 1)
        return pltpu.make_async_remote_copy(
            source, target, edge_send.at[k], edge_recv.at[k], device_id={ROWS: here + o}
        )

    def tile_copy(o):
        return pltpu.make_async_remote_copy(
            tile,
            window.at[REACH - o],
            send_sem.at[REACH - o],
            recv_sem.at[REACH - o],
            device_id={ROWS: here + o},
        )

    if with_edges:
        for o in (-1, 1):

            @pl.when(reached(o))
            def _(o=o):
                edge_copy(o).start()

    for o in offsets:

        @pl.when(reached(o))
        def _(o=o):
            tile_copy(o).start()

        @pl.when(jnp.logical_not(reached(-o)))
        def _(o=o):
            window[REACH - o] = jnp.zeros_like(tile)

    window[REACH] = tile[...]
    if with_edges:

        @pl.when(jnp.logical_not(reached(-1)))
        def _():
            above[...] = jnp.zeros_like(above)

        @pl.when(jnp.logical_not(reached(1)))
        def _():
            below[...] = jnp.zeros_like(below)

    for o in offsets:

        @pl.when(reached(o))
        def _(o=o):
            tile_copy(o).wait_send()

        @pl.when(reached(-o))
        def _(o=o):
            tile_copy(o).wait_recv()

    if with_edges:
        for o in (-1, 1):

            @pl.when(reached(o))
            def _(o=o):
                edge_copy(o).wait_send()

            @pl.when(reached(-o))
            def _(o=o):
                edge_copy(o).wait_recv()


def exchange(ident, slots, tile, edges=None):
    vmem = pl.BlockSpec(memory_space=pltpu.VMEM)
    shapes = [jax.ShapeDtypeStruct((2 * REACH + 1,) + tile.shape, tile.dtype)]
    scratch = [pltpu.SemaphoreType.DMA((2 * REACH + 1,))] * 2
    operands = [tile]
    if edges is not None:
        shapes += [jax.ShapeDtypeStruct(e.shape, e.dtype) for e in edges]
        scratch += [pltpu.SemaphoreType.DMA((2,))] * 2
        operands += list(edges)
    return pl.pallas_call(
        functools.partial(exchange_kernel, slots, edges is not None),
        out_shape=tuple(shapes),
        in_specs=[vmem] * len(operands),
        out_specs=(vmem,) * len(shapes),
        scratch_shapes=scratch,
        compiler_params=pltpu.CompilerParams(collective_id=ident, has_side_effects=True),
        name=f"exchange_{ident}",
    )(*operands)


def head_kernel(
    items, y_ref, t_ref, z_ref, zt_ref, xt, vx, tt, tvx, s_ref, p_ref, dk, dv, dkt, dvt
):
    low = jnp.bfloat16
    full = jnp.float32
    bands, pixels = y_ref.shape[0], y_ref.shape[1]
    text = t_ref.shape[1]
    scale = HEAD ** (-0.5)

    def widened(values, rows):
        lanes = lax.broadcasted_iota(jnp.int32, (rows, 2 * HEAD), 1)
        units = jnp.where(lanes < HEAD + 2, 1.0, 0.0).astype(low)
        return jnp.where(lanes < HEAD, values, units)

    def prepare(b, carry):
        block = y_ref[b]
        xt[b] = block.T
        vx[b] = widened(block[:, 2 * HEAD :], pixels)
        words = t_ref[b]
        tt[b] = words.T
        tvx[b] = widened(pltpu.roll(words.astype(full), HEAD, 1).astype(low), text)
        dk[b] = jnp.zeros((pixels, 2 * HEAD), full)
        dv[b] = jnp.zeros((pixels, 2 * HEAD), full)
        dkt[b] = jnp.zeros((text, 2 * HEAD), full)
        dvt[b] = jnp.zeros((text, 2 * HEAD), full)
        return carry

    lax.fori_loop(0, bands, prepare, 0)

    def one_row(columns):
        rows = lax.broadcasted_iota(jnp.int32, (16, columns), 0)
        return jnp.where(rows == 0, 1.0, 0.0).astype(low)

    ones_pixels = one_row(pixels)
    ones_text = one_row(text)
    zeros = jnp.zeros((HEAD, pixels), low)

    base = (lax.axis_index(ROWS) // SPAN) * SPAN

    def query_band(i, carry):
        mine = items[base + i]
        start = 0
        allowed = []
        for b in range(bands):
            other = items[base + b]
            start = start + jnp.where(other < mine, 1, 0)
            allowed.append(other == mine)
        query_t = (xt[i, 0:HEAD, :].astype(full) * scale).astype(low)
        query_rhs = jnp.concatenate([zeros, query_t], 0)
        query_text = jnp.concatenate([query_t, zeros], 0)

        top = jnp.full((8, pixels), -jnp.inf, full)
        for j in range(bands):
            scores = dot(y_ref[j, :, 0 : 2 * HEAD], query_rhs)
            s_ref[j] = scores
            highest = jnp.max(scores.reshape(pixels // 8, 8, pixels), axis=0)
            top = jnp.where(allowed[j], jnp.maximum(top, highest), top)
        scores = dot(t_ref[start], query_text)
        top = jnp.maximum(top, jnp.max(scores.reshape(text // 8, 8, pixels), axis=0))
        top = jnp.max(top, axis=0, keepdims=True)
        weights_text = jnp.exp2((scores - top) * LOG2E).astype(low)
        total = dot(jnp.concatenate([tt[start, HEAD:, :], ones_text], 0), weights_text)

        for j in range(bands):
            ceiling = top + jnp.where(allowed[j], 0.0, FAR_ABOVE)
            weights = jnp.exp2((s_ref[j] - ceiling) * LOG2E).astype(low)
            p_ref[j] = weights
            values = jnp.concatenate([xt[j, 2 * HEAD : 3 * HEAD, :], ones_pixels], 0)
            total = total + dot(values, weights)
        inverse = 1.0 / total[HEAD : HEAD + 1, :]
        attended = total[0:HEAD, :] * inverse
        grad = xt[i, 3 * HEAD :, :].astype(full)
        minus_dots = -jnp.sum(grad * attended, axis=0, keepdims=True) * inverse
        grad_scaled = (grad * inverse).astype(low)
        coarse = minus_dots.astype(low)
        fine = minus_dots - coarse.astype(full)
        rows = lax.broadcasted_iota(jnp.int32, (HEAD, pixels), 0)
        extra = jnp.where(rows == 0, coarse.astype(full), jnp.where(rows == 1, fine, 0.0))
        grad_rhs = jnp.concatenate([grad_scaled, extra.astype(low)], 0)
        grad_rows = jnp.concatenate([grad_scaled, zeros], 0).T
        query_rows = jnp.concatenate([query_t, zeros], 0).T

        steps = (weights_text.astype(full) * dot(tvx[start], grad_rhs)).astype(low)
        dvt[start] += dot(weights_text, grad_rows)
        dkt[start] += dot(steps, query_rows)
        query_grad = dot(tt[start, 0:HEAD, :], steps)
        for j in range(bands):
            for begin in range(0, pixels, pixels // 2):
                keys = slice(begin, begin + pixels // 2)
                weights = p_ref[j, keys]
                steps = (weights.astype(full) * dot(vx[j, keys], grad_rhs)).astype(low)
                dv[j, keys] += dot(weights, grad_rows)
                dk[j, keys] += dot(steps, query_rows)
                query_grad = query_grad + dot(xt[j, HEAD : 2 * HEAD, keys], steps)
        z_ref[i, :, 0 : 2 * HEAD] = jnp.concatenate(
            [attended.astype(low), (query_grad * scale).astype(low)], 0
        ).T
        return carry

    lax.fori_loop(0, bands, query_band, 0)

    def finish(b, carry):
        lanes = lax.broadcasted_iota(jnp.int32, (pixels, 2 * HEAD), 1)
        z_ref[b, :, 2 * HEAD :] = jnp.where(
            lanes < HEAD, dk[b], pltpu.roll(dv[b], HEAD, 1)
        ).astype(low)
        lanes = lax.broadcasted_iota(jnp.int32, (text, 2 * HEAD), 1)
        zt_ref[b] = jnp.where(lanes < HEAD, dkt[b], pltpu.roll(dvt[b], HEAD, 1)).astype(low)
        return carry

    lax.fori_loop(0, bands, finish, 0)


def one_head(items, pieces, words):
    bands, pixels, _ = pieces.shape
    text = words.shape[1]
    low, full = jnp.bfloat16, jnp.float32
    smem = pl.BlockSpec(memory_space=pltpu.SMEM)
    vmem = pl.BlockSpec(memory_space=pltpu.VMEM)
    return pl.pallas_call(
        head_kernel,
        out_shape=(
            jax.ShapeDtypeStruct(pieces.shape, low),
            jax.ShapeDtypeStruct(words.shape, low),
        ),
        in_specs=[smem, vmem, vmem],
        out_specs=(vmem, vmem),
        scratch_shapes=[
            pltpu.VMEM((bands, 4 * HEAD, pixels), low),
            pltpu.VMEM((bands, pixels, 2 * HEAD), low),
            pltpu.VMEM((bands, 2 * HEAD, text), low),
            pltpu.VMEM((bands, text, 2 * HEAD), low),
            pltpu.VMEM((bands, pixels, pixels), full),
            pltpu.VMEM((bands, pixels, pixels), low),
            pltpu.VMEM((bands, pixels, 2 * HEAD), full),
            pltpu.VMEM((bands, pixels, 2 * HEAD), full),
            pltpu.VMEM((bands, text, 2 * HEAD), full),
            pltpu.VMEM((bands, text, 2 * HEAD), full),
        ],
        compiler_params=pltpu.CompilerParams(vmem_limit_bytes=56 << 20),
        name="one_head",
    )(items, pieces, words)


def attention_by_band(band_items, position, queries, keys_values, text_kv, attended_grad):
    my_item = band_items[position]
    pixels = queries.shape[0]
    own_allowed, own_same = source_masks(band_items, position, my_item, pixels)
    packed = jnp.concatenate([keys_values, text_kv], axis=0)
    pieces = [(0, packed, own_allowed, own_same)]
    for distance in range(1, SPAN):
        for offset in (distance, -distance):
            arrived = from_behind(packed, ROWS, offset)
            allowed, same_item = source_masks(band_items, position - offset, my_item, pixels)
            pieces.append((offset, arrived, allowed, same_item))
    query_heads = head_split(queries)
    row_top = jnp.full((HEADS, pixels), -jnp.inf, jnp.float32)
    weight_sum = jnp.zeros((HEADS, pixels), jnp.float32)
    for offset, key_piece, allowed, same_item in pieces:

        def gather_scores(state, key_piece=key_piece, allowed=allowed):
            top_old, sum_old = state
            scores = piece_scores(query_heads, key_piece, allowed)
            top_new = jnp.maximum(top_old, jnp.max(scores, axis=2))
            sum_new = sum_old * jnp.exp(top_old - top_new) + jnp.sum(
                jnp.exp(scores - top_new[:, :, None]), axis=2
            )
            return (top_new, sum_new)

        row_top, weight_sum = lax.cond(same_item, gather_scores, keep_state, (row_top, weight_sum))
    log_total = row_top + jnp.log(weight_sum)
    attended = jnp.zeros((pixels, HEADS, HEAD), jnp.float32)
    for offset, key_piece, allowed, same_item in pieces:

        def add_values(totals, key_piece=key_piece, allowed=allowed):
            scores = piece_scores(query_heads, key_piece, allowed)
            weights = jnp.exp(scores - log_total[:, :, None]).astype(jnp.bfloat16)
            return totals + jnp.einsum(
                "hqk,khd->qhd",
                weights,
                head_split(key_piece[:, C:]),
                preferred_element_type=jnp.float32,
            )

        attended = lax.cond(same_item, add_values, keep_state, attended)
    attended_flat = attended.reshape(pixels, C)
    row_dots = jnp.sum(
        (attended_grad.astype(jnp.float32) * attended_flat).reshape(pixels, HEADS, HEAD), axis=2
    ).T
    grad_heads = head_split(attended_grad)
    query_grad = jnp.zeros((pixels, C), jnp.float32)
    packed_grad = jnp.zeros((pixels + TEXT, 2 * C), jnp.float32)
    zero_piece = jnp.zeros((pixels + TEXT, 2 * C), jnp.float32)
    for offset, key_piece, allowed, same_item in pieces:

        def grad_both(totals, key_piece=key_piece, allowed=allowed):
            outcome = piece_grads(query_heads, grad_heads, log_total, row_dots, key_piece, allowed)
            return (totals + outcome[0], outcome[1])

        def grad_none(totals):
            return (totals, zero_piece)

        query_grad, piece_grad = lax.cond(same_item, grad_both, grad_none, query_grad)
        if offset == 0:
            packed_grad = packed_grad + piece_grad
        else:
            packed_grad = packed_grad + from_behind(
                as_sent(piece_grad), ROWS, -offset
            ).astype(jnp.float32)
    packed_low = packed_grad.astype(jnp.bfloat16)
    return (
        attended_flat.astype(jnp.bfloat16),
        query_grad.astype(jnp.bfloat16),
        packed_low[:pixels],
        packed_low[pixels:],
    )


def taps_of(rows, reverse):
    padded = rows.reshape(-1, W, rows.shape[1])
    row_list = [padded[:-2], padded[1:-1], padded[2:]]
    if reverse:
        row_list = row_list[::-1]
    zero_column = jnp.zeros_like(row_list[0][:, :1])
    views = []
    for row_view in row_list:
        left_view = jnp.concatenate([zero_column, row_view[:, :-1]], axis=1)
        right_view = jnp.concatenate([row_view[:, 1:], zero_column], axis=1)
        view_list = [left_view, row_view, right_view]
        if reverse:
            view_list = view_list[::-1]
        views = views + view_list
    return [view.reshape(-1, rows.shape[1]) for view in views]


class Vectors(typing.NamedTuple):
    mean_one: jax.Array
    scale_one: jax.Array
    gain_one: jax.Array
    bias_one: jax.Array
    mean_two: jax.Array
    scale_two: jax.Array
    gain_two: jax.Array
    bias_two: jax.Array
    mean_three: jax.Array
    scale_three: jax.Array
    gain_three: jax.Array
    bias_three: jax.Array
    stretch: jax.Array
    shift: jax.Array
    proj_bias: jax.Array
    keep_above: jax.Array
    keep_below: jax.Array
    per_item: jax.Array


def grouped(names, refs):
    found, position = types.SimpleNamespace(), 0
    for name, count in names:
        if count is None:
            setattr(found, name, refs[position])
            position += 1
        else:
            setattr(found, name, refs[position : position + count])
            position += count
    return found


def call_named(kernel, ident, scalars, inputs, anywhere, outs, scratch, semaphores):
    names = [(name, None) for name in [*scalars, *inputs, *anywhere, *outs]]
    buffers = []
    for name, entry in scratch.items():
        many = isinstance(entry, list)
        names.append((name, len(entry) if many else None))
        buffers += [pltpu.VMEM(*e) for e in (entry if many else [entry])]
    names += [(name, None) for name in semaphores]
    vmem = pl.BlockSpec(memory_space=pltpu.VMEM)
    outcome = pl.pallas_call(
        functools.partial(kernel, names),
        out_shape=tuple(jax.ShapeDtypeStruct(*o) for o in outs.values()),
        in_specs=[pl.BlockSpec(memory_space=pltpu.SMEM)] * len(scalars)
        + [vmem] * len(inputs)
        + [pl.BlockSpec(memory_space=pl.ANY)] * len(anywhere),
        out_specs=(vmem,) * len(outs),
        scratch_shapes=buffers + [pltpu.SemaphoreType.DMA(s) for s in semaphores.values()],
        compiler_params=pltpu.CompilerParams(
            collective_id=ident, has_side_effects=True, vmem_limit_bytes=60 << 20
        ),
        name=kernel.__name__,
    )(*[v for group in (scalars, inputs, anywhere) for v in dict(group).values()])
    return types.SimpleNamespace(**dict(zip(outs, outcome)))


VECTOR_ROWS = 24
FAR, NEAR, SIDE, CORE, GROUP = range(5)
CROSS = (FAR, NEAR, SIDE)
SIDE_FIRST = (SIDE, GROUP, NEAR, FAR)
GROUP_FIRST = (GROUP, NEAR, SIDE, FAR)
NEAR_FIRST = (NEAR, SIDE, GROUP, FAR)
STREAMS = (
    (48, C // 2, SIDE_FIRST),
    (48, C // 2, GROUP_FIRST),
    (48, C // 2, NEAR_FIRST),
    (48, C // 2, SIDE_FIRST),
    (48, C // 2, GROUP_FIRST),
    (48, C // 2, NEAR_FIRST),
    (32, C, SIDE_FIRST),
    (32, C, NEAR_FIRST),
    (16, 3 * C // 2, GROUP_FIRST),
    (16, C // 2, GROUP_FIRST),
)
FIRST_CONV, SECOND_CONV, WORDS, QKV, PROJ = 0, 3, 6, 8, 9
LANDINGS = 4
IMAGE_ROWS = 8


class Band:
    def __init__(self, r):
        self.r = r
        self.row = lax.axis_index(ROWS)
        self.group = lax.axis_index(ITEMS)
        self.lane = self.row % SPAN
        self.base = self.row - self.lane
        row = self.row
        self.place = [row // 8, (row // 4) % 2, (row // 2) % 2, row % 2, self.group]
        self.partner = [
            {ROWS: row + (1 - 2 * self.place[d]) * (8 >> d)} for d in range(CORE + 1)
        ]
        self.partner.append({ITEMS: 1 - self.group})
        self.others = [(self.lane + o) % SPAN for o in range(1, SPAN)]
        self.peers = [{ROWS: self.base + other} for other in self.others]
        self.has_above, self.has_below = self.lane > 0, self.lane < SPAN - 1

    def meet(self, further=()):
        barrier = pltpu.get_barrier_semaphore()
        targets = self.peers + [self.partner[d] for d in further]
        for target in targets:
            pl.semaphore_signal(barrier, 1, device_id=target)
        pl.semaphore_wait(barrier, len(targets))

    def remote(self, source, target, send, recv, device):
        return pltpu.make_async_remote_copy(source, target, send, recv, device_id=device)

    def edges(self, k, top, bottom, target):
        r = self.r
        up = self.remote(
            top,
            target.at[IMAGE_ROWS + 1],
            r.edge_send.at[k, 0],
            r.edge_recv.at[k, 0],
            {ROWS: self.row - 1},
        )
        down = self.remote(
            bottom,
            target.at[0],
            r.edge_send.at[k, 1],
            r.edge_recv.at[k, 1],
            {ROWS: self.row + 1},
        )
        pl.when(self.has_above)(up.start)
        pl.when(self.has_below)(down.start)
        return up, down

    def wait_edges(self, pair):
        up, down = pair

        @pl.when(self.has_above)
        def _():
            up.wait_send()
            down.wait_recv()

        @pl.when(self.has_below)
        def _():
            down.wait_send()
            up.wait_recv()

    def zero_edges(self, target):
        @pl.when(jnp.logical_not(self.has_above))
        def _():
            target[0] = jnp.zeros(target.shape[1:], target.dtype)

        @pl.when(jnp.logical_not(self.has_below))
        def _():
            target[IMAGE_ROWS + 1] = jnp.zeros(target.shape[1:], target.dtype)

    def send_tile(self, k, source, target):
        r = self.r
        copies = []
        for o in range(1, SPAN):
            copies.append(
                self.remote(
                    source,
                    target.at[self.lane],
                    r.tile_send.at[k, o],
                    r.tile_recv.at[k, o],
                    self.peers[o - 1],
                )
            )
        for copy in copies:
            copy.start()
        target[self.lane] = source[...]
        return copies

    def swap(self, k, source, target, order=range(1, SPAN)):
        r = self.r
        copies = []
        for o in order:
            copies.append(
                self.remote(
                    source.at[self.others[o - 1]],
                    target.at[self.lane],
                    r.swap_send.at[k, o],
                    r.swap_recv.at[k, o],
                    self.peers[o - 1],
                )
            )
            copies[-1].start()
        return copies

    def fill_blocks(self):
        rows = lax.broadcasted_iota(jnp.int32, (C, C), 0) // (C // NORM_GROUPS)
        columns = lax.broadcasted_iota(jnp.int32, (C, C), 1) // (C // NORM_GROUPS)
        self.r.blocks[...] = jnp.where(rows == columns, 1.0, 0.0).astype(jnp.bfloat16)

    def item_means(self, window, masks, per_item):
        low, full = jnp.bfloat16, jnp.float32
        total = jnp.zeros((8, C), full)
        for b in range(SPAN):
            total = total + jnp.where(masks[b] > 0.0, window[b], 0.0)
        total = total * per_item
        coarse = total.astype(low)
        rest = total - coarse.astype(full)
        finer = rest.astype(low)
        finest = (rest - finer.astype(full)).astype(low)
        blocks = self.r.blocks[...]
        return dot(coarse, blocks) + dot(finer, blocks) + dot(finest, blocks)


def sums_tile(first, second):
    rows = lax.broadcasted_iota(jnp.int32, (8, C), 0)
    return jnp.where(rows == 0, first, jnp.where(rows == 1, second, 0.0))


def column_sum(values):
    return jnp.sum(values, axis=0, keepdims=True)


def side_shifts(values):
    rows = lax.broadcasted_iota(jnp.int32, (W, C), 0)
    from_left = jnp.where(rows == 0, 0.0, pltpu.roll(values, 1, 0))
    from_right = jnp.where(rows == W - 1, 0.0, pltpu.roll(values, W - 1, 0))
    return from_left, from_right


def kept(i, values, vec):
    keep = jnp.where(i == 0, vec.keep_above, jnp.where(i == IMAGE_ROWS + 1, vec.keep_below, 1.0))
    return jnp.where(keep > 0.0, values, 0.0)


def back_kernel(names, *refs):
    low, full = jnp.bfloat16, jnp.float32
    r = grouped(names, refs)
    band = Band(r)
    lane, group, place, partner = band.lane, band.group, band.place, band.partner
    core = place[CORE]
    remote = band.remote
    band.meet((FAR, GROUP))

    swaps = band.swap(0, r.pieces, r.heads) + band.swap(1, r.words, r.head_words)

    loads = types.SimpleNamespace()

    def load(k, source, target):
        copy = pltpu.make_async_copy(source, target, r.load_sem.at[k])
        copy.start()
        return copy

    loads.own = load(0, r.pieces.at[lane], r.heads.at[lane])
    loads.own_words = load(1, r.words.at[lane], r.head_words.at[lane])
    loads.middle = load(2, r.middle, r.mid)
    loads.qkv_weight = load(3, r.qkv_weight, r.qkv_w)
    loads.proj_weight = load(4, r.proj_weight, r.proj_w)
    loads.upstream = load(5, r.upstream, r.up)
    loads.act_three = load(6, r.act_three, r.act3)
    loads.caption = load(7, r.caption, r.cap)
    loads.conv_second = load(8, r.conv_second, r.conv_w)
    loads.hidden = load(9, r.hidden, r.hid)
    loads.act_two = load(10, r.act_two, r.act2)
    loads.act_one = load(11, r.act_one, r.act1)
    loads.image = load(12, r.image, r.img)
    loads.text_weight = load(13, r.text_weight, r.text_w)

    sibling = types.SimpleNamespace()

    def to_sibling(k, source, target):
        copy = remote(source, target, r.sib_send.at[k], r.sib_recv.at[k], partner[CORE])
        copy.start()
        return copy

    half = pl.ds(pl.multiple_of((1 - core) * (C // 2), C // 2), C // 2)
    sibling.upstream = to_sibling(0, r.upstream.at[:, half], r.sib_up)
    sibling.act3 = to_sibling(1, r.act_three, r.sib_act3)
    sibling.cap = to_sibling(2, r.caption, r.sib_cap)
    sibling.act2 = to_sibling(3, r.act_two, r.sib_act2)
    sibling.act1 = to_sibling(4, r.act_one, r.sib_act1)

    share_copy = remote(
        r.silu_share, r.other_share, r.small_send.at[2], r.small_recv.at[2], partner[GROUP]
    )
    share_copy.start()
    for target in (r.part_two, r.part_one):
        band.zero_edges(target)

    vec = Vectors(*[r.vectors[i : i + 1, :] for i in range(len(Vectors._fields))])
    norm_one = (vec.mean_one, vec.scale_one)
    norm_two = (vec.mean_two, vec.scale_two)
    norm_three = (vec.mean_three, vec.scale_three)

    masks = [r.vectors[VECTOR_ROWS + b : VECTOR_ROWS + b + 1, :] for b in range(SPAN)]
    band.fill_blocks()

    def item_means(window):
        return band.item_means(window, masks, vec.per_item)

    class Stream:
        def __init__(self, k):
            self.k = k
            self.order = STREAMS[k][2]
            self.dims = [FAR, NEAR, SIDE, CORE, GROUP]
            self.step = 0
            self.copy = None

        def at(self, ref, d, index):
            return ref.at[(slice(None),) * self.dims.index(d) + (index,)]

        def start(self):
            self.launch(r.grads[self.k])

        def launch(self, ref):
            k, step = self.k, self.step
            if step < LANDINGS:
                d = self.order[step]
                self.copy = remote(
                    self.at(ref, d, 1 - place[d]),
                    r.landings[k * LANDINGS + step],
                    r.fold_send.at[k, step],
                    r.fold_recv.at[k, step],
                    partner[d],
                )
                self.mine = self.at(ref, d, place[d])
                self.dims.remove(d)
            elif step == LANDINGS:
                fin = r.folded[self.k]
                self.copy = remote(
                    ref.at[1 - core],
                    fin.at[core],
                    r.fold_send.at[k, step],
                    r.fold_recv.at[k, step],
                    partner[CORE],
                )
                self.mine = ref.at[core]
            else:
                self.copy = remote(
                    r.folded[self.k],
                    r.whole[self.k],
                    r.fold_send.at[k, step],
                    r.fold_recv.at[k, step],
                    partner[GROUP],
                )
            self.copy.start()

        def advance(self):
            self.copy.wait()
            if self.step < LANDINGS:
                landed, mine = r.landings[self.k * LANDINGS + self.step], self.mine
                lead = landed.shape[:-2]
                pieces = 1
                for n in lead:
                    pieces *= n

                def add(i, carry):
                    index = []
                    for n in reversed(lead):
                        index.insert(0, i % n)
                        i = i // n
                    index = tuple(index)
                    total = landed[index].astype(full) + mine[index].astype(full)
                    landed[index] = total.astype(low)
                    return carry

                lax.fori_loop(0, pieces, add, 0)
                self.step += 1
                self.launch(landed)
            elif self.step == LANDINGS:
                r.folded[self.k][core] = self.mine[...]
                self.step += 1
                self.launch(None)
            else:
                self.step += 1

    streams = [Stream(k) for k in range(len(STREAMS))]

    loads.own.wait()
    loads.own_words.wait()
    for copy in swaps:
        copy.wait()
    for h in range(0, HEADS, 2):
        for k in range(4):
            pair = [r.heads[h + i, :, k * HEAD : (k + 1) * HEAD] for i in range(2)]
            r.joined[:, k * C + h * HEAD : k * C + (h + 2) * HEAD] = jnp.concatenate(pair, axis=1)
        for k in range(2):
            pair = [r.head_words[h + i, :, k * HEAD : (k + 1) * HEAD] for i in range(2)]
            r.joined_words[:, k * C + h * HEAD : k * C + (h + 2) * HEAD] = jnp.concatenate(
                pair, axis=1
            )
    sibling.attended = to_sibling(5, r.joined.at[:, 0:C], r.sib_attended)
    three_half = C + (1 - core) * (3 * C // 2)
    sibling.qkv = to_sibling(
        6,
        r.joined.at[:, pl.ds(pl.multiple_of(three_half, C // 2), 3 * C // 2)],
        r.sib_qkv,
    )
    sibling.words = to_sibling(
        7,
        r.joined_words.at[:, pl.ds(pl.multiple_of((1 - core) * C, C), C)],
        r.sib_words,
    )
    for copy in (loads.middle, loads.qkv_weight, loads.proj_weight, loads.upstream):
        copy.wait()

    def pixel_block(ref, i, count=4):
        return ref[1 + i * count : 1 + (i + 1) * count].reshape(count * W, C)

    def unit(values, norm):
        return (values - norm[0]) * norm[1]

    plain = jnp.zeros((1, C), full)
    crossed = jnp.zeros((1, C), full)
    up_sum = jnp.zeros((1, C), full)
    for i in range(2):
        block = slice(i * 4 * W, (i + 1) * 4 * W)
        middle = pixel_block(r.mid, i)
        upstream = r.up[block, :].astype(full)
        result = middle + dot(r.joined[block, 0:C], r.proj_w[...]) + vec.proj_bias
        r.result[block, :] = result.astype(low)
        grad = dot_last(r.joined[block, C:], r.qkv_w[...])
        plain = plain + column_sum(grad)
        crossed = crossed + column_sum(grad * unit(middle, norm_three))
        up_sum = up_sum + column_sum(upstream)
        part = upstream + grad * (vec.gain_three * vec.scale_three)
        r.part_two[1 + i * 4 : 5 + i * 4] = part.reshape(4, W, C)
    gain_three, bias_three = crossed, plain
    r.tile[0] = sums_tile(plain * vec.gain_three, crossed * vec.gain_three)
    three_edges = band.edges(0, r.part_two.at[1], r.part_two.at[IMAGE_ROWS], r.part_two)
    tiles = band.send_tile(0, r.tile.at[0], r.window.at[0])

    def mine_of(ref, start, size):
        return ref[:, pl.ds(pl.multiple_of(start, size if size % 256 else 256), size)]

    for copy in (sibling.upstream, sibling.act3, sibling.cap, sibling.attended, sibling.qkv, sibling.words):
        copy.wait()
    for copy in (loads.act_three, loads.caption):
        copy.wait()
    grad = dot_first(r.joined[:, 0:C], mine_of(r.up, core * (C // 2), C // 2))
    grad = grad + dot_first(r.sib_attended[...], r.sib_up[...])
    r.grads[PROJ][...] = grad.astype(low).reshape(r.grads[PROJ].shape)
    streams[PROJ].start()
    for n in range(3):
        own = mine_of(r.joined, C + core * (3 * C // 2) + n * (C // 2), C // 2)
        columns = slice(n * (C // 2), (n + 1) * (C // 2))
        grad = dot_first(r.act3[...], own)
        grad = grad + dot_first(r.sib_act3[...], r.sib_qkv[:, columns])
        r.grads[QKV][:, :, :, :, :, :, columns] = grad.astype(low).reshape(2, 2, 2, 2, 2, 16, C // 2)
    streams[QKV].start()

    def text_rows(s, carry):
        columns = pl.ds(pl.multiple_of(s * 128, 128), 128)
        own = mine_of(r.joined_words, core * C, C)
        grad = dot_first(r.cap[:, columns], own)
        grad = grad + dot_first(r.sib_cap[:, columns], r.sib_words[...])
        grad = grad.astype(low)
        index = (s // 8, (s // 4) % 2, (s // 2) % 2, s % 2)
        r.grads[WORDS][index] = grad[0:64].reshape(2, 32, C)
        r.grads[WORDS + 1][index] = grad[64:128].reshape(2, 32, C)
        return carry

    lax.fori_loop(0, 2 ** len(CROSS) * 2, text_rows, 0)
    streams[WORDS].start()
    streams[WORDS + 1].start()
    query_sum = column_sum(r.joined[:, C : 2 * C].astype(full))
    value_sum = column_sum(r.joined[:, 3 * C :].astype(full))
    word_sum = [column_sum(r.joined_words[:, k * C : (k + 1) * C].astype(full)) for k in range(2)]

    def spread_rows(i, values):
        from_left, from_right = side_shifts(values)
        r.shifts[0, i] = from_right.astype(low)
        r.shifts[1, i] = values.astype(low)
        r.shifts[2, i] = from_left.astype(low)

    def conv_back():
        total = jnp.zeros((IMAGE_ROWS * W, C), full)
        for t in range(9):
            dy, dx = t // 3, t % 3
            view = r.shifts[dx, 2 - dy : 2 - dy + IMAGE_ROWS].reshape(IMAGE_ROWS * W, C)
            total = total + dot_last(view, r.conv_w[t * C : (t + 1) * C, :])
        return total

    def conv_grads(kind, own, other, landing):
        for t in range(9):
            dy, dx = t // 3, t % 3
            shifted = r.shifts[
                dx, 1 : IMAGE_ROWS + 1, :, pl.ds(pl.multiple_of(core * (C // 2), C // 2), C // 2)
            ].reshape(IMAGE_ROWS * W, C // 2)
            grad = dot_first(own[dy * W : dy * W + IMAGE_ROWS * W, :], shifted)
            grad = grad + dot_first(
                other[dy * W : dy * W + IMAGE_ROWS * W, :],
                landing[dx].reshape(IMAGE_ROWS * W, C // 2),
            )
            grad = grad.astype(low)
            begin = t * C
            while begin < (t + 1) * C:
                shard, within = divmod(begin, 288)
                stream, offset = divmod(within, 96)
                part, offset = divmod(offset, 48)
                size = min(48 - offset, (t + 1) * C - begin)
                target = r.grads[kind + stream]
                target[
                    shard // 8, (shard // 4) % 2, (shard // 2) % 2, shard % 2, part, offset : offset + size
                ] = grad[begin - t * C : begin - t * C + size]
                begin += size
        for j in range(3):
            streams[kind + j].start()

    for copy in tiles:
        copy.wait()
    band.wait_edges(three_edges)
    means = item_means(r.window.at[0])
    offset_three, slope_three = means[0:1] * vec.scale_three, means[1:2] * vec.scale_three

    def middle_row(i, bias):
        values = r.part_two[i] - offset_three - unit(r.mid[i], norm_three) * slope_three
        r.part_two[i] = values
        values = kept(i, values, vec)
        spread_rows(i, values)
        inside = jnp.where((i > 0) & (i <= IMAGE_ROWS), 1.0, 0.0)
        return bias + inside * column_sum(values.astype(low).astype(full))

    conv_bias_two = lax.fori_loop(0, IMAGE_ROWS + 2, middle_row, jnp.zeros((1, C), full))
    shift_half = r.shifts.at[:, 1 : IMAGE_ROWS + 1, :, half]
    sibling.shifts_two = to_sibling(8, shift_half, r.sib_shifts_two)
    loads.conv_second.wait()
    loads.hidden.wait()
    r.product[...] = conv_back().reshape(IMAGE_ROWS, W, C)
    loads.conv_first = load(8, r.conv_first, r.conv_w)
    stretched = vec.stretch * vec.gain_two * vec.scale_two

    def second_row(i, sums):
        unit_two = unit(r.hid[i + 1], norm_two)
        normed = unit_two * vec.gain_two + vec.bias_two
        grad = r.product[i] * silu_slope_of(normed * vec.stretch + vec.shift)
        r.part_one[i + 1] = grad * stretched
        return sums[0] + column_sum(grad), sums[1] + column_sum(grad * unit_two)

    nothing = (jnp.zeros((1, C), full), jnp.zeros((1, C), full))
    plain, crossed = lax.fori_loop(0, IMAGE_ROWS, second_row, nothing)
    scale_grad = crossed * vec.gain_two + plain * vec.bias_two
    shift_grad = plain
    gain_two, bias_two = crossed * vec.stretch, plain * vec.stretch
    r.tile[1] = sums_tile(bias_two * vec.gain_two, gain_two * vec.gain_two)
    two_edges = band.edges(1, r.part_one.at[1], r.part_one.at[IMAGE_ROWS], r.part_one)
    tiles = band.send_tile(1, r.tile.at[1], r.window.at[1])
    loads.act_two.wait()
    sibling.act2.wait()
    sibling.shifts_two.wait()
    conv_grads(SECOND_CONV, r.act2, r.sib_act2, r.sib_shifts_two)
    for copy in tiles:
        copy.wait()
    band.wait_edges(two_edges)
    means = item_means(r.window.at[1])
    offset_two, slope_two = means[0:1] * vec.scale_two, means[1:2] * vec.scale_two

    def hidden_row(i, bias):
        values = r.part_one[i] - offset_two - unit(r.hid[i], norm_two) * slope_two
        values = kept(i, values, vec)
        spread_rows(i, values)
        inside = jnp.where((i > 0) & (i <= IMAGE_ROWS), 1.0, 0.0)
        return bias + inside * column_sum(values.astype(low).astype(full))

    conv_bias_one = lax.fori_loop(0, IMAGE_ROWS + 2, hidden_row, jnp.zeros((1, C), full))
    sibling.shifts_one = to_sibling(9, shift_half, r.sib_shifts_one)
    for k in (PROJ, QKV, WORDS, WORDS + 1):
        streams[k].advance()
    loads.conv_first.wait()
    loads.image.wait()
    r.product[...] = conv_back().reshape(IMAGE_ROWS, W, C)

    def first_row(i, sums):
        unit_one = unit(r.img[i].astype(full), norm_one)
        normed = unit_one * vec.gain_one + vec.bias_one
        grad = r.product[i] * silu_slope_of(normed)
        r.product[i] = grad
        return sums[0] + column_sum(grad), sums[1] + column_sum(grad * unit_one)

    plain, crossed = lax.fori_loop(0, IMAGE_ROWS, first_row, nothing)
    gain_one, bias_one = crossed, plain
    r.tile[2] = sums_tile(plain * vec.gain_one, crossed * vec.gain_one)
    tiles = band.send_tile(2, r.tile.at[2], r.window.at[2])
    rows = [
        gain_one,
        gain_two,
        gain_three,
        bias_one,
        bias_two,
        bias_three,
        conv_bias_one,
        conv_bias_two,
        query_sum,
        value_sum,
        word_sum[0],
        word_sum[1],
        up_sum,
        jnp.zeros((1, C), full),
        scale_grad,
        shift_grad,
    ]
    for i, values in enumerate(rows):
        r.own_rows[i : i + 1, :] = values
    row_copies = band.send_tile(3, r.own_rows, r.band_rows)
    loads.act_one.wait()
    sibling.act1.wait()
    sibling.shifts_one.wait()
    conv_grads(FIRST_CONV, r.act1, r.sib_act1, r.sib_shifts_one)
    for copy in tiles:
        copy.wait()
    means = item_means(r.window.at[2])
    offset_one, slope_one = means[0:1] * vec.scale_one, means[1:2] * vec.scale_one
    ratio = vec.gain_one * vec.scale_one

    def image_row(i, carry):
        unit_one = unit(r.img[i].astype(full), norm_one)
        values = r.part_two[i + 1] + r.product[i] * ratio - offset_one - unit_one * slope_one
        r.image_grad[i] = values
        return carry

    lax.fori_loop(0, IMAGE_ROWS, image_row, 0)

    for copy in row_copies:
        copy.wait()
    total = jnp.zeros((16, C), full)
    for b in range(SPAN):
        total = total + r.band_rows[b]
    r.half_rows[0:16, :] = total
    for b in range(SPAN):
        r.half_rows[16 + 2 * b : 18 + 2 * b, :] = r.band_rows[b, 14:16, :]
    far_copy = remote(
        r.half_rows, r.far_rows, r.small_send.at[0], r.small_recv.at[0], partner[FAR]
    )
    far_copy.start()
    for k in range(SECOND_CONV, len(STREAMS)):
        streams[k].advance()
    loads.text_weight.wait()

    def caption_columns(n, carry):
        columns = pl.ds(pl.multiple_of(n * C, C), C)
        r.caption_grad[:, columns] = dot_last(r.joined_words[...], r.text_w[columns, :])
        return carry

    lax.fori_loop(0, EMB // C, caption_columns, 0)
    loads.embed_weight = load(13, r.embed_weight, r.text_w)
    far_copy.wait()
    first_half = jnp.where(place[FAR] == 0, r.half_rows[16:32, :], r.far_rows[16:32, :])
    other_half = jnp.where(place[FAR] == 0, r.far_rows[16:32, :], r.half_rows[16:32, :])
    r.group_rows[0:16, :] = r.half_rows[0:16, :] + r.far_rows[0:16, :]
    r.group_rows[16:32, :] = first_half
    r.group_rows[32:48, :] = other_half
    slots = r.slot_of_band.shape[0]
    for k in range(2):
        table = jnp.zeros((slots, C), full)
        for b in range(2 * SPAN):
            values = r.group_rows[16 + 2 * b + k : 17 + 2 * b + k, :]
            table = table + jnp.where(r.slot_of_band[:, b * 128 : b * 128 + 1] > 0.0, values, 0.0)
        r.own_table[slots * k : slots * (k + 1), :] = table
    r.own_table[2 * slots :, :] = r.group_rows[0:16, :]
    group_copy = remote(
        r.own_table,
        r.other_table,
        r.small_send.at[1],
        r.small_recv.at[1],
        partner[GROUP],
    )
    group_copy.start()
    def advance_all():
        for stream in streams:
            if stream.step < LANDINGS + 2:
                stream.advance()

    advance_all()
    loads.embed_weight.wait()
    table = [r.own_table[slots * k : slots * (k + 1), :].astype(low) for k in range(2)]

    def embedding_columns(n, carry):
        columns = pl.ds(pl.multiple_of(n * C, C), C)
        grad = dot_last(table[0], r.text_w[columns, 0:C]) + dot_last(table[1], r.text_w[columns, C:])
        source = r.embedding[:, columns].astype(full)
        r.embedding_grad[:, columns] = grad * silu_slope_of(source)
        return carry

    lax.fori_loop(0, EMB // C, embedding_columns, 0)
    advance_all()
    group_copy.wait()
    share_copy.wait()
    for k in range(2):
        columns = slice(k * C, (k + 1) * C)
        other = r.other_table[slots * k : slots * (k + 1), :].astype(low)
        r.embed_weight_grad[:, columns] = dot_first(r.silu_share[...], table[k]) + dot_first(
            r.other_share[...], other
        )
        r.embed_bias_grad[:, columns] = column_sum(table[k].astype(full)) + column_sum(
            other.astype(full)
        )
    sums = r.own_table[2 * slots :, :] + r.other_table[2 * slots :, :]
    r.norm_gains_grad[...] = sums[0:3]
    r.norm_biases_grad[...] = sums[3:6]
    r.conv_biases_grad[...] = sums[6:8]
    for target, k in ((r.qv_bias_grad, 8), (r.text_bias_grad, 10)):
        target[:, 0:C] = sums[k : k + 1]
        target[:, C:] = sums[k + 1 : k + 2]
    r.proj_bias_grad[...] = sums[12:13]
    for _ in range(LANDINGS):
        advance_all()

    def write(stream, target, first_row):
        rows, columns = STREAMS[stream][:2]
        for side, source in ((group, r.folded[stream]), (1 - group, r.whole[stream])):
            for k in range(2):
                target[
                    pl.ds(pl.multiple_of(first_row + side * rows, rows), rows),
                    k * columns : (k + 1) * columns,
                ] = source[k].astype(full)

    for j in range(3):
        write(FIRST_CONV + j, r.conv_first_grad, j * 96)
        write(SECOND_CONV + j, r.conv_second_grad, j * 96)
    for j in range(2):
        write(WORDS + j, r.text_grad, j * 64)
    write(QKV, r.qkv_grad, 0)
    write(PROJ, r.proj_grad, 0)


def silu_slope_of(source):
    sigma = 1.0 / (1.0 + jnp.exp(-source))
    return sigma * (1.0 + source * (1.0 - sigma))


def back(ident, vectors, slot_of_band, silu_share, embedding, anywhere):
    low, full = jnp.bfloat16, jnp.float32
    pixels = IMAGE_ROWS * W
    slots = slot_of_band.shape[0]
    outs = dict(
        result=((pixels, C), low),
        image_grad=((IMAGE_ROWS, W, C), full),
        caption_grad=((TEXT, EMB), full),
        conv_first_grad=((288, C), full),
        conv_second_grad=((288, C), full),
        qkv_grad=((32, 3 * C), full),
        text_grad=((128, 2 * C), full),
        proj_grad=((32, C), full),
        embedding_grad=(embedding.shape, full),
        embed_weight_grad=((silu_share.shape[1], 2 * C), full),
        norm_gains_grad=((3, C), full),
        norm_biases_grad=((3, C), full),
        conv_biases_grad=((2, C), full),
        embed_bias_grad=((1, 2 * C), full),
        qv_bias_grad=((1, 2 * C), full),
        text_bias_grad=((1, 2 * C), full),
        proj_bias_grad=((1, C), full),
    )
    padded = (IMAGE_ROWS + 2, W, C)
    scratch = dict(
        heads=((HEADS, pixels, 4 * HEAD), low),
        head_words=((HEADS, TEXT, 2 * HEAD), low),
        joined=((pixels, 4 * C), low),
        joined_words=((TEXT, 2 * C), low),
        mid=(padded, full),
        part_two=(padded, full),
        part_one=(padded, full),
        hid=(padded, full),
        product=((IMAGE_ROWS, W, C), full),
        img=((IMAGE_ROWS, W, C), low),
        up=((pixels, C), low),
        act1=((pixels + 2 * W, C), low),
        act2=((pixels + 2 * W, C), low),
        act3=((pixels, C), low),
        cap=((TEXT, EMB), low),
        conv_w=((9 * C, C), low),
        qkv_w=((C, 3 * C), low),
        proj_w=((C, C), low),
        text_w=((EMB, 2 * C), low),
        sib_up=((pixels, C // 2), low),
        sib_act1=((pixels + 2 * W, C), low),
        sib_act2=((pixels + 2 * W, C), low),
        sib_act3=((pixels, C), low),
        sib_cap=((TEXT, EMB), low),
        sib_attended=((pixels, C), low),
        sib_qkv=((pixels, 3 * C // 2), low),
        sib_words=((TEXT, C), low),
        sib_shifts_one=((3, IMAGE_ROWS, W, C // 2), low),
        sib_shifts_two=((3, IMAGE_ROWS, W, C // 2), low),
        shifts=((3,) + padded, low),
        blocks=((C, C), low),
        tile=((3, 8, C), full),
        window=((3, SPAN, 8, C), full),
        own_rows=((16, C), full),
        band_rows=((SPAN, 16, C), full),
        half_rows=((32, C), full),
        far_rows=((32, C), full),
        group_rows=((48, C), full),
        own_table=((2 * slots + 16, C), full),
        other_table=((2 * slots + 16, C), full),
        other_share=(silu_share.shape, low),
    )
    scratch.update(grads=[((2,) * 5 + s[:2], low) for s in STREAMS])
    scratch.update(landings=[((2,) * (4 - i) + s[:2], low) for s in STREAMS for i in range(LANDINGS)])
    scratch.update(folded=[((2,) + s[:2], low) for s in STREAMS])
    scratch.update(whole=[((2,) + s[:2], low) for s in STREAMS])
    semaphores = dict(
        swap_send=(2, SPAN),
        swap_recv=(2, SPAN),
        load_sem=(14,),
        sib_send=(10,),
        sib_recv=(10,),
        edge_send=(2, 2),
        edge_recv=(2, 2),
        tile_send=(4, SPAN),
        tile_recv=(4, SPAN),
        fold_send=(len(STREAMS), LANDINGS + 2),
        fold_recv=(len(STREAMS), LANDINGS + 2),
        small_send=(3,),
        small_recv=(3,),
    )
    inputs = dict(
        vectors=vectors, slot_of_band=slot_of_band, silu_share=silu_share, embedding=embedding
    )
    return call_named(back_kernel, ident, (), inputs, anywhere, outs, scratch, semaphores)


def front_kernel(names, *refs):
    low, full = jnp.bfloat16, jnp.float32
    r = grouped(names, refs)
    band = Band(r)
    band.meet()
    loads = types.SimpleNamespace()

    def load(k, source, target):
        copy = pltpu.make_async_copy(source, target, r.load_sem.at[k])
        copy.start()
        return copy

    loads.image = load(0, r.image, r.img.at[1 : IMAGE_ROWS + 1])
    image_edges = band.edges(0, r.image.at[0], r.image.at[IMAGE_ROWS - 1], r.img)
    loads.conv_first = load(1, r.conv_first, r.first_w)
    loads.embed_weight = load(2, r.embed_weight, r.embed_w)
    loads.upstream = load(3, r.upstream, r.up)
    loads.proj_weight = load(4, r.proj_weight, r.proj_w)
    loads.conv_second = load(5, r.conv_second, r.second_w)
    loads.caption = load(6, r.caption, r.cap)
    loads.text_weight = load(7, r.text_weight, r.text_w)
    loads.qkv_weight = load(8, r.qkv_weight, r.qkv_w)

    mine = r.items[band.row]
    same = [(r.items[band.base + b] == mine).astype(full) for b in range(SPAN)]
    masks = [jnp.full((1, C), m, full) for m in same]
    bands = masks[0]
    for m in masks[1:]:
        bands = bands + m
    per_item = 1.0 / (bands * (IMAGE_ROWS * W * (C // NORM_GROUPS)))
    before = jnp.where(band.has_above, r.items[jnp.maximum(band.row - 1, 0)], -1)
    after = jnp.where(
        band.has_below, r.items[jnp.minimum(band.row + 1, r.items.shape[0] - 1)], -1
    )
    found = types.SimpleNamespace(
        gain_one=r.norm_gains[0:1, :],
        gain_two=r.norm_gains[1:2, :],
        gain_three=r.norm_gains[2:3, :],
        bias_one=r.norm_biases[0:1, :],
        bias_two=r.norm_biases[1:2, :],
        bias_three=r.norm_biases[2:3, :],
        proj_bias=r.proj_bias[...],
        keep_above=jnp.full((1, C), (before == mine).astype(full)),
        keep_below=jnp.full((1, C), (after == mine).astype(full)),
        per_item=per_item,
    )
    for target in (r.img, r.hidden, r.middle):
        band.zero_edges(target)
    nothing = (jnp.zeros((1, C), full), jnp.zeros((1, C), full))

    def norm_of(k):
        means = band.item_means(r.window.at[k], masks, per_item)
        return means[0:1], lax.rsqrt(means[1:2] - means[0:1] * means[0:1] + epsilon)

    loads.image.wait()

    def image_sums(i, sums):
        values = r.img[i + 1].astype(full)
        return sums[0] + column_sum(values), sums[1] + column_sum(values * values)

    r.tile[0] = sums_tile(*lax.fori_loop(0, IMAGE_ROWS, image_sums, nothing))
    tiles = band.send_tile(0, r.tile.at[0], r.window.at[0])

    band.fill_blocks()
    slot = lax.broadcasted_iota(jnp.int32, r.embedding.shape, 0)
    chosen = jnp.where(slot == mine, r.embedding[...].astype(full), 0.0)
    chosen = jnp.sum(chosen, axis=0, keepdims=True)
    chosen = chosen / (1.0 + jnp.exp(-chosen))
    chosen = jnp.broadcast_to(chosen, (16, EMB)).astype(low)
    loads.embed_weight.wait()
    modulation = dot(chosen, r.embed_w[...])[0:1] + r.embed_bias[...]
    found.stretch = 1.0 + modulation[:, 0:C]
    found.shift = modulation[:, C:]

    def spread_rows(i, values, target):
        values = kept(i, values, found)
        from_left, from_right = side_shifts(values)
        r.shifts[0, i] = from_left.astype(low)
        r.shifts[1, i] = values.astype(low)
        r.shifts[2, i] = from_right.astype(low)
        target[pl.ds(pl.multiple_of(i * W, W), W), :] = values.astype(low)

    def conv(weight):
        total = jnp.zeros((IMAGE_ROWS * W, C), full)
        for t in range(9):
            view = r.shifts[t % 3, t // 3 : t // 3 + IMAGE_ROWS].reshape(IMAGE_ROWS * W, C)
            total = total + dot(view, weight[t * C : (t + 1) * C, :])
        return total

    for copy in tiles:
        copy.wait()
    band.wait_edges(image_edges)
    found.mean_one, found.scale_one = norm_of(0)

    def first_row(i, carry):
        unit = (r.img[i].astype(full) - found.mean_one) * found.scale_one
        normed = unit * found.gain_one + found.bias_one
        spread_rows(i, normed / (1.0 + jnp.exp(-normed)), r.act_one)
        return carry

    lax.fori_loop(0, IMAGE_ROWS + 2, first_row, 0)
    loads.conv_first.wait()
    total = conv(r.first_w) + r.conv_biases[0:1, :]
    r.hidden[1 : IMAGE_ROWS + 1] = total.reshape(IMAGE_ROWS, W, C)
    hidden_edges = band.edges(1, r.hidden.at[1], r.hidden.at[IMAGE_ROWS], r.hidden)
    r.tile[1] = sums_tile(column_sum(total), column_sum(total * total))
    tiles = band.send_tile(1, r.tile.at[1], r.window.at[1])

    loads.caption.wait()
    loads.text_weight.wait()
    words = (dot(r.cap[...], r.text_w[...]) + r.text_bias[...]).astype(low)
    for h in range(HEADS):
        parts = [words[:, k * C + h * HEAD : k * C + (h + 1) * HEAD] for k in range(2)]
        r.words[h] = jnp.concatenate(parts, axis=1)
    swaps = band.swap(0, r.words, r.head_words)
    r.head_words[band.lane] = r.words[band.lane]
    for copy in tiles:
        copy.wait()
    band.wait_edges(hidden_edges)
    found.mean_two, found.scale_two = norm_of(1)

    def second_row(i, carry):
        unit = (r.hidden[i] - found.mean_two) * found.scale_two
        normed = unit * found.gain_two + found.bias_two
        shifted = normed * found.stretch + found.shift
        spread_rows(i, shifted / (1.0 + jnp.exp(-shifted)), r.act_two)
        return carry

    lax.fori_loop(0, IMAGE_ROWS + 2, second_row, 0)
    loads.conv_second.wait()
    total = conv(r.second_w) + r.conv_biases[1:2, :]
    total = total + r.img[1 : IMAGE_ROWS + 1].astype(full).reshape(IMAGE_ROWS * W, C)
    r.middle[1 : IMAGE_ROWS + 1] = total.reshape(IMAGE_ROWS, W, C)
    r.tile[2] = sums_tile(column_sum(total), column_sum(total * total))
    tiles = band.send_tile(2, r.tile.at[2], r.window.at[2])
    middle_edges = band.edges(2, r.middle.at[1], r.middle.at[IMAGE_ROWS], r.middle)

    loads.upstream.wait()
    loads.proj_weight.wait()
    attended_grad = dot_last(r.up[...], r.proj_w[...]).astype(low)
    loads.qkv_weight.wait()
    for h in range(HEADS):
        r.pieces[h, :, 3 * HEAD :] = attended_grad[:, h * HEAD : (h + 1) * HEAD]
    for copy in tiles:
        copy.wait()
    found.mean_three, found.scale_three = norm_of(2)
    for i in range(2):
        middle = r.middle[1 + 4 * i : 5 + 4 * i].reshape(4 * W, C)
        unit = (middle - found.mean_three) * found.scale_three
        block = slice(i * 4 * W, (i + 1) * 4 * W)
        act = (unit * found.gain_three + found.bias_three).astype(low)
        r.act_three[block, :] = act
        projected = dot(act, r.qkv_w[...])
        queries = (projected[:, 0:C] + r.qv_bias[:, 0:C]).astype(low)
        keys = projected[:, C : 2 * C].astype(low)
        values = (projected[:, 2 * C :] + r.qv_bias[:, C:]).astype(low)
        for h in range(HEADS):
            head = slice(h * HEAD, (h + 1) * HEAD)
            r.pieces[h, block, 0 : 2 * HEAD] = jnp.concatenate([queries[:, head], keys[:, head]], axis=1)
            r.pieces[h, block, 2 * HEAD : 3 * HEAD] = values[:, head]
    swaps = swaps + band.swap(1, r.pieces, r.heads)
    r.heads[band.lane] = r.pieces[band.lane]
    fields = [getattr(found, name) for name in Vectors._fields]
    for i, values in enumerate(fields):
        r.vectors[i : i + 1, :] = values
    r.vectors[len(fields) : VECTOR_ROWS, :] = jnp.zeros((VECTOR_ROWS - len(fields), C), full)
    for b in range(SPAN):
        r.vectors[VECTOR_ROWS + b : VECTOR_ROWS + b + 1, :] = masks[b]
    band.wait_edges(middle_edges)
    for copy in swaps:
        copy.wait()


def front(ident, items, inputs, anywhere):
    low, full = jnp.bfloat16, jnp.float32
    pixels = IMAGE_ROWS * W
    padded = (IMAGE_ROWS + 2, W, C)
    outs = dict(
        heads=((HEADS, pixels, 4 * HEAD), low),
        head_words=((HEADS, TEXT, 2 * HEAD), low),
        act_one=((pixels + 2 * W, C), low),
        act_two=((pixels + 2 * W, C), low),
        act_three=((pixels, C), low),
        hidden=(padded, full),
        middle=(padded, full),
        vectors=((VECTOR_ROWS + SPAN, C), full),
    )
    scratch = dict(
        img=(padded, low),
        up=((pixels, C), low),
        cap=((TEXT, EMB), low),
        first_w=((9 * C, C), low),
        second_w=((9 * C, C), low),
        embed_w=((EMB, 2 * C), low),
        text_w=((EMB, 2 * C), low),
        qkv_w=((C, 3 * C), low),
        proj_w=((C, C), low),
        shifts=((3,) + padded, low),
        blocks=((C, C), low),
        tile=((3, 8, C), full),
        window=((3, SPAN, 8, C), full),
        words=((HEADS, TEXT, 2 * HEAD), low),
        pieces=((HEADS, pixels, 4 * HEAD), low),
    )
    semaphores = dict(
        load_sem=(9,),
        edge_send=(3, 2),
        edge_recv=(3, 2),
        tile_send=(3, SPAN),
        tile_recv=(3, SPAN),
        swap_send=(2, SPAN),
        swap_recv=(2, SPAN),
    )
    return call_named(
        front_kernel, ident, dict(items=items), inputs, anywhere, outs, scratch, semaphores
    )


def hand_over_kernel(count, *refs):
    sources, targets, sem = refs[:count], refs[count : 2 * count], refs[2 * count]
    copies = [
        pltpu.make_async_copy(source, target, sem.at[k])
        for k, (source, target) in enumerate(zip(sources, targets))
    ]
    for copy in copies:
        copy.start()
    for copy in copies:
        copy.wait()


def hand_over(arrays):
    anywhere = pl.BlockSpec(memory_space=pl.ANY)
    return pl.pallas_call(
        functools.partial(hand_over_kernel, len(arrays)),
        out_shape=tuple(jax.ShapeDtypeStruct(a.shape, a.dtype) for a in arrays),
        in_specs=[pl.BlockSpec(memory_space=pltpu.VMEM)] * len(arrays),
        out_specs=(anywhere,) * len(arrays),
        scratch_shapes=[pltpu.SemaphoreType.DMA((len(arrays),))],
        name=hand_over.__name__,
    )(*arrays)


def blocks_of(rows):
    return rows.reshape(rows.shape[0], NORM_GROUPS, -1)


def spread(values):
    return jnp.repeat(values, C // NORM_GROUPS)


def in_halves(
    image,
    embedding,
    caption,
    item_of_band,
    out_grad,
    norm_gains,
    norm_biases,
    conv_first,
    conv_second,
    conv_biases,
    embed_weight,
    embed_bias,
    qkv_weight,
    qv_bias,
    text_weight,
    text_bias,
    proj_weight,
    proj_bias,
):
    low = jnp.bfloat16
    pixels = image.shape[1]
    position = lax.axis_index(ROWS)
    items = item_of_band[0]
    slots = items.shape[0]
    by_row = (-1, W, C)
    ahead = front(
        0,
        items,
        dict(
            embedding=embedding[0],
            norm_gains=norm_gains,
            norm_biases=norm_biases,
            conv_biases=conv_biases,
            embed_bias=embed_bias[None],
            qv_bias=qv_bias[None],
            text_bias=text_bias[None],
            proj_bias=proj_bias[None],
        ),
        dict(
            image=image.reshape(by_row),
            conv_first=conv_first,
            embed_weight=embed_weight,
            upstream=out_grad[0],
            proj_weight=proj_weight,
            conv_second=conv_second,
            caption=caption[0, 0],
            text_weight=text_weight,
            qkv_weight=qkv_weight,
        ),
    )
    pieces, words = one_head(items, ahead.heads, ahead.head_words)
    slot_of_band = (jnp.arange(slots)[:, None] == items[None, :]).astype(jnp.float32)
    row_share = EMB // lax.axis_size(ROWS)
    share = lax.dynamic_slice_in_dim(embedding[0], position * row_share, row_share, 1)
    silu_share = jax.nn.silu(share.astype(jnp.float32)).astype(low)
    out = back(
        1,
        ahead.vectors,
        jnp.repeat(slot_of_band, 128, axis=1),
        silu_share,
        embedding[0],
        dict(
            pieces=pieces,
            words=words,
            middle=ahead.middle,
            qkv_weight=qkv_weight,
            proj_weight=proj_weight,
            upstream=out_grad[0],
            act_three=ahead.act_three,
            caption=caption[0, 0],
            conv_second=conv_second,
            conv_first=conv_first,
            hidden=ahead.hidden,
            act_two=ahead.act_two,
            act_one=ahead.act_one,
            image=image.reshape(by_row),
            text_weight=text_weight,
            embed_weight=embed_weight,
        ),
    )
    out = types.SimpleNamespace(**dict(zip(vars(out), hand_over(list(vars(out).values())))))
    return (
        out.result[None],
        out.image_grad.reshape(1, pixels, C),
        out.embedding_grad[None],
        out.caption_grad[None, None],
        out.norm_gains_grad,
        out.norm_biases_grad,
        out.conv_first_grad,
        out.conv_second_grad,
        out.conv_biases_grad,
        out.embed_weight_grad,
        out.embed_bias_grad.reshape(-1),
        out.qkv_grad,
        out.qv_bias_grad.reshape(-1),
        out.text_grad,
        out.text_bias_grad.reshape(-1),
        out.proj_grad,
        out.proj_bias_grad.reshape(-1),
    )


def shards(
    image,
    embedding,
    caption,
    item_of_band,
    out_grad,
    norm_gains,
    norm_biases,
    conv_first,
    conv_second,
    conv_biases,
    embed_weight,
    embed_bias,
    qkv_weight,
    qv_bias,
    text_weight,
    text_bias,
    proj_weight,
    proj_bias,
):
    low = jnp.bfloat16
    full = jnp.float32
    pixels = image.shape[1]
    band_items = item_of_band[0]
    slots = band_items.shape[0]
    if slots == 2 * SPAN and lax.axis_size(ITEMS) == 2 and HEADS == SPAN:
        return in_halves(
            image,
            embedding,
            caption,
            item_of_band,
            out_grad,
            norm_gains,
            norm_biases,
            conv_first,
            conv_second,
            conv_biases,
            embed_weight,
            embed_bias,
            qkv_weight,
            qv_bias,
            text_weight,
            text_bias,
            proj_weight,
            proj_bias,
        )
    position = lax.axis_index(ROWS)
    my_item = band_items[position]
    slot_hot = (jnp.arange(slots) == my_item).astype(full)
    item_count = jnp.sum((band_items == my_item).astype(full)) * pixels * (C // NORM_GROUPS)
    reach = position + jnp.arange(-REACH, REACH + 1)
    near = (reach >= 0) & (reach < slots)
    near = near & (band_items[jnp.clip(reach, 0, slots - 1)] == my_item)
    keep = jnp.concatenate(
        [
            jnp.full((W, 1), near[REACH - 1]),
            jnp.full((pixels, 1), True),
            jnp.full((W, 1), near[REACH + 1]),
        ]
    )
    own_lead = jnp.logical_not(near[REACH - 1])

    def totals(ident, first, second, edges=None):
        sums = jnp.stack([jnp.sum(blocks_of(first), axis=(0, 2)), jnp.sum(blocks_of(second), axis=(0, 2))])
        tile = jnp.pad(sums, ((0, 6), (0, 128 - NORM_GROUPS)))
        if edges is not None:
            outcome = exchange(ident, slots, tile, (edges[:W], edges[-W:]))
        else:
            outcome = exchange(ident, slots, tile)
        summed = jnp.sum(jnp.where(near[:, None, None], outcome[0], 0.0), axis=0)
        summed = summed[:2, :NORM_GROUPS] / item_count
        return summed, outcome[1:]

    def stats(summed):
        scales = lax.rsqrt(summed[1] - summed[0] * summed[0] + epsilon)
        return spread(summed[0]), spread(scales)

    inputs = image[0].astype(full)
    summed, (above, below) = totals(0, inputs, inputs * inputs, image[0])
    means_one, scales_one = stats(summed)
    padded = jnp.concatenate([above, image[0], below]).astype(full)
    unit_padded = (padded - means_one) * scales_one
    normed_padded = unit_padded * norm_gains[0] + norm_biases[0]
    act_one_padded = jnp.where(keep, jax.nn.silu(normed_padded), 0.0).astype(low)
    unit_one = unit_padded[W:-W]
    normed_one = normed_padded[W:-W]
    taps_one = jnp.concatenate(taps_of(act_one_padded, False), axis=1)
    hidden_one = dot(taps_one, conv_first) + conv_biases[0]
    embed_silu = jax.nn.silu(embedding[0].astype(full)).astype(low)
    my_silu = dot(slot_hot.astype(low)[None], embed_silu).astype(low)
    modulation = dot(my_silu, embed_weight)[0] + embed_bias
    scale_part = modulation[:C]
    shift_part = modulation[C:]
    summed, (above, below) = totals(1, hidden_one, hidden_one * hidden_one, hidden_one)
    means_two, scales_two = stats(summed)
    hidden_padded = jnp.concatenate([above, hidden_one, below])
    unit_padded = (hidden_padded - means_two) * scales_two
    normed_padded = unit_padded * norm_gains[1] + norm_biases[1]
    shifted_padded = normed_padded * (1.0 + scale_part) + shift_part
    act_two_padded = jnp.where(keep, jax.nn.silu(shifted_padded), 0.0).astype(low)
    unit_two = unit_padded[W:-W]
    normed_two = normed_padded[W:-W]
    shifted = shifted_padded[W:-W]
    taps_two = jnp.concatenate(taps_of(act_two_padded, False), axis=1)
    middle = inputs + dot(taps_two, conv_second) + conv_biases[1]
    summed, _ = totals(2, middle, middle * middle)
    means_three, scales_three = stats(summed)
    unit_three = (middle - means_three) * scales_three
    act_three = (unit_three * norm_gains[2] + norm_biases[2]).astype(low)
    projected = dot(act_three, qkv_weight)
    queries = (projected[:, :C] + qv_bias[:C]).astype(low)
    keys_values = jnp.concatenate(
        [projected[:, C : 2 * C], projected[:, 2 * C :] + qv_bias[C:]], axis=1
    ).astype(low)
    captions = caption[0, 0]
    text_kv = lax.cond(
        own_lead,
        lambda: (dot(captions, text_weight) + text_bias).astype(low),
        lambda: jnp.zeros((TEXT, 2 * C), low),
    )
    upstream = out_grad[0]
    upstream_float = upstream.astype(full)
    attended_grad = dot_last(upstream, proj_weight).astype(low)
    group = lax.axis_index(ITEMS)
    groups = lax.axis_size(ITEMS)
    attended_low, query_low, key_value_low, text_low = attention_by_band(
        band_items, position, queries, keys_values, text_kv, attended_grad
    )
    result = middle + dot(attended_low, proj_weight) + proj_bias
    proj_weight_grad = dot_first(attended_low, upstream)
    proj_bias_grad = jnp.sum(upstream_float, axis=0)
    qkv_grad = jnp.concatenate([query_low, key_value_low], axis=1)
    qkv_weight_grad = dot_first(act_three, qkv_grad)
    qv_bias_grad = jnp.sum(
        jnp.concatenate([query_low, key_value_low[:, C:]], axis=1).astype(full), axis=0
    )
    text_weight_grad = dot_first(captions, text_low)
    text_bias_grad = jnp.sum(text_low.astype(full), axis=0)
    caption_grad = dot_last(text_low, text_weight)[None, None]
    three_grad = dot_last(qkv_grad, qkv_weight)
    gain_three = jnp.sum(three_grad * unit_three, axis=0)
    bias_three = jnp.sum(three_grad, axis=0)

    def conv_back(padded, weight):
        views = jnp.stack(taps_of(padded, True))
        return jnp.einsum(
            "tpd,tcd->pc", views, weight.reshape(9, C, C), preferred_element_type=full
        )

    def norm_back(ident, grad_unit, unit_value, scales, base, with_edges=True):
        scaled = base + grad_unit * scales
        edges = jnp.concatenate([scaled, unit_value], axis=1) if with_edges else None
        summed, around = totals(ident, grad_unit, grad_unit * unit_value, edges)
        mean_grad, mean_cross = spread(summed[0]) * scales, spread(summed[1]) * scales
        if not with_edges:
            return scaled - mean_grad - unit_value * mean_cross
        both = jnp.concatenate([around[0], edges, around[1]])
        return both[:, :C] - mean_grad - both[:, C:] * mean_cross

    middle_padded = norm_back(3, three_grad * norm_gains[2], unit_three, scales_three, upstream_float)
    middle_grad = middle_padded[W:-W]
    low_padded = jnp.where(keep, middle_padded, 0.0).astype(low)
    hidden_two_low = low_padded[W:-W]
    conv_bias_two = jnp.sum(hidden_two_low.astype(full), axis=0)
    conv_second_grad = dot_first(taps_two, hidden_two_low)
    act_two_grad = conv_back(low_padded, conv_second)
    shifted_grad = act_two_grad * silu_slope(shifted)
    modulation_grad = jnp.concatenate(
        [jnp.sum(shifted_grad * normed_two, axis=0), jnp.sum(shifted_grad, axis=0)]
    )
    normed_two_grad = shifted_grad * (1.0 + scale_part)
    gain_two = jnp.sum(normed_two_grad * unit_two, axis=0)
    bias_two = jnp.sum(normed_two_grad, axis=0)
    hidden_back = norm_back(4, normed_two_grad * norm_gains[1], unit_two, scales_two, 0.0)
    low_padded = jnp.where(keep, hidden_back, 0.0).astype(low)
    hidden_one_low = low_padded[W:-W]
    conv_bias_one = jnp.sum(hidden_one_low.astype(full), axis=0)
    conv_first_grad = dot_first(taps_one, hidden_one_low)
    act_one_grad = conv_back(low_padded, conv_first)
    normed_one_grad = act_one_grad * silu_slope(normed_one)
    gain_one = jnp.sum(normed_one_grad * unit_one, axis=0)
    bias_one = jnp.sum(normed_one_grad, axis=0)
    image_grad = norm_back(
        5, normed_one_grad * norm_gains[0], unit_one, scales_one, middle_grad, False
    )
    group_hot = (jnp.arange(groups) == group).astype(full)
    tables = group_hot[:, None, None] * slot_hot[None, :, None] * modulation_grad
    vectors = jnp.concatenate(
        [
            gain_one,
            gain_two,
            gain_three,
            bias_one,
            bias_two,
            bias_three,
            conv_bias_one,
            conv_bias_two,
            qv_bias_grad,
            text_bias_grad,
            proj_bias_grad,
        ]
    )
    small = jnp.concatenate([tables.reshape(-1, C), vectors.reshape(-1, C)])
    row_share = EMB // lax.axis_size(ROWS)
    silu_share = lax.dynamic_slice_in_dim(embed_silu, position * row_share, row_share, 1)
    grads = (conv_first_grad, conv_second_grad, qkv_weight_grad, text_weight_grad, proj_weight_grad)
    grads = [g.astype(low) for g in grads]
    small = lax.psum(small.astype(low), (ROWS, ITEMS)).astype(full)
    tables_sum = small[: groups * slots * 2].reshape(groups, slots, 2 * C).astype(low)
    part = dot_first(silu_share, jnp.take(tables_sum, group, axis=0)).astype(low)
    matrices = [lax.psum_scatter(g, ROWS, scatter_dimension=0, tiled=True) for g in grads]
    *matrices, embed_weight_grad = [
        lax.psum(m, ITEMS).astype(full) for m in matrices + [part]
    ]
    vectors_sum = small[groups * slots * 2 :]
    modulation_low = jnp.take(tables_sum, group, axis=0)
    embed_bias_grad = jnp.sum(tables_sum.astype(full), axis=(0, 1))
    embedding_grad = dot_last(modulation_low, embed_weight) * silu_slope(embedding[0].astype(full))
    return (
        result.astype(low)[None],
        image_grad[None],
        embedding_grad[None],
        caption_grad,
        vectors_sum[0:3],
        vectors_sum[3:6],
        matrices[0],
        matrices[1],
        vectors_sum[6:8],
        embed_weight_grad,
        embed_bias_grad,
        matrices[2],
        vectors_sum[8:10].reshape(-1),
        matrices[3],
        vectors_sum[10:12].reshape(-1),
        matrices[4],
        vectors_sum[12],
    )


def solution(mesh):
    in_specs = (
        P(ITEMS, ROWS, None),
        P(ITEMS, None, None),
        P(ITEMS, ROWS, None, None),
        P(ITEMS, None),
        P(ITEMS, ROWS, None),
        P(),
        P(),
        P(),
        P(),
        P(),
        P(),
        P(),
        P(),
        P(),
        P(),
        P(),
        P(),
        P(),
    )
    out_specs = (
        P(ITEMS, ROWS, None),
        P(ITEMS, ROWS, None),
        P(ITEMS, None, None),
        P(ITEMS, ROWS, None, None),
        P(),
        P(),
        P(ROWS, None),
        P(ROWS, None),
        P(),
        P(ROWS, None),
        P(),
        P(ROWS, None),
        P(),
        P(ROWS, None),
        P(),
        P(ROWS, None),
        P(),
    )
    return jax.shard_map(shards, mesh=mesh, in_specs=in_specs, out_specs=out_specs, check_vma=False)
```

```python
import functools
import types
import typing

import jax
import jax.numpy as jnp
from jax import lax
from jax.experimental import pallas as pl
from jax.experimental.pallas import tpu as pltpu
from jax.sharding import PartitionSpec as P

C = 512
HEADS = 8
HEAD = 64
EMB = 2048
TEXT = 128
NORM_GROUPS = 32
W = 64
SPAN = 8
ROWS, ITEMS = "rows", "items"


epsilon = 1e-05


def from_behind(array, axis, by):
    length = lax.axis_size(axis)
    pairs = [(i, i + by) for i in range(length) if 0 <= i + by < length]
    return lax.ppermute(array, axis, pairs)


def as_sent(array):
    return jax.tree.map(lambda a: a.astype(jnp.bfloat16) if a.dtype == jnp.float32 else a, array)


def keep_state(state):
    return state


def silu_slope(source):
    sigma = jax.nn.sigmoid(source)
    return sigma * (1.0 + source * (1.0 - sigma))


def dot_first(left_side, right_side):
    return lax.dot_general(
        left_side, right_side, (((0,), (0,)), ((), ())), preferred_element_type=jnp.float32
    )


def dot_last(left_side, right_side):
    return lax.dot_general(
        left_side, right_side, (((1,), (1,)), ((), ())), preferred_element_type=jnp.float32
    )


def head_split(source):
    return source.reshape(source.shape[0], HEADS, HEAD)


def piece_scores(query_heads, key_piece, allowed):
    key_heads = head_split(key_piece[:, :C])
    scores = jnp.einsum(
        "qhd,khd->hqk", query_heads, key_heads, preferred_element_type=jnp.float32
    ) * HEAD ** (-0.5)
    return jnp.where(allowed[None, None, :], scores, -jnp.inf)


def piece_grads(query_heads, grad_heads, log_total, row_dots, key_piece, allowed):
    scores = piece_scores(query_heads, key_piece, allowed)
    weights = jnp.exp(scores - log_total[:, :, None])
    value_heads = head_split(key_piece[:, C:])
    weight_grad = jnp.einsum(
        "qhd,khd->hqk", grad_heads, value_heads, preferred_element_type=jnp.float32
    )
    score_grad = (weights * (weight_grad - row_dots[:, :, None])).astype(jnp.bfloat16)
    outcome = []
    key_heads = head_split(key_piece[:, :C])
    query_grad = jnp.einsum(
        "hqk,khd->qhd", score_grad, key_heads, preferred_element_type=jnp.float32
    ) * HEAD ** (-0.5)
    outcome.append(query_grad.reshape(query_grad.shape[0], C))
    key_grad = jnp.einsum(
        "hqk,qhd->khd", score_grad, query_heads, preferred_element_type=jnp.float32
    ) * HEAD ** (-0.5)
    value_grad = jnp.einsum(
        "hqk,qhd->khd", weights.astype(jnp.bfloat16), grad_heads, preferred_element_type=jnp.float32
    )
    outcome.append(jnp.concatenate([key_grad.reshape(-1, C), value_grad.reshape(-1, C)], axis=1))
    return tuple(outcome)


def source_masks(band_items, source, my_item, pixels):
    slots = band_items.shape[0]
    inside = (source >= 0) & (source < slots)
    clipped = jnp.clip(source, 0, slots - 1)
    source_item = band_items[clipped]
    before_item = band_items[jnp.maximum(clipped - 1, 0)]
    same_item = inside & (source_item == my_item)
    leading = same_item & ((clipped == 0) | (before_item != source_item))
    allowed = jnp.concatenate(
        [jnp.broadcast_to(same_item, (pixels,)), jnp.broadcast_to(leading, (TEXT,))]
    )
    return (allowed, same_item)


REACH = SPAN - 1
LOG2E = 1.4426950408889634
FAR_ABOVE = 1e30
PIX = 512


def dot(left, right):
    return jnp.dot(left, right, preferred_element_type=jnp.float32)


def reach_of(here, slots):
    first = here < SPAN
    low = jnp.maximum(jnp.where(first, 0, SPAN), here - REACH)
    high = jnp.minimum(jnp.where(first, SPAN - 1, slots - 1), here + REACH)
    return low, high


def exchange_kernel(slots, with_edges, *refs):
    if with_edges:
        tile, top, bottom, window, above, below, send_sem, recv_sem, edge_send, edge_recv = refs
    else:
        tile, window, send_sem, recv_sem = refs
    here = lax.axis_index(ROWS)
    low, high = reach_of(here, slots)
    offsets = [o for o in range(-REACH, REACH + 1) if o != 0]

    def reached(offset):
        return (here + offset >= low) & (here + offset <= high)

    barrier = pltpu.get_barrier_semaphore()
    for o in offsets:

        @pl.when(reached(o))
        def _(o=o):
            pl.semaphore_signal(barrier, 1, device_id={ROWS: here + o})

    pl.semaphore_wait(barrier, high - low)

    def edge_copy(o):
        source, target, k = (top, below, 0) if o < 0 else (bottom, above, 1)
        return pltpu.make_async_remote_copy(
            source, target, edge_send.at[k], edge_recv.at[k], device_id={ROWS: here + o}
        )

    def tile_copy(o):
        return pltpu.make_async_remote_copy(
            tile,
            window.at[REACH - o],
            send_sem.at[REACH - o],
            recv_sem.at[REACH - o],
            device_id={ROWS: here + o},
        )

    if with_edges:
        for o in (-1, 1):

            @pl.when(reached(o))
            def _(o=o):
                edge_copy(o).start()

    for o in offsets:

        @pl.when(reached(o))
        def _(o=o):
            tile_copy(o).start()

        @pl.when(jnp.logical_not(reached(-o)))
        def _(o=o):
            window[REACH - o] = jnp.zeros_like(tile)

    window[REACH] = tile[...]
    if with_edges:

        @pl.when(jnp.logical_not(reached(-1)))
        def _():
            above[...] = jnp.zeros_like(above)

        @pl.when(jnp.logical_not(reached(1)))
        def _():
            below[...] = jnp.zeros_like(below)

    for o in offsets:

        @pl.when(reached(o))
        def _(o=o):
            tile_copy(o).wait_send()

        @pl.when(reached(-o))
        def _(o=o):
            tile_copy(o).wait_recv()

    if with_edges:
        for o in (-1, 1):

            @pl.when(reached(o))
            def _(o=o):
                edge_copy(o).wait_send()

            @pl.when(reached(-o))
            def _(o=o):
                edge_copy(o).wait_recv()


def exchange(ident, slots, tile, edges=None):
    vmem = pl.BlockSpec(memory_space=pltpu.VMEM)
    shapes = [jax.ShapeDtypeStruct((2 * REACH + 1,) + tile.shape, tile.dtype)]
    scratch = [pltpu.SemaphoreType.DMA((2 * REACH + 1,))] * 2
    operands = [tile]
    if edges is not None:
        shapes += [jax.ShapeDtypeStruct(e.shape, e.dtype) for e in edges]
        scratch += [pltpu.SemaphoreType.DMA((2,))] * 2
        operands += list(edges)
    return pl.pallas_call(
        functools.partial(exchange_kernel, slots, edges is not None),
        out_shape=tuple(shapes),
        in_specs=[vmem] * len(operands),
        out_specs=(vmem,) * len(shapes),
        scratch_shapes=scratch,
        compiler_params=pltpu.CompilerParams(collective_id=ident, has_side_effects=True),
        name=f"exchange_{ident}",
    )(*operands)


def attention_by_band(band_items, position, queries, keys_values, text_kv, attended_grad):
    my_item = band_items[position]
    pixels = queries.shape[0]
    own_allowed, own_same = source_masks(band_items, position, my_item, pixels)
    packed = jnp.concatenate([keys_values, text_kv], axis=0)
    pieces = [(0, packed, own_allowed, own_same)]
    for distance in range(1, SPAN):
        for offset in (distance, -distance):
            arrived = from_behind(packed, ROWS, offset)
            allowed, same_item = source_masks(band_items, position - offset, my_item, pixels)
            pieces.append((offset, arrived, allowed, same_item))
    query_heads = head_split(queries)
    row_top = jnp.full((HEADS, pixels), -jnp.inf, jnp.float32)
    weight_sum = jnp.zeros((HEADS, pixels), jnp.float32)
    for offset, key_piece, allowed, same_item in pieces:

        def gather_scores(state, key_piece=key_piece, allowed=allowed):
            top_old, sum_old = state
            scores = piece_scores(query_heads, key_piece, allowed)
            top_new = jnp.maximum(top_old, jnp.max(scores, axis=2))
            sum_new = sum_old * jnp.exp(top_old - top_new) + jnp.sum(
                jnp.exp(scores - top_new[:, :, None]), axis=2
            )
            return (top_new, sum_new)

        row_top, weight_sum = lax.cond(same_item, gather_scores, keep_state, (row_top, weight_sum))
    log_total = row_top + jnp.log(weight_sum)
    attended = jnp.zeros((pixels, HEADS, HEAD), jnp.float32)
    for offset, key_piece, allowed, same_item in pieces:

        def add_values(totals, key_piece=key_piece, allowed=allowed):
            scores = piece_scores(query_heads, key_piece, allowed)
            weights = jnp.exp(scores - log_total[:, :, None]).astype(jnp.bfloat16)
            return totals + jnp.einsum(
                "hqk,khd->qhd",
                weights,
                head_split(key_piece[:, C:]),
                preferred_element_type=jnp.float32,
            )

        attended = lax.cond(same_item, add_values, keep_state, attended)
    attended_flat = attended.reshape(pixels, C)
    row_dots = jnp.sum(
        (attended_grad.astype(jnp.float32) * attended_flat).reshape(pixels, HEADS, HEAD), axis=2
    ).T
    grad_heads = head_split(attended_grad)
    query_grad = jnp.zeros((pixels, C), jnp.float32)
    packed_grad = jnp.zeros((pixels + TEXT, 2 * C), jnp.float32)
    zero_piece = jnp.zeros((pixels + TEXT, 2 * C), jnp.float32)
    for offset, key_piece, allowed, same_item in pieces:

        def grad_both(totals, key_piece=key_piece, allowed=allowed):
            outcome = piece_grads(query_heads, grad_heads, log_total, row_dots, key_piece, allowed)
            return (totals + outcome[0], outcome[1])

        def grad_none(totals):
            return (totals, zero_piece)

        query_grad, piece_grad = lax.cond(same_item, grad_both, grad_none, query_grad)
        if offset == 0:
            packed_grad = packed_grad + piece_grad
        else:
            packed_grad = packed_grad + from_behind(
                as_sent(piece_grad), ROWS, -offset
            ).astype(jnp.float32)
    packed_low = packed_grad.astype(jnp.bfloat16)
    return (
        attended_flat.astype(jnp.bfloat16),
        query_grad.astype(jnp.bfloat16),
        packed_low[:pixels],
        packed_low[pixels:],
    )


def taps_of(rows, reverse):
    padded = rows.reshape(-1, W, rows.shape[1])
    row_list = [padded[:-2], padded[1:-1], padded[2:]]
    if reverse:
        row_list = row_list[::-1]
    zero_column = jnp.zeros_like(row_list[0][:, :1])
    views = []
    for row_view in row_list:
        left_view = jnp.concatenate([zero_column, row_view[:, :-1]], axis=1)
        right_view = jnp.concatenate([row_view[:, 1:], zero_column], axis=1)
        view_list = [left_view, row_view, right_view]
        if reverse:
            view_list = view_list[::-1]
        views = views + view_list
    return [view.reshape(-1, rows.shape[1]) for view in views]


class Vectors(typing.NamedTuple):
    mean_one: jax.Array
    scale_one: jax.Array
    gain_one: jax.Array
    bias_one: jax.Array
    mean_two: jax.Array
    scale_two: jax.Array
    gain_two: jax.Array
    bias_two: jax.Array
    mean_three: jax.Array
    scale_three: jax.Array
    gain_three: jax.Array
    bias_three: jax.Array
    stretch: jax.Array
    shift: jax.Array
    proj_bias: jax.Array
    keep_above: jax.Array
    keep_below: jax.Array
    per_item: jax.Array


def grouped(names, refs):
    found, position = types.SimpleNamespace(), 0
    for name, count in names:
        if count is None:
            setattr(found, name, refs[position])
            position += 1
        else:
            setattr(found, name, refs[position : position + count])
            position += count
    return found


def call_named(kernel, ident, scalars, inputs, anywhere, outs, scratch, semaphores):
    names = [(name, None) for name in [*scalars, *inputs, *anywhere, *outs]]
    buffers = []
    for name, entry in scratch.items():
        many = isinstance(entry, list)
        names.append((name, len(entry) if many else None))
        buffers += [pltpu.VMEM(*e) for e in (entry if many else [entry])]
    names += [(name, None) for name in semaphores]
    vmem = pl.BlockSpec(memory_space=pltpu.VMEM)
    outcome = pl.pallas_call(
        functools.partial(kernel, names),
        out_shape=tuple(jax.ShapeDtypeStruct(*o) for o in outs.values()),
        in_specs=[pl.BlockSpec(memory_space=pltpu.SMEM)] * len(scalars)
        + [vmem] * len(inputs)
        + [pl.BlockSpec(memory_space=pl.ANY)] * len(anywhere),
        out_specs=(vmem,) * len(outs),
        scratch_shapes=buffers + [pltpu.SemaphoreType.DMA(s) for s in semaphores.values()],
        compiler_params=pltpu.CompilerParams(
            collective_id=ident, has_side_effects=True, vmem_limit_bytes=60 << 20
        ),
        name=kernel.__name__,
    )(*[v for group in (scalars, inputs, anywhere) for v in dict(group).values()])
    return types.SimpleNamespace(**dict(zip(outs, outcome)))


VECTOR_ROWS = 24
FAR, NEAR, SIDE, CORE, GROUP = range(5)
CROSS = (FAR, NEAR, SIDE)
SIDE_FIRST = (SIDE, GROUP, NEAR, FAR)
GROUP_FIRST = (GROUP, NEAR, SIDE, FAR)
NEAR_FIRST = (NEAR, SIDE, GROUP, FAR)
STREAMS = (
    (48, C // 2, SIDE_FIRST),
    (48, C // 2, GROUP_FIRST),
    (48, C // 2, NEAR_FIRST),
    (48, C // 2, SIDE_FIRST),
    (48, C // 2, GROUP_FIRST),
    (48, C // 2, NEAR_FIRST),
    (32, C, SIDE_FIRST),
    (32, C, NEAR_FIRST),
    (16, 3 * C // 2, GROUP_FIRST),
    (16, C // 2, GROUP_FIRST),
)
FIRST_CONV, SECOND_CONV, WORDS, QKV, PROJ = 0, 3, 6, 8, 9
LANDINGS = 4
TAIL = (
    9, 7, 3, 5, 6, 8, 0, 4, 1, 7, 8, 4, 5, 6, 3, 2, 7, 0,
    6, 4, 5, 3, 2, 4, 1, 0, 5, 3, 2, 1, 0, 0, 2, 1, 2, 1,
)
IMAGE_ROWS = 8


class Band:
    def __init__(self, r):
        self.r = r
        self.row = lax.axis_index(ROWS)
        self.group = lax.axis_index(ITEMS)
        self.lane = self.row % SPAN
        self.base = self.row - self.lane
        row = self.row
        self.place = [row // 8, (row // 4) % 2, (row // 2) % 2, row % 2, self.group]
        self.partner = [
            {ROWS: row + (1 - 2 * self.place[d]) * (8 >> d)} for d in range(CORE + 1)
        ]
        self.partner.append({ITEMS: 1 - self.group})
        self.others = [(self.lane + o) % SPAN for o in range(1, SPAN)]
        self.peers = [{ROWS: self.base + other} for other in self.others]
        self.has_above, self.has_below = self.lane > 0, self.lane < SPAN - 1

    def meet(self, further=()):
        barrier = pltpu.get_barrier_semaphore()
        targets = self.peers + list(further)
        for target in targets:
            pl.semaphore_signal(barrier, 1, device_id=target)
        pl.semaphore_wait(barrier, len(targets))

    def remote(self, source, target, send, recv, device):
        return pltpu.make_async_remote_copy(source, target, send, recv, device_id=device)

    def edges(self, k, top, bottom, target):
        r = self.r
        up = self.remote(
            top,
            target.at[IMAGE_ROWS + 1],
            r.edge_send.at[k, 0],
            r.edge_recv.at[k, 0],
            {ROWS: self.row - 1},
        )
        down = self.remote(
            bottom,
            target.at[0],
            r.edge_send.at[k, 1],
            r.edge_recv.at[k, 1],
            {ROWS: self.row + 1},
        )
        pl.when(self.has_above)(up.start)
        pl.when(self.has_below)(down.start)
        return up, down

    def wait_edges(self, pair):
        up, down = pair

        @pl.when(self.has_above)
        def _():
            up.wait_send()
            down.wait_recv()

        @pl.when(self.has_below)
        def _():
            down.wait_send()
            up.wait_recv()

    def zero_edges(self, target):
        @pl.when(jnp.logical_not(self.has_above))
        def _():
            target[0] = jnp.zeros(target.shape[1:], target.dtype)

        @pl.when(jnp.logical_not(self.has_below))
        def _():
            target[IMAGE_ROWS + 1] = jnp.zeros(target.shape[1:], target.dtype)

    def send_tile(self, k, source, target):
        r = self.r
        copies = []
        for o in range(1, SPAN):
            copies.append(
                self.remote(
                    source,
                    target.at[self.lane],
                    r.tile_send.at[k, o],
                    r.tile_recv.at[k, o],
                    self.peers[o - 1],
                )
            )
        for copy in copies:
            copy.start()
        target[self.lane] = source[...]
        return copies

    def swap(self, k, source, target, order=range(1, SPAN)):
        r = self.r
        copies = []
        for o in order:
            copies.append(
                self.remote(
                    source.at[self.others[o - 1]],
                    target.at[self.lane],
                    r.swap_send.at[k, o],
                    r.swap_recv.at[k, o],
                    self.peers[o - 1],
                )
            )
            copies[-1].start()
        return copies

    def fill_blocks(self):
        rows = lax.broadcasted_iota(jnp.int32, (C, C), 0) // (C // NORM_GROUPS)
        columns = lax.broadcasted_iota(jnp.int32, (C, C), 1) // (C // NORM_GROUPS)
        self.r.blocks[...] = jnp.where(rows == columns, 1.0, 0.0).astype(jnp.bfloat16)

    def item_means(self, window, masks, per_item):
        low, full = jnp.bfloat16, jnp.float32
        total = jnp.zeros((8, C), full)
        for b in range(SPAN):
            total = total + jnp.where(masks[b] > 0.0, window[b], 0.0)
        total = total * per_item
        coarse = total.astype(low)
        rest = total - coarse.astype(full)
        finer = rest.astype(low)
        finest = (rest - finer.astype(full)).astype(low)
        blocks = self.r.blocks[...]
        return dot(coarse, blocks) + dot(finer, blocks) + dot(finest, blocks)


def sums_tile(first, second):
    rows = lax.broadcasted_iota(jnp.int32, (8, C), 0)
    return jnp.where(rows == 0, first, jnp.where(rows == 1, second, 0.0))


def column_sum(values):
    return jnp.sum(values, axis=0, keepdims=True)


def side_shifts(values):
    rows = lax.broadcasted_iota(jnp.int32, (W, C), 0)
    from_left = jnp.where(rows == 0, 0.0, pltpu.roll(values, 1, 0))
    from_right = jnp.where(rows == W - 1, 0.0, pltpu.roll(values, W - 1, 0))
    return from_left, from_right


def kept(i, values, vec):
    keep = jnp.where(i == 0, vec.keep_above, jnp.where(i == IMAGE_ROWS + 1, vec.keep_below, 1.0))
    return jnp.where(keep > 0.0, values, 0.0)


def back_kernel(names, *refs):
    low, full = jnp.bfloat16, jnp.float32
    r = grouped(names, refs)
    band = Band(r)
    lane, group, place, partner = band.lane, band.group, band.place, band.partner
    core = place[CORE]
    remote = band.remote
    across = {ROWS: partner[CORE][ROWS], ITEMS: 1 - group}
    band.meet((partner[FAR], partner[GROUP], across))

    swaps = band.swap(0, r.pair_grads, r.head_pairs) + band.swap(1, r.word_grads, r.head_words)

    loads = types.SimpleNamespace()

    def load(k, source, target):
        copy = pltpu.make_async_copy(source, target, r.load_sem.at[k])
        copy.start()
        return copy

    loads.outcome = load(0, r.outcome, r.heads)
    loads.pair_grads = load(1, r.pair_grads.at[lane], r.head_pairs.at[lane])
    loads.word_grads = load(14, r.word_grads.at[lane], r.head_words.at[lane])
    loads.middle = load(2, r.middle, r.mid)
    loads.qkv_weight = load(3, r.qkv_weight, r.qkv_w)
    loads.proj_weight = load(4, r.proj_weight, r.proj_w)
    loads.upstream = load(5, r.upstream, r.up)
    loads.act_three = load(6, r.act_three, r.act3)
    loads.caption = load(7, r.caption, r.cap)
    loads.conv_second = load(8, r.conv_second, r.conv_w)
    loads.hidden = load(9, r.hidden, r.hid)
    loads.act_two = load(10, r.act_two, r.act2)
    loads.act_one = load(11, r.act_one, r.act1)
    loads.image = load(12, r.image, r.img)
    loads.text_weight = load(13, r.text_weight, r.text_w)

    sibling = types.SimpleNamespace()

    def to_sibling(k, source, target):
        copy = remote(source, target, r.sib_send.at[k], r.sib_recv.at[k], partner[CORE])
        copy.start()
        return copy

    half = pl.ds(pl.multiple_of((1 - core) * (C // 2), C // 2), C // 2)
    sibling.upstream = to_sibling(0, r.upstream.at[:, half], r.sib_up)
    sibling.act3 = to_sibling(1, r.act_three, r.sib_act3)
    sibling.cap = to_sibling(2, r.caption, r.sib_cap)
    sibling.act2 = to_sibling(3, r.act_two, r.sib_act2)
    sibling.act1 = to_sibling(4, r.act_one, r.sib_act1)

    share_copy = remote(
        r.silu_share, r.other_share, r.small_send.at[2], r.small_recv.at[2], partner[GROUP]
    )
    share_copy.start()
    for target in (r.part_two, r.part_one):
        band.zero_edges(target)

    vec = Vectors(*[r.vectors[i : i + 1, :] for i in range(len(Vectors._fields))])
    norm_one = (vec.mean_one, vec.scale_one)
    norm_two = (vec.mean_two, vec.scale_two)
    norm_three = (vec.mean_three, vec.scale_three)

    masks = [r.vectors[VECTOR_ROWS + b : VECTOR_ROWS + b + 1, :] for b in range(SPAN)]
    band.fill_blocks()

    def item_means(window):
        return band.item_means(window, masks, vec.per_item)

    class Stream:
        def __init__(self, k):
            self.k = k
            self.order = STREAMS[k][2]
            self.dims = [FAR, NEAR, SIDE, CORE, GROUP]
            self.step = 0
            self.copies = []

        def at(self, ref, d, index):
            return ref.at[(slice(None),) * self.dims.index(d) + (index,)]

        def start(self):
            self.launch(r.grads[self.k])

        def launch(self, ref):
            k, step = self.k, self.step
            if step < LANDINGS:
                d = self.order[step]
                self.copies = [
                    remote(
                        self.at(ref, d, 1 - place[d]),
                        r.landings[k * LANDINGS + step],
                        r.fold_send.at[k, step],
                        r.fold_recv.at[k, step],
                        partner[d],
                    )
                ]
                self.mine = self.at(ref, d, place[d])
                self.dims.remove(d)
            else:
                ends = (
                    (ref.at[1 - core], r.folded[k].at[core], partner[CORE]),
                    (ref.at[core], r.whole[k].at[core], partner[GROUP]),
                    (ref.at[1 - core], r.whole[k].at[core], across),
                )
                self.copies = [
                    remote(
                        source,
                        target,
                        r.fold_send.at[k, step + i],
                        r.fold_recv.at[k, step + i],
                        device,
                    )
                    for i, (source, target, device) in enumerate(ends)
                ]
                self.mine = ref.at[core]
            for copy in self.copies:
                copy.start()

        def advance(self):
            for copy in self.copies:
                copy.wait()
            if self.step < LANDINGS:
                landed, mine = r.landings[self.k * LANDINGS + self.step], self.mine
                lead = landed.shape[:-2]
                pieces = 1
                for n in lead:
                    pieces *= n

                def add(i, carry):
                    index = []
                    for n in reversed(lead):
                        index.insert(0, i % n)
                        i = i // n
                    index = tuple(index)
                    total = landed[index].astype(full) + mine[index].astype(full)
                    landed[index] = total.astype(low)
                    return carry

                lax.fori_loop(0, pieces, add, 0)
                self.step += 1
                self.launch(landed)
            else:
                r.folded[self.k][core] = self.mine[...]
                self.step += 1

    streams = [Stream(k) for k in range(len(STREAMS))]

    def advance(*order):
        for k in order:
            streams[k].advance()

    loads.outcome.wait()
    for h in range(0, HEADS, 2):
        for k in range(2):
            pair = [r.heads[h + i, :, k * HEAD : (k + 1) * HEAD] for i in range(2)]
            r.joined[:, k * C + h * HEAD : k * C + (h + 2) * HEAD] = jnp.concatenate(pair, axis=1)
    sibling.attended = to_sibling(5, r.joined.at[:, 0:C], r.sib_attended)

    def pixel_block(ref, i, count=4):
        return ref[1 + i * count : 1 + (i + 1) * count].reshape(count * W, C)

    def unit(values, norm):
        return (values - norm[0]) * norm[1]

    def mine_of(ref, start, size):
        return ref[:, pl.ds(pl.multiple_of(start, size if size % 256 else 256), size)]

    for copy in (loads.middle, loads.qkv_weight, loads.proj_weight, loads.upstream):
        copy.wait()
    up_sum = jnp.zeros((1, C), full)
    for i in range(2):
        block = slice(i * 4 * W, (i + 1) * 4 * W)
        upstream = r.up[block, :].astype(full)
        up_sum = up_sum + column_sum(upstream)
        result = pixel_block(r.mid, i) + dot(r.joined[block, 0:C], r.proj_w[...]) + vec.proj_bias
        r.result[block, :] = result.astype(low)
        grad = dot_last(r.joined[block, C : 2 * C], r.qkv_w[:, 0:C])
        r.product[i * 4 : i * 4 + 4] = grad.reshape(4, W, C)
    sibling.upstream.wait()
    sibling.attended.wait()
    grad = dot_first(r.joined[:, 0:C], mine_of(r.up, core * (C // 2), C // 2))
    grad = grad + dot_first(r.sib_attended[...], r.sib_up[...])
    r.grads[PROJ][...] = grad.astype(low).reshape(r.grads[PROJ].shape)
    streams[PROJ].start()
    query_sum = column_sum(r.joined[:, C : 2 * C].astype(full))

    for copy in (loads.pair_grads, loads.word_grads):
        copy.wait()
    for copy in swaps:
        copy.wait()
    for h in range(0, HEADS, 2):
        for k in range(2):
            lanes = slice(k * HEAD, (k + 1) * HEAD)
            pair = [r.head_pairs[h + i, :, lanes] for i in range(2)]
            first = (2 + k) * C + h * HEAD
            r.joined[:, first : first + 2 * HEAD] = jnp.concatenate(pair, axis=1)
            pair = [r.head_words[h + i, :, lanes] for i in range(2)]
            first = k * C + h * HEAD
            r.joined_words[:, first : first + 2 * HEAD] = jnp.concatenate(pair, axis=1)
    three_half = C + (1 - core) * (3 * C // 2)
    sibling.qkv = to_sibling(
        6, r.joined.at[:, pl.ds(pl.multiple_of(three_half, C // 2), 3 * C // 2)], r.sib_qkv
    )
    sibling.words = to_sibling(
        7, r.joined_words.at[:, pl.ds(pl.multiple_of((1 - core) * C, C), C)], r.sib_words
    )

    plain = jnp.zeros((1, C), full)
    crossed = jnp.zeros((1, C), full)
    for i in range(2):
        block = slice(i * 4 * W, (i + 1) * 4 * W)
        grad = dot_last(r.joined[block, 2 * C :], r.qkv_w[:, C:])
        grad = grad + r.product[i * 4 : i * 4 + 4].reshape(4 * W, C)
        plain = plain + column_sum(grad)
        crossed = crossed + column_sum(grad * unit(pixel_block(r.mid, i), norm_three))
        part = r.up[block, :].astype(full) + grad * (vec.gain_three * vec.scale_three)
        r.part_two[1 + i * 4 : 5 + i * 4] = part.reshape(4, W, C)
    gain_three, bias_three = crossed, plain
    r.tile[0] = sums_tile(plain * vec.gain_three, crossed * vec.gain_three)
    three_edges = band.edges(0, r.part_two.at[1], r.part_two.at[IMAGE_ROWS], r.part_two)
    tiles = band.send_tile(0, r.tile.at[0], r.window.at[0])

    for copy in (sibling.act3, sibling.cap, sibling.qkv, sibling.words):
        copy.wait()
    for copy in (loads.act_three, loads.caption):
        copy.wait()
    for n in range(3):
        own = mine_of(r.joined, C + core * (3 * C // 2) + n * (C // 2), C // 2)
        columns = slice(n * (C // 2), (n + 1) * (C // 2))
        grad = dot_first(r.act3[...], own)
        grad = grad + dot_first(r.sib_act3[...], r.sib_qkv[:, columns])
        r.grads[QKV][:, :, :, :, :, :, columns] = grad.astype(low).reshape(2, 2, 2, 2, 2, 16, C // 2)
    streams[QKV].start()

    def text_rows(s, carry):
        columns = pl.ds(pl.multiple_of(s * 128, 128), 128)
        own = mine_of(r.joined_words, core * C, C)
        grad = dot_first(r.cap[:, columns], own)
        grad = grad + dot_first(r.sib_cap[:, columns], r.sib_words[...])
        grad = grad.astype(low)
        index = (s // 8, (s // 4) % 2, (s // 2) % 2, s % 2)
        r.grads[WORDS][index] = grad[0:64].reshape(2, 32, C)
        r.grads[WORDS + 1][index] = grad[64:128].reshape(2, 32, C)
        return carry

    lax.fori_loop(0, 2 ** len(CROSS) * 2, text_rows, 0)
    streams[WORDS].start()
    streams[WORDS + 1].start()
    value_sum = column_sum(r.joined[:, 3 * C :].astype(full))
    word_sum = [column_sum(r.joined_words[:, k * C : (k + 1) * C].astype(full)) for k in range(2)]

    def spread_rows(i, values):
        from_left, from_right = side_shifts(values)
        r.shifts[0, i] = from_right.astype(low)
        r.shifts[1, i] = values.astype(low)
        r.shifts[2, i] = from_left.astype(low)

    def conv_back():
        total = jnp.zeros((IMAGE_ROWS * W, C), full)
        for t in range(9):
            dy, dx = t // 3, t % 3
            view = r.shifts[dx, 2 - dy : 2 - dy + IMAGE_ROWS].reshape(IMAGE_ROWS * W, C)
            total = total + dot_last(view, r.conv_w[t * C : (t + 1) * C, :])
        return total

    def conv_grads(kind, own, other, landing):
        for t in range(9):
            dy, dx = t // 3, t % 3
            shifted = r.shifts[
                dx, 1 : IMAGE_ROWS + 1, :, pl.ds(pl.multiple_of(core * (C // 2), C // 2), C // 2)
            ].reshape(IMAGE_ROWS * W, C // 2)
            grad = dot_first(own[dy * W : dy * W + IMAGE_ROWS * W, :], shifted)
            grad = grad + dot_first(
                other[dy * W : dy * W + IMAGE_ROWS * W, :],
                landing[dx].reshape(IMAGE_ROWS * W, C // 2),
            )
            grad = grad.astype(low)
            begin = t * C
            while begin < (t + 1) * C:
                shard, within = divmod(begin, 288)
                stream, offset = divmod(within, 96)
                part, offset = divmod(offset, 48)
                size = min(48 - offset, (t + 1) * C - begin)
                target = r.grads[kind + stream]
                target[
                    shard // 8, (shard // 4) % 2, (shard // 2) % 2, shard % 2, part, offset : offset + size
                ] = grad[begin - t * C : begin - t * C + size]
                begin += size
        for j in range(3):
            streams[kind + j].start()

    for copy in tiles:
        copy.wait()
    band.wait_edges(three_edges)
    means = item_means(r.window.at[0])
    offset_three, slope_three = means[0:1] * vec.scale_three, means[1:2] * vec.scale_three

    def middle_row(i, bias):
        values = r.part_two[i] - offset_three - unit(r.mid[i], norm_three) * slope_three
        r.part_two[i] = values
        values = kept(i, values, vec)
        spread_rows(i, values)
        inside = jnp.where((i > 0) & (i <= IMAGE_ROWS), 1.0, 0.0)
        return bias + inside * column_sum(values.astype(low).astype(full))

    conv_bias_two = lax.fori_loop(0, IMAGE_ROWS + 2, middle_row, jnp.zeros((1, C), full))
    shift_half = r.shifts.at[:, 1 : IMAGE_ROWS + 1, :, half]
    sibling.shifts_two = to_sibling(8, shift_half, r.sib_shifts_two)
    advance(PROJ)
    loads.conv_second.wait()
    loads.hidden.wait()
    r.product[...] = conv_back().reshape(IMAGE_ROWS, W, C)
    loads.conv_first = load(8, r.conv_first, r.conv_w)
    stretched = vec.stretch * vec.gain_two * vec.scale_two

    def second_row(i, sums):
        unit_two = unit(r.hid[i + 1], norm_two)
        normed = unit_two * vec.gain_two + vec.bias_two
        grad = r.product[i] * silu_slope_of(normed * vec.stretch + vec.shift)
        r.part_one[i + 1] = grad * stretched
        return sums[0] + column_sum(grad), sums[1] + column_sum(grad * unit_two)

    nothing = (jnp.zeros((1, C), full), jnp.zeros((1, C), full))
    plain, crossed = lax.fori_loop(0, IMAGE_ROWS, second_row, nothing)
    scale_grad = crossed * vec.gain_two + plain * vec.bias_two
    shift_grad = plain
    gain_two, bias_two = crossed * vec.stretch, plain * vec.stretch
    r.tile[1] = sums_tile(bias_two * vec.gain_two, gain_two * vec.gain_two)
    two_edges = band.edges(1, r.part_one.at[1], r.part_one.at[IMAGE_ROWS], r.part_one)
    tiles = band.send_tile(1, r.tile.at[1], r.window.at[1])
    loads.act_two.wait()
    sibling.act2.wait()
    sibling.shifts_two.wait()
    advance(PROJ)
    conv_grads(SECOND_CONV, r.act2, r.sib_act2, r.sib_shifts_two)
    advance(PROJ, QKV)
    for copy in tiles:
        copy.wait()
    band.wait_edges(two_edges)
    means = item_means(r.window.at[1])
    offset_two, slope_two = means[0:1] * vec.scale_two, means[1:2] * vec.scale_two

    def hidden_row(i, bias):
        values = r.part_one[i] - offset_two - unit(r.hid[i], norm_two) * slope_two
        values = kept(i, values, vec)
        spread_rows(i, values)
        inside = jnp.where((i > 0) & (i <= IMAGE_ROWS), 1.0, 0.0)
        return bias + inside * column_sum(values.astype(low).astype(full))

    conv_bias_one = lax.fori_loop(0, IMAGE_ROWS + 2, hidden_row, jnp.zeros((1, C), full))
    sibling.shifts_one = to_sibling(9, shift_half, r.sib_shifts_one)
    advance(PROJ, WORDS, WORDS + 1)
    loads.conv_first.wait()
    loads.image.wait()
    r.product[...] = conv_back().reshape(IMAGE_ROWS, W, C)

    def first_row(i, sums):
        unit_one = unit(r.img[i].astype(full), norm_one)
        normed = unit_one * vec.gain_one + vec.bias_one
        grad = r.product[i] * silu_slope_of(normed)
        r.product[i] = grad
        return sums[0] + column_sum(grad), sums[1] + column_sum(grad * unit_one)

    plain, crossed = lax.fori_loop(0, IMAGE_ROWS, first_row, nothing)
    gain_one, bias_one = crossed, plain
    r.tile[2] = sums_tile(plain * vec.gain_one, crossed * vec.gain_one)
    tiles = band.send_tile(2, r.tile.at[2], r.window.at[2])
    rows = [
        gain_one,
        gain_two,
        gain_three,
        bias_one,
        bias_two,
        bias_three,
        conv_bias_one,
        conv_bias_two,
        query_sum,
        value_sum,
        word_sum[0],
        word_sum[1],
        up_sum,
        jnp.zeros((1, C), full),
        scale_grad,
        shift_grad,
    ]
    for i, values in enumerate(rows):
        r.own_rows[i : i + 1, :] = values
    row_copies = band.send_tile(3, r.own_rows, r.band_rows)
    loads.act_one.wait()
    sibling.act1.wait()
    sibling.shifts_one.wait()
    conv_grads(FIRST_CONV, r.act1, r.sib_act1, r.sib_shifts_one)
    advance(QKV, 3, 4, 7, 6, 5)
    for copy in tiles:
        copy.wait()
    means = item_means(r.window.at[2])
    offset_one, slope_one = means[0:1] * vec.scale_one, means[1:2] * vec.scale_one
    ratio = vec.gain_one * vec.scale_one

    def image_row(i, carry):
        unit_one = unit(r.img[i].astype(full), norm_one)
        values = r.part_two[i + 1] + r.product[i] * ratio - offset_one - unit_one * slope_one
        r.image_grad[i] = values
        return carry

    lax.fori_loop(0, IMAGE_ROWS, image_row, 0)

    for copy in row_copies:
        copy.wait()
    total = jnp.zeros((16, C), full)
    for b in range(SPAN):
        total = total + r.band_rows[b]
    r.half_rows[0:16, :] = total
    for b in range(SPAN):
        r.half_rows[16 + 2 * b : 18 + 2 * b, :] = r.band_rows[b, 14:16, :]
    far_copy = remote(
        r.half_rows, r.far_rows, r.small_send.at[0], r.small_recv.at[0], partner[FAR]
    )
    far_copy.start()
    loads.text_weight.wait()

    def caption_columns(n, carry):
        columns = pl.ds(pl.multiple_of(n * C, C), C)
        r.caption_grad[:, columns] = dot_last(r.joined_words[...], r.text_w[columns, :])
        return carry

    lax.fori_loop(0, EMB // C, caption_columns, 0)
    loads.embed_weight = load(13, r.embed_weight, r.text_w)
    far_copy.wait()
    first_half = jnp.where(place[FAR] == 0, r.half_rows[16:32, :], r.far_rows[16:32, :])
    other_half = jnp.where(place[FAR] == 0, r.far_rows[16:32, :], r.half_rows[16:32, :])
    r.group_rows[0:16, :] = r.half_rows[0:16, :] + r.far_rows[0:16, :]
    r.group_rows[16:32, :] = first_half
    r.group_rows[32:48, :] = other_half
    slots = r.slot_of_band.shape[0]
    for k in range(2):
        table = jnp.zeros((slots, C), full)
        for b in range(2 * SPAN):
            values = r.group_rows[16 + 2 * b + k : 17 + 2 * b + k, :]
            table = table + jnp.where(r.slot_of_band[:, b * 128 : b * 128 + 1] > 0.0, values, 0.0)
        r.own_table[slots * k : slots * (k + 1), :] = table
    r.own_table[2 * slots :, :] = r.group_rows[0:16, :]
    group_copy = remote(
        r.own_table,
        r.other_table,
        r.small_send.at[1],
        r.small_recv.at[1],
        partner[GROUP],
    )
    group_copy.start()
    advance(QKV, *TAIL[:8])
    loads.embed_weight.wait()
    table = [r.own_table[slots * k : slots * (k + 1), :].astype(low) for k in range(2)]

    def embedding_columns(n, carry):
        columns = pl.ds(pl.multiple_of(n * C, C), C)
        grad = dot_last(table[0], r.text_w[columns, 0:C]) + dot_last(table[1], r.text_w[columns, C:])
        source = r.embedding[:, columns].astype(full)
        r.embedding_grad[:, columns] = grad * silu_slope_of(source)
        return carry

    lax.fori_loop(0, EMB // C, embedding_columns, 0)
    advance(*TAIL[8:18])
    group_copy.wait()
    share_copy.wait()
    for k in range(2):
        columns = slice(k * C, (k + 1) * C)
        other = r.other_table[slots * k : slots * (k + 1), :].astype(low)
        r.embed_weight_grad[:, columns] = dot_first(r.silu_share[...], table[k]) + dot_first(
            r.other_share[...], other
        )
        r.embed_bias_grad[:, columns] = column_sum(table[k].astype(full)) + column_sum(
            other.astype(full)
        )
    sums = r.own_table[2 * slots :, :] + r.other_table[2 * slots :, :]
    r.norm_gains_grad[...] = sums[0:3]
    r.norm_biases_grad[...] = sums[3:6]
    r.conv_biases_grad[...] = sums[6:8]
    for target, k in ((r.qv_bias_grad, 8), (r.text_bias_grad, 10)):
        target[:, 0:C] = sums[k : k + 1]
        target[:, C:] = sums[k + 1 : k + 2]
    r.proj_bias_grad[...] = sums[12:13]
    advance(*TAIL[18:])

    def write(stream, target, first_row):
        rows, columns = STREAMS[stream][:2]
        for side, source in ((group, r.folded[stream]), (1 - group, r.whole[stream])):
            for k in range(2):
                target[
                    pl.ds(pl.multiple_of(first_row + side * rows, rows), rows),
                    k * columns : (k + 1) * columns,
                ] = source[k].astype(full)

    for j in range(3):
        write(FIRST_CONV + j, r.conv_first_grad, j * 96)
        write(SECOND_CONV + j, r.conv_second_grad, j * 96)
    for j in range(2):
        write(WORDS + j, r.text_grad, j * 64)
    write(QKV, r.qkv_grad, 0)
    write(PROJ, r.proj_grad, 0)


def silu_slope_of(source):
    sigma = 1.0 / (1.0 + jnp.exp(-source))
    return sigma * (1.0 + source * (1.0 - sigma))


def back(ident, vectors, slot_of_band, silu_share, embedding, anywhere):
    low, full = jnp.bfloat16, jnp.float32
    pixels = IMAGE_ROWS * W
    slots = slot_of_band.shape[0]
    outs = dict(
        result=((pixels, C), low),
        image_grad=((IMAGE_ROWS, W, C), full),
        caption_grad=((TEXT, EMB), full),
        conv_first_grad=((288, C), full),
        conv_second_grad=((288, C), full),
        qkv_grad=((32, 3 * C), full),
        text_grad=((128, 2 * C), full),
        proj_grad=((32, C), full),
        embedding_grad=(embedding.shape, full),
        embed_weight_grad=((silu_share.shape[1], 2 * C), full),
        norm_gains_grad=((3, C), full),
        norm_biases_grad=((3, C), full),
        conv_biases_grad=((2, C), full),
        embed_bias_grad=((1, 2 * C), full),
        qv_bias_grad=((1, 2 * C), full),
        text_bias_grad=((1, 2 * C), full),
        proj_bias_grad=((1, C), full),
    )
    padded = (IMAGE_ROWS + 2, W, C)
    scratch = dict(
        heads=((HEADS, pixels, 2 * HEAD), low),
        head_pairs=((HEADS, pixels, 2 * HEAD), low),
        head_words=((HEADS, TEXT, 2 * HEAD), low),
        joined=((pixels, 4 * C), low),
        joined_words=((TEXT, 2 * C), low),
        mid=(padded, full),
        part_two=(padded, full),
        part_one=(padded, full),
        hid=(padded, full),
        product=((IMAGE_ROWS, W, C), full),
        img=((IMAGE_ROWS, W, C), low),
        up=((pixels, C), low),
        act1=((pixels + 2 * W, C), low),
        act2=((pixels + 2 * W, C), low),
        act3=((pixels, C), low),
        cap=((TEXT, EMB), low),
        conv_w=((9 * C, C), low),
        qkv_w=((C, 3 * C), low),
        proj_w=((C, C), low),
        text_w=((EMB, 2 * C), low),
        sib_up=((pixels, C // 2), low),
        sib_act1=((pixels + 2 * W, C), low),
        sib_act2=((pixels + 2 * W, C), low),
        sib_act3=((pixels, C), low),
        sib_cap=((TEXT, EMB), low),
        sib_attended=((pixels, C), low),
        sib_qkv=((pixels, 3 * C // 2), low),
        sib_words=((TEXT, C), low),
        sib_shifts_one=((3, IMAGE_ROWS, W, C // 2), low),
        sib_shifts_two=((3, IMAGE_ROWS, W, C // 2), low),
        shifts=((3,) + padded, low),
        blocks=((C, C), low),
        tile=((3, 8, C), full),
        window=((3, SPAN, 8, C), full),
        own_rows=((16, C), full),
        band_rows=((SPAN, 16, C), full),
        half_rows=((32, C), full),
        far_rows=((32, C), full),
        group_rows=((48, C), full),
        own_table=((2 * slots + 16, C), full),
        other_table=((2 * slots + 16, C), full),
        other_share=(silu_share.shape, low),
    )
    scratch.update(grads=[((2,) * 5 + s[:2], low) for s in STREAMS])
    scratch.update(landings=[((2,) * (4 - i) + s[:2], low) for s in STREAMS for i in range(LANDINGS)])
    scratch.update(folded=[((2,) + s[:2], low) for s in STREAMS])
    scratch.update(whole=[((2,) + s[:2], low) for s in STREAMS])
    semaphores = dict(
        swap_send=(2, SPAN),
        swap_recv=(2, SPAN),
        load_sem=(15,),
        sib_send=(10,),
        sib_recv=(10,),
        edge_send=(2, 2),
        edge_recv=(2, 2),
        tile_send=(4, SPAN),
        tile_recv=(4, SPAN),
        fold_send=(len(STREAMS), LANDINGS + 3),
        fold_recv=(len(STREAMS), LANDINGS + 3),
        small_send=(3,),
        small_recv=(3,),
    )
    inputs = dict(
        vectors=vectors, slot_of_band=slot_of_band, silu_share=silu_share, embedding=embedding
    )
    return call_named(back_kernel, ident, (), inputs, anywhere, outs, scratch, semaphores)


def attend_kernel(names, *refs):
    low, full = jnp.bfloat16, jnp.float32
    r = grouped(names, refs)
    band = Band(r)
    band.meet()
    bands, pixels = r.pairs.shape[:2]
    text = r.words.shape[1]
    scale = HEAD ** (-0.5)

    def with_units(values, rows):
        lanes = lax.broadcasted_iota(jnp.int32, (rows, 2 * HEAD), 1)
        units = jnp.where(lanes < 2, 1.0, 0.0).astype(low)
        return jnp.where(lanes < HEAD, units, values)

    def prepare(b, carry):
        r.across[b] = r.pairs[b].T
        r.valued[b] = with_units(r.pairs[b], pixels)
        r.words_across[b] = r.words[b].T
        r.words_valued[b] = with_units(r.words[b], text)
        r.pair_sums[b] = jnp.zeros((pixels, 2 * HEAD), full)
        return carry

    lax.fori_loop(0, bands, prepare, 0)

    def one_row(columns):
        rows = lax.broadcasted_iota(jnp.int32, (16, columns), 0)
        return jnp.where(rows == 0, 1.0, 0.0).astype(low)

    ones_pixels = one_row(pixels)
    ones_text = one_row(text)
    zeros = jnp.zeros((HEAD, pixels), low)

    def outcome_copy(i):
        return band.remote(
            r.own_outcome.at[i],
            r.outcome.at[band.lane],
            r.outcome_send.at[i],
            r.outcome_recv.at[band.lane],
            {ROWS: band.base + i},
        )

    def query_band(step, carry):
        i = (band.lane + 1 + step) % bands
        mine = r.items[band.base + i]
        start = 0
        allowed = []
        for b in range(bands):
            other = r.items[band.base + b]
            start = start + jnp.where(other < mine, 1, 0)
            allowed.append(other == mine)
        query = (r.queries[i].astype(full) * scale).astype(low)
        query_rhs = jnp.concatenate([query, zeros], 0)

        top = jnp.full((8, pixels), -jnp.inf, full)
        for j in range(bands):
            scores = dot(r.pairs[j], query_rhs)
            r.scores[j] = scores
            highest = jnp.max(scores.reshape(pixels // 8, 8, pixels), axis=0)
            top = jnp.where(allowed[j], jnp.maximum(top, highest), top)
        scores = dot(r.words[start], query_rhs)
        top = jnp.maximum(top, jnp.max(scores.reshape(text // 8, 8, pixels), axis=0))
        top = jnp.max(top, axis=0, keepdims=True)
        weights_text = jnp.exp2((scores - top) * LOG2E).astype(low)
        values = jnp.concatenate([r.words_across[start, HEAD:, :], ones_text], 0)
        total = dot(values, weights_text)

        for j in range(bands):
            ceiling = top + jnp.where(allowed[j], 0.0, FAR_ABOVE)
            weights = jnp.exp2((r.scores[j] - ceiling) * LOG2E).astype(low)
            r.weights[j] = weights
            values = jnp.concatenate([r.across[j, HEAD:, :], ones_pixels], 0)
            total = total + dot(values, weights)
        inverse = 1.0 / total[HEAD : HEAD + 1, :]
        attended = total[0:HEAD, :] * inverse
        grad = r.upstream[i].astype(full)
        minus_dots = -jnp.sum(grad * attended, axis=0, keepdims=True) * inverse
        grad_scaled = (grad * inverse).astype(low)
        coarse = minus_dots.astype(low)
        fine = minus_dots - coarse.astype(full)
        rows = lax.broadcasted_iota(jnp.int32, (HEAD, pixels), 0)
        extra = jnp.where(rows == 0, coarse.astype(full), jnp.where(rows == 1, fine, 0.0))
        grad_rhs = jnp.concatenate([extra.astype(low), grad_scaled], 0)
        grad_rows = jnp.concatenate([zeros, grad_scaled], 0).T
        query_rows = jnp.concatenate([query, zeros], 0).T

        steps = (weights_text.astype(full) * dot(r.words_valued[start], grad_rhs)).astype(low)
        word_sum = dot(weights_text, grad_rows) + dot(steps, query_rows)
        r.word_parts[i] = word_sum
        query_grad = dot(r.words_across[start, 0:HEAD, :], steps)
        for j in range(bands):
            for begin in range(0, pixels, pixels // 2):
                keys = slice(begin, begin + pixels // 2)
                weights = r.weights[j, keys]
                steps = (weights.astype(full) * dot(r.valued[j, keys], grad_rhs)).astype(low)
                r.pair_sums[j, keys] += dot(weights, grad_rows) + dot(steps, query_rows)
                query_grad = query_grad + dot(r.across[j, 0:HEAD, keys], steps)
        r.own_outcome[i] = jnp.concatenate(
            [attended.astype(low), (query_grad * scale).astype(low)], 0
        ).T
        pl.when(step < bands - 1)(outcome_copy(i).start)
        return carry

    lax.fori_loop(0, bands, query_band, 0)
    r.outcome[band.lane] = r.own_outcome[band.lane]

    def finish(b, carry):
        r.pair_grads[b] = r.pair_sums[b].astype(low)
        word_sum = jnp.zeros((text, 2 * HEAD), full)
        for i in range(bands):
            mine = r.items[band.base + i]
            start = 0
            for c in range(bands):
                start = start + jnp.where(r.items[band.base + c] < mine, 1, 0)
            word_sum = word_sum + jnp.where(start == b, r.word_parts[i], 0.0)
        r.word_grads[b] = word_sum.astype(low)
        return carry

    lax.fori_loop(0, bands, finish, 0)

    def wait_outcome(step, carry):
        i = (band.lane + 1 + step) % bands
        outcome_copy(i).wait_send()
        band.remote(
            r.own_outcome.at[i],
            r.outcome.at[i],
            r.outcome_send.at[i],
            r.outcome_recv.at[i],
            {ROWS: band.base + i},
        ).wait_recv()
        return carry

    lax.fori_loop(0, bands - 1, wait_outcome, 0)


def attend(ident, items, ahead):
    low, full = jnp.bfloat16, jnp.float32
    bands, pixels, _ = ahead.pairs.shape
    text = ahead.words.shape[1]
    outs = dict(
        outcome=((bands, pixels, 2 * HEAD), low),
        pair_grads=((bands, pixels, 2 * HEAD), low),
        word_grads=((bands, text, 2 * HEAD), low),
    )
    scratch = dict(
        across=((bands, 2 * HEAD, pixels), low),
        valued=((bands, pixels, 2 * HEAD), low),
        words_across=((bands, 2 * HEAD, text), low),
        words_valued=((bands, text, 2 * HEAD), low),
        scores=((bands, pixels, pixels), full),
        weights=((bands, pixels, pixels), low),
        pair_sums=((bands, pixels, 2 * HEAD), full),
        word_parts=((bands, text, 2 * HEAD), full),
        own_outcome=((bands, pixels, 2 * HEAD), low),
    )
    semaphores = dict(outcome_send=(bands,), outcome_recv=(bands,))
    inputs = dict(
        pairs=ahead.pairs, queries=ahead.queries, upstream=ahead.upstream, words=ahead.words
    )
    return call_named(
        attend_kernel, ident, dict(items=items), inputs, {}, outs, scratch, semaphores
    )


def front_kernel(names, *refs):
    low, full = jnp.bfloat16, jnp.float32
    r = grouped(names, refs)
    band = Band(r)
    band.meet()
    loads = types.SimpleNamespace()

    def load(k, source, target):
        copy = pltpu.make_async_copy(source, target, r.load_sem.at[k])
        copy.start()
        return copy

    loads.image = load(0, r.image, r.img.at[1 : IMAGE_ROWS + 1])
    image_edges = band.edges(0, r.image.at[0], r.image.at[IMAGE_ROWS - 1], r.img)
    loads.upstream = load(3, r.upstream_pixels, r.up)
    loads.proj_weight = load(4, r.proj_weight, r.proj_w)
    loads.conv_first = load(1, r.conv_first, r.first_w)
    loads.embed_weight = load(2, r.embed_weight, r.embed_w)
    loads.conv_second = load(5, r.conv_second, r.second_w)
    loads.caption = load(6, r.caption, r.cap)
    loads.text_weight = load(7, r.text_weight, r.text_w)
    loads.qkv_weight = load(8, r.qkv_weight, r.qkv_w)

    mine = r.items[band.row]
    same = [(r.items[band.base + b] == mine).astype(full) for b in range(SPAN)]
    masks = [jnp.full((1, C), m, full) for m in same]
    bands = masks[0]
    for m in masks[1:]:
        bands = bands + m
    per_item = 1.0 / (bands * (IMAGE_ROWS * W * (C // NORM_GROUPS)))
    before = jnp.where(band.has_above, r.items[jnp.maximum(band.row - 1, 0)], -1)
    after = jnp.where(
        band.has_below, r.items[jnp.minimum(band.row + 1, r.items.shape[0] - 1)], -1
    )
    found = types.SimpleNamespace(
        gain_one=r.norm_gains[0:1, :],
        gain_two=r.norm_gains[1:2, :],
        gain_three=r.norm_gains[2:3, :],
        bias_one=r.norm_biases[0:1, :],
        bias_two=r.norm_biases[1:2, :],
        bias_three=r.norm_biases[2:3, :],
        proj_bias=r.proj_bias[...],
        keep_above=jnp.full((1, C), (before == mine).astype(full)),
        keep_below=jnp.full((1, C), (after == mine).astype(full)),
        per_item=per_item,
    )
    for target in (r.img, r.hidden, r.middle):
        band.zero_edges(target)
    nothing = (jnp.zeros((1, C), full), jnp.zeros((1, C), full))

    def norm_of(k):
        means = band.item_means(r.window.at[k], masks, per_item)
        return means[0:1], lax.rsqrt(means[1:2] - means[0:1] * means[0:1] + epsilon)

    loads.image.wait()

    def image_sums(i, sums):
        values = r.img[i + 1].astype(full)
        return sums[0] + column_sum(values), sums[1] + column_sum(values * values)

    r.tile[0] = sums_tile(*lax.fori_loop(0, IMAGE_ROWS, image_sums, nothing))
    tiles = band.send_tile(0, r.tile.at[0], r.window.at[0])

    loads.upstream.wait()
    loads.proj_weight.wait()
    attended_grad = dot_last(r.proj_w[...], r.up[...]).astype(low)
    for h in range(HEADS):
        r.own_upstream[h] = attended_grad[h * HEAD : (h + 1) * HEAD, :]
    swaps = band.swap(0, r.own_upstream, r.upstream)
    r.upstream[band.lane] = r.own_upstream[band.lane]
    band.fill_blocks()
    slot = lax.broadcasted_iota(jnp.int32, r.embedding.shape, 0)
    chosen = jnp.where(slot == mine, r.embedding[...].astype(full), 0.0)
    chosen = jnp.sum(chosen, axis=0, keepdims=True)
    chosen = chosen / (1.0 + jnp.exp(-chosen))
    chosen = jnp.broadcast_to(chosen, (16, EMB)).astype(low)
    loads.embed_weight.wait()
    modulation = dot(chosen, r.embed_w[...])[0:1] + r.embed_bias[...]
    found.stretch = 1.0 + modulation[:, 0:C]
    found.shift = modulation[:, C:]

    def spread_rows(i, values, target):
        values = kept(i, values, found)
        from_left, from_right = side_shifts(values)
        r.shifts[0, i] = from_left.astype(low)
        r.shifts[1, i] = values.astype(low)
        r.shifts[2, i] = from_right.astype(low)
        target[pl.ds(pl.multiple_of(i * W, W), W), :] = values.astype(low)

    def conv(weight):
        total = jnp.zeros((IMAGE_ROWS * W, C), full)
        for t in range(9):
            view = r.shifts[t % 3, t // 3 : t // 3 + IMAGE_ROWS].reshape(IMAGE_ROWS * W, C)
            total = total + dot(view, weight[t * C : (t + 1) * C, :])
        return total

    for copy in tiles:
        copy.wait()
    band.wait_edges(image_edges)
    found.mean_one, found.scale_one = norm_of(0)

    def first_row(i, carry):
        unit = (r.img[i].astype(full) - found.mean_one) * found.scale_one
        normed = unit * found.gain_one + found.bias_one
        spread_rows(i, normed / (1.0 + jnp.exp(-normed)), r.act_one)
        return carry

    lax.fori_loop(0, IMAGE_ROWS + 2, first_row, 0)
    loads.conv_first.wait()
    total = conv(r.first_w) + r.conv_biases[0:1, :]
    r.hidden[1 : IMAGE_ROWS + 1] = total.reshape(IMAGE_ROWS, W, C)
    hidden_edges = band.edges(1, r.hidden.at[1], r.hidden.at[IMAGE_ROWS], r.hidden)
    r.tile[1] = sums_tile(column_sum(total), column_sum(total * total))
    tiles = band.send_tile(1, r.tile.at[1], r.window.at[1])

    loads.caption.wait()
    loads.text_weight.wait()
    words = (dot(r.cap[...], r.text_w[...]) + r.text_bias[...]).astype(low)
    for h in range(HEADS):
        parts = [words[:, k * C + h * HEAD : k * C + (h + 1) * HEAD] for k in range(2)]
        r.own_words[h] = jnp.concatenate(parts, axis=1)
    swaps = swaps + band.swap(1, r.own_words, r.words)
    r.words[band.lane] = r.own_words[band.lane]
    for copy in tiles:
        copy.wait()
    band.wait_edges(hidden_edges)
    found.mean_two, found.scale_two = norm_of(1)

    def second_row(i, carry):
        unit = (r.hidden[i] - found.mean_two) * found.scale_two
        normed = unit * found.gain_two + found.bias_two
        shifted = normed * found.stretch + found.shift
        spread_rows(i, shifted / (1.0 + jnp.exp(-shifted)), r.act_two)
        return carry

    lax.fori_loop(0, IMAGE_ROWS + 2, second_row, 0)
    loads.conv_second.wait()
    total = conv(r.second_w) + r.conv_biases[1:2, :]
    total = total + r.img[1 : IMAGE_ROWS + 1].astype(full).reshape(IMAGE_ROWS * W, C)
    r.middle[1 : IMAGE_ROWS + 1] = total.reshape(IMAGE_ROWS, W, C)
    r.tile[2] = sums_tile(column_sum(total), column_sum(total * total))
    tiles = band.send_tile(2, r.tile.at[2], r.window.at[2])
    middle_edges = band.edges(2, r.middle.at[1], r.middle.at[IMAGE_ROWS], r.middle)

    loads.qkv_weight.wait()
    for copy in tiles:
        copy.wait()
    found.mean_three, found.scale_three = norm_of(2)
    for i in range(2):
        middle = r.middle[1 + 4 * i : 5 + 4 * i].reshape(4 * W, C)
        unit = (middle - found.mean_three) * found.scale_three
        block = slice(i * 4 * W, (i + 1) * 4 * W)
        act = (unit * found.gain_three + found.bias_three).astype(low)
        r.act_three[block, :] = act
        projected = dot(act, r.qkv_w[...])
        queries = (projected[:, 0:C] + r.qv_bias[:, 0:C]).astype(low)
        keys = projected[:, C : 2 * C].astype(low)
        values = (projected[:, 2 * C :] + r.qv_bias[:, C:]).astype(low)
        queries = queries.T
        for h in range(HEADS):
            head = slice(h * HEAD, (h + 1) * HEAD)
            r.own_queries[h, :, block] = queries[head, :]
            r.own_pairs[h, block, :] = jnp.concatenate([keys[:, head], values[:, head]], axis=1)
    swaps = swaps + band.swap(2, r.own_pairs, r.pairs) + band.swap(3, r.own_queries, r.queries)
    r.pairs[band.lane] = r.own_pairs[band.lane]
    r.queries[band.lane] = r.own_queries[band.lane]
    fields = [getattr(found, name) for name in Vectors._fields]
    for i, values in enumerate(fields):
        r.vectors[i : i + 1, :] = values
    r.vectors[len(fields) : VECTOR_ROWS, :] = jnp.zeros((VECTOR_ROWS - len(fields), C), full)
    for b in range(SPAN):
        r.vectors[VECTOR_ROWS + b : VECTOR_ROWS + b + 1, :] = masks[b]
    band.wait_edges(middle_edges)
    for copy in swaps:
        copy.wait()


def front(ident, items, inputs, anywhere):
    low, full = jnp.bfloat16, jnp.float32
    pixels = IMAGE_ROWS * W
    padded = (IMAGE_ROWS + 2, W, C)
    outs = dict(
        pairs=((HEADS, pixels, 2 * HEAD), low),
        queries=((HEADS, HEAD, pixels), low),
        upstream=((HEADS, HEAD, pixels), low),
        words=((HEADS, TEXT, 2 * HEAD), low),
        act_one=((pixels + 2 * W, C), low),
        act_two=((pixels + 2 * W, C), low),
        act_three=((pixels, C), low),
        hidden=(padded, full),
        middle=(padded, full),
        vectors=((VECTOR_ROWS + SPAN, C), full),
    )
    scratch = dict(
        img=(padded, low),
        up=((pixels, C), low),
        cap=((TEXT, EMB), low),
        first_w=((9 * C, C), low),
        second_w=((9 * C, C), low),
        embed_w=((EMB, 2 * C), low),
        text_w=((EMB, 2 * C), low),
        qkv_w=((C, 3 * C), low),
        proj_w=((C, C), low),
        shifts=((3,) + padded, low),
        blocks=((C, C), low),
        tile=((3, 8, C), full),
        window=((3, SPAN, 8, C), full),
        own_pairs=((HEADS, pixels, 2 * HEAD), low),
        own_queries=((HEADS, HEAD, pixels), low),
        own_upstream=((HEADS, HEAD, pixels), low),
        own_words=((HEADS, TEXT, 2 * HEAD), low),
    )
    semaphores = dict(
        load_sem=(9,),
        edge_send=(3, 2),
        edge_recv=(3, 2),
        tile_send=(3, SPAN),
        tile_recv=(3, SPAN),
        swap_send=(4, SPAN),
        swap_recv=(4, SPAN),
    )
    return call_named(
        front_kernel, ident, dict(items=items), inputs, anywhere, outs, scratch, semaphores
    )


def hand_over_kernel(count, *refs):
    sources, targets, sem = refs[:count], refs[count : 2 * count], refs[2 * count]
    copies = [
        pltpu.make_async_copy(source, target, sem.at[k])
        for k, (source, target) in enumerate(zip(sources, targets))
    ]
    for copy in copies:
        copy.start()
    for copy in copies:
        copy.wait()


def hand_over(arrays):
    anywhere = pl.BlockSpec(memory_space=pl.ANY)
    return pl.pallas_call(
        functools.partial(hand_over_kernel, len(arrays)),
        out_shape=tuple(jax.ShapeDtypeStruct(a.shape, a.dtype) for a in arrays),
        in_specs=[pl.BlockSpec(memory_space=pltpu.VMEM)] * len(arrays),
        out_specs=(anywhere,) * len(arrays),
        scratch_shapes=[pltpu.SemaphoreType.DMA((len(arrays),))],
        name=hand_over.__name__,
    )(*arrays)


def blocks_of(rows):
    return rows.reshape(rows.shape[0], NORM_GROUPS, -1)


def spread(values):
    return jnp.repeat(values, C // NORM_GROUPS)


def in_halves(
    image,
    embedding,
    caption,
    item_of_band,
    out_grad,
    norm_gains,
    norm_biases,
    conv_first,
    conv_second,
    conv_biases,
    embed_weight,
    embed_bias,
    qkv_weight,
    qv_bias,
    text_weight,
    text_bias,
    proj_weight,
    proj_bias,
):
    low = jnp.bfloat16
    pixels = image.shape[1]
    position = lax.axis_index(ROWS)
    items = item_of_band[0]
    slots = items.shape[0]
    by_row = (-1, W, C)
    ahead = front(
        0,
        items,
        dict(
            embedding=embedding[0],
            norm_gains=norm_gains,
            norm_biases=norm_biases,
            conv_biases=conv_biases,
            embed_bias=embed_bias[None],
            qv_bias=qv_bias[None],
            text_bias=text_bias[None],
            proj_bias=proj_bias[None],
        ),
        dict(
            image=image.reshape(by_row),
            conv_first=conv_first,
            embed_weight=embed_weight,
            upstream_pixels=out_grad[0],
            proj_weight=proj_weight,
            conv_second=conv_second,
            caption=caption[0, 0],
            text_weight=text_weight,
            qkv_weight=qkv_weight,
        ),
    )
    found = attend(2, items, ahead)
    slot_of_band = (jnp.arange(slots)[:, None] == items[None, :]).astype(jnp.float32)
    row_share = EMB // lax.axis_size(ROWS)
    share = lax.dynamic_slice_in_dim(embedding[0], position * row_share, row_share, 1)
    silu_share = jax.nn.silu(share.astype(jnp.float32)).astype(low)
    out = back(
        1,
        ahead.vectors,
        jnp.repeat(slot_of_band, 128, axis=1),
        silu_share,
        embedding[0],
        dict(
            outcome=found.outcome,
            pair_grads=found.pair_grads,
            word_grads=found.word_grads,
            middle=ahead.middle,
            qkv_weight=qkv_weight,
            proj_weight=proj_weight,
            upstream=out_grad[0],
            act_three=ahead.act_three,
            caption=caption[0, 0],
            conv_second=conv_second,
            conv_first=conv_first,
            hidden=ahead.hidden,
            act_two=ahead.act_two,
            act_one=ahead.act_one,
            image=image.reshape(by_row),
            text_weight=text_weight,
            embed_weight=embed_weight,
        ),
    )
    out = types.SimpleNamespace(**dict(zip(vars(out), hand_over(list(vars(out).values())))))
    return (
        out.result[None],
        out.image_grad.reshape(1, pixels, C),
        out.embedding_grad[None],
        out.caption_grad[None, None],
        out.norm_gains_grad,
        out.norm_biases_grad,
        out.conv_first_grad,
        out.conv_second_grad,
        out.conv_biases_grad,
        out.embed_weight_grad,
        out.embed_bias_grad.reshape(-1),
        out.qkv_grad,
        out.qv_bias_grad.reshape(-1),
        out.text_grad,
        out.text_bias_grad.reshape(-1),
        out.proj_grad,
        out.proj_bias_grad.reshape(-1),
    )


def shards(
    image,
    embedding,
    caption,
    item_of_band,
    out_grad,
    norm_gains,
    norm_biases,
    conv_first,
    conv_second,
    conv_biases,
    embed_weight,
    embed_bias,
    qkv_weight,
    qv_bias,
    text_weight,
    text_bias,
    proj_weight,
    proj_bias,
):
    low = jnp.bfloat16
    full = jnp.float32
    pixels = image.shape[1]
    band_items = item_of_band[0]
    slots = band_items.shape[0]
    if slots == 2 * SPAN and lax.axis_size(ITEMS) == 2 and HEADS == SPAN:
        return in_halves(
            image,
            embedding,
            caption,
            item_of_band,
            out_grad,
            norm_gains,
            norm_biases,
            conv_first,
            conv_second,
            conv_biases,
            embed_weight,
            embed_bias,
            qkv_weight,
            qv_bias,
            text_weight,
            text_bias,
            proj_weight,
            proj_bias,
        )
    position = lax.axis_index(ROWS)
    my_item = band_items[position]
    slot_hot = (jnp.arange(slots) == my_item).astype(full)
    item_count = jnp.sum((band_items == my_item).astype(full)) * pixels * (C // NORM_GROUPS)
    reach = position + jnp.arange(-REACH, REACH + 1)
    near = (reach >= 0) & (reach < slots)
    near = near & (band_items[jnp.clip(reach, 0, slots - 1)] == my_item)
    keep = jnp.concatenate(
        [
            jnp.full((W, 1), near[REACH - 1]),
            jnp.full((pixels, 1), True),
            jnp.full((W, 1), near[REACH + 1]),
        ]
    )
    own_lead = jnp.logical_not(near[REACH - 1])

    def totals(ident, first, second, edges=None):
        sums = jnp.stack([jnp.sum(blocks_of(first), axis=(0, 2)), jnp.sum(blocks_of(second), axis=(0, 2))])
        tile = jnp.pad(sums, ((0, 6), (0, 128 - NORM_GROUPS)))
        if edges is not None:
            outcome = exchange(ident, slots, tile, (edges[:W], edges[-W:]))
        else:
            outcome = exchange(ident, slots, tile)
        summed = jnp.sum(jnp.where(near[:, None, None], outcome[0], 0.0), axis=0)
        summed = summed[:2, :NORM_GROUPS] / item_count
        return summed, outcome[1:]

    def stats(summed):
        scales = lax.rsqrt(summed[1] - summed[0] * summed[0] + epsilon)
        return spread(summed[0]), spread(scales)

    inputs = image[0].astype(full)
    summed, (above, below) = totals(0, inputs, inputs * inputs, image[0])
    means_one, scales_one = stats(summed)
    padded = jnp.concatenate([above, image[0], below]).astype(full)
    unit_padded = (padded - means_one) * scales_one
    normed_padded = unit_padded * norm_gains[0] + norm_biases[0]
    act_one_padded = jnp.where(keep, jax.nn.silu(normed_padded), 0.0).astype(low)
    unit_one = unit_padded[W:-W]
    normed_one = normed_padded[W:-W]
    taps_one = jnp.concatenate(taps_of(act_one_padded, False), axis=1)
    hidden_one = dot(taps_one, conv_first) + conv_biases[0]
    embed_silu = jax.nn.silu(embedding[0].astype(full)).astype(low)
    my_silu = dot(slot_hot.astype(low)[None], embed_silu).astype(low)
    modulation = dot(my_silu, embed_weight)[0] + embed_bias
    scale_part = modulation[:C]
    shift_part = modulation[C:]
    summed, (above, below) = totals(1, hidden_one, hidden_one * hidden_one, hidden_one)
    means_two, scales_two = stats(summed)
    hidden_padded = jnp.concatenate([above, hidden_one, below])
    unit_padded = (hidden_padded - means_two) * scales_two
    normed_padded = unit_padded * norm_gains[1] + norm_biases[1]
    shifted_padded = normed_padded * (1.0 + scale_part) + shift_part
    act_two_padded = jnp.where(keep, jax.nn.silu(shifted_padded), 0.0).astype(low)
    unit_two = unit_padded[W:-W]
    normed_two = normed_padded[W:-W]
    shifted = shifted_padded[W:-W]
    taps_two = jnp.concatenate(taps_of(act_two_padded, False), axis=1)
    middle = inputs + dot(taps_two, conv_second) + conv_biases[1]
    summed, _ = totals(2, middle, middle * middle)
    means_three, scales_three = stats(summed)
    unit_three = (middle - means_three) * scales_three
    act_three = (unit_three * norm_gains[2] + norm_biases[2]).astype(low)
    projected = dot(act_three, qkv_weight)
    queries = (projected[:, :C] + qv_bias[:C]).astype(low)
    keys_values = jnp.concatenate(
        [projected[:, C : 2 * C], projected[:, 2 * C :] + qv_bias[C:]], axis=1
    ).astype(low)
    captions = caption[0, 0]
    text_kv = lax.cond(
        own_lead,
        lambda: (dot(captions, text_weight) + text_bias).astype(low),
        lambda: jnp.zeros((TEXT, 2 * C), low),
    )
    upstream = out_grad[0]
    upstream_float = upstream.astype(full)
    attended_grad = dot_last(upstream, proj_weight).astype(low)
    group = lax.axis_index(ITEMS)
    groups = lax.axis_size(ITEMS)
    attended_low, query_low, key_value_low, text_low = attention_by_band(
        band_items, position, queries, keys_values, text_kv, attended_grad
    )
    result = middle + dot(attended_low, proj_weight) + proj_bias
    proj_weight_grad = dot_first(attended_low, upstream)
    proj_bias_grad = jnp.sum(upstream_float, axis=0)
    qkv_grad = jnp.concatenate([query_low, key_value_low], axis=1)
    qkv_weight_grad = dot_first(act_three, qkv_grad)
    qv_bias_grad = jnp.sum(
        jnp.concatenate([query_low, key_value_low[:, C:]], axis=1).astype(full), axis=0
    )
    text_weight_grad = dot_first(captions, text_low)
    text_bias_grad = jnp.sum(text_low.astype(full), axis=0)
    caption_grad = dot_last(text_low, text_weight)[None, None]
    three_grad = dot_last(qkv_grad, qkv_weight)
    gain_three = jnp.sum(three_grad * unit_three, axis=0)
    bias_three = jnp.sum(three_grad, axis=0)

    def conv_back(padded, weight):
        views = jnp.stack(taps_of(padded, True))
        return jnp.einsum(
            "tpd,tcd->pc", views, weight.reshape(9, C, C), preferred_element_type=full
        )

    def norm_back(ident, grad_unit, unit_value, scales, base, with_edges=True):
        scaled = base + grad_unit * scales
        edges = jnp.concatenate([scaled, unit_value], axis=1) if with_edges else None
        summed, around = totals(ident, grad_unit, grad_unit * unit_value, edges)
        mean_grad, mean_cross = spread(summed[0]) * scales, spread(summed[1]) * scales
        if not with_edges:
            return scaled - mean_grad - unit_value * mean_cross
        both = jnp.concatenate([around[0], edges, around[1]])
        return both[:, :C] - mean_grad - both[:, C:] * mean_cross

    middle_padded = norm_back(3, three_grad * norm_gains[2], unit_three, scales_three, upstream_float)
    middle_grad = middle_padded[W:-W]
    low_padded = jnp.where(keep, middle_padded, 0.0).astype(low)
    hidden_two_low = low_padded[W:-W]
    conv_bias_two = jnp.sum(hidden_two_low.astype(full), axis=0)
    conv_second_grad = dot_first(taps_two, hidden_two_low)
    act_two_grad = conv_back(low_padded, conv_second)
    shifted_grad = act_two_grad * silu_slope(shifted)
    modulation_grad = jnp.concatenate(
        [jnp.sum(shifted_grad * normed_two, axis=0), jnp.sum(shifted_grad, axis=0)]
    )
    normed_two_grad = shifted_grad * (1.0 + scale_part)
    gain_two = jnp.sum(normed_two_grad * unit_two, axis=0)
    bias_two = jnp.sum(normed_two_grad, axis=0)
    hidden_back = norm_back(4, normed_two_grad * norm_gains[1], unit_two, scales_two, 0.0)
    low_padded = jnp.where(keep, hidden_back, 0.0).astype(low)
    hidden_one_low = low_padded[W:-W]
    conv_bias_one = jnp.sum(hidden_one_low.astype(full), axis=0)
    conv_first_grad = dot_first(taps_one, hidden_one_low)
    act_one_grad = conv_back(low_padded, conv_first)
    normed_one_grad = act_one_grad * silu_slope(normed_one)
    gain_one = jnp.sum(normed_one_grad * unit_one, axis=0)
    bias_one = jnp.sum(normed_one_grad, axis=0)
    image_grad = norm_back(
        5, normed_one_grad * norm_gains[0], unit_one, scales_one, middle_grad, False
    )
    group_hot = (jnp.arange(groups) == group).astype(full)
    tables = group_hot[:, None, None] * slot_hot[None, :, None] * modulation_grad
    vectors = jnp.concatenate(
        [
            gain_one,
            gain_two,
            gain_three,
            bias_one,
            bias_two,
            bias_three,
            conv_bias_one,
            conv_bias_two,
            qv_bias_grad,
            text_bias_grad,
            proj_bias_grad,
        ]
    )
    small = jnp.concatenate([tables.reshape(-1, C), vectors.reshape(-1, C)])
    row_share = EMB // lax.axis_size(ROWS)
    silu_share = lax.dynamic_slice_in_dim(embed_silu, position * row_share, row_share, 1)
    grads = (conv_first_grad, conv_second_grad, qkv_weight_grad, text_weight_grad, proj_weight_grad)
    grads = [g.astype(low) for g in grads]
    small = lax.psum(small.astype(low), (ROWS, ITEMS)).astype(full)
    tables_sum = small[: groups * slots * 2].reshape(groups, slots, 2 * C).astype(low)
    part = dot_first(silu_share, jnp.take(tables_sum, group, axis=0)).astype(low)
    matrices = [lax.psum_scatter(g, ROWS, scatter_dimension=0, tiled=True) for g in grads]
    *matrices, embed_weight_grad = [
        lax.psum(m, ITEMS).astype(full) for m in matrices + [part]
    ]
    vectors_sum = small[groups * slots * 2 :]
    modulation_low = jnp.take(tables_sum, group, axis=0)
    embed_bias_grad = jnp.sum(tables_sum.astype(full), axis=(0, 1))
    embedding_grad = dot_last(modulation_low, embed_weight) * silu_slope(embedding[0].astype(full))
    return (
        result.astype(low)[None],
        image_grad[None],
        embedding_grad[None],
        caption_grad,
        vectors_sum[0:3],
        vectors_sum[3:6],
        matrices[0],
        matrices[1],
        vectors_sum[6:8],
        embed_weight_grad,
        embed_bias_grad,
        matrices[2],
        vectors_sum[8:10].reshape(-1),
        matrices[3],
        vectors_sum[10:12].reshape(-1),
        matrices[4],
        vectors_sum[12],
    )


def solution(mesh):
    in_specs = (
        P(ITEMS, ROWS, None),
        P(ITEMS, None, None),
        P(ITEMS, ROWS, None, None),
        P(ITEMS, None),
        P(ITEMS, ROWS, None),
        P(),
        P(),
        P(),
        P(),
        P(),
        P(),
        P(),
        P(),
        P(),
        P(),
        P(),
        P(),
        P(),
    )
    out_specs = (
        P(ITEMS, ROWS, None),
        P(ITEMS, ROWS, None),
        P(ITEMS, None, None),
        P(ITEMS, ROWS, None, None),
        P(),
        P(),
        P(ROWS, None),
        P(ROWS, None),
        P(),
        P(ROWS, None),
        P(),
        P(ROWS, None),
        P(),
        P(ROWS, None),
        P(),
        P(ROWS, None),
        P(),
    )
    return jax.shard_map(shards, mesh=mesh, in_specs=in_specs, out_specs=out_specs, check_vma=False)
```

```python
import functools
import types
import typing

import jax
import jax.numpy as jnp
from jax import lax
from jax.experimental import pallas as pl
from jax.experimental.pallas import tpu as pltpu
from jax.sharding import PartitionSpec as P

C = 512
HEADS = 8
HEAD = 64
EMB = 2048
TEXT = 128
NORM_GROUPS = 32
W = 64
SPAN = 8
ROWS, ITEMS = "rows", "items"


epsilon = 1e-05


def from_behind(array, axis, by):
    length = lax.axis_size(axis)
    pairs = [(i, i + by) for i in range(length) if 0 <= i + by < length]
    return lax.ppermute(array, axis, pairs)


def as_sent(array):
    return jax.tree.map(lambda a: a.astype(jnp.bfloat16) if a.dtype == jnp.float32 else a, array)


def keep_state(state):
    return state


def silu_slope(source):
    sigma = jax.nn.sigmoid(source)
    return sigma * (1.0 + source * (1.0 - sigma))


def dot_first(left_side, right_side):
    return lax.dot_general(
        left_side, right_side, (((0,), (0,)), ((), ())), preferred_element_type=jnp.float32
    )


def dot_last(left_side, right_side):
    return lax.dot_general(
        left_side, right_side, (((1,), (1,)), ((), ())), preferred_element_type=jnp.float32
    )


def head_split(source):
    return source.reshape(source.shape[0], HEADS, HEAD)


def piece_scores(query_heads, key_piece, allowed):
    key_heads = head_split(key_piece[:, :C])
    scores = jnp.einsum(
        "qhd,khd->hqk", query_heads, key_heads, preferred_element_type=jnp.float32
    ) * HEAD ** (-0.5)
    return jnp.where(allowed[None, None, :], scores, -jnp.inf)


def piece_grads(query_heads, grad_heads, log_total, row_dots, key_piece, allowed):
    scores = piece_scores(query_heads, key_piece, allowed)
    weights = jnp.exp(scores - log_total[:, :, None])
    value_heads = head_split(key_piece[:, C:])
    weight_grad = jnp.einsum(
        "qhd,khd->hqk", grad_heads, value_heads, preferred_element_type=jnp.float32
    )
    score_grad = (weights * (weight_grad - row_dots[:, :, None])).astype(jnp.bfloat16)
    outcome = []
    key_heads = head_split(key_piece[:, :C])
    query_grad = jnp.einsum(
        "hqk,khd->qhd", score_grad, key_heads, preferred_element_type=jnp.float32
    ) * HEAD ** (-0.5)
    outcome.append(query_grad.reshape(query_grad.shape[0], C))
    key_grad = jnp.einsum(
        "hqk,qhd->khd", score_grad, query_heads, preferred_element_type=jnp.float32
    ) * HEAD ** (-0.5)
    value_grad = jnp.einsum(
        "hqk,qhd->khd", weights.astype(jnp.bfloat16), grad_heads, preferred_element_type=jnp.float32
    )
    outcome.append(jnp.concatenate([key_grad.reshape(-1, C), value_grad.reshape(-1, C)], axis=1))
    return tuple(outcome)


def source_masks(band_items, source, my_item, pixels):
    slots = band_items.shape[0]
    inside = (source >= 0) & (source < slots)
    clipped = jnp.clip(source, 0, slots - 1)
    source_item = band_items[clipped]
    before_item = band_items[jnp.maximum(clipped - 1, 0)]
    same_item = inside & (source_item == my_item)
    leading = same_item & ((clipped == 0) | (before_item != source_item))
    allowed = jnp.concatenate(
        [jnp.broadcast_to(same_item, (pixels,)), jnp.broadcast_to(leading, (TEXT,))]
    )
    return (allowed, same_item)


REACH = SPAN - 1
LOG2E = 1.4426950408889634
FAR_ABOVE = 1e30
PIX = 512


def dot(left, right):
    return jnp.dot(left, right, preferred_element_type=jnp.float32)


def reach_of(here, slots):
    first = here < SPAN
    low = jnp.maximum(jnp.where(first, 0, SPAN), here - REACH)
    high = jnp.minimum(jnp.where(first, SPAN - 1, slots - 1), here + REACH)
    return low, high


def exchange_kernel(slots, with_edges, *refs):
    if with_edges:
        tile, top, bottom, window, above, below, send_sem, recv_sem, edge_send, edge_recv = refs
    else:
        tile, window, send_sem, recv_sem = refs
    here = lax.axis_index(ROWS)
    low, high = reach_of(here, slots)
    offsets = [o for o in range(-REACH, REACH + 1) if o != 0]

    def reached(offset):
        return (here + offset >= low) & (here + offset <= high)

    barrier = pltpu.get_barrier_semaphore()
    for o in offsets:

        @pl.when(reached(o))
        def _(o=o):
            pl.semaphore_signal(barrier, 1, device_id={ROWS: here + o})

    pl.semaphore_wait(barrier, high - low)

    def edge_copy(o):
        source, target, k = (top, below, 0) if o < 0 else (bottom, above, 1)
        return pltpu.make_async_remote_copy(
            source, target, edge_send.at[k], edge_recv.at[k], device_id={ROWS: here + o}
        )

    def tile_copy(o):
        return pltpu.make_async_remote_copy(
            tile,
            window.at[REACH - o],
            send_sem.at[REACH - o],
            recv_sem.at[REACH - o],
            device_id={ROWS: here + o},
        )

    if with_edges:
        for o in (-1, 1):

            @pl.when(reached(o))
            def _(o=o):
                edge_copy(o).start()

    for o in offsets:

        @pl.when(reached(o))
        def _(o=o):
            tile_copy(o).start()

        @pl.when(jnp.logical_not(reached(-o)))
        def _(o=o):
            window[REACH - o] = jnp.zeros_like(tile)

    window[REACH] = tile[...]
    if with_edges:

        @pl.when(jnp.logical_not(reached(-1)))
        def _():
            above[...] = jnp.zeros_like(above)

        @pl.when(jnp.logical_not(reached(1)))
        def _():
            below[...] = jnp.zeros_like(below)

    for o in offsets:

        @pl.when(reached(o))
        def _(o=o):
            tile_copy(o).wait_send()

        @pl.when(reached(-o))
        def _(o=o):
            tile_copy(o).wait_recv()

    if with_edges:
        for o in (-1, 1):

            @pl.when(reached(o))
            def _(o=o):
                edge_copy(o).wait_send()

            @pl.when(reached(-o))
            def _(o=o):
                edge_copy(o).wait_recv()


def exchange(ident, slots, tile, edges=None):
    vmem = pl.BlockSpec(memory_space=pltpu.VMEM)
    shapes = [jax.ShapeDtypeStruct((2 * REACH + 1,) + tile.shape, tile.dtype)]
    scratch = [pltpu.SemaphoreType.DMA((2 * REACH + 1,))] * 2
    operands = [tile]
    if edges is not None:
        shapes += [jax.ShapeDtypeStruct(e.shape, e.dtype) for e in edges]
        scratch += [pltpu.SemaphoreType.DMA((2,))] * 2
        operands += list(edges)
    return pl.pallas_call(
        functools.partial(exchange_kernel, slots, edges is not None),
        out_shape=tuple(shapes),
        in_specs=[vmem] * len(operands),
        out_specs=(vmem,) * len(shapes),
        scratch_shapes=scratch,
        compiler_params=pltpu.CompilerParams(collective_id=ident, has_side_effects=True),
        name=f"exchange_{ident}",
    )(*operands)


def attention_by_band(band_items, position, queries, keys_values, text_kv, attended_grad):
    my_item = band_items[position]
    pixels = queries.shape[0]
    own_allowed, own_same = source_masks(band_items, position, my_item, pixels)
    packed = jnp.concatenate([keys_values, text_kv], axis=0)
    pieces = [(0, packed, own_allowed, own_same)]
    for distance in range(1, SPAN):
        for offset in (distance, -distance):
            arrived = from_behind(packed, ROWS, offset)
            allowed, same_item = source_masks(band_items, position - offset, my_item, pixels)
            pieces.append((offset, arrived, allowed, same_item))
    query_heads = head_split(queries)
    row_top = jnp.full((HEADS, pixels), -jnp.inf, jnp.float32)
    weight_sum = jnp.zeros((HEADS, pixels), jnp.float32)
    for offset, key_piece, allowed, same_item in pieces:

        def gather_scores(state, key_piece=key_piece, allowed=allowed):
            top_old, sum_old = state
            scores = piece_scores(query_heads, key_piece, allowed)
            top_new = jnp.maximum(top_old, jnp.max(scores, axis=2))
            sum_new = sum_old * jnp.exp(top_old - top_new) + jnp.sum(
                jnp.exp(scores - top_new[:, :, None]), axis=2
            )
            return (top_new, sum_new)

        row_top, weight_sum = lax.cond(same_item, gather_scores, keep_state, (row_top, weight_sum))
    log_total = row_top + jnp.log(weight_sum)
    attended = jnp.zeros((pixels, HEADS, HEAD), jnp.float32)
    for offset, key_piece, allowed, same_item in pieces:

        def add_values(totals, key_piece=key_piece, allowed=allowed):
            scores = piece_scores(query_heads, key_piece, allowed)
            weights = jnp.exp(scores - log_total[:, :, None]).astype(jnp.bfloat16)
            return totals + jnp.einsum(
                "hqk,khd->qhd",
                weights,
                head_split(key_piece[:, C:]),
                preferred_element_type=jnp.float32,
            )

        attended = lax.cond(same_item, add_values, keep_state, attended)
    attended_flat = attended.reshape(pixels, C)
    row_dots = jnp.sum(
        (attended_grad.astype(jnp.float32) * attended_flat).reshape(pixels, HEADS, HEAD), axis=2
    ).T
    grad_heads = head_split(attended_grad)
    query_grad = jnp.zeros((pixels, C), jnp.float32)
    packed_grad = jnp.zeros((pixels + TEXT, 2 * C), jnp.float32)
    zero_piece = jnp.zeros((pixels + TEXT, 2 * C), jnp.float32)
    for offset, key_piece, allowed, same_item in pieces:

        def grad_both(totals, key_piece=key_piece, allowed=allowed):
            outcome = piece_grads(query_heads, grad_heads, log_total, row_dots, key_piece, allowed)
            return (totals + outcome[0], outcome[1])

        def grad_none(totals):
            return (totals, zero_piece)

        query_grad, piece_grad = lax.cond(same_item, grad_both, grad_none, query_grad)
        if offset == 0:
            packed_grad = packed_grad + piece_grad
        else:
            packed_grad = packed_grad + from_behind(
                as_sent(piece_grad), ROWS, -offset
            ).astype(jnp.float32)
    packed_low = packed_grad.astype(jnp.bfloat16)
    return (
        attended_flat.astype(jnp.bfloat16),
        query_grad.astype(jnp.bfloat16),
        packed_low[:pixels],
        packed_low[pixels:],
    )


def taps_of(rows, reverse):
    padded = rows.reshape(-1, W, rows.shape[1])
    row_list = [padded[:-2], padded[1:-1], padded[2:]]
    if reverse:
        row_list = row_list[::-1]
    zero_column = jnp.zeros_like(row_list[0][:, :1])
    views = []
    for row_view in row_list:
        left_view = jnp.concatenate([zero_column, row_view[:, :-1]], axis=1)
        right_view = jnp.concatenate([row_view[:, 1:], zero_column], axis=1)
        view_list = [left_view, row_view, right_view]
        if reverse:
            view_list = view_list[::-1]
        views = views + view_list
    return [view.reshape(-1, rows.shape[1]) for view in views]


class Vectors(typing.NamedTuple):
    mean_one: jax.Array
    scale_one: jax.Array
    gain_one: jax.Array
    bias_one: jax.Array
    mean_two: jax.Array
    scale_two: jax.Array
    gain_two: jax.Array
    bias_two: jax.Array
    mean_three: jax.Array
    scale_three: jax.Array
    gain_three: jax.Array
    bias_three: jax.Array
    stretch: jax.Array
    shift: jax.Array
    proj_bias: jax.Array
    keep_above: jax.Array
    keep_below: jax.Array
    per_item: jax.Array


def grouped(names, refs):
    found, position = types.SimpleNamespace(), 0
    for name, count in names:
        if count is None:
            setattr(found, name, refs[position])
            position += 1
        else:
            setattr(found, name, refs[position : position + count])
            position += count
    return found


def call_named(kernel, ident, scalars, inputs, anywhere, outs, scratch, semaphores):
    names = [(name, None) for name in [*scalars, *inputs, *anywhere, *outs]]
    buffers = []
    for name, entry in scratch.items():
        many = isinstance(entry, list)
        names.append((name, len(entry) if many else None))
        buffers += [pltpu.VMEM(*e) for e in (entry if many else [entry])]
    names += [(name, None) for name in semaphores]
    vmem = pl.BlockSpec(memory_space=pltpu.VMEM)
    outcome = pl.pallas_call(
        functools.partial(kernel, names),
        out_shape=tuple(jax.ShapeDtypeStruct(*o) for o in outs.values()),
        in_specs=[pl.BlockSpec(memory_space=pltpu.SMEM)] * len(scalars)
        + [vmem] * len(inputs)
        + [pl.BlockSpec(memory_space=pl.ANY)] * len(anywhere),
        out_specs=(vmem,) * len(outs),
        scratch_shapes=buffers + [pltpu.SemaphoreType.DMA(s) for s in semaphores.values()],
        compiler_params=pltpu.CompilerParams(
            collective_id=ident, has_side_effects=True, vmem_limit_bytes=60 << 20
        ),
        name=kernel.__name__,
    )(*[v for group in (scalars, inputs, anywhere) for v in dict(group).values()])
    return types.SimpleNamespace(**dict(zip(outs, outcome)))


VECTOR_ROWS = 24
FAR, NEAR, SIDE, CORE, GROUP = range(5)
CROSS = (FAR, NEAR, SIDE)
GROUP_FIRST = (GROUP, NEAR, SIDE, FAR)
STREAMS = (
    (144, C // 4, (SIDE, NEAR, FAR)),
    (144, C // 4, (NEAR, SIDE, FAR)),
    (144, C // 4, (SIDE, NEAR, FAR)),
    (144, C // 4, (NEAR, SIDE, FAR)),
    (64, C // 2, (SIDE, NEAR, FAR)),
    (64, C // 2, (NEAR, SIDE, FAR)),
    (16, 3 * C // 2, GROUP_FIRST),
    (16, C // 2, GROUP_FIRST),
)
FIRST_CONV, SECOND_CONV, WORDS, QKV, PROJ = 0, 2, 4, 6, 7
FIRST_LANDING = [sum(len(s[2]) for s in STREAMS[:k]) for k in range(len(STREAMS))]
HALF_SUMS, GROUP_SUMS = -1, -2
TAIL = (6, 4, 5, 6, 2, -1, 0, 1, 3, 2, -2, 1, 3, 2, 0, 3, 1, 0, 1, 0)
IMAGE_ROWS = 8


class Band:
    def __init__(self, r):
        self.r = r
        self.row = lax.axis_index(ROWS)
        self.group = lax.axis_index(ITEMS)
        self.lane = self.row % SPAN
        self.base = self.row - self.lane
        row = self.row
        self.place = [row // 8, (row // 4) % 2, (row // 2) % 2, row % 2, self.group]
        self.partner = [
            {ROWS: row + (1 - 2 * self.place[d]) * (8 >> d)} for d in range(CORE + 1)
        ]
        self.partner.append({ITEMS: 1 - self.group})
        self.others = [(self.lane + o) % SPAN for o in range(1, SPAN)]
        self.peers = [{ROWS: self.base + other} for other in self.others]
        self.has_above, self.has_below = self.lane > 0, self.lane < SPAN - 1

    def meet(self, further=()):
        barrier = pltpu.get_barrier_semaphore()
        targets = self.peers + list(further)
        for target in targets:
            pl.semaphore_signal(barrier, 1, device_id=target)
        pl.semaphore_wait(barrier, len(targets))

    def remote(self, source, target, send, recv, device):
        return pltpu.make_async_remote_copy(source, target, send, recv, device_id=device)

    def edges(self, k, top, bottom, target):
        r = self.r
        up = self.remote(
            top,
            target.at[IMAGE_ROWS + 1],
            r.edge_send.at[k, 0],
            r.edge_recv.at[k, 0],
            {ROWS: self.row - 1},
        )
        down = self.remote(
            bottom,
            target.at[0],
            r.edge_send.at[k, 1],
            r.edge_recv.at[k, 1],
            {ROWS: self.row + 1},
        )
        pl.when(self.has_above)(up.start)
        pl.when(self.has_below)(down.start)
        return up, down

    def wait_edges(self, pair):
        up, down = pair

        @pl.when(self.has_above)
        def _():
            up.wait_send()
            down.wait_recv()

        @pl.when(self.has_below)
        def _():
            down.wait_send()
            up.wait_recv()

    def zero_edges(self, target):
        @pl.when(jnp.logical_not(self.has_above))
        def _():
            target[0] = jnp.zeros(target.shape[1:], target.dtype)

        @pl.when(jnp.logical_not(self.has_below))
        def _():
            target[IMAGE_ROWS + 1] = jnp.zeros(target.shape[1:], target.dtype)

    def send_tile(self, k, source, target):
        r = self.r
        copies = []
        for o in range(1, SPAN):
            copies.append(
                self.remote(
                    source,
                    target.at[self.lane],
                    r.tile_send.at[k, o],
                    r.tile_recv.at[k, o],
                    self.peers[o - 1],
                )
            )
        for copy in copies:
            copy.start()
        target[self.lane] = source[...]
        return copies

    def swap(self, k, source, target, order=range(1, SPAN)):
        r = self.r
        copies = []
        for o in order:
            copies.append(
                self.remote(
                    source.at[self.others[o - 1]],
                    target.at[self.lane],
                    r.swap_send.at[k, o],
                    r.swap_recv.at[k, o],
                    self.peers[o - 1],
                )
            )
            copies[-1].start()
        return copies

    def fill_blocks(self):
        rows = lax.broadcasted_iota(jnp.int32, (C, C), 0) // (C // NORM_GROUPS)
        columns = lax.broadcasted_iota(jnp.int32, (C, C), 1) // (C // NORM_GROUPS)
        self.r.blocks[...] = jnp.where(rows == columns, 1.0, 0.0).astype(jnp.bfloat16)

    def item_means(self, window, masks, per_item):
        low, full = jnp.bfloat16, jnp.float32
        total = jnp.zeros((8, C), full)
        for b in range(SPAN):
            total = total + jnp.where(masks[b] > 0.0, window[b], 0.0)
        total = total * per_item
        coarse = total.astype(low)
        rest = total - coarse.astype(full)
        finer = rest.astype(low)
        finest = (rest - finer.astype(full)).astype(low)
        blocks = self.r.blocks[...]
        return dot(coarse, blocks) + dot(finer, blocks) + dot(finest, blocks)


def sums_tile(first, second):
    rows = lax.broadcasted_iota(jnp.int32, (8, C), 0)
    return jnp.where(rows == 0, first, jnp.where(rows == 1, second, 0.0))


def column_sum(values):
    return jnp.sum(values, axis=0, keepdims=True)


def side_shifts(values):
    rows = lax.broadcasted_iota(jnp.int32, values.shape, 0)
    from_left = jnp.where(rows == 0, 0.0, pltpu.roll(values, 1, 0))
    from_right = jnp.where(rows == W - 1, 0.0, pltpu.roll(values, W - 1, 0))
    return from_left, from_right


def kept(i, values, vec):
    keep = jnp.where(i == 0, vec.keep_above, jnp.where(i == IMAGE_ROWS + 1, vec.keep_below, 1.0))
    return jnp.where(keep > 0.0, values, 0.0)


def back_kernel(names, *refs):
    low, full = jnp.bfloat16, jnp.float32
    r = grouped(names, refs)
    band = Band(r)
    lane, group, place, partner = band.lane, band.group, band.place, band.partner
    core = place[CORE]
    remote = band.remote
    across = {ROWS: partner[CORE][ROWS], ITEMS: 1 - group}
    band.meet((partner[FAR], partner[GROUP], across))
    quad = (partner[CORE], partner[GROUP], across)
    quarter = 2 * group + core
    quarters = (2 * group + 1 - core, 2 * (1 - group) + core, 2 * (1 - group) + 1 - core)

    def columns_of(which, size):
        return pl.ds(pl.multiple_of(which * size, size), size)

    def to_quad(kind, source, target):
        copies = [
            remote(
                source(quarters[i]), target.at[i], r.quad_send.at[kind, i], r.quad_recv.at[kind, i], quad[i]
            )
            for i in range(3)
        ]
        for copy in copies:
            copy.start()
        return copies


    swaps = band.swap(0, r.pair_grads, r.head_pairs) + band.swap(1, r.word_grads, r.head_words)

    loads = types.SimpleNamespace()

    def load(k, source, target):
        copy = pltpu.make_async_copy(source, target, r.load_sem.at[k])
        copy.start()
        return copy

    loads.outcome = load(0, r.outcome, r.heads)
    loads.pair_grads = load(1, r.pair_grads.at[lane], r.head_pairs.at[lane])
    loads.word_grads = load(14, r.word_grads.at[lane], r.head_words.at[lane])
    loads.middle = load(2, r.middle, r.mid)
    loads.qkv_weight = load(3, r.qkv_weight, r.qkv_w)
    loads.proj_weight = load(4, r.proj_weight, r.proj_w)
    loads.upstream = load(5, r.upstream, r.up)
    loads.act_three = load(6, r.act_three, r.act3)
    loads.caption = load(7, r.caption, r.caps.at[0])
    loads.far_caption = load(15, r.far_caption, r.caps.at[2])
    loads.conv_second = load(8, r.conv_second, r.conv_w)
    loads.hidden = load(9, r.hidden, r.hid)
    loads.act_two = load(10, r.act_two, r.acts_two.at[0])
    loads.far_act_two = load(16, r.far_act_two, r.acts_two.at[2])
    loads.act_one = load(11, r.act_one, r.acts_one.at[0])
    loads.far_act_one = load(17, r.far_act_one, r.acts_one.at[2])
    loads.image = load(12, r.image, r.img)
    loads.text_weight = load(13, r.text_weight, r.text_w)

    sibling = types.SimpleNamespace()

    def to_sibling(k, source, target):
        copy = remote(source, target, r.sib_send.at[k], r.sib_recv.at[k], partner[CORE])
        copy.start()
        return copy

    half = pl.ds(pl.multiple_of((1 - core) * (C // 2), C // 2), C // 2)
    sibling.upstream = to_sibling(0, r.upstream.at[:, half], r.sib_up)
    sibling.act3 = to_sibling(1, r.act_three, r.sib_act3)
    sibling.cap = to_sibling(2, r.caption, r.caps.at[1])
    sibling.far_cap = to_sibling(7, r.far_caption, r.caps.at[3])

    share_copy = remote(
        r.silu_share, r.other_share, r.small_send.at[2], r.small_recv.at[2], partner[GROUP]
    )
    share_copy.start()
    for target in (r.part_two, r.part_one):
        band.zero_edges(target)

    vec = Vectors(*[r.vectors[i : i + 1, :] for i in range(len(Vectors._fields))])
    norm_one = (vec.mean_one, vec.scale_one)
    norm_two = (vec.mean_two, vec.scale_two)
    norm_three = (vec.mean_three, vec.scale_three)

    masks = [r.vectors[VECTOR_ROWS + b : VECTOR_ROWS + b + 1, :] for b in range(SPAN)]
    band.fill_blocks()

    def item_means(window):
        return band.item_means(window, masks, vec.per_item)

    class Stream:
        def __init__(self, k):
            self.k = k
            self.order = STREAMS[k][2]
            self.dims = [FAR, NEAR, SIDE, CORE, GROUP][: len(self.order) + 1]
            self.step = 0
            self.copies = []

        def at(self, ref, d, index):
            return ref.at[(slice(None),) * self.dims.index(d) + (index,)]

        def start(self):
            self.launch(r.grads[self.k])

        def launch(self, ref):
            k, step = self.k, self.step
            if step < len(self.order):
                d = self.order[step]
                self.copies = [
                    remote(
                        self.at(ref, d, 1 - place[d]),
                        r.landings[FIRST_LANDING[k] + step],
                        r.fold_send.at[k, step],
                        r.fold_recv.at[k, step],
                        partner[d],
                    )
                ]
                self.mine = self.at(ref, d, place[d])
                self.dims.remove(d)
            else:
                if GROUP in self.order:
                    places = (r.folded[k], r.whole[k - QKV], r.whole[k - QKV])
                    self.place = core
                else:
                    places = (r.folded[k],) * 3
                    self.place = quarter
                sources = (ref.at[1 - core], ref.at[core], ref.at[1 - core])
                ends = [
                    (source, target.at[self.place], device)
                    for source, target, device in zip(sources, places, quad)
                ]
                self.copies = [
                    remote(
                        source,
                        target,
                        r.fold_send.at[k, step + i],
                        r.fold_recv.at[k, step + i],
                        device,
                    )
                    for i, (source, target, device) in enumerate(ends)
                ]
                self.mine = ref.at[core]
            for copy in self.copies:
                copy.start()

        def advance(self):
            for copy in self.copies:
                copy.wait()
            if self.step < len(self.order):
                landed, mine = r.landings[FIRST_LANDING[self.k] + self.step], self.mine
                lead = landed.shape[:-2]
                pieces = 1
                for n in lead:
                    pieces *= n

                def add(i, carry):
                    index = []
                    for n in reversed(lead):
                        index.insert(0, i % n)
                        i = i // n
                    index = tuple(index)
                    total = landed[index].astype(full) + mine[index].astype(full)
                    landed[index] = total.astype(low)
                    return carry

                lax.fori_loop(0, pieces, add, 0)
                self.step += 1
                self.launch(landed)
            else:
                r.folded[self.k][self.place] = self.mine[...]
                self.step += 1

    streams = [Stream(k) for k in range(len(STREAMS))]

    def advance(*order):
        for k in order:
            streams[k].advance()

    loads.outcome.wait()
    for h in range(0, HEADS, 2):
        for k in range(2):
            pair = [r.heads[h + i, :, k * HEAD : (k + 1) * HEAD] for i in range(2)]
            r.joined[:, k * C + h * HEAD : k * C + (h + 2) * HEAD] = jnp.concatenate(pair, axis=1)
    sibling.attended = to_sibling(5, r.joined.at[:, 0:C], r.sib_attended)

    def pixel_block(ref, i, count=4):
        return ref[1 + i * count : 1 + (i + 1) * count].reshape(count * W, C)

    def unit(values, norm):
        return (values - norm[0]) * norm[1]

    def mine_of(ref, start, size):
        return ref[:, pl.ds(pl.multiple_of(start, size if size % 256 else 256), size)]

    for copy in (loads.middle, loads.qkv_weight, loads.proj_weight, loads.upstream):
        copy.wait()
    up_sum = jnp.zeros((1, C), full)
    for i in range(2):
        block = slice(i * 4 * W, (i + 1) * 4 * W)
        upstream = r.up[block, :].astype(full)
        up_sum = up_sum + column_sum(upstream)
        result = pixel_block(r.mid, i) + dot(r.joined[block, 0:C], r.proj_w[...]) + vec.proj_bias
        r.result[block, :] = result.astype(low)
        grad = dot_last(r.joined[block, C : 2 * C], r.qkv_w[:, 0:C])
        r.product[i * 4 : i * 4 + 4] = grad.reshape(4, W, C)
    sibling.upstream.wait()
    sibling.attended.wait()
    grad = dot_first(r.joined[:, 0:C], mine_of(r.up, core * (C // 2), C // 2))
    grad = grad + dot_first(r.sib_attended[...], r.sib_up[...])
    r.grads[PROJ][...] = grad.astype(low).reshape(r.grads[PROJ].shape)
    streams[PROJ].start()
    query_sum = column_sum(r.joined[:, C : 2 * C].astype(full))

    for copy in (loads.pair_grads, loads.word_grads):
        copy.wait()
    for copy in swaps:
        copy.wait()
    for h in range(0, HEADS, 2):
        for k in range(2):
            lanes = slice(k * HEAD, (k + 1) * HEAD)
            pair = [r.head_pairs[h + i, :, lanes] for i in range(2)]
            first = (2 + k) * C + h * HEAD
            r.joined[:, first : first + 2 * HEAD] = jnp.concatenate(pair, axis=1)
            pair = [r.head_words[h + i, :, lanes] for i in range(2)]
            first = k * C + h * HEAD
            r.joined_words[:, first : first + 2 * HEAD] = jnp.concatenate(pair, axis=1)
    three_half = C + (1 - core) * (3 * C // 2)
    sibling.qkv = to_sibling(
        6, r.joined.at[:, pl.ds(pl.multiple_of(three_half, C // 2), 3 * C // 2)], r.sib_qkv
    )
    word_copies = to_quad(0, lambda q: r.joined_words.at[:, columns_of(q, C // 2)], r.word_parts)
    r.own_word_part[...] = r.joined_words[:, columns_of(quarter, C // 2)]
    sibling.act2 = to_sibling(3, r.act_two, r.acts_two.at[1])
    sibling.far_act2 = to_sibling(8, r.far_act_two, r.acts_two.at[3])
    sibling.act1 = to_sibling(4, r.act_one, r.acts_one.at[1])
    sibling.far_act1 = to_sibling(9, r.far_act_one, r.acts_one.at[3])

    plain = jnp.zeros((1, C), full)
    crossed = jnp.zeros((1, C), full)
    for i in range(2):
        block = slice(i * 4 * W, (i + 1) * 4 * W)
        grad = dot_last(r.joined[block, 2 * C :], r.qkv_w[:, C:])
        grad = grad + r.product[i * 4 : i * 4 + 4].reshape(4 * W, C)
        plain = plain + column_sum(grad)
        crossed = crossed + column_sum(grad * unit(pixel_block(r.mid, i), norm_three))
        part = r.up[block, :].astype(full) + grad * (vec.gain_three * vec.scale_three)
        r.part_two[1 + i * 4 : 5 + i * 4] = part.reshape(4, W, C)
    gain_three, bias_three = crossed, plain
    r.tile[0] = sums_tile(plain * vec.gain_three, crossed * vec.gain_three)
    three_edges = band.edges(0, r.part_two.at[1], r.part_two.at[IMAGE_ROWS], r.part_two)
    tiles = band.send_tile(0, r.tile.at[0], r.window.at[0])

    for copy in (sibling.act3, sibling.qkv, loads.act_three):
        copy.wait()
    for n in range(3):
        own = mine_of(r.joined, C + core * (3 * C // 2) + n * (C // 2), C // 2)
        columns = slice(n * (C // 2), (n + 1) * (C // 2))
        grad = dot_first(r.act3[...], own)
        grad = grad + dot_first(r.sib_act3[...], r.sib_qkv[:, columns])
        r.grads[QKV][:, :, :, :, :, :, columns] = grad.astype(low).reshape(2, 2, 2, 2, 2, 16, C // 2)
    streams[QKV].start()

    for copy in (sibling.cap, sibling.far_cap, loads.caption, loads.far_caption):
        copy.wait()
    for copy in word_copies:
        copy.wait()

    def text_rows(s, carry):
        columns = pl.ds(pl.multiple_of(s * 128, 128), 128)
        grad = dot_first(r.caps[0, :, columns], r.own_word_part[...])
        for i in range(3):
            grad = grad + dot_first(r.caps[i + 1, :, columns], r.word_parts[i])
        grad = grad.astype(low)
        index = (s // 8, (s // 4) % 2, (s // 2) % 2, s % 2)
        r.grads[WORDS][index] = grad[0:64]
        r.grads[WORDS + 1][index] = grad[64:128]
        return carry

    lax.fori_loop(0, 2 ** len(CROSS) * 2, text_rows, 0)
    streams[WORDS].start()
    streams[WORDS + 1].start()
    value_sum = column_sum(r.joined[:, 3 * C :].astype(full))
    word_sum = [column_sum(r.joined_words[:, k * C : (k + 1) * C].astype(full)) for k in range(2)]

    def spread_rows(i, values):
        from_left, from_right = side_shifts(values)
        r.shifts[0, i] = from_right.astype(low)
        r.shifts[1, i] = values.astype(low)
        r.shifts[2, i] = from_left.astype(low)

    def conv_back():
        total = jnp.zeros((IMAGE_ROWS * W, C), full)
        for t in range(9):
            dy, dx = t // 3, t % 3
            view = r.shifts[dx, 2 - dy : 2 - dy + IMAGE_ROWS].reshape(IMAGE_ROWS * W, C)
            total = total + dot_last(view, r.conv_w[t * C : (t + 1) * C, :])
        return total

    def gather_shifts(landing):
        width = C // 4

        def one_row(i, carry):
            for dx in range(3):
                lanes = slice(dx * width, (dx + 1) * width)
                r.sides[0, i, :, lanes] = r.shifts[dx, i + 1, :, columns_of(quarter, width)]
            for k in range(3):
                values = landing[k, i].astype(full)
                from_left, from_right = side_shifts(values)
                r.sides[k + 1, i, :, 0:width] = from_right.astype(low)
                r.sides[k + 1, i, :, width : 2 * width] = landing[k, i]
                r.sides[k + 1, i, :, 2 * width :] = from_left.astype(low)
            return carry

        lax.fori_loop(0, IMAGE_ROWS, one_row, 0)

    def conv_grads(kind, acts, landing):
        gather_shifts(landing)
        width = C // 4
        for dy in range(3):
            grad = jnp.zeros((C, 3 * width), full)
            for k in range(4):
                sides = r.sides[k].reshape(IMAGE_ROWS * W, 3 * width)
                grad = grad + dot_first(acts[k, dy * W : dy * W + IMAGE_ROWS * W, :], sides)
            grad = grad.astype(low)
            for dx in range(3):
                begin = first = (dy * 3 + dx) * C
                while begin < first + C:
                    shard, within = divmod(begin, 288)
                    stream, offset = divmod(within, 144)
                    size = min(144 - offset, first + C - begin)
                    target = r.grads[kind + stream]
                    target[
                        shard // 8,
                        (shard // 4) % 2,
                        (shard // 2) % 2,
                        shard % 2,
                        offset : offset + size,
                    ] = grad[begin - first : begin - first + size, dx * width : (dx + 1) * width]
                    begin += size
        for j in range(2):
            streams[kind + j].start()

    for copy in tiles:
        copy.wait()
    band.wait_edges(three_edges)
    means = item_means(r.window.at[0])
    offset_three, slope_three = means[0:1] * vec.scale_three, means[1:2] * vec.scale_three

    def middle_row(i, bias):
        values = r.part_two[i] - offset_three - unit(r.mid[i], norm_three) * slope_three
        r.part_two[i] = values
        values = kept(i, values, vec)
        spread_rows(i, values)
        inside = jnp.where((i > 0) & (i <= IMAGE_ROWS), 1.0, 0.0)
        return bias + inside * column_sum(values.astype(low).astype(full))

    conv_bias_two = lax.fori_loop(0, IMAGE_ROWS + 2, middle_row, jnp.zeros((1, C), full))
    def center(q):
        return r.shifts.at[1, 1 : IMAGE_ROWS + 1, :, columns_of(q, C // 4)]

    side_copies = to_quad(1, center, r.sides_two)
    advance(PROJ)
    loads.conv_second.wait()
    loads.hidden.wait()
    r.product[...] = conv_back().reshape(IMAGE_ROWS, W, C)
    loads.conv_first = load(8, r.conv_first, r.conv_w)
    stretched = vec.stretch * vec.gain_two * vec.scale_two

    def second_row(i, sums):
        unit_two = unit(r.hid[i + 1], norm_two)
        normed = unit_two * vec.gain_two + vec.bias_two
        grad = r.product[i] * silu_slope_of(normed * vec.stretch + vec.shift)
        r.part_one[i + 1] = grad * stretched
        return sums[0] + column_sum(grad), sums[1] + column_sum(grad * unit_two)

    nothing = (jnp.zeros((1, C), full), jnp.zeros((1, C), full))
    plain, crossed = lax.fori_loop(0, IMAGE_ROWS, second_row, nothing)
    scale_grad = crossed * vec.gain_two + plain * vec.bias_two
    shift_grad = plain
    gain_two, bias_two = crossed * vec.stretch, plain * vec.stretch
    r.tile[1] = sums_tile(bias_two * vec.gain_two, gain_two * vec.gain_two)
    two_edges = band.edges(1, r.part_one.at[1], r.part_one.at[IMAGE_ROWS], r.part_one)
    tiles = band.send_tile(1, r.tile.at[1], r.window.at[1])
    for copy in (loads.act_two, loads.far_act_two, sibling.act2, sibling.far_act2):
        copy.wait()
    for copy in side_copies:
        copy.wait()
    advance(PROJ, QKV, WORDS, WORDS + 1)
    conv_grads(SECOND_CONV, r.acts_two, r.sides_two)
    advance(PROJ)
    for copy in tiles:
        copy.wait()
    band.wait_edges(two_edges)
    means = item_means(r.window.at[1])
    offset_two, slope_two = means[0:1] * vec.scale_two, means[1:2] * vec.scale_two

    def hidden_row(i, bias):
        values = r.part_one[i] - offset_two - unit(r.hid[i], norm_two) * slope_two
        values = kept(i, values, vec)
        spread_rows(i, values)
        inside = jnp.where((i > 0) & (i <= IMAGE_ROWS), 1.0, 0.0)
        return bias + inside * column_sum(values.astype(low).astype(full))

    conv_bias_one = lax.fori_loop(0, IMAGE_ROWS + 2, hidden_row, jnp.zeros((1, C), full))
    side_copies = to_quad(2, center, r.sides_one)
    advance(PROJ, QKV, WORDS, WORDS + 1)
    loads.conv_first.wait()
    loads.image.wait()
    r.product[...] = conv_back().reshape(IMAGE_ROWS, W, C)

    def first_row(i, sums):
        unit_one = unit(r.img[i].astype(full), norm_one)
        normed = unit_one * vec.gain_one + vec.bias_one
        grad = r.product[i] * silu_slope_of(normed)
        r.product[i] = grad
        return sums[0] + column_sum(grad), sums[1] + column_sum(grad * unit_one)

    plain, crossed = lax.fori_loop(0, IMAGE_ROWS, first_row, nothing)
    gain_one, bias_one = crossed, plain
    r.tile[2] = sums_tile(plain * vec.gain_one, crossed * vec.gain_one)
    tiles = band.send_tile(2, r.tile.at[2], r.window.at[2])
    rows = [
        gain_one,
        gain_two,
        gain_three,
        bias_one,
        bias_two,
        bias_three,
        conv_bias_one,
        conv_bias_two,
        query_sum,
        value_sum,
        word_sum[0],
        word_sum[1],
        up_sum,
        jnp.zeros((1, C), full),
        scale_grad,
        shift_grad,
    ]
    for i, values in enumerate(rows):
        r.own_rows[i : i + 1, :] = values
    row_copies = band.send_tile(3, r.own_rows, r.band_rows)
    for copy in (loads.act_one, loads.far_act_one, sibling.act1, sibling.far_act1):
        copy.wait()
    for copy in side_copies:
        copy.wait()
    conv_grads(FIRST_CONV, r.acts_one, r.sides_one)
    advance(PROJ, QKV, WORDS, WORDS + 1, 2, 3)
    for copy in tiles:
        copy.wait()
    means = item_means(r.window.at[2])
    offset_one, slope_one = means[0:1] * vec.scale_one, means[1:2] * vec.scale_one
    ratio = vec.gain_one * vec.scale_one

    def image_row(i, carry):
        unit_one = unit(r.img[i].astype(full), norm_one)
        values = r.part_two[i + 1] + r.product[i] * ratio - offset_one - unit_one * slope_one
        r.image_grad[i] = values
        return carry

    lax.fori_loop(0, IMAGE_ROWS, image_row, 0)

    for copy in row_copies:
        copy.wait()
    total = jnp.zeros((16, C), full)
    for b in range(SPAN):
        total = total + r.band_rows[b]
    r.half_rows[0:16, :] = total
    for b in range(SPAN):
        r.half_rows[16 + 2 * b : 18 + 2 * b, :] = r.band_rows[b, 14:16, :]
    far_copy = remote(
        r.half_rows, r.far_rows, r.small_send.at[0], r.small_recv.at[0], partner[FAR]
    )
    far_copy.start()
    loads.text_weight.wait()

    def caption_columns(n, carry):
        columns = pl.ds(pl.multiple_of(n * C, C), C)
        r.caption_grad[:, columns] = dot_last(r.joined_words[...], r.text_w[columns, :])
        return carry

    lax.fori_loop(0, EMB // C, caption_columns, 0)
    loads.embed_weight = load(13, r.embed_weight, r.text_w)
    slots = r.slot_of_band.shape[0]
    held = types.SimpleNamespace()

    def half_sums_arrived():
        far_copy.wait()
        first_half = jnp.where(place[FAR] == 0, r.half_rows[16:32, :], r.far_rows[16:32, :])
        other_half = jnp.where(place[FAR] == 0, r.far_rows[16:32, :], r.half_rows[16:32, :])
        r.group_rows[0:16, :] = r.half_rows[0:16, :] + r.far_rows[0:16, :]
        r.group_rows[16:32, :] = first_half
        r.group_rows[32:48, :] = other_half
        for k in range(2):
            table = jnp.zeros((slots, C), full)
            for b in range(2 * SPAN):
                values = r.group_rows[16 + 2 * b + k : 17 + 2 * b + k, :]
                table = table + jnp.where(r.slot_of_band[:, b * 128 : b * 128 + 1] > 0.0, values, 0.0)
            r.own_table[slots * k : slots * (k + 1), :] = table
        r.own_table[2 * slots :, :] = r.group_rows[0:16, :]
        held.group_copy = remote(
            r.own_table,
            r.other_table,
            r.small_send.at[1],
            r.small_recv.at[1],
            partner[GROUP],
        )
        held.group_copy.start()
        loads.embed_weight.wait()
        held.table = table = [r.own_table[slots * k : slots * (k + 1), :].astype(low) for k in range(2)]

        def embedding_columns(n, carry):
            columns = pl.ds(pl.multiple_of(n * C, C), C)
            grad = dot_last(table[0], r.text_w[columns, 0:C]) + dot_last(table[1], r.text_w[columns, C:])
            source = r.embedding[:, columns].astype(full)
            r.embedding_grad[:, columns] = grad * silu_slope_of(source)
            return carry

        lax.fori_loop(0, EMB // C, embedding_columns, 0)

    def group_sums_arrived():
        held.group_copy.wait()
        share_copy.wait()
        table = held.table
        for k in range(2):
            columns = slice(k * C, (k + 1) * C)
            other = r.other_table[slots * k : slots * (k + 1), :].astype(low)
            r.embed_weight_grad[:, columns] = dot_first(r.silu_share[...], table[k]) + dot_first(
                r.other_share[...], other
            )
            r.embed_bias_grad[:, columns] = column_sum(table[k].astype(full)) + column_sum(
                other.astype(full)
            )
        sums = r.own_table[2 * slots :, :] + r.other_table[2 * slots :, :]
        r.norm_gains_grad[...] = sums[0:3]
        r.norm_biases_grad[...] = sums[3:6]
        r.conv_biases_grad[...] = sums[6:8]
        for target, k in ((r.qv_bias_grad, 8), (r.text_bias_grad, 10)):
            target[:, 0:C] = sums[k : k + 1]
            target[:, C:] = sums[k + 1 : k + 2]
        r.proj_bias_grad[...] = sums[12:13]

    for k in TAIL:
        if k == HALF_SUMS:
            half_sums_arrived()
        elif k == GROUP_SUMS:
            group_sums_arrived()
        else:
            advance(k)

    def write(stream, target, first_row):
        rows, columns = STREAMS[stream][:2]
        for k in range(4):
            target[first_row : first_row + rows, k * columns : (k + 1) * columns] = r.folded[stream][
                k
            ].astype(full)

    def write_halves(stream, target):
        rows, columns = STREAMS[stream][:2]
        for side, source in ((group, r.folded[stream]), (1 - group, r.whole[stream - QKV])):
            for k in range(2):
                target[
                    pl.ds(pl.multiple_of(side * rows, rows), rows), k * columns : (k + 1) * columns
                ] = source[k].astype(full)

    for j in range(2):
        write(FIRST_CONV + j, r.conv_first_grad, j * 144)
        write(SECOND_CONV + j, r.conv_second_grad, j * 144)
        write(WORDS + j, r.text_grad, j * 64)
    write_halves(QKV, r.qkv_grad)
    write_halves(PROJ, r.proj_grad)


def silu_slope_of(source):
    sigma = 1.0 / (1.0 + jnp.exp(-source))
    return sigma * (1.0 + source * (1.0 - sigma))


def back(ident, vectors, slot_of_band, silu_share, embedding, anywhere):
    low, full = jnp.bfloat16, jnp.float32
    pixels = IMAGE_ROWS * W
    slots = slot_of_band.shape[0]
    outs = dict(
        result=((pixels, C), low),
        image_grad=((IMAGE_ROWS, W, C), full),
        caption_grad=((TEXT, EMB), full),
        conv_first_grad=((288, C), full),
        conv_second_grad=((288, C), full),
        qkv_grad=((32, 3 * C), full),
        text_grad=((128, 2 * C), full),
        proj_grad=((32, C), full),
        embedding_grad=(embedding.shape, full),
        embed_weight_grad=((silu_share.shape[1], 2 * C), full),
        norm_gains_grad=((3, C), full),
        norm_biases_grad=((3, C), full),
        conv_biases_grad=((2, C), full),
        embed_bias_grad=((1, 2 * C), full),
        qv_bias_grad=((1, 2 * C), full),
        text_bias_grad=((1, 2 * C), full),
        proj_bias_grad=((1, C), full),
    )
    padded = (IMAGE_ROWS + 2, W, C)
    scratch = dict(
        heads=((HEADS, pixels, 2 * HEAD), low),
        head_pairs=((HEADS, pixels, 2 * HEAD), low),
        head_words=((HEADS, TEXT, 2 * HEAD), low),
        joined=((pixels, 4 * C), low),
        joined_words=((TEXT, 2 * C), low),
        mid=(padded, full),
        part_two=(padded, full),
        part_one=(padded, full),
        hid=(padded, full),
        product=((IMAGE_ROWS, W, C), full),
        img=((IMAGE_ROWS, W, C), low),
        up=((pixels, C), low),
        act3=((pixels, C), low),
        conv_w=((9 * C, C), low),
        qkv_w=((C, 3 * C), low),
        proj_w=((C, C), low),
        text_w=((EMB, 2 * C), low),
        sib_up=((pixels, C // 2), low),
        sib_act3=((pixels, C), low),
        sib_attended=((pixels, C), low),
        sib_qkv=((pixels, 3 * C // 2), low),
        acts_one=((4, pixels + 2 * W, C), low),
        acts_two=((4, pixels + 2 * W, C), low),
        caps=((4, TEXT, EMB), low),
        own_word_part=((TEXT, C // 2), low),
        word_parts=((3, TEXT, C // 2), low),
        sides_one=((3, IMAGE_ROWS, W, C // 4), low),
        sides_two=((3, IMAGE_ROWS, W, C // 4), low),
        sides=((4, IMAGE_ROWS, W, 3 * C // 4), low),
        shifts=((3,) + padded, low),
        blocks=((C, C), low),
        tile=((3, 8, C), full),
        window=((3, SPAN, 8, C), full),
        own_rows=((16, C), full),
        band_rows=((SPAN, 16, C), full),
        half_rows=((32, C), full),
        far_rows=((32, C), full),
        group_rows=((48, C), full),
        own_table=((2 * slots + 16, C), full),
        other_table=((2 * slots + 16, C), full),
        other_share=(silu_share.shape, low),
    )
    def halved(stream, step):
        return ((2,) * (len(stream[2]) + 1 - step) + stream[:2], low)

    scratch.update(grads=[halved(s, 0) for s in STREAMS])
    scratch.update(landings=[halved(s, i + 1) for s in STREAMS for i in range(len(s[2]))])
    scratch.update(folded=[((2 if GROUP in s[2] else 4,) + s[:2], low) for s in STREAMS])
    scratch.update(whole=[((2,) + s[:2], low) for s in STREAMS[QKV:]])
    semaphores = dict(
        swap_send=(2, SPAN),
        swap_recv=(2, SPAN),
        load_sem=(18,),
        quad_send=(3, 3),
        quad_recv=(3, 3),
        sib_send=(10,),
        sib_recv=(10,),
        edge_send=(2, 2),
        edge_recv=(2, 2),
        tile_send=(4, SPAN),
        tile_recv=(4, SPAN),
        fold_send=(len(STREAMS), len(GROUP_FIRST) + 3),
        fold_recv=(len(STREAMS), len(GROUP_FIRST) + 3),
        small_send=(3,),
        small_recv=(3,),
    )
    inputs = dict(
        vectors=vectors, slot_of_band=slot_of_band, silu_share=silu_share, embedding=embedding
    )
    return call_named(back_kernel, ident, (), inputs, anywhere, outs, scratch, semaphores)


def attend_kernel(names, *refs):
    low, full = jnp.bfloat16, jnp.float32
    r = grouped(names, refs)
    band = Band(r)
    band.meet()
    bands, pixels = r.pairs.shape[:2]
    text = r.words.shape[1]
    scale = HEAD ** (-0.5)

    def with_units(values, rows):
        lanes = lax.broadcasted_iota(jnp.int32, (rows, 2 * HEAD), 1)
        units = jnp.where(lanes < 2, 1.0, 0.0).astype(low)
        return jnp.where(lanes < HEAD, units, values)

    def prepare(b, carry):
        r.across[b] = r.pairs[b].T
        r.valued[b] = with_units(r.pairs[b], pixels)
        r.words_across[b] = r.words[b].T
        r.words_valued[b] = with_units(r.words[b], text)
        r.pair_sums[b] = jnp.zeros((pixels, 2 * HEAD), full)
        return carry

    lax.fori_loop(0, bands, prepare, 0)

    def one_row(columns):
        rows = lax.broadcasted_iota(jnp.int32, (16, columns), 0)
        return jnp.where(rows == 0, 1.0, 0.0).astype(low)

    ones_pixels = one_row(pixels)
    ones_text = one_row(text)
    zeros = jnp.zeros((HEAD, pixels), low)

    def outcome_copy(i):
        return band.remote(
            r.own_outcome.at[i],
            r.outcome.at[band.lane],
            r.outcome_send.at[i],
            r.outcome_recv.at[band.lane],
            {ROWS: band.base + i},
        )

    def query_band(step, carry):
        i = (band.lane + 1 + step) % bands
        mine = r.items[band.base + i]
        start = 0
        allowed = []
        for b in range(bands):
            other = r.items[band.base + b]
            start = start + jnp.where(other < mine, 1, 0)
            allowed.append(other == mine)
        query = (r.queries[i].astype(full) * scale).astype(low)
        query_rhs = jnp.concatenate([query, zeros], 0)

        top = jnp.full((8, pixels), -jnp.inf, full)
        for j in range(bands):
            scores = dot(r.pairs[j], query_rhs)
            r.scores[j] = scores
            highest = jnp.max(scores.reshape(pixels // 8, 8, pixels), axis=0)
            top = jnp.where(allowed[j], jnp.maximum(top, highest), top)
        scores = dot(r.words[start], query_rhs)
        top = jnp.maximum(top, jnp.max(scores.reshape(text // 8, 8, pixels), axis=0))
        top = jnp.max(top, axis=0, keepdims=True)
        weights_text = jnp.exp2((scores - top) * LOG2E).astype(low)
        values = jnp.concatenate([r.words_across[start, HEAD:, :], ones_text], 0)
        total = dot(values, weights_text)

        for j in range(bands):
            ceiling = top + jnp.where(allowed[j], 0.0, FAR_ABOVE)
            weights = jnp.exp2((r.scores[j] - ceiling) * LOG2E).astype(low)
            r.weights[j] = weights
            values = jnp.concatenate([r.across[j, HEAD:, :], ones_pixels], 0)
            total = total + dot(values, weights)
        inverse = 1.0 / total[HEAD : HEAD + 1, :]
        attended = total[0:HEAD, :] * inverse
        grad = r.upstream[i].astype(full)
        minus_dots = -jnp.sum(grad * attended, axis=0, keepdims=True) * inverse
        grad_scaled = (grad * inverse).astype(low)
        coarse = minus_dots.astype(low)
        fine = minus_dots - coarse.astype(full)
        rows = lax.broadcasted_iota(jnp.int32, (HEAD, pixels), 0)
        extra = jnp.where(rows == 0, coarse.astype(full), jnp.where(rows == 1, fine, 0.0))
        grad_rhs = jnp.concatenate([extra.astype(low), grad_scaled], 0)
        grad_rows = jnp.concatenate([zeros, grad_scaled], 0).T
        query_rows = jnp.concatenate([query, zeros], 0).T

        steps = (weights_text.astype(full) * dot(r.words_valued[start], grad_rhs)).astype(low)
        word_sum = dot(weights_text, grad_rows) + dot(steps, query_rows)
        r.word_parts[i] = word_sum
        query_grad = dot(r.words_across[start, 0:HEAD, :], steps)
        for j in range(bands):
            for begin in range(0, pixels, pixels // 2):
                keys = slice(begin, begin + pixels // 2)
                weights = r.weights[j, keys]
                steps = (weights.astype(full) * dot(r.valued[j, keys], grad_rhs)).astype(low)
                r.pair_sums[j, keys] += dot(weights, grad_rows) + dot(steps, query_rows)
                query_grad = query_grad + dot(r.across[j, 0:HEAD, keys], steps)
        r.own_outcome[i] = jnp.concatenate(
            [attended.astype(low), (query_grad * scale).astype(low)], 0
        ).T
        pl.when(step < bands - 1)(outcome_copy(i).start)
        return carry

    lax.fori_loop(0, bands, query_band, 0)
    r.outcome[band.lane] = r.own_outcome[band.lane]

    def finish(b, carry):
        r.pair_grads[b] = r.pair_sums[b].astype(low)
        word_sum = jnp.zeros((text, 2 * HEAD), full)
        for i in range(bands):
            mine = r.items[band.base + i]
            start = 0
            for c in range(bands):
                start = start + jnp.where(r.items[band.base + c] < mine, 1, 0)
            word_sum = word_sum + jnp.where(start == b, r.word_parts[i], 0.0)
        r.word_grads[b] = word_sum.astype(low)
        return carry

    lax.fori_loop(0, bands, finish, 0)

    def wait_outcome(step, carry):
        i = (band.lane + 1 + step) % bands
        outcome_copy(i).wait_send()
        band.remote(
            r.own_outcome.at[i],
            r.outcome.at[i],
            r.outcome_send.at[i],
            r.outcome_recv.at[i],
            {ROWS: band.base + i},
        ).wait_recv()
        return carry

    lax.fori_loop(0, bands - 1, wait_outcome, 0)


def attend(ident, items, ahead):
    low, full = jnp.bfloat16, jnp.float32
    bands, pixels, _ = ahead.pairs.shape
    text = ahead.words.shape[1]
    outs = dict(
        outcome=((bands, pixels, 2 * HEAD), low),
        pair_grads=((bands, pixels, 2 * HEAD), low),
        word_grads=((bands, text, 2 * HEAD), low),
    )
    scratch = dict(
        across=((bands, 2 * HEAD, pixels), low),
        valued=((bands, pixels, 2 * HEAD), low),
        words_across=((bands, 2 * HEAD, text), low),
        words_valued=((bands, text, 2 * HEAD), low),
        scores=((bands, pixels, pixels), full),
        weights=((bands, pixels, pixels), low),
        pair_sums=((bands, pixels, 2 * HEAD), full),
        word_parts=((bands, text, 2 * HEAD), full),
        own_outcome=((bands, pixels, 2 * HEAD), low),
    )
    semaphores = dict(outcome_send=(bands,), outcome_recv=(bands,))
    inputs = dict(
        pairs=ahead.pairs, queries=ahead.queries, upstream=ahead.upstream, words=ahead.words
    )
    return call_named(
        attend_kernel, ident, dict(items=items), inputs, {}, outs, scratch, semaphores
    )


def front_kernel(names, *refs):
    low, full = jnp.bfloat16, jnp.float32
    r = grouped(names, refs)
    band = Band(r)
    partner = band.partner[GROUP]
    band.meet((partner,))
    loads = types.SimpleNamespace()

    def load(k, source, target):
        copy = pltpu.make_async_copy(source, target, r.load_sem.at[k])
        copy.start()
        return copy

    loads.image = load(0, r.image, r.img.at[1 : IMAGE_ROWS + 1])
    image_edges = band.edges(0, r.image.at[0], r.image.at[IMAGE_ROWS - 1], r.img)
    loads.upstream = load(3, r.upstream_pixels, r.up)
    loads.proj_weight = load(4, r.proj_weight, r.proj_w)
    loads.conv_first = load(1, r.conv_first, r.first_w)
    loads.embed_weight = load(2, r.embed_weight, r.embed_w)
    loads.conv_second = load(5, r.conv_second, r.second_w)
    loads.caption = load(6, r.caption, r.cap)
    loads.text_weight = load(7, r.text_weight, r.text_w)
    loads.qkv_weight = load(8, r.qkv_weight, r.qkv_w)

    def to_counterpart(k, source, target):
        copy = band.remote(source, target, r.pair_send.at[k], r.pair_recv.at[k], partner)
        copy.start()
        return copy

    pair_copies = [to_counterpart(0, r.caption, r.far_caption)]

    mine = r.items[band.row]
    same = [(r.items[band.base + b] == mine).astype(full) for b in range(SPAN)]
    masks = [jnp.full((1, C), m, full) for m in same]
    bands = masks[0]
    for m in masks[1:]:
        bands = bands + m
    per_item = 1.0 / (bands * (IMAGE_ROWS * W * (C // NORM_GROUPS)))
    before = jnp.where(band.has_above, r.items[jnp.maximum(band.row - 1, 0)], -1)
    after = jnp.where(
        band.has_below, r.items[jnp.minimum(band.row + 1, r.items.shape[0] - 1)], -1
    )
    found = types.SimpleNamespace(
        gain_one=r.norm_gains[0:1, :],
        gain_two=r.norm_gains[1:2, :],
        gain_three=r.norm_gains[2:3, :],
        bias_one=r.norm_biases[0:1, :],
        bias_two=r.norm_biases[1:2, :],
        bias_three=r.norm_biases[2:3, :],
        proj_bias=r.proj_bias[...],
        keep_above=jnp.full((1, C), (before == mine).astype(full)),
        keep_below=jnp.full((1, C), (after == mine).astype(full)),
        per_item=per_item,
    )
    for target in (r.img, r.hidden, r.middle):
        band.zero_edges(target)
    nothing = (jnp.zeros((1, C), full), jnp.zeros((1, C), full))

    def norm_of(k):
        means = band.item_means(r.window.at[k], masks, per_item)
        return means[0:1], lax.rsqrt(means[1:2] - means[0:1] * means[0:1] + epsilon)

    loads.image.wait()

    def image_sums(i, sums):
        values = r.img[i + 1].astype(full)
        return sums[0] + column_sum(values), sums[1] + column_sum(values * values)

    r.tile[0] = sums_tile(*lax.fori_loop(0, IMAGE_ROWS, image_sums, nothing))
    tiles = band.send_tile(0, r.tile.at[0], r.window.at[0])

    loads.upstream.wait()
    loads.proj_weight.wait()
    attended_grad = dot_last(r.proj_w[...], r.up[...]).astype(low)
    for h in range(HEADS):
        r.own_upstream[h] = attended_grad[h * HEAD : (h + 1) * HEAD, :]
    swaps = band.swap(0, r.own_upstream, r.upstream)
    r.upstream[band.lane] = r.own_upstream[band.lane]
    band.fill_blocks()
    slot = lax.broadcasted_iota(jnp.int32, r.embedding.shape, 0)
    chosen = jnp.where(slot == mine, r.embedding[...].astype(full), 0.0)
    chosen = jnp.sum(chosen, axis=0, keepdims=True)
    chosen = chosen / (1.0 + jnp.exp(-chosen))
    chosen = jnp.broadcast_to(chosen, (16, EMB)).astype(low)
    loads.embed_weight.wait()
    modulation = dot(chosen, r.embed_w[...])[0:1] + r.embed_bias[...]
    found.stretch = 1.0 + modulation[:, 0:C]
    found.shift = modulation[:, C:]

    def spread_rows(i, values, target):
        values = kept(i, values, found)
        from_left, from_right = side_shifts(values)
        r.shifts[0, i] = from_left.astype(low)
        r.shifts[1, i] = values.astype(low)
        r.shifts[2, i] = from_right.astype(low)
        target[pl.ds(pl.multiple_of(i * W, W), W), :] = values.astype(low)

    def conv(weight):
        total = jnp.zeros((IMAGE_ROWS * W, C), full)
        for t in range(9):
            view = r.shifts[t % 3, t // 3 : t // 3 + IMAGE_ROWS].reshape(IMAGE_ROWS * W, C)
            total = total + dot(view, weight[t * C : (t + 1) * C, :])
        return total

    for copy in tiles:
        copy.wait()
    band.wait_edges(image_edges)
    found.mean_one, found.scale_one = norm_of(0)

    def first_row(i, carry):
        unit = (r.img[i].astype(full) - found.mean_one) * found.scale_one
        normed = unit * found.gain_one + found.bias_one
        spread_rows(i, normed / (1.0 + jnp.exp(-normed)), r.act_one)
        return carry

    lax.fori_loop(0, IMAGE_ROWS + 2, first_row, 0)
    pair_copies.append(to_counterpart(1, r.act_one, r.far_act_one))
    loads.conv_first.wait()
    total = conv(r.first_w) + r.conv_biases[0:1, :]
    r.hidden[1 : IMAGE_ROWS + 1] = total.reshape(IMAGE_ROWS, W, C)
    hidden_edges = band.edges(1, r.hidden.at[1], r.hidden.at[IMAGE_ROWS], r.hidden)
    r.tile[1] = sums_tile(column_sum(total), column_sum(total * total))
    tiles = band.send_tile(1, r.tile.at[1], r.window.at[1])

    loads.caption.wait()
    loads.text_weight.wait()
    words = (dot(r.cap[...], r.text_w[...]) + r.text_bias[...]).astype(low)
    for h in range(HEADS):
        parts = [words[:, k * C + h * HEAD : k * C + (h + 1) * HEAD] for k in range(2)]
        r.own_words[h] = jnp.concatenate(parts, axis=1)
    swaps = swaps + band.swap(1, r.own_words, r.words)
    r.words[band.lane] = r.own_words[band.lane]
    for copy in tiles:
        copy.wait()
    band.wait_edges(hidden_edges)
    found.mean_two, found.scale_two = norm_of(1)

    def second_row(i, carry):
        unit = (r.hidden[i] - found.mean_two) * found.scale_two
        normed = unit * found.gain_two + found.bias_two
        shifted = normed * found.stretch + found.shift
        spread_rows(i, shifted / (1.0 + jnp.exp(-shifted)), r.act_two)
        return carry

    lax.fori_loop(0, IMAGE_ROWS + 2, second_row, 0)
    pair_copies.append(to_counterpart(2, r.act_two, r.far_act_two))
    loads.conv_second.wait()
    total = conv(r.second_w) + r.conv_biases[1:2, :]
    total = total + r.img[1 : IMAGE_ROWS + 1].astype(full).reshape(IMAGE_ROWS * W, C)
    r.middle[1 : IMAGE_ROWS + 1] = total.reshape(IMAGE_ROWS, W, C)
    r.tile[2] = sums_tile(column_sum(total), column_sum(total * total))
    tiles = band.send_tile(2, r.tile.at[2], r.window.at[2])
    middle_edges = band.edges(2, r.middle.at[1], r.middle.at[IMAGE_ROWS], r.middle)

    loads.qkv_weight.wait()
    for copy in tiles:
        copy.wait()
    found.mean_three, found.scale_three = norm_of(2)
    for i in range(2):
        middle = r.middle[1 + 4 * i : 5 + 4 * i].reshape(4 * W, C)
        unit = (middle - found.mean_three) * found.scale_three
        block = slice(i * 4 * W, (i + 1) * 4 * W)
        act = (unit * found.gain_three + found.bias_three).astype(low)
        r.act_three[block, :] = act
        projected = dot(act, r.qkv_w[...])
        queries = (projected[:, 0:C] + r.qv_bias[:, 0:C]).astype(low)
        keys = projected[:, C : 2 * C].astype(low)
        values = (projected[:, 2 * C :] + r.qv_bias[:, C:]).astype(low)
        queries = queries.T
        for h in range(HEADS):
            head = slice(h * HEAD, (h + 1) * HEAD)
            r.own_queries[h, :, block] = queries[head, :]
            r.own_pairs[h, block, :] = jnp.concatenate([keys[:, head], values[:, head]], axis=1)
    swaps = swaps + band.swap(2, r.own_pairs, r.pairs) + band.swap(3, r.own_queries, r.queries)
    r.pairs[band.lane] = r.own_pairs[band.lane]
    r.queries[band.lane] = r.own_queries[band.lane]
    fields = [getattr(found, name) for name in Vectors._fields]
    for i, values in enumerate(fields):
        r.vectors[i : i + 1, :] = values
    r.vectors[len(fields) : VECTOR_ROWS, :] = jnp.zeros((VECTOR_ROWS - len(fields), C), full)
    for b in range(SPAN):
        r.vectors[VECTOR_ROWS + b : VECTOR_ROWS + b + 1, :] = masks[b]
    band.wait_edges(middle_edges)
    for copy in swaps + pair_copies:
        copy.wait()


def front(ident, items, inputs, anywhere):
    low, full = jnp.bfloat16, jnp.float32
    pixels = IMAGE_ROWS * W
    padded = (IMAGE_ROWS + 2, W, C)
    outs = dict(
        pairs=((HEADS, pixels, 2 * HEAD), low),
        queries=((HEADS, HEAD, pixels), low),
        upstream=((HEADS, HEAD, pixels), low),
        words=((HEADS, TEXT, 2 * HEAD), low),
        act_one=((pixels + 2 * W, C), low),
        act_two=((pixels + 2 * W, C), low),
        act_three=((pixels, C), low),
        far_caption=((TEXT, EMB), low),
        far_act_one=((pixels + 2 * W, C), low),
        far_act_two=((pixels + 2 * W, C), low),
        hidden=(padded, full),
        middle=(padded, full),
        vectors=((VECTOR_ROWS + SPAN, C), full),
    )
    scratch = dict(
        img=(padded, low),
        up=((pixels, C), low),
        cap=((TEXT, EMB), low),
        first_w=((9 * C, C), low),
        second_w=((9 * C, C), low),
        embed_w=((EMB, 2 * C), low),
        text_w=((EMB, 2 * C), low),
        qkv_w=((C, 3 * C), low),
        proj_w=((C, C), low),
        shifts=((3,) + padded, low),
        blocks=((C, C), low),
        tile=((3, 8, C), full),
        window=((3, SPAN, 8, C), full),
        own_pairs=((HEADS, pixels, 2 * HEAD), low),
        own_queries=((HEADS, HEAD, pixels), low),
        own_upstream=((HEADS, HEAD, pixels), low),
        own_words=((HEADS, TEXT, 2 * HEAD), low),
    )
    semaphores = dict(
        load_sem=(9,),
        pair_send=(3,),
        pair_recv=(3,),
        edge_send=(3, 2),
        edge_recv=(3, 2),
        tile_send=(3, SPAN),
        tile_recv=(3, SPAN),
        swap_send=(4, SPAN),
        swap_recv=(4, SPAN),
    )
    return call_named(
        front_kernel, ident, dict(items=items), inputs, anywhere, outs, scratch, semaphores
    )


def hand_over_kernel(count, *refs):
    sources, targets, sem = refs[:count], refs[count : 2 * count], refs[2 * count]
    copies = [
        pltpu.make_async_copy(source, target, sem.at[k])
        for k, (source, target) in enumerate(zip(sources, targets))
    ]
    for copy in copies:
        copy.start()
    for copy in copies:
        copy.wait()


def hand_over(arrays):
    anywhere = pl.BlockSpec(memory_space=pl.ANY)
    return pl.pallas_call(
        functools.partial(hand_over_kernel, len(arrays)),
        out_shape=tuple(jax.ShapeDtypeStruct(a.shape, a.dtype) for a in arrays),
        in_specs=[pl.BlockSpec(memory_space=pltpu.VMEM)] * len(arrays),
        out_specs=(anywhere,) * len(arrays),
        scratch_shapes=[pltpu.SemaphoreType.DMA((len(arrays),))],
        name=hand_over.__name__,
    )(*arrays)


def blocks_of(rows):
    return rows.reshape(rows.shape[0], NORM_GROUPS, -1)


def spread(values):
    return jnp.repeat(values, C // NORM_GROUPS)


def in_halves(
    image,
    embedding,
    caption,
    item_of_band,
    out_grad,
    norm_gains,
    norm_biases,
    conv_first,
    conv_second,
    conv_biases,
    embed_weight,
    embed_bias,
    qkv_weight,
    qv_bias,
    text_weight,
    text_bias,
    proj_weight,
    proj_bias,
):
    low = jnp.bfloat16
    pixels = image.shape[1]
    position = lax.axis_index(ROWS)
    items = item_of_band[0]
    slots = items.shape[0]
    by_row = (-1, W, C)
    ahead = front(
        0,
        items,
        dict(
            embedding=embedding[0],
            norm_gains=norm_gains,
            norm_biases=norm_biases,
            conv_biases=conv_biases,
            embed_bias=embed_bias[None],
            qv_bias=qv_bias[None],
            text_bias=text_bias[None],
            proj_bias=proj_bias[None],
        ),
        dict(
            image=image.reshape(by_row),
            conv_first=conv_first,
            embed_weight=embed_weight,
            upstream_pixels=out_grad[0],
            proj_weight=proj_weight,
            conv_second=conv_second,
            caption=caption[0, 0],
            text_weight=text_weight,
            qkv_weight=qkv_weight,
        ),
    )
    found = attend(2, items, ahead)
    slot_of_band = (jnp.arange(slots)[:, None] == items[None, :]).astype(jnp.float32)
    row_share = EMB // lax.axis_size(ROWS)
    share = lax.dynamic_slice_in_dim(embedding[0], position * row_share, row_share, 1)
    silu_share = jax.nn.silu(share.astype(jnp.float32)).astype(low)
    out = back(
        1,
        ahead.vectors,
        jnp.repeat(slot_of_band, 128, axis=1),
        silu_share,
        embedding[0],
        dict(
            outcome=found.outcome,
            pair_grads=found.pair_grads,
            word_grads=found.word_grads,
            middle=ahead.middle,
            qkv_weight=qkv_weight,
            proj_weight=proj_weight,
            upstream=out_grad[0],
            act_three=ahead.act_three,
            caption=caption[0, 0],
            conv_second=conv_second,
            conv_first=conv_first,
            hidden=ahead.hidden,
            act_two=ahead.act_two,
            act_one=ahead.act_one,
            far_caption=ahead.far_caption,
            far_act_one=ahead.far_act_one,
            far_act_two=ahead.far_act_two,
            image=image.reshape(by_row),
            text_weight=text_weight,
            embed_weight=embed_weight,
        ),
    )
    out = types.SimpleNamespace(**dict(zip(vars(out), hand_over(list(vars(out).values())))))
    return (
        out.result[None],
        out.image_grad.reshape(1, pixels, C),
        out.embedding_grad[None],
        out.caption_grad[None, None],
        out.norm_gains_grad,
        out.norm_biases_grad,
        out.conv_first_grad,
        out.conv_second_grad,
        out.conv_biases_grad,
        out.embed_weight_grad,
        out.embed_bias_grad.reshape(-1),
        out.qkv_grad,
        out.qv_bias_grad.reshape(-1),
        out.text_grad,
        out.text_bias_grad.reshape(-1),
        out.proj_grad,
        out.proj_bias_grad.reshape(-1),
    )


def shards(
    image,
    embedding,
    caption,
    item_of_band,
    out_grad,
    norm_gains,
    norm_biases,
    conv_first,
    conv_second,
    conv_biases,
    embed_weight,
    embed_bias,
    qkv_weight,
    qv_bias,
    text_weight,
    text_bias,
    proj_weight,
    proj_bias,
):
    low = jnp.bfloat16
    full = jnp.float32
    pixels = image.shape[1]
    band_items = item_of_band[0]
    slots = band_items.shape[0]
    if slots == 2 * SPAN and lax.axis_size(ITEMS) == 2 and HEADS == SPAN:
        return in_halves(
            image,
            embedding,
            caption,
            item_of_band,
            out_grad,
            norm_gains,
            norm_biases,
            conv_first,
            conv_second,
            conv_biases,
            embed_weight,
            embed_bias,
            qkv_weight,
            qv_bias,
            text_weight,
            text_bias,
            proj_weight,
            proj_bias,
        )
    position = lax.axis_index(ROWS)
    my_item = band_items[position]
    slot_hot = (jnp.arange(slots) == my_item).astype(full)
    item_count = jnp.sum((band_items == my_item).astype(full)) * pixels * (C // NORM_GROUPS)
    reach = position + jnp.arange(-REACH, REACH + 1)
    near = (reach >= 0) & (reach < slots)
    near = near & (band_items[jnp.clip(reach, 0, slots - 1)] == my_item)
    keep = jnp.concatenate(
        [
            jnp.full((W, 1), near[REACH - 1]),
            jnp.full((pixels, 1), True),
            jnp.full((W, 1), near[REACH + 1]),
        ]
    )
    own_lead = jnp.logical_not(near[REACH - 1])

    def totals(ident, first, second, edges=None):
        sums = jnp.stack([jnp.sum(blocks_of(first), axis=(0, 2)), jnp.sum(blocks_of(second), axis=(0, 2))])
        tile = jnp.pad(sums, ((0, 6), (0, 128 - NORM_GROUPS)))
        if edges is not None:
            outcome = exchange(ident, slots, tile, (edges[:W], edges[-W:]))
        else:
            outcome = exchange(ident, slots, tile)
        summed = jnp.sum(jnp.where(near[:, None, None], outcome[0], 0.0), axis=0)
        summed = summed[:2, :NORM_GROUPS] / item_count
        return summed, outcome[1:]

    def stats(summed):
        scales = lax.rsqrt(summed[1] - summed[0] * summed[0] + epsilon)
        return spread(summed[0]), spread(scales)

    inputs = image[0].astype(full)
    summed, (above, below) = totals(0, inputs, inputs * inputs, image[0])
    means_one, scales_one = stats(summed)
    padded = jnp.concatenate([above, image[0], below]).astype(full)
    unit_padded = (padded - means_one) * scales_one
    normed_padded = unit_padded * norm_gains[0] + norm_biases[0]
    act_one_padded = jnp.where(keep, jax.nn.silu(normed_padded), 0.0).astype(low)
    unit_one = unit_padded[W:-W]
    normed_one = normed_padded[W:-W]
    taps_one = jnp.concatenate(taps_of(act_one_padded, False), axis=1)
    hidden_one = dot(taps_one, conv_first) + conv_biases[0]
    embed_silu = jax.nn.silu(embedding[0].astype(full)).astype(low)
    my_silu = dot(slot_hot.astype(low)[None], embed_silu).astype(low)
    modulation = dot(my_silu, embed_weight)[0] + embed_bias
    scale_part = modulation[:C]
    shift_part = modulation[C:]
    summed, (above, below) = totals(1, hidden_one, hidden_one * hidden_one, hidden_one)
    means_two, scales_two = stats(summed)
    hidden_padded = jnp.concatenate([above, hidden_one, below])
    unit_padded = (hidden_padded - means_two) * scales_two
    normed_padded = unit_padded * norm_gains[1] + norm_biases[1]
    shifted_padded = normed_padded * (1.0 + scale_part) + shift_part
    act_two_padded = jnp.where(keep, jax.nn.silu(shifted_padded), 0.0).astype(low)
    unit_two = unit_padded[W:-W]
    normed_two = normed_padded[W:-W]
    shifted = shifted_padded[W:-W]
    taps_two = jnp.concatenate(taps_of(act_two_padded, False), axis=1)
    middle = inputs + dot(taps_two, conv_second) + conv_biases[1]
    summed, _ = totals(2, middle, middle * middle)
    means_three, scales_three = stats(summed)
    unit_three = (middle - means_three) * scales_three
    act_three = (unit_three * norm_gains[2] + norm_biases[2]).astype(low)
    projected = dot(act_three, qkv_weight)
    queries = (projected[:, :C] + qv_bias[:C]).astype(low)
    keys_values = jnp.concatenate(
        [projected[:, C : 2 * C], projected[:, 2 * C :] + qv_bias[C:]], axis=1
    ).astype(low)
    captions = caption[0, 0]
    text_kv = lax.cond(
        own_lead,
        lambda: (dot(captions, text_weight) + text_bias).astype(low),
        lambda: jnp.zeros((TEXT, 2 * C), low),
    )
    upstream = out_grad[0]
    upstream_float = upstream.astype(full)
    attended_grad = dot_last(upstream, proj_weight).astype(low)
    group = lax.axis_index(ITEMS)
    groups = lax.axis_size(ITEMS)
    attended_low, query_low, key_value_low, text_low = attention_by_band(
        band_items, position, queries, keys_values, text_kv, attended_grad
    )
    result = middle + dot(attended_low, proj_weight) + proj_bias
    proj_weight_grad = dot_first(attended_low, upstream)
    proj_bias_grad = jnp.sum(upstream_float, axis=0)
    qkv_grad = jnp.concatenate([query_low, key_value_low], axis=1)
    qkv_weight_grad = dot_first(act_three, qkv_grad)
    qv_bias_grad = jnp.sum(
        jnp.concatenate([query_low, key_value_low[:, C:]], axis=1).astype(full), axis=0
    )
    text_weight_grad = dot_first(captions, text_low)
    text_bias_grad = jnp.sum(text_low.astype(full), axis=0)
    caption_grad = dot_last(text_low, text_weight)[None, None]
    three_grad = dot_last(qkv_grad, qkv_weight)
    gain_three = jnp.sum(three_grad * unit_three, axis=0)
    bias_three = jnp.sum(three_grad, axis=0)

    def conv_back(padded, weight):
        views = jnp.stack(taps_of(padded, True))
        return jnp.einsum(
            "tpd,tcd->pc", views, weight.reshape(9, C, C), preferred_element_type=full
        )

    def norm_back(ident, grad_unit, unit_value, scales, base, with_edges=True):
        scaled = base + grad_unit * scales
        edges = jnp.concatenate([scaled, unit_value], axis=1) if with_edges else None
        summed, around = totals(ident, grad_unit, grad_unit * unit_value, edges)
        mean_grad, mean_cross = spread(summed[0]) * scales, spread(summed[1]) * scales
        if not with_edges:
            return scaled - mean_grad - unit_value * mean_cross
        both = jnp.concatenate([around[0], edges, around[1]])
        return both[:, :C] - mean_grad - both[:, C:] * mean_cross

    middle_padded = norm_back(3, three_grad * norm_gains[2], unit_three, scales_three, upstream_float)
    middle_grad = middle_padded[W:-W]
    low_padded = jnp.where(keep, middle_padded, 0.0).astype(low)
    hidden_two_low = low_padded[W:-W]
    conv_bias_two = jnp.sum(hidden_two_low.astype(full), axis=0)
    conv_second_grad = dot_first(taps_two, hidden_two_low)
    act_two_grad = conv_back(low_padded, conv_second)
    shifted_grad = act_two_grad * silu_slope(shifted)
    modulation_grad = jnp.concatenate(
        [jnp.sum(shifted_grad * normed_two, axis=0), jnp.sum(shifted_grad, axis=0)]
    )
    normed_two_grad = shifted_grad * (1.0 + scale_part)
    gain_two = jnp.sum(normed_two_grad * unit_two, axis=0)
    bias_two = jnp.sum(normed_two_grad, axis=0)
    hidden_back = norm_back(4, normed_two_grad * norm_gains[1], unit_two, scales_two, 0.0)
    low_padded = jnp.where(keep, hidden_back, 0.0).astype(low)
    hidden_one_low = low_padded[W:-W]
    conv_bias_one = jnp.sum(hidden_one_low.astype(full), axis=0)
    conv_first_grad = dot_first(taps_one, hidden_one_low)
    act_one_grad = conv_back(low_padded, conv_first)
    normed_one_grad = act_one_grad * silu_slope(normed_one)
    gain_one = jnp.sum(normed_one_grad * unit_one, axis=0)
    bias_one = jnp.sum(normed_one_grad, axis=0)
    image_grad = norm_back(
        5, normed_one_grad * norm_gains[0], unit_one, scales_one, middle_grad, False
    )
    group_hot = (jnp.arange(groups) == group).astype(full)
    tables = group_hot[:, None, None] * slot_hot[None, :, None] * modulation_grad
    vectors = jnp.concatenate(
        [
            gain_one,
            gain_two,
            gain_three,
            bias_one,
            bias_two,
            bias_three,
            conv_bias_one,
            conv_bias_two,
            qv_bias_grad,
            text_bias_grad,
            proj_bias_grad,
        ]
    )
    small = jnp.concatenate([tables.reshape(-1, C), vectors.reshape(-1, C)])
    row_share = EMB // lax.axis_size(ROWS)
    silu_share = lax.dynamic_slice_in_dim(embed_silu, position * row_share, row_share, 1)
    grads = (conv_first_grad, conv_second_grad, qkv_weight_grad, text_weight_grad, proj_weight_grad)
    grads = [g.astype(low) for g in grads]
    small = lax.psum(small.astype(low), (ROWS, ITEMS)).astype(full)
    tables_sum = small[: groups * slots * 2].reshape(groups, slots, 2 * C).astype(low)
    part = dot_first(silu_share, jnp.take(tables_sum, group, axis=0)).astype(low)
    matrices = [lax.psum_scatter(g, ROWS, scatter_dimension=0, tiled=True) for g in grads]
    *matrices, embed_weight_grad = [
        lax.psum(m, ITEMS).astype(full) for m in matrices + [part]
    ]
    vectors_sum = small[groups * slots * 2 :]
    modulation_low = jnp.take(tables_sum, group, axis=0)
    embed_bias_grad = jnp.sum(tables_sum.astype(full), axis=(0, 1))
    embedding_grad = dot_last(modulation_low, embed_weight) * silu_slope(embedding[0].astype(full))
    return (
        result.astype(low)[None],
        image_grad[None],
        embedding_grad[None],
        caption_grad,
        vectors_sum[0:3],
        vectors_sum[3:6],
        matrices[0],
        matrices[1],
        vectors_sum[6:8],
        embed_weight_grad,
        embed_bias_grad,
        matrices[2],
        vectors_sum[8:10].reshape(-1),
        matrices[3],
        vectors_sum[10:12].reshape(-1),
        matrices[4],
        vectors_sum[12],
    )


def solution(mesh):
    in_specs = (
        P(ITEMS, ROWS, None),
        P(ITEMS, None, None),
        P(ITEMS, ROWS, None, None),
        P(ITEMS, None),
        P(ITEMS, ROWS, None),
        P(),
        P(),
        P(),
        P(),
        P(),
        P(),
        P(),
        P(),
        P(),
        P(),
        P(),
        P(),
        P(),
    )
    out_specs = (
        P(ITEMS, ROWS, None),
        P(ITEMS, ROWS, None),
        P(ITEMS, None, None),
        P(ITEMS, ROWS, None, None),
        P(),
        P(),
        P(ROWS, None),
        P(ROWS, None),
        P(),
        P(ROWS, None),
        P(),
        P(ROWS, None),
        P(),
        P(ROWS, None),
        P(),
        P(ROWS, None),
        P(),
    )
    return jax.shard_map(shards, mesh=mesh, in_specs=in_specs, out_specs=out_specs, check_vma=False)
```

```python
import functools
import types
import typing

import jax
import jax.numpy as jnp
from jax import lax
from jax.experimental import pallas as pl
from jax.experimental.pallas import tpu as pltpu
from jax.sharding import PartitionSpec as P

C = 512
HEADS = 8
HEAD = 64
EMB = 2048
TEXT = 128
NORM_GROUPS = 32
W = 64
SPAN = 8
ROWS, ITEMS = "rows", "items"


epsilon = 1e-05


def from_behind(array, axis, by):
    length = lax.axis_size(axis)
    pairs = [(i, i + by) for i in range(length) if 0 <= i + by < length]
    return lax.ppermute(array, axis, pairs)


def as_sent(array):
    return jax.tree.map(lambda a: a.astype(jnp.bfloat16) if a.dtype == jnp.float32 else a, array)


def keep_state(state):
    return state


def silu_slope(source):
    sigma = jax.nn.sigmoid(source)
    return sigma * (1.0 + source * (1.0 - sigma))


def dot_first(left_side, right_side):
    return lax.dot_general(
        left_side, right_side, (((0,), (0,)), ((), ())), preferred_element_type=jnp.float32
    )


def dot_last(left_side, right_side):
    return lax.dot_general(
        left_side, right_side, (((1,), (1,)), ((), ())), preferred_element_type=jnp.float32
    )


def head_split(source):
    return source.reshape(source.shape[0], HEADS, HEAD)


def piece_scores(query_heads, key_piece, allowed):
    key_heads = head_split(key_piece[:, :C])
    scores = jnp.einsum(
        "qhd,khd->hqk", query_heads, key_heads, preferred_element_type=jnp.float32
    ) * HEAD ** (-0.5)
    return jnp.where(allowed[None, None, :], scores, -jnp.inf)


def piece_grads(query_heads, grad_heads, log_total, row_dots, key_piece, allowed):
    scores = piece_scores(query_heads, key_piece, allowed)
    weights = jnp.exp(scores - log_total[:, :, None])
    value_heads = head_split(key_piece[:, C:])
    weight_grad = jnp.einsum(
        "qhd,khd->hqk", grad_heads, value_heads, preferred_element_type=jnp.float32
    )
    score_grad = (weights * (weight_grad - row_dots[:, :, None])).astype(jnp.bfloat16)
    outcome = []
    key_heads = head_split(key_piece[:, :C])
    query_grad = jnp.einsum(
        "hqk,khd->qhd", score_grad, key_heads, preferred_element_type=jnp.float32
    ) * HEAD ** (-0.5)
    outcome.append(query_grad.reshape(query_grad.shape[0], C))
    key_grad = jnp.einsum(
        "hqk,qhd->khd", score_grad, query_heads, preferred_element_type=jnp.float32
    ) * HEAD ** (-0.5)
    value_grad = jnp.einsum(
        "hqk,qhd->khd", weights.astype(jnp.bfloat16), grad_heads, preferred_element_type=jnp.float32
    )
    outcome.append(jnp.concatenate([key_grad.reshape(-1, C), value_grad.reshape(-1, C)], axis=1))
    return tuple(outcome)


def source_masks(band_items, source, my_item, pixels):
    slots = band_items.shape[0]
    inside = (source >= 0) & (source < slots)
    clipped = jnp.clip(source, 0, slots - 1)
    source_item = band_items[clipped]
    before_item = band_items[jnp.maximum(clipped - 1, 0)]
    same_item = inside & (source_item == my_item)
    leading = same_item & ((clipped == 0) | (before_item != source_item))
    allowed = jnp.concatenate(
        [jnp.broadcast_to(same_item, (pixels,)), jnp.broadcast_to(leading, (TEXT,))]
    )
    return (allowed, same_item)


REACH = SPAN - 1
LOG2E = 1.4426950408889634
FAR_ABOVE = 1e30
PIX = 512


def dot(left, right):
    return jnp.dot(left, right, preferred_element_type=jnp.float32)


def reach_of(here, slots):
    first = here < SPAN
    low = jnp.maximum(jnp.where(first, 0, SPAN), here - REACH)
    high = jnp.minimum(jnp.where(first, SPAN - 1, slots - 1), here + REACH)
    return low, high


def exchange_kernel(slots, with_edges, *refs):
    if with_edges:
        tile, top, bottom, window, above, below, send_sem, recv_sem, edge_send, edge_recv = refs
    else:
        tile, window, send_sem, recv_sem = refs
    here = lax.axis_index(ROWS)
    low, high = reach_of(here, slots)
    offsets = [o for o in range(-REACH, REACH + 1) if o != 0]

    def reached(offset):
        return (here + offset >= low) & (here + offset <= high)

    barrier = pltpu.get_barrier_semaphore()
    for o in offsets:

        @pl.when(reached(o))
        def _(o=o):
            pl.semaphore_signal(barrier, 1, device_id={ROWS: here + o})

    pl.semaphore_wait(barrier, high - low)

    def edge_copy(o):
        source, target, k = (top, below, 0) if o < 0 else (bottom, above, 1)
        return pltpu.make_async_remote_copy(
            source, target, edge_send.at[k], edge_recv.at[k], device_id={ROWS: here + o}
        )

    def tile_copy(o):
        return pltpu.make_async_remote_copy(
            tile,
            window.at[REACH - o],
            send_sem.at[REACH - o],
            recv_sem.at[REACH - o],
            device_id={ROWS: here + o},
        )

    if with_edges:
        for o in (-1, 1):

            @pl.when(reached(o))
            def _(o=o):
                edge_copy(o).start()

    for o in offsets:

        @pl.when(reached(o))
        def _(o=o):
            tile_copy(o).start()

        @pl.when(jnp.logical_not(reached(-o)))
        def _(o=o):
            window[REACH - o] = jnp.zeros_like(tile)

    window[REACH] = tile[...]
    if with_edges:

        @pl.when(jnp.logical_not(reached(-1)))
        def _():
            above[...] = jnp.zeros_like(above)

        @pl.when(jnp.logical_not(reached(1)))
        def _():
            below[...] = jnp.zeros_like(below)

    for o in offsets:

        @pl.when(reached(o))
        def _(o=o):
            tile_copy(o).wait_send()

        @pl.when(reached(-o))
        def _(o=o):
            tile_copy(o).wait_recv()

    if with_edges:
        for o in (-1, 1):

            @pl.when(reached(o))
            def _(o=o):
                edge_copy(o).wait_send()

            @pl.when(reached(-o))
            def _(o=o):
                edge_copy(o).wait_recv()


def exchange(ident, slots, tile, edges=None):
    vmem = pl.BlockSpec(memory_space=pltpu.VMEM)
    shapes = [jax.ShapeDtypeStruct((2 * REACH + 1,) + tile.shape, tile.dtype)]
    scratch = [pltpu.SemaphoreType.DMA((2 * REACH + 1,))] * 2
    operands = [tile]
    if edges is not None:
        shapes += [jax.ShapeDtypeStruct(e.shape, e.dtype) for e in edges]
        scratch += [pltpu.SemaphoreType.DMA((2,))] * 2
        operands += list(edges)
    return pl.pallas_call(
        functools.partial(exchange_kernel, slots, edges is not None),
        out_shape=tuple(shapes),
        in_specs=[vmem] * len(operands),
        out_specs=(vmem,) * len(shapes),
        scratch_shapes=scratch,
        compiler_params=pltpu.CompilerParams(collective_id=ident, has_side_effects=True),
        name=f"exchange_{ident}",
    )(*operands)


def attention_by_band(band_items, position, queries, keys_values, text_kv, attended_grad):
    my_item = band_items[position]
    pixels = queries.shape[0]
    own_allowed, own_same = source_masks(band_items, position, my_item, pixels)
    packed = jnp.concatenate([keys_values, text_kv], axis=0)
    pieces = [(0, packed, own_allowed, own_same)]
    for distance in range(1, SPAN):
        for offset in (distance, -distance):
            arrived = from_behind(packed, ROWS, offset)
            allowed, same_item = source_masks(band_items, position - offset, my_item, pixels)
            pieces.append((offset, arrived, allowed, same_item))
    query_heads = head_split(queries)
    row_top = jnp.full((HEADS, pixels), -jnp.inf, jnp.float32)
    weight_sum = jnp.zeros((HEADS, pixels), jnp.float32)
    for offset, key_piece, allowed, same_item in pieces:

        def gather_scores(state, key_piece=key_piece, allowed=allowed):
            top_old, sum_old = state
            scores = piece_scores(query_heads, key_piece, allowed)
            top_new = jnp.maximum(top_old, jnp.max(scores, axis=2))
            sum_new = sum_old * jnp.exp(top_old - top_new) + jnp.sum(
                jnp.exp(scores - top_new[:, :, None]), axis=2
            )
            return (top_new, sum_new)

        row_top, weight_sum = lax.cond(same_item, gather_scores, keep_state, (row_top, weight_sum))
    log_total = row_top + jnp.log(weight_sum)
    attended = jnp.zeros((pixels, HEADS, HEAD), jnp.float32)
    for offset, key_piece, allowed, same_item in pieces:

        def add_values(totals, key_piece=key_piece, allowed=allowed):
            scores = piece_scores(query_heads, key_piece, allowed)
            weights = jnp.exp(scores - log_total[:, :, None]).astype(jnp.bfloat16)
            return totals + jnp.einsum(
                "hqk,khd->qhd",
                weights,
                head_split(key_piece[:, C:]),
                preferred_element_type=jnp.float32,
            )

        attended = lax.cond(same_item, add_values, keep_state, attended)
    attended_flat = attended.reshape(pixels, C)
    row_dots = jnp.sum(
        (attended_grad.astype(jnp.float32) * attended_flat).reshape(pixels, HEADS, HEAD), axis=2
    ).T
    grad_heads = head_split(attended_grad)
    query_grad = jnp.zeros((pixels, C), jnp.float32)
    packed_grad = jnp.zeros((pixels + TEXT, 2 * C), jnp.float32)
    zero_piece = jnp.zeros((pixels + TEXT, 2 * C), jnp.float32)
    for offset, key_piece, allowed, same_item in pieces:

        def grad_both(totals, key_piece=key_piece, allowed=allowed):
            outcome = piece_grads(query_heads, grad_heads, log_total, row_dots, key_piece, allowed)
            return (totals + outcome[0], outcome[1])

        def grad_none(totals):
            return (totals, zero_piece)

        query_grad, piece_grad = lax.cond(same_item, grad_both, grad_none, query_grad)
        if offset == 0:
            packed_grad = packed_grad + piece_grad
        else:
            packed_grad = packed_grad + from_behind(
                as_sent(piece_grad), ROWS, -offset
            ).astype(jnp.float32)
    packed_low = packed_grad.astype(jnp.bfloat16)
    return (
        attended_flat.astype(jnp.bfloat16),
        query_grad.astype(jnp.bfloat16),
        packed_low[:pixels],
        packed_low[pixels:],
    )


def taps_of(rows, reverse):
    padded = rows.reshape(-1, W, rows.shape[1])
    row_list = [padded[:-2], padded[1:-1], padded[2:]]
    if reverse:
        row_list = row_list[::-1]
    zero_column = jnp.zeros_like(row_list[0][:, :1])
    views = []
    for row_view in row_list:
        left_view = jnp.concatenate([zero_column, row_view[:, :-1]], axis=1)
        right_view = jnp.concatenate([row_view[:, 1:], zero_column], axis=1)
        view_list = [left_view, row_view, right_view]
        if reverse:
            view_list = view_list[::-1]
        views = views + view_list
    return [view.reshape(-1, rows.shape[1]) for view in views]


class Vectors(typing.NamedTuple):
    mean_one: jax.Array
    scale_one: jax.Array
    gain_one: jax.Array
    bias_one: jax.Array
    mean_two: jax.Array
    scale_two: jax.Array
    gain_two: jax.Array
    bias_two: jax.Array
    mean_three: jax.Array
    scale_three: jax.Array
    gain_three: jax.Array
    bias_three: jax.Array
    stretch: jax.Array
    shift: jax.Array
    proj_bias: jax.Array
    keep_above: jax.Array
    keep_below: jax.Array
    per_item: jax.Array


def grouped(names, refs):
    found, position = types.SimpleNamespace(), 0
    for name, count in names:
        if count is None:
            setattr(found, name, refs[position])
            position += 1
        else:
            setattr(found, name, refs[position : position + count])
            position += count
    return found


def call_named(kernel, ident, scalars, inputs, anywhere, outs, scratch, semaphores):
    names = [(name, None) for name in [*scalars, *inputs, *anywhere, *outs]]
    buffers = []
    for name, entry in scratch.items():
        many = isinstance(entry, list)
        names.append((name, len(entry) if many else None))
        buffers += [pltpu.VMEM(*e) for e in (entry if many else [entry])]
    names += [(name, None) for name in semaphores]
    vmem = pl.BlockSpec(memory_space=pltpu.VMEM)
    outcome = pl.pallas_call(
        functools.partial(kernel, names),
        out_shape=tuple(jax.ShapeDtypeStruct(*o) for o in outs.values()),
        in_specs=[pl.BlockSpec(memory_space=pltpu.SMEM)] * len(scalars)
        + [vmem] * len(inputs)
        + [pl.BlockSpec(memory_space=pl.ANY)] * len(anywhere),
        out_specs=(vmem,) * len(outs),
        scratch_shapes=buffers + [pltpu.SemaphoreType.DMA(s) for s in semaphores.values()],
        compiler_params=pltpu.CompilerParams(
            collective_id=ident, has_side_effects=True, vmem_limit_bytes=60 << 20
        ),
        name=kernel.__name__,
    )(*[v for group in (scalars, inputs, anywhere) for v in dict(group).values()])
    return types.SimpleNamespace(**dict(zip(outs, outcome)))


VECTOR_ROWS = 24
FAR, NEAR, SIDE, CORE, GROUP = range(5)
CROSS = (FAR, NEAR, SIDE)
GROUP_FIRST = (GROUP, NEAR, SIDE, FAR)
STREAMS = (
    (144, C // 4, (SIDE, NEAR, FAR)),
    (144, C // 4, (NEAR, SIDE, FAR)),
    (144, C // 4, (SIDE, NEAR, FAR)),
    (144, C // 4, (NEAR, SIDE, FAR)),
    (64, C // 2, (SIDE, NEAR, FAR)),
    (64, C // 2, (NEAR, SIDE, FAR)),
    (16, 3 * C // 2, GROUP_FIRST),
    (16, C // 2, GROUP_FIRST),
)
FIRST_CONV, SECOND_CONV, WORDS, QKV, PROJ = 0, 2, 4, 6, 7
FIRST_LANDING = [sum(len(s[2]) for s in STREAMS[:k]) for k in range(len(STREAMS))]
HALF_SUMS, GROUP_SUMS = -1, -2
TAIL = (6, 4, 5, 6, 2, -1, 0, 1, 3, 2, -2, 1, 3, 2, 0, 3, 1, 0, 1, 0)
IMAGE_ROWS = 8


class Band:
    def __init__(self, r):
        self.r = r
        self.row = lax.axis_index(ROWS)
        self.group = lax.axis_index(ITEMS)
        self.lane = self.row % SPAN
        self.base = self.row - self.lane
        row = self.row
        self.place = [row // 8, (row // 4) % 2, (row // 2) % 2, row % 2, self.group]
        self.partner = [
            {ROWS: row + (1 - 2 * self.place[d]) * (8 >> d)} for d in range(CORE + 1)
        ]
        self.partner.append({ITEMS: 1 - self.group})
        self.others = [(self.lane + o) % SPAN for o in range(1, SPAN)]
        self.peers = [{ROWS: self.base + other} for other in self.others]
        self.has_above, self.has_below = self.lane > 0, self.lane < SPAN - 1

    def meet(self, further=()):
        barrier = pltpu.get_barrier_semaphore()
        targets = self.peers + list(further)
        for target in targets:
            pl.semaphore_signal(barrier, 1, device_id=target)
        pl.semaphore_wait(barrier, len(targets))

    def remote(self, source, target, send, recv, device):
        return pltpu.make_async_remote_copy(source, target, send, recv, device_id=device)

    def edges(self, k, top, bottom, target):
        r = self.r
        up = self.remote(
            top,
            target.at[IMAGE_ROWS + 1],
            r.edge_send.at[k, 0],
            r.edge_recv.at[k, 0],
            {ROWS: self.row - 1},
        )
        down = self.remote(
            bottom,
            target.at[0],
            r.edge_send.at[k, 1],
            r.edge_recv.at[k, 1],
            {ROWS: self.row + 1},
        )
        pl.when(self.has_above)(up.start)
        pl.when(self.has_below)(down.start)
        return up, down

    def wait_edges(self, pair):
        up, down = pair

        @pl.when(self.has_above)
        def _():
            up.wait_send()
            down.wait_recv()

        @pl.when(self.has_below)
        def _():
            down.wait_send()
            up.wait_recv()

    def zero_edges(self, target):
        @pl.when(jnp.logical_not(self.has_above))
        def _():
            target[0] = jnp.zeros(target.shape[1:], target.dtype)

        @pl.when(jnp.logical_not(self.has_below))
        def _():
            target[IMAGE_ROWS + 1] = jnp.zeros(target.shape[1:], target.dtype)

    def send_tile(self, k, source, target):
        r = self.r
        copies = []
        for o in range(1, SPAN):
            copies.append(
                self.remote(
                    source,
                    target.at[self.lane],
                    r.tile_send.at[k, o],
                    r.tile_recv.at[k, o],
                    self.peers[o - 1],
                )
            )
        for copy in copies:
            copy.start()
        target[self.lane] = source[...]
        return copies

    def swap(self, k, source, target, order=range(1, SPAN)):
        r = self.r
        copies = []
        for o in order:
            copies.append(
                self.remote(
                    source.at[self.others[o - 1]],
                    target.at[self.lane],
                    r.swap_send.at[k, o],
                    r.swap_recv.at[k, o],
                    self.peers[o - 1],
                )
            )
            copies[-1].start()
        return copies

    def fill_blocks(self):
        rows = lax.broadcasted_iota(jnp.int32, (C, C), 0) // (C // NORM_GROUPS)
        columns = lax.broadcasted_iota(jnp.int32, (C, C), 1) // (C // NORM_GROUPS)
        self.r.blocks[...] = jnp.where(rows == columns, 1.0, 0.0).astype(jnp.bfloat16)

    def item_means(self, window, masks, per_item):
        low, full = jnp.bfloat16, jnp.float32
        tile = jnp.zeros((8, C // 4), full)
        for b in range(SPAN):
            tile = tile + jnp.where(masks[b][:, 0 : C // 4] > 0.0, window[b], 0.0)
        first, second = [
            jnp.concatenate([tile[j : j + 1, :] for j in range(4 * k, 4 * k + 4)], axis=1)
            for k in range(2)
        ]
        rows = lax.broadcasted_iota(jnp.int32, (8, C), 0)
        total = jnp.where(rows == 0, first, jnp.where(rows == 1, second, 0.0)) * per_item
        coarse = total.astype(low)
        rest = total - coarse.astype(full)
        finer = rest.astype(low)
        finest = (rest - finer.astype(full)).astype(low)
        blocks = self.r.blocks[...]
        return dot(coarse, blocks) + dot(finer, blocks) + dot(finest, blocks)


def sums_tile(first, second):
    rows = lax.broadcasted_iota(jnp.int32, (8, C // 4), 0)
    tile = jnp.zeros((8, C // 4), jnp.float32)
    for k, values in enumerate((first, second)):
        for j in range(4):
            part = values[:, j * (C // 4) : (j + 1) * (C // 4)]
            tile = jnp.where(rows == 4 * k + j, part, tile)
    return tile


def column_sum(values):
    return jnp.sum(values, axis=0, keepdims=True)


def side_shifts(values):
    rows = lax.broadcasted_iota(jnp.int32, values.shape, 0)
    from_left = jnp.where(rows == 0, 0.0, pltpu.roll(values, 1, 0))
    from_right = jnp.where(rows == W - 1, 0.0, pltpu.roll(values, W - 1, 0))
    return from_left, from_right


def kept(i, values, vec):
    keep = jnp.where(i == 0, vec.keep_above, jnp.where(i == IMAGE_ROWS + 1, vec.keep_below, 1.0))
    return jnp.where(keep > 0.0, values, 0.0)


def back_kernel(names, *refs):
    low, full = jnp.bfloat16, jnp.float32
    r = grouped(names, refs)
    band = Band(r)
    lane, group, place, partner = band.lane, band.group, band.place, band.partner
    core = place[CORE]
    remote = band.remote
    across = {ROWS: partner[CORE][ROWS], ITEMS: 1 - group}
    band.meet((partner[FAR], partner[GROUP], across))
    quad = (partner[CORE], partner[GROUP], across)
    quarter = 2 * group + core
    quarters = (2 * group + 1 - core, 2 * (1 - group) + core, 2 * (1 - group) + 1 - core)

    def columns_of(which, size):
        return pl.ds(pl.multiple_of(which * size, size), size)

    def to_quad(kind, source, target):
        copies = [
            remote(
                source(quarters[i]), target.at[i], r.quad_send.at[kind, i], r.quad_recv.at[kind, i], quad[i]
            )
            for i in range(3)
        ]
        for copy in copies:
            copy.start()
        return copies


    swaps = band.swap(0, r.pair_grads, r.head_pairs) + band.swap(1, r.word_grads, r.head_words)

    loads = types.SimpleNamespace()

    def load(k, source, target):
        copy = pltpu.make_async_copy(source, target, r.load_sem.at[k])
        copy.start()
        return copy

    loads.outcome = load(0, r.outcome, r.heads)
    loads.pair_grads = load(1, r.pair_grads.at[lane], r.head_pairs.at[lane])
    loads.word_grads = load(14, r.word_grads.at[lane], r.head_words.at[lane])
    loads.middle = load(2, r.middle, r.mid)
    loads.qkv_weight = load(3, r.qkv_weight, r.qkv_w)
    loads.proj_weight = load(4, r.proj_weight, r.proj_w)
    loads.upstream = load(5, r.upstream, r.up)
    loads.act_three = load(6, r.act_three, r.act3)
    loads.caption = load(7, r.caption, r.caps.at[0])
    loads.far_caption = load(15, r.far_caption, r.caps.at[2])
    loads.conv_second = load(8, r.conv_second, r.conv_w)
    loads.hidden = load(9, r.hidden, r.hid)
    loads.act_two = load(10, r.act_two, r.acts_two.at[0])
    loads.far_act_two = load(16, r.far_act_two, r.acts_two.at[2])
    loads.act_one = load(11, r.act_one, r.acts_one.at[0])
    loads.far_act_one = load(17, r.far_act_one, r.acts_one.at[2])
    loads.image = load(12, r.image, r.img)
    loads.text_weight = load(13, r.text_weight, r.text_w)

    sibling = types.SimpleNamespace()

    def to_sibling(k, source, target):
        copy = remote(source, target, r.sib_send.at[k], r.sib_recv.at[k], partner[CORE])
        copy.start()
        return copy

    half = pl.ds(pl.multiple_of((1 - core) * (C // 2), C // 2), C // 2)
    sibling.upstream = to_sibling(0, r.upstream.at[:, half], r.sib_up)
    sibling.act3 = to_sibling(1, r.act_three, r.sib_act3)
    sibling.cap = to_sibling(2, r.caption, r.caps.at[1])
    sibling.far_cap = to_sibling(7, r.far_caption, r.caps.at[3])

    share_copy = remote(
        r.silu_share, r.other_share, r.small_send.at[2], r.small_recv.at[2], partner[GROUP]
    )
    share_copy.start()
    for target in (r.part_two, r.part_one):
        band.zero_edges(target)

    vec = Vectors(*[r.vectors[i : i + 1, :] for i in range(len(Vectors._fields))])
    norm_one = (vec.mean_one, vec.scale_one)
    norm_two = (vec.mean_two, vec.scale_two)
    norm_three = (vec.mean_three, vec.scale_three)

    masks = [r.vectors[VECTOR_ROWS + b : VECTOR_ROWS + b + 1, :] for b in range(SPAN)]
    band.fill_blocks()

    def item_means(window):
        return band.item_means(window, masks, vec.per_item)

    class Stream:
        def __init__(self, k):
            self.k = k
            self.order = STREAMS[k][2]
            self.dims = [FAR, NEAR, SIDE, CORE, GROUP][: len(self.order) + 1]
            self.step = 0
            self.copies = []

        def at(self, ref, d, index):
            return ref.at[(slice(None),) * self.dims.index(d) + (index,)]

        def start(self):
            self.launch(r.grads[self.k])

        def launch(self, ref):
            k, step = self.k, self.step
            if step < len(self.order):
                d = self.order[step]
                self.copies = [
                    remote(
                        self.at(ref, d, 1 - place[d]),
                        r.landings[FIRST_LANDING[k] + step],
                        r.fold_send.at[k, step],
                        r.fold_recv.at[k, step],
                        partner[d],
                    )
                ]
                self.mine = self.at(ref, d, place[d])
                self.dims.remove(d)
            else:
                if GROUP in self.order:
                    places = (r.folded[k], r.whole[k - QKV], r.whole[k - QKV])
                    self.place = core
                else:
                    places = (r.folded[k],) * 3
                    self.place = quarter
                sources = (ref.at[1 - core], ref.at[core], ref.at[1 - core])
                ends = [
                    (source, target.at[self.place], device)
                    for source, target, device in zip(sources, places, quad)
                ]
                self.copies = [
                    remote(
                        source,
                        target,
                        r.fold_send.at[k, step + i],
                        r.fold_recv.at[k, step + i],
                        device,
                    )
                    for i, (source, target, device) in enumerate(ends)
                ]
                self.mine = ref.at[core]
            for copy in self.copies:
                copy.start()

        def advance(self):
            for copy in self.copies:
                copy.wait()
            if self.step < len(self.order):
                landed, mine = r.landings[FIRST_LANDING[self.k] + self.step], self.mine
                lead = landed.shape[:-2]
                pieces = 1
                for n in lead:
                    pieces *= n

                def add(i, carry):
                    index = []
                    for n in reversed(lead):
                        index.insert(0, i % n)
                        i = i // n
                    index = tuple(index)
                    total = landed[index].astype(full) + mine[index].astype(full)
                    landed[index] = total.astype(low)
                    return carry

                lax.fori_loop(0, pieces, add, 0)
                self.step += 1
                self.launch(landed)
            else:
                r.folded[self.k][self.place] = self.mine[...]
                self.step += 1

    streams = [Stream(k) for k in range(len(STREAMS))]

    def advance(*order):
        for k in order:
            streams[k].advance()

    loads.outcome.wait()
    for h in range(0, HEADS, 2):
        for k in range(2):
            pair = [r.heads[h + i, :, k * HEAD : (k + 1) * HEAD] for i in range(2)]
            r.joined[:, k * C + h * HEAD : k * C + (h + 2) * HEAD] = jnp.concatenate(pair, axis=1)
    sibling.attended = to_sibling(5, r.joined.at[:, 0:C], r.sib_attended)

    def pixel_block(ref, i, count=4):
        return ref[1 + i * count : 1 + (i + 1) * count].reshape(count * W, C)

    def unit(values, norm):
        return (values - norm[0]) * norm[1]

    def mine_of(ref, start, size):
        return ref[:, pl.ds(pl.multiple_of(start, size if size % 256 else 256), size)]

    for copy in (loads.middle, loads.qkv_weight, loads.proj_weight, loads.upstream):
        copy.wait()
    up_sum = jnp.zeros((1, C), full)
    for i in range(2):
        block = slice(i * 4 * W, (i + 1) * 4 * W)
        upstream = r.up[block, :].astype(full)
        up_sum = up_sum + column_sum(upstream)
        result = pixel_block(r.mid, i) + dot(r.joined[block, 0:C], r.proj_w[...]) + vec.proj_bias
        r.result[block, :] = result.astype(low)
        grad = dot_last(r.joined[block, C : 2 * C], r.qkv_w[:, 0:C])
        r.product[i * 4 : i * 4 + 4] = grad.reshape(4, W, C)
    sibling.upstream.wait()
    sibling.attended.wait()
    grad = dot_first(r.joined[:, 0:C], mine_of(r.up, core * (C // 2), C // 2))
    grad = grad + dot_first(r.sib_attended[...], r.sib_up[...])
    r.grads[PROJ][...] = grad.astype(low).reshape(r.grads[PROJ].shape)
    streams[PROJ].start()
    query_sum = column_sum(r.joined[:, C : 2 * C].astype(full))

    for copy in (loads.pair_grads, loads.word_grads):
        copy.wait()
    for copy in swaps:
        copy.wait()
    for h in range(0, HEADS, 2):
        for k in range(2):
            lanes = slice(k * HEAD, (k + 1) * HEAD)
            pair = [r.head_pairs[h + i, :, lanes] for i in range(2)]
            first = (2 + k) * C + h * HEAD
            r.joined[:, first : first + 2 * HEAD] = jnp.concatenate(pair, axis=1)
            pair = [r.head_words[h + i, :, lanes] for i in range(2)]
            first = k * C + h * HEAD
            r.joined_words[:, first : first + 2 * HEAD] = jnp.concatenate(pair, axis=1)
    three_half = C + (1 - core) * (3 * C // 2)
    sibling.qkv = to_sibling(
        6, r.joined.at[:, pl.ds(pl.multiple_of(three_half, C // 2), 3 * C // 2)], r.sib_qkv
    )
    word_copies = to_quad(0, lambda q: r.joined_words.at[:, columns_of(q, C // 2)], r.word_parts)
    r.own_word_part[...] = r.joined_words[:, columns_of(quarter, C // 2)]
    sibling.act2 = to_sibling(3, r.act_two, r.acts_two.at[1])
    sibling.far_act2 = to_sibling(8, r.far_act_two, r.acts_two.at[3])
    sibling.act1 = to_sibling(4, r.act_one, r.acts_one.at[1])
    sibling.far_act1 = to_sibling(9, r.far_act_one, r.acts_one.at[3])

    plain = jnp.zeros((1, C), full)
    crossed = jnp.zeros((1, C), full)
    for i in range(2):
        block = slice(i * 4 * W, (i + 1) * 4 * W)
        grad = dot_last(r.joined[block, 2 * C :], r.qkv_w[:, C:])
        grad = grad + r.product[i * 4 : i * 4 + 4].reshape(4 * W, C)
        plain = plain + column_sum(grad)
        crossed = crossed + column_sum(grad * unit(pixel_block(r.mid, i), norm_three))
        part = r.up[block, :].astype(full) + grad * (vec.gain_three * vec.scale_three)
        r.part_two[1 + i * 4 : 5 + i * 4] = part.reshape(4, W, C)
    gain_three, bias_three = crossed, plain
    r.tile[0] = sums_tile(plain * vec.gain_three, crossed * vec.gain_three)
    three_edges = band.edges(0, r.part_two.at[1], r.part_two.at[IMAGE_ROWS], r.part_two)
    tiles = band.send_tile(0, r.tile.at[0], r.window.at[0])

    for copy in (sibling.act3, sibling.qkv, loads.act_three):
        copy.wait()
    for n in range(3):
        own = mine_of(r.joined, C + core * (3 * C // 2) + n * (C // 2), C // 2)
        columns = slice(n * (C // 2), (n + 1) * (C // 2))
        grad = dot_first(r.act3[...], own)
        grad = grad + dot_first(r.sib_act3[...], r.sib_qkv[:, columns])
        r.grads[QKV][:, :, :, :, :, :, columns] = grad.astype(low).reshape(2, 2, 2, 2, 2, 16, C // 2)
    streams[QKV].start()

    for copy in (sibling.cap, sibling.far_cap, loads.caption, loads.far_caption):
        copy.wait()
    for copy in word_copies:
        copy.wait()

    def text_rows(s, carry):
        columns = pl.ds(pl.multiple_of(s * 128, 128), 128)
        grad = dot_first(r.caps[0, :, columns], r.own_word_part[...])
        for i in range(3):
            grad = grad + dot_first(r.caps[i + 1, :, columns], r.word_parts[i])
        grad = grad.astype(low)
        index = (s // 8, (s // 4) % 2, (s // 2) % 2, s % 2)
        r.grads[WORDS][index] = grad[0:64]
        r.grads[WORDS + 1][index] = grad[64:128]
        return carry

    lax.fori_loop(0, 2 ** len(CROSS) * 2, text_rows, 0)
    streams[WORDS].start()
    streams[WORDS + 1].start()
    value_sum = column_sum(r.joined[:, 3 * C :].astype(full))
    word_sum = [column_sum(r.joined_words[:, k * C : (k + 1) * C].astype(full)) for k in range(2)]

    def spread_rows(i, values):
        from_left, from_right = side_shifts(values)
        r.shifts[0, i] = from_right.astype(low)
        r.shifts[1, i] = values.astype(low)
        r.shifts[2, i] = from_left.astype(low)

    def conv_back():
        total = jnp.zeros((IMAGE_ROWS * W, C), full)
        for t in range(9):
            dy, dx = t // 3, t % 3
            view = r.shifts[dx, 2 - dy : 2 - dy + IMAGE_ROWS].reshape(IMAGE_ROWS * W, C)
            total = total + dot_last(view, r.conv_w[t * C : (t + 1) * C, :])
        return total

    def gather_shifts(landing):
        width = C // 4

        def one_row(i, carry):
            for dx in range(3):
                lanes = slice(dx * width, (dx + 1) * width)
                r.sides[0, i, :, lanes] = r.shifts[dx, i + 1, :, columns_of(quarter, width)]
            for k in range(3):
                values = landing[k, i].astype(full)
                from_left, from_right = side_shifts(values)
                r.sides[k + 1, i, :, 0:width] = from_right.astype(low)
                r.sides[k + 1, i, :, width : 2 * width] = landing[k, i]
                r.sides[k + 1, i, :, 2 * width :] = from_left.astype(low)
            return carry

        lax.fori_loop(0, IMAGE_ROWS, one_row, 0)

    def conv_grads(kind, acts, landing):
        gather_shifts(landing)
        width = C // 4
        for dy in range(3):
            grad = jnp.zeros((C, 3 * width), full)
            for k in range(4):
                sides = r.sides[k].reshape(IMAGE_ROWS * W, 3 * width)
                grad = grad + dot_first(acts[k, dy * W : dy * W + IMAGE_ROWS * W, :], sides)
            grad = grad.astype(low)
            for dx in range(3):
                begin = first = (dy * 3 + dx) * C
                while begin < first + C:
                    shard, within = divmod(begin, 288)
                    stream, offset = divmod(within, 144)
                    size = min(144 - offset, first + C - begin)
                    target = r.grads[kind + stream]
                    target[
                        shard // 8,
                        (shard // 4) % 2,
                        (shard // 2) % 2,
                        shard % 2,
                        offset : offset + size,
                    ] = grad[begin - first : begin - first + size, dx * width : (dx + 1) * width]
                    begin += size
        for j in range(2):
            streams[kind + j].start()

    for copy in tiles:
        copy.wait()
    band.wait_edges(three_edges)
    means = item_means(r.window.at[0])
    offset_three, slope_three = means[0:1] * vec.scale_three, means[1:2] * vec.scale_three

    def middle_row(i, bias):
        values = r.part_two[i] - offset_three - unit(r.mid[i], norm_three) * slope_three
        r.part_two[i] = values
        values = kept(i, values, vec)
        spread_rows(i, values)
        inside = jnp.where((i > 0) & (i <= IMAGE_ROWS), 1.0, 0.0)
        return bias + inside * column_sum(values.astype(low).astype(full))

    conv_bias_two = lax.fori_loop(0, IMAGE_ROWS + 2, middle_row, jnp.zeros((1, C), full))
    def center(q):
        return r.shifts.at[1, 1 : IMAGE_ROWS + 1, :, columns_of(q, C // 4)]

    side_copies = to_quad(1, center, r.sides_two)
    advance(PROJ)
    loads.conv_second.wait()
    loads.hidden.wait()
    r.product[...] = conv_back().reshape(IMAGE_ROWS, W, C)
    loads.conv_first = load(8, r.conv_first, r.conv_w)
    stretched = vec.stretch * vec.gain_two * vec.scale_two

    def second_row(i, sums):
        unit_two = unit(r.hid[i + 1], norm_two)
        normed = unit_two * vec.gain_two + vec.bias_two
        grad = r.product[i] * silu_slope_of(normed * vec.stretch + vec.shift)
        r.part_one[i + 1] = grad * stretched
        return sums[0] + column_sum(grad), sums[1] + column_sum(grad * unit_two)

    nothing = (jnp.zeros((1, C), full), jnp.zeros((1, C), full))
    plain, crossed = lax.fori_loop(0, IMAGE_ROWS, second_row, nothing)
    scale_grad = crossed * vec.gain_two + plain * vec.bias_two
    shift_grad = plain
    gain_two, bias_two = crossed * vec.stretch, plain * vec.stretch
    r.tile[1] = sums_tile(bias_two * vec.gain_two, gain_two * vec.gain_two)
    two_edges = band.edges(1, r.part_one.at[1], r.part_one.at[IMAGE_ROWS], r.part_one)
    tiles = band.send_tile(1, r.tile.at[1], r.window.at[1])
    for copy in (loads.act_two, loads.far_act_two, sibling.act2, sibling.far_act2):
        copy.wait()
    for copy in side_copies:
        copy.wait()
    advance(PROJ, QKV, WORDS, WORDS + 1)
    conv_grads(SECOND_CONV, r.acts_two, r.sides_two)
    advance(PROJ)
    for copy in tiles:
        copy.wait()
    band.wait_edges(two_edges)
    means = item_means(r.window.at[1])
    offset_two, slope_two = means[0:1] * vec.scale_two, means[1:2] * vec.scale_two

    def hidden_row(i, bias):
        values = r.part_one[i] - offset_two - unit(r.hid[i], norm_two) * slope_two
        values = kept(i, values, vec)
        spread_rows(i, values)
        inside = jnp.where((i > 0) & (i <= IMAGE_ROWS), 1.0, 0.0)
        return bias + inside * column_sum(values.astype(low).astype(full))

    conv_bias_one = lax.fori_loop(0, IMAGE_ROWS + 2, hidden_row, jnp.zeros((1, C), full))
    side_copies = to_quad(2, center, r.sides_one)
    advance(PROJ, QKV, WORDS, WORDS + 1)
    loads.conv_first.wait()
    loads.image.wait()
    r.product[...] = conv_back().reshape(IMAGE_ROWS, W, C)

    def first_row(i, sums):
        unit_one = unit(r.img[i].astype(full), norm_one)
        normed = unit_one * vec.gain_one + vec.bias_one
        grad = r.product[i] * silu_slope_of(normed)
        r.product[i] = grad
        return sums[0] + column_sum(grad), sums[1] + column_sum(grad * unit_one)

    plain, crossed = lax.fori_loop(0, IMAGE_ROWS, first_row, nothing)
    gain_one, bias_one = crossed, plain
    r.tile[2] = sums_tile(plain * vec.gain_one, crossed * vec.gain_one)
    tiles = band.send_tile(2, r.tile.at[2], r.window.at[2])
    rows = [
        gain_one,
        gain_two,
        gain_three,
        bias_one,
        bias_two,
        bias_three,
        conv_bias_one,
        conv_bias_two,
        query_sum,
        value_sum,
        word_sum[0],
        word_sum[1],
        up_sum,
        jnp.zeros((1, C), full),
        scale_grad,
        shift_grad,
    ]
    for i, values in enumerate(rows):
        r.own_rows[i : i + 1, :] = values
    row_copies = band.send_tile(3, r.own_rows, r.band_rows)
    for copy in (loads.act_one, loads.far_act_one, sibling.act1, sibling.far_act1):
        copy.wait()
    for copy in side_copies:
        copy.wait()
    conv_grads(FIRST_CONV, r.acts_one, r.sides_one)
    advance(PROJ, QKV, WORDS, WORDS + 1, 2, 3)
    for copy in tiles:
        copy.wait()
    means = item_means(r.window.at[2])
    offset_one, slope_one = means[0:1] * vec.scale_one, means[1:2] * vec.scale_one
    ratio = vec.gain_one * vec.scale_one

    def image_row(i, carry):
        unit_one = unit(r.img[i].astype(full), norm_one)
        values = r.part_two[i + 1] + r.product[i] * ratio - offset_one - unit_one * slope_one
        r.image_grad[i] = values
        return carry

    lax.fori_loop(0, IMAGE_ROWS, image_row, 0)

    for copy in row_copies:
        copy.wait()
    total = jnp.zeros((16, C), full)
    for b in range(SPAN):
        total = total + r.band_rows[b]
    r.half_rows[0:16, :] = total
    for b in range(SPAN):
        r.half_rows[16 + 2 * b : 18 + 2 * b, :] = r.band_rows[b, 14:16, :]
    far_copy = remote(
        r.half_rows, r.far_rows, r.small_send.at[0], r.small_recv.at[0], partner[FAR]
    )
    far_copy.start()
    loads.text_weight.wait()

    def caption_columns(n, carry):
        columns = pl.ds(pl.multiple_of(n * C, C), C)
        r.caption_grad[:, columns] = dot_last(r.joined_words[...], r.text_w[columns, :])
        return carry

    lax.fori_loop(0, EMB // C, caption_columns, 0)
    loads.embed_weight = load(13, r.embed_weight, r.text_w)
    slots = r.slot_of_band.shape[0]
    held = types.SimpleNamespace()

    def half_sums_arrived():
        far_copy.wait()
        first_half = jnp.where(place[FAR] == 0, r.half_rows[16:32, :], r.far_rows[16:32, :])
        other_half = jnp.where(place[FAR] == 0, r.far_rows[16:32, :], r.half_rows[16:32, :])
        r.group_rows[0:16, :] = r.half_rows[0:16, :] + r.far_rows[0:16, :]
        r.group_rows[16:32, :] = first_half
        r.group_rows[32:48, :] = other_half
        for k in range(2):
            table = jnp.zeros((slots, C), full)
            for b in range(2 * SPAN):
                values = r.group_rows[16 + 2 * b + k : 17 + 2 * b + k, :]
                table = table + jnp.where(r.slot_of_band[:, b * 128 : b * 128 + 1] > 0.0, values, 0.0)
            r.own_table[slots * k : slots * (k + 1), :] = table
        r.own_table[2 * slots :, :] = r.group_rows[0:16, :]
        held.group_copy = remote(
            r.own_table,
            r.other_table,
            r.small_send.at[1],
            r.small_recv.at[1],
            partner[GROUP],
        )
        held.group_copy.start()
        loads.embed_weight.wait()
        held.table = table = [r.own_table[slots * k : slots * (k + 1), :].astype(low) for k in range(2)]

        def embedding_columns(n, carry):
            columns = pl.ds(pl.multiple_of(n * C, C), C)
            grad = dot_last(table[0], r.text_w[columns, 0:C]) + dot_last(table[1], r.text_w[columns, C:])
            source = r.embedding[:, columns].astype(full)
            r.embedding_grad[:, columns] = grad * silu_slope_of(source)
            return carry

        lax.fori_loop(0, EMB // C, embedding_columns, 0)

    def group_sums_arrived():
        held.group_copy.wait()
        share_copy.wait()
        table = held.table
        for k in range(2):
            columns = slice(k * C, (k + 1) * C)
            other = r.other_table[slots * k : slots * (k + 1), :].astype(low)
            r.embed_weight_grad[:, columns] = dot_first(r.silu_share[...], table[k]) + dot_first(
                r.other_share[...], other
            )
            r.embed_bias_grad[:, columns] = column_sum(table[k].astype(full)) + column_sum(
                other.astype(full)
            )
        sums = r.own_table[2 * slots :, :] + r.other_table[2 * slots :, :]
        r.norm_gains_grad[...] = sums[0:3]
        r.norm_biases_grad[...] = sums[3:6]
        r.conv_biases_grad[...] = sums[6:8]
        for target, k in ((r.qv_bias_grad, 8), (r.text_bias_grad, 10)):
            target[:, 0:C] = sums[k : k + 1]
            target[:, C:] = sums[k + 1 : k + 2]
        r.proj_bias_grad[...] = sums[12:13]

    for k in TAIL:
        if k == HALF_SUMS:
            half_sums_arrived()
        elif k == GROUP_SUMS:
            group_sums_arrived()
        else:
            advance(k)

    def write(stream, target, first_row):
        rows, columns = STREAMS[stream][:2]
        for k in range(4):
            target[first_row : first_row + rows, k * columns : (k + 1) * columns] = r.folded[stream][
                k
            ].astype(full)

    def write_halves(stream, target):
        rows, columns = STREAMS[stream][:2]
        for side, source in ((group, r.folded[stream]), (1 - group, r.whole[stream - QKV])):
            for k in range(2):
                target[
                    pl.ds(pl.multiple_of(side * rows, rows), rows), k * columns : (k + 1) * columns
                ] = source[k].astype(full)

    for j in range(2):
        write(FIRST_CONV + j, r.conv_first_grad, j * 144)
        write(SECOND_CONV + j, r.conv_second_grad, j * 144)
        write(WORDS + j, r.text_grad, j * 64)
    write_halves(QKV, r.qkv_grad)
    write_halves(PROJ, r.proj_grad)


def silu_slope_of(source):
    sigma = 1.0 / (1.0 + jnp.exp(-source))
    return sigma * (1.0 + source * (1.0 - sigma))


def back(ident, vectors, slot_of_band, silu_share, embedding, anywhere):
    low, full = jnp.bfloat16, jnp.float32
    pixels = IMAGE_ROWS * W
    slots = slot_of_band.shape[0]
    outs = dict(
        result=((pixels, C), low),
        image_grad=((IMAGE_ROWS, W, C), full),
        caption_grad=((TEXT, EMB), full),
        conv_first_grad=((288, C), full),
        conv_second_grad=((288, C), full),
        qkv_grad=((32, 3 * C), full),
        text_grad=((128, 2 * C), full),
        proj_grad=((32, C), full),
        embedding_grad=(embedding.shape, full),
        embed_weight_grad=((silu_share.shape[1], 2 * C), full),
        norm_gains_grad=((3, C), full),
        norm_biases_grad=((3, C), full),
        conv_biases_grad=((2, C), full),
        embed_bias_grad=((1, 2 * C), full),
        qv_bias_grad=((1, 2 * C), full),
        text_bias_grad=((1, 2 * C), full),
        proj_bias_grad=((1, C), full),
    )
    padded = (IMAGE_ROWS + 2, W, C)
    scratch = dict(
        heads=((HEADS, pixels, 2 * HEAD), low),
        head_pairs=((HEADS, pixels, 2 * HEAD), low),
        head_words=((HEADS, TEXT, 2 * HEAD), low),
        joined=((pixels, 4 * C), low),
        joined_words=((TEXT, 2 * C), low),
        mid=(padded, full),
        part_two=(padded, full),
        part_one=(padded, full),
        hid=(padded, full),
        product=((IMAGE_ROWS, W, C), full),
        img=((IMAGE_ROWS, W, C), low),
        up=((pixels, C), low),
        act3=((pixels, C), low),
        conv_w=((9 * C, C), low),
        qkv_w=((C, 3 * C), low),
        proj_w=((C, C), low),
        text_w=((EMB, 2 * C), low),
        sib_up=((pixels, C // 2), low),
        sib_act3=((pixels, C), low),
        sib_attended=((pixels, C), low),
        sib_qkv=((pixels, 3 * C // 2), low),
        acts_one=((4, pixels + 2 * W, C), low),
        acts_two=((4, pixels + 2 * W, C), low),
        caps=((4, TEXT, EMB), low),
        own_word_part=((TEXT, C // 2), low),
        word_parts=((3, TEXT, C // 2), low),
        sides_one=((3, IMAGE_ROWS, W, C // 4), low),
        sides_two=((3, IMAGE_ROWS, W, C // 4), low),
        sides=((4, IMAGE_ROWS, W, 3 * C // 4), low),
        shifts=((3,) + padded, low),
        blocks=((C, C), low),
        tile=((3, 8, C // 4), full),
        window=((3, SPAN, 8, C // 4), full),
        own_rows=((16, C), full),
        band_rows=((SPAN, 16, C), full),
        half_rows=((32, C), full),
        far_rows=((32, C), full),
        group_rows=((48, C), full),
        own_table=((2 * slots + 16, C), full),
        other_table=((2 * slots + 16, C), full),
        other_share=(silu_share.shape, low),
    )
    def halved(stream, step):
        return ((2,) * (len(stream[2]) + 1 - step) + stream[:2], low)

    scratch.update(grads=[halved(s, 0) for s in STREAMS])
    scratch.update(landings=[halved(s, i + 1) for s in STREAMS for i in range(len(s[2]))])
    scratch.update(folded=[((2 if GROUP in s[2] else 4,) + s[:2], low) for s in STREAMS])
    scratch.update(whole=[((2,) + s[:2], low) for s in STREAMS[QKV:]])
    semaphores = dict(
        swap_send=(2, SPAN),
        swap_recv=(2, SPAN),
        load_sem=(18,),
        quad_send=(3, 3),
        quad_recv=(3, 3),
        sib_send=(10,),
        sib_recv=(10,),
        edge_send=(2, 2),
        edge_recv=(2, 2),
        tile_send=(4, SPAN),
        tile_recv=(4, SPAN),
        fold_send=(len(STREAMS), len(GROUP_FIRST) + 3),
        fold_recv=(len(STREAMS), len(GROUP_FIRST) + 3),
        small_send=(3,),
        small_recv=(3,),
    )
    inputs = dict(
        vectors=vectors, slot_of_band=slot_of_band, silu_share=silu_share, embedding=embedding
    )
    return call_named(back_kernel, ident, (), inputs, anywhere, outs, scratch, semaphores)


def attend_kernel(names, *refs):
    low, full = jnp.bfloat16, jnp.float32
    r = grouped(names, refs)
    band = Band(r)
    band.meet()
    bands, pixels = r.pairs.shape[:2]
    text = r.words.shape[1]
    scale = HEAD ** (-0.5)

    def with_units(values, rows):
        lanes = lax.broadcasted_iota(jnp.int32, (rows, 2 * HEAD), 1)
        units = jnp.where(lanes < 2, 1.0, 0.0).astype(low)
        return jnp.where(lanes < HEAD, units, values)

    def prepare(b, carry):
        r.across[b] = r.pairs[b].T
        r.valued[b] = with_units(r.pairs[b], pixels)
        r.words_across[b] = r.words[b].T
        r.words_valued[b] = with_units(r.words[b], text)
        r.pair_sums[b] = jnp.zeros((pixels, 2 * HEAD), full)
        return carry

    lax.fori_loop(0, bands, prepare, 0)

    def one_row(columns):
        rows = lax.broadcasted_iota(jnp.int32, (16, columns), 0)
        return jnp.where(rows == 0, 1.0, 0.0).astype(low)

    ones_pixels = one_row(pixels)
    ones_text = one_row(text)
    zeros = jnp.zeros((HEAD, pixels), low)

    def outcome_copy(i):
        return band.remote(
            r.own_outcome.at[i],
            r.outcome.at[band.lane],
            r.outcome_send.at[i],
            r.outcome_recv.at[band.lane],
            {ROWS: band.base + i},
        )

    def query_band(step, carry):
        i = (band.lane + 1 + step) % bands
        mine = r.items[band.base + i]
        start = 0
        allowed = []
        for b in range(bands):
            other = r.items[band.base + b]
            start = start + jnp.where(other < mine, 1, 0)
            allowed.append(other == mine)
        query = (r.queries[i].astype(full) * scale).astype(low)
        query_rhs = jnp.concatenate([query, zeros], 0)

        top = jnp.full((8, pixels), -jnp.inf, full)
        for j in range(bands):
            scores = dot(r.pairs[j], query_rhs)
            r.scores[j] = scores
            highest = jnp.max(scores.reshape(pixels // 8, 8, pixels), axis=0)
            top = jnp.where(allowed[j], jnp.maximum(top, highest), top)
        scores = dot(r.words[start], query_rhs)
        top = jnp.maximum(top, jnp.max(scores.reshape(text // 8, 8, pixels), axis=0))
        top = jnp.max(top, axis=0, keepdims=True)
        weights_text = jnp.exp2((scores - top) * LOG2E).astype(low)
        values = jnp.concatenate([r.words_across[start, HEAD:, :], ones_text], 0)
        total = dot(values, weights_text)

        for j in range(bands):
            ceiling = top + jnp.where(allowed[j], 0.0, FAR_ABOVE)
            weights = jnp.exp2((r.scores[j] - ceiling) * LOG2E).astype(low)
            r.weights[j] = weights
            values = jnp.concatenate([r.across[j, HEAD:, :], ones_pixels], 0)
            total = total + dot(values, weights)
        inverse = 1.0 / total[HEAD : HEAD + 1, :]
        attended = total[0:HEAD, :] * inverse
        grad = r.upstream[i].astype(full)
        minus_dots = -jnp.sum(grad * attended, axis=0, keepdims=True) * inverse
        grad_scaled = (grad * inverse).astype(low)
        coarse = minus_dots.astype(low)
        fine = minus_dots - coarse.astype(full)
        rows = lax.broadcasted_iota(jnp.int32, (HEAD, pixels), 0)
        extra = jnp.where(rows == 0, coarse.astype(full), jnp.where(rows == 1, fine, 0.0))
        grad_rhs = jnp.concatenate([extra.astype(low), grad_scaled], 0)
        grad_rows = jnp.concatenate([zeros, grad_scaled], 0).T
        query_rows = jnp.concatenate([query, zeros], 0).T

        steps = (weights_text.astype(full) * dot(r.words_valued[start], grad_rhs)).astype(low)
        word_sum = dot(weights_text, grad_rows) + dot(steps, query_rows)
        r.word_parts[i] = word_sum
        query_grad = dot(r.words_across[start, 0:HEAD, :], steps)
        for j in range(bands):
            for begin in range(0, pixels, pixels // 2):
                keys = slice(begin, begin + pixels // 2)
                weights = r.weights[j, keys]
                steps = (weights.astype(full) * dot(r.valued[j, keys], grad_rhs)).astype(low)
                r.pair_sums[j, keys] += dot(weights, grad_rows) + dot(steps, query_rows)
                query_grad = query_grad + dot(r.across[j, 0:HEAD, keys], steps)
        r.own_outcome[i] = jnp.concatenate(
            [attended.astype(low), (query_grad * scale).astype(low)], 0
        ).T
        pl.when(step < bands - 1)(outcome_copy(i).start)
        return carry

    lax.fori_loop(0, bands, query_band, 0)
    r.outcome[band.lane] = r.own_outcome[band.lane]

    def finish(b, carry):
        r.pair_grads[b] = r.pair_sums[b].astype(low)
        word_sum = jnp.zeros((text, 2 * HEAD), full)
        for i in range(bands):
            mine = r.items[band.base + i]
            start = 0
            for c in range(bands):
                start = start + jnp.where(r.items[band.base + c] < mine, 1, 0)
            word_sum = word_sum + jnp.where(start == b, r.word_parts[i], 0.0)
        r.word_grads[b] = word_sum.astype(low)
        return carry

    lax.fori_loop(0, bands, finish, 0)

    def wait_outcome(step, carry):
        i = (band.lane + 1 + step) % bands
        outcome_copy(i).wait_send()
        band.remote(
            r.own_outcome.at[i],
            r.outcome.at[i],
            r.outcome_send.at[i],
            r.outcome_recv.at[i],
            {ROWS: band.base + i},
        ).wait_recv()
        return carry

    lax.fori_loop(0, bands - 1, wait_outcome, 0)


def attend(ident, items, ahead):
    low, full = jnp.bfloat16, jnp.float32
    bands, pixels, _ = ahead.pairs.shape
    text = ahead.words.shape[1]
    outs = dict(
        outcome=((bands, pixels, 2 * HEAD), low),
        pair_grads=((bands, pixels, 2 * HEAD), low),
        word_grads=((bands, text, 2 * HEAD), low),
    )
    scratch = dict(
        across=((bands, 2 * HEAD, pixels), low),
        valued=((bands, pixels, 2 * HEAD), low),
        words_across=((bands, 2 * HEAD, text), low),
        words_valued=((bands, text, 2 * HEAD), low),
        scores=((bands, pixels, pixels), full),
        weights=((bands, pixels, pixels), low),
        pair_sums=((bands, pixels, 2 * HEAD), full),
        word_parts=((bands, text, 2 * HEAD), full),
        own_outcome=((bands, pixels, 2 * HEAD), low),
    )
    semaphores = dict(outcome_send=(bands,), outcome_recv=(bands,))
    inputs = dict(
        pairs=ahead.pairs, queries=ahead.queries, upstream=ahead.upstream, words=ahead.words
    )
    return call_named(
        attend_kernel, ident, dict(items=items), inputs, {}, outs, scratch, semaphores
    )


def front_kernel(names, *refs):
    low, full = jnp.bfloat16, jnp.float32
    r = grouped(names, refs)
    band = Band(r)
    partner = band.partner[GROUP]
    band.meet((partner,))
    loads = types.SimpleNamespace()

    def load(k, source, target):
        copy = pltpu.make_async_copy(source, target, r.load_sem.at[k])
        copy.start()
        return copy

    loads.image = load(0, r.image, r.img.at[1 : IMAGE_ROWS + 1])
    image_edges = band.edges(0, r.image.at[0], r.image.at[IMAGE_ROWS - 1], r.img)
    loads.upstream = load(3, r.upstream_pixels, r.up)
    loads.proj_weight = load(4, r.proj_weight, r.proj_w)
    loads.conv_first = load(1, r.conv_first, r.first_w)
    loads.embed_weight = load(2, r.embed_weight, r.embed_w)
    loads.conv_second = load(5, r.conv_second, r.second_w)
    loads.caption = load(6, r.caption, r.cap)
    loads.text_weight = load(7, r.text_weight, r.text_w)
    loads.qkv_weight = load(8, r.qkv_weight, r.qkv_w)

    def to_counterpart(k, source, target):
        copy = band.remote(source, target, r.pair_send.at[k], r.pair_recv.at[k], partner)
        copy.start()
        return copy

    pair_copies = [to_counterpart(0, r.caption, r.far_caption)]

    mine = r.items[band.row]
    same = [(r.items[band.base + b] == mine).astype(full) for b in range(SPAN)]
    masks = [jnp.full((1, C), m, full) for m in same]
    bands = masks[0]
    for m in masks[1:]:
        bands = bands + m
    per_item = 1.0 / (bands * (IMAGE_ROWS * W * (C // NORM_GROUPS)))
    before = jnp.where(band.has_above, r.items[jnp.maximum(band.row - 1, 0)], -1)
    after = jnp.where(
        band.has_below, r.items[jnp.minimum(band.row + 1, r.items.shape[0] - 1)], -1
    )
    found = types.SimpleNamespace(
        gain_one=r.norm_gains[0:1, :],
        gain_two=r.norm_gains[1:2, :],
        gain_three=r.norm_gains[2:3, :],
        bias_one=r.norm_biases[0:1, :],
        bias_two=r.norm_biases[1:2, :],
        bias_three=r.norm_biases[2:3, :],
        proj_bias=r.proj_bias[...],
        keep_above=jnp.full((1, C), (before == mine).astype(full)),
        keep_below=jnp.full((1, C), (after == mine).astype(full)),
        per_item=per_item,
    )
    for target in (r.img, r.hidden, r.middle):
        band.zero_edges(target)
    nothing = (jnp.zeros((1, C), full), jnp.zeros((1, C), full))

    def norm_of(k):
        means = band.item_means(r.window.at[k], masks, per_item)
        return means[0:1], lax.rsqrt(means[1:2] - means[0:1] * means[0:1] + epsilon)

    loads.image.wait()

    def image_sums(i, sums):
        values = r.img[i + 1].astype(full)
        return sums[0] + column_sum(values), sums[1] + column_sum(values * values)

    r.tile[0] = sums_tile(*lax.fori_loop(0, IMAGE_ROWS, image_sums, nothing))
    tiles = band.send_tile(0, r.tile.at[0], r.window.at[0])

    loads.upstream.wait()
    loads.proj_weight.wait()
    attended_grad = dot_last(r.proj_w[...], r.up[...]).astype(low)
    for h in range(HEADS):
        r.own_upstream[h] = attended_grad[h * HEAD : (h + 1) * HEAD, :]
    swaps = band.swap(0, r.own_upstream, r.upstream)
    r.upstream[band.lane] = r.own_upstream[band.lane]
    band.fill_blocks()
    slot = lax.broadcasted_iota(jnp.int32, r.embedding.shape, 0)
    chosen = jnp.where(slot == mine, r.embedding[...].astype(full), 0.0)
    chosen = jnp.sum(chosen, axis=0, keepdims=True)
    chosen = chosen / (1.0 + jnp.exp(-chosen))
    chosen = jnp.broadcast_to(chosen, (16, EMB)).astype(low)
    loads.embed_weight.wait()
    modulation = dot(chosen, r.embed_w[...])[0:1] + r.embed_bias[...]
    found.stretch = 1.0 + modulation[:, 0:C]
    found.shift = modulation[:, C:]

    def spread_rows(i, values, target):
        values = kept(i, values, found)
        from_left, from_right = side_shifts(values)
        r.shifts[0, i] = from_left.astype(low)
        r.shifts[1, i] = values.astype(low)
        r.shifts[2, i] = from_right.astype(low)
        target[pl.ds(pl.multiple_of(i * W, W), W), :] = values.astype(low)

    def conv(weight):
        total = jnp.zeros((IMAGE_ROWS * W, C), full)
        for t in range(9):
            view = r.shifts[t % 3, t // 3 : t // 3 + IMAGE_ROWS].reshape(IMAGE_ROWS * W, C)
            total = total + dot(view, weight[t * C : (t + 1) * C, :])
        return total

    for copy in tiles:
        copy.wait()
    band.wait_edges(image_edges)
    found.mean_one, found.scale_one = norm_of(0)

    def first_row(i, carry):
        unit = (r.img[i].astype(full) - found.mean_one) * found.scale_one
        normed = unit * found.gain_one + found.bias_one
        spread_rows(i, normed / (1.0 + jnp.exp(-normed)), r.act_one)
        return carry

    lax.fori_loop(0, IMAGE_ROWS + 2, first_row, 0)
    pair_copies.append(to_counterpart(1, r.act_one, r.far_act_one))
    loads.conv_first.wait()
    total = conv(r.first_w) + r.conv_biases[0:1, :]
    r.hidden[1 : IMAGE_ROWS + 1] = total.reshape(IMAGE_ROWS, W, C)
    hidden_edges = band.edges(1, r.hidden.at[1], r.hidden.at[IMAGE_ROWS], r.hidden)
    r.tile[1] = sums_tile(column_sum(total), column_sum(total * total))
    tiles = band.send_tile(1, r.tile.at[1], r.window.at[1])

    loads.caption.wait()
    loads.text_weight.wait()
    words = (dot(r.cap[...], r.text_w[...]) + r.text_bias[...]).astype(low)
    for h in range(HEADS):
        parts = [words[:, k * C + h * HEAD : k * C + (h + 1) * HEAD] for k in range(2)]
        r.own_words[h] = jnp.concatenate(parts, axis=1)
    swaps = swaps + band.swap(1, r.own_words, r.words)
    r.words[band.lane] = r.own_words[band.lane]
    for copy in tiles:
        copy.wait()
    band.wait_edges(hidden_edges)
    found.mean_two, found.scale_two = norm_of(1)

    def second_row(i, carry):
        unit = (r.hidden[i] - found.mean_two) * found.scale_two
        normed = unit * found.gain_two + found.bias_two
        shifted = normed * found.stretch + found.shift
        spread_rows(i, shifted / (1.0 + jnp.exp(-shifted)), r.act_two)
        return carry

    lax.fori_loop(0, IMAGE_ROWS + 2, second_row, 0)
    pair_copies.append(to_counterpart(2, r.act_two, r.far_act_two))
    loads.conv_second.wait()
    total = conv(r.second_w) + r.conv_biases[1:2, :]
    total = total + r.img[1 : IMAGE_ROWS + 1].astype(full).reshape(IMAGE_ROWS * W, C)
    r.middle[1 : IMAGE_ROWS + 1] = total.reshape(IMAGE_ROWS, W, C)
    r.tile[2] = sums_tile(column_sum(total), column_sum(total * total))
    tiles = band.send_tile(2, r.tile.at[2], r.window.at[2])
    middle_edges = band.edges(2, r.middle.at[1], r.middle.at[IMAGE_ROWS], r.middle)

    loads.qkv_weight.wait()
    for copy in tiles:
        copy.wait()
    found.mean_three, found.scale_three = norm_of(2)
    for i in range(2):
        middle = r.middle[1 + 4 * i : 5 + 4 * i].reshape(4 * W, C)
        unit = (middle - found.mean_three) * found.scale_three
        block = slice(i * 4 * W, (i + 1) * 4 * W)
        act = (unit * found.gain_three + found.bias_three).astype(low)
        r.act_three[block, :] = act
        projected = dot(act, r.qkv_w[...])
        queries = (projected[:, 0:C] + r.qv_bias[:, 0:C]).astype(low)
        keys = projected[:, C : 2 * C].astype(low)
        values = (projected[:, 2 * C :] + r.qv_bias[:, C:]).astype(low)
        queries = queries.T
        for h in range(HEADS):
            head = slice(h * HEAD, (h + 1) * HEAD)
            r.own_queries[h, :, block] = queries[head, :]
            r.own_pairs[h, block, :] = jnp.concatenate([keys[:, head], values[:, head]], axis=1)
    swaps = swaps + band.swap(2, r.own_pairs, r.pairs) + band.swap(3, r.own_queries, r.queries)
    r.pairs[band.lane] = r.own_pairs[band.lane]
    r.queries[band.lane] = r.own_queries[band.lane]
    fields = [getattr(found, name) for name in Vectors._fields]
    for i, values in enumerate(fields):
        r.vectors[i : i + 1, :] = values
    r.vectors[len(fields) : VECTOR_ROWS, :] = jnp.zeros((VECTOR_ROWS - len(fields), C), full)
    for b in range(SPAN):
        r.vectors[VECTOR_ROWS + b : VECTOR_ROWS + b + 1, :] = masks[b]
    band.wait_edges(middle_edges)
    for copy in swaps + pair_copies:
        copy.wait()


def front(ident, items, inputs, anywhere):
    low, full = jnp.bfloat16, jnp.float32
    pixels = IMAGE_ROWS * W
    padded = (IMAGE_ROWS + 2, W, C)
    outs = dict(
        pairs=((HEADS, pixels, 2 * HEAD), low),
        queries=((HEADS, HEAD, pixels), low),
        upstream=((HEADS, HEAD, pixels), low),
        words=((HEADS, TEXT, 2 * HEAD), low),
        act_one=((pixels + 2 * W, C), low),
        act_two=((pixels + 2 * W, C), low),
        act_three=((pixels, C), low),
        far_caption=((TEXT, EMB), low),
        far_act_one=((pixels + 2 * W, C), low),
        far_act_two=((pixels + 2 * W, C), low),
        hidden=(padded, full),
        middle=(padded, full),
        vectors=((VECTOR_ROWS + SPAN, C), full),
    )
    scratch = dict(
        img=(padded, low),
        up=((pixels, C), low),
        cap=((TEXT, EMB), low),
        first_w=((9 * C, C), low),
        second_w=((9 * C, C), low),
        embed_w=((EMB, 2 * C), low),
        text_w=((EMB, 2 * C), low),
        qkv_w=((C, 3 * C), low),
        proj_w=((C, C), low),
        shifts=((3,) + padded, low),
        blocks=((C, C), low),
        tile=((3, 8, C // 4), full),
        window=((3, SPAN, 8, C // 4), full),
        own_pairs=((HEADS, pixels, 2 * HEAD), low),
        own_queries=((HEADS, HEAD, pixels), low),
        own_upstream=((HEADS, HEAD, pixels), low),
        own_words=((HEADS, TEXT, 2 * HEAD), low),
    )
    semaphores = dict(
        load_sem=(9,),
        pair_send=(3,),
        pair_recv=(3,),
        edge_send=(3, 2),
        edge_recv=(3, 2),
        tile_send=(3, SPAN),
        tile_recv=(3, SPAN),
        swap_send=(4, SPAN),
        swap_recv=(4, SPAN),
    )
    return call_named(
        front_kernel, ident, dict(items=items), inputs, anywhere, outs, scratch, semaphores
    )


def hand_over_kernel(count, *refs):
    sources, targets, sem = refs[:count], refs[count : 2 * count], refs[2 * count]
    copies = [
        pltpu.make_async_copy(source, target, sem.at[k])
        for k, (source, target) in enumerate(zip(sources, targets))
    ]
    for copy in copies:
        copy.start()
    for copy in copies:
        copy.wait()


def hand_over(arrays):
    anywhere = pl.BlockSpec(memory_space=pl.ANY)
    return pl.pallas_call(
        functools.partial(hand_over_kernel, len(arrays)),
        out_shape=tuple(jax.ShapeDtypeStruct(a.shape, a.dtype) for a in arrays),
        in_specs=[pl.BlockSpec(memory_space=pltpu.VMEM)] * len(arrays),
        out_specs=(anywhere,) * len(arrays),
        scratch_shapes=[pltpu.SemaphoreType.DMA((len(arrays),))],
        name=hand_over.__name__,
    )(*arrays)


def blocks_of(rows):
    return rows.reshape(rows.shape[0], NORM_GROUPS, -1)


def spread(values):
    return jnp.repeat(values, C // NORM_GROUPS)


def in_halves(
    image,
    embedding,
    caption,
    item_of_band,
    out_grad,
    norm_gains,
    norm_biases,
    conv_first,
    conv_second,
    conv_biases,
    embed_weight,
    embed_bias,
    qkv_weight,
    qv_bias,
    text_weight,
    text_bias,
    proj_weight,
    proj_bias,
):
    low = jnp.bfloat16
    pixels = image.shape[1]
    position = lax.axis_index(ROWS)
    items = item_of_band[0]
    slots = items.shape[0]
    by_row = (-1, W, C)
    ahead = front(
        0,
        items,
        dict(
            embedding=embedding[0],
            norm_gains=norm_gains,
            norm_biases=norm_biases,
            conv_biases=conv_biases,
            embed_bias=embed_bias[None],
            qv_bias=qv_bias[None],
            text_bias=text_bias[None],
            proj_bias=proj_bias[None],
        ),
        dict(
            image=image.reshape(by_row),
            conv_first=conv_first,
            embed_weight=embed_weight,
            upstream_pixels=out_grad[0],
            proj_weight=proj_weight,
            conv_second=conv_second,
            caption=caption[0, 0],
            text_weight=text_weight,
            qkv_weight=qkv_weight,
        ),
    )
    found = attend(2, items, ahead)
    slot_of_band = (jnp.arange(slots)[:, None] == items[None, :]).astype(jnp.float32)
    row_share = EMB // lax.axis_size(ROWS)
    share = lax.dynamic_slice_in_dim(embedding[0], position * row_share, row_share, 1)
    silu_share = jax.nn.silu(share.astype(jnp.float32)).astype(low)
    out = back(
        1,
        ahead.vectors,
        jnp.repeat(slot_of_band, 128, axis=1),
        silu_share,
        embedding[0],
        dict(
            outcome=found.outcome,
            pair_grads=found.pair_grads,
            word_grads=found.word_grads,
            middle=ahead.middle,
            qkv_weight=qkv_weight,
            proj_weight=proj_weight,
            upstream=out_grad[0],
            act_three=ahead.act_three,
            caption=caption[0, 0],
            conv_second=conv_second,
            conv_first=conv_first,
            hidden=ahead.hidden,
            act_two=ahead.act_two,
            act_one=ahead.act_one,
            far_caption=ahead.far_caption,
            far_act_one=ahead.far_act_one,
            far_act_two=ahead.far_act_two,
            image=image.reshape(by_row),
            text_weight=text_weight,
            embed_weight=embed_weight,
        ),
    )
    out = types.SimpleNamespace(**dict(zip(vars(out), hand_over(list(vars(out).values())))))
    return (
        out.result[None],
        out.image_grad.reshape(1, pixels, C),
        out.embedding_grad[None],
        out.caption_grad[None, None],
        out.norm_gains_grad,
        out.norm_biases_grad,
        out.conv_first_grad,
        out.conv_second_grad,
        out.conv_biases_grad,
        out.embed_weight_grad,
        out.embed_bias_grad.reshape(-1),
        out.qkv_grad,
        out.qv_bias_grad.reshape(-1),
        out.text_grad,
        out.text_bias_grad.reshape(-1),
        out.proj_grad,
        out.proj_bias_grad.reshape(-1),
    )


def shards(
    image,
    embedding,
    caption,
    item_of_band,
    out_grad,
    norm_gains,
    norm_biases,
    conv_first,
    conv_second,
    conv_biases,
    embed_weight,
    embed_bias,
    qkv_weight,
    qv_bias,
    text_weight,
    text_bias,
    proj_weight,
    proj_bias,
):
    low = jnp.bfloat16
    full = jnp.float32
    pixels = image.shape[1]
    band_items = item_of_band[0]
    slots = band_items.shape[0]
    if slots == 2 * SPAN and lax.axis_size(ITEMS) == 2 and HEADS == SPAN:
        return in_halves(
            image,
            embedding,
            caption,
            item_of_band,
            out_grad,
            norm_gains,
            norm_biases,
            conv_first,
            conv_second,
            conv_biases,
            embed_weight,
            embed_bias,
            qkv_weight,
            qv_bias,
            text_weight,
            text_bias,
            proj_weight,
            proj_bias,
        )
    position = lax.axis_index(ROWS)
    my_item = band_items[position]
    slot_hot = (jnp.arange(slots) == my_item).astype(full)
    item_count = jnp.sum((band_items == my_item).astype(full)) * pixels * (C // NORM_GROUPS)
    reach = position + jnp.arange(-REACH, REACH + 1)
    near = (reach >= 0) & (reach < slots)
    near = near & (band_items[jnp.clip(reach, 0, slots - 1)] == my_item)
    keep = jnp.concatenate(
        [
            jnp.full((W, 1), near[REACH - 1]),
            jnp.full((pixels, 1), True),
            jnp.full((W, 1), near[REACH + 1]),
        ]
    )
    own_lead = jnp.logical_not(near[REACH - 1])

    def totals(ident, first, second, edges=None):
        sums = jnp.stack([jnp.sum(blocks_of(first), axis=(0, 2)), jnp.sum(blocks_of(second), axis=(0, 2))])
        tile = jnp.pad(sums, ((0, 6), (0, 128 - NORM_GROUPS)))
        if edges is not None:
            outcome = exchange(ident, slots, tile, (edges[:W], edges[-W:]))
        else:
            outcome = exchange(ident, slots, tile)
        summed = jnp.sum(jnp.where(near[:, None, None], outcome[0], 0.0), axis=0)
        summed = summed[:2, :NORM_GROUPS] / item_count
        return summed, outcome[1:]

    def stats(summed):
        scales = lax.rsqrt(summed[1] - summed[0] * summed[0] + epsilon)
        return spread(summed[0]), spread(scales)

    inputs = image[0].astype(full)
    summed, (above, below) = totals(0, inputs, inputs * inputs, image[0])
    means_one, scales_one = stats(summed)
    padded = jnp.concatenate([above, image[0], below]).astype(full)
    unit_padded = (padded - means_one) * scales_one
    normed_padded = unit_padded * norm_gains[0] + norm_biases[0]
    act_one_padded = jnp.where(keep, jax.nn.silu(normed_padded), 0.0).astype(low)
    unit_one = unit_padded[W:-W]
    normed_one = normed_padded[W:-W]
    taps_one = jnp.concatenate(taps_of(act_one_padded, False), axis=1)
    hidden_one = dot(taps_one, conv_first) + conv_biases[0]
    embed_silu = jax.nn.silu(embedding[0].astype(full)).astype(low)
    my_silu = dot(slot_hot.astype(low)[None], embed_silu).astype(low)
    modulation = dot(my_silu, embed_weight)[0] + embed_bias
    scale_part = modulation[:C]
    shift_part = modulation[C:]
    summed, (above, below) = totals(1, hidden_one, hidden_one * hidden_one, hidden_one)
    means_two, scales_two = stats(summed)
    hidden_padded = jnp.concatenate([above, hidden_one, below])
    unit_padded = (hidden_padded - means_two) * scales_two
    normed_padded = unit_padded * norm_gains[1] + norm_biases[1]
    shifted_padded = normed_padded * (1.0 + scale_part) + shift_part
    act_two_padded = jnp.where(keep, jax.nn.silu(shifted_padded), 0.0).astype(low)
    unit_two = unit_padded[W:-W]
    normed_two = normed_padded[W:-W]
    shifted = shifted_padded[W:-W]
    taps_two = jnp.concatenate(taps_of(act_two_padded, False), axis=1)
    middle = inputs + dot(taps_two, conv_second) + conv_biases[1]
    summed, _ = totals(2, middle, middle * middle)
    means_three, scales_three = stats(summed)
    unit_three = (middle - means_three) * scales_three
    act_three = (unit_three * norm_gains[2] + norm_biases[2]).astype(low)
    projected = dot(act_three, qkv_weight)
    queries = (projected[:, :C] + qv_bias[:C]).astype(low)
    keys_values = jnp.concatenate(
        [projected[:, C : 2 * C], projected[:, 2 * C :] + qv_bias[C:]], axis=1
    ).astype(low)
    captions = caption[0, 0]
    text_kv = lax.cond(
        own_lead,
        lambda: (dot(captions, text_weight) + text_bias).astype(low),
        lambda: jnp.zeros((TEXT, 2 * C), low),
    )
    upstream = out_grad[0]
    upstream_float = upstream.astype(full)
    attended_grad = dot_last(upstream, proj_weight).astype(low)
    group = lax.axis_index(ITEMS)
    groups = lax.axis_size(ITEMS)
    attended_low, query_low, key_value_low, text_low = attention_by_band(
        band_items, position, queries, keys_values, text_kv, attended_grad
    )
    result = middle + dot(attended_low, proj_weight) + proj_bias
    proj_weight_grad = dot_first(attended_low, upstream)
    proj_bias_grad = jnp.sum(upstream_float, axis=0)
    qkv_grad = jnp.concatenate([query_low, key_value_low], axis=1)
    qkv_weight_grad = dot_first(act_three, qkv_grad)
    qv_bias_grad = jnp.sum(
        jnp.concatenate([query_low, key_value_low[:, C:]], axis=1).astype(full), axis=0
    )
    text_weight_grad = dot_first(captions, text_low)
    text_bias_grad = jnp.sum(text_low.astype(full), axis=0)
    caption_grad = dot_last(text_low, text_weight)[None, None]
    three_grad = dot_last(qkv_grad, qkv_weight)
    gain_three = jnp.sum(three_grad * unit_three, axis=0)
    bias_three = jnp.sum(three_grad, axis=0)

    def conv_back(padded, weight):
        views = jnp.stack(taps_of(padded, True))
        return jnp.einsum(
            "tpd,tcd->pc", views, weight.reshape(9, C, C), preferred_element_type=full
        )

    def norm_back(ident, grad_unit, unit_value, scales, base, with_edges=True):
        scaled = base + grad_unit * scales
        edges = jnp.concatenate([scaled, unit_value], axis=1) if with_edges else None
        summed, around = totals(ident, grad_unit, grad_unit * unit_value, edges)
        mean_grad, mean_cross = spread(summed[0]) * scales, spread(summed[1]) * scales
        if not with_edges:
            return scaled - mean_grad - unit_value * mean_cross
        both = jnp.concatenate([around[0], edges, around[1]])
        return both[:, :C] - mean_grad - both[:, C:] * mean_cross

    middle_padded = norm_back(3, three_grad * norm_gains[2], unit_three, scales_three, upstream_float)
    middle_grad = middle_padded[W:-W]
    low_padded = jnp.where(keep, middle_padded, 0.0).astype(low)
    hidden_two_low = low_padded[W:-W]
    conv_bias_two = jnp.sum(hidden_two_low.astype(full), axis=0)
    conv_second_grad = dot_first(taps_two, hidden_two_low)
    act_two_grad = conv_back(low_padded, conv_second)
    shifted_grad = act_two_grad * silu_slope(shifted)
    modulation_grad = jnp.concatenate(
        [jnp.sum(shifted_grad * normed_two, axis=0), jnp.sum(shifted_grad, axis=0)]
    )
    normed_two_grad = shifted_grad * (1.0 + scale_part)
    gain_two = jnp.sum(normed_two_grad * unit_two, axis=0)
    bias_two = jnp.sum(normed_two_grad, axis=0)
    hidden_back = norm_back(4, normed_two_grad * norm_gains[1], unit_two, scales_two, 0.0)
    low_padded = jnp.where(keep, hidden_back, 0.0).astype(low)
    hidden_one_low = low_padded[W:-W]
    conv_bias_one = jnp.sum(hidden_one_low.astype(full), axis=0)
    conv_first_grad = dot_first(taps_one, hidden_one_low)
    act_one_grad = conv_back(low_padded, conv_first)
    normed_one_grad = act_one_grad * silu_slope(normed_one)
    gain_one = jnp.sum(normed_one_grad * unit_one, axis=0)
    bias_one = jnp.sum(normed_one_grad, axis=0)
    image_grad = norm_back(
        5, normed_one_grad * norm_gains[0], unit_one, scales_one, middle_grad, False
    )
    group_hot = (jnp.arange(groups) == group).astype(full)
    tables = group_hot[:, None, None] * slot_hot[None, :, None] * modulation_grad
    vectors = jnp.concatenate(
        [
            gain_one,
            gain_two,
            gain_three,
            bias_one,
            bias_two,
            bias_three,
            conv_bias_one,
            conv_bias_two,
            qv_bias_grad,
            text_bias_grad,
            proj_bias_grad,
        ]
    )
    small = jnp.concatenate([tables.reshape(-1, C), vectors.reshape(-1, C)])
    row_share = EMB // lax.axis_size(ROWS)
    silu_share = lax.dynamic_slice_in_dim(embed_silu, position * row_share, row_share, 1)
    grads = (conv_first_grad, conv_second_grad, qkv_weight_grad, text_weight_grad, proj_weight_grad)
    grads = [g.astype(low) for g in grads]
    small = lax.psum(small.astype(low), (ROWS, ITEMS)).astype(full)
    tables_sum = small[: groups * slots * 2].reshape(groups, slots, 2 * C).astype(low)
    part = dot_first(silu_share, jnp.take(tables_sum, group, axis=0)).astype(low)
    matrices = [lax.psum_scatter(g, ROWS, scatter_dimension=0, tiled=True) for g in grads]
    *matrices, embed_weight_grad = [
        lax.psum(m, ITEMS).astype(full) for m in matrices + [part]
    ]
    vectors_sum = small[groups * slots * 2 :]
    modulation_low = jnp.take(tables_sum, group, axis=0)
    embed_bias_grad = jnp.sum(tables_sum.astype(full), axis=(0, 1))
    embedding_grad = dot_last(modulation_low, embed_weight) * silu_slope(embedding[0].astype(full))
    return (
        result.astype(low)[None],
        image_grad[None],
        embedding_grad[None],
        caption_grad,
        vectors_sum[0:3],
        vectors_sum[3:6],
        matrices[0],
        matrices[1],
        vectors_sum[6:8],
        embed_weight_grad,
        embed_bias_grad,
        matrices[2],
        vectors_sum[8:10].reshape(-1),
        matrices[3],
        vectors_sum[10:12].reshape(-1),
        matrices[4],
        vectors_sum[12],
    )


def solution(mesh):
    in_specs = (
        P(ITEMS, ROWS, None),
        P(ITEMS, None, None),
        P(ITEMS, ROWS, None, None),
        P(ITEMS, None),
        P(ITEMS, ROWS, None),
        P(),
        P(),
        P(),
        P(),
        P(),
        P(),
        P(),
        P(),
        P(),
        P(),
        P(),
        P(),
        P(),
    )
    out_specs = (
        P(ITEMS, ROWS, None),
        P(ITEMS, ROWS, None),
        P(ITEMS, None, None),
        P(ITEMS, ROWS, None, None),
        P(),
        P(),
        P(ROWS, None),
        P(ROWS, None),
        P(),
        P(ROWS, None),
        P(),
        P(ROWS, None),
        P(),
        P(ROWS, None),
        P(),
        P(ROWS, None),
        P(),
    )
    return jax.shard_map(shards, mesh=mesh, in_specs=in_specs, out_specs=out_specs, check_vma=False)
```

```python
import functools
import types
import typing

import jax
import jax.numpy as jnp
from jax import lax
from jax.experimental import pallas as pl
from jax.experimental.pallas import tpu as pltpu
from jax.sharding import PartitionSpec as P

C = 512
HEADS = 8
HEAD = 64
EMB = 2048
TEXT = 128
NORM_GROUPS = 32
W = 64
SPAN = 8
ROWS, ITEMS = "rows", "items"


epsilon = 1e-05


def from_behind(array, axis, by):
    length = lax.axis_size(axis)
    pairs = [(i, i + by) for i in range(length) if 0 <= i + by < length]
    return lax.ppermute(array, axis, pairs)


def as_sent(array):
    return jax.tree.map(lambda a: a.astype(jnp.bfloat16) if a.dtype == jnp.float32 else a, array)


def keep_state(state):
    return state


def silu_slope(source):
    sigma = jax.nn.sigmoid(source)
    return sigma * (1.0 + source * (1.0 - sigma))


def dot_first(left_side, right_side):
    return lax.dot_general(
        left_side, right_side, (((0,), (0,)), ((), ())), preferred_element_type=jnp.float32
    )


def dot_last(left_side, right_side):
    return lax.dot_general(
        left_side, right_side, (((1,), (1,)), ((), ())), preferred_element_type=jnp.float32
    )


def head_split(source):
    return source.reshape(source.shape[0], HEADS, HEAD)


def piece_scores(query_heads, key_piece, allowed):
    key_heads = head_split(key_piece[:, :C])
    scores = jnp.einsum(
        "qhd,khd->hqk", query_heads, key_heads, preferred_element_type=jnp.float32
    ) * HEAD ** (-0.5)
    return jnp.where(allowed[None, None, :], scores, -jnp.inf)


def piece_grads(query_heads, grad_heads, log_total, row_dots, key_piece, allowed):
    scores = piece_scores(query_heads, key_piece, allowed)
    weights = jnp.exp(scores - log_total[:, :, None])
    value_heads = head_split(key_piece[:, C:])
    weight_grad = jnp.einsum(
        "qhd,khd->hqk", grad_heads, value_heads, preferred_element_type=jnp.float32
    )
    score_grad = (weights * (weight_grad - row_dots[:, :, None])).astype(jnp.bfloat16)
    outcome = []
    key_heads = head_split(key_piece[:, :C])
    query_grad = jnp.einsum(
        "hqk,khd->qhd", score_grad, key_heads, preferred_element_type=jnp.float32
    ) * HEAD ** (-0.5)
    outcome.append(query_grad.reshape(query_grad.shape[0], C))
    key_grad = jnp.einsum(
        "hqk,qhd->khd", score_grad, query_heads, preferred_element_type=jnp.float32
    ) * HEAD ** (-0.5)
    value_grad = jnp.einsum(
        "hqk,qhd->khd", weights.astype(jnp.bfloat16), grad_heads, preferred_element_type=jnp.float32
    )
    outcome.append(jnp.concatenate([key_grad.reshape(-1, C), value_grad.reshape(-1, C)], axis=1))
    return tuple(outcome)


def source_masks(band_items, source, my_item, pixels):
    slots = band_items.shape[0]
    inside = (source >= 0) & (source < slots)
    clipped = jnp.clip(source, 0, slots - 1)
    source_item = band_items[clipped]
    before_item = band_items[jnp.maximum(clipped - 1, 0)]
    same_item = inside & (source_item == my_item)
    leading = same_item & ((clipped == 0) | (before_item != source_item))
    allowed = jnp.concatenate(
        [jnp.broadcast_to(same_item, (pixels,)), jnp.broadcast_to(leading, (TEXT,))]
    )
    return (allowed, same_item)


REACH = SPAN - 1
LOG2E = 1.4426950408889634
FAR_ABOVE = 1e30
PIX = 512


def dot(left, right):
    return jnp.dot(left, right, preferred_element_type=jnp.float32)


def reach_of(here, slots):
    first = here < SPAN
    low = jnp.maximum(jnp.where(first, 0, SPAN), here - REACH)
    high = jnp.minimum(jnp.where(first, SPAN - 1, slots - 1), here + REACH)
    return low, high


def exchange_kernel(slots, with_edges, *refs):
    if with_edges:
        tile, top, bottom, window, above, below, send_sem, recv_sem, edge_send, edge_recv = refs
    else:
        tile, window, send_sem, recv_sem = refs
    here = lax.axis_index(ROWS)
    low, high = reach_of(here, slots)
    offsets = [o for o in range(-REACH, REACH + 1) if o != 0]

    def reached(offset):
        return (here + offset >= low) & (here + offset <= high)

    barrier = pltpu.get_barrier_semaphore()
    for o in offsets:

        @pl.when(reached(o))
        def _(o=o):
            pl.semaphore_signal(barrier, 1, device_id={ROWS: here + o})

    pl.semaphore_wait(barrier, high - low)

    def edge_copy(o):
        source, target, k = (top, below, 0) if o < 0 else (bottom, above, 1)
        return pltpu.make_async_remote_copy(
            source, target, edge_send.at[k], edge_recv.at[k], device_id={ROWS: here + o}
        )

    def tile_copy(o):
        return pltpu.make_async_remote_copy(
            tile,
            window.at[REACH - o],
            send_sem.at[REACH - o],
            recv_sem.at[REACH - o],
            device_id={ROWS: here + o},
        )

    if with_edges:
        for o in (-1, 1):

            @pl.when(reached(o))
            def _(o=o):
                edge_copy(o).start()

    for o in offsets:

        @pl.when(reached(o))
        def _(o=o):
            tile_copy(o).start()

        @pl.when(jnp.logical_not(reached(-o)))
        def _(o=o):
            window[REACH - o] = jnp.zeros_like(tile)

    window[REACH] = tile[...]
    if with_edges:

        @pl.when(jnp.logical_not(reached(-1)))
        def _():
            above[...] = jnp.zeros_like(above)

        @pl.when(jnp.logical_not(reached(1)))
        def _():
            below[...] = jnp.zeros_like(below)

    for o in offsets:

        @pl.when(reached(o))
        def _(o=o):
            tile_copy(o).wait_send()

        @pl.when(reached(-o))
        def _(o=o):
            tile_copy(o).wait_recv()

    if with_edges:
        for o in (-1, 1):

            @pl.when(reached(o))
            def _(o=o):
                edge_copy(o).wait_send()

            @pl.when(reached(-o))
            def _(o=o):
                edge_copy(o).wait_recv()


def exchange(ident, slots, tile, edges=None):
    vmem = pl.BlockSpec(memory_space=pltpu.VMEM)
    shapes = [jax.ShapeDtypeStruct((2 * REACH + 1,) + tile.shape, tile.dtype)]
    scratch = [pltpu.SemaphoreType.DMA((2 * REACH + 1,))] * 2
    operands = [tile]
    if edges is not None:
        shapes += [jax.ShapeDtypeStruct(e.shape, e.dtype) for e in edges]
        scratch += [pltpu.SemaphoreType.DMA((2,))] * 2
        operands += list(edges)
    return pl.pallas_call(
        functools.partial(exchange_kernel, slots, edges is not None),
        out_shape=tuple(shapes),
        in_specs=[vmem] * len(operands),
        out_specs=(vmem,) * len(shapes),
        scratch_shapes=scratch,
        compiler_params=pltpu.CompilerParams(collective_id=ident, has_side_effects=True),
        name=f"exchange_{ident}",
    )(*operands)


def attention_by_band(band_items, position, queries, keys_values, text_kv, attended_grad):
    my_item = band_items[position]
    pixels = queries.shape[0]
    own_allowed, own_same = source_masks(band_items, position, my_item, pixels)
    packed = jnp.concatenate([keys_values, text_kv], axis=0)
    pieces = [(0, packed, own_allowed, own_same)]
    for distance in range(1, SPAN):
        for offset in (distance, -distance):
            arrived = from_behind(packed, ROWS, offset)
            allowed, same_item = source_masks(band_items, position - offset, my_item, pixels)
            pieces.append((offset, arrived, allowed, same_item))
    query_heads = head_split(queries)
    row_top = jnp.full((HEADS, pixels), -jnp.inf, jnp.float32)
    weight_sum = jnp.zeros((HEADS, pixels), jnp.float32)
    for offset, key_piece, allowed, same_item in pieces:

        def gather_scores(state, key_piece=key_piece, allowed=allowed):
            top_old, sum_old = state
            scores = piece_scores(query_heads, key_piece, allowed)
            top_new = jnp.maximum(top_old, jnp.max(scores, axis=2))
            sum_new = sum_old * jnp.exp(top_old - top_new) + jnp.sum(
                jnp.exp(scores - top_new[:, :, None]), axis=2
            )
            return (top_new, sum_new)

        row_top, weight_sum = lax.cond(same_item, gather_scores, keep_state, (row_top, weight_sum))
    log_total = row_top + jnp.log(weight_sum)
    attended = jnp.zeros((pixels, HEADS, HEAD), jnp.float32)
    for offset, key_piece, allowed, same_item in pieces:

        def add_values(totals, key_piece=key_piece, allowed=allowed):
            scores = piece_scores(query_heads, key_piece, allowed)
            weights = jnp.exp(scores - log_total[:, :, None]).astype(jnp.bfloat16)
            return totals + jnp.einsum(
                "hqk,khd->qhd",
                weights,
                head_split(key_piece[:, C:]),
                preferred_element_type=jnp.float32,
            )

        attended = lax.cond(same_item, add_values, keep_state, attended)
    attended_flat = attended.reshape(pixels, C)
    row_dots = jnp.sum(
        (attended_grad.astype(jnp.float32) * attended_flat).reshape(pixels, HEADS, HEAD), axis=2
    ).T
    grad_heads = head_split(attended_grad)
    query_grad = jnp.zeros((pixels, C), jnp.float32)
    packed_grad = jnp.zeros((pixels + TEXT, 2 * C), jnp.float32)
    zero_piece = jnp.zeros((pixels + TEXT, 2 * C), jnp.float32)
    for offset, key_piece, allowed, same_item in pieces:

        def grad_both(totals, key_piece=key_piece, allowed=allowed):
            outcome = piece_grads(query_heads, grad_heads, log_total, row_dots, key_piece, allowed)
            return (totals + outcome[0], outcome[1])

        def grad_none(totals):
            return (totals, zero_piece)

        query_grad, piece_grad = lax.cond(same_item, grad_both, grad_none, query_grad)
        if offset == 0:
            packed_grad = packed_grad + piece_grad
        else:
            packed_grad = packed_grad + from_behind(
                as_sent(piece_grad), ROWS, -offset
            ).astype(jnp.float32)
    packed_low = packed_grad.astype(jnp.bfloat16)
    return (
        attended_flat.astype(jnp.bfloat16),
        query_grad.astype(jnp.bfloat16),
        packed_low[:pixels],
        packed_low[pixels:],
    )


def taps_of(rows, reverse):
    padded = rows.reshape(-1, W, rows.shape[1])
    row_list = [padded[:-2], padded[1:-1], padded[2:]]
    if reverse:
        row_list = row_list[::-1]
    zero_column = jnp.zeros_like(row_list[0][:, :1])
    views = []
    for row_view in row_list:
        left_view = jnp.concatenate([zero_column, row_view[:, :-1]], axis=1)
        right_view = jnp.concatenate([row_view[:, 1:], zero_column], axis=1)
        view_list = [left_view, row_view, right_view]
        if reverse:
            view_list = view_list[::-1]
        views = views + view_list
    return [view.reshape(-1, rows.shape[1]) for view in views]


class Vectors(typing.NamedTuple):
    mean_one: jax.Array
    scale_one: jax.Array
    gain_one: jax.Array
    bias_one: jax.Array
    mean_two: jax.Array
    scale_two: jax.Array
    gain_two: jax.Array
    bias_two: jax.Array
    mean_three: jax.Array
    scale_three: jax.Array
    gain_three: jax.Array
    bias_three: jax.Array
    stretch: jax.Array
    shift: jax.Array
    proj_bias: jax.Array
    keep_above: jax.Array
    keep_below: jax.Array
    per_item: jax.Array


def grouped(names, refs):
    found, position = types.SimpleNamespace(), 0
    for name, count in names:
        if count is None:
            setattr(found, name, refs[position])
            position += 1
        else:
            setattr(found, name, refs[position : position + count])
            position += count
    return found


def call_named(
    kernel, ident, scalars, inputs, anywhere, outs, scratch, semaphores, far=types.MappingProxyType({})
):
    names = [(name, None) for name in [*scalars, *inputs, *anywhere, *outs, *far]]
    buffers = []
    for name, entry in scratch.items():
        many = isinstance(entry, list)
        names.append((name, len(entry) if many else None))
        buffers += [pltpu.VMEM(*e) for e in (entry if many else [entry])]
    names += [(name, None) for name in semaphores]
    vmem = pl.BlockSpec(memory_space=pltpu.VMEM)
    outcome = pl.pallas_call(
        functools.partial(kernel, names),
        out_shape=tuple(jax.ShapeDtypeStruct(*o) for o in [*outs.values(), *far.values()]),
        in_specs=[pl.BlockSpec(memory_space=pltpu.SMEM)] * len(scalars)
        + [vmem] * len(inputs)
        + [pl.BlockSpec(memory_space=pl.ANY)] * len(anywhere),
        out_specs=(vmem,) * len(outs) + (pl.BlockSpec(memory_space=pl.ANY),) * len(far),
        scratch_shapes=buffers + [pltpu.SemaphoreType.DMA(s) for s in semaphores.values()],
        compiler_params=pltpu.CompilerParams(
            collective_id=ident, has_side_effects=True, vmem_limit_bytes=60 << 20
        ),
        name=kernel.__name__,
    )(*[v for group in (scalars, inputs, anywhere) for v in dict(group).values()])
    return types.SimpleNamespace(**dict(zip([*outs, *far], outcome)))


VECTOR_ROWS = 24
FAR, NEAR, SIDE, CORE, GROUP = range(5)
CROSS = (FAR, NEAR, SIDE)
GROUP_FIRST = (GROUP, NEAR, SIDE, FAR)
STREAMS = (
    (144, C // 4, (SIDE, NEAR, FAR)),
    (144, C // 4, (NEAR, SIDE, FAR)),
    (144, C // 4, (SIDE, NEAR, FAR)),
    (144, C // 4, (NEAR, SIDE, FAR)),
    (64, C // 2, (SIDE, NEAR, FAR)),
    (64, C // 2, (NEAR, SIDE, FAR)),
    (16, 3 * C // 2, GROUP_FIRST),
    (16, C // 2, GROUP_FIRST),
)
FIRST_CONV, SECOND_CONV, WORDS, QKV, PROJ = 0, 2, 4, 6, 7
FIRST_LANDING = [sum(len(s[2]) for s in STREAMS[:k]) for k in range(len(STREAMS))]
HALF_SUMS, GROUP_SUMS = -1, -2
TAIL = (6, 4, 5, 6, 2, -1, 0, 1, 3, 2, -2, 1, 3, 2, 0, 3, 1, 0, 1, 0)
IMAGE_ROWS = 8


class Band:
    def __init__(self, r):
        self.r = r
        self.row = lax.axis_index(ROWS)
        self.group = lax.axis_index(ITEMS)
        self.lane = self.row % SPAN
        self.base = self.row - self.lane
        row = self.row
        self.place = [row // 8, (row // 4) % 2, (row // 2) % 2, row % 2, self.group]
        self.partner = [
            {ROWS: row + (1 - 2 * self.place[d]) * (8 >> d)} for d in range(CORE + 1)
        ]
        self.partner.append({ITEMS: 1 - self.group})
        self.others = [(self.lane + o) % SPAN for o in range(1, SPAN)]
        self.peers = [{ROWS: self.base + other} for other in self.others]
        self.has_above, self.has_below = self.lane > 0, self.lane < SPAN - 1

    def meet(self, further=()):
        barrier = pltpu.get_barrier_semaphore()
        targets = self.peers + list(further)
        for target in targets:
            pl.semaphore_signal(barrier, 1, device_id=target)
        pl.semaphore_wait(barrier, len(targets))

    def remote(self, source, target, send, recv, device):
        return pltpu.make_async_remote_copy(source, target, send, recv, device_id=device)

    def edges(self, k, top, bottom, target):
        r = self.r
        up = self.remote(
            top,
            target.at[IMAGE_ROWS + 1],
            r.edge_send.at[k, 0],
            r.edge_recv.at[k, 0],
            {ROWS: self.row - 1},
        )
        down = self.remote(
            bottom,
            target.at[0],
            r.edge_send.at[k, 1],
            r.edge_recv.at[k, 1],
            {ROWS: self.row + 1},
        )
        pl.when(self.has_above)(up.start)
        pl.when(self.has_below)(down.start)
        return up, down

    def wait_edges(self, pair):
        up, down = pair

        @pl.when(self.has_above)
        def _():
            up.wait_send()
            down.wait_recv()

        @pl.when(self.has_below)
        def _():
            down.wait_send()
            up.wait_recv()

    def zero_edges(self, target):
        @pl.when(jnp.logical_not(self.has_above))
        def _():
            target[0] = jnp.zeros(target.shape[1:], target.dtype)

        @pl.when(jnp.logical_not(self.has_below))
        def _():
            target[IMAGE_ROWS + 1] = jnp.zeros(target.shape[1:], target.dtype)

    def send_tile(self, k, source, target):
        r = self.r
        copies = []
        for o in range(1, SPAN):
            copies.append(
                self.remote(
                    source,
                    target.at[self.lane],
                    r.tile_send.at[k, o],
                    r.tile_recv.at[k, o],
                    self.peers[o - 1],
                )
            )
        for copy in copies:
            copy.start()
        target[self.lane] = source[...]
        return copies

    def swap(self, k, source, target, order=range(1, SPAN)):
        r = self.r
        copies = []
        for o in order:
            copies.append(
                self.remote(
                    source.at[self.others[o - 1]],
                    target.at[self.lane],
                    r.swap_send.at[k, o],
                    r.swap_recv.at[k, o],
                    self.peers[o - 1],
                )
            )
            copies[-1].start()
        return copies

    def fill_blocks(self):
        rows = lax.broadcasted_iota(jnp.int32, (C, C), 0) // (C // NORM_GROUPS)
        columns = lax.broadcasted_iota(jnp.int32, (C, C), 1) // (C // NORM_GROUPS)
        self.r.blocks[...] = jnp.where(rows == columns, 1.0, 0.0).astype(jnp.bfloat16)

    def item_means(self, window, masks, per_item):
        low, full = jnp.bfloat16, jnp.float32
        tile = jnp.zeros((8, C // 4), full)
        for b in range(SPAN):
            tile = tile + jnp.where(masks[b][:, 0 : C // 4] > 0.0, window[b], 0.0)
        first, second = [
            jnp.concatenate([tile[j : j + 1, :] for j in range(4 * k, 4 * k + 4)], axis=1)
            for k in range(2)
        ]
        rows = lax.broadcasted_iota(jnp.int32, (8, C), 0)
        total = jnp.where(rows == 0, first, jnp.where(rows == 1, second, 0.0)) * per_item
        coarse = total.astype(low)
        rest = total - coarse.astype(full)
        finer = rest.astype(low)
        finest = (rest - finer.astype(full)).astype(low)
        blocks = self.r.blocks[...]
        return dot(coarse, blocks) + dot(finer, blocks) + dot(finest, blocks)


def sums_tile(first, second):
    rows = lax.broadcasted_iota(jnp.int32, (8, C // 4), 0)
    tile = jnp.zeros((8, C // 4), jnp.float32)
    for k, values in enumerate((first, second)):
        for j in range(4):
            part = values[:, j * (C // 4) : (j + 1) * (C // 4)]
            tile = jnp.where(rows == 4 * k + j, part, tile)
    return tile


def column_sum(values):
    return jnp.sum(values, axis=0, keepdims=True)


def side_shifts(values):
    rows = lax.broadcasted_iota(jnp.int32, values.shape, 0)
    from_left = jnp.where(rows == 0, 0.0, pltpu.roll(values, 1, 0))
    from_right = jnp.where(rows == W - 1, 0.0, pltpu.roll(values, W - 1, 0))
    return from_left, from_right


def kept(i, values, vec):
    keep = jnp.where(i == 0, vec.keep_above, jnp.where(i == IMAGE_ROWS + 1, vec.keep_below, 1.0))
    return jnp.where(keep > 0.0, values, 0.0)


def back_kernel(names, *refs):
    low, full = jnp.bfloat16, jnp.float32
    r = grouped(names, refs)
    band = Band(r)
    lane, group, place, partner = band.lane, band.group, band.place, band.partner
    core = place[CORE]
    remote = band.remote
    across = {ROWS: partner[CORE][ROWS], ITEMS: 1 - group}
    band.meet((partner[FAR], partner[GROUP], across))
    quad = (partner[CORE], partner[GROUP], across)
    quarter = 2 * group + core
    quarters = (2 * group + 1 - core, 2 * (1 - group) + core, 2 * (1 - group) + 1 - core)

    def columns_of(which, size):
        return pl.ds(pl.multiple_of(which * size, size), size)

    def to_quad(kind, source, target):
        copies = [
            remote(
                source(quarters[i]), target.at[i], r.quad_send.at[kind, i], r.quad_recv.at[kind, i], quad[i]
            )
            for i in range(3)
        ]
        for copy in copies:
            copy.start()
        return copies


    swaps = band.swap(0, r.pair_grads, r.head_pairs) + band.swap(1, r.word_grads, r.head_words)

    loads = types.SimpleNamespace()

    def load(k, source, target):
        copy = pltpu.make_async_copy(source, target, r.load_sem.at[k])
        copy.start()
        return copy

    loads.outcome = load(0, r.outcome, r.heads)
    loads.pair_grads = load(1, r.pair_grads.at[lane], r.head_pairs.at[lane])
    loads.word_grads = load(14, r.word_grads.at[lane], r.head_words.at[lane])
    loads.middle = load(2, r.middle, r.mid)
    loads.qkv_weight = load(3, r.qkv_weight, r.qkv_w)
    loads.proj_weight = load(4, r.proj_weight, r.proj_w)
    loads.upstream = load(5, r.upstream, r.up)
    loads.act_three = load(6, r.act_three, r.act3)
    loads.caption = load(7, r.caption, r.caps.at[0])
    loads.far_caption = load(15, r.far_caption, r.caps.at[2])
    loads.conv_second = load(8, r.conv_second, r.conv_w)
    loads.hidden = load(9, r.hidden, r.hid)
    loads.act_two = load(10, r.act_two, r.acts_two.at[0])
    loads.far_act_two = load(16, r.far_act_two, r.acts_two.at[2])
    loads.act_one = load(11, r.act_one, r.acts_one.at[0])
    loads.far_act_one = load(17, r.far_act_one, r.acts_one.at[2])
    loads.image = load(12, r.image, r.img)
    loads.text_weight = load(13, r.text_weight, r.text_w)

    sibling = types.SimpleNamespace()

    def to_sibling(k, source, target):
        copy = remote(source, target, r.sib_send.at[k], r.sib_recv.at[k], partner[CORE])
        copy.start()
        return copy

    half = pl.ds(pl.multiple_of((1 - core) * (C // 2), C // 2), C // 2)
    sibling.upstream = to_sibling(0, r.upstream.at[:, half], r.sib_up)
    sibling.act3 = to_sibling(1, r.act_three, r.sib_act3)
    sibling.cap = to_sibling(2, r.caption, r.caps.at[1])
    sibling.far_cap = to_sibling(7, r.far_caption, r.caps.at[3])

    share_copy = remote(
        r.silu_share, r.other_share, r.small_send.at[2], r.small_recv.at[2], partner[GROUP]
    )
    share_copy.start()
    for target in (r.part_two, r.part_one):
        band.zero_edges(target)

    vec = Vectors(*[r.vectors[i : i + 1, :] for i in range(len(Vectors._fields))])
    norm_one = (vec.mean_one, vec.scale_one)
    norm_two = (vec.mean_two, vec.scale_two)
    norm_three = (vec.mean_three, vec.scale_three)

    masks = [r.vectors[VECTOR_ROWS + b : VECTOR_ROWS + b + 1, :] for b in range(SPAN)]
    band.fill_blocks()

    def item_means(window):
        return band.item_means(window, masks, vec.per_item)

    class Stream:
        def __init__(self, k):
            self.k = k
            self.order = STREAMS[k][2]
            self.dims = [FAR, NEAR, SIDE, CORE, GROUP][: len(self.order) + 1]
            self.step = 0
            self.copies = []

        def at(self, ref, d, index):
            return ref.at[(slice(None),) * self.dims.index(d) + (index,)]

        def start(self):
            self.launch(r.grads[self.k])

        def launch(self, ref):
            k, step = self.k, self.step
            if step < len(self.order):
                d = self.order[step]
                self.copies = [
                    remote(
                        self.at(ref, d, 1 - place[d]),
                        r.landings[FIRST_LANDING[k] + step],
                        r.fold_send.at[k, step],
                        r.fold_recv.at[k, step],
                        partner[d],
                    )
                ]
                self.mine = self.at(ref, d, place[d])
                self.dims.remove(d)
            else:
                if GROUP in self.order:
                    places = (r.folded[k], r.whole[k - QKV], r.whole[k - QKV])
                    self.place = core
                else:
                    places = (r.folded[k],) * 3
                    self.place = quarter
                sources = (ref.at[1 - core], ref.at[core], ref.at[1 - core])
                ends = [
                    (source, target.at[self.place], device)
                    for source, target, device in zip(sources, places, quad)
                ]
                self.copies = [
                    remote(
                        source,
                        target,
                        r.fold_send.at[k, step + i],
                        r.fold_recv.at[k, step + i],
                        device,
                    )
                    for i, (source, target, device) in enumerate(ends)
                ]
                self.mine = ref.at[core]
            for copy in self.copies:
                copy.start()

        def advance(self):
            for copy in self.copies:
                copy.wait()
            if self.step < len(self.order):
                landed, mine = r.landings[FIRST_LANDING[self.k] + self.step], self.mine
                lead = landed.shape[:-2]
                pieces = 1
                for n in lead:
                    pieces *= n

                def add(i, carry):
                    index = []
                    for n in reversed(lead):
                        index.insert(0, i % n)
                        i = i // n
                    index = tuple(index)
                    landed[index] = landed[index] + mine[index]
                    return carry

                lax.fori_loop(0, pieces, add, 0)
                self.step += 1
                self.launch(landed)
            else:
                r.folded[self.k][self.place] = self.mine[...]
                self.step += 1

    streams = [Stream(k) for k in range(len(STREAMS))]

    def advance(*order):
        for k in order:
            streams[k].advance()

    loads.outcome.wait()
    for h in range(0, HEADS, 2):
        for k in range(2):
            pair = [r.heads[h + i, :, k * HEAD : (k + 1) * HEAD] for i in range(2)]
            r.joined[:, k * C + h * HEAD : k * C + (h + 2) * HEAD] = jnp.concatenate(pair, axis=1)
    sibling.attended = to_sibling(5, r.joined.at[:, 0:C], r.sib_attended)

    def pixel_block(ref, i, count=4):
        return ref[1 + i * count : 1 + (i + 1) * count].reshape(count * W, C)

    def unit(values, norm):
        return (values - norm[0]) * norm[1]

    def mine_of(ref, start, size):
        return ref[:, pl.ds(pl.multiple_of(start, size if size % 256 else 256), size)]

    for copy in (loads.middle, loads.qkv_weight, loads.proj_weight, loads.upstream):
        copy.wait()
    up_sum = jnp.zeros((1, C), full)
    for i in range(2):
        block = slice(i * 4 * W, (i + 1) * 4 * W)
        upstream = r.up[block, :].astype(full)
        up_sum = up_sum + column_sum(upstream)
        result = pixel_block(r.mid, i) + dot(r.joined[block, 0:C], r.proj_w[...]) + vec.proj_bias
        r.result[block, :] = result.astype(low)
        grad = dot_last(r.joined[block, C : 2 * C], r.qkv_w[:, 0:C])
        r.product[i * 4 : i * 4 + 4] = grad.reshape(4, W, C)
    sibling.upstream.wait()
    sibling.attended.wait()
    grad = dot_first(r.joined[:, 0:C], mine_of(r.up, core * (C // 2), C // 2))
    grad = grad + dot_first(r.sib_attended[...], r.sib_up[...])
    r.grads[PROJ][...] = grad.astype(low).reshape(r.grads[PROJ].shape)
    streams[PROJ].start()
    query_sum = column_sum(r.joined[:, C : 2 * C].astype(full))

    for copy in (loads.pair_grads, loads.word_grads):
        copy.wait()
    for copy in swaps:
        copy.wait()
    for h in range(0, HEADS, 2):
        for k in range(2):
            lanes = slice(k * HEAD, (k + 1) * HEAD)
            pair = [r.head_pairs[h + i, :, lanes] for i in range(2)]
            first = (2 + k) * C + h * HEAD
            r.joined[:, first : first + 2 * HEAD] = jnp.concatenate(pair, axis=1)
            pair = [r.head_words[h + i, :, lanes] for i in range(2)]
            first = k * C + h * HEAD
            r.joined_words[:, first : first + 2 * HEAD] = jnp.concatenate(pair, axis=1)
    three_half = C + (1 - core) * (3 * C // 2)
    sibling.qkv = to_sibling(
        6, r.joined.at[:, pl.ds(pl.multiple_of(three_half, C // 2), 3 * C // 2)], r.sib_qkv
    )
    word_copies = to_quad(0, lambda q: r.joined_words.at[:, columns_of(q, C // 2)], r.word_parts)
    r.own_word_part[...] = r.joined_words[:, columns_of(quarter, C // 2)]
    sibling.act2 = to_sibling(3, r.act_two, r.acts_two.at[1])
    sibling.far_act2 = to_sibling(8, r.far_act_two, r.acts_two.at[3])
    sibling.act1 = to_sibling(4, r.act_one, r.acts_one.at[1])
    sibling.far_act1 = to_sibling(9, r.far_act_one, r.acts_one.at[3])

    plain = jnp.zeros((1, C), full)
    crossed = jnp.zeros((1, C), full)
    for i in range(2):
        block = slice(i * 4 * W, (i + 1) * 4 * W)
        grad = dot_last(r.joined[block, 2 * C :], r.qkv_w[:, C:])
        grad = grad + r.product[i * 4 : i * 4 + 4].reshape(4 * W, C)
        plain = plain + column_sum(grad)
        crossed = crossed + column_sum(grad * unit(pixel_block(r.mid, i), norm_three))
        part = r.up[block, :].astype(full) + grad * (vec.gain_three * vec.scale_three)
        r.part_two[1 + i * 4 : 5 + i * 4] = part.reshape(4, W, C)
    gain_three, bias_three = crossed, plain
    r.tile[0] = sums_tile(plain * vec.gain_three, crossed * vec.gain_three)
    three_edges = band.edges(0, r.part_two.at[1], r.part_two.at[IMAGE_ROWS], r.part_two)
    tiles = band.send_tile(0, r.tile.at[0], r.window.at[0])

    for copy in (sibling.act3, sibling.qkv, loads.act_three):
        copy.wait()
    for n in range(3):
        own = mine_of(r.joined, C + core * (3 * C // 2) + n * (C // 2), C // 2)
        columns = slice(n * (C // 2), (n + 1) * (C // 2))
        grad = dot_first(r.act3[...], own)
        grad = grad + dot_first(r.sib_act3[...], r.sib_qkv[:, columns])
        r.grads[QKV][:, :, :, :, :, :, columns] = grad.astype(low).reshape(2, 2, 2, 2, 2, 16, C // 2)
    streams[QKV].start()

    for copy in (sibling.cap, sibling.far_cap, loads.caption, loads.far_caption):
        copy.wait()
    for copy in word_copies:
        copy.wait()

    def text_rows(s, carry):
        columns = pl.ds(pl.multiple_of(s * 128, 128), 128)
        grad = dot_first(r.caps[0, :, columns], r.own_word_part[...])
        for i in range(3):
            grad = grad + dot_first(r.caps[i + 1, :, columns], r.word_parts[i])
        grad = grad.astype(low)
        index = (s // 8, (s // 4) % 2, (s // 2) % 2, s % 2)
        r.grads[WORDS][index] = grad[0:64]
        r.grads[WORDS + 1][index] = grad[64:128]
        return carry

    lax.fori_loop(0, 2 ** len(CROSS) * 2, text_rows, 0)
    streams[WORDS].start()
    streams[WORDS + 1].start()
    value_sum = column_sum(r.joined[:, 3 * C :].astype(full))
    word_sum = [column_sum(r.joined_words[:, k * C : (k + 1) * C].astype(full)) for k in range(2)]

    def spread_rows(i, values):
        from_left, from_right = side_shifts(values)
        r.shifts[0, i] = from_right.astype(low)
        r.shifts[1, i] = values.astype(low)
        r.shifts[2, i] = from_left.astype(low)

    def conv_back():
        total = jnp.zeros((IMAGE_ROWS * W, C), full)
        for t in range(9):
            dy, dx = t // 3, t % 3
            view = r.shifts[dx, 2 - dy : 2 - dy + IMAGE_ROWS].reshape(IMAGE_ROWS * W, C)
            total = total + dot_last(view, r.conv_w[t * C : (t + 1) * C, :])
        return total

    def gather_shifts(landing, places):
        width = C // 4

        def one_row(i, carry):
            for k in places:
                if k == 0:
                    for dx in range(3):
                        lanes = slice(dx * width, (dx + 1) * width)
                        r.sides[0, i, :, lanes] = r.shifts[dx, i + 1, :, columns_of(quarter, width)]
                    continue
                values = landing[k - 1, i].astype(full)
                from_left, from_right = side_shifts(values)
                r.sides[k, i, :, 0:width] = from_right.astype(low)
                r.sides[k, i, :, width : 2 * width] = landing[k - 1, i]
                r.sides[k, i, :, 2 * width :] = from_left.astype(low)
            return carry

        lax.fori_loop(0, IMAGE_ROWS, one_row, 0)

    def conv_grads(kind, acts, landing, arrivals):
        width = C // 4

        def products(dy, places):
            grad = jnp.zeros((C, 3 * width), full)
            for k in places:
                sides = r.sides[k].reshape(IMAGE_ROWS * W, 3 * width)
                grad = grad + dot_first(acts[k, dy * W : dy * W + IMAGE_ROWS * W, :], sides)
            return grad

        arrivals[0].wait()
        gather_shifts(landing, (0, 1))
        for dy in range(3):
            r.partial[dy] = products(dy, (0, 1))
        for copy in arrivals[1:]:
            copy.wait()
        gather_shifts(landing, (2, 3))
        for dy in range(3):
            grad = r.partial[dy] + products(dy, (2, 3))
            grad = grad.astype(low)
            for dx in range(3):
                begin = first = (dy * 3 + dx) * C
                while begin < first + C:
                    shard, within = divmod(begin, 288)
                    stream, offset = divmod(within, 144)
                    size = min(144 - offset, first + C - begin)
                    target = r.grads[kind + stream]
                    target[
                        shard // 8,
                        (shard // 4) % 2,
                        (shard // 2) % 2,
                        shard % 2,
                        offset : offset + size,
                    ] = grad[begin - first : begin - first + size, dx * width : (dx + 1) * width]
                    begin += size
        for j in range(2):
            streams[kind + j].start()

    for copy in tiles:
        copy.wait()
    band.wait_edges(three_edges)
    means = item_means(r.window.at[0])
    offset_three, slope_three = means[0:1] * vec.scale_three, means[1:2] * vec.scale_three

    def middle_row(i, bias):
        values = r.part_two[i] - offset_three - unit(r.mid[i], norm_three) * slope_three
        r.part_two[i] = values
        values = kept(i, values, vec)
        spread_rows(i, values)
        inside = jnp.where((i > 0) & (i <= IMAGE_ROWS), 1.0, 0.0)
        return bias + inside * column_sum(values.astype(low).astype(full))

    conv_bias_two = lax.fori_loop(0, IMAGE_ROWS + 2, middle_row, jnp.zeros((1, C), full))
    def center(q):
        return r.shifts.at[1, 1 : IMAGE_ROWS + 1, :, columns_of(q, C // 4)]

    side_copies = to_quad(1, center, r.sides_two)
    advance(PROJ)
    loads.conv_second.wait()
    loads.hidden.wait()
    r.product[...] = conv_back().reshape(IMAGE_ROWS, W, C)
    loads.conv_first = load(8, r.conv_first, r.conv_w)
    stretched = vec.stretch * vec.gain_two * vec.scale_two

    def second_row(i, sums):
        unit_two = unit(r.hid[i + 1], norm_two)
        normed = unit_two * vec.gain_two + vec.bias_two
        grad = r.product[i] * silu_slope_of(normed * vec.stretch + vec.shift)
        r.part_one[i + 1] = grad * stretched
        return sums[0] + column_sum(grad), sums[1] + column_sum(grad * unit_two)

    nothing = (jnp.zeros((1, C), full), jnp.zeros((1, C), full))
    plain, crossed = lax.fori_loop(0, IMAGE_ROWS, second_row, nothing)
    scale_grad = crossed * vec.gain_two + plain * vec.bias_two
    shift_grad = plain
    gain_two, bias_two = crossed * vec.stretch, plain * vec.stretch
    r.tile[1] = sums_tile(bias_two * vec.gain_two, gain_two * vec.gain_two)
    two_edges = band.edges(1, r.part_one.at[1], r.part_one.at[IMAGE_ROWS], r.part_one)
    tiles = band.send_tile(1, r.tile.at[1], r.window.at[1])
    for copy in (loads.act_two, loads.far_act_two, sibling.act2, sibling.far_act2):
        copy.wait()
    advance(PROJ, QKV, WORDS, WORDS + 1)
    conv_grads(SECOND_CONV, r.acts_two, r.sides_two, side_copies)
    advance(PROJ)
    for copy in tiles:
        copy.wait()
    band.wait_edges(two_edges)
    means = item_means(r.window.at[1])
    offset_two, slope_two = means[0:1] * vec.scale_two, means[1:2] * vec.scale_two

    def hidden_row(i, bias):
        values = r.part_one[i] - offset_two - unit(r.hid[i], norm_two) * slope_two
        values = kept(i, values, vec)
        spread_rows(i, values)
        inside = jnp.where((i > 0) & (i <= IMAGE_ROWS), 1.0, 0.0)
        return bias + inside * column_sum(values.astype(low).astype(full))

    conv_bias_one = lax.fori_loop(0, IMAGE_ROWS + 2, hidden_row, jnp.zeros((1, C), full))
    side_copies = to_quad(2, center, r.sides_one)
    advance(PROJ, QKV, WORDS, WORDS + 1)
    loads.conv_first.wait()
    loads.image.wait()
    r.product[...] = conv_back().reshape(IMAGE_ROWS, W, C)

    def first_row(i, sums):
        unit_one = unit(r.img[i].astype(full), norm_one)
        normed = unit_one * vec.gain_one + vec.bias_one
        grad = r.product[i] * silu_slope_of(normed)
        r.product[i] = grad
        return sums[0] + column_sum(grad), sums[1] + column_sum(grad * unit_one)

    plain, crossed = lax.fori_loop(0, IMAGE_ROWS, first_row, nothing)
    gain_one, bias_one = crossed, plain
    r.tile[2] = sums_tile(plain * vec.gain_one, crossed * vec.gain_one)
    tiles = band.send_tile(2, r.tile.at[2], r.window.at[2])
    rows = [
        gain_one,
        gain_two,
        gain_three,
        bias_one,
        bias_two,
        bias_three,
        conv_bias_one,
        conv_bias_two,
        query_sum,
        value_sum,
        word_sum[0],
        word_sum[1],
        up_sum,
        jnp.zeros((1, C), full),
        scale_grad,
        shift_grad,
    ]
    for i, values in enumerate(rows):
        r.own_rows[i : i + 1, :] = values
    row_copies = band.send_tile(3, r.own_rows, r.band_rows)
    for copy in (loads.act_one, loads.far_act_one, sibling.act1, sibling.far_act1):
        copy.wait()
    conv_grads(FIRST_CONV, r.acts_one, r.sides_one, side_copies)
    advance(PROJ, QKV, WORDS, WORDS + 1, 2, 3)
    for copy in tiles:
        copy.wait()
    means = item_means(r.window.at[2])
    offset_one, slope_one = means[0:1] * vec.scale_one, means[1:2] * vec.scale_one
    ratio = vec.gain_one * vec.scale_one

    def image_row(i, carry):
        unit_one = unit(r.img[i].astype(full), norm_one)
        values = r.part_two[i + 1] + r.product[i] * ratio - offset_one - unit_one * slope_one
        r.image_grad[i] = values
        return carry

    lax.fori_loop(0, IMAGE_ROWS, image_row, 0)

    for copy in row_copies:
        copy.wait()
    total = jnp.zeros((16, C), full)
    for b in range(SPAN):
        total = total + r.band_rows[b]
    r.half_rows[0:16, :] = total
    for b in range(SPAN):
        r.half_rows[16 + 2 * b : 18 + 2 * b, :] = r.band_rows[b, 14:16, :]
    far_copy = remote(
        r.half_rows, r.far_rows, r.small_send.at[0], r.small_recv.at[0], partner[FAR]
    )
    far_copy.start()
    loads.text_weight.wait()

    def caption_columns(n, carry):
        columns = pl.ds(pl.multiple_of(n * C, C), C)
        r.caption_grad[:, columns] = dot_last(r.joined_words[...], r.text_w[columns, :])
        return carry

    lax.fori_loop(0, EMB // C, caption_columns, 0)
    loads.embed_weight = load(13, r.embed_weight, r.text_w)
    slots = r.slot_of_band.shape[0]
    held = types.SimpleNamespace()

    def half_sums_arrived():
        far_copy.wait()
        first_half = jnp.where(place[FAR] == 0, r.half_rows[16:32, :], r.far_rows[16:32, :])
        other_half = jnp.where(place[FAR] == 0, r.far_rows[16:32, :], r.half_rows[16:32, :])
        r.group_rows[0:16, :] = r.half_rows[0:16, :] + r.far_rows[0:16, :]
        r.group_rows[16:32, :] = first_half
        r.group_rows[32:48, :] = other_half
        for k in range(2):
            table = jnp.zeros((slots, C), full)
            for b in range(2 * SPAN):
                values = r.group_rows[16 + 2 * b + k : 17 + 2 * b + k, :]
                table = table + jnp.where(r.slot_of_band[:, b * 128 : b * 128 + 1] > 0.0, values, 0.0)
            r.own_table[slots * k : slots * (k + 1), :] = table
        r.own_table[2 * slots :, :] = r.group_rows[0:16, :]
        held.group_copy = remote(
            r.own_table,
            r.other_table,
            r.small_send.at[1],
            r.small_recv.at[1],
            partner[GROUP],
        )
        held.group_copy.start()
        loads.embed_weight.wait()
        held.table = table = [r.own_table[slots * k : slots * (k + 1), :].astype(low) for k in range(2)]

        def embedding_columns(n, carry):
            columns = pl.ds(pl.multiple_of(n * C, C), C)
            grad = dot_last(table[0], r.text_w[columns, 0:C]) + dot_last(table[1], r.text_w[columns, C:])
            source = r.embedding[:, columns].astype(full)
            r.embedding_grad[:, columns] = grad * silu_slope_of(source)
            return carry

        lax.fori_loop(0, EMB // C, embedding_columns, 0)

    def group_sums_arrived():
        held.group_copy.wait()
        share_copy.wait()
        table = held.table
        for k in range(2):
            columns = slice(k * C, (k + 1) * C)
            other = r.other_table[slots * k : slots * (k + 1), :].astype(low)
            r.embed_weight_grad[:, columns] = dot_first(r.silu_share[...], table[k]) + dot_first(
                r.other_share[...], other
            )
            r.embed_bias_grad[:, columns] = column_sum(table[k].astype(full)) + column_sum(
                other.astype(full)
            )
        sums = r.own_table[2 * slots :, :] + r.other_table[2 * slots :, :]
        r.norm_gains_grad[...] = sums[0:3]
        r.norm_biases_grad[...] = sums[3:6]
        r.conv_biases_grad[...] = sums[6:8]
        for target, k in ((r.qv_bias_grad, 8), (r.text_bias_grad, 10)):
            target[:, 0:C] = sums[k : k + 1]
            target[:, C:] = sums[k + 1 : k + 2]
        r.proj_bias_grad[...] = sums[12:13]

    for k in TAIL:
        if k == HALF_SUMS:
            half_sums_arrived()
        elif k == GROUP_SUMS:
            group_sums_arrived()
        else:
            advance(k)

    def write(stream, target, first_row):
        rows, columns = STREAMS[stream][:2]
        for k in range(4):
            target[first_row : first_row + rows, k * columns : (k + 1) * columns] = r.folded[stream][
                k
            ].astype(full)

    def write_halves(stream, target):
        rows, columns = STREAMS[stream][:2]
        for side, source in ((group, r.folded[stream]), (1 - group, r.whole[stream - QKV])):
            for k in range(2):
                target[
                    pl.ds(pl.multiple_of(side * rows, rows), rows), k * columns : (k + 1) * columns
                ] = source[k].astype(full)

    for j in range(2):
        write(FIRST_CONV + j, r.conv_first_grad, j * 144)
        write(SECOND_CONV + j, r.conv_second_grad, j * 144)
        write(WORDS + j, r.text_grad, j * 64)
    write_halves(QKV, r.qkv_grad)
    write_halves(PROJ, r.proj_grad)


def silu_slope_of(source):
    sigma = 1.0 / (1.0 + jnp.exp(-source))
    return sigma * (1.0 + source * (1.0 - sigma))


def back(ident, vectors, slot_of_band, silu_share, embedding, anywhere):
    low, full = jnp.bfloat16, jnp.float32
    pixels = IMAGE_ROWS * W
    slots = slot_of_band.shape[0]
    outs = dict(
        result=((pixels, C), low),
        image_grad=((IMAGE_ROWS, W, C), full),
        caption_grad=((TEXT, EMB), full),
        conv_first_grad=((288, C), full),
        conv_second_grad=((288, C), full),
        qkv_grad=((32, 3 * C), full),
        text_grad=((128, 2 * C), full),
        proj_grad=((32, C), full),
        embedding_grad=(embedding.shape, full),
        embed_weight_grad=((silu_share.shape[1], 2 * C), full),
        norm_gains_grad=((3, C), full),
        norm_biases_grad=((3, C), full),
        conv_biases_grad=((2, C), full),
        embed_bias_grad=((1, 2 * C), full),
        qv_bias_grad=((1, 2 * C), full),
        text_bias_grad=((1, 2 * C), full),
        proj_bias_grad=((1, C), full),
    )
    padded = (IMAGE_ROWS + 2, W, C)
    scratch = dict(
        heads=((HEADS, pixels, 2 * HEAD), low),
        head_pairs=((HEADS, pixels, 2 * HEAD), low),
        head_words=((HEADS, TEXT, 2 * HEAD), low),
        joined=((pixels, 4 * C), low),
        joined_words=((TEXT, 2 * C), low),
        mid=(padded, full),
        part_two=(padded, full),
        part_one=(padded, full),
        hid=(padded, full),
        product=((IMAGE_ROWS, W, C), full),
        img=((IMAGE_ROWS, W, C), low),
        up=((pixels, C), low),
        act3=((pixels, C), low),
        conv_w=((9 * C, C), low),
        qkv_w=((C, 3 * C), low),
        proj_w=((C, C), low),
        text_w=((EMB, 2 * C), low),
        sib_up=((pixels, C // 2), low),
        sib_act3=((pixels, C), low),
        sib_attended=((pixels, C), low),
        sib_qkv=((pixels, 3 * C // 2), low),
        acts_one=((4, pixels + 2 * W, C), low),
        acts_two=((4, pixels + 2 * W, C), low),
        caps=((4, TEXT, EMB), low),
        own_word_part=((TEXT, C // 2), low),
        word_parts=((3, TEXT, C // 2), low),
        sides_one=((3, IMAGE_ROWS, W, C // 4), low),
        sides_two=((3, IMAGE_ROWS, W, C // 4), low),
        sides=((4, IMAGE_ROWS, W, 3 * C // 4), low),
        partial=((3, C, 3 * C // 4), full),
        shifts=((3,) + padded, low),
        blocks=((C, C), low),
        tile=((3, 8, C // 4), full),
        window=((3, SPAN, 8, C // 4), full),
        own_rows=((16, C), full),
        band_rows=((SPAN, 16, C), full),
        half_rows=((32, C), full),
        far_rows=((32, C), full),
        group_rows=((48, C), full),
        own_table=((2 * slots + 16, C), full),
        other_table=((2 * slots + 16, C), full),
        other_share=(silu_share.shape, low),
    )
    def halved(stream, step):
        return ((2,) * (len(stream[2]) + 1 - step) + stream[:2], low)

    scratch.update(grads=[halved(s, 0) for s in STREAMS])
    scratch.update(landings=[halved(s, i + 1) for s in STREAMS for i in range(len(s[2]))])
    scratch.update(folded=[((2 if GROUP in s[2] else 4,) + s[:2], low) for s in STREAMS])
    scratch.update(whole=[((2,) + s[:2], low) for s in STREAMS[QKV:]])
    semaphores = dict(
        swap_send=(2, SPAN),
        swap_recv=(2, SPAN),
        load_sem=(18,),
        quad_send=(3, 3),
        quad_recv=(3, 3),
        sib_send=(10,),
        sib_recv=(10,),
        edge_send=(2, 2),
        edge_recv=(2, 2),
        tile_send=(4, SPAN),
        tile_recv=(4, SPAN),
        fold_send=(len(STREAMS), len(GROUP_FIRST) + 3),
        fold_recv=(len(STREAMS), len(GROUP_FIRST) + 3),
        small_send=(3,),
        small_recv=(3,),
    )
    inputs = dict(
        vectors=vectors, slot_of_band=slot_of_band, silu_share=silu_share, embedding=embedding
    )
    return call_named(back_kernel, ident, (), inputs, anywhere, outs, scratch, semaphores)


def attend_kernel(names, *refs):
    low, full = jnp.bfloat16, jnp.float32
    r = grouped(names, refs)
    band = Band(r)
    counterpart = band.partner[GROUP]
    band.meet((counterpart,))
    query_swaps = band.swap(0, r.own_queries, r.queries, range(SPAN - 1, 0, -1))
    r.queries[band.lane] = r.own_queries[band.lane]
    far_copies = [
        band.remote(source, target, r.far_send.at[k], r.far_recv.at[k], counterpart)
        for k, (source, target) in enumerate(
            (
                (r.caption, r.far_caption),
                (r.act_two, r.far_act_two),
                (r.act_one, r.far_act_one),
            )
        )
    ]
    for copy in far_copies:
        copy.start()
    bands, pixels = r.pairs.shape[:2]
    text = r.words.shape[1]
    scale = HEAD ** (-0.5)

    def with_units(values, rows):
        lanes = lax.broadcasted_iota(jnp.int32, (rows, 2 * HEAD), 1)
        units = jnp.where(lanes < 2, 1.0, 0.0).astype(low)
        return jnp.where(lanes < HEAD, units, values)

    def prepare(b, carry):
        r.across[b] = r.pairs[b].T
        r.valued[b] = with_units(r.pairs[b], pixels)
        r.words_across[b] = r.words[b].T
        r.words_valued[b] = with_units(r.words[b], text)
        r.pair_sums[b] = jnp.zeros((pixels, 2 * HEAD), full)
        return carry

    lax.fori_loop(0, bands, prepare, 0)

    def one_row(columns):
        rows = lax.broadcasted_iota(jnp.int32, (16, columns), 0)
        return jnp.where(rows == 0, 1.0, 0.0).astype(low)

    ones_pixels = one_row(pixels)
    ones_text = one_row(text)
    zeros = jnp.zeros((HEAD, pixels), low)

    def outcome_copy(i):
        return band.remote(
            r.own_outcome.at[i],
            r.outcome.at[band.lane],
            r.outcome_send.at[i],
            r.outcome_recv.at[band.lane],
            {ROWS: band.base + i},
        )

    def query_band(step, carry):
        i = (band.lane + 1 + step) % bands
        mine = r.items[band.base + i]
        start = 0
        allowed = []
        for b in range(bands):
            other = r.items[band.base + b]
            start = start + jnp.where(other < mine, 1, 0)
            allowed.append(other == mine)

        @pl.when(step < bands - 1)
        def _():
            band.remote(
                r.own_queries.at[i],
                r.queries.at[i],
                r.swap_send.at[0, SPAN - 1 - step],
                r.swap_recv.at[0, SPAN - 1 - step],
                {ROWS: band.base + i},
            ).wait_recv()

        query = (r.queries[i].astype(full) * scale).astype(low)
        query_rhs = jnp.concatenate([query, zeros], 0)

        top = jnp.full((8, pixels), -jnp.inf, full)
        for j in range(bands):
            scores = dot(r.pairs[j], query_rhs)
            r.scores[j] = scores
            highest = jnp.max(scores.reshape(pixels // 8, 8, pixels), axis=0)
            top = jnp.where(allowed[j], jnp.maximum(top, highest), top)
        scores = dot(r.words[start], query_rhs)
        top = jnp.maximum(top, jnp.max(scores.reshape(text // 8, 8, pixels), axis=0))
        top = jnp.max(top, axis=0, keepdims=True)
        weights_text = jnp.exp2((scores - top) * LOG2E).astype(low)
        values = jnp.concatenate([r.words_across[start, HEAD:, :], ones_text], 0)
        total = dot(values, weights_text)

        for j in range(bands):
            ceiling = top + jnp.where(allowed[j], 0.0, FAR_ABOVE)
            weights = jnp.exp2((r.scores[j] - ceiling) * LOG2E).astype(low)
            r.weights[j] = weights
            values = jnp.concatenate([r.across[j, HEAD:, :], ones_pixels], 0)
            total = total + dot(values, weights)
        inverse = 1.0 / total[HEAD : HEAD + 1, :]
        attended = total[0:HEAD, :] * inverse
        grad = r.upstream[i].astype(full)
        minus_dots = -jnp.sum(grad * attended, axis=0, keepdims=True) * inverse
        grad_scaled = (grad * inverse).astype(low)
        coarse = minus_dots.astype(low)
        fine = minus_dots - coarse.astype(full)
        rows = lax.broadcasted_iota(jnp.int32, (HEAD, pixels), 0)
        extra = jnp.where(rows == 0, coarse.astype(full), jnp.where(rows == 1, fine, 0.0))
        grad_rhs = jnp.concatenate([extra.astype(low), grad_scaled], 0)
        grad_rows = jnp.concatenate([zeros, grad_scaled], 0).T
        query_rows = jnp.concatenate([query, zeros], 0).T

        steps = (weights_text.astype(full) * dot(r.words_valued[start], grad_rhs)).astype(low)
        word_sum = dot(weights_text, grad_rows) + dot(steps, query_rows)
        r.word_parts[i] = word_sum
        query_grad = dot(r.words_across[start, 0:HEAD, :], steps)
        for j in range(bands):
            for begin in range(0, pixels, pixels // 2):
                keys = slice(begin, begin + pixels // 2)
                weights = r.weights[j, keys]
                steps = (weights.astype(full) * dot(r.valued[j, keys], grad_rhs)).astype(low)
                r.pair_sums[j, keys] += dot(weights, grad_rows) + dot(steps, query_rows)
                query_grad = query_grad + dot(r.across[j, 0:HEAD, keys], steps)
        r.own_outcome[i] = jnp.concatenate(
            [attended.astype(low), (query_grad * scale).astype(low)], 0
        ).T
        pl.when(step < bands - 1)(outcome_copy(i).start)
        return carry

    lax.fori_loop(0, bands, query_band, 0)
    r.outcome[band.lane] = r.own_outcome[band.lane]

    def finish(b, carry):
        r.pair_grads[b] = r.pair_sums[b].astype(low)
        word_sum = jnp.zeros((text, 2 * HEAD), full)
        for i in range(bands):
            mine = r.items[band.base + i]
            start = 0
            for c in range(bands):
                start = start + jnp.where(r.items[band.base + c] < mine, 1, 0)
            word_sum = word_sum + jnp.where(start == b, r.word_parts[i], 0.0)
        r.word_grads[b] = word_sum.astype(low)
        return carry

    lax.fori_loop(0, bands, finish, 0)

    def wait_outcome(step, carry):
        i = (band.lane + 1 + step) % bands
        outcome_copy(i).wait_send()
        band.remote(
            r.own_outcome.at[i],
            r.outcome.at[i],
            r.outcome_send.at[i],
            r.outcome_recv.at[i],
            {ROWS: band.base + i},
        ).wait_recv()
        return carry

    lax.fori_loop(0, bands - 1, wait_outcome, 0)
    for copy in query_swaps:
        copy.wait_send()
    for copy in far_copies:
        copy.wait()


def attend(ident, items, ahead, caption):
    low, full = jnp.bfloat16, jnp.float32
    bands, pixels, _ = ahead.pairs.shape
    text = ahead.words.shape[1]
    outs = dict(
        outcome=((bands, pixels, 2 * HEAD), low),
        pair_grads=((bands, pixels, 2 * HEAD), low),
        word_grads=((bands, text, 2 * HEAD), low),
    )
    anywhere = dict(caption=caption, act_one=ahead.act_one, act_two=ahead.act_two)
    far = dict(
        far_caption=(caption.shape, low),
        far_act_one=(ahead.act_one.shape, low),
        far_act_two=(ahead.act_two.shape, low),
    )
    scratch = dict(
        queries=(ahead.own_queries.shape, low),
        across=((bands, 2 * HEAD, pixels), low),
        valued=((bands, pixels, 2 * HEAD), low),
        words_across=((bands, 2 * HEAD, text), low),
        words_valued=((bands, text, 2 * HEAD), low),
        scores=((bands, pixels, pixels), full),
        weights=((bands, pixels, pixels), low),
        pair_sums=((bands, pixels, 2 * HEAD), full),
        word_parts=((bands, text, 2 * HEAD), full),
        own_outcome=((bands, pixels, 2 * HEAD), low),
    )
    semaphores = dict(
        outcome_send=(bands,), outcome_recv=(bands,), far_send=(3,), far_recv=(3,),
        swap_send=(1, SPAN), swap_recv=(1, SPAN),
    )
    inputs = dict(
        pairs=ahead.pairs,
        own_queries=ahead.own_queries,
        upstream=ahead.upstream,
        words=ahead.words,
    )
    return call_named(
        attend_kernel, ident, dict(items=items), inputs, anywhere, outs, scratch, semaphores, far
    )


def front_kernel(names, *refs):
    low, full = jnp.bfloat16, jnp.float32
    r = grouped(names, refs)
    band = Band(r)
    band.meet()
    loads = types.SimpleNamespace()

    def load(k, source, target):
        copy = pltpu.make_async_copy(source, target, r.load_sem.at[k])
        copy.start()
        return copy

    loads.image = load(0, r.image, r.img.at[1 : IMAGE_ROWS + 1])
    image_edges = band.edges(0, r.image.at[0], r.image.at[IMAGE_ROWS - 1], r.img)
    loads.upstream = load(3, r.upstream_pixels, r.up)
    loads.proj_weight = load(4, r.proj_weight, r.proj_w)
    loads.conv_first = load(1, r.conv_first, r.first_w)
    loads.embed_weight = load(2, r.embed_weight, r.embed_w)
    loads.conv_second = load(5, r.conv_second, r.second_w)
    loads.caption = load(6, r.caption, r.cap)
    loads.text_weight = load(7, r.text_weight, r.text_w)
    loads.qkv_weight = load(8, r.qkv_weight, r.qkv_w)

    mine = r.items[band.row]
    same = [(r.items[band.base + b] == mine).astype(full) for b in range(SPAN)]
    masks = [jnp.full((1, C), m, full) for m in same]
    bands = masks[0]
    for m in masks[1:]:
        bands = bands + m
    per_item = 1.0 / (bands * (IMAGE_ROWS * W * (C // NORM_GROUPS)))
    before = jnp.where(band.has_above, r.items[jnp.maximum(band.row - 1, 0)], -1)
    after = jnp.where(
        band.has_below, r.items[jnp.minimum(band.row + 1, r.items.shape[0] - 1)], -1
    )
    found = types.SimpleNamespace(
        gain_one=r.norm_gains[0:1, :],
        gain_two=r.norm_gains[1:2, :],
        gain_three=r.norm_gains[2:3, :],
        bias_one=r.norm_biases[0:1, :],
        bias_two=r.norm_biases[1:2, :],
        bias_three=r.norm_biases[2:3, :],
        proj_bias=r.proj_bias[...],
        keep_above=jnp.full((1, C), (before == mine).astype(full)),
        keep_below=jnp.full((1, C), (after == mine).astype(full)),
        per_item=per_item,
    )
    for target in (r.img, r.hidden, r.middle):
        band.zero_edges(target)
    nothing = (jnp.zeros((1, C), full), jnp.zeros((1, C), full))

    def norm_of(k):
        means = band.item_means(r.window.at[k], masks, per_item)
        return means[0:1], lax.rsqrt(means[1:2] - means[0:1] * means[0:1] + epsilon)

    loads.image.wait()

    def image_sums(i, sums):
        values = r.img[i + 1].astype(full)
        return sums[0] + column_sum(values), sums[1] + column_sum(values * values)

    r.tile[0] = sums_tile(*lax.fori_loop(0, IMAGE_ROWS, image_sums, nothing))
    tiles = band.send_tile(0, r.tile.at[0], r.window.at[0])

    loads.upstream.wait()
    loads.proj_weight.wait()
    attended_grad = dot_last(r.proj_w[...], r.up[...]).astype(low)
    for h in range(HEADS):
        r.own_upstream[h] = attended_grad[h * HEAD : (h + 1) * HEAD, :]
    swaps = band.swap(0, r.own_upstream, r.upstream)
    r.upstream[band.lane] = r.own_upstream[band.lane]
    band.fill_blocks()
    slot = lax.broadcasted_iota(jnp.int32, r.embedding.shape, 0)
    chosen = jnp.where(slot == mine, r.embedding[...].astype(full), 0.0)
    chosen = jnp.sum(chosen, axis=0, keepdims=True)
    chosen = chosen / (1.0 + jnp.exp(-chosen))
    chosen = jnp.broadcast_to(chosen, (16, EMB)).astype(low)
    loads.embed_weight.wait()
    modulation = dot(chosen, r.embed_w[...])[0:1] + r.embed_bias[...]
    found.stretch = 1.0 + modulation[:, 0:C]
    found.shift = modulation[:, C:]

    def spread_rows(i, values, target):
        values = kept(i, values, found)
        from_left, from_right = side_shifts(values)
        r.shifts[0, i] = from_left.astype(low)
        r.shifts[1, i] = values.astype(low)
        r.shifts[2, i] = from_right.astype(low)
        target[pl.ds(pl.multiple_of(i * W, W), W), :] = values.astype(low)

    def conv(weight):
        total = jnp.zeros((IMAGE_ROWS * W, C), full)
        for t in range(9):
            view = r.shifts[t % 3, t // 3 : t // 3 + IMAGE_ROWS].reshape(IMAGE_ROWS * W, C)
            total = total + dot(view, weight[t * C : (t + 1) * C, :])
        return total

    for copy in tiles:
        copy.wait()
    band.wait_edges(image_edges)
    found.mean_one, found.scale_one = norm_of(0)

    def first_row(i, carry):
        unit = (r.img[i].astype(full) - found.mean_one) * found.scale_one
        normed = unit * found.gain_one + found.bias_one
        spread_rows(i, normed / (1.0 + jnp.exp(-normed)), r.act_one)
        return carry

    lax.fori_loop(0, IMAGE_ROWS + 2, first_row, 0)
    loads.conv_first.wait()
    total = conv(r.first_w) + r.conv_biases[0:1, :]
    r.hidden[1 : IMAGE_ROWS + 1] = total.reshape(IMAGE_ROWS, W, C)
    hidden_edges = band.edges(1, r.hidden.at[1], r.hidden.at[IMAGE_ROWS], r.hidden)
    r.tile[1] = sums_tile(column_sum(total), column_sum(total * total))
    tiles = band.send_tile(1, r.tile.at[1], r.window.at[1])

    loads.caption.wait()
    loads.text_weight.wait()
    words = (dot(r.cap[...], r.text_w[...]) + r.text_bias[...]).astype(low)
    for h in range(HEADS):
        parts = [words[:, k * C + h * HEAD : k * C + (h + 1) * HEAD] for k in range(2)]
        r.own_words[h] = jnp.concatenate(parts, axis=1)
    swaps = swaps + band.swap(1, r.own_words, r.words)
    r.words[band.lane] = r.own_words[band.lane]
    for copy in tiles:
        copy.wait()
    band.wait_edges(hidden_edges)
    found.mean_two, found.scale_two = norm_of(1)

    def second_row(i, carry):
        unit = (r.hidden[i] - found.mean_two) * found.scale_two
        normed = unit * found.gain_two + found.bias_two
        shifted = normed * found.stretch + found.shift
        spread_rows(i, shifted / (1.0 + jnp.exp(-shifted)), r.act_two)
        return carry

    lax.fori_loop(0, IMAGE_ROWS + 2, second_row, 0)
    loads.conv_second.wait()
    total = conv(r.second_w) + r.conv_biases[1:2, :]
    total = total + r.img[1 : IMAGE_ROWS + 1].astype(full).reshape(IMAGE_ROWS * W, C)
    r.middle[1 : IMAGE_ROWS + 1] = total.reshape(IMAGE_ROWS, W, C)
    r.tile[2] = sums_tile(column_sum(total), column_sum(total * total))
    tiles = band.send_tile(2, r.tile.at[2], r.window.at[2])
    middle_edges = band.edges(2, r.middle.at[1], r.middle.at[IMAGE_ROWS], r.middle)

    loads.qkv_weight.wait()
    for copy in tiles:
        copy.wait()
    found.mean_three, found.scale_three = norm_of(2)
    for i in range(2):
        middle = r.middle[1 + 4 * i : 5 + 4 * i].reshape(4 * W, C)
        unit = (middle - found.mean_three) * found.scale_three
        block = slice(i * 4 * W, (i + 1) * 4 * W)
        act = (unit * found.gain_three + found.bias_three).astype(low)
        r.act_three[block, :] = act
        projected = dot(act, r.qkv_w[...])
        queries = (projected[:, 0:C] + r.qv_bias[:, 0:C]).astype(low)
        keys = projected[:, C : 2 * C].astype(low)
        values = (projected[:, 2 * C :] + r.qv_bias[:, C:]).astype(low)
        queries = queries.T
        for h in range(HEADS):
            head = slice(h * HEAD, (h + 1) * HEAD)
            r.own_queries[h, :, block] = queries[head, :]
            r.own_pairs[h, block, :] = jnp.concatenate([keys[:, head], values[:, head]], axis=1)
    swaps = swaps + band.swap(2, r.own_pairs, r.pairs)
    r.pairs[band.lane] = r.own_pairs[band.lane]
    fields = [getattr(found, name) for name in Vectors._fields]
    for i, values in enumerate(fields):
        r.vectors[i : i + 1, :] = values
    r.vectors[len(fields) : VECTOR_ROWS, :] = jnp.zeros((VECTOR_ROWS - len(fields), C), full)
    for b in range(SPAN):
        r.vectors[VECTOR_ROWS + b : VECTOR_ROWS + b + 1, :] = masks[b]
    band.wait_edges(middle_edges)
    for copy in swaps:
        copy.wait()


def front(ident, items, inputs, anywhere):
    low, full = jnp.bfloat16, jnp.float32
    pixels = IMAGE_ROWS * W
    padded = (IMAGE_ROWS + 2, W, C)
    outs = dict(
        pairs=((HEADS, pixels, 2 * HEAD), low),
        own_queries=((HEADS, HEAD, pixels), low),
        upstream=((HEADS, HEAD, pixels), low),
        words=((HEADS, TEXT, 2 * HEAD), low),
        act_one=((pixels + 2 * W, C), low),
        act_two=((pixels + 2 * W, C), low),
        act_three=((pixels, C), low),
        hidden=(padded, full),
        middle=(padded, full),
        vectors=((VECTOR_ROWS + SPAN, C), full),
    )
    scratch = dict(
        img=(padded, low),
        up=((pixels, C), low),
        cap=((TEXT, EMB), low),
        first_w=((9 * C, C), low),
        second_w=((9 * C, C), low),
        embed_w=((EMB, 2 * C), low),
        text_w=((EMB, 2 * C), low),
        qkv_w=((C, 3 * C), low),
        proj_w=((C, C), low),
        shifts=((3,) + padded, low),
        blocks=((C, C), low),
        tile=((3, 8, C // 4), full),
        window=((3, SPAN, 8, C // 4), full),
        own_pairs=((HEADS, pixels, 2 * HEAD), low),
        own_upstream=((HEADS, HEAD, pixels), low),
        own_words=((HEADS, TEXT, 2 * HEAD), low),
    )
    semaphores = dict(
        load_sem=(9,),
        edge_send=(3, 2),
        edge_recv=(3, 2),
        tile_send=(3, SPAN),
        tile_recv=(3, SPAN),
        swap_send=(3, SPAN),
        swap_recv=(3, SPAN),
    )
    return call_named(
        front_kernel, ident, dict(items=items), inputs, anywhere, outs, scratch, semaphores
    )


def hand_over_kernel(count, *refs):
    sources, targets, held = refs[:count], refs[count : 2 * count], refs[2 * count : 3 * count]
    load_sem, store_sem = refs[3 * count :]
    loads = [
        pltpu.make_async_copy(source, buffer, load_sem.at[k])
        for k, (source, buffer) in enumerate(zip(sources, held))
    ]
    stores = [
        pltpu.make_async_copy(buffer, target, store_sem.at[k])
        for k, (buffer, target) in enumerate(zip(held, targets))
    ]
    for copy in loads:
        copy.start()
    for load, store in zip(loads, stores):
        load.wait()
        store.start()
    for copy in stores:
        copy.wait()


def hand_over(arrays):
    anywhere = pl.BlockSpec(memory_space=pl.ANY)
    count = len(arrays)
    return pl.pallas_call(
        functools.partial(hand_over_kernel, count),
        out_shape=tuple(jax.ShapeDtypeStruct(a.shape, a.dtype) for a in arrays),
        in_specs=[anywhere] * count,
        out_specs=(anywhere,) * count,
        scratch_shapes=[pltpu.VMEM(a.shape, a.dtype) for a in arrays]
        + [pltpu.SemaphoreType.DMA((count,))] * 2,
        name=hand_over.__name__,
    )(*arrays)


def blocks_of(rows):
    return rows.reshape(rows.shape[0], NORM_GROUPS, -1)


def spread(values):
    return jnp.repeat(values, C // NORM_GROUPS)


def in_halves(
    image,
    embedding,
    caption,
    item_of_band,
    out_grad,
    norm_gains,
    norm_biases,
    conv_first,
    conv_second,
    conv_biases,
    embed_weight,
    embed_bias,
    qkv_weight,
    qv_bias,
    text_weight,
    text_bias,
    proj_weight,
    proj_bias,
):
    low = jnp.bfloat16
    pixels = image.shape[1]
    position = lax.axis_index(ROWS)
    items = item_of_band[0]
    slots = items.shape[0]
    by_row = (-1, W, C)
    ahead = front(
        0,
        items,
        dict(
            embedding=embedding[0],
            norm_gains=norm_gains,
            norm_biases=norm_biases,
            conv_biases=conv_biases,
            embed_bias=embed_bias[None],
            qv_bias=qv_bias[None],
            text_bias=text_bias[None],
            proj_bias=proj_bias[None],
        ),
        dict(
            image=image.reshape(by_row),
            conv_first=conv_first,
            embed_weight=embed_weight,
            upstream_pixels=out_grad[0],
            proj_weight=proj_weight,
            conv_second=conv_second,
            caption=caption[0, 0],
            text_weight=text_weight,
            qkv_weight=qkv_weight,
        ),
    )
    found = attend(2, items, ahead, caption[0, 0])
    slot_of_band = (jnp.arange(slots)[:, None] == items[None, :]).astype(jnp.float32)
    row_share = EMB // lax.axis_size(ROWS)
    share = lax.dynamic_slice_in_dim(embedding[0], position * row_share, row_share, 1)
    silu_share = jax.nn.silu(share.astype(jnp.float32)).astype(low)
    out = back(
        1,
        ahead.vectors,
        jnp.repeat(slot_of_band, 128, axis=1),
        silu_share,
        embedding[0],
        dict(
            outcome=found.outcome,
            pair_grads=found.pair_grads,
            word_grads=found.word_grads,
            middle=ahead.middle,
            qkv_weight=qkv_weight,
            proj_weight=proj_weight,
            upstream=out_grad[0],
            act_three=ahead.act_three,
            caption=caption[0, 0],
            conv_second=conv_second,
            conv_first=conv_first,
            hidden=ahead.hidden,
            act_two=ahead.act_two,
            act_one=ahead.act_one,
            far_caption=found.far_caption,
            far_act_one=found.far_act_one,
            far_act_two=found.far_act_two,
            image=image.reshape(by_row),
            text_weight=text_weight,
            embed_weight=embed_weight,
        ),
    )
    out = types.SimpleNamespace(**dict(zip(vars(out), hand_over(list(vars(out).values())))))
    return (
        out.result[None],
        out.image_grad.reshape(1, pixels, C),
        out.embedding_grad[None],
        out.caption_grad[None, None],
        out.norm_gains_grad,
        out.norm_biases_grad,
        out.conv_first_grad,
        out.conv_second_grad,
        out.conv_biases_grad,
        out.embed_weight_grad,
        out.embed_bias_grad.reshape(-1),
        out.qkv_grad,
        out.qv_bias_grad.reshape(-1),
        out.text_grad,
        out.text_bias_grad.reshape(-1),
        out.proj_grad,
        out.proj_bias_grad.reshape(-1),
    )


def shards(
    image,
    embedding,
    caption,
    item_of_band,
    out_grad,
    norm_gains,
    norm_biases,
    conv_first,
    conv_second,
    conv_biases,
    embed_weight,
    embed_bias,
    qkv_weight,
    qv_bias,
    text_weight,
    text_bias,
    proj_weight,
    proj_bias,
):
    low = jnp.bfloat16
    full = jnp.float32
    pixels = image.shape[1]
    band_items = item_of_band[0]
    slots = band_items.shape[0]
    if slots == 2 * SPAN and lax.axis_size(ITEMS) == 2 and HEADS == SPAN:
        return in_halves(
            image,
            embedding,
            caption,
            item_of_band,
            out_grad,
            norm_gains,
            norm_biases,
            conv_first,
            conv_second,
            conv_biases,
            embed_weight,
            embed_bias,
            qkv_weight,
            qv_bias,
            text_weight,
            text_bias,
            proj_weight,
            proj_bias,
        )
    position = lax.axis_index(ROWS)
    my_item = band_items[position]
    slot_hot = (jnp.arange(slots) == my_item).astype(full)
    item_count = jnp.sum((band_items == my_item).astype(full)) * pixels * (C // NORM_GROUPS)
    reach = position + jnp.arange(-REACH, REACH + 1)
    near = (reach >= 0) & (reach < slots)
    near = near & (band_items[jnp.clip(reach, 0, slots - 1)] == my_item)
    keep = jnp.concatenate(
        [
            jnp.full((W, 1), near[REACH - 1]),
            jnp.full((pixels, 1), True),
            jnp.full((W, 1), near[REACH + 1]),
        ]
    )
    own_lead = jnp.logical_not(near[REACH - 1])

    def totals(ident, first, second, edges=None):
        sums = jnp.stack([jnp.sum(blocks_of(first), axis=(0, 2)), jnp.sum(blocks_of(second), axis=(0, 2))])
        tile = jnp.pad(sums, ((0, 6), (0, 128 - NORM_GROUPS)))
        if edges is not None:
            outcome = exchange(ident, slots, tile, (edges[:W], edges[-W:]))
        else:
            outcome = exchange(ident, slots, tile)
        summed = jnp.sum(jnp.where(near[:, None, None], outcome[0], 0.0), axis=0)
        summed = summed[:2, :NORM_GROUPS] / item_count
        return summed, outcome[1:]

    def stats(summed):
        scales = lax.rsqrt(summed[1] - summed[0] * summed[0] + epsilon)
        return spread(summed[0]), spread(scales)

    inputs = image[0].astype(full)
    summed, (above, below) = totals(0, inputs, inputs * inputs, image[0])
    means_one, scales_one = stats(summed)
    padded = jnp.concatenate([above, image[0], below]).astype(full)
    unit_padded = (padded - means_one) * scales_one
    normed_padded = unit_padded * norm_gains[0] + norm_biases[0]
    act_one_padded = jnp.where(keep, jax.nn.silu(normed_padded), 0.0).astype(low)
    unit_one = unit_padded[W:-W]
    normed_one = normed_padded[W:-W]
    taps_one = jnp.concatenate(taps_of(act_one_padded, False), axis=1)
    hidden_one = dot(taps_one, conv_first) + conv_biases[0]
    embed_silu = jax.nn.silu(embedding[0].astype(full)).astype(low)
    my_silu = dot(slot_hot.astype(low)[None], embed_silu).astype(low)
    modulation = dot(my_silu, embed_weight)[0] + embed_bias
    scale_part = modulation[:C]
    shift_part = modulation[C:]
    summed, (above, below) = totals(1, hidden_one, hidden_one * hidden_one, hidden_one)
    means_two, scales_two = stats(summed)
    hidden_padded = jnp.concatenate([above, hidden_one, below])
    unit_padded = (hidden_padded - means_two) * scales_two
    normed_padded = unit_padded * norm_gains[1] + norm_biases[1]
    shifted_padded = normed_padded * (1.0 + scale_part) + shift_part
    act_two_padded = jnp.where(keep, jax.nn.silu(shifted_padded), 0.0).astype(low)
    unit_two = unit_padded[W:-W]
    normed_two = normed_padded[W:-W]
    shifted = shifted_padded[W:-W]
    taps_two = jnp.concatenate(taps_of(act_two_padded, False), axis=1)
    middle = inputs + dot(taps_two, conv_second) + conv_biases[1]
    summed, _ = totals(2, middle, middle * middle)
    means_three, scales_three = stats(summed)
    unit_three = (middle - means_three) * scales_three
    act_three = (unit_three * norm_gains[2] + norm_biases[2]).astype(low)
    projected = dot(act_three, qkv_weight)
    queries = (projected[:, :C] + qv_bias[:C]).astype(low)
    keys_values = jnp.concatenate(
        [projected[:, C : 2 * C], projected[:, 2 * C :] + qv_bias[C:]], axis=1
    ).astype(low)
    captions = caption[0, 0]
    text_kv = lax.cond(
        own_lead,
        lambda: (dot(captions, text_weight) + text_bias).astype(low),
        lambda: jnp.zeros((TEXT, 2 * C), low),
    )
    upstream = out_grad[0]
    upstream_float = upstream.astype(full)
    attended_grad = dot_last(upstream, proj_weight).astype(low)
    group = lax.axis_index(ITEMS)
    groups = lax.axis_size(ITEMS)
    attended_low, query_low, key_value_low, text_low = attention_by_band(
        band_items, position, queries, keys_values, text_kv, attended_grad
    )
    result = middle + dot(attended_low, proj_weight) + proj_bias
    proj_weight_grad = dot_first(attended_low, upstream)
    proj_bias_grad = jnp.sum(upstream_float, axis=0)
    qkv_grad = jnp.concatenate([query_low, key_value_low], axis=1)
    qkv_weight_grad = dot_first(act_three, qkv_grad)
    qv_bias_grad = jnp.sum(
        jnp.concatenate([query_low, key_value_low[:, C:]], axis=1).astype(full), axis=0
    )
    text_weight_grad = dot_first(captions, text_low)
    text_bias_grad = jnp.sum(text_low.astype(full), axis=0)
    caption_grad = dot_last(text_low, text_weight)[None, None]
    three_grad = dot_last(qkv_grad, qkv_weight)
    gain_three = jnp.sum(three_grad * unit_three, axis=0)
    bias_three = jnp.sum(three_grad, axis=0)

    def conv_back(padded, weight):
        views = jnp.stack(taps_of(padded, True))
        return jnp.einsum(
            "tpd,tcd->pc", views, weight.reshape(9, C, C), preferred_element_type=full
        )

    def norm_back(ident, grad_unit, unit_value, scales, base, with_edges=True):
        scaled = base + grad_unit * scales
        edges = jnp.concatenate([scaled, unit_value], axis=1) if with_edges else None
        summed, around = totals(ident, grad_unit, grad_unit * unit_value, edges)
        mean_grad, mean_cross = spread(summed[0]) * scales, spread(summed[1]) * scales
        if not with_edges:
            return scaled - mean_grad - unit_value * mean_cross
        both = jnp.concatenate([around[0], edges, around[1]])
        return both[:, :C] - mean_grad - both[:, C:] * mean_cross

    middle_padded = norm_back(3, three_grad * norm_gains[2], unit_three, scales_three, upstream_float)
    middle_grad = middle_padded[W:-W]
    low_padded = jnp.where(keep, middle_padded, 0.0).astype(low)
    hidden_two_low = low_padded[W:-W]
    conv_bias_two = jnp.sum(hidden_two_low.astype(full), axis=0)
    conv_second_grad = dot_first(taps_two, hidden_two_low)
    act_two_grad = conv_back(low_padded, conv_second)
    shifted_grad = act_two_grad * silu_slope(shifted)
    modulation_grad = jnp.concatenate(
        [jnp.sum(shifted_grad * normed_two, axis=0), jnp.sum(shifted_grad, axis=0)]
    )
    normed_two_grad = shifted_grad * (1.0 + scale_part)
    gain_two = jnp.sum(normed_two_grad * unit_two, axis=0)
    bias_two = jnp.sum(normed_two_grad, axis=0)
    hidden_back = norm_back(4, normed_two_grad * norm_gains[1], unit_two, scales_two, 0.0)
    low_padded = jnp.where(keep, hidden_back, 0.0).astype(low)
    hidden_one_low = low_padded[W:-W]
    conv_bias_one = jnp.sum(hidden_one_low.astype(full), axis=0)
    conv_first_grad = dot_first(taps_one, hidden_one_low)
    act_one_grad = conv_back(low_padded, conv_first)
    normed_one_grad = act_one_grad * silu_slope(normed_one)
    gain_one = jnp.sum(normed_one_grad * unit_one, axis=0)
    bias_one = jnp.sum(normed_one_grad, axis=0)
    image_grad = norm_back(
        5, normed_one_grad * norm_gains[0], unit_one, scales_one, middle_grad, False
    )
    group_hot = (jnp.arange(groups) == group).astype(full)
    tables = group_hot[:, None, None] * slot_hot[None, :, None] * modulation_grad
    vectors = jnp.concatenate(
        [
            gain_one,
            gain_two,
            gain_three,
            bias_one,
            bias_two,
            bias_three,
            conv_bias_one,
            conv_bias_two,
            qv_bias_grad,
            text_bias_grad,
            proj_bias_grad,
        ]
    )
    small = jnp.concatenate([tables.reshape(-1, C), vectors.reshape(-1, C)])
    row_share = EMB // lax.axis_size(ROWS)
    silu_share = lax.dynamic_slice_in_dim(embed_silu, position * row_share, row_share, 1)
    grads = (conv_first_grad, conv_second_grad, qkv_weight_grad, text_weight_grad, proj_weight_grad)
    grads = [g.astype(low) for g in grads]
    small = lax.psum(small.astype(low), (ROWS, ITEMS)).astype(full)
    tables_sum = small[: groups * slots * 2].reshape(groups, slots, 2 * C).astype(low)
    part = dot_first(silu_share, jnp.take(tables_sum, group, axis=0)).astype(low)
    matrices = [lax.psum_scatter(g, ROWS, scatter_dimension=0, tiled=True) for g in grads]
    *matrices, embed_weight_grad = [
        lax.psum(m, ITEMS).astype(full) for m in matrices + [part]
    ]
    vectors_sum = small[groups * slots * 2 :]
    modulation_low = jnp.take(tables_sum, group, axis=0)
    embed_bias_grad = jnp.sum(tables_sum.astype(full), axis=(0, 1))
    embedding_grad = dot_last(modulation_low, embed_weight) * silu_slope(embedding[0].astype(full))
    return (
        result.astype(low)[None],
        image_grad[None],
        embedding_grad[None],
        caption_grad,
        vectors_sum[0:3],
        vectors_sum[3:6],
        matrices[0],
        matrices[1],
        vectors_sum[6:8],
        embed_weight_grad,
        embed_bias_grad,
        matrices[2],
        vectors_sum[8:10].reshape(-1),
        matrices[3],
        vectors_sum[10:12].reshape(-1),
        matrices[4],
        vectors_sum[12],
    )


def solution(mesh):
    in_specs = (
        P(ITEMS, ROWS, None),
        P(ITEMS, None, None),
        P(ITEMS, ROWS, None, None),
        P(ITEMS, None),
        P(ITEMS, ROWS, None),
        P(),
        P(),
        P(),
        P(),
        P(),
        P(),
        P(),
        P(),
        P(),
        P(),
        P(),
        P(),
        P(),
    )
    out_specs = (
        P(ITEMS, ROWS, None),
        P(ITEMS, ROWS, None),
        P(ITEMS, None, None),
        P(ITEMS, ROWS, None, None),
        P(),
        P(),
        P(ROWS, None),
        P(ROWS, None),
        P(),
        P(ROWS, None),
        P(),
        P(ROWS, None),
        P(),
        P(ROWS, None),
        P(),
        P(ROWS, None),
        P(),
    )
    return jax.shard_map(shards, mesh=mesh, in_specs=in_specs, out_specs=out_specs, check_vma=False)
```

```python
import functools
import types
import typing

import jax
import jax.numpy as jnp
from jax import lax
from jax.experimental import pallas as pl
from jax.experimental.pallas import tpu as pltpu
from jax.sharding import PartitionSpec as P

C = 512
HEADS = 8
HEAD = 64
EMB = 2048
TEXT = 128
NORM_GROUPS = 32
W = 64
SPAN = 8
ROWS, ITEMS = "rows", "items"


epsilon = 1e-05


def from_behind(array, axis, by):
    length = lax.axis_size(axis)
    pairs = [(i, i + by) for i in range(length) if 0 <= i + by < length]
    return lax.ppermute(array, axis, pairs)


def as_sent(array):
    return jax.tree.map(lambda a: a.astype(jnp.bfloat16) if a.dtype == jnp.float32 else a, array)


def keep_state(state):
    return state


def silu_slope(source):
    sigma = jax.nn.sigmoid(source)
    return sigma * (1.0 + source * (1.0 - sigma))


def dot_first(left_side, right_side):
    return lax.dot_general(
        left_side, right_side, (((0,), (0,)), ((), ())), preferred_element_type=jnp.float32
    )


def dot_last(left_side, right_side):
    return lax.dot_general(
        left_side, right_side, (((1,), (1,)), ((), ())), preferred_element_type=jnp.float32
    )


def head_split(source):
    return source.reshape(source.shape[0], HEADS, HEAD)


def piece_scores(query_heads, key_piece, allowed):
    key_heads = head_split(key_piece[:, :C])
    scores = jnp.einsum(
        "qhd,khd->hqk", query_heads, key_heads, preferred_element_type=jnp.float32
    ) * HEAD ** (-0.5)
    return jnp.where(allowed[None, None, :], scores, -jnp.inf)


def piece_grads(query_heads, grad_heads, log_total, row_dots, key_piece, allowed):
    scores = piece_scores(query_heads, key_piece, allowed)
    weights = jnp.exp(scores - log_total[:, :, None])
    value_heads = head_split(key_piece[:, C:])
    weight_grad = jnp.einsum(
        "qhd,khd->hqk", grad_heads, value_heads, preferred_element_type=jnp.float32
    )
    score_grad = (weights * (weight_grad - row_dots[:, :, None])).astype(jnp.bfloat16)
    outcome = []
    key_heads = head_split(key_piece[:, :C])
    query_grad = jnp.einsum(
        "hqk,khd->qhd", score_grad, key_heads, preferred_element_type=jnp.float32
    ) * HEAD ** (-0.5)
    outcome.append(query_grad.reshape(query_grad.shape[0], C))
    key_grad = jnp.einsum(
        "hqk,qhd->khd", score_grad, query_heads, preferred_element_type=jnp.float32
    ) * HEAD ** (-0.5)
    value_grad = jnp.einsum(
        "hqk,qhd->khd", weights.astype(jnp.bfloat16), grad_heads, preferred_element_type=jnp.float32
    )
    outcome.append(jnp.concatenate([key_grad.reshape(-1, C), value_grad.reshape(-1, C)], axis=1))
    return tuple(outcome)


def source_masks(band_items, source, my_item, pixels):
    slots = band_items.shape[0]
    inside = (source >= 0) & (source < slots)
    clipped = jnp.clip(source, 0, slots - 1)
    source_item = band_items[clipped]
    before_item = band_items[jnp.maximum(clipped - 1, 0)]
    same_item = inside & (source_item == my_item)
    leading = same_item & ((clipped == 0) | (before_item != source_item))
    allowed = jnp.concatenate(
        [jnp.broadcast_to(same_item, (pixels,)), jnp.broadcast_to(leading, (TEXT,))]
    )
    return (allowed, same_item)


REACH = SPAN - 1
LOG2E = 1.4426950408889634
FAR_ABOVE = 1e30
PIX = 512


def dot(left, right):
    return jnp.dot(left, right, preferred_element_type=jnp.float32)


def reach_of(here, slots):
    first = here < SPAN
    low = jnp.maximum(jnp.where(first, 0, SPAN), here - REACH)
    high = jnp.minimum(jnp.where(first, SPAN - 1, slots - 1), here + REACH)
    return low, high


def exchange_kernel(slots, with_edges, *refs):
    if with_edges:
        tile, top, bottom, window, above, below, send_sem, recv_sem, edge_send, edge_recv = refs
    else:
        tile, window, send_sem, recv_sem = refs
    here = lax.axis_index(ROWS)
    low, high = reach_of(here, slots)
    offsets = [o for o in range(-REACH, REACH + 1) if o != 0]

    def reached(offset):
        return (here + offset >= low) & (here + offset <= high)

    barrier = pltpu.get_barrier_semaphore()
    for o in offsets:

        @pl.when(reached(o))
        def _(o=o):
            pl.semaphore_signal(barrier, 1, device_id={ROWS: here + o})

    pl.semaphore_wait(barrier, high - low)

    def edge_copy(o):
        source, target, k = (top, below, 0) if o < 0 else (bottom, above, 1)
        return pltpu.make_async_remote_copy(
            source, target, edge_send.at[k], edge_recv.at[k], device_id={ROWS: here + o}
        )

    def tile_copy(o):
        return pltpu.make_async_remote_copy(
            tile,
            window.at[REACH - o],
            send_sem.at[REACH - o],
            recv_sem.at[REACH - o],
            device_id={ROWS: here + o},
        )

    if with_edges:
        for o in (-1, 1):

            @pl.when(reached(o))
            def _(o=o):
                edge_copy(o).start()

    for o in offsets:

        @pl.when(reached(o))
        def _(o=o):
            tile_copy(o).start()

        @pl.when(jnp.logical_not(reached(-o)))
        def _(o=o):
            window[REACH - o] = jnp.zeros_like(tile)

    window[REACH] = tile[...]
    if with_edges:

        @pl.when(jnp.logical_not(reached(-1)))
        def _():
            above[...] = jnp.zeros_like(above)

        @pl.when(jnp.logical_not(reached(1)))
        def _():
            below[...] = jnp.zeros_like(below)

    for o in offsets:

        @pl.when(reached(o))
        def _(o=o):
            tile_copy(o).wait_send()

        @pl.when(reached(-o))
        def _(o=o):
            tile_copy(o).wait_recv()

    if with_edges:
        for o in (-1, 1):

            @pl.when(reached(o))
            def _(o=o):
                edge_copy(o).wait_send()

            @pl.when(reached(-o))
            def _(o=o):
                edge_copy(o).wait_recv()


def exchange(ident, slots, tile, edges=None):
    vmem = pl.BlockSpec(memory_space=pltpu.VMEM)
    shapes = [jax.ShapeDtypeStruct((2 * REACH + 1,) + tile.shape, tile.dtype)]
    scratch = [pltpu.SemaphoreType.DMA((2 * REACH + 1,))] * 2
    operands = [tile]
    if edges is not None:
        shapes += [jax.ShapeDtypeStruct(e.shape, e.dtype) for e in edges]
        scratch += [pltpu.SemaphoreType.DMA((2,))] * 2
        operands += list(edges)
    return pl.pallas_call(
        functools.partial(exchange_kernel, slots, edges is not None),
        out_shape=tuple(shapes),
        in_specs=[vmem] * len(operands),
        out_specs=(vmem,) * len(shapes),
        scratch_shapes=scratch,
        compiler_params=pltpu.CompilerParams(collective_id=ident, has_side_effects=True),
        name=f"exchange_{ident}",
    )(*operands)


def attention_by_band(band_items, position, queries, keys_values, text_kv, attended_grad):
    my_item = band_items[position]
    pixels = queries.shape[0]
    own_allowed, own_same = source_masks(band_items, position, my_item, pixels)
    packed = jnp.concatenate([keys_values, text_kv], axis=0)
    pieces = [(0, packed, own_allowed, own_same)]
    for distance in range(1, SPAN):
        for offset in (distance, -distance):
            arrived = from_behind(packed, ROWS, offset)
            allowed, same_item = source_masks(band_items, position - offset, my_item, pixels)
            pieces.append((offset, arrived, allowed, same_item))
    query_heads = head_split(queries)
    row_top = jnp.full((HEADS, pixels), -jnp.inf, jnp.float32)
    weight_sum = jnp.zeros((HEADS, pixels), jnp.float32)
    for offset, key_piece, allowed, same_item in pieces:

        def gather_scores(state, key_piece=key_piece, allowed=allowed):
            top_old, sum_old = state
            scores = piece_scores(query_heads, key_piece, allowed)
            top_new = jnp.maximum(top_old, jnp.max(scores, axis=2))
            sum_new = sum_old * jnp.exp(top_old - top_new) + jnp.sum(
                jnp.exp(scores - top_new[:, :, None]), axis=2
            )
            return (top_new, sum_new)

        row_top, weight_sum = lax.cond(same_item, gather_scores, keep_state, (row_top, weight_sum))
    log_total = row_top + jnp.log(weight_sum)
    attended = jnp.zeros((pixels, HEADS, HEAD), jnp.float32)
    for offset, key_piece, allowed, same_item in pieces:

        def add_values(totals, key_piece=key_piece, allowed=allowed):
            scores = piece_scores(query_heads, key_piece, allowed)
            weights = jnp.exp(scores - log_total[:, :, None]).astype(jnp.bfloat16)
            return totals + jnp.einsum(
                "hqk,khd->qhd",
                weights,
                head_split(key_piece[:, C:]),
                preferred_element_type=jnp.float32,
            )

        attended = lax.cond(same_item, add_values, keep_state, attended)
    attended_flat = attended.reshape(pixels, C)
    row_dots = jnp.sum(
        (attended_grad.astype(jnp.float32) * attended_flat).reshape(pixels, HEADS, HEAD), axis=2
    ).T
    grad_heads = head_split(attended_grad)
    query_grad = jnp.zeros((pixels, C), jnp.float32)
    packed_grad = jnp.zeros((pixels + TEXT, 2 * C), jnp.float32)
    zero_piece = jnp.zeros((pixels + TEXT, 2 * C), jnp.float32)
    for offset, key_piece, allowed, same_item in pieces:

        def grad_both(totals, key_piece=key_piece, allowed=allowed):
            outcome = piece_grads(query_heads, grad_heads, log_total, row_dots, key_piece, allowed)
            return (totals + outcome[0], outcome[1])

        def grad_none(totals):
            return (totals, zero_piece)

        query_grad, piece_grad = lax.cond(same_item, grad_both, grad_none, query_grad)
        if offset == 0:
            packed_grad = packed_grad + piece_grad
        else:
            packed_grad = packed_grad + from_behind(
                as_sent(piece_grad), ROWS, -offset
            ).astype(jnp.float32)
    packed_low = packed_grad.astype(jnp.bfloat16)
    return (
        attended_flat.astype(jnp.bfloat16),
        query_grad.astype(jnp.bfloat16),
        packed_low[:pixels],
        packed_low[pixels:],
    )


def taps_of(rows, reverse):
    padded = rows.reshape(-1, W, rows.shape[1])
    row_list = [padded[:-2], padded[1:-1], padded[2:]]
    if reverse:
        row_list = row_list[::-1]
    zero_column = jnp.zeros_like(row_list[0][:, :1])
    views = []
    for row_view in row_list:
        left_view = jnp.concatenate([zero_column, row_view[:, :-1]], axis=1)
        right_view = jnp.concatenate([row_view[:, 1:], zero_column], axis=1)
        view_list = [left_view, row_view, right_view]
        if reverse:
            view_list = view_list[::-1]
        views = views + view_list
    return [view.reshape(-1, rows.shape[1]) for view in views]


class Vectors(typing.NamedTuple):
    mean_one: jax.Array
    scale_one: jax.Array
    gain_one: jax.Array
    bias_one: jax.Array
    mean_two: jax.Array
    scale_two: jax.Array
    gain_two: jax.Array
    bias_two: jax.Array
    mean_three: jax.Array
    scale_three: jax.Array
    gain_three: jax.Array
    bias_three: jax.Array
    stretch: jax.Array
    shift: jax.Array
    proj_bias: jax.Array
    keep_above: jax.Array
    keep_below: jax.Array
    per_item: jax.Array


def grouped(names, refs):
    found, position = types.SimpleNamespace(), 0
    for name, count in names:
        if count is None:
            setattr(found, name, refs[position])
            position += 1
        else:
            setattr(found, name, refs[position : position + count])
            position += count
    return found


def call_named(
    kernel, ident, scalars, inputs, anywhere, outs, scratch, semaphores, far=types.MappingProxyType({})
):
    names = [(name, None) for name in [*scalars, *inputs, *anywhere, *outs, *far]]
    buffers = []
    for name, entry in scratch.items():
        many = isinstance(entry, list)
        names.append((name, len(entry) if many else None))
        buffers += [pltpu.VMEM(*e) for e in (entry if many else [entry])]
    names += [(name, None) for name in semaphores]
    vmem = pl.BlockSpec(memory_space=pltpu.VMEM)
    outcome = pl.pallas_call(
        functools.partial(kernel, names),
        out_shape=tuple(jax.ShapeDtypeStruct(*o) for o in [*outs.values(), *far.values()]),
        in_specs=[pl.BlockSpec(memory_space=pltpu.SMEM)] * len(scalars)
        + [vmem] * len(inputs)
        + [pl.BlockSpec(memory_space=pl.ANY)] * len(anywhere),
        out_specs=(vmem,) * len(outs) + (pl.BlockSpec(memory_space=pl.ANY),) * len(far),
        scratch_shapes=buffers + [pltpu.SemaphoreType.DMA(s) for s in semaphores.values()],
        compiler_params=pltpu.CompilerParams(
            collective_id=ident, has_side_effects=True, vmem_limit_bytes=60 << 20
        ),
        name=kernel.__name__,
    )(*[v for group in (scalars, inputs, anywhere) for v in dict(group).values()])
    return types.SimpleNamespace(**dict(zip([*outs, *far], outcome)))


VECTOR_ROWS = 24
FAR, NEAR, SIDE, CORE, GROUP = range(5)
CROSS = (FAR, NEAR, SIDE)
GROUP_FIRST = (GROUP, NEAR, SIDE, FAR)
STREAMS = (
    (144, C // 4, (SIDE, NEAR, FAR)),
    (144, C // 4, (NEAR, SIDE, FAR)),
    (144, C // 4, (SIDE, NEAR, FAR)),
    (144, C // 4, (NEAR, SIDE, FAR)),
    (64, C // 2, (SIDE, NEAR, FAR)),
    (64, C // 2, (NEAR, SIDE, FAR)),
    (16, 3 * C // 2, GROUP_FIRST),
    (16, C // 2, GROUP_FIRST),
)
FIRST_CONV, SECOND_CONV, WORDS, QKV, PROJ = 0, 2, 4, 6, 7
FIRST_LANDING = [sum(len(s[2]) for s in STREAMS[:k]) for k in range(len(STREAMS))]
HALF_SUMS, GROUP_SUMS = -1, -2
TAIL = (2, 3, 6, 0, 1, 4, 5, -1, 2, 3, 0, 1, 6, -2, 2, 3, 0, 1, 0, 1)
IMAGE_ROWS = 8


class Band:
    def __init__(self, r):
        self.r = r
        self.row = lax.axis_index(ROWS)
        self.group = lax.axis_index(ITEMS)
        self.lane = self.row % SPAN
        self.base = self.row - self.lane
        row = self.row
        self.place = [row // 8, (row // 4) % 2, (row // 2) % 2, row % 2, self.group]
        self.partner = [
            {ROWS: row + (1 - 2 * self.place[d]) * (8 >> d)} for d in range(CORE + 1)
        ]
        self.partner.append({ITEMS: 1 - self.group})
        self.others = [(self.lane + o) % SPAN for o in range(1, SPAN)]
        self.peers = [{ROWS: self.base + other} for other in self.others]
        self.has_above, self.has_below = self.lane > 0, self.lane < SPAN - 1

    def meet(self, further=()):
        barrier = pltpu.get_barrier_semaphore()
        targets = self.peers + list(further)
        for target in targets:
            pl.semaphore_signal(barrier, 1, device_id=target)
        pl.semaphore_wait(barrier, len(targets))

    def remote(self, source, target, send, recv, device):
        return pltpu.make_async_remote_copy(source, target, send, recv, device_id=device)

    def edges(self, k, top, bottom, target):
        r = self.r
        up = self.remote(
            top,
            target.at[IMAGE_ROWS + 1],
            r.edge_send.at[k, 0],
            r.edge_recv.at[k, 0],
            {ROWS: self.row - 1},
        )
        down = self.remote(
            bottom,
            target.at[0],
            r.edge_send.at[k, 1],
            r.edge_recv.at[k, 1],
            {ROWS: self.row + 1},
        )
        pl.when(self.has_above)(up.start)
        pl.when(self.has_below)(down.start)
        return up, down

    def wait_edges(self, pair):
        up, down = pair

        @pl.when(self.has_above)
        def _():
            up.wait_send()
            down.wait_recv()

        @pl.when(self.has_below)
        def _():
            down.wait_send()
            up.wait_recv()

    def zero_edges(self, target):
        @pl.when(jnp.logical_not(self.has_above))
        def _():
            target[0] = jnp.zeros(target.shape[1:], target.dtype)

        @pl.when(jnp.logical_not(self.has_below))
        def _():
            target[IMAGE_ROWS + 1] = jnp.zeros(target.shape[1:], target.dtype)

    def send_tile(self, k, source, target):
        r = self.r
        copies = []
        for o in range(1, SPAN):
            copies.append(
                self.remote(
                    source,
                    target.at[self.lane],
                    r.tile_send.at[k, o],
                    r.tile_recv.at[k, o],
                    self.peers[o - 1],
                )
            )
        for copy in copies:
            copy.start()
        target[self.lane] = source[...]
        return copies

    def swap(self, k, source, target, order=range(1, SPAN)):
        r = self.r
        copies = []
        for o in order:
            copies.append(
                self.remote(
                    source.at[self.others[o - 1]],
                    target.at[self.lane],
                    r.swap_send.at[k, o],
                    r.swap_recv.at[k, o],
                    self.peers[o - 1],
                )
            )
            copies[-1].start()
        return copies

    def fill_blocks(self):
        rows = lax.broadcasted_iota(jnp.int32, (C, C), 0) // (C // NORM_GROUPS)
        columns = lax.broadcasted_iota(jnp.int32, (C, C), 1) // (C // NORM_GROUPS)
        self.r.blocks[...] = jnp.where(rows == columns, 1.0, 0.0).astype(jnp.bfloat16)

    def item_means(self, window, masks, per_item):
        low, full = jnp.bfloat16, jnp.float32
        tile = jnp.zeros((8, C // 4), full)
        for b in range(SPAN):
            tile = tile + jnp.where(masks[b][:, 0 : C // 4] > 0.0, window[b], 0.0)
        first, second = [
            jnp.concatenate([tile[j : j + 1, :] for j in range(4 * k, 4 * k + 4)], axis=1)
            for k in range(2)
        ]
        rows = lax.broadcasted_iota(jnp.int32, (8, C), 0)
        total = jnp.where(rows == 0, first, jnp.where(rows == 1, second, 0.0)) * per_item
        coarse = total.astype(low)
        rest = total - coarse.astype(full)
        finer = rest.astype(low)
        finest = (rest - finer.astype(full)).astype(low)
        blocks = self.r.blocks[...]
        return dot(coarse, blocks) + dot(finer, blocks) + dot(finest, blocks)


def sums_tile(first, second):
    rows = lax.broadcasted_iota(jnp.int32, (8, C // 4), 0)
    tile = jnp.zeros((8, C // 4), jnp.float32)
    for k, values in enumerate((first, second)):
        for j in range(4):
            part = values[:, j * (C // 4) : (j + 1) * (C // 4)]
            tile = jnp.where(rows == 4 * k + j, part, tile)
    return tile


def column_sum(values):
    return jnp.sum(values, axis=0, keepdims=True)


def side_shifts(values):
    rows = lax.broadcasted_iota(jnp.int32, values.shape, 0)
    from_left = jnp.where(rows == 0, 0.0, pltpu.roll(values, 1, 0))
    from_right = jnp.where(rows == W - 1, 0.0, pltpu.roll(values, W - 1, 0))
    return from_left, from_right


def kept(i, values, vec):
    keep = jnp.where(i == 0, vec.keep_above, jnp.where(i == IMAGE_ROWS + 1, vec.keep_below, 1.0))
    return jnp.where(keep > 0.0, values, 0.0)


def back_kernel(names, *refs):
    low, full = jnp.bfloat16, jnp.float32
    r = grouped(names, refs)
    band = Band(r)
    lane, group, place, partner = band.lane, band.group, band.place, band.partner
    core = place[CORE]
    remote = band.remote
    across = {ROWS: partner[CORE][ROWS], ITEMS: 1 - group}
    band.meet((partner[FAR], partner[GROUP], across))
    quad = (partner[CORE], partner[GROUP], across)
    quarter = 2 * group + core
    quarters = (2 * group + 1 - core, 2 * (1 - group) + core, 2 * (1 - group) + 1 - core)

    def columns_of(which, size):
        return pl.ds(pl.multiple_of(which * size, size), size)

    def to_quad(kind, source, target):
        copies = [
            remote(
                source(quarters[i]), target.at[i], r.quad_send.at[kind, i], r.quad_recv.at[kind, i], quad[i]
            )
            for i in range(3)
        ]
        for copy in copies:
            copy.start()
        return copies


    swaps = band.swap(0, r.pair_grads, r.head_pairs) + band.swap(1, r.word_grads, r.head_words)

    loads = types.SimpleNamespace()

    def load(k, source, target):
        copy = pltpu.make_async_copy(source, target, r.load_sem.at[k])
        copy.start()
        return copy

    loads.outcome = load(0, r.outcome, r.heads)
    loads.pair_grads = load(1, r.pair_grads.at[lane], r.head_pairs.at[lane])
    loads.word_grads = load(14, r.word_grads.at[lane], r.head_words.at[lane])
    loads.middle = load(2, r.middle, r.mid)
    loads.qkv_weight = load(3, r.qkv_weight, r.qkv_w)
    loads.proj_weight = load(4, r.proj_weight, r.proj_w)
    loads.upstream = load(5, r.upstream, r.up)
    loads.act_three = load(6, r.act_three, r.act3)
    loads.caption = load(7, r.caption, r.caps.at[0])
    loads.far_caption = load(15, r.far_caption, r.caps.at[2])
    loads.conv_second = load(8, r.conv_second, r.conv_w)
    loads.hidden = load(9, r.hidden, r.hid)
    loads.act_two = load(10, r.act_two, r.acts_two.at[0])
    loads.far_act_two = load(16, r.far_act_two, r.acts_two.at[2])
    loads.act_one = load(11, r.act_one, r.acts_one.at[0])
    loads.far_act_one = load(17, r.far_act_one, r.acts_one.at[2])
    loads.image = load(12, r.image, r.img)
    loads.text_weight = load(13, r.text_weight, r.text_w)

    sibling = types.SimpleNamespace()

    def to_sibling(k, source, target):
        copy = remote(source, target, r.sib_send.at[k], r.sib_recv.at[k], partner[CORE])
        copy.start()
        return copy

    half = pl.ds(pl.multiple_of((1 - core) * (C // 2), C // 2), C // 2)
    sibling.upstream = to_sibling(0, r.upstream.at[:, half], r.sib_up)
    sibling.act3 = to_sibling(1, r.act_three, r.sib_act3)
    sibling.cap = to_sibling(2, r.caption, r.caps.at[1])
    sibling.far_cap = to_sibling(7, r.far_caption, r.caps.at[3])

    share_copy = remote(
        r.silu_share, r.other_share, r.small_send.at[2], r.small_recv.at[2], partner[GROUP]
    )
    share_copy.start()
    for target in (r.part_two, r.part_one):
        band.zero_edges(target)

    vec = Vectors(*[r.vectors[i : i + 1, :] for i in range(len(Vectors._fields))])
    norm_one = (vec.mean_one, vec.scale_one)
    norm_two = (vec.mean_two, vec.scale_two)
    norm_three = (vec.mean_three, vec.scale_three)

    masks = [r.vectors[VECTOR_ROWS + b : VECTOR_ROWS + b + 1, :] for b in range(SPAN)]
    band.fill_blocks()

    def item_means(window):
        return band.item_means(window, masks, vec.per_item)

    class Stream:
        def __init__(self, k):
            self.k = k
            self.order = STREAMS[k][2]
            self.dims = [FAR, NEAR, SIDE, CORE, GROUP][: len(self.order) + 1]
            self.step = 0
            self.copies = []

        def at(self, ref, d, index):
            return ref.at[(slice(None),) * self.dims.index(d) + (index,)]

        def start(self):
            self.launch(r.grads[self.k])

        def launch(self, ref):
            k, step = self.k, self.step
            if step < len(self.order):
                d = self.order[step]
                self.copies = [
                    remote(
                        self.at(ref, d, 1 - place[d]),
                        r.landings[FIRST_LANDING[k] + step],
                        r.fold_send.at[k, step],
                        r.fold_recv.at[k, step],
                        partner[d],
                    )
                ]
                self.mine = self.at(ref, d, place[d])
                self.dims.remove(d)
            else:
                if GROUP in self.order:
                    places = (r.folded[k], r.whole[k - QKV], r.whole[k - QKV])
                    self.place = core
                else:
                    places = (r.folded[k],) * 3
                    self.place = quarter
                sources = (ref.at[1 - core], ref.at[core], ref.at[1 - core])
                ends = [
                    (source, target.at[self.place], device)
                    for source, target, device in zip(sources, places, quad)
                ]
                self.copies = [
                    remote(
                        source,
                        target,
                        r.fold_send.at[k, step + i],
                        r.fold_recv.at[k, step + i],
                        device,
                    )
                    for i, (source, target, device) in enumerate(ends)
                ]
                self.mine = ref.at[core]
            for copy in self.copies:
                copy.start()

        def advance(self):
            for copy in self.copies:
                copy.wait()
            if self.step < len(self.order):
                landed, mine = r.landings[FIRST_LANDING[self.k] + self.step], self.mine
                lead = landed.shape[:-2]
                pieces = 1
                for n in lead:
                    pieces *= n

                def add(i, carry):
                    index = []
                    for n in reversed(lead):
                        index.insert(0, i % n)
                        i = i // n
                    index = tuple(index)
                    landed[index] = landed[index] + mine[index]
                    return carry

                lax.fori_loop(0, pieces, add, 0)
                self.step += 1
                self.launch(landed)
            else:
                r.folded[self.k][self.place] = self.mine[...]
                self.step += 1

    streams = [Stream(k) for k in range(len(STREAMS))]

    def advance(*order):
        for k in order:
            streams[k].advance()

    loads.outcome.wait()
    for h in range(0, HEADS, 2):
        for k in range(2):
            pair = [r.heads[h + i, :, k * HEAD : (k + 1) * HEAD] for i in range(2)]
            r.joined[:, k * C + h * HEAD : k * C + (h + 2) * HEAD] = jnp.concatenate(pair, axis=1)
    sibling.attended = to_sibling(5, r.joined.at[:, 0:C], r.sib_attended)

    def pixel_block(ref, i, count=4):
        return ref[1 + i * count : 1 + (i + 1) * count].reshape(count * W, C)

    def unit(values, norm):
        return (values - norm[0]) * norm[1]

    def mine_of(ref, start, size):
        return ref[:, pl.ds(pl.multiple_of(start, size if size % 256 else 256), size)]

    for copy in (loads.middle, loads.qkv_weight, loads.proj_weight, loads.upstream):
        copy.wait()
    up_sum = jnp.zeros((1, C), full)
    for i in range(2):
        block = slice(i * 4 * W, (i + 1) * 4 * W)
        upstream = r.up[block, :].astype(full)
        up_sum = up_sum + column_sum(upstream)
        result = pixel_block(r.mid, i) + dot(r.joined[block, 0:C], r.proj_w[...]) + vec.proj_bias
        r.result[block, :] = result.astype(low)
        grad = dot_last(r.joined[block, C : 2 * C], r.qkv_w[:, 0:C])
        r.product[i * 4 : i * 4 + 4] = grad.reshape(4, W, C)
    sibling.upstream.wait()
    sibling.attended.wait()
    grad = dot_first(r.joined[:, 0:C], mine_of(r.up, core * (C // 2), C // 2))
    grad = grad + dot_first(r.sib_attended[...], r.sib_up[...])
    r.grads[PROJ][...] = grad.astype(low).reshape(r.grads[PROJ].shape)
    streams[PROJ].start()
    query_sum = column_sum(r.joined[:, C : 2 * C].astype(full))

    for copy in (loads.pair_grads, loads.word_grads):
        copy.wait()
    for copy in swaps:
        copy.wait()
    for h in range(0, HEADS, 2):
        for k in range(2):
            lanes = slice(k * HEAD, (k + 1) * HEAD)
            pair = [r.head_pairs[h + i, :, lanes] for i in range(2)]
            first = (2 + k) * C + h * HEAD
            r.joined[:, first : first + 2 * HEAD] = jnp.concatenate(pair, axis=1)
            pair = [r.head_words[h + i, :, lanes] for i in range(2)]
            first = k * C + h * HEAD
            r.joined_words[:, first : first + 2 * HEAD] = jnp.concatenate(pair, axis=1)
    three_half = C + (1 - core) * (3 * C // 2)
    sibling.qkv = to_sibling(
        6, r.joined.at[:, pl.ds(pl.multiple_of(three_half, C // 2), 3 * C // 2)], r.sib_qkv
    )
    word_copies = to_quad(0, lambda q: r.joined_words.at[:, columns_of(q, C // 2)], r.word_parts)
    r.own_word_part[...] = r.joined_words[:, columns_of(quarter, C // 2)]
    sibling.act2 = to_sibling(3, r.act_two, r.acts_two.at[1])
    sibling.far_act2 = to_sibling(8, r.far_act_two, r.acts_two.at[3])
    sibling.act1 = to_sibling(4, r.act_one, r.acts_one.at[1])
    sibling.far_act1 = to_sibling(9, r.far_act_one, r.acts_one.at[3])

    plain = jnp.zeros((1, C), full)
    crossed = jnp.zeros((1, C), full)
    for i in range(2):
        block = slice(i * 4 * W, (i + 1) * 4 * W)
        grad = dot_last(r.joined[block, 2 * C :], r.qkv_w[:, C:])
        grad = grad + r.product[i * 4 : i * 4 + 4].reshape(4 * W, C)
        plain = plain + column_sum(grad)
        crossed = crossed + column_sum(grad * unit(pixel_block(r.mid, i), norm_three))
        part = r.up[block, :].astype(full) + grad * (vec.gain_three * vec.scale_three)
        r.part_two[1 + i * 4 : 5 + i * 4] = part.reshape(4, W, C)
    gain_three, bias_three = crossed, plain
    r.tile[0] = sums_tile(plain * vec.gain_three, crossed * vec.gain_three)
    three_edges = band.edges(0, r.part_two.at[1], r.part_two.at[IMAGE_ROWS], r.part_two)
    tiles = band.send_tile(0, r.tile.at[0], r.window.at[0])

    for copy in (sibling.act3, sibling.qkv, loads.act_three):
        copy.wait()
    for n in range(3):
        own = mine_of(r.joined, C + core * (3 * C // 2) + n * (C // 2), C // 2)
        columns = slice(n * (C // 2), (n + 1) * (C // 2))
        grad = dot_first(r.act3[...], own)
        grad = grad + dot_first(r.sib_act3[...], r.sib_qkv[:, columns])
        r.grads[QKV][:, :, :, :, :, :, columns] = grad.astype(low).reshape(2, 2, 2, 2, 2, 16, C // 2)
    streams[QKV].start()

    for copy in (sibling.cap, sibling.far_cap, loads.caption, loads.far_caption):
        copy.wait()
    for copy in word_copies:
        copy.wait()

    def text_rows(s, carry):
        columns = pl.ds(pl.multiple_of(s * 128, 128), 128)
        grad = dot_first(r.caps[0, :, columns], r.own_word_part[...])
        for i in range(3):
            grad = grad + dot_first(r.caps[i + 1, :, columns], r.word_parts[i])
        grad = grad.astype(low)
        index = (s // 8, (s // 4) % 2, (s // 2) % 2, s % 2)
        r.grads[WORDS][index] = grad[0:64]
        r.grads[WORDS + 1][index] = grad[64:128]
        return carry

    lax.fori_loop(0, 2 ** len(CROSS) * 2, text_rows, 0)
    streams[WORDS].start()
    streams[WORDS + 1].start()
    value_sum = column_sum(r.joined[:, 3 * C :].astype(full))
    word_sum = [column_sum(r.joined_words[:, k * C : (k + 1) * C].astype(full)) for k in range(2)]

    def spread_rows(i, values):
        from_left, from_right = side_shifts(values)
        r.shifts[0, i] = from_right.astype(low)
        r.shifts[1, i] = values.astype(low)
        r.shifts[2, i] = from_left.astype(low)

    def conv_back():
        total = jnp.zeros((IMAGE_ROWS * W, C), full)
        for t in range(9):
            dy, dx = t // 3, t % 3
            view = r.shifts[dx, 2 - dy : 2 - dy + IMAGE_ROWS].reshape(IMAGE_ROWS * W, C)
            total = total + dot_last(view, r.conv_w[t * C : (t + 1) * C, :])
        return total

    def gather_shifts(landing, places):
        width = C // 4

        def one_row(i, carry):
            for k in places:
                if k == 0:
                    for dx in range(3):
                        lanes = slice(dx * width, (dx + 1) * width)
                        r.sides[0, i, :, lanes] = r.shifts[dx, i + 1, :, columns_of(quarter, width)]
                    continue
                values = landing[k - 1, i].astype(full)
                from_left, from_right = side_shifts(values)
                r.sides[k, i, :, 0:width] = from_right.astype(low)
                r.sides[k, i, :, width : 2 * width] = landing[k - 1, i]
                r.sides[k, i, :, 2 * width :] = from_left.astype(low)
            return carry

        lax.fori_loop(0, IMAGE_ROWS, one_row, 0)

    def conv_grads(kind, acts, landing, arrivals):
        width = C // 4

        def products(dy, places):
            grad = jnp.zeros((C, 3 * width), full)
            for k in places:
                sides = r.sides[k].reshape(IMAGE_ROWS * W, 3 * width)
                grad = grad + dot_first(acts[k, dy * W : dy * W + IMAGE_ROWS * W, :], sides)
            return grad

        arrivals[0].wait()
        gather_shifts(landing, (0, 1))
        for dy in range(3):
            r.partial[dy] = products(dy, (0, 1))
        for copy in arrivals[1:]:
            copy.wait()
        gather_shifts(landing, (2, 3))
        for dy in range(3):
            grad = r.partial[dy] + products(dy, (2, 3))
            grad = grad.astype(low)
            for dx in range(3):
                begin = first = (dy * 3 + dx) * C
                while begin < first + C:
                    shard, within = divmod(begin, 288)
                    stream, offset = divmod(within, 144)
                    size = min(144 - offset, first + C - begin)
                    target = r.grads[kind + stream]
                    target[
                        shard // 8,
                        (shard // 4) % 2,
                        (shard // 2) % 2,
                        shard % 2,
                        offset : offset + size,
                    ] = grad[begin - first : begin - first + size, dx * width : (dx + 1) * width]
                    begin += size
        for j in range(2):
            streams[kind + j].start()

    for copy in tiles:
        copy.wait()
    band.wait_edges(three_edges)
    means = item_means(r.window.at[0])
    offset_three, slope_three = means[0:1] * vec.scale_three, means[1:2] * vec.scale_three

    def middle_row(i, bias):
        values = r.part_two[i] - offset_three - unit(r.mid[i], norm_three) * slope_three
        r.part_two[i] = values
        values = kept(i, values, vec)
        spread_rows(i, values)
        inside = jnp.where((i > 0) & (i <= IMAGE_ROWS), 1.0, 0.0)
        return bias + inside * column_sum(values.astype(low).astype(full))

    conv_bias_two = lax.fori_loop(0, IMAGE_ROWS + 2, middle_row, jnp.zeros((1, C), full))
    def center(q):
        return r.shifts.at[1, 1 : IMAGE_ROWS + 1, :, columns_of(q, C // 4)]

    side_copies = to_quad(1, center, r.sides_two)
    advance(PROJ)
    loads.conv_second.wait()
    loads.hidden.wait()
    r.product[...] = conv_back().reshape(IMAGE_ROWS, W, C)
    loads.conv_first = load(8, r.conv_first, r.conv_w)
    stretched = vec.stretch * vec.gain_two * vec.scale_two

    def second_row(i, sums):
        unit_two = unit(r.hid[i + 1], norm_two)
        normed = unit_two * vec.gain_two + vec.bias_two
        grad = r.product[i] * silu_slope_of(normed * vec.stretch + vec.shift)
        r.part_one[i + 1] = grad * stretched
        return sums[0] + column_sum(grad), sums[1] + column_sum(grad * unit_two)

    nothing = (jnp.zeros((1, C), full), jnp.zeros((1, C), full))
    plain, crossed = lax.fori_loop(0, IMAGE_ROWS, second_row, nothing)
    scale_grad = crossed * vec.gain_two + plain * vec.bias_two
    shift_grad = plain
    gain_two, bias_two = crossed * vec.stretch, plain * vec.stretch
    r.tile[1] = sums_tile(bias_two * vec.gain_two, gain_two * vec.gain_two)
    two_edges = band.edges(1, r.part_one.at[1], r.part_one.at[IMAGE_ROWS], r.part_one)
    tiles = band.send_tile(1, r.tile.at[1], r.window.at[1])
    for copy in (loads.act_two, loads.far_act_two, sibling.act2, sibling.far_act2):
        copy.wait()
    advance(PROJ, QKV, WORDS, WORDS + 1)
    conv_grads(SECOND_CONV, r.acts_two, r.sides_two, side_copies)
    advance(PROJ)
    for copy in tiles:
        copy.wait()
    band.wait_edges(two_edges)
    means = item_means(r.window.at[1])
    offset_two, slope_two = means[0:1] * vec.scale_two, means[1:2] * vec.scale_two

    def hidden_row(i, bias):
        values = r.part_one[i] - offset_two - unit(r.hid[i], norm_two) * slope_two
        values = kept(i, values, vec)
        spread_rows(i, values)
        inside = jnp.where((i > 0) & (i <= IMAGE_ROWS), 1.0, 0.0)
        return bias + inside * column_sum(values.astype(low).astype(full))

    conv_bias_one = lax.fori_loop(0, IMAGE_ROWS + 2, hidden_row, jnp.zeros((1, C), full))
    side_copies = to_quad(2, center, r.sides_one)
    advance(PROJ, QKV, WORDS, WORDS + 1)
    loads.conv_first.wait()
    loads.image.wait()
    r.product[...] = conv_back().reshape(IMAGE_ROWS, W, C)

    def first_row(i, sums):
        unit_one = unit(r.img[i].astype(full), norm_one)
        normed = unit_one * vec.gain_one + vec.bias_one
        grad = r.product[i] * silu_slope_of(normed)
        r.product[i] = grad
        return sums[0] + column_sum(grad), sums[1] + column_sum(grad * unit_one)

    plain, crossed = lax.fori_loop(0, IMAGE_ROWS, first_row, nothing)
    gain_one, bias_one = crossed, plain
    r.tile[2] = sums_tile(plain * vec.gain_one, crossed * vec.gain_one)
    tiles = band.send_tile(2, r.tile.at[2], r.window.at[2])
    rows = [
        gain_one,
        gain_two,
        gain_three,
        bias_one,
        bias_two,
        bias_three,
        conv_bias_one,
        conv_bias_two,
        query_sum,
        value_sum,
        word_sum[0],
        word_sum[1],
        up_sum,
        jnp.zeros((1, C), full),
        scale_grad,
        shift_grad,
    ]
    for i, values in enumerate(rows):
        r.own_rows[i : i + 1, :] = values
    row_copies = band.send_tile(3, r.own_rows, r.band_rows)
    for copy in (loads.act_one, loads.far_act_one, sibling.act1, sibling.far_act1):
        copy.wait()
    advance(PROJ, QKV, WORDS, WORDS + 1, 2, 3)
    conv_grads(FIRST_CONV, r.acts_one, r.sides_one, side_copies)
    for copy in tiles:
        copy.wait()
    means = item_means(r.window.at[2])
    offset_one, slope_one = means[0:1] * vec.scale_one, means[1:2] * vec.scale_one
    ratio = vec.gain_one * vec.scale_one

    def image_row(i, carry):
        unit_one = unit(r.img[i].astype(full), norm_one)
        values = r.part_two[i + 1] + r.product[i] * ratio - offset_one - unit_one * slope_one
        r.image_grad[i] = values
        return carry

    lax.fori_loop(0, IMAGE_ROWS, image_row, 0)

    for copy in row_copies:
        copy.wait()
    total = jnp.zeros((16, C), full)
    for b in range(SPAN):
        total = total + r.band_rows[b]
    r.half_rows[0:16, :] = total
    for b in range(SPAN):
        r.half_rows[16 + 2 * b : 18 + 2 * b, :] = r.band_rows[b, 14:16, :]
    far_copy = remote(
        r.half_rows, r.far_rows, r.small_send.at[0], r.small_recv.at[0], partner[FAR]
    )
    far_copy.start()
    loads.text_weight.wait()

    def caption_columns(n, carry):
        columns = pl.ds(pl.multiple_of(n * C, C), C)
        r.caption_grad[:, columns] = dot_last(r.joined_words[...], r.text_w[columns, :])
        return carry

    lax.fori_loop(0, EMB // C, caption_columns, 0)
    loads.embed_weight = load(13, r.embed_weight, r.text_w)
    slots = r.slot_of_band.shape[0]
    held = types.SimpleNamespace()

    def half_sums_arrived():
        far_copy.wait()
        first_half = jnp.where(place[FAR] == 0, r.half_rows[16:32, :], r.far_rows[16:32, :])
        other_half = jnp.where(place[FAR] == 0, r.far_rows[16:32, :], r.half_rows[16:32, :])
        r.group_rows[0:16, :] = r.half_rows[0:16, :] + r.far_rows[0:16, :]
        r.group_rows[16:32, :] = first_half
        r.group_rows[32:48, :] = other_half
        for k in range(2):
            table = jnp.zeros((slots, C), full)
            for b in range(2 * SPAN):
                values = r.group_rows[16 + 2 * b + k : 17 + 2 * b + k, :]
                table = table + jnp.where(r.slot_of_band[:, b * 128 : b * 128 + 1] > 0.0, values, 0.0)
            r.own_table[slots * k : slots * (k + 1), :] = table
        r.own_table[2 * slots :, :] = r.group_rows[0:16, :]
        held.group_copy = remote(
            r.own_table,
            r.other_table,
            r.small_send.at[1],
            r.small_recv.at[1],
            partner[GROUP],
        )
        held.group_copy.start()
        loads.embed_weight.wait()
        held.table = table = [r.own_table[slots * k : slots * (k + 1), :].astype(low) for k in range(2)]

        def embedding_columns(n, carry):
            columns = pl.ds(pl.multiple_of(n * C, C), C)
            grad = dot_last(table[0], r.text_w[columns, 0:C]) + dot_last(table[1], r.text_w[columns, C:])
            source = r.embedding[:, columns].astype(full)
            r.embedding_grad[:, columns] = grad * silu_slope_of(source)
            return carry

        lax.fori_loop(0, EMB // C, embedding_columns, 0)

    def group_sums_arrived():
        held.group_copy.wait()
        share_copy.wait()
        table = held.table
        for k in range(2):
            columns = slice(k * C, (k + 1) * C)
            other = r.other_table[slots * k : slots * (k + 1), :].astype(low)
            r.embed_weight_grad[:, columns] = dot_first(r.silu_share[...], table[k]) + dot_first(
                r.other_share[...], other
            )
            r.embed_bias_grad[:, columns] = column_sum(table[k].astype(full)) + column_sum(
                other.astype(full)
            )
        sums = r.own_table[2 * slots :, :] + r.other_table[2 * slots :, :]
        r.norm_gains_grad[...] = sums[0:3]
        r.norm_biases_grad[...] = sums[3:6]
        r.conv_biases_grad[...] = sums[6:8]
        for target, k in ((r.qv_bias_grad, 8), (r.text_bias_grad, 10)):
            target[:, 0:C] = sums[k : k + 1]
            target[:, C:] = sums[k + 1 : k + 2]
        r.proj_bias_grad[...] = sums[12:13]

    for k in TAIL:
        if k == HALF_SUMS:
            half_sums_arrived()
        elif k == GROUP_SUMS:
            group_sums_arrived()
        else:
            advance(k)

    def write(stream, target, first_row):
        rows, columns = STREAMS[stream][:2]
        for k in range(4):
            target[first_row : first_row + rows, k * columns : (k + 1) * columns] = r.folded[stream][
                k
            ].astype(full)

    def write_halves(stream, target):
        rows, columns = STREAMS[stream][:2]
        for side, source in ((group, r.folded[stream]), (1 - group, r.whole[stream - QKV])):
            for k in range(2):
                target[
                    pl.ds(pl.multiple_of(side * rows, rows), rows), k * columns : (k + 1) * columns
                ] = source[k].astype(full)

    for j in range(2):
        write(FIRST_CONV + j, r.conv_first_grad, j * 144)
        write(SECOND_CONV + j, r.conv_second_grad, j * 144)
        write(WORDS + j, r.text_grad, j * 64)
    write_halves(QKV, r.qkv_grad)
    write_halves(PROJ, r.proj_grad)


def silu_slope_of(source):
    sigma = 1.0 / (1.0 + jnp.exp(-source))
    return sigma * (1.0 + source * (1.0 - sigma))


def back(ident, vectors, slot_of_band, silu_share, embedding, anywhere):
    low, full = jnp.bfloat16, jnp.float32
    pixels = IMAGE_ROWS * W
    slots = slot_of_band.shape[0]
    outs = dict(
        result=((pixels, C), low),
        image_grad=((IMAGE_ROWS, W, C), full),
        caption_grad=((TEXT, EMB), full),
        conv_first_grad=((288, C), full),
        conv_second_grad=((288, C), full),
        qkv_grad=((32, 3 * C), full),
        text_grad=((128, 2 * C), full),
        proj_grad=((32, C), full),
        embedding_grad=(embedding.shape, full),
        embed_weight_grad=((silu_share.shape[1], 2 * C), full),
        norm_gains_grad=((3, C), full),
        norm_biases_grad=((3, C), full),
        conv_biases_grad=((2, C), full),
        embed_bias_grad=((1, 2 * C), full),
        qv_bias_grad=((1, 2 * C), full),
        text_bias_grad=((1, 2 * C), full),
        proj_bias_grad=((1, C), full),
    )
    padded = (IMAGE_ROWS + 2, W, C)
    scratch = dict(
        heads=((HEADS, pixels, 2 * HEAD), low),
        head_pairs=((HEADS, pixels, 2 * HEAD), low),
        head_words=((HEADS, TEXT, 2 * HEAD), low),
        joined=((pixels, 4 * C), low),
        joined_words=((TEXT, 2 * C), low),
        mid=(padded, full),
        part_two=(padded, full),
        part_one=(padded, full),
        hid=(padded, full),
        product=((IMAGE_ROWS, W, C), full),
        img=((IMAGE_ROWS, W, C), low),
        up=((pixels, C), low),
        act3=((pixels, C), low),
        conv_w=((9 * C, C), low),
        qkv_w=((C, 3 * C), low),
        proj_w=((C, C), low),
        text_w=((EMB, 2 * C), low),
        sib_up=((pixels, C // 2), low),
        sib_act3=((pixels, C), low),
        sib_attended=((pixels, C), low),
        sib_qkv=((pixels, 3 * C // 2), low),
        acts_one=((4, pixels + 2 * W, C), low),
        acts_two=((4, pixels + 2 * W, C), low),
        caps=((4, TEXT, EMB), low),
        own_word_part=((TEXT, C // 2), low),
        word_parts=((3, TEXT, C // 2), low),
        sides_one=((3, IMAGE_ROWS, W, C // 4), low),
        sides_two=((3, IMAGE_ROWS, W, C // 4), low),
        sides=((4, IMAGE_ROWS, W, 3 * C // 4), low),
        partial=((3, C, 3 * C // 4), full),
        shifts=((3,) + padded, low),
        blocks=((C, C), low),
        tile=((3, 8, C // 4), full),
        window=((3, SPAN, 8, C // 4), full),
        own_rows=((16, C), full),
        band_rows=((SPAN, 16, C), full),
        half_rows=((32, C), full),
        far_rows=((32, C), full),
        group_rows=((48, C), full),
        own_table=((2 * slots + 16, C), full),
        other_table=((2 * slots + 16, C), full),
        other_share=(silu_share.shape, low),
    )
    def halved(stream, step):
        return ((2,) * (len(stream[2]) + 1 - step) + stream[:2], low)

    scratch.update(grads=[halved(s, 0) for s in STREAMS])
    scratch.update(landings=[halved(s, i + 1) for s in STREAMS for i in range(len(s[2]))])
    scratch.update(folded=[((2 if GROUP in s[2] else 4,) + s[:2], low) for s in STREAMS])
    scratch.update(whole=[((2,) + s[:2], low) for s in STREAMS[QKV:]])
    semaphores = dict(
        swap_send=(2, SPAN),
        swap_recv=(2, SPAN),
        load_sem=(18,),
        quad_send=(3, 3),
        quad_recv=(3, 3),
        sib_send=(10,),
        sib_recv=(10,),
        edge_send=(2, 2),
        edge_recv=(2, 2),
        tile_send=(4, SPAN),
        tile_recv=(4, SPAN),
        fold_send=(len(STREAMS), len(GROUP_FIRST) + 3),
        fold_recv=(len(STREAMS), len(GROUP_FIRST) + 3),
        small_send=(3,),
        small_recv=(3,),
    )
    inputs = dict(
        vectors=vectors, slot_of_band=slot_of_band, silu_share=silu_share, embedding=embedding
    )
    return call_named(back_kernel, ident, (), inputs, anywhere, outs, scratch, semaphores)


def attend_kernel(names, *refs):
    low, full = jnp.bfloat16, jnp.float32
    r = grouped(names, refs)
    band = Band(r)
    counterpart = band.partner[GROUP]
    band.meet((counterpart,))
    query_swaps = band.swap(0, r.own_queries, r.queries, range(SPAN - 1, 0, -1))
    r.queries[band.lane] = r.own_queries[band.lane]
    far_copies = [
        band.remote(source, target, r.far_send.at[k], r.far_recv.at[k], counterpart)
        for k, (source, target) in enumerate(
            (
                (r.caption, r.far_caption),
                (r.act_two, r.far_act_two),
                (r.act_one, r.far_act_one),
            )
        )
    ]
    for copy in far_copies:
        copy.start()
    bands, pixels = r.pairs.shape[:2]
    text = r.words.shape[1]
    scale = HEAD ** (-0.5)

    def with_units(values, rows):
        lanes = lax.broadcasted_iota(jnp.int32, (rows, 2 * HEAD), 1)
        units = jnp.where(lanes < 2, 1.0, 0.0).astype(low)
        return jnp.where(lanes < HEAD, units, values)

    def prepare(b, carry):
        r.across[b] = r.pairs[b].T
        r.valued[b] = with_units(r.pairs[b], pixels)
        r.words_across[b] = r.words[b].T
        r.words_valued[b] = with_units(r.words[b], text)
        r.pair_sums[b] = jnp.zeros((pixels, 2 * HEAD), full)
        return carry

    lax.fori_loop(0, bands, prepare, 0)

    def one_row(columns):
        rows = lax.broadcasted_iota(jnp.int32, (16, columns), 0)
        return jnp.where(rows == 0, 1.0, 0.0).astype(low)

    ones_pixels = one_row(pixels)
    ones_text = one_row(text)
    zeros = jnp.zeros((HEAD, pixels), low)

    def outcome_copy(i):
        return band.remote(
            r.own_outcome.at[i],
            r.outcome.at[band.lane],
            r.outcome_send.at[i],
            r.outcome_recv.at[band.lane],
            {ROWS: band.base + i},
        )

    def query_band(step, carry):
        i = (band.lane + 1 + step) % bands
        mine = r.items[band.base + i]
        start = 0
        allowed = []
        for b in range(bands):
            other = r.items[band.base + b]
            start = start + jnp.where(other < mine, 1, 0)
            allowed.append(other == mine)

        @pl.when(step < bands - 1)
        def _():
            band.remote(
                r.own_queries.at[i],
                r.queries.at[i],
                r.swap_send.at[0, SPAN - 1 - step],
                r.swap_recv.at[0, SPAN - 1 - step],
                {ROWS: band.base + i},
            ).wait_recv()

        query = (r.queries[i].astype(full) * scale).astype(low)
        query_rhs = jnp.concatenate([query, zeros], 0)

        top = jnp.full((8, pixels), -jnp.inf, full)
        for j in range(bands):
            scores = dot(r.pairs[j], query_rhs)
            r.scores[j] = scores
            highest = jnp.max(scores.reshape(pixels // 8, 8, pixels), axis=0)
            top = jnp.where(allowed[j], jnp.maximum(top, highest), top)
        scores = dot(r.words[start], query_rhs)
        top = jnp.maximum(top, jnp.max(scores.reshape(text // 8, 8, pixels), axis=0))
        top = jnp.max(top, axis=0, keepdims=True)
        weights_text = jnp.exp2((scores - top) * LOG2E).astype(low)
        values = jnp.concatenate([r.words_across[start, HEAD:, :], ones_text], 0)
        total = dot(values, weights_text)

        for j in range(bands):
            ceiling = top + jnp.where(allowed[j], 0.0, FAR_ABOVE)
            weights = jnp.exp2((r.scores[j] - ceiling) * LOG2E).astype(low)
            r.weights[j] = weights
            values = jnp.concatenate([r.across[j, HEAD:, :], ones_pixels], 0)
            total = total + dot(values, weights)
        inverse = 1.0 / total[HEAD : HEAD + 1, :]
        attended = total[0:HEAD, :] * inverse
        grad = r.upstream[i].astype(full)
        minus_dots = -jnp.sum(grad * attended, axis=0, keepdims=True) * inverse
        grad_scaled = (grad * inverse).astype(low)
        coarse = minus_dots.astype(low)
        fine = minus_dots - coarse.astype(full)
        rows = lax.broadcasted_iota(jnp.int32, (HEAD, pixels), 0)
        extra = jnp.where(rows == 0, coarse.astype(full), jnp.where(rows == 1, fine, 0.0))
        grad_rhs = jnp.concatenate([extra.astype(low), grad_scaled], 0)
        grad_rows = jnp.concatenate([zeros, grad_scaled], 0).T
        query_rows = jnp.concatenate([query, zeros], 0).T

        steps = (weights_text.astype(full) * dot(r.words_valued[start], grad_rhs)).astype(low)
        word_sum = dot(weights_text, grad_rows) + dot(steps, query_rows)
        r.word_parts[i] = word_sum
        query_grad = dot(r.words_across[start, 0:HEAD, :], steps)
        for j in range(bands):
            for begin in range(0, pixels, pixels // 2):
                keys = slice(begin, begin + pixels // 2)
                weights = r.weights[j, keys]
                steps = (weights.astype(full) * dot(r.valued[j, keys], grad_rhs)).astype(low)
                r.pair_sums[j, keys] += dot(weights, grad_rows) + dot(steps, query_rows)
                query_grad = query_grad + dot(r.across[j, 0:HEAD, keys], steps)
        r.own_outcome[i] = jnp.concatenate(
            [attended.astype(low), (query_grad * scale).astype(low)], 0
        ).T
        pl.when(step < bands - 1)(outcome_copy(i).start)
        return carry

    lax.fori_loop(0, bands, query_band, 0)
    r.outcome[band.lane] = r.own_outcome[band.lane]

    def finish(b, carry):
        r.pair_grads[b] = r.pair_sums[b].astype(low)
        word_sum = jnp.zeros((text, 2 * HEAD), full)
        for i in range(bands):
            mine = r.items[band.base + i]
            start = 0
            for c in range(bands):
                start = start + jnp.where(r.items[band.base + c] < mine, 1, 0)
            word_sum = word_sum + jnp.where(start == b, r.word_parts[i], 0.0)
        r.word_grads[b] = word_sum.astype(low)
        return carry

    lax.fori_loop(0, bands, finish, 0)

    def wait_outcome(step, carry):
        i = (band.lane + 1 + step) % bands
        outcome_copy(i).wait_send()
        band.remote(
            r.own_outcome.at[i],
            r.outcome.at[i],
            r.outcome_send.at[i],
            r.outcome_recv.at[i],
            {ROWS: band.base + i},
        ).wait_recv()
        return carry

    lax.fori_loop(0, bands - 1, wait_outcome, 0)
    for copy in query_swaps:
        copy.wait_send()
    for copy in far_copies:
        copy.wait()


def attend(ident, items, ahead, caption):
    low, full = jnp.bfloat16, jnp.float32
    bands, pixels, _ = ahead.pairs.shape
    text = ahead.words.shape[1]
    outs = dict(
        outcome=((bands, pixels, 2 * HEAD), low),
        pair_grads=((bands, pixels, 2 * HEAD), low),
        word_grads=((bands, text, 2 * HEAD), low),
    )
    anywhere = dict(caption=caption, act_one=ahead.act_one, act_two=ahead.act_two)
    far = dict(
        far_caption=(caption.shape, low),
        far_act_one=(ahead.act_one.shape, low),
        far_act_two=(ahead.act_two.shape, low),
    )
    scratch = dict(
        queries=(ahead.own_queries.shape, low),
        across=((bands, 2 * HEAD, pixels), low),
        valued=((bands, pixels, 2 * HEAD), low),
        words_across=((bands, 2 * HEAD, text), low),
        words_valued=((bands, text, 2 * HEAD), low),
        scores=((bands, pixels, pixels), full),
        weights=((bands, pixels, pixels), low),
        pair_sums=((bands, pixels, 2 * HEAD), full),
        word_parts=((bands, text, 2 * HEAD), full),
        own_outcome=((bands, pixels, 2 * HEAD), low),
    )
    semaphores = dict(
        outcome_send=(bands,), outcome_recv=(bands,), far_send=(3,), far_recv=(3,),
        swap_send=(1, SPAN), swap_recv=(1, SPAN),
    )
    inputs = dict(
        pairs=ahead.pairs,
        own_queries=ahead.own_queries,
        upstream=ahead.upstream,
        words=ahead.words,
    )
    return call_named(
        attend_kernel, ident, dict(items=items), inputs, anywhere, outs, scratch, semaphores, far
    )


def front_kernel(names, *refs):
    low, full = jnp.bfloat16, jnp.float32
    r = grouped(names, refs)
    band = Band(r)
    band.meet()
    loads = types.SimpleNamespace()

    def load(k, source, target):
        copy = pltpu.make_async_copy(source, target, r.load_sem.at[k])
        copy.start()
        return copy

    loads.image = load(0, r.image, r.img.at[1 : IMAGE_ROWS + 1])
    image_edges = band.edges(0, r.image.at[0], r.image.at[IMAGE_ROWS - 1], r.img)
    loads.upstream = load(3, r.upstream_pixels, r.up)
    loads.proj_weight = load(4, r.proj_weight, r.proj_w)
    loads.conv_first = load(1, r.conv_first, r.first_w)
    loads.embed_weight = load(2, r.embed_weight, r.embed_w)
    loads.conv_second = load(5, r.conv_second, r.second_w)
    loads.caption = load(6, r.caption, r.cap)
    loads.text_weight = load(7, r.text_weight, r.text_w)
    loads.qkv_weight = load(8, r.qkv_weight, r.qkv_w)

    mine = r.items[band.row]
    same = [(r.items[band.base + b] == mine).astype(full) for b in range(SPAN)]
    masks = [jnp.full((1, C), m, full) for m in same]
    bands = masks[0]
    for m in masks[1:]:
        bands = bands + m
    per_item = 1.0 / (bands * (IMAGE_ROWS * W * (C // NORM_GROUPS)))
    before = jnp.where(band.has_above, r.items[jnp.maximum(band.row - 1, 0)], -1)
    after = jnp.where(
        band.has_below, r.items[jnp.minimum(band.row + 1, r.items.shape[0] - 1)], -1
    )
    found = types.SimpleNamespace(
        gain_one=r.norm_gains[0:1, :],
        gain_two=r.norm_gains[1:2, :],
        gain_three=r.norm_gains[2:3, :],
        bias_one=r.norm_biases[0:1, :],
        bias_two=r.norm_biases[1:2, :],
        bias_three=r.norm_biases[2:3, :],
        proj_bias=r.proj_bias[...],
        keep_above=jnp.full((1, C), (before == mine).astype(full)),
        keep_below=jnp.full((1, C), (after == mine).astype(full)),
        per_item=per_item,
    )
    for target in (r.img, r.hidden, r.middle):
        band.zero_edges(target)
    nothing = (jnp.zeros((1, C), full), jnp.zeros((1, C), full))

    def norm_of(k):
        means = band.item_means(r.window.at[k], masks, per_item)
        return means[0:1], lax.rsqrt(means[1:2] - means[0:1] * means[0:1] + epsilon)

    loads.image.wait()

    def image_sums(i, sums):
        values = r.img[i + 1].astype(full)
        return sums[0] + column_sum(values), sums[1] + column_sum(values * values)

    r.tile[0] = sums_tile(*lax.fori_loop(0, IMAGE_ROWS, image_sums, nothing))
    tiles = band.send_tile(0, r.tile.at[0], r.window.at[0])

    loads.upstream.wait()
    loads.proj_weight.wait()
    attended_grad = dot_last(r.proj_w[...], r.up[...]).astype(low)
    for h in range(HEADS):
        r.own_upstream[h] = attended_grad[h * HEAD : (h + 1) * HEAD, :]
    swaps = band.swap(0, r.own_upstream, r.upstream)
    r.upstream[band.lane] = r.own_upstream[band.lane]
    band.fill_blocks()
    slot = lax.broadcasted_iota(jnp.int32, r.embedding.shape, 0)
    chosen = jnp.where(slot == mine, r.embedding[...].astype(full), 0.0)
    chosen = jnp.sum(chosen, axis=0, keepdims=True)
    chosen = chosen / (1.0 + jnp.exp(-chosen))
    chosen = jnp.broadcast_to(chosen, (16, EMB)).astype(low)
    loads.embed_weight.wait()
    modulation = dot(chosen, r.embed_w[...])[0:1] + r.embed_bias[...]
    found.stretch = 1.0 + modulation[:, 0:C]
    found.shift = modulation[:, C:]

    def spread_rows(i, values, target):
        values = kept(i, values, found)
        from_left, from_right = side_shifts(values)
        r.shifts[0, i] = from_left.astype(low)
        r.shifts[1, i] = values.astype(low)
        r.shifts[2, i] = from_right.astype(low)
        target[pl.ds(pl.multiple_of(i * W, W), W), :] = values.astype(low)

    def conv(weight):
        total = jnp.zeros((IMAGE_ROWS * W, C), full)
        for t in range(9):
            view = r.shifts[t % 3, t // 3 : t // 3 + IMAGE_ROWS].reshape(IMAGE_ROWS * W, C)
            total = total + dot(view, weight[t * C : (t + 1) * C, :])
        return total

    for copy in tiles:
        copy.wait()
    band.wait_edges(image_edges)
    found.mean_one, found.scale_one = norm_of(0)

    def first_row(i, carry):
        unit = (r.img[i].astype(full) - found.mean_one) * found.scale_one
        normed = unit * found.gain_one + found.bias_one
        spread_rows(i, normed / (1.0 + jnp.exp(-normed)), r.act_one)
        return carry

    lax.fori_loop(0, IMAGE_ROWS + 2, first_row, 0)
    loads.conv_first.wait()
    total = conv(r.first_w) + r.conv_biases[0:1, :]
    r.hidden[1 : IMAGE_ROWS + 1] = total.reshape(IMAGE_ROWS, W, C)
    hidden_edges = band.edges(1, r.hidden.at[1], r.hidden.at[IMAGE_ROWS], r.hidden)
    r.tile[1] = sums_tile(column_sum(total), column_sum(total * total))
    tiles = band.send_tile(1, r.tile.at[1], r.window.at[1])

    loads.caption.wait()
    loads.text_weight.wait()
    words = (dot(r.cap[...], r.text_w[...]) + r.text_bias[...]).astype(low)
    for h in range(HEADS):
        parts = [words[:, k * C + h * HEAD : k * C + (h + 1) * HEAD] for k in range(2)]
        r.own_words[h] = jnp.concatenate(parts, axis=1)
    swaps = swaps + band.swap(1, r.own_words, r.words)
    r.words[band.lane] = r.own_words[band.lane]
    for copy in tiles:
        copy.wait()
    band.wait_edges(hidden_edges)
    found.mean_two, found.scale_two = norm_of(1)

    def second_row(i, carry):
        unit = (r.hidden[i] - found.mean_two) * found.scale_two
        normed = unit * found.gain_two + found.bias_two
        shifted = normed * found.stretch + found.shift
        spread_rows(i, shifted / (1.0 + jnp.exp(-shifted)), r.act_two)
        return carry

    lax.fori_loop(0, IMAGE_ROWS + 2, second_row, 0)
    loads.conv_second.wait()
    total = conv(r.second_w) + r.conv_biases[1:2, :]
    total = total + r.img[1 : IMAGE_ROWS + 1].astype(full).reshape(IMAGE_ROWS * W, C)
    r.middle[1 : IMAGE_ROWS + 1] = total.reshape(IMAGE_ROWS, W, C)
    r.tile[2] = sums_tile(column_sum(total), column_sum(total * total))
    tiles = band.send_tile(2, r.tile.at[2], r.window.at[2])
    middle_edges = band.edges(2, r.middle.at[1], r.middle.at[IMAGE_ROWS], r.middle)

    loads.qkv_weight.wait()
    for copy in tiles:
        copy.wait()
    found.mean_three, found.scale_three = norm_of(2)
    for i in range(2):
        middle = r.middle[1 + 4 * i : 5 + 4 * i].reshape(4 * W, C)
        unit = (middle - found.mean_three) * found.scale_three
        block = slice(i * 4 * W, (i + 1) * 4 * W)
        act = (unit * found.gain_three + found.bias_three).astype(low)
        r.act_three[block, :] = act
        projected = dot(act, r.qkv_w[...])
        queries = (projected[:, 0:C] + r.qv_bias[:, 0:C]).astype(low)
        keys = projected[:, C : 2 * C].astype(low)
        values = (projected[:, 2 * C :] + r.qv_bias[:, C:]).astype(low)
        queries = queries.T
        for h in range(HEADS):
            head = slice(h * HEAD, (h + 1) * HEAD)
            r.own_queries[h, :, block] = queries[head, :]
            r.own_pairs[h, block, :] = jnp.concatenate([keys[:, head], values[:, head]], axis=1)
    swaps = swaps + band.swap(2, r.own_pairs, r.pairs)
    r.pairs[band.lane] = r.own_pairs[band.lane]
    fields = [getattr(found, name) for name in Vectors._fields]
    for i, values in enumerate(fields):
        r.vectors[i : i + 1, :] = values
    r.vectors[len(fields) : VECTOR_ROWS, :] = jnp.zeros((VECTOR_ROWS - len(fields), C), full)
    for b in range(SPAN):
        r.vectors[VECTOR_ROWS + b : VECTOR_ROWS + b + 1, :] = masks[b]
    band.wait_edges(middle_edges)
    for copy in swaps:
        copy.wait()


def front(ident, items, inputs, anywhere):
    low, full = jnp.bfloat16, jnp.float32
    pixels = IMAGE_ROWS * W
    padded = (IMAGE_ROWS + 2, W, C)
    outs = dict(
        pairs=((HEADS, pixels, 2 * HEAD), low),
        own_queries=((HEADS, HEAD, pixels), low),
        upstream=((HEADS, HEAD, pixels), low),
        words=((HEADS, TEXT, 2 * HEAD), low),
        act_one=((pixels + 2 * W, C), low),
        act_two=((pixels + 2 * W, C), low),
        act_three=((pixels, C), low),
        hidden=(padded, full),
        middle=(padded, full),
        vectors=((VECTOR_ROWS + SPAN, C), full),
    )
    scratch = dict(
        img=(padded, low),
        up=((pixels, C), low),
        cap=((TEXT, EMB), low),
        first_w=((9 * C, C), low),
        second_w=((9 * C, C), low),
        embed_w=((EMB, 2 * C), low),
        text_w=((EMB, 2 * C), low),
        qkv_w=((C, 3 * C), low),
        proj_w=((C, C), low),
        shifts=((3,) + padded, low),
        blocks=((C, C), low),
        tile=((3, 8, C // 4), full),
        window=((3, SPAN, 8, C // 4), full),
        own_pairs=((HEADS, pixels, 2 * HEAD), low),
        own_upstream=((HEADS, HEAD, pixels), low),
        own_words=((HEADS, TEXT, 2 * HEAD), low),
    )
    semaphores = dict(
        load_sem=(9,),
        edge_send=(3, 2),
        edge_recv=(3, 2),
        tile_send=(3, SPAN),
        tile_recv=(3, SPAN),
        swap_send=(3, SPAN),
        swap_recv=(3, SPAN),
    )
    return call_named(
        front_kernel, ident, dict(items=items), inputs, anywhere, outs, scratch, semaphores
    )


def hand_over_kernel(count, *refs):
    sources, targets, held = refs[:count], refs[count : 2 * count], refs[2 * count : 3 * count]
    load_sem, store_sem = refs[3 * count :]
    loads = [
        pltpu.make_async_copy(source, buffer, load_sem.at[k])
        for k, (source, buffer) in enumerate(zip(sources, held))
    ]
    stores = [
        pltpu.make_async_copy(buffer, target, store_sem.at[k])
        for k, (buffer, target) in enumerate(zip(held, targets))
    ]
    for copy in loads:
        copy.start()
    for load, store in zip(loads, stores):
        load.wait()
        store.start()
    for copy in stores:
        copy.wait()


def hand_over(arrays):
    anywhere = pl.BlockSpec(memory_space=pl.ANY)
    count = len(arrays)
    return pl.pallas_call(
        functools.partial(hand_over_kernel, count),
        out_shape=tuple(jax.ShapeDtypeStruct(a.shape, a.dtype) for a in arrays),
        in_specs=[anywhere] * count,
        out_specs=(anywhere,) * count,
        scratch_shapes=[pltpu.VMEM(a.shape, a.dtype) for a in arrays]
        + [pltpu.SemaphoreType.DMA((count,))] * 2,
        name=hand_over.__name__,
    )(*arrays)


def blocks_of(rows):
    return rows.reshape(rows.shape[0], NORM_GROUPS, -1)


def spread(values):
    return jnp.repeat(values, C // NORM_GROUPS)


def in_halves(
    image,
    embedding,
    caption,
    item_of_band,
    out_grad,
    norm_gains,
    norm_biases,
    conv_first,
    conv_second,
    conv_biases,
    embed_weight,
    embed_bias,
    qkv_weight,
    qv_bias,
    text_weight,
    text_bias,
    proj_weight,
    proj_bias,
):
    low = jnp.bfloat16
    pixels = image.shape[1]
    position = lax.axis_index(ROWS)
    items = item_of_band[0]
    slots = items.shape[0]
    by_row = (-1, W, C)
    ahead = front(
        0,
        items,
        dict(
            embedding=embedding[0],
            norm_gains=norm_gains,
            norm_biases=norm_biases,
            conv_biases=conv_biases,
            embed_bias=embed_bias[None],
            qv_bias=qv_bias[None],
            text_bias=text_bias[None],
            proj_bias=proj_bias[None],
        ),
        dict(
            image=image.reshape(by_row),
            conv_first=conv_first,
            embed_weight=embed_weight,
            upstream_pixels=out_grad[0],
            proj_weight=proj_weight,
            conv_second=conv_second,
            caption=caption[0, 0],
            text_weight=text_weight,
            qkv_weight=qkv_weight,
        ),
    )
    found = attend(2, items, ahead, caption[0, 0])
    slot_of_band = (jnp.arange(slots)[:, None] == items[None, :]).astype(jnp.float32)
    row_share = EMB // lax.axis_size(ROWS)
    share = lax.dynamic_slice_in_dim(embedding[0], position * row_share, row_share, 1)
    silu_share = jax.nn.silu(share.astype(jnp.float32)).astype(low)
    out = back(
        1,
        ahead.vectors,
        jnp.repeat(slot_of_band, 128, axis=1),
        silu_share,
        embedding[0],
        dict(
            outcome=found.outcome,
            pair_grads=found.pair_grads,
            word_grads=found.word_grads,
            middle=ahead.middle,
            qkv_weight=qkv_weight,
            proj_weight=proj_weight,
            upstream=out_grad[0],
            act_three=ahead.act_three,
            caption=caption[0, 0],
            conv_second=conv_second,
            conv_first=conv_first,
            hidden=ahead.hidden,
            act_two=ahead.act_two,
            act_one=ahead.act_one,
            far_caption=found.far_caption,
            far_act_one=found.far_act_one,
            far_act_two=found.far_act_two,
            image=image.reshape(by_row),
            text_weight=text_weight,
            embed_weight=embed_weight,
        ),
    )
    out = types.SimpleNamespace(**dict(zip(vars(out), hand_over(list(vars(out).values())))))
    return (
        out.result[None],
        out.image_grad.reshape(1, pixels, C),
        out.embedding_grad[None],
        out.caption_grad[None, None],
        out.norm_gains_grad,
        out.norm_biases_grad,
        out.conv_first_grad,
        out.conv_second_grad,
        out.conv_biases_grad,
        out.embed_weight_grad,
        out.embed_bias_grad.reshape(-1),
        out.qkv_grad,
        out.qv_bias_grad.reshape(-1),
        out.text_grad,
        out.text_bias_grad.reshape(-1),
        out.proj_grad,
        out.proj_bias_grad.reshape(-1),
    )


def shards(
    image,
    embedding,
    caption,
    item_of_band,
    out_grad,
    norm_gains,
    norm_biases,
    conv_first,
    conv_second,
    conv_biases,
    embed_weight,
    embed_bias,
    qkv_weight,
    qv_bias,
    text_weight,
    text_bias,
    proj_weight,
    proj_bias,
):
    low = jnp.bfloat16
    full = jnp.float32
    pixels = image.shape[1]
    band_items = item_of_band[0]
    slots = band_items.shape[0]
    if slots == 2 * SPAN and lax.axis_size(ITEMS) == 2 and HEADS == SPAN:
        return in_halves(
            image,
            embedding,
            caption,
            item_of_band,
            out_grad,
            norm_gains,
            norm_biases,
            conv_first,
            conv_second,
            conv_biases,
            embed_weight,
            embed_bias,
            qkv_weight,
            qv_bias,
            text_weight,
            text_bias,
            proj_weight,
            proj_bias,
        )
    position = lax.axis_index(ROWS)
    my_item = band_items[position]
    slot_hot = (jnp.arange(slots) == my_item).astype(full)
    item_count = jnp.sum((band_items == my_item).astype(full)) * pixels * (C // NORM_GROUPS)
    reach = position + jnp.arange(-REACH, REACH + 1)
    near = (reach >= 0) & (reach < slots)
    near = near & (band_items[jnp.clip(reach, 0, slots - 1)] == my_item)
    keep = jnp.concatenate(
        [
            jnp.full((W, 1), near[REACH - 1]),
            jnp.full((pixels, 1), True),
            jnp.full((W, 1), near[REACH + 1]),
        ]
    )
    own_lead = jnp.logical_not(near[REACH - 1])

    def totals(ident, first, second, edges=None):
        sums = jnp.stack([jnp.sum(blocks_of(first), axis=(0, 2)), jnp.sum(blocks_of(second), axis=(0, 2))])
        tile = jnp.pad(sums, ((0, 6), (0, 128 - NORM_GROUPS)))
        if edges is not None:
            outcome = exchange(ident, slots, tile, (edges[:W], edges[-W:]))
        else:
            outcome = exchange(ident, slots, tile)
        summed = jnp.sum(jnp.where(near[:, None, None], outcome[0], 0.0), axis=0)
        summed = summed[:2, :NORM_GROUPS] / item_count
        return summed, outcome[1:]

    def stats(summed):
        scales = lax.rsqrt(summed[1] - summed[0] * summed[0] + epsilon)
        return spread(summed[0]), spread(scales)

    inputs = image[0].astype(full)
    summed, (above, below) = totals(0, inputs, inputs * inputs, image[0])
    means_one, scales_one = stats(summed)
    padded = jnp.concatenate([above, image[0], below]).astype(full)
    unit_padded = (padded - means_one) * scales_one
    normed_padded = unit_padded * norm_gains[0] + norm_biases[0]
    act_one_padded = jnp.where(keep, jax.nn.silu(normed_padded), 0.0).astype(low)
    unit_one = unit_padded[W:-W]
    normed_one = normed_padded[W:-W]
    taps_one = jnp.concatenate(taps_of(act_one_padded, False), axis=1)
    hidden_one = dot(taps_one, conv_first) + conv_biases[0]
    embed_silu = jax.nn.silu(embedding[0].astype(full)).astype(low)
    my_silu = dot(slot_hot.astype(low)[None], embed_silu).astype(low)
    modulation = dot(my_silu, embed_weight)[0] + embed_bias
    scale_part = modulation[:C]
    shift_part = modulation[C:]
    summed, (above, below) = totals(1, hidden_one, hidden_one * hidden_one, hidden_one)
    means_two, scales_two = stats(summed)
    hidden_padded = jnp.concatenate([above, hidden_one, below])
    unit_padded = (hidden_padded - means_two) * scales_two
    normed_padded = unit_padded * norm_gains[1] + norm_biases[1]
    shifted_padded = normed_padded * (1.0 + scale_part) + shift_part
    act_two_padded = jnp.where(keep, jax.nn.silu(shifted_padded), 0.0).astype(low)
    unit_two = unit_padded[W:-W]
    normed_two = normed_padded[W:-W]
    shifted = shifted_padded[W:-W]
    taps_two = jnp.concatenate(taps_of(act_two_padded, False), axis=1)
    middle = inputs + dot(taps_two, conv_second) + conv_biases[1]
    summed, _ = totals(2, middle, middle * middle)
    means_three, scales_three = stats(summed)
    unit_three = (middle - means_three) * scales_three
    act_three = (unit_three * norm_gains[2] + norm_biases[2]).astype(low)
    projected = dot(act_three, qkv_weight)
    queries = (projected[:, :C] + qv_bias[:C]).astype(low)
    keys_values = jnp.concatenate(
        [projected[:, C : 2 * C], projected[:, 2 * C :] + qv_bias[C:]], axis=1
    ).astype(low)
    captions = caption[0, 0]
    text_kv = lax.cond(
        own_lead,
        lambda: (dot(captions, text_weight) + text_bias).astype(low),
        lambda: jnp.zeros((TEXT, 2 * C), low),
    )
    upstream = out_grad[0]
    upstream_float = upstream.astype(full)
    attended_grad = dot_last(upstream, proj_weight).astype(low)
    group = lax.axis_index(ITEMS)
    groups = lax.axis_size(ITEMS)
    attended_low, query_low, key_value_low, text_low = attention_by_band(
        band_items, position, queries, keys_values, text_kv, attended_grad
    )
    result = middle + dot(attended_low, proj_weight) + proj_bias
    proj_weight_grad = dot_first(attended_low, upstream)
    proj_bias_grad = jnp.sum(upstream_float, axis=0)
    qkv_grad = jnp.concatenate([query_low, key_value_low], axis=1)
    qkv_weight_grad = dot_first(act_three, qkv_grad)
    qv_bias_grad = jnp.sum(
        jnp.concatenate([query_low, key_value_low[:, C:]], axis=1).astype(full), axis=0
    )
    text_weight_grad = dot_first(captions, text_low)
    text_bias_grad = jnp.sum(text_low.astype(full), axis=0)
    caption_grad = dot_last(text_low, text_weight)[None, None]
    three_grad = dot_last(qkv_grad, qkv_weight)
    gain_three = jnp.sum(three_grad * unit_three, axis=0)
    bias_three = jnp.sum(three_grad, axis=0)

    def conv_back(padded, weight):
        views = jnp.stack(taps_of(padded, True))
        return jnp.einsum(
            "tpd,tcd->pc", views, weight.reshape(9, C, C), preferred_element_type=full
        )

    def norm_back(ident, grad_unit, unit_value, scales, base, with_edges=True):
        scaled = base + grad_unit * scales
        edges = jnp.concatenate([scaled, unit_value], axis=1) if with_edges else None
        summed, around = totals(ident, grad_unit, grad_unit * unit_value, edges)
        mean_grad, mean_cross = spread(summed[0]) * scales, spread(summed[1]) * scales
        if not with_edges:
            return scaled - mean_grad - unit_value * mean_cross
        both = jnp.concatenate([around[0], edges, around[1]])
        return both[:, :C] - mean_grad - both[:, C:] * mean_cross

    middle_padded = norm_back(3, three_grad * norm_gains[2], unit_three, scales_three, upstream_float)
    middle_grad = middle_padded[W:-W]
    low_padded = jnp.where(keep, middle_padded, 0.0).astype(low)
    hidden_two_low = low_padded[W:-W]
    conv_bias_two = jnp.sum(hidden_two_low.astype(full), axis=0)
    conv_second_grad = dot_first(taps_two, hidden_two_low)
    act_two_grad = conv_back(low_padded, conv_second)
    shifted_grad = act_two_grad * silu_slope(shifted)
    modulation_grad = jnp.concatenate(
        [jnp.sum(shifted_grad * normed_two, axis=0), jnp.sum(shifted_grad, axis=0)]
    )
    normed_two_grad = shifted_grad * (1.0 + scale_part)
    gain_two = jnp.sum(normed_two_grad * unit_two, axis=0)
    bias_two = jnp.sum(normed_two_grad, axis=0)
    hidden_back = norm_back(4, normed_two_grad * norm_gains[1], unit_two, scales_two, 0.0)
    low_padded = jnp.where(keep, hidden_back, 0.0).astype(low)
    hidden_one_low = low_padded[W:-W]
    conv_bias_one = jnp.sum(hidden_one_low.astype(full), axis=0)
    conv_first_grad = dot_first(taps_one, hidden_one_low)
    act_one_grad = conv_back(low_padded, conv_first)
    normed_one_grad = act_one_grad * silu_slope(normed_one)
    gain_one = jnp.sum(normed_one_grad * unit_one, axis=0)
    bias_one = jnp.sum(normed_one_grad, axis=0)
    image_grad = norm_back(
        5, normed_one_grad * norm_gains[0], unit_one, scales_one, middle_grad, False
    )
    group_hot = (jnp.arange(groups) == group).astype(full)
    tables = group_hot[:, None, None] * slot_hot[None, :, None] * modulation_grad
    vectors = jnp.concatenate(
        [
            gain_one,
            gain_two,
            gain_three,
            bias_one,
            bias_two,
            bias_three,
            conv_bias_one,
            conv_bias_two,
            qv_bias_grad,
            text_bias_grad,
            proj_bias_grad,
        ]
    )
    small = jnp.concatenate([tables.reshape(-1, C), vectors.reshape(-1, C)])
    row_share = EMB // lax.axis_size(ROWS)
    silu_share = lax.dynamic_slice_in_dim(embed_silu, position * row_share, row_share, 1)
    grads = (conv_first_grad, conv_second_grad, qkv_weight_grad, text_weight_grad, proj_weight_grad)
    grads = [g.astype(low) for g in grads]
    small = lax.psum(small.astype(low), (ROWS, ITEMS)).astype(full)
    tables_sum = small[: groups * slots * 2].reshape(groups, slots, 2 * C).astype(low)
    part = dot_first(silu_share, jnp.take(tables_sum, group, axis=0)).astype(low)
    matrices = [lax.psum_scatter(g, ROWS, scatter_dimension=0, tiled=True) for g in grads]
    *matrices, embed_weight_grad = [
        lax.psum(m, ITEMS).astype(full) for m in matrices + [part]
    ]
    vectors_sum = small[groups * slots * 2 :]
    modulation_low = jnp.take(tables_sum, group, axis=0)
    embed_bias_grad = jnp.sum(tables_sum.astype(full), axis=(0, 1))
    embedding_grad = dot_last(modulation_low, embed_weight) * silu_slope(embedding[0].astype(full))
    return (
        result.astype(low)[None],
        image_grad[None],
        embedding_grad[None],
        caption_grad,
        vectors_sum[0:3],
        vectors_sum[3:6],
        matrices[0],
        matrices[1],
        vectors_sum[6:8],
        embed_weight_grad,
        embed_bias_grad,
        matrices[2],
        vectors_sum[8:10].reshape(-1),
        matrices[3],
        vectors_sum[10:12].reshape(-1),
        matrices[4],
        vectors_sum[12],
    )


def solution(mesh):
    in_specs = (
        P(ITEMS, ROWS, None),
        P(ITEMS, None, None),
        P(ITEMS, ROWS, None, None),
        P(ITEMS, None),
        P(ITEMS, ROWS, None),
        P(),
        P(),
        P(),
        P(),
        P(),
        P(),
        P(),
        P(),
        P(),
        P(),
        P(),
        P(),
        P(),
    )
    out_specs = (
        P(ITEMS, ROWS, None),
        P(ITEMS, ROWS, None),
        P(ITEMS, None, None),
        P(ITEMS, ROWS, None, None),
        P(),
        P(),
        P(ROWS, None),
        P(ROWS, None),
        P(),
        P(ROWS, None),
        P(),
        P(ROWS, None),
        P(),
        P(ROWS, None),
        P(),
        P(ROWS, None),
        P(),
    )
    return jax.shard_map(shards, mesh=mesh, in_specs=in_specs, out_specs=out_specs, check_vma=False)
```

```python
import functools
import types
import typing

import jax
import jax.numpy as jnp
from jax import lax
from jax.experimental import pallas as pl
from jax.experimental.pallas import tpu as pltpu
from jax.sharding import PartitionSpec as P

C = 512
HEADS = 8
HEAD = 64
EMB = 2048
TEXT = 128
NORM_GROUPS = 32
W = 64
SPAN = 8
ROWS, ITEMS = "rows", "items"


epsilon = 1e-05


def from_behind(array, axis, by):
    length = lax.axis_size(axis)
    pairs = [(i, i + by) for i in range(length) if 0 <= i + by < length]
    return lax.ppermute(array, axis, pairs)


def as_sent(array):
    return jax.tree.map(lambda a: a.astype(jnp.bfloat16) if a.dtype == jnp.float32 else a, array)


def keep_state(state):
    return state


def silu_slope(source):
    sigma = jax.nn.sigmoid(source)
    return sigma * (1.0 + source * (1.0 - sigma))


def dot_first(left_side, right_side):
    return lax.dot_general(
        left_side, right_side, (((0,), (0,)), ((), ())), preferred_element_type=jnp.float32
    )


def dot_last(left_side, right_side):
    return lax.dot_general(
        left_side, right_side, (((1,), (1,)), ((), ())), preferred_element_type=jnp.float32
    )


def head_split(source):
    return source.reshape(source.shape[0], HEADS, HEAD)


def piece_scores(query_heads, key_piece, allowed):
    key_heads = head_split(key_piece[:, :C])
    scores = jnp.einsum(
        "qhd,khd->hqk", query_heads, key_heads, preferred_element_type=jnp.float32
    ) * HEAD ** (-0.5)
    return jnp.where(allowed[None, None, :], scores, -jnp.inf)


def piece_grads(query_heads, grad_heads, log_total, row_dots, key_piece, allowed):
    scores = piece_scores(query_heads, key_piece, allowed)
    weights = jnp.exp(scores - log_total[:, :, None])
    value_heads = head_split(key_piece[:, C:])
    weight_grad = jnp.einsum(
        "qhd,khd->hqk", grad_heads, value_heads, preferred_element_type=jnp.float32
    )
    score_grad = (weights * (weight_grad - row_dots[:, :, None])).astype(jnp.bfloat16)
    outcome = []
    key_heads = head_split(key_piece[:, :C])
    query_grad = jnp.einsum(
        "hqk,khd->qhd", score_grad, key_heads, preferred_element_type=jnp.float32
    ) * HEAD ** (-0.5)
    outcome.append(query_grad.reshape(query_grad.shape[0], C))
    key_grad = jnp.einsum(
        "hqk,qhd->khd", score_grad, query_heads, preferred_element_type=jnp.float32
    ) * HEAD ** (-0.5)
    value_grad = jnp.einsum(
        "hqk,qhd->khd", weights.astype(jnp.bfloat16), grad_heads, preferred_element_type=jnp.float32
    )
    outcome.append(jnp.concatenate([key_grad.reshape(-1, C), value_grad.reshape(-1, C)], axis=1))
    return tuple(outcome)


def source_masks(band_items, source, my_item, pixels):
    slots = band_items.shape[0]
    inside = (source >= 0) & (source < slots)
    clipped = jnp.clip(source, 0, slots - 1)
    source_item = band_items[clipped]
    before_item = band_items[jnp.maximum(clipped - 1, 0)]
    same_item = inside & (source_item == my_item)
    leading = same_item & ((clipped == 0) | (before_item != source_item))
    allowed = jnp.concatenate(
        [jnp.broadcast_to(same_item, (pixels,)), jnp.broadcast_to(leading, (TEXT,))]
    )
    return (allowed, same_item)


REACH = SPAN - 1
LOG2E = 1.4426950408889634
FAR_ABOVE = 1e30
PIX = 512


def dot(left, right):
    return jnp.dot(left, right, preferred_element_type=jnp.float32)


def reach_of(here, slots):
    first = here < SPAN
    low = jnp.maximum(jnp.where(first, 0, SPAN), here - REACH)
    high = jnp.minimum(jnp.where(first, SPAN - 1, slots - 1), here + REACH)
    return low, high


def exchange_kernel(slots, with_edges, *refs):
    if with_edges:
        tile, top, bottom, window, above, below, send_sem, recv_sem, edge_send, edge_recv = refs
    else:
        tile, window, send_sem, recv_sem = refs
    here = lax.axis_index(ROWS)
    low, high = reach_of(here, slots)
    offsets = [o for o in range(-REACH, REACH + 1) if o != 0]

    def reached(offset):
        return (here + offset >= low) & (here + offset <= high)

    barrier = pltpu.get_barrier_semaphore()
    for o in offsets:

        @pl.when(reached(o))
        def _(o=o):
            pl.semaphore_signal(barrier, 1, device_id={ROWS: here + o})

    pl.semaphore_wait(barrier, high - low)

    def edge_copy(o):
        source, target, k = (top, below, 0) if o < 0 else (bottom, above, 1)
        return pltpu.make_async_remote_copy(
            source, target, edge_send.at[k], edge_recv.at[k], device_id={ROWS: here + o}
        )

    def tile_copy(o):
        return pltpu.make_async_remote_copy(
            tile,
            window.at[REACH - o],
            send_sem.at[REACH - o],
            recv_sem.at[REACH - o],
            device_id={ROWS: here + o},
        )

    if with_edges:
        for o in (-1, 1):

            @pl.when(reached(o))
            def _(o=o):
                edge_copy(o).start()

    for o in offsets:

        @pl.when(reached(o))
        def _(o=o):
            tile_copy(o).start()

        @pl.when(jnp.logical_not(reached(-o)))
        def _(o=o):
            window[REACH - o] = jnp.zeros_like(tile)

    window[REACH] = tile[...]
    if with_edges:

        @pl.when(jnp.logical_not(reached(-1)))
        def _():
            above[...] = jnp.zeros_like(above)

        @pl.when(jnp.logical_not(reached(1)))
        def _():
            below[...] = jnp.zeros_like(below)

    for o in offsets:

        @pl.when(reached(o))
        def _(o=o):
            tile_copy(o).wait_send()

        @pl.when(reached(-o))
        def _(o=o):
            tile_copy(o).wait_recv()

    if with_edges:
        for o in (-1, 1):

            @pl.when(reached(o))
            def _(o=o):
                edge_copy(o).wait_send()

            @pl.when(reached(-o))
            def _(o=o):
                edge_copy(o).wait_recv()


def exchange(ident, slots, tile, edges=None):
    vmem = pl.BlockSpec(memory_space=pltpu.VMEM)
    shapes = [jax.ShapeDtypeStruct((2 * REACH + 1,) + tile.shape, tile.dtype)]
    scratch = [pltpu.SemaphoreType.DMA((2 * REACH + 1,))] * 2
    operands = [tile]
    if edges is not None:
        shapes += [jax.ShapeDtypeStruct(e.shape, e.dtype) for e in edges]
        scratch += [pltpu.SemaphoreType.DMA((2,))] * 2
        operands += list(edges)
    return pl.pallas_call(
        functools.partial(exchange_kernel, slots, edges is not None),
        out_shape=tuple(shapes),
        in_specs=[vmem] * len(operands),
        out_specs=(vmem,) * len(shapes),
        scratch_shapes=scratch,
        compiler_params=pltpu.CompilerParams(collective_id=ident, has_side_effects=True),
        name=f"exchange_{ident}",
    )(*operands)


def attention_by_band(band_items, position, queries, keys_values, text_kv, attended_grad):
    my_item = band_items[position]
    pixels = queries.shape[0]
    own_allowed, own_same = source_masks(band_items, position, my_item, pixels)
    packed = jnp.concatenate([keys_values, text_kv], axis=0)
    pieces = [(0, packed, own_allowed, own_same)]
    for distance in range(1, SPAN):
        for offset in (distance, -distance):
            arrived = from_behind(packed, ROWS, offset)
            allowed, same_item = source_masks(band_items, position - offset, my_item, pixels)
            pieces.append((offset, arrived, allowed, same_item))
    query_heads = head_split(queries)
    row_top = jnp.full((HEADS, pixels), -jnp.inf, jnp.float32)
    weight_sum = jnp.zeros((HEADS, pixels), jnp.float32)
    for offset, key_piece, allowed, same_item in pieces:

        def gather_scores(state, key_piece=key_piece, allowed=allowed):
            top_old, sum_old = state
            scores = piece_scores(query_heads, key_piece, allowed)
            top_new = jnp.maximum(top_old, jnp.max(scores, axis=2))
            sum_new = sum_old * jnp.exp(top_old - top_new) + jnp.sum(
                jnp.exp(scores - top_new[:, :, None]), axis=2
            )
            return (top_new, sum_new)

        row_top, weight_sum = lax.cond(same_item, gather_scores, keep_state, (row_top, weight_sum))
    log_total = row_top + jnp.log(weight_sum)
    attended = jnp.zeros((pixels, HEADS, HEAD), jnp.float32)
    for offset, key_piece, allowed, same_item in pieces:

        def add_values(totals, key_piece=key_piece, allowed=allowed):
            scores = piece_scores(query_heads, key_piece, allowed)
            weights = jnp.exp(scores - log_total[:, :, None]).astype(jnp.bfloat16)
            return totals + jnp.einsum(
                "hqk,khd->qhd",
                weights,
                head_split(key_piece[:, C:]),
                preferred_element_type=jnp.float32,
            )

        attended = lax.cond(same_item, add_values, keep_state, attended)
    attended_flat = attended.reshape(pixels, C)
    row_dots = jnp.sum(
        (attended_grad.astype(jnp.float32) * attended_flat).reshape(pixels, HEADS, HEAD), axis=2
    ).T
    grad_heads = head_split(attended_grad)
    query_grad = jnp.zeros((pixels, C), jnp.float32)
    packed_grad = jnp.zeros((pixels + TEXT, 2 * C), jnp.float32)
    zero_piece = jnp.zeros((pixels + TEXT, 2 * C), jnp.float32)
    for offset, key_piece, allowed, same_item in pieces:

        def grad_both(totals, key_piece=key_piece, allowed=allowed):
            outcome = piece_grads(query_heads, grad_heads, log_total, row_dots, key_piece, allowed)
            return (totals + outcome[0], outcome[1])

        def grad_none(totals):
            return (totals, zero_piece)

        query_grad, piece_grad = lax.cond(same_item, grad_both, grad_none, query_grad)
        if offset == 0:
            packed_grad = packed_grad + piece_grad
        else:
            packed_grad = packed_grad + from_behind(
                as_sent(piece_grad), ROWS, -offset
            ).astype(jnp.float32)
    packed_low = packed_grad.astype(jnp.bfloat16)
    return (
        attended_flat.astype(jnp.bfloat16),
        query_grad.astype(jnp.bfloat16),
        packed_low[:pixels],
        packed_low[pixels:],
    )


def taps_of(rows, reverse):
    padded = rows.reshape(-1, W, rows.shape[1])
    row_list = [padded[:-2], padded[1:-1], padded[2:]]
    if reverse:
        row_list = row_list[::-1]
    zero_column = jnp.zeros_like(row_list[0][:, :1])
    views = []
    for row_view in row_list:
        left_view = jnp.concatenate([zero_column, row_view[:, :-1]], axis=1)
        right_view = jnp.concatenate([row_view[:, 1:], zero_column], axis=1)
        view_list = [left_view, row_view, right_view]
        if reverse:
            view_list = view_list[::-1]
        views = views + view_list
    return [view.reshape(-1, rows.shape[1]) for view in views]


class Vectors(typing.NamedTuple):
    mean_one: jax.Array
    scale_one: jax.Array
    gain_one: jax.Array
    bias_one: jax.Array
    mean_two: jax.Array
    scale_two: jax.Array
    gain_two: jax.Array
    bias_two: jax.Array
    mean_three: jax.Array
    scale_three: jax.Array
    gain_three: jax.Array
    bias_three: jax.Array
    stretch: jax.Array
    shift: jax.Array
    proj_bias: jax.Array
    keep_above: jax.Array
    keep_below: jax.Array
    per_item: jax.Array


def grouped(names, refs):
    found, position = types.SimpleNamespace(), 0
    for name, count in names:
        if count is None:
            setattr(found, name, refs[position])
            position += 1
        else:
            setattr(found, name, refs[position : position + count])
            position += count
    return found


def call_named(
    kernel, ident, scalars, inputs, anywhere, outs, scratch, semaphores, far=types.MappingProxyType({})
):
    names = [(name, None) for name in [*scalars, *inputs, *anywhere, *outs, *far]]
    buffers = []
    for name, entry in scratch.items():
        many = isinstance(entry, list)
        names.append((name, len(entry) if many else None))
        buffers += [pltpu.VMEM(*e) for e in (entry if many else [entry])]
    names += [(name, None) for name in semaphores]
    vmem = pl.BlockSpec(memory_space=pltpu.VMEM)
    outcome = pl.pallas_call(
        functools.partial(kernel, names),
        out_shape=tuple(jax.ShapeDtypeStruct(*o) for o in [*outs.values(), *far.values()]),
        in_specs=[pl.BlockSpec(memory_space=pltpu.SMEM)] * len(scalars)
        + [vmem] * len(inputs)
        + [pl.BlockSpec(memory_space=pl.ANY)] * len(anywhere),
        out_specs=(vmem,) * len(outs) + (pl.BlockSpec(memory_space=pl.ANY),) * len(far),
        scratch_shapes=buffers + [pltpu.SemaphoreType.DMA(s) for s in semaphores.values()],
        compiler_params=pltpu.CompilerParams(
            collective_id=ident, has_side_effects=True, vmem_limit_bytes=60 << 20
        ),
        name=kernel.__name__,
    )(*[v for group in (scalars, inputs, anywhere) for v in dict(group).values()])
    return types.SimpleNamespace(**dict(zip([*outs, *far], outcome)))


VECTOR_ROWS = 24
FAR, NEAR, SIDE, CORE, GROUP = range(5)
CROSS = (FAR, NEAR, SIDE)
GROUP_FIRST = (GROUP, SIDE, NEAR, FAR)
STREAMS = (
    (144, C // 4, (SIDE, NEAR, FAR)),
    (144, C // 4, (NEAR, SIDE, FAR)),
    (144, C // 4, (SIDE, NEAR, FAR)),
    (144, C // 4, (NEAR, SIDE, FAR)),
    (64, C // 2, (SIDE, NEAR, FAR)),
    (64, C // 2, (NEAR, SIDE, FAR)),
    (16, 3 * C // 2, GROUP_FIRST),
    (16, C // 2, GROUP_FIRST),
)
FIRST_CONV, SECOND_CONV, WORDS, QKV, PROJ = 0, 2, 4, 6, 7
FIRST_LANDING = [sum(len(s[2]) for s in STREAMS[:k]) for k in range(len(STREAMS))]
HALF_SUMS, GROUP_SUMS = -1, -2
TAIL = (2, 3, 6, 0, 1, 4, 5, -1, 2, 3, 0, 1, 6, -2, 2, 3, 0, 1, 0, 1)
IMAGE_ROWS = 8


class Band:
    def __init__(self, r):
        self.r = r
        self.row = lax.axis_index(ROWS)
        self.group = lax.axis_index(ITEMS)
        self.lane = self.row % SPAN
        self.base = self.row - self.lane
        row = self.row
        self.place = [row // 8, (row // 4) % 2, (row // 2) % 2, row % 2, self.group]
        self.partner = [
            {ROWS: row + (1 - 2 * self.place[d]) * (8 >> d)} for d in range(CORE + 1)
        ]
        self.partner.append({ITEMS: 1 - self.group})
        self.others = [(self.lane + o) % SPAN for o in range(1, SPAN)]
        self.peers = [{ROWS: self.base + other} for other in self.others]
        self.has_above, self.has_below = self.lane > 0, self.lane < SPAN - 1

    def meet(self, further=()):
        barrier = pltpu.get_barrier_semaphore()
        targets = self.peers + list(further)
        for target in targets:
            pl.semaphore_signal(barrier, 1, device_id=target)
        pl.semaphore_wait(barrier, len(targets))

    def remote(self, source, target, send, recv, device):
        return pltpu.make_async_remote_copy(source, target, send, recv, device_id=device)

    def edges(self, k, top, bottom, target):
        r = self.r
        up = self.remote(
            top,
            target.at[IMAGE_ROWS + 1],
            r.edge_send.at[k, 0],
            r.edge_recv.at[k, 0],
            {ROWS: self.row - 1},
        )
        down = self.remote(
            bottom,
            target.at[0],
            r.edge_send.at[k, 1],
            r.edge_recv.at[k, 1],
            {ROWS: self.row + 1},
        )
        pl.when(self.has_above)(up.start)
        pl.when(self.has_below)(down.start)
        return up, down

    def wait_edges(self, pair):
        up, down = pair

        @pl.when(self.has_above)
        def _():
            up.wait_send()
            down.wait_recv()

        @pl.when(self.has_below)
        def _():
            down.wait_send()
            up.wait_recv()

    def zero_edges(self, target):
        @pl.when(jnp.logical_not(self.has_above))
        def _():
            target[0] = jnp.zeros(target.shape[1:], target.dtype)

        @pl.when(jnp.logical_not(self.has_below))
        def _():
            target[IMAGE_ROWS + 1] = jnp.zeros(target.shape[1:], target.dtype)

    def send_tile(self, k, source, target):
        r = self.r
        copies = []
        for o in range(1, SPAN):
            copies.append(
                self.remote(
                    source,
                    target.at[self.lane],
                    r.tile_send.at[k, o],
                    r.tile_recv.at[k, o],
                    self.peers[o - 1],
                )
            )
        for copy in copies:
            copy.start()
        target[self.lane] = source[...]
        return copies

    def swap(self, k, source, target, order=range(1, SPAN)):
        r = self.r
        copies = []
        for o in order:
            copies.append(
                self.remote(
                    source.at[self.others[o - 1]],
                    target.at[self.lane],
                    r.swap_send.at[k, o],
                    r.swap_recv.at[k, o],
                    self.peers[o - 1],
                )
            )
            copies[-1].start()
        return copies

    def fill_blocks(self):
        rows = lax.broadcasted_iota(jnp.int32, (C, C), 0) // (C // NORM_GROUPS)
        columns = lax.broadcasted_iota(jnp.int32, (C, C), 1) // (C // NORM_GROUPS)
        self.r.blocks[...] = jnp.where(rows == columns, 1.0, 0.0).astype(jnp.bfloat16)

    def item_means(self, window, masks, per_item):
        low, full = jnp.bfloat16, jnp.float32
        tile = jnp.zeros((8, C // 4), full)
        for b in range(SPAN):
            tile = tile + jnp.where(masks[b][:, 0 : C // 4] > 0.0, window[b], 0.0)
        first, second = [
            jnp.concatenate([tile[j : j + 1, :] for j in range(4 * k, 4 * k + 4)], axis=1)
            for k in range(2)
        ]
        rows = lax.broadcasted_iota(jnp.int32, (8, C), 0)
        total = jnp.where(rows == 0, first, jnp.where(rows == 1, second, 0.0)) * per_item
        coarse = total.astype(low)
        rest = total - coarse.astype(full)
        finer = rest.astype(low)
        finest = (rest - finer.astype(full)).astype(low)
        blocks = self.r.blocks[...]
        return dot(coarse, blocks) + dot(finer, blocks) + dot(finest, blocks)


def sums_tile(first, second):
    rows = lax.broadcasted_iota(jnp.int32, (8, C // 4), 0)
    tile = jnp.zeros((8, C // 4), jnp.float32)
    for k, values in enumerate((first, second)):
        for j in range(4):
            part = values[:, j * (C // 4) : (j + 1) * (C // 4)]
            tile = jnp.where(rows == 4 * k + j, part, tile)
    return tile


def column_sum(values):
    return jnp.sum(values, axis=0, keepdims=True)


def side_shifts(values):
    rows = lax.broadcasted_iota(jnp.int32, values.shape, 0)
    from_left = jnp.where(rows == 0, 0.0, pltpu.roll(values, 1, 0))
    from_right = jnp.where(rows == W - 1, 0.0, pltpu.roll(values, W - 1, 0))
    return from_left, from_right


def kept(i, values, vec):
    keep = jnp.where(i == 0, vec.keep_above, jnp.where(i == IMAGE_ROWS + 1, vec.keep_below, 1.0))
    return jnp.where(keep > 0.0, values, 0.0)


def back_kernel(names, *refs):
    low, full = jnp.bfloat16, jnp.float32
    r = grouped(names, refs)
    band = Band(r)
    lane, group, place, partner = band.lane, band.group, band.place, band.partner
    core = place[CORE]
    remote = band.remote
    across = {ROWS: partner[CORE][ROWS], ITEMS: 1 - group}
    band.meet((partner[FAR], partner[GROUP], across))
    quad = (partner[CORE], partner[GROUP], across)
    quarter = 2 * group + core
    quarters = (2 * group + 1 - core, 2 * (1 - group) + core, 2 * (1 - group) + 1 - core)

    def columns_of(which, size):
        return pl.ds(pl.multiple_of(which * size, size), size)

    def to_quad(kind, source, target):
        copies = [
            remote(
                source(quarters[i]), target.at[i], r.quad_send.at[kind, i], r.quad_recv.at[kind, i], quad[i]
            )
            for i in range(3)
        ]
        for copy in copies:
            copy.start()
        return copies


    swaps = band.swap(0, r.pair_grads, r.head_pairs) + band.swap(1, r.word_grads, r.head_words)

    loads = types.SimpleNamespace()

    def load(k, source, target):
        copy = pltpu.make_async_copy(source, target, r.load_sem.at[k])
        copy.start()
        return copy

    loads.outcome = load(0, r.outcome, r.heads)
    loads.pair_grads = load(1, r.pair_grads.at[lane], r.head_pairs.at[lane])
    loads.word_grads = load(14, r.word_grads.at[lane], r.head_words.at[lane])
    loads.middle = load(2, r.middle, r.mid)
    loads.qkv_weight = load(3, r.qkv_weight, r.qkv_w)
    loads.proj_weight = load(4, r.proj_weight, r.proj_w)
    loads.upstream = load(5, r.upstream, r.up)
    loads.act_three = load(6, r.act_three, r.act3)
    loads.caption = load(7, r.caption, r.caps.at[0])
    loads.far_caption = load(15, r.far_caption, r.caps.at[2])
    loads.conv_second = load(8, r.conv_second, r.conv_w)
    loads.hidden = load(9, r.hidden, r.hid)
    loads.act_two = load(10, r.act_two, r.acts_two.at[0])
    loads.far_act_two = load(16, r.far_act_two, r.acts_two.at[2])
    loads.act_one = load(11, r.act_one, r.acts_one.at[0])
    loads.far_act_one = load(17, r.far_act_one, r.acts_one.at[2])
    loads.image = load(12, r.image, r.img)
    loads.text_weight = load(13, r.text_weight, r.text_w)

    sibling = types.SimpleNamespace()

    def to_sibling(k, source, target):
        copy = remote(source, target, r.sib_send.at[k], r.sib_recv.at[k], partner[CORE])
        copy.start()
        return copy

    half = pl.ds(pl.multiple_of((1 - core) * (C // 2), C // 2), C // 2)
    sibling.upstream = to_sibling(0, r.upstream.at[:, half], r.sib_up)
    sibling.act3 = to_sibling(1, r.act_three, r.sib_act3)
    sibling.cap = to_sibling(2, r.caption, r.caps.at[1])
    sibling.far_cap = to_sibling(7, r.far_caption, r.caps.at[3])

    share_copy = remote(
        r.silu_share, r.other_share, r.small_send.at[2], r.small_recv.at[2], partner[GROUP]
    )
    share_copy.start()
    for target in (r.part_two, r.part_one):
        band.zero_edges(target)

    vec = Vectors(*[r.vectors[i : i + 1, :] for i in range(len(Vectors._fields))])
    norm_one = (vec.mean_one, vec.scale_one)
    norm_two = (vec.mean_two, vec.scale_two)
    norm_three = (vec.mean_three, vec.scale_three)

    masks = [r.vectors[VECTOR_ROWS + b : VECTOR_ROWS + b + 1, :] for b in range(SPAN)]
    band.fill_blocks()

    def item_means(window):
        return band.item_means(window, masks, vec.per_item)

    class Stream:
        def __init__(self, k):
            self.k = k
            self.order = STREAMS[k][2]
            self.dims = [FAR, NEAR, SIDE, CORE, GROUP][: len(self.order) + 1]
            self.step = 0
            self.copies = []

        def at(self, ref, d, index):
            return ref.at[(slice(None),) * self.dims.index(d) + (index,)]

        def start(self):
            self.launch(r.grads[self.k])

        def launch(self, ref):
            k, step = self.k, self.step
            if step < len(self.order):
                d = self.order[step]
                self.copies = [
                    remote(
                        self.at(ref, d, 1 - place[d]),
                        r.landings[FIRST_LANDING[k] + step],
                        r.fold_send.at[k, step],
                        r.fold_recv.at[k, step],
                        partner[d],
                    )
                ]
                self.mine = self.at(ref, d, place[d])
                self.dims.remove(d)
            else:
                if GROUP in self.order:
                    places = (r.folded[k], r.whole[k - QKV], r.whole[k - QKV])
                    self.place = core
                else:
                    places = (r.folded[k],) * 3
                    self.place = quarter
                sources = (ref.at[1 - core], ref.at[core], ref.at[1 - core])
                ends = [
                    (source, target.at[self.place], device)
                    for source, target, device in zip(sources, places, quad)
                ]
                self.copies = [
                    remote(
                        source,
                        target,
                        r.fold_send.at[k, step + i],
                        r.fold_recv.at[k, step + i],
                        device,
                    )
                    for i, (source, target, device) in enumerate(ends)
                ]
                self.mine = ref.at[core]
            for copy in self.copies:
                copy.start()

        def advance(self):
            for copy in self.copies:
                copy.wait()
            if self.step < len(self.order):
                landed, mine = r.landings[FIRST_LANDING[self.k] + self.step], self.mine
                lead = landed.shape[:-2]
                pieces = 1
                for n in lead:
                    pieces *= n

                def add(i, carry):
                    index = []
                    for n in reversed(lead):
                        index.insert(0, i % n)
                        i = i // n
                    index = tuple(index)
                    landed[index] = landed[index] + mine[index]
                    return carry

                lax.fori_loop(0, pieces, add, 0)
                self.step += 1
                self.launch(landed)
            else:
                r.folded[self.k][self.place] = self.mine[...]
                self.step += 1

    streams = [Stream(k) for k in range(len(STREAMS))]

    def advance(*order):
        for k in order:
            streams[k].advance()

    loads.outcome.wait()
    for h in range(0, HEADS, 2):
        for k in range(2):
            pair = [r.heads[h + i, :, k * HEAD : (k + 1) * HEAD] for i in range(2)]
            r.joined[:, k * C + h * HEAD : k * C + (h + 2) * HEAD] = jnp.concatenate(pair, axis=1)
    sibling.attended = to_sibling(5, r.joined.at[:, 0:C], r.sib_attended)

    def pixel_block(ref, i, count=4):
        return ref[1 + i * count : 1 + (i + 1) * count].reshape(count * W, C)

    def unit(values, norm):
        return (values - norm[0]) * norm[1]

    def mine_of(ref, start, size):
        return ref[:, pl.ds(pl.multiple_of(start, size if size % 256 else 256), size)]

    for copy in (loads.middle, loads.qkv_weight, loads.proj_weight, loads.upstream):
        copy.wait()
    up_sum = jnp.zeros((1, C), full)
    for i in range(2):
        block = slice(i * 4 * W, (i + 1) * 4 * W)
        upstream = r.up[block, :].astype(full)
        up_sum = up_sum + column_sum(upstream)
        result = pixel_block(r.mid, i) + dot(r.joined[block, 0:C], r.proj_w[...]) + vec.proj_bias
        r.result[block, :] = result.astype(low)
        grad = dot_last(r.joined[block, C : 2 * C], r.qkv_w[:, 0:C])
        r.product[i * 4 : i * 4 + 4] = grad.reshape(4, W, C)
    sibling.upstream.wait()
    sibling.attended.wait()
    grad = dot_first(r.joined[:, 0:C], mine_of(r.up, core * (C // 2), C // 2))
    grad = grad + dot_first(r.sib_attended[...], r.sib_up[...])
    r.grads[PROJ][...] = grad.astype(low).reshape(r.grads[PROJ].shape)
    streams[PROJ].start()
    query_sum = column_sum(r.joined[:, C : 2 * C].astype(full))

    for copy in (loads.pair_grads, loads.word_grads):
        copy.wait()
    for copy in swaps:
        copy.wait()
    for h in range(0, HEADS, 2):
        for k in range(2):
            lanes = slice(k * HEAD, (k + 1) * HEAD)
            pair = [r.head_pairs[h + i, :, lanes] for i in range(2)]
            first = (2 + k) * C + h * HEAD
            r.joined[:, first : first + 2 * HEAD] = jnp.concatenate(pair, axis=1)
            pair = [r.head_words[h + i, :, lanes] for i in range(2)]
            first = k * C + h * HEAD
            r.joined_words[:, first : first + 2 * HEAD] = jnp.concatenate(pair, axis=1)
    three_half = C + (1 - core) * (3 * C // 2)
    sibling.qkv = to_sibling(
        6, r.joined.at[:, pl.ds(pl.multiple_of(three_half, C // 2), 3 * C // 2)], r.sib_qkv
    )
    word_copies = to_quad(0, lambda q: r.joined_words.at[:, columns_of(q, C // 2)], r.word_parts)
    r.own_word_part[...] = r.joined_words[:, columns_of(quarter, C // 2)]
    sibling.act2 = to_sibling(3, r.act_two, r.acts_two.at[1])
    sibling.far_act2 = to_sibling(8, r.far_act_two, r.acts_two.at[3])
    sibling.act1 = to_sibling(4, r.act_one, r.acts_one.at[1])
    sibling.far_act1 = to_sibling(9, r.far_act_one, r.acts_one.at[3])

    plain = jnp.zeros((1, C), full)
    crossed = jnp.zeros((1, C), full)
    for i in range(2):
        block = slice(i * 4 * W, (i + 1) * 4 * W)
        grad = dot_last(r.joined[block, 2 * C :], r.qkv_w[:, C:])
        grad = grad + r.product[i * 4 : i * 4 + 4].reshape(4 * W, C)
        plain = plain + column_sum(grad)
        crossed = crossed + column_sum(grad * unit(pixel_block(r.mid, i), norm_three))
        part = r.up[block, :].astype(full) + grad * (vec.gain_three * vec.scale_three)
        r.part_two[1 + i * 4 : 5 + i * 4] = part.reshape(4, W, C)
    gain_three, bias_three = crossed, plain
    r.tile[0] = sums_tile(plain * vec.gain_three, crossed * vec.gain_three)
    three_edges = band.edges(0, r.part_two.at[1], r.part_two.at[IMAGE_ROWS], r.part_two)
    tiles = band.send_tile(0, r.tile.at[0], r.window.at[0])

    for copy in (sibling.act3, sibling.qkv, loads.act_three):
        copy.wait()
    for n in range(3):
        own = mine_of(r.joined, C + core * (3 * C // 2) + n * (C // 2), C // 2)
        columns = slice(n * (C // 2), (n + 1) * (C // 2))
        grad = dot_first(r.act3[...], own)
        grad = grad + dot_first(r.sib_act3[...], r.sib_qkv[:, columns])
        r.grads[QKV][:, :, :, :, :, :, columns] = grad.astype(low).reshape(2, 2, 2, 2, 2, 16, C // 2)
    streams[QKV].start()

    for copy in (sibling.cap, sibling.far_cap, loads.caption, loads.far_caption):
        copy.wait()
    for copy in word_copies:
        copy.wait()

    def text_rows(s, carry):
        columns = pl.ds(pl.multiple_of(s * 128, 128), 128)
        grad = dot_first(r.caps[0, :, columns], r.own_word_part[...])
        for i in range(3):
            grad = grad + dot_first(r.caps[i + 1, :, columns], r.word_parts[i])
        grad = grad.astype(low)
        index = (s // 8, (s // 4) % 2, (s // 2) % 2, s % 2)
        r.grads[WORDS][index] = grad[0:64]
        r.grads[WORDS + 1][index] = grad[64:128]
        return carry

    lax.fori_loop(0, 2 ** len(CROSS) * 2, text_rows, 0)
    streams[WORDS].start()
    streams[WORDS + 1].start()
    value_sum = column_sum(r.joined[:, 3 * C :].astype(full))
    word_sum = [column_sum(r.joined_words[:, k * C : (k + 1) * C].astype(full)) for k in range(2)]

    def spread_rows(i, values):
        from_left, from_right = side_shifts(values)
        r.shifts[0, i] = from_right.astype(low)
        r.shifts[1, i] = values.astype(low)
        r.shifts[2, i] = from_left.astype(low)

    def conv_back():
        total = jnp.zeros((IMAGE_ROWS * W, C), full)
        for t in range(9):
            dy, dx = t // 3, t % 3
            view = r.shifts[dx, 2 - dy : 2 - dy + IMAGE_ROWS].reshape(IMAGE_ROWS * W, C)
            total = total + dot_last(view, r.conv_w[t * C : (t + 1) * C, :])
        return total

    def gather_shifts(landing, places):
        width = C // 4

        def one_row(i, carry):
            for k in places:
                if k == 0:
                    for dx in range(3):
                        lanes = slice(dx * width, (dx + 1) * width)
                        r.sides[0, i, :, lanes] = r.shifts[dx, i + 1, :, columns_of(quarter, width)]
                    continue
                values = landing[k - 1, i].astype(full)
                from_left, from_right = side_shifts(values)
                r.sides[k, i, :, 0:width] = from_right.astype(low)
                r.sides[k, i, :, width : 2 * width] = landing[k - 1, i]
                r.sides[k, i, :, 2 * width :] = from_left.astype(low)
            return carry

        lax.fori_loop(0, IMAGE_ROWS, one_row, 0)

    def conv_grads(kind, acts, landing, arrivals):
        width = C // 4

        def products(dy, places):
            grad = jnp.zeros((C, 3 * width), full)
            for k in places:
                sides = r.sides[k].reshape(IMAGE_ROWS * W, 3 * width)
                grad = grad + dot_first(acts[k, dy * W : dy * W + IMAGE_ROWS * W, :], sides)
            return grad

        arrivals[0].wait()
        gather_shifts(landing, (0, 1))
        for dy in range(3):
            r.partial[dy] = products(dy, (0, 1))
        for copy in arrivals[1:]:
            copy.wait()
        gather_shifts(landing, (2, 3))
        for dy in range(3):
            grad = r.partial[dy] + products(dy, (2, 3))
            grad = grad.astype(low)
            for dx in range(3):
                begin = first = (dy * 3 + dx) * C
                while begin < first + C:
                    shard, within = divmod(begin, 288)
                    stream, offset = divmod(within, 144)
                    size = min(144 - offset, first + C - begin)
                    target = r.grads[kind + stream]
                    target[
                        shard // 8,
                        (shard // 4) % 2,
                        (shard // 2) % 2,
                        shard % 2,
                        offset : offset + size,
                    ] = grad[begin - first : begin - first + size, dx * width : (dx + 1) * width]
                    begin += size
        for j in range(2):
            streams[kind + j].start()

    for copy in tiles:
        copy.wait()
    band.wait_edges(three_edges)
    means = item_means(r.window.at[0])
    offset_three, slope_three = means[0:1] * vec.scale_three, means[1:2] * vec.scale_three

    def middle_row(i, bias):
        values = r.part_two[i] - offset_three - unit(r.mid[i], norm_three) * slope_three
        r.part_two[i] = values
        values = kept(i, values, vec)
        spread_rows(i, values)
        inside = jnp.where((i > 0) & (i <= IMAGE_ROWS), 1.0, 0.0)
        return bias + inside * column_sum(values.astype(low).astype(full))

    conv_bias_two = lax.fori_loop(0, IMAGE_ROWS + 2, middle_row, jnp.zeros((1, C), full))
    def center(q):
        return r.shifts.at[1, 1 : IMAGE_ROWS + 1, :, columns_of(q, C // 4)]

    side_copies = to_quad(1, center, r.sides_two)
    advance(PROJ)
    loads.conv_second.wait()
    loads.hidden.wait()
    r.product[...] = conv_back().reshape(IMAGE_ROWS, W, C)
    loads.conv_first = load(8, r.conv_first, r.conv_w)
    stretched = vec.stretch * vec.gain_two * vec.scale_two

    def second_row(i, sums):
        unit_two = unit(r.hid[i + 1], norm_two)
        normed = unit_two * vec.gain_two + vec.bias_two
        grad = r.product[i] * silu_slope_of(normed * vec.stretch + vec.shift)
        r.part_one[i + 1] = grad * stretched
        return sums[0] + column_sum(grad), sums[1] + column_sum(grad * unit_two)

    nothing = (jnp.zeros((1, C), full), jnp.zeros((1, C), full))
    plain, crossed = lax.fori_loop(0, IMAGE_ROWS, second_row, nothing)
    scale_grad = crossed * vec.gain_two + plain * vec.bias_two
    shift_grad = plain
    gain_two, bias_two = crossed * vec.stretch, plain * vec.stretch
    r.tile[1] = sums_tile(bias_two * vec.gain_two, gain_two * vec.gain_two)
    two_edges = band.edges(1, r.part_one.at[1], r.part_one.at[IMAGE_ROWS], r.part_one)
    tiles = band.send_tile(1, r.tile.at[1], r.window.at[1])
    for copy in (loads.act_two, loads.far_act_two, sibling.act2, sibling.far_act2):
        copy.wait()
    advance(PROJ, QKV, WORDS, WORDS + 1)
    conv_grads(SECOND_CONV, r.acts_two, r.sides_two, side_copies)
    advance(PROJ)
    for copy in tiles:
        copy.wait()
    band.wait_edges(two_edges)
    means = item_means(r.window.at[1])
    offset_two, slope_two = means[0:1] * vec.scale_two, means[1:2] * vec.scale_two

    def hidden_row(i, bias):
        values = r.part_one[i] - offset_two - unit(r.hid[i], norm_two) * slope_two
        values = kept(i, values, vec)
        spread_rows(i, values)
        inside = jnp.where((i > 0) & (i <= IMAGE_ROWS), 1.0, 0.0)
        return bias + inside * column_sum(values.astype(low).astype(full))

    conv_bias_one = lax.fori_loop(0, IMAGE_ROWS + 2, hidden_row, jnp.zeros((1, C), full))
    side_copies = to_quad(2, center, r.sides_one)
    advance(PROJ, QKV, WORDS, WORDS + 1)
    loads.conv_first.wait()
    loads.image.wait()
    r.product[...] = conv_back().reshape(IMAGE_ROWS, W, C)

    def first_row(i, sums):
        unit_one = unit(r.img[i].astype(full), norm_one)
        normed = unit_one * vec.gain_one + vec.bias_one
        grad = r.product[i] * silu_slope_of(normed)
        r.product[i] = grad
        return sums[0] + column_sum(grad), sums[1] + column_sum(grad * unit_one)

    plain, crossed = lax.fori_loop(0, IMAGE_ROWS, first_row, nothing)
    gain_one, bias_one = crossed, plain
    r.tile[2] = sums_tile(plain * vec.gain_one, crossed * vec.gain_one)
    tiles = band.send_tile(2, r.tile.at[2], r.window.at[2])
    rows = [
        gain_one,
        gain_two,
        gain_three,
        bias_one,
        bias_two,
        bias_three,
        conv_bias_one,
        conv_bias_two,
        query_sum,
        value_sum,
        word_sum[0],
        word_sum[1],
        up_sum,
        jnp.zeros((1, C), full),
        scale_grad,
        shift_grad,
    ]
    for i, values in enumerate(rows):
        r.own_rows[i : i + 1, :] = values
    row_copies = band.send_tile(3, r.own_rows, r.band_rows)
    for copy in (loads.act_one, loads.far_act_one, sibling.act1, sibling.far_act1):
        copy.wait()
    advance(PROJ, QKV, WORDS, WORDS + 1, 2, 3)
    conv_grads(FIRST_CONV, r.acts_one, r.sides_one, side_copies)
    for copy in tiles:
        copy.wait()
    means = item_means(r.window.at[2])
    offset_one, slope_one = means[0:1] * vec.scale_one, means[1:2] * vec.scale_one
    ratio = vec.gain_one * vec.scale_one

    def image_row(i, carry):
        unit_one = unit(r.img[i].astype(full), norm_one)
        values = r.part_two[i + 1] + r.product[i] * ratio - offset_one - unit_one * slope_one
        r.image_grad[i] = values
        return carry

    lax.fori_loop(0, IMAGE_ROWS, image_row, 0)

    for copy in row_copies:
        copy.wait()
    total = jnp.zeros((16, C), full)
    for b in range(SPAN):
        total = total + r.band_rows[b]
    r.half_rows[0:16, :] = total
    for b in range(SPAN):
        r.half_rows[16 + 2 * b : 18 + 2 * b, :] = r.band_rows[b, 14:16, :]
    far_copy = remote(
        r.half_rows, r.far_rows, r.small_send.at[0], r.small_recv.at[0], partner[FAR]
    )
    far_copy.start()
    loads.text_weight.wait()

    def caption_columns(n, carry):
        columns = pl.ds(pl.multiple_of(n * C, C), C)
        r.caption_grad[:, columns] = dot_last(r.joined_words[...], r.text_w[columns, :])
        return carry

    lax.fori_loop(0, EMB // C, caption_columns, 0)
    loads.embed_weight = load(13, r.embed_weight, r.text_w)
    slots = r.slot_of_band.shape[0]
    held = types.SimpleNamespace()

    def half_sums_arrived():
        far_copy.wait()
        first_half = jnp.where(place[FAR] == 0, r.half_rows[16:32, :], r.far_rows[16:32, :])
        other_half = jnp.where(place[FAR] == 0, r.far_rows[16:32, :], r.half_rows[16:32, :])
        r.group_rows[0:16, :] = r.half_rows[0:16, :] + r.far_rows[0:16, :]
        r.group_rows[16:32, :] = first_half
        r.group_rows[32:48, :] = other_half
        for k in range(2):
            table = jnp.zeros((slots, C), full)
            for b in range(2 * SPAN):
                values = r.group_rows[16 + 2 * b + k : 17 + 2 * b + k, :]
                table = table + jnp.where(r.slot_of_band[:, b * 128 : b * 128 + 1] > 0.0, values, 0.0)
            r.own_table[slots * k : slots * (k + 1), :] = table
        r.own_table[2 * slots :, :] = r.group_rows[0:16, :]
        held.group_copy = remote(
            r.own_table,
            r.other_table,
            r.small_send.at[1],
            r.small_recv.at[1],
            partner[GROUP],
        )
        held.group_copy.start()
        loads.embed_weight.wait()
        held.table = table = [r.own_table[slots * k : slots * (k + 1), :].astype(low) for k in range(2)]

        def embedding_columns(n, carry):
            columns = pl.ds(pl.multiple_of(n * C, C), C)
            grad = dot_last(table[0], r.text_w[columns, 0:C]) + dot_last(table[1], r.text_w[columns, C:])
            source = r.embedding[:, columns].astype(full)
            r.embedding_grad[:, columns] = grad * silu_slope_of(source)
            return carry

        lax.fori_loop(0, EMB // C, embedding_columns, 0)

    def group_sums_arrived():
        held.group_copy.wait()
        share_copy.wait()
        table = held.table
        for k in range(2):
            columns = slice(k * C, (k + 1) * C)
            other = r.other_table[slots * k : slots * (k + 1), :].astype(low)
            r.embed_weight_grad[:, columns] = dot_first(r.silu_share[...], table[k]) + dot_first(
                r.other_share[...], other
            )
            r.embed_bias_grad[:, columns] = column_sum(table[k].astype(full)) + column_sum(
                other.astype(full)
            )
        sums = r.own_table[2 * slots :, :] + r.other_table[2 * slots :, :]
        r.norm_gains_grad[...] = sums[0:3]
        r.norm_biases_grad[...] = sums[3:6]
        r.conv_biases_grad[...] = sums[6:8]
        for target, k in ((r.qv_bias_grad, 8), (r.text_bias_grad, 10)):
            target[:, 0:C] = sums[k : k + 1]
            target[:, C:] = sums[k + 1 : k + 2]
        r.proj_bias_grad[...] = sums[12:13]

    for k in TAIL:
        if k == HALF_SUMS:
            half_sums_arrived()
        elif k == GROUP_SUMS:
            group_sums_arrived()
        else:
            advance(k)

    def write(stream, target, first_row):
        rows, columns = STREAMS[stream][:2]
        for k in range(4):
            target[first_row : first_row + rows, k * columns : (k + 1) * columns] = r.folded[stream][
                k
            ].astype(full)

    def write_halves(stream, target):
        rows, columns = STREAMS[stream][:2]
        for side, source in ((group, r.folded[stream]), (1 - group, r.whole[stream - QKV])):
            for k in range(2):
                target[
                    pl.ds(pl.multiple_of(side * rows, rows), rows), k * columns : (k + 1) * columns
                ] = source[k].astype(full)

    for j in range(2):
        write(FIRST_CONV + j, r.conv_first_grad, j * 144)
        write(SECOND_CONV + j, r.conv_second_grad, j * 144)
        write(WORDS + j, r.text_grad, j * 64)
    write_halves(QKV, r.qkv_grad)
    write_halves(PROJ, r.proj_grad)


def silu_slope_of(source):
    sigma = 1.0 / (1.0 + jnp.exp(-source))
    return sigma * (1.0 + source * (1.0 - sigma))


def back(ident, vectors, slot_of_band, silu_share, embedding, anywhere):
    low, full = jnp.bfloat16, jnp.float32
    pixels = IMAGE_ROWS * W
    slots = slot_of_band.shape[0]
    outs = dict(
        result=((pixels, C), low),
        image_grad=((IMAGE_ROWS, W, C), full),
        caption_grad=((TEXT, EMB), full),
        conv_first_grad=((288, C), full),
        conv_second_grad=((288, C), full),
        qkv_grad=((32, 3 * C), full),
        text_grad=((128, 2 * C), full),
        proj_grad=((32, C), full),
        embedding_grad=(embedding.shape, full),
        embed_weight_grad=((silu_share.shape[1], 2 * C), full),
        norm_gains_grad=((3, C), full),
        norm_biases_grad=((3, C), full),
        conv_biases_grad=((2, C), full),
        embed_bias_grad=((1, 2 * C), full),
        qv_bias_grad=((1, 2 * C), full),
        text_bias_grad=((1, 2 * C), full),
        proj_bias_grad=((1, C), full),
    )
    padded = (IMAGE_ROWS + 2, W, C)
    scratch = dict(
        heads=((HEADS, pixels, 2 * HEAD), low),
        head_pairs=((HEADS, pixels, 2 * HEAD), low),
        head_words=((HEADS, TEXT, 2 * HEAD), low),
        joined=((pixels, 4 * C), low),
        joined_words=((TEXT, 2 * C), low),
        mid=(padded, full),
        part_two=(padded, full),
        part_one=(padded, full),
        hid=(padded, full),
        product=((IMAGE_ROWS, W, C), full),
        img=((IMAGE_ROWS, W, C), low),
        up=((pixels, C), low),
        act3=((pixels, C), low),
        conv_w=((9 * C, C), low),
        qkv_w=((C, 3 * C), low),
        proj_w=((C, C), low),
        text_w=((EMB, 2 * C), low),
        sib_up=((pixels, C // 2), low),
        sib_act3=((pixels, C), low),
        sib_attended=((pixels, C), low),
        sib_qkv=((pixels, 3 * C // 2), low),
        acts_one=((4, pixels + 2 * W, C), low),
        acts_two=((4, pixels + 2 * W, C), low),
        caps=((4, TEXT, EMB), low),
        own_word_part=((TEXT, C // 2), low),
        word_parts=((3, TEXT, C // 2), low),
        sides_one=((3, IMAGE_ROWS, W, C // 4), low),
        sides_two=((3, IMAGE_ROWS, W, C // 4), low),
        sides=((4, IMAGE_ROWS, W, 3 * C // 4), low),
        partial=((3, C, 3 * C // 4), full),
        shifts=((3,) + padded, low),
        blocks=((C, C), low),
        tile=((3, 8, C // 4), full),
        window=((3, SPAN, 8, C // 4), full),
        own_rows=((16, C), full),
        band_rows=((SPAN, 16, C), full),
        half_rows=((32, C), full),
        far_rows=((32, C), full),
        group_rows=((48, C), full),
        own_table=((2 * slots + 16, C), full),
        other_table=((2 * slots + 16, C), full),
        other_share=(silu_share.shape, low),
    )
    def halved(stream, step):
        return ((2,) * (len(stream[2]) + 1 - step) + stream[:2], low)

    scratch.update(grads=[halved(s, 0) for s in STREAMS])
    scratch.update(landings=[halved(s, i + 1) for s in STREAMS for i in range(len(s[2]))])
    scratch.update(folded=[((2 if GROUP in s[2] else 4,) + s[:2], low) for s in STREAMS])
    scratch.update(whole=[((2,) + s[:2], low) for s in STREAMS[QKV:]])
    semaphores = dict(
        swap_send=(2, SPAN),
        swap_recv=(2, SPAN),
        load_sem=(18,),
        quad_send=(3, 3),
        quad_recv=(3, 3),
        sib_send=(10,),
        sib_recv=(10,),
        edge_send=(2, 2),
        edge_recv=(2, 2),
        tile_send=(4, SPAN),
        tile_recv=(4, SPAN),
        fold_send=(len(STREAMS), len(GROUP_FIRST) + 3),
        fold_recv=(len(STREAMS), len(GROUP_FIRST) + 3),
        small_send=(3,),
        small_recv=(3,),
    )
    inputs = dict(
        vectors=vectors, slot_of_band=slot_of_band, silu_share=silu_share, embedding=embedding
    )
    return call_named(back_kernel, ident, (), inputs, anywhere, outs, scratch, semaphores)


def attend_kernel(names, *refs):
    low, full = jnp.bfloat16, jnp.float32
    r = grouped(names, refs)
    band = Band(r)
    counterpart = band.partner[GROUP]
    band.meet((counterpart,))
    query_swaps = band.swap(0, r.own_queries, r.queries, range(SPAN - 1, 0, -1))
    r.queries[band.lane] = r.own_queries[band.lane]
    far_copies = [
        band.remote(source, target, r.far_send.at[k], r.far_recv.at[k], counterpart)
        for k, (source, target) in enumerate(
            (
                (r.caption, r.far_caption),
                (r.act_two, r.far_act_two),
                (r.act_one, r.far_act_one),
            )
        )
    ]
    for copy in far_copies:
        copy.start()
    bands, pixels = r.pairs.shape[:2]
    text = r.words.shape[1]
    scale = HEAD ** (-0.5)

    def with_units(values, rows):
        lanes = lax.broadcasted_iota(jnp.int32, (rows, 2 * HEAD), 1)
        units = jnp.where(lanes < 2, 1.0, 0.0).astype(low)
        return jnp.where(lanes < HEAD, units, values)

    def prepare(b, carry):
        r.across[b] = r.pairs[b].T
        r.valued[b] = with_units(r.pairs[b], pixels)
        r.words_across[b] = r.words[b].T
        r.words_valued[b] = with_units(r.words[b], text)
        r.pair_sums[b] = jnp.zeros((pixels, 2 * HEAD), full)
        return carry

    lax.fori_loop(0, bands, prepare, 0)

    def one_row(columns):
        rows = lax.broadcasted_iota(jnp.int32, (16, columns), 0)
        return jnp.where(rows == 0, 1.0, 0.0).astype(low)

    ones_pixels = one_row(pixels)
    ones_text = one_row(text)
    zeros = jnp.zeros((HEAD, pixels), low)

    def outcome_copy(i):
        return band.remote(
            r.own_outcome.at[i],
            r.outcome.at[band.lane],
            r.outcome_send.at[i],
            r.outcome_recv.at[band.lane],
            {ROWS: band.base + i},
        )

    def query_band(step, carry):
        i = (band.lane + 1 + step) % bands
        mine = r.items[band.base + i]
        start = 0
        allowed = []
        for b in range(bands):
            other = r.items[band.base + b]
            start = start + jnp.where(other < mine, 1, 0)
            allowed.append(other == mine)

        @pl.when(step < bands - 1)
        def _():
            band.remote(
                r.own_queries.at[i],
                r.queries.at[i],
                r.swap_send.at[0, SPAN - 1 - step],
                r.swap_recv.at[0, SPAN - 1 - step],
                {ROWS: band.base + i},
            ).wait_recv()

        query = (r.queries[i].astype(full) * scale).astype(low)
        query_rhs = jnp.concatenate([query, zeros], 0)

        top = jnp.full((8, pixels), -jnp.inf, full)
        for j in range(bands):
            scores = dot(r.pairs[j], query_rhs)
            r.scores[j] = scores
            highest = jnp.max(scores.reshape(pixels // 8, 8, pixels), axis=0)
            top = jnp.where(allowed[j], jnp.maximum(top, highest), top)
        scores = dot(r.words[start], query_rhs)
        top = jnp.maximum(top, jnp.max(scores.reshape(text // 8, 8, pixels), axis=0))
        top = jnp.max(top, axis=0, keepdims=True)
        weights_text = jnp.exp2((scores - top) * LOG2E).astype(low)
        values = jnp.concatenate([r.words_across[start, HEAD:, :], ones_text], 0)
        total = dot(values, weights_text)

        for j in range(bands):
            ceiling = top + jnp.where(allowed[j], 0.0, FAR_ABOVE)
            weights = jnp.exp2((r.scores[j] - ceiling) * LOG2E).astype(low)
            r.weights[j] = weights
            values = jnp.concatenate([r.across[j, HEAD:, :], ones_pixels], 0)
            total = total + dot(values, weights)
        inverse = 1.0 / total[HEAD : HEAD + 1, :]
        attended = total[0:HEAD, :] * inverse
        grad = r.upstream[i].astype(full)
        minus_dots = -jnp.sum(grad * attended, axis=0, keepdims=True) * inverse
        grad_scaled = (grad * inverse).astype(low)
        coarse = minus_dots.astype(low)
        fine = minus_dots - coarse.astype(full)
        rows = lax.broadcasted_iota(jnp.int32, (HEAD, pixels), 0)
        extra = jnp.where(rows == 0, coarse.astype(full), jnp.where(rows == 1, fine, 0.0))
        grad_rhs = jnp.concatenate([extra.astype(low), grad_scaled], 0)
        grad_rows = jnp.concatenate([zeros, grad_scaled], 0).T
        query_rows = jnp.concatenate([query, zeros], 0).T

        steps = (weights_text.astype(full) * dot(r.words_valued[start], grad_rhs)).astype(low)
        word_sum = dot(weights_text, grad_rows) + dot(steps, query_rows)
        r.word_parts[i] = word_sum
        query_grad = dot(r.words_across[start, 0:HEAD, :], steps)
        for j in range(bands):
            for begin in range(0, pixels, pixels // 2):
                keys = slice(begin, begin + pixels // 2)
                weights = r.weights[j, keys]
                steps = (weights.astype(full) * dot(r.valued[j, keys], grad_rhs)).astype(low)
                r.pair_sums[j, keys] += dot(weights, grad_rows) + dot(steps, query_rows)
                query_grad = query_grad + dot(r.across[j, 0:HEAD, keys], steps)
        r.own_outcome[i] = jnp.concatenate(
            [attended.astype(low), (query_grad * scale).astype(low)], 0
        ).T
        pl.when(step < bands - 1)(outcome_copy(i).start)
        return carry

    lax.fori_loop(0, bands, query_band, 0)
    r.outcome[band.lane] = r.own_outcome[band.lane]

    def finish(b, carry):
        r.pair_grads[b] = r.pair_sums[b].astype(low)
        word_sum = jnp.zeros((text, 2 * HEAD), full)
        for i in range(bands):
            mine = r.items[band.base + i]
            start = 0
            for c in range(bands):
                start = start + jnp.where(r.items[band.base + c] < mine, 1, 0)
            word_sum = word_sum + jnp.where(start == b, r.word_parts[i], 0.0)
        r.word_grads[b] = word_sum.astype(low)
        return carry

    lax.fori_loop(0, bands, finish, 0)

    def wait_outcome(step, carry):
        i = (band.lane + 1 + step) % bands
        outcome_copy(i).wait_send()
        band.remote(
            r.own_outcome.at[i],
            r.outcome.at[i],
            r.outcome_send.at[i],
            r.outcome_recv.at[i],
            {ROWS: band.base + i},
        ).wait_recv()
        return carry

    lax.fori_loop(0, bands - 1, wait_outcome, 0)
    for copy in query_swaps:
        copy.wait_send()
    for copy in far_copies:
        copy.wait()


def attend(ident, items, ahead, caption):
    low, full = jnp.bfloat16, jnp.float32
    bands, pixels, _ = ahead.pairs.shape
    text = ahead.words.shape[1]
    outs = dict(
        outcome=((bands, pixels, 2 * HEAD), low),
        pair_grads=((bands, pixels, 2 * HEAD), low),
        word_grads=((bands, text, 2 * HEAD), low),
    )
    anywhere = dict(caption=caption, act_one=ahead.act_one, act_two=ahead.act_two)
    far = dict(
        far_caption=(caption.shape, low),
        far_act_one=(ahead.act_one.shape, low),
        far_act_two=(ahead.act_two.shape, low),
    )
    scratch = dict(
        queries=(ahead.own_queries.shape, low),
        across=((bands, 2 * HEAD, pixels), low),
        valued=((bands, pixels, 2 * HEAD), low),
        words_across=((bands, 2 * HEAD, text), low),
        words_valued=((bands, text, 2 * HEAD), low),
        scores=((bands, pixels, pixels), full),
        weights=((bands, pixels, pixels), low),
        pair_sums=((bands, pixels, 2 * HEAD), full),
        word_parts=((bands, text, 2 * HEAD), full),
        own_outcome=((bands, pixels, 2 * HEAD), low),
    )
    semaphores = dict(
        outcome_send=(bands,), outcome_recv=(bands,), far_send=(3,), far_recv=(3,),
        swap_send=(1, SPAN), swap_recv=(1, SPAN),
    )
    inputs = dict(
        pairs=ahead.pairs,
        own_queries=ahead.own_queries,
        upstream=ahead.upstream,
        words=ahead.words,
    )
    return call_named(
        attend_kernel, ident, dict(items=items), inputs, anywhere, outs, scratch, semaphores, far
    )


def front_kernel(names, *refs):
    low, full = jnp.bfloat16, jnp.float32
    r = grouped(names, refs)
    band = Band(r)
    band.meet()
    loads = types.SimpleNamespace()

    def load(k, source, target):
        copy = pltpu.make_async_copy(source, target, r.load_sem.at[k])
        copy.start()
        return copy

    loads.image = load(0, r.image, r.img.at[1 : IMAGE_ROWS + 1])
    image_edges = band.edges(0, r.image.at[0], r.image.at[IMAGE_ROWS - 1], r.img)
    loads.upstream = load(3, r.upstream_pixels, r.up)
    loads.proj_weight = load(4, r.proj_weight, r.proj_w)
    loads.conv_first = load(1, r.conv_first, r.first_w)
    loads.embed_weight = load(2, r.embed_weight, r.embed_w)
    loads.conv_second = load(5, r.conv_second, r.second_w)
    loads.caption = load(6, r.caption, r.cap)
    loads.text_weight = load(7, r.text_weight, r.text_w)
    loads.qkv_weight = load(8, r.qkv_weight, r.qkv_w)

    mine = r.items[band.row]
    same = [(r.items[band.base + b] == mine).astype(full) for b in range(SPAN)]
    masks = [jnp.full((1, C), m, full) for m in same]
    bands = masks[0]
    for m in masks[1:]:
        bands = bands + m
    per_item = 1.0 / (bands * (IMAGE_ROWS * W * (C // NORM_GROUPS)))
    before = jnp.where(band.has_above, r.items[jnp.maximum(band.row - 1, 0)], -1)
    after = jnp.where(
        band.has_below, r.items[jnp.minimum(band.row + 1, r.items.shape[0] - 1)], -1
    )
    found = types.SimpleNamespace(
        gain_one=r.norm_gains[0:1, :],
        gain_two=r.norm_gains[1:2, :],
        gain_three=r.norm_gains[2:3, :],
        bias_one=r.norm_biases[0:1, :],
        bias_two=r.norm_biases[1:2, :],
        bias_three=r.norm_biases[2:3, :],
        proj_bias=r.proj_bias[...],
        keep_above=jnp.full((1, C), (before == mine).astype(full)),
        keep_below=jnp.full((1, C), (after == mine).astype(full)),
        per_item=per_item,
    )
    for target in (r.img, r.hidden, r.middle):
        band.zero_edges(target)
    nothing = (jnp.zeros((1, C), full), jnp.zeros((1, C), full))

    def norm_of(k):
        means = band.item_means(r.window.at[k], masks, per_item)
        return means[0:1], lax.rsqrt(means[1:2] - means[0:1] * means[0:1] + epsilon)

    loads.image.wait()

    def image_sums(i, sums):
        values = r.img[i + 1].astype(full)
        return sums[0] + column_sum(values), sums[1] + column_sum(values * values)

    r.tile[0] = sums_tile(*lax.fori_loop(0, IMAGE_ROWS, image_sums, nothing))
    tiles = band.send_tile(0, r.tile.at[0], r.window.at[0])

    loads.upstream.wait()
    loads.proj_weight.wait()
    attended_grad = dot_last(r.proj_w[...], r.up[...]).astype(low)
    for h in range(HEADS):
        r.own_upstream[h] = attended_grad[h * HEAD : (h + 1) * HEAD, :]
    swaps = band.swap(0, r.own_upstream, r.upstream)
    r.upstream[band.lane] = r.own_upstream[band.lane]
    band.fill_blocks()
    slot = lax.broadcasted_iota(jnp.int32, r.embedding.shape, 0)
    chosen = jnp.where(slot == mine, r.embedding[...].astype(full), 0.0)
    chosen = jnp.sum(chosen, axis=0, keepdims=True)
    chosen = chosen / (1.0 + jnp.exp(-chosen))
    chosen = jnp.broadcast_to(chosen, (16, EMB)).astype(low)
    loads.embed_weight.wait()
    modulation = dot(chosen, r.embed_w[...])[0:1] + r.embed_bias[...]
    found.stretch = 1.0 + modulation[:, 0:C]
    found.shift = modulation[:, C:]

    def spread_rows(i, values, target):
        values = kept(i, values, found)
        from_left, from_right = side_shifts(values)
        r.shifts[0, i] = from_left.astype(low)
        r.shifts[1, i] = values.astype(low)
        r.shifts[2, i] = from_right.astype(low)
        target[pl.ds(pl.multiple_of(i * W, W), W), :] = values.astype(low)

    def conv(weight):
        total = jnp.zeros((IMAGE_ROWS * W, C), full)
        for t in range(9):
            view = r.shifts[t % 3, t // 3 : t // 3 + IMAGE_ROWS].reshape(IMAGE_ROWS * W, C)
            total = total + dot(view, weight[t * C : (t + 1) * C, :])
        return total

    for copy in tiles:
        copy.wait()
    band.wait_edges(image_edges)
    found.mean_one, found.scale_one = norm_of(0)

    def first_row(i, carry):
        unit = (r.img[i].astype(full) - found.mean_one) * found.scale_one
        normed = unit * found.gain_one + found.bias_one
        spread_rows(i, normed / (1.0 + jnp.exp(-normed)), r.act_one)
        return carry

    lax.fori_loop(0, IMAGE_ROWS + 2, first_row, 0)
    loads.conv_first.wait()
    total = conv(r.first_w) + r.conv_biases[0:1, :]
    r.hidden[1 : IMAGE_ROWS + 1] = total.reshape(IMAGE_ROWS, W, C)
    hidden_edges = band.edges(1, r.hidden.at[1], r.hidden.at[IMAGE_ROWS], r.hidden)
    r.tile[1] = sums_tile(column_sum(total), column_sum(total * total))
    tiles = band.send_tile(1, r.tile.at[1], r.window.at[1])

    loads.caption.wait()
    loads.text_weight.wait()
    words = (dot(r.cap[...], r.text_w[...]) + r.text_bias[...]).astype(low)
    for h in range(HEADS):
        parts = [words[:, k * C + h * HEAD : k * C + (h + 1) * HEAD] for k in range(2)]
        r.own_words[h] = jnp.concatenate(parts, axis=1)
    swaps = swaps + band.swap(1, r.own_words, r.words)
    r.words[band.lane] = r.own_words[band.lane]
    for copy in tiles:
        copy.wait()
    band.wait_edges(hidden_edges)
    found.mean_two, found.scale_two = norm_of(1)

    def second_row(i, carry):
        unit = (r.hidden[i] - found.mean_two) * found.scale_two
        normed = unit * found.gain_two + found.bias_two
        shifted = normed * found.stretch + found.shift
        spread_rows(i, shifted / (1.0 + jnp.exp(-shifted)), r.act_two)
        return carry

    lax.fori_loop(0, IMAGE_ROWS + 2, second_row, 0)
    loads.conv_second.wait()
    total = conv(r.second_w) + r.conv_biases[1:2, :]
    total = total + r.img[1 : IMAGE_ROWS + 1].astype(full).reshape(IMAGE_ROWS * W, C)
    r.middle[1 : IMAGE_ROWS + 1] = total.reshape(IMAGE_ROWS, W, C)
    r.tile[2] = sums_tile(column_sum(total), column_sum(total * total))
    tiles = band.send_tile(2, r.tile.at[2], r.window.at[2])
    middle_edges = band.edges(2, r.middle.at[1], r.middle.at[IMAGE_ROWS], r.middle)

    loads.qkv_weight.wait()
    for copy in tiles:
        copy.wait()
    found.mean_three, found.scale_three = norm_of(2)
    for i in range(2):
        middle = r.middle[1 + 4 * i : 5 + 4 * i].reshape(4 * W, C)
        unit = (middle - found.mean_three) * found.scale_three
        block = slice(i * 4 * W, (i + 1) * 4 * W)
        act = (unit * found.gain_three + found.bias_three).astype(low)
        r.act_three[block, :] = act
        projected = dot(act, r.qkv_w[...])
        queries = (projected[:, 0:C] + r.qv_bias[:, 0:C]).astype(low)
        keys = projected[:, C : 2 * C].astype(low)
        values = (projected[:, 2 * C :] + r.qv_bias[:, C:]).astype(low)
        queries = queries.T
        for h in range(HEADS):
            head = slice(h * HEAD, (h + 1) * HEAD)
            r.own_queries[h, :, block] = queries[head, :]
            r.own_pairs[h, block, :] = jnp.concatenate([keys[:, head], values[:, head]], axis=1)
    swaps = swaps + band.swap(2, r.own_pairs, r.pairs)
    r.pairs[band.lane] = r.own_pairs[band.lane]
    fields = [getattr(found, name) for name in Vectors._fields]
    for i, values in enumerate(fields):
        r.vectors[i : i + 1, :] = values
    r.vectors[len(fields) : VECTOR_ROWS, :] = jnp.zeros((VECTOR_ROWS - len(fields), C), full)
    for b in range(SPAN):
        r.vectors[VECTOR_ROWS + b : VECTOR_ROWS + b + 1, :] = masks[b]
    band.wait_edges(middle_edges)
    for copy in swaps:
        copy.wait()


def front(ident, items, inputs, anywhere):
    low, full = jnp.bfloat16, jnp.float32
    pixels = IMAGE_ROWS * W
    padded = (IMAGE_ROWS + 2, W, C)
    outs = dict(
        pairs=((HEADS, pixels, 2 * HEAD), low),
        own_queries=((HEADS, HEAD, pixels), low),
        upstream=((HEADS, HEAD, pixels), low),
        words=((HEADS, TEXT, 2 * HEAD), low),
        act_one=((pixels + 2 * W, C), low),
        act_two=((pixels + 2 * W, C), low),
        act_three=((pixels, C), low),
        hidden=(padded, full),
        middle=(padded, full),
        vectors=((VECTOR_ROWS + SPAN, C), full),
    )
    scratch = dict(
        img=(padded, low),
        up=((pixels, C), low),
        cap=((TEXT, EMB), low),
        first_w=((9 * C, C), low),
        second_w=((9 * C, C), low),
        embed_w=((EMB, 2 * C), low),
        text_w=((EMB, 2 * C), low),
        qkv_w=((C, 3 * C), low),
        proj_w=((C, C), low),
        shifts=((3,) + padded, low),
        blocks=((C, C), low),
        tile=((3, 8, C // 4), full),
        window=((3, SPAN, 8, C // 4), full),
        own_pairs=((HEADS, pixels, 2 * HEAD), low),
        own_upstream=((HEADS, HEAD, pixels), low),
        own_words=((HEADS, TEXT, 2 * HEAD), low),
    )
    semaphores = dict(
        load_sem=(9,),
        edge_send=(3, 2),
        edge_recv=(3, 2),
        tile_send=(3, SPAN),
        tile_recv=(3, SPAN),
        swap_send=(3, SPAN),
        swap_recv=(3, SPAN),
    )
    return call_named(
        front_kernel, ident, dict(items=items), inputs, anywhere, outs, scratch, semaphores
    )


def hand_over_kernel(count, *refs):
    sources, targets, held = refs[:count], refs[count : 2 * count], refs[2 * count : 3 * count]
    load_sem, store_sem = refs[3 * count :]
    loads = [
        pltpu.make_async_copy(source, buffer, load_sem.at[k])
        for k, (source, buffer) in enumerate(zip(sources, held))
    ]
    stores = [
        pltpu.make_async_copy(buffer, target, store_sem.at[k])
        for k, (buffer, target) in enumerate(zip(held, targets))
    ]
    for copy in loads:
        copy.start()
    for load, store in zip(loads, stores):
        load.wait()
        store.start()
    for copy in stores:
        copy.wait()


def hand_over(arrays):
    anywhere = pl.BlockSpec(memory_space=pl.ANY)
    count = len(arrays)
    return pl.pallas_call(
        functools.partial(hand_over_kernel, count),
        out_shape=tuple(jax.ShapeDtypeStruct(a.shape, a.dtype) for a in arrays),
        in_specs=[anywhere] * count,
        out_specs=(anywhere,) * count,
        scratch_shapes=[pltpu.VMEM(a.shape, a.dtype) for a in arrays]
        + [pltpu.SemaphoreType.DMA((count,))] * 2,
        name=hand_over.__name__,
    )(*arrays)


def blocks_of(rows):
    return rows.reshape(rows.shape[0], NORM_GROUPS, -1)


def spread(values):
    return jnp.repeat(values, C // NORM_GROUPS)


def in_halves(
    image,
    embedding,
    caption,
    item_of_band,
    out_grad,
    norm_gains,
    norm_biases,
    conv_first,
    conv_second,
    conv_biases,
    embed_weight,
    embed_bias,
    qkv_weight,
    qv_bias,
    text_weight,
    text_bias,
    proj_weight,
    proj_bias,
):
    low = jnp.bfloat16
    pixels = image.shape[1]
    position = lax.axis_index(ROWS)
    items = item_of_band[0]
    slots = items.shape[0]
    by_row = (-1, W, C)
    ahead = front(
        0,
        items,
        dict(
            embedding=embedding[0],
            norm_gains=norm_gains,
            norm_biases=norm_biases,
            conv_biases=conv_biases,
            embed_bias=embed_bias[None],
            qv_bias=qv_bias[None],
            text_bias=text_bias[None],
            proj_bias=proj_bias[None],
        ),
        dict(
            image=image.reshape(by_row),
            conv_first=conv_first,
            embed_weight=embed_weight,
            upstream_pixels=out_grad[0],
            proj_weight=proj_weight,
            conv_second=conv_second,
            caption=caption[0, 0],
            text_weight=text_weight,
            qkv_weight=qkv_weight,
        ),
    )
    found = attend(2, items, ahead, caption[0, 0])
    slot_of_band = (jnp.arange(slots)[:, None] == items[None, :]).astype(jnp.float32)
    row_share = EMB // lax.axis_size(ROWS)
    share = lax.dynamic_slice_in_dim(embedding[0], position * row_share, row_share, 1)
    silu_share = jax.nn.silu(share.astype(jnp.float32)).astype(low)
    out = back(
        1,
        ahead.vectors,
        jnp.repeat(slot_of_band, 128, axis=1),
        silu_share,
        embedding[0],
        dict(
            outcome=found.outcome,
            pair_grads=found.pair_grads,
            word_grads=found.word_grads,
            middle=ahead.middle,
            qkv_weight=qkv_weight,
            proj_weight=proj_weight,
            upstream=out_grad[0],
            act_three=ahead.act_three,
            caption=caption[0, 0],
            conv_second=conv_second,
            conv_first=conv_first,
            hidden=ahead.hidden,
            act_two=ahead.act_two,
            act_one=ahead.act_one,
            far_caption=found.far_caption,
            far_act_one=found.far_act_one,
            far_act_two=found.far_act_two,
            image=image.reshape(by_row),
            text_weight=text_weight,
            embed_weight=embed_weight,
        ),
    )
    out = types.SimpleNamespace(**dict(zip(vars(out), hand_over(list(vars(out).values())))))
    return (
        out.result[None],
        out.image_grad.reshape(1, pixels, C),
        out.embedding_grad[None],
        out.caption_grad[None, None],
        out.norm_gains_grad,
        out.norm_biases_grad,
        out.conv_first_grad,
        out.conv_second_grad,
        out.conv_biases_grad,
        out.embed_weight_grad,
        out.embed_bias_grad.reshape(-1),
        out.qkv_grad,
        out.qv_bias_grad.reshape(-1),
        out.text_grad,
        out.text_bias_grad.reshape(-1),
        out.proj_grad,
        out.proj_bias_grad.reshape(-1),
    )


def shards(
    image,
    embedding,
    caption,
    item_of_band,
    out_grad,
    norm_gains,
    norm_biases,
    conv_first,
    conv_second,
    conv_biases,
    embed_weight,
    embed_bias,
    qkv_weight,
    qv_bias,
    text_weight,
    text_bias,
    proj_weight,
    proj_bias,
):
    low = jnp.bfloat16
    full = jnp.float32
    pixels = image.shape[1]
    band_items = item_of_band[0]
    slots = band_items.shape[0]
    if slots == 2 * SPAN and lax.axis_size(ITEMS) == 2 and HEADS == SPAN:
        return in_halves(
            image,
            embedding,
            caption,
            item_of_band,
            out_grad,
            norm_gains,
            norm_biases,
            conv_first,
            conv_second,
            conv_biases,
            embed_weight,
            embed_bias,
            qkv_weight,
            qv_bias,
            text_weight,
            text_bias,
            proj_weight,
            proj_bias,
        )
    position = lax.axis_index(ROWS)
    my_item = band_items[position]
    slot_hot = (jnp.arange(slots) == my_item).astype(full)
    item_count = jnp.sum((band_items == my_item).astype(full)) * pixels * (C // NORM_GROUPS)
    reach = position + jnp.arange(-REACH, REACH + 1)
    near = (reach >= 0) & (reach < slots)
    near = near & (band_items[jnp.clip(reach, 0, slots - 1)] == my_item)
    keep = jnp.concatenate(
        [
            jnp.full((W, 1), near[REACH - 1]),
            jnp.full((pixels, 1), True),
            jnp.full((W, 1), near[REACH + 1]),
        ]
    )
    own_lead = jnp.logical_not(near[REACH - 1])

    def totals(ident, first, second, edges=None):
        sums = jnp.stack([jnp.sum(blocks_of(first), axis=(0, 2)), jnp.sum(blocks_of(second), axis=(0, 2))])
        tile = jnp.pad(sums, ((0, 6), (0, 128 - NORM_GROUPS)))
        if edges is not None:
            outcome = exchange(ident, slots, tile, (edges[:W], edges[-W:]))
        else:
            outcome = exchange(ident, slots, tile)
        summed = jnp.sum(jnp.where(near[:, None, None], outcome[0], 0.0), axis=0)
        summed = summed[:2, :NORM_GROUPS] / item_count
        return summed, outcome[1:]

    def stats(summed):
        scales = lax.rsqrt(summed[1] - summed[0] * summed[0] + epsilon)
        return spread(summed[0]), spread(scales)

    inputs = image[0].astype(full)
    summed, (above, below) = totals(0, inputs, inputs * inputs, image[0])
    means_one, scales_one = stats(summed)
    padded = jnp.concatenate([above, image[0], below]).astype(full)
    unit_padded = (padded - means_one) * scales_one
    normed_padded = unit_padded * norm_gains[0] + norm_biases[0]
    act_one_padded = jnp.where(keep, jax.nn.silu(normed_padded), 0.0).astype(low)
    unit_one = unit_padded[W:-W]
    normed_one = normed_padded[W:-W]
    taps_one = jnp.concatenate(taps_of(act_one_padded, False), axis=1)
    hidden_one = dot(taps_one, conv_first) + conv_biases[0]
    embed_silu = jax.nn.silu(embedding[0].astype(full)).astype(low)
    my_silu = dot(slot_hot.astype(low)[None], embed_silu).astype(low)
    modulation = dot(my_silu, embed_weight)[0] + embed_bias
    scale_part = modulation[:C]
    shift_part = modulation[C:]
    summed, (above, below) = totals(1, hidden_one, hidden_one * hidden_one, hidden_one)
    means_two, scales_two = stats(summed)
    hidden_padded = jnp.concatenate([above, hidden_one, below])
    unit_padded = (hidden_padded - means_two) * scales_two
    normed_padded = unit_padded * norm_gains[1] + norm_biases[1]
    shifted_padded = normed_padded * (1.0 + scale_part) + shift_part
    act_two_padded = jnp.where(keep, jax.nn.silu(shifted_padded), 0.0).astype(low)
    unit_two = unit_padded[W:-W]
    normed_two = normed_padded[W:-W]
    shifted = shifted_padded[W:-W]
    taps_two = jnp.concatenate(taps_of(act_two_padded, False), axis=1)
    middle = inputs + dot(taps_two, conv_second) + conv_biases[1]
    summed, _ = totals(2, middle, middle * middle)
    means_three, scales_three = stats(summed)
    unit_three = (middle - means_three) * scales_three
    act_three = (unit_three * norm_gains[2] + norm_biases[2]).astype(low)
    projected = dot(act_three, qkv_weight)
    queries = (projected[:, :C] + qv_bias[:C]).astype(low)
    keys_values = jnp.concatenate(
        [projected[:, C : 2 * C], projected[:, 2 * C :] + qv_bias[C:]], axis=1
    ).astype(low)
    captions = caption[0, 0]
    text_kv = lax.cond(
        own_lead,
        lambda: (dot(captions, text_weight) + text_bias).astype(low),
        lambda: jnp.zeros((TEXT, 2 * C), low),
    )
    upstream = out_grad[0]
    upstream_float = upstream.astype(full)
    attended_grad = dot_last(upstream, proj_weight).astype(low)
    group = lax.axis_index(ITEMS)
    groups = lax.axis_size(ITEMS)
    attended_low, query_low, key_value_low, text_low = attention_by_band(
        band_items, position, queries, keys_values, text_kv, attended_grad
    )
    result = middle + dot(attended_low, proj_weight) + proj_bias
    proj_weight_grad = dot_first(attended_low, upstream)
    proj_bias_grad = jnp.sum(upstream_float, axis=0)
    qkv_grad = jnp.concatenate([query_low, key_value_low], axis=1)
    qkv_weight_grad = dot_first(act_three, qkv_grad)
    qv_bias_grad = jnp.sum(
        jnp.concatenate([query_low, key_value_low[:, C:]], axis=1).astype(full), axis=0
    )
    text_weight_grad = dot_first(captions, text_low)
    text_bias_grad = jnp.sum(text_low.astype(full), axis=0)
    caption_grad = dot_last(text_low, text_weight)[None, None]
    three_grad = dot_last(qkv_grad, qkv_weight)
    gain_three = jnp.sum(three_grad * unit_three, axis=0)
    bias_three = jnp.sum(three_grad, axis=0)

    def conv_back(padded, weight):
        views = jnp.stack(taps_of(padded, True))
        return jnp.einsum(
            "tpd,tcd->pc", views, weight.reshape(9, C, C), preferred_element_type=full
        )

    def norm_back(ident, grad_unit, unit_value, scales, base, with_edges=True):
        scaled = base + grad_unit * scales
        edges = jnp.concatenate([scaled, unit_value], axis=1) if with_edges else None
        summed, around = totals(ident, grad_unit, grad_unit * unit_value, edges)
        mean_grad, mean_cross = spread(summed[0]) * scales, spread(summed[1]) * scales
        if not with_edges:
            return scaled - mean_grad - unit_value * mean_cross
        both = jnp.concatenate([around[0], edges, around[1]])
        return both[:, :C] - mean_grad - both[:, C:] * mean_cross

    middle_padded = norm_back(3, three_grad * norm_gains[2], unit_three, scales_three, upstream_float)
    middle_grad = middle_padded[W:-W]
    low_padded = jnp.where(keep, middle_padded, 0.0).astype(low)
    hidden_two_low = low_padded[W:-W]
    conv_bias_two = jnp.sum(hidden_two_low.astype(full), axis=0)
    conv_second_grad = dot_first(taps_two, hidden_two_low)
    act_two_grad = conv_back(low_padded, conv_second)
    shifted_grad = act_two_grad * silu_slope(shifted)
    modulation_grad = jnp.concatenate(
        [jnp.sum(shifted_grad * normed_two, axis=0), jnp.sum(shifted_grad, axis=0)]
    )
    normed_two_grad = shifted_grad * (1.0 + scale_part)
    gain_two = jnp.sum(normed_two_grad * unit_two, axis=0)
    bias_two = jnp.sum(normed_two_grad, axis=0)
    hidden_back = norm_back(4, normed_two_grad * norm_gains[1], unit_two, scales_two, 0.0)
    low_padded = jnp.where(keep, hidden_back, 0.0).astype(low)
    hidden_one_low = low_padded[W:-W]
    conv_bias_one = jnp.sum(hidden_one_low.astype(full), axis=0)
    conv_first_grad = dot_first(taps_one, hidden_one_low)
    act_one_grad = conv_back(low_padded, conv_first)
    normed_one_grad = act_one_grad * silu_slope(normed_one)
    gain_one = jnp.sum(normed_one_grad * unit_one, axis=0)
    bias_one = jnp.sum(normed_one_grad, axis=0)
    image_grad = norm_back(
        5, normed_one_grad * norm_gains[0], unit_one, scales_one, middle_grad, False
    )
    group_hot = (jnp.arange(groups) == group).astype(full)
    tables = group_hot[:, None, None] * slot_hot[None, :, None] * modulation_grad
    vectors = jnp.concatenate(
        [
            gain_one,
            gain_two,
            gain_three,
            bias_one,
            bias_two,
            bias_three,
            conv_bias_one,
            conv_bias_two,
            qv_bias_grad,
            text_bias_grad,
            proj_bias_grad,
        ]
    )
    small = jnp.concatenate([tables.reshape(-1, C), vectors.reshape(-1, C)])
    row_share = EMB // lax.axis_size(ROWS)
    silu_share = lax.dynamic_slice_in_dim(embed_silu, position * row_share, row_share, 1)
    grads = (conv_first_grad, conv_second_grad, qkv_weight_grad, text_weight_grad, proj_weight_grad)
    grads = [g.astype(low) for g in grads]
    small = lax.psum(small.astype(low), (ROWS, ITEMS)).astype(full)
    tables_sum = small[: groups * slots * 2].reshape(groups, slots, 2 * C).astype(low)
    part = dot_first(silu_share, jnp.take(tables_sum, group, axis=0)).astype(low)
    matrices = [lax.psum_scatter(g, ROWS, scatter_dimension=0, tiled=True) for g in grads]
    *matrices, embed_weight_grad = [
        lax.psum(m, ITEMS).astype(full) for m in matrices + [part]
    ]
    vectors_sum = small[groups * slots * 2 :]
    modulation_low = jnp.take(tables_sum, group, axis=0)
    embed_bias_grad = jnp.sum(tables_sum.astype(full), axis=(0, 1))
    embedding_grad = dot_last(modulation_low, embed_weight) * silu_slope(embedding[0].astype(full))
    return (
        result.astype(low)[None],
        image_grad[None],
        embedding_grad[None],
        caption_grad,
        vectors_sum[0:3],
        vectors_sum[3:6],
        matrices[0],
        matrices[1],
        vectors_sum[6:8],
        embed_weight_grad,
        embed_bias_grad,
        matrices[2],
        vectors_sum[8:10].reshape(-1),
        matrices[3],
        vectors_sum[10:12].reshape(-1),
        matrices[4],
        vectors_sum[12],
    )


def solution(mesh):
    in_specs = (
        P(ITEMS, ROWS, None),
        P(ITEMS, None, None),
        P(ITEMS, ROWS, None, None),
        P(ITEMS, None),
        P(ITEMS, ROWS, None),
        P(),
        P(),
        P(),
        P(),
        P(),
        P(),
        P(),
        P(),
        P(),
        P(),
        P(),
        P(),
        P(),
    )
    out_specs = (
        P(ITEMS, ROWS, None),
        P(ITEMS, ROWS, None),
        P(ITEMS, None, None),
        P(ITEMS, ROWS, None, None),
        P(),
        P(),
        P(ROWS, None),
        P(ROWS, None),
        P(),
        P(ROWS, None),
        P(),
        P(ROWS, None),
        P(),
        P(ROWS, None),
        P(),
        P(ROWS, None),
        P(),
    )
    return jax.shard_map(shards, mesh=mesh, in_specs=in_specs, out_specs=out_specs, check_vma=False)
```
